32 devices in a mesh: narrow: 4 (over y, x), wide: 8 (over z, core).
Axes of the slice: x: 2, y: 2, z: 4, core: 2. Of those that a mesh axis runs over, the one named last changes fastest.
Arguments:
- byte_ids: int32 [8192], P(('narrow', 'wide')), may hold values from 0 to 255
- doc_patches: int32 [9], replicated, may hold values from 1 to 341, 1024 in all
- pad_bytes: int32 [9], replicated, may hold values from 0 to 7
- byte_table: bfloat16 [256, 128], P(('narrow', 'wide')), may hold values from -6 to 6
- patch_weight: bfloat16 [1024, 1024], P(('narrow', 'wide')), may hold values from -0.1875 to 0.1875
- gain_mix: float32 [1024], replicated, may hold values from 0.5 to 1.5
- in_weight: bfloat16 [1024, 4384], P(('narrow', 'wide')), may hold values from -0.1875 to 0.1875
- conv_weight: float32 [4, 2304], replicated, may hold values from -3 to 3
- conv_bias: float32 [2304], replicated, may hold values from -2 to 2
- step_bias: float32 [32], replicated, may hold values from -6.9 to -2.25
- log_rate: float32 [32], replicated, may hold values from 0 to 2.77
- skip_gain: float32 [32], replicated, may hold values from 0.5 to 1.5
- gated_gain: float32 [2048], replicated, may hold values from 0.5 to 1.5
- out_weight: bfloat16 [2048, 1024], P(('narrow', 'wide')), may hold values from -0.125 to 0.125
- local_weight: bfloat16 [128, 1024], P(None, ('narrow', 'wide')), may hold values from -0.5 to 0.5
- gain_attn: float32 [1024], replicated, may hold values from 0.5 to 1.5
- query_weight: bfloat16 [1024, 1024], P(('narrow', 'wide')), may hold values from -0.1875 to 0.1875
- key_weight: bfloat16 [1024, 1024], P(('narrow', 'wide')), may hold values from -0.1875 to 0.1875
- value_weight: bfloat16 [1024, 1024], P(('narrow', 'wide')), may hold values from -0.1875 to 0.1875
- attn_weight: bfloat16 [1024, 1024], P(('narrow', 'wide')), may hold values from -0.5 to 0.5
- feed_gain: float32 [1024], replicated, may hold values from 0.5 to 1.5
- gate_weight: bfloat16 [1024, 4096], P('narrow', 'wide'), may hold values from -0.1875 to 0.1875
- up_weight: bfloat16 [1024, 4096], P('narrow', 'wide'), may hold values from -0.1875 to 0.1875
- down_weight: bfloat16 [4096, 1024], P('wide', 'narrow'), may hold values from -0.09375 to 0.09375
- cotangent: bfloat16 [8192, 1024], P(('narrow', 'wide')), may hold values from -6 to 6
Outputs:
- out_rows: bfloat16 [8192, 1024], P(('narrow', 'wide'))
- grad_table: float32 [256, 128], P(('narrow', 'wide'))
- grad_patch: float32 [1024, 1024], P(('narrow', 'wide'))
- grad_gain_mix: float32 [1024], replicated
- grad_in: float32 [1024, 4384], P(('narrow', 'wide'))
- grad_conv_weight: float32 [4, 2304], replicated
- grad_conv_bias: float32 [2304], replicated
- grad_step_bias: float32 [32], replicated
- grad_log_rate: float32 [32], replicated
- grad_skip_gain: float32 [32], replicated
- grad_gated_gain: float32 [2048], replicated
- grad_out: float32 [2048, 1024], P(('narrow', 'wide'))
- grad_local: float32 [128, 1024], P(None, ('narrow', 'wide'))
- grad_gain_attn: float32 [1024], replicated
- grad_query: float32 [1024, 1024], P(('narrow', 'wide'))
- grad_key: float32 [1024, 1024], P(('narrow', 'wide'))
- grad_value: float32 [1024, 1024], P(('narrow', 'wide'))
- grad_attn: float32 [1024, 1024], P(('narrow', 'wide'))
- grad_feed_gain: float32 [1024], replicated
- grad_gate: float32 [1024, 4096], P('narrow', 'wide')
- grad_up: float32 [1024, 4096], P('narrow', 'wide')
- grad_down: float32 [4096, 1024], P('wide', 'narrow')
The draws below stay inside these ranges and needn't reach their ends.
Inputs may be any that keep to these rules, and one draw needn't show every extreme that they name: `doc_patches`: documents lie end to end over all patches; the longest has exactly 341 patches.
All inputs are finite; a program needn't handle non-finite values.
Results may differ from the reference program's by a relative error of at most 0.04.
Values may be sent and summed in bfloat16 or wider, within the bound.
A program may use at most 448 MiB of HBM per device.

```python
import math
from functools import partial
import jax
import jax.numpy as jnp
import numpy as np
from jax import lax

D = 1024
PATCH = 8
EMB = 128
VOCAB = 256
HEADS_M = 32
HEAD_M = 64
DI = 2048
STATE = 128
CONV = 4
XBC = 2304
IN_W = 4384
HEADS_A = 16
HEAD_A = 64
FF = 4096
SEQS = 9
PATCHES = 1024
BYTES = 8192
MOST_PATCHES = 341
N_NARROW = 4


def plant(entries, rng, smallest, top_value):
    longest = entries.shape.index(max(entries.shape))
    spots = []
    for shift in (0, 1):
        where = [jax.random.randint(jax.random.fold_in(rng, axis), (), 0, length) for axis, length in enumerate(entries.shape)]
        where[longest] = (where[longest] + shift) % entries.shape[longest]
        spots.append(tuple(where))
    return entries.at[spots[0]].set(smallest).at[spots[1]].set(top_value)


def steps_of(own_key, extent, cuts, least, largest):
    level = 1.0
    for axis_at, parts in cuts:
        draws = jax.random.uniform(jax.random.fold_in(jax.random.fold_in(own_key, 6), axis_at), (parts,), jnp.float32, least / len(cuts), largest / len(cuts))
        level = level * jnp.repeat(jnp.exp(draws), extent[axis_at] // parts).reshape((-1,) + (1,) * (len(extent) - 1 - axis_at))
    return level


def rank_table(count, slope):
    portions = [(1 << 20) // math.isqrt(standing ** slope) + 1 for standing in range(1, count + 1)]
    width = 1 + sum(portions) // (1 << 30)
    return np.cumsum(np.array([max(1, weight // width) for weight in portions]))


def skewed_ids(rng, shape, amount, lean):
    table = rank_table(amount, lean)
    ticket = jax.random.randint(jax.random.fold_in(rng, 1), shape, 0, int(table[amount - 1]))
    grade = jnp.searchsorted(jnp.asarray(table, jnp.int32), ticket, side="right")
    return jax.random.permutation(jax.random.fold_in(rng, 2), amount)[grade].astype(jnp.int32)


def length_profile(count, total, bound, lean):
    weights = [(1 << 20) // math.isqrt(grade ** lean) + 1 for grade in range(2, count + 1)]
    rest, given = total - bound - (count - 1), [1] * (count - 1)
    while rest > 0:
        candidates = [i for i in range(count - 1) if given[i] < bound]
        pool, budget = sum([weights[i] for i in candidates]), rest
        for i in candidates:
            addition = min(bound - given[i], max(1, budget * weights[i] // pool), rest)
            given[i] = given[i] + addition
            rest = rest - addition
    return np.array([bound] + given)


def ragged(key, count, total, most, lean):
    if count == 2:
        one = jax.random.randint(key, (), max(1, total - most), min(most, total - 1) + 1)
        return jnp.stack([one, total - one])
    tallies = jnp.asarray(length_profile(count, total, most, lean), jnp.int32)
    pairs = (count - 1) // 2
    donor, sink = tallies[1:1 + 2 * pairs:2], tallies[2:2 + 2 * pairs:2]
    slack = jnp.minimum(donor - 1, most - sink)
    moved = jax.random.randint(jax.random.fold_in(key, 1), (pairs,), 0, 1 << 20) % (slack + 1)
    tallies = tallies.at[1:1 + 2 * pairs:2].set(donor - moved).at[2:2 + 2 * pairs:2].set(sink + moved)
    return tallies[jax.random.permutation(jax.random.fold_in(key, 2), count)]


def scatter_about(key, shape, width, reach, split=(), held_as=jnp.bfloat16):
    array = jax.random.normal(key, shape, jnp.float32) * width
    if len(split) > 0:
        array = steps_of(key, shape, split, -0.22, 0.18) * array
    return jnp.clip(array, min=-reach, max=reach).astype(held_as)


def setup_inputs(seed: int = 0) -> dict:
    splits = jax.random.split(jax.random.key(seed), 26)
    return {
        "byte_ids": plant(skewed_ids(splits[0], (BYTES,), VOCAB, 2), jax.random.fold_in(splits[0], 3), 0, VOCAB - 1).astype(jnp.int32),
        "doc_patches": ragged(splits[1], SEQS, PATCHES, MOST_PATCHES, 1).astype(jnp.int32),
        "pad_bytes": plant(jax.random.randint(splits[2], (SEQS,), 0, PATCH), jax.random.fold_in(splits[2], 1), 0, PATCH - 1).astype(jnp.int32),
        "byte_table": scatter_about(splits[3], (VOCAB, EMB), 1.0, 6.0, ((0, 32),)),
        "patch_weight": scatter_about(splits[4], (D, D), D ** -0.5, 0.1875, ((0, 32),)),
        "gain_mix": jnp.clip(1.0 + 0.1 * jax.random.normal(splits[5], (D,), jnp.float32), 0.5, 1.5),
        "in_weight": scatter_about(splits[6], (D, IN_W), D ** -0.5, 0.1875, ((0, 32),)),
        "conv_weight": scatter_about(splits[7], (CONV, XBC), 0.5, 3.0, (), jnp.float32),
        "conv_bias": scatter_about(splits[8], (XBC,), 0.3, 2.0, (), jnp.float32),
        "step_bias": jnp.clip(jax.random.uniform(splits[9], (HEADS_M,), jnp.float32, -6.9, -2.25), -6.9, -2.25),
        "log_rate": jnp.clip(jax.random.uniform(splits[10], (HEADS_M,), jnp.float32, 0.0, 2.77), 0.0, 2.77),
        "skip_gain": jnp.clip(jax.random.uniform(splits[11], (HEADS_M,), jnp.float32, 0.5, 1.5), 0.5, 1.5),
        "gated_gain": jnp.clip(1.0 + 0.1 * jax.random.normal(splits[12], (DI,), jnp.float32), 0.5, 1.5),
        "out_weight": scatter_about(splits[13], (DI, D), DI ** -0.5, 0.125, ((0, 32),)),
        "local_weight": scatter_about(splits[14], (EMB, D), EMB ** -0.5, 0.5, ((1, 32),)),
        "gain_attn": jnp.clip(1.0 + 0.1 * jax.random.normal(splits[15], (D,), jnp.float32), 0.5, 1.5),
        "query_weight": scatter_about(splits[16], (D, D), D ** -0.5, 0.1875, ((0, 32),)),
        "key_weight": scatter_about(splits[17], (D, D), D ** -0.5, 0.1875, ((0, 32),)),
        "value_weight": scatter_about(splits[18], (D, D), D ** -0.5, 0.1875, ((0, 32),)),
        "attn_weight": scatter_about(splits[19], (D, D), (D // 8) ** -0.5, 0.5, ((0, 32),)),
        "feed_gain": jnp.clip(1.0 + 0.1 * jax.random.normal(splits[20], (D,), jnp.float32), 0.5, 1.5),
        "gate_weight": scatter_about(splits[21], (D, FF), D ** -0.5, 0.1875, ((0, 4), (1, 8))),
        "up_weight": scatter_about(splits[22], (D, FF), D ** -0.5, 0.1875, ((0, 4), (1, 8))),
        "down_weight": scatter_about(splits[23], (FF, D), FF ** -0.5, 0.09375, ((0, 8), (1, 4))),
        "cotangent": scatter_about(splits[24], (BYTES, D), 1.0, 6.0, ((0, 32),)),
    }


@jax.custom_vjp
def low(v):
    return lax.optimization_barrier(v.astype(jnp.bfloat16)).astype(jnp.float32)

@jax.custom_vjp
def low_back(v):
    return v

def low_keep(v):
    return (low(v), None)

def low_pass(kept, grad):
    return (grad,)

def back_keep(v):
    return (v, None)

def back_low(kept, grad):
    return (low(grad),)
low.defvjp(low_keep, low_pass)
low_back.defvjp(back_keep, back_low)
epsilon = 1e-05
highest = lax.Precision.HIGHEST
masked_score = -1e+30

def product(first_op, second_op):
    return jnp.dot(first_op, second_op, precision=highest)

def root_norm(values, gain):
    return values * lax.rsqrt(lax.optimization_barrier(jnp.mean(values * values, axis=-1, keepdims=True)) + epsilon) * gain

def doc_layout(doc_patches, pad_bytes):
    doc_ends = jnp.cumsum(doc_patches).astype(jnp.int32)
    patch_index = jnp.arange(PATCHES, dtype=jnp.int32)
    doc_index = jnp.arange(SEQS, dtype=jnp.int32)
    segment = lax.optimization_barrier(jnp.sum((patch_index[:, None] >= doc_ends[None, :]).astype(jnp.int32), axis=1))
    owner_mask = segment[:, None] == doc_index[None, :]
    last_end = lax.optimization_barrier(jnp.sum(jnp.where(owner_mask, doc_ends[None, :] - 1, 0), axis=1))
    pad_count = lax.optimization_barrier(jnp.sum(jnp.where(owner_mask, pad_bytes[None, :], 0), axis=1))
    first_patch = jnp.concatenate([jnp.ones((1,), jnp.int32), (segment[1:] != segment[:-1]).astype(jnp.int32)])
    offset = jnp.arange(PATCH, dtype=jnp.int32)
    padded = (patch_index == last_end)[:, None] & (offset[None, :] >= PATCH - pad_count[:, None])
    keep_mask = 1.0 - padded.astype(jnp.float32).reshape(BYTES)
    return (segment, first_patch, keep_mask)

def ssd_block(skip_gain, state_in, inputs):
    values, input_map, output_map, time_steps, log_decay, segment, first_patch = inputs
    block_len = values.shape[0]
    cumulative = jnp.cumsum(log_decay, axis=0)
    position = jnp.arange(block_len)
    visible = (segment[:, None] == segment[None, :]) & (position[:, None] >= position[None, :])
    log_gap = jnp.where(visible[:, :, None], cumulative[:, None, :] - cumulative[None, :, :], 0.0)
    weight = jnp.exp(log_gap) * visible[:, :, None].astype(jnp.float32) * time_steps[None, :, :] * product(output_map, input_map.T)[:, :, None]
    within = jnp.einsum('tsh,shp->thp', weight, values, precision=highest)
    no_reset = (jnp.cumsum(first_patch) == 0).astype(jnp.float32)
    carried_in = jnp.einsum('tn,hpn->thp', output_map, state_in, precision=highest) * (jnp.exp(cumulative) * no_reset[:, None])[:, :, None]
    result = within + carried_in + skip_gain[None, :, None] * values
    decay_tail = jnp.exp(cumulative[-1][None, :] - cumulative) * (segment == segment[-1]).astype(jnp.float32)[:, None] * time_steps
    fresh_state = jnp.einsum('sh,shp,sn->hpn', decay_tail, values, input_map, precision=highest)
    carried = state_in * (jnp.exp(cumulative[-1]) * no_reset[-1])[:, None, None]
    return (carried + fresh_state, result)

def local_block(weights, stream):
    gain_attn, query_weight, key_weight, value_weight, attn_weight, feed_gain, gate_weight, up_weight, down_weight = weights
    head_shape = (-1, PATCH, HEADS_A, HEAD_A)
    normed = low(root_norm(stream, gain_attn))
    queries = low_back(low(product(normed, query_weight))).reshape(head_shape)
    key_rows = low_back(low(product(normed, key_weight))).reshape(head_shape)
    value_rows = low_back(low(product(normed, value_weight))).reshape(head_shape)
    scores = low_back(jnp.einsum('pqhe,pkhe->phqk', queries, key_rows, precision=highest) * HEAD_A ** (-0.5))
    position = jnp.arange(PATCH)
    causal = position[:, None] >= position[None, :]
    scores = jnp.where(causal, scores, masked_score)
    attn_probs = low(jax.nn.softmax(scores, axis=-1))
    mixed_heads = low_back(low(jnp.einsum('phqk,pkhe->pqhe', attn_probs, value_rows, precision=highest))).reshape(-1, D)
    after_attn = stream + low_back(product(mixed_heads, attn_weight))
    normed_feed = low_back(low(root_norm(after_attn, feed_gain)))
    slice_width = D // N_NARROW
    gate_sum = jnp.zeros((stream.shape[0], FF), stream.dtype)
    up_sum = jnp.zeros((stream.shape[0], FF), stream.dtype)
    for narrow_index in range(N_NARROW):
        lower = narrow_index * slice_width
        gate_sum = gate_sum + low(product(normed_feed[:, lower:lower + slice_width], gate_weight[lower:lower + slice_width]))
        up_sum = up_sum + low(product(normed_feed[:, lower:lower + slice_width], up_weight[lower:lower + slice_width]))
    hidden = low(jax.nn.silu(low_back(gate_sum)) * low_back(up_sum))
    down_parts = []
    for narrow_index in range(N_NARROW):
        lower = narrow_index * slice_width
        down_parts.append(product(low_back(hidden), down_weight[:, lower:lower + slice_width]))
    down_rows = jnp.concatenate(down_parts, axis=1)
    return after_attn + low_back(low(down_rows))

def forward(onehot, keep_mask, segment, first_patch, byte_table, patch_weight, gain_mix, in_weight, conv_weight, conv_bias, step_bias, log_rate, skip_gain, gated_gain, out_weight, local_weight, gain_attn, query_weight, key_weight, value_weight, attn_weight, feed_gain, gate_weight, up_weight, down_weight):
    embedded = (product(onehot, byte_table) * keep_mask[:, None]).reshape(PATCHES, D)
    mixed_in = low_back(product(embedded, patch_weight))
    normed_mix = low(root_norm(mixed_in, gain_mix))
    projected = low_back(low(product(normed_mix, in_weight)))
    conv_in = projected[:, DI:2 * DI + 2 * STATE]
    leading = jnp.zeros((CONV - 1, XBC), conv_in.dtype)
    padded = jnp.concatenate([leading, conv_in], 0)
    padded_seg = jnp.concatenate([jnp.full((CONV - 1,), -1, jnp.int32), segment])
    conv_sum = conv_bias
    for conv_tap in range(CONV):
        same_doc = (padded_seg[conv_tap:conv_tap + PATCHES] == segment).astype(conv_in.dtype)[:, None]
        conv_sum = conv_sum + conv_weight[conv_tap] * padded[conv_tap:conv_tap + PATCHES] * same_doc
    activated = jax.nn.silu(conv_sum)
    values = activated[:, :DI].reshape(PATCHES, HEADS_M, HEAD_M)
    input_map = activated[:, DI:DI + STATE]
    output_map = activated[:, DI + STATE:]
    time_steps = jax.nn.softplus(projected[:, 2 * DI + 2 * STATE:] + step_bias)
    log_decay = -time_steps * jnp.exp(log_rate)
    blocks = PATCHES // 64
    inputs = (values.reshape(blocks, 64, HEADS_M, HEAD_M), input_map.reshape(blocks, 64, STATE), output_map.reshape(blocks, 64, STATE), time_steps.reshape(blocks, 64, HEADS_M), log_decay.reshape(blocks, 64, HEADS_M), segment.reshape(blocks, 64), first_patch.reshape(blocks, 64))
    zero_state = jnp.zeros((HEADS_M, HEAD_M, STATE), values.dtype)
    final_state, results = lax.scan(jax.checkpoint(partial(ssd_block, skip_gain)), zero_state, inputs)
    gated_rows = results.reshape(PATCHES, DI) * jax.nn.silu(projected[:, :DI])
    gated_norm = low(root_norm(gated_rows, gated_gain))
    global_out = mixed_in + low_back(product(gated_norm, out_weight))
    local_rows = low(global_out).reshape(BYTES, EMB)
    stream = low_back(product(local_rows, local_weight))
    block_fn = jax.checkpoint(partial(local_block, (gain_attn, query_weight, key_weight, value_weight, attn_weight, feed_gain, gate_weight, up_weight, down_weight)))
    final_rows = lax.map(block_fn, stream.reshape(BYTES // 512, 512, D)).reshape(BYTES, D)
    return final_rows * keep_mask[:, None]

def reference(byte_ids, doc_patches, pad_bytes, byte_table, patch_weight, gain_mix, in_weight, conv_weight, conv_bias, step_bias, log_rate, skip_gain, gated_gain, out_weight, local_weight, gain_attn, query_weight, key_weight, value_weight, attn_weight, feed_gain, gate_weight, up_weight, down_weight, cotangent):
    segment, first_patch, keep_mask = doc_layout(doc_patches, pad_bytes)
    onehot = (byte_ids[:, None] == jnp.arange(VOCAB, dtype=jnp.int32)[None, :]).astype(jnp.float32)
    final_rows, pullback = jax.vjp(partial(forward, onehot, keep_mask, segment, first_patch), byte_table.astype(jnp.float32), patch_weight.astype(jnp.float32), gain_mix.astype(jnp.float32), in_weight.astype(jnp.float32), conv_weight.astype(jnp.float32), conv_bias.astype(jnp.float32), step_bias.astype(jnp.float32), log_rate.astype(jnp.float32), skip_gain.astype(jnp.float32), gated_gain.astype(jnp.float32), out_weight.astype(jnp.float32), local_weight.astype(jnp.float32), gain_attn.astype(jnp.float32), query_weight.astype(jnp.float32), key_weight.astype(jnp.float32), value_weight.astype(jnp.float32), attn_weight.astype(jnp.float32), feed_gain.astype(jnp.float32), gate_weight.astype(jnp.float32), up_weight.astype(jnp.float32), down_weight.astype(jnp.float32))
    grads = pullback(cotangent.astype(jnp.float32))
    return (final_rows.astype(jnp.bfloat16), grads[0], grads[1], grads[2], grads[3], grads[4], grads[5], grads[6], grads[7], grads[8], grads[9], grads[10], grads[11], grads[12], grads[13], grads[14], grads[15], grads[16], grads[17], grads[18], grads[19], grads[20])
```

```python
from functools import partial

import jax
import jax.numpy as jnp
from jax import lax
from jax.experimental import pallas as pl
from jax.experimental.pallas import tpu as pltpu
from jax.sharding import PartitionSpec as P

D = 1024
PATCH = 8
EMB = 128
VOCAB = 256
HEADS_M = 32
HEAD_M = 64
DI = 2048
STATE = 128
CONV = 4
HEADS_A = 16
HEAD_A = 64


epsilon = 1e-05
highest = lax.Precision.HIGHEST
masked_score = -1e30


def running_sum(x):
    place = jnp.arange(x.shape[0])
    seen = place[:, None] >= place[None, :]
    if x.ndim == 1:
        return jnp.sum(jnp.where(seen, x[None, :], 0), axis=1).astype(x.dtype)
    return jnp.dot(seen.astype(x.dtype), x, precision=highest)


def passed_along(x, axis, by):
    peers = lax.axis_size(axis)
    pairs = [(i, i + by) for i in range(peers) if 0 <= i + by < peers]
    return lax.ppermute(x, axis, pairs)


def prefix_2(x, axis, join, neutral):
    place = lax.axis_index(axis)
    gathered = jax.tree.map(
        lambda a, kind: lax.all_gather(a.astype(kind), axis), x, (jnp.bfloat16, jnp.bfloat16)
    )
    state = jax.tree.map(lambda a, e: jnp.zeros_like(a) + jnp.asarray(e, a.dtype), x, neutral)

    def prefix_one(hop, state):
        return join(
            state,
            jax.tree.map(
                lambda a, own: lax.dynamic_index_in_dim(a, hop, 0, False).astype(own.dtype),
                gathered,
                x,
            ),
        )

    return lax.fori_loop(0, place, prefix_one, state)


def carried_in_2(x, axis, join, neutral):
    count = lax.axis_size(axis)
    place = lax.axis_index(axis)
    ahead = count - 1 - place
    gathered = jax.tree.map(
        lambda a, kind: lax.all_gather(a.astype(kind), axis),
        x,
        jax.tree.map(lambda a: jnp.bfloat16 if a.dtype == jnp.float32 else a.dtype, x),
    )
    state = jax.tree.map(lambda a, e: jnp.zeros_like(a) + jnp.asarray(e, a.dtype), x, neutral)

    def carried_one(hop, state):
        source = count - 1 - hop
        return join(
            state,
            jax.tree.map(
                lambda a, own: lax.dynamic_index_in_dim(a, source, 0, False).astype(own.dtype),
                gathered,
                x,
            ),
        )

    return lax.fori_loop(0, ahead, carried_one, state)


def root_norm(values, gain):
    return values * lax.rsqrt(jnp.mean(values * values, axis=-1, keepdims=True) + epsilon) * gain


def patch_layout(doc_patches, pad_bytes, first_index, patch_count):
    patch_index = first_index + jnp.arange(patch_count, dtype=jnp.int32)
    doc_ends = running_sum(doc_patches)
    doc_index = jnp.arange(doc_patches.shape[0], dtype=jnp.int32)
    segment = jnp.sum((patch_index[:, None] >= doc_ends[None, :]).astype(jnp.int32), axis=1)
    owner_mask = segment[:, None] == doc_index[None, :]
    last_end = jnp.sum(jnp.where(owner_mask, doc_ends[None, :] - 1, 0), axis=1)
    doc_starts = jnp.sum(jnp.where(owner_mask, (doc_ends - doc_patches)[None, :], 0), axis=1)
    pad_count = jnp.sum(jnp.where(owner_mask, pad_bytes[None, :], 0), axis=1)
    offset = jnp.arange(PATCH, dtype=jnp.int32)
    padded = (patch_index == last_end)[:, None] & (offset[None, :] >= PATCH - pad_count[:, None])
    keep_mask = 1.0 - padded.astype(jnp.float32).reshape(-1)
    return (segment, (patch_index == doc_starts).astype(jnp.int32), keep_mask)


def ssd_terms(layout, projected, rim_rows, small_params):
    conv_weight, conv_bias, step_bias, log_rate, skip_gain = small_params
    segment, rim_segment, first_patch = layout
    conv_in = projected[:, DI : 2 * DI + 2 * STATE]
    patch_count = conv_in.shape[0]
    padded = jnp.concatenate([rim_rows, conv_in], 0)
    padded_seg = jnp.concatenate([rim_segment, segment], 0)
    conv_sum = conv_bias
    for conv_tap in range(CONV):
        same_doc = (padded_seg[conv_tap : conv_tap + patch_count] == segment).astype(jnp.float32)[
            :, None
        ]
        conv_sum = (
            conv_sum + conv_weight[conv_tap] * padded[conv_tap : conv_tap + patch_count] * same_doc
        )
    activated = jax.nn.silu(conv_sum)
    values = activated[:, :DI].reshape(patch_count, HEADS_M, HEAD_M)
    input_map = activated[:, DI : DI + STATE]
    output_map = activated[:, DI + STATE :]
    time_steps = jax.nn.softplus(projected[:, 2 * DI + 2 * STATE :] + step_bias)
    cumulative = running_sum(-time_steps * jnp.exp(log_rate))
    no_reset = (running_sum(first_patch) == 0).astype(jnp.float32)
    return (values, input_map, output_map, time_steps, cumulative, no_reset)


def local_state(layout, projected, rim_rows, small_params):
    values, input_map, output_map, time_steps, cumulative, no_reset = ssd_terms(
        layout, projected, rim_rows, small_params
    )
    segment = layout[0]
    decay_tail = (
        jnp.exp(cumulative[-1][None, :] - cumulative)
        * (segment == segment[-1]).astype(jnp.float32)[:, None]
        * time_steps
    )
    state_local = jnp.einsum("sh,shp,sn->hpn", decay_tail, values, input_map, precision=highest)
    decay_total = jnp.exp(cumulative[-1]) * no_reset[-1]
    return (decay_total, state_local)


def mixer_output(layout, projected, rim_rows, small_params, incoming, gated_gain):
    values, input_map, output_map, time_steps, cumulative, no_reset = ssd_terms(
        layout, projected, rim_rows, small_params
    )
    segment = layout[0]
    patch_count = values.shape[0]
    position = jnp.arange(patch_count)
    visible = (segment[:, None] == segment[None, :]) & (position[:, None] >= position[None, :])
    log_gap = jnp.where(visible[:, :, None], cumulative[:, None, :] - cumulative[None, :, :], 0.0)
    inner = jnp.dot(output_map, input_map.T, precision=highest)
    weight = (
        jnp.exp(log_gap)
        * visible[:, :, None].astype(jnp.float32)
        * time_steps[None, :, :]
        * inner[:, :, None]
    )
    within = jnp.einsum("tsh,shp->thp", weight, values, precision=highest)
    carried_in = (
        jnp.einsum("tn,hpn->thp", output_map, incoming, precision=highest)
        * (jnp.exp(cumulative) * no_reset[:, None])[:, :, None]
    )
    result = (within + carried_in + small_params[4][None, :, None] * values).reshape(
        patch_count, DI
    )
    gated_rows = result * jax.nn.silu(projected[:, :DI])
    return root_norm(gated_rows, gated_gain)


def combine_states(earlier, following):
    return (earlier[0] * following[0], following[0][:, None, None] * earlier[1] + following[1])


def attend(stream, gain_attn, query_all, key_all, value_all):
    head_shape = (-1, PATCH, HEADS_A, HEAD_A)
    normed_attn = root_norm(stream, gain_attn).astype(jnp.bfloat16)
    queries = jnp.dot(normed_attn, query_all, preferred_element_type=jnp.float32).astype(
        jnp.bfloat16
    )
    key_rows = jnp.dot(normed_attn, key_all, preferred_element_type=jnp.float32).astype(
        jnp.bfloat16
    )
    value_rows = jnp.dot(normed_attn, value_all, preferred_element_type=jnp.float32).astype(
        jnp.bfloat16
    )
    scores = jnp.einsum(
        "pqhe,pkhe->phqk",
        queries.reshape(head_shape),
        key_rows.reshape(head_shape),
        preferred_element_type=jnp.float32,
    ) * HEAD_A ** (-0.5)
    position = jnp.arange(PATCH)
    causal = position[:, None] >= position[None, :]
    attn_probs = jax.nn.softmax(jnp.where(causal, scores, masked_score), axis=-1)
    mixed_heads = jnp.einsum(
        "phqk,pkhe->pqhe",
        attn_probs.astype(jnp.bfloat16),
        value_rows.reshape(head_shape),
        preferred_element_type=jnp.float32,
    )
    mixed_heads = mixed_heads.reshape(stream.shape[0], -1).astype(jnp.bfloat16)
    return (normed_attn, queries, key_rows, value_rows, attn_probs, mixed_heads)


def spread(values):
    by_rows = lax.all_to_all(values, "narrow", split_axis=1, concat_axis=0, tiled=True)
    return lax.all_gather(by_rows, "wide", axis=0, tiled=True)


def collect(term_fn, row_count):
    summed = lax.psum_scatter(
        term_fn(jnp.int32(0), row_count * lax.axis_size("wide")).astype(jnp.bfloat16),
        "wide",
        scatter_dimension=0,
        tiled=True,
    )
    return lax.all_to_all(summed, "narrow", split_axis=0, concat_axis=1, tiled=True)


def narrow_total(partial_rows):
    return lax.psum(partial_rows, "narrow").astype(jnp.float32)


def silu_back(gate_up, hidden_grad, hidden_width):
    gate_rows = gate_up[:, :hidden_width]
    up_rows = gate_up[:, hidden_width:]
    sigmoid = jax.nn.sigmoid(gate_rows)
    gate_grad = hidden_grad * up_rows * sigmoid * (1.0 + gate_rows * (1.0 - sigmoid))
    up_grad = hidden_grad * gate_rows * sigmoid
    return jnp.concatenate([gate_grad, up_grad], axis=1)


def per_device_rows(
    byte_ids,
    doc_patches,
    pad_bytes,
    byte_table,
    patch_weight,
    gain_mix,
    in_weight,
    conv_weight,
    conv_bias,
    step_bias,
    log_rate,
    skip_gain,
    gated_gain,
    out_weight,
    local_weight,
    gain_attn,
    query_weight,
    key_weight,
    value_weight,
    attn_weight,
    feed_gain,
    gate_weight,
    up_weight,
    down_weight,
    cotangent,
):
    byte_rows = byte_ids.shape[0]
    patches = byte_rows // PATCH
    device = lax.axis_index(("narrow", "wide"))
    wide_count = lax.axis_size("wide")
    segment, first_patch, keep_mask = patch_layout(
        doc_patches, pad_bytes, device * patches, patches
    )
    rim_segment = patch_layout(doc_patches, pad_bytes, device * patches - (CONV - 1), CONV - 1)[0]
    layout = (segment, rim_segment, first_patch)
    gathered = (
        lax.all_gather(byte_table, ("narrow", "wide"), axis=0, tiled=True),
        lax.all_gather(patch_weight, ("narrow", "wide"), axis=0, tiled=True),
        lax.all_gather(in_weight, ("narrow", "wide"), axis=0, tiled=True),
        lax.all_gather(out_weight, ("narrow", "wide"), axis=0, tiled=True),
        lax.all_gather(local_weight, ("narrow", "wide"), axis=1, tiled=True),
        lax.all_gather(query_weight, ("narrow", "wide"), axis=0, tiled=True),
        lax.all_gather(key_weight, ("narrow", "wide"), axis=0, tiled=True),
        lax.all_gather(value_weight, ("narrow", "wide"), axis=0, tiled=True),
        lax.all_gather(attn_weight, ("narrow", "wide"), axis=0, tiled=True),
    )
    table_all, patch_all, in_all, out_all, local_all, query_all, key_all, value_all, attn_all = (
        gathered
    )
    onehot = (byte_ids[:, None] == jnp.arange(VOCAB, dtype=jnp.int32)[None, :]).astype(jnp.bfloat16)
    embedded = (
        (jnp.dot(onehot, table_all, preferred_element_type=jnp.float32) * keep_mask[:, None])
        .astype(jnp.bfloat16)
        .reshape(patches, D)
    )
    mixed_in = jnp.dot(embedded, patch_all, preferred_element_type=jnp.float32)
    normed_mix = root_norm(mixed_in, gain_mix).astype(jnp.bfloat16)
    projected = jnp.dot(normed_mix, in_all, preferred_element_type=jnp.float32).astype(jnp.bfloat16)
    rim_rows = passed_along(
        projected[patches - (CONV - 1) :, DI : 2 * DI + 2 * STATE], ("narrow", "wide"), 1
    ).astype(jnp.float32)
    projected_f = projected.astype(jnp.float32)
    small_params = (conv_weight, conv_bias, step_bias, log_rate, skip_gain)
    (decay_total, state_local), state_back = jax.vjp(
        partial(local_state, layout), projected_f, rim_rows, small_params
    )
    prefix = prefix_2(
        (decay_total, state_local),
        ("narrow", "wide"),
        combine_states,
        (jnp.ones_like(decay_total), jnp.zeros_like(state_local)),
    )
    incoming = prefix[1]
    gated_norm, mixer_back = jax.vjp(
        partial(mixer_output, layout), projected_f, rim_rows, small_params, incoming, gated_gain
    )
    gated_low = gated_norm.astype(jnp.bfloat16)
    global_out = mixed_in + jnp.dot(gated_low, out_all, preferred_element_type=jnp.float32)
    local_rows = global_out.astype(jnp.bfloat16).reshape(byte_rows, EMB)
    stream = jnp.dot(local_rows, local_all, preferred_element_type=jnp.float32)
    normed_attn, queries, key_rows, value_rows, attn_probs, mixed_heads = attend(
        stream, gain_attn, query_all, key_all, value_all
    )
    after_attn = stream + jnp.dot(mixed_heads, attn_all, preferred_element_type=jnp.float32)
    normed_feed = root_norm(after_attn, feed_gain).astype(jnp.bfloat16)
    out_grad = cotangent.astype(jnp.float32) * keep_mask[:, None]
    feed_grad = out_grad.astype(jnp.bfloat16)
    grid_in = spread(normed_feed)
    both_weights = jnp.concatenate([gate_weight, up_weight], axis=1)
    hidden_width = gate_weight.shape[1]
    grid_share = grid_in.shape[0] // wide_count
    gate_up_part = jnp.dot(grid_in, both_weights, preferred_element_type=jnp.float32).astype(
        jnp.bfloat16
    )
    gate_up = narrow_total(gate_up_part)
    hidden = (jax.nn.silu(gate_up[:, :hidden_width]) * gate_up[:, hidden_width:]).astype(
        jnp.bfloat16
    )

    def down_term(first_row, row_count):
        return jnp.dot(hidden, down_weight, preferred_element_type=jnp.float32)

    feed_out = collect(down_term, grid_share)
    grid_grad = spread(feed_grad)
    grad_down = jnp.einsum("gf,gd->fd", hidden, grid_grad, preferred_element_type=jnp.float32)
    hidden_part = jnp.einsum(
        "gd,fd->gf", grid_grad, down_weight, preferred_element_type=jnp.float32
    ).astype(jnp.bfloat16)
    hidden_grad = narrow_total(hidden_part)
    gate_up_grad = silu_back(gate_up, hidden_grad, hidden_width).astype(jnp.bfloat16)
    grad_both = jnp.einsum("gd,gf->df", grid_in, gate_up_grad, preferred_element_type=jnp.float32)

    def back_term(first_row, row_count):
        return jnp.einsum(
            "gf,df->gd", gate_up_grad, both_weights, preferred_element_type=jnp.float32
        )

    feed_in_grad = collect(back_term, grid_share)
    grad_gate = grad_both[:, :hidden_width]
    grad_up = grad_both[:, hidden_width:]
    after_feed = after_attn + feed_out.astype(jnp.float32)
    out_rows = (after_feed * keep_mask[:, None]).astype(jnp.bfloat16)
    feed_normed, feed_norm_back = jax.vjp(root_norm, after_attn, feed_gain)
    after_norm_grad, grad_feed_gain = feed_norm_back(feed_in_grad.astype(jnp.float32))
    after_grad = out_grad + after_norm_grad
    head_shape = (-1, PATCH, HEADS_A, HEAD_A)
    score_scale = HEAD_A ** (-0.5)
    attn_grad = after_grad.astype(jnp.bfloat16)
    grad_attn = jnp.einsum("rd,re->de", mixed_heads, attn_grad, preferred_element_type=jnp.float32)
    heads_grad = (
        jnp.einsum("re,de->rd", attn_grad, attn_all, preferred_element_type=jnp.float32)
        .astype(jnp.bfloat16)
        .reshape(head_shape)
    )
    probs_grad = jnp.einsum(
        "pqhe,pkhe->phqk",
        heads_grad,
        value_rows.reshape(head_shape),
        preferred_element_type=jnp.float32,
    )
    value_grad = (
        jnp.einsum(
            "phqk,pqhe->pkhe",
            attn_probs.astype(jnp.bfloat16),
            heads_grad,
            preferred_element_type=jnp.float32,
        )
        .reshape(byte_rows, D)
        .astype(jnp.bfloat16)
    )
    score_grad = (
        attn_probs * (probs_grad - jnp.sum(attn_probs * probs_grad, axis=-1, keepdims=True))
    ).astype(jnp.bfloat16)
    query_grad = (
        (
            jnp.einsum(
                "phqk,pkhe->pqhe",
                score_grad,
                key_rows.reshape(head_shape),
                preferred_element_type=jnp.float32,
            )
            * score_scale
        )
        .reshape(byte_rows, D)
        .astype(jnp.bfloat16)
    )
    key_grad = (
        (
            jnp.einsum(
                "phqk,pqhe->pkhe",
                score_grad,
                queries.reshape(head_shape),
                preferred_element_type=jnp.float32,
            )
            * score_scale
        )
        .reshape(byte_rows, D)
        .astype(jnp.bfloat16)
    )
    grad_query = jnp.einsum(
        "rd,re->de", normed_attn, query_grad, preferred_element_type=jnp.float32
    )
    grad_key = jnp.einsum("rd,re->de", normed_attn, key_grad, preferred_element_type=jnp.float32)
    grad_value = jnp.einsum(
        "rd,re->de", normed_attn, value_grad, preferred_element_type=jnp.float32
    )
    normed_grad = jnp.einsum("re,de->rd", query_grad, query_all, preferred_element_type=jnp.float32)
    normed_grad = normed_grad + jnp.einsum(
        "re,de->rd", key_grad, key_all, preferred_element_type=jnp.float32
    )
    normed_grad = normed_grad + jnp.einsum(
        "re,de->rd", value_grad, value_all, preferred_element_type=jnp.float32
    )
    attn_normed, attn_norm_back = jax.vjp(root_norm, stream, gain_attn)
    stream_norm_grad, grad_gain_attn = attn_norm_back(normed_grad)
    stream_grad = (after_grad + stream_norm_grad).astype(jnp.bfloat16)
    grad_local = jnp.einsum(
        "re,rd->ed", local_rows, stream_grad, preferred_element_type=jnp.float32
    )
    global_grad = jnp.einsum(
        "rd,ed->re", stream_grad, local_all, preferred_element_type=jnp.float32
    ).reshape(patches, D)
    mix_grad = global_grad.astype(jnp.bfloat16)
    grad_out = jnp.einsum("pi,pd->id", gated_low, mix_grad, preferred_element_type=jnp.float32)
    gated_grad = jnp.einsum("pd,id->pi", mix_grad, out_all, preferred_element_type=jnp.float32)
    proj_grad_mix, rim_grad_mix, small_grad_mix, incoming_grad, grad_gated_gain = mixer_back(
        gated_grad
    )
    suffix = carried_in_2(
        (decay_total, incoming_grad),
        ("narrow", "wide"),
        combine_states,
        (jnp.ones_like(decay_total), jnp.zeros_like(incoming_grad)),
    )
    later_grad = suffix[1]
    decay_grad = jnp.sum(later_grad * incoming, axis=(1, 2))
    proj_grad_state, rim_grad_state, small_grad_state = state_back((decay_grad, later_grad))
    rim_from_next = passed_along(rim_grad_mix + rim_grad_state, ("narrow", "wide"), -1)
    proj_grad = proj_grad_mix + proj_grad_state
    proj_grad = proj_grad.at[patches - (CONV - 1) :, DI : 2 * DI + 2 * STATE].add(rim_from_next)
    proj_low = proj_grad.astype(jnp.bfloat16)
    grad_in = jnp.einsum("pd,pk->dk", normed_mix, proj_low, preferred_element_type=jnp.float32)
    normed_mix_grad = jnp.einsum("pk,dk->pd", proj_low, in_all, preferred_element_type=jnp.float32)
    mix_normed, mix_norm_back = jax.vjp(root_norm, mixed_in, gain_mix)
    mixed_norm_grad, grad_gain_mix = mix_norm_back(normed_mix_grad)
    embed_grad = (global_grad + mixed_norm_grad).astype(jnp.bfloat16)
    grad_patch = jnp.einsum("pi,pd->id", embedded, embed_grad, preferred_element_type=jnp.float32)
    byte_grad = (
        jnp.einsum("pd,id->pi", embed_grad, patch_all, preferred_element_type=jnp.float32).reshape(
            byte_rows, EMB
        )
        * keep_mask[:, None]
    )
    grad_table = jnp.dot(onehot.astype(jnp.float32).T, byte_grad, precision=highest)
    shared = (
        lax.psum_scatter(grad_table, ("narrow", "wide"), scatter_dimension=0, tiled=True),
        lax.psum_scatter(grad_patch, ("narrow", "wide"), scatter_dimension=0, tiled=True),
        lax.psum_scatter(grad_in, ("narrow", "wide"), scatter_dimension=0, tiled=True),
        lax.psum_scatter(grad_out, ("narrow", "wide"), scatter_dimension=0, tiled=True),
        lax.psum_scatter(grad_local, ("narrow", "wide"), scatter_dimension=1, tiled=True),
        lax.psum_scatter(grad_query, ("narrow", "wide"), scatter_dimension=0, tiled=True),
        lax.psum_scatter(grad_key, ("narrow", "wide"), scatter_dimension=0, tiled=True),
        lax.psum_scatter(grad_value, ("narrow", "wide"), scatter_dimension=0, tiled=True),
        lax.psum_scatter(grad_attn, ("narrow", "wide"), scatter_dimension=0, tiled=True),
    )
    small_sum = lax.psum(
        (
            small_grad_mix[0] + small_grad_state[0],
            small_grad_mix[1] + small_grad_state[1],
            small_grad_mix[2] + small_grad_state[2],
            small_grad_mix[3] + small_grad_state[3],
            small_grad_mix[4] + small_grad_state[4],
            grad_gain_mix,
            grad_gated_gain,
            grad_gain_attn,
            grad_feed_gain,
        ),
        ("narrow", "wide"),
    )
    return (
        out_rows,
        shared[0],
        shared[1],
        small_sum[5],
        shared[2],
        small_sum[0],
        small_sum[1],
        small_sum[2],
        small_sum[3],
        small_sum[4],
        small_sum[6],
        shared[3],
        shared[4],
        small_sum[7],
        shared[5],
        shared[6],
        shared[7],
        shared[8],
        small_sum[8],
        grad_gate,
        grad_up,
        grad_down,
    )


QUERY = 128
BYTE_BLOCK = 128
MESH = pl.DeviceIdType.MESH
LOW = jnp.bfloat16
FULL = jnp.float32
BOTH = ("narrow", "wide")


def nn(a, b, precision=None):
    return lax.dot_general(
        a, b, (((1,), (0,)), ((), ())), precision=precision, preferred_element_type=FULL
    )


def nt(a, b, precision=None):
    return lax.dot_general(
        a, b, (((1,), (1,)), ((), ())), precision=precision, preferred_element_type=FULL
    )


def tn(a, b, precision=None):
    return lax.dot_general(
        a, b, (((0,), (0,)), ((), ())), precision=precision, preferred_element_type=FULL
    )


def gather_kernel(count, narrow, depth, *refs):
    ins, outs = refs[:count], refs[count : 2 * count]
    local, z_send, z_recv, n_send, n_recv, c_send, c_recv = refs[2 * count :]
    n, w = lax.axis_index("narrow"), lax.axis_index("wide")
    z, c = lax.div(w, 2), lax.rem(w, 2)
    z_peers = [(n, lax.rem(z + k, depth) * 2 + c) for k in range(1, depth)]
    n_peers = [lax.rem(n + k, narrow) for k in range(1, narrow)]
    twin = (n, z * 2 + 1 - c)
    barrier = pltpu.get_barrier_semaphore()
    for peer in z_peers:
        pl.semaphore_signal(barrier, inc=1, device_id=peer, device_id_type=MESH)
    for m in n_peers:
        pl.semaphore_signal(barrier, inc=1, device_id=(m, w), device_id_type=MESH)
    pl.semaphore_signal(barrier, inc=1, device_id=twin, device_id_type=MESH)
    pl.semaphore_wait(barrier, len(z_peers) + len(n_peers) + 1)

    def remote(src, dst, send, recv, peer):
        return pltpu.make_async_remote_copy(
            src_ref=src, dst_ref=dst, send_sem=send, recv_sem=recv, device_id=peer, device_id_type=MESH
        )

    own = [pltpu.make_async_copy(ins[i], outs[i].at[n, z, c], local.at[i]) for i in range(count)]
    for i in range(count):
        own[i].start()
        for peer in z_peers:
            remote(ins[i], outs[i].at[n, z, c], z_send.at[i], z_recv.at[i], peer).start()
    for i in range(count):
        own[i].wait()
        part = outs[i].at[n, pl.ds(0, depth - 1), c]
        remote(part, part, z_send.at[i], z_recv.at[i], twin).wait_recv()
        mine = outs[i].at[n, :, c]
        for m in n_peers:
            remote(mine, mine, n_send.at[i], n_recv.at[i], (m, w)).start()
        remote(mine, mine, c_send.at[i], c_recv.at[i], twin).start()
    for i in range(count):
        part = outs[i].at[pl.ds(0, narrow - 1), :, c]
        remote(part, part, n_send.at[i], n_recv.at[i], twin).wait_recv()
        for m in n_peers:
            theirs = outs[i].at[m, :, c]
            remote(theirs, theirs, c_send.at[i], c_recv.at[i], twin).start()
    for i in range(count):
        half = outs[i].at[:, :, 1 - c]
        remote(half, half, c_send.at[i], c_recv.at[i], twin).wait()
        part = outs[i].at[n, pl.ds(0, depth - 1), c]
        remote(part, part, z_send.at[i], z_recv.at[i], twin).wait_send()
        part = outs[i].at[pl.ds(0, narrow - 1), :, c]
        remote(part, part, n_send.at[i], n_recv.at[i], twin).wait_send()


def gather_all(arrays, collective_id):
    narrow, wide = lax.axis_size("narrow"), lax.axis_size("wide")
    count = len(arrays)
    dma = pltpu.SemaphoreType.DMA((count,))
    outs = pl.pallas_call(
        partial(gather_kernel, count, narrow, wide // 2),
        out_shape=[
            jax.ShapeDtypeStruct((narrow, wide // 2, 2) + a.shape, a.dtype) for a in arrays
        ],
        in_specs=[pl.BlockSpec(memory_space=pl.ANY)] * count,
        out_specs=[pl.BlockSpec(memory_space=pl.ANY)] * count,
        scratch_shapes=[dma] * 7,
        compiler_params=pltpu.CompilerParams(collective_id=collective_id, has_side_effects=True),
        name="gather_all",
    )(*arrays)
    return [o.reshape((-1,) + a.shape[1:]) for o, a in zip(outs, arrays)]


def exchange(blocks, axis):
    return lax.all_to_all(blocks, axis, split_axis=0, concat_axis=0, tiled=True)


def softplus(v):
    return jnp.maximum(v, 0.0) + jnp.log1p(jnp.exp(-jnp.abs(v)))


def convolved(window, marks, weight, bias):
    pre = bias + weight[CONV - 1 :] * window[8:]
    for lag in range(1, CONV):
        pre = pre + weight[CONV - 1 - lag : CONV - lag] * (
            window[8 - lag : 8 - lag + QUERY] * marks[:, lag : lag + 1]
        )
    return pre


def decays(marks, dt, step_bias, rate_scale):
    shape = (QUERY, QUERY)
    row = lax.broadcasted_iota(jnp.int32, shape, 0)
    column = lax.broadcasted_iota(jnp.int32, shape, 1)
    lower = (row >= column).astype(FULL)
    segment = jnp.broadcast_to(marks[:, :1], shape)
    visible = (segment == segment.T) & (row >= column)
    delta = jnp.broadcast_to(softplus(dt + step_bias), shape)
    total = nn(lower, -delta * rate_scale, highest)
    gap = jnp.where(visible, total - total.T, 0.0)
    decay = jnp.where(visible, jnp.exp(gap), 0.0)
    last = total[QUERY - 1 :, :]
    begun = jnp.exp(total) * marks[:, 4:5]
    tail = jnp.exp(last - total) * marks[:, 5:6]
    kept = jnp.exp(last) * marks[:1, 6:7]
    return lower, delta, decay, begun, tail, kept


def mixer_forward_kernel(
    numbers, xz, bc, dt, marks, wx, bx, wbc, bbc, u_out, y_out, states, xz_pad, bc_pad, state
):
    count = xz.shape[0]
    xz_pad[pl.ds(0, 8), :] = jnp.zeros((8, xz_pad.shape[1]), FULL)
    bc_pad[pl.ds(0, 8), :] = jnp.zeros((8, bc_pad.shape[1]), FULL)
    state[...] = jnp.zeros_like(state)
    step_bias, rate_scale, skip = numbers[0], numbers[1], numbers[2]

    xz_pad[pl.ds(8, count), :] = xz[...].astype(FULL)
    bc_pad[pl.ds(8, count), :] = bc[...].astype(FULL)

    def block(i, carry):
        start = pl.multiple_of(i * QUERY, QUERY)
        rows = pl.ds(start, QUERY)
        mark = marks[rows, :]
        act_x = jax.nn.silu(convolved(xz_pad[pl.ds(start, QUERY + 8), :], mark, wx[...], bx[...]))
        act = jax.nn.silu(convolved(bc_pad[pl.ds(start, QUERY + 8), :], mark, wbc[...], bbc[...]))
        x, b, c = act_x[:, :HEAD_M], act[:, :STATE], act[:, STATE:]
        lower, delta, decay, begun, tail, kept = decays(mark, dt[rows, :], step_bias, rate_scale)
        weight = nt(c, b, highest) * decay * delta.T
        held = state[...]
        states[i] = held
        y = (
            nn(weight, x, highest)
            + nt(c, held, highest) * begun[:, :HEAD_M]
            + skip * x
        )
        state[...] = held * kept + tn(x * (tail * delta)[:, :HEAD_M], b, highest)
        z = xz[rows, :].astype(FULL)[:, HEAD_M:]
        y_out[rows, :] = y
        u_out[rows, :] = y * jax.nn.silu(z)
        return carry

    lax.fori_loop(0, count // QUERY, block, 0)


def mixer_backward_kernel(
    numbers,
    xz,
    bc,
    dt,
    marks,
    wx,
    bx,
    wbc,
    bbc,
    y_in,
    states,
    du_in,
    dxz,
    dbc,
    ddt,
    dwx,
    dwbc,
    dnumbers,
    xz_pad,
    bc_pad,
    dx_pad,
    dbc_pad,
    dstate,
):
    count = xz.shape[0]
    blocks = count // QUERY
    xz_pad[pl.ds(0, 8), :] = jnp.zeros((8, xz_pad.shape[1]), FULL)
    bc_pad[pl.ds(0, 8), :] = jnp.zeros((8, bc_pad.shape[1]), FULL)
    dx_pad[pl.ds(count, 8), :] = jnp.zeros((8, dx_pad.shape[1]), FULL)
    dbc_pad[pl.ds(count, 8), :] = jnp.zeros((8, dbc_pad.shape[1]), FULL)
    dstate[...] = jnp.zeros_like(dstate)
    dwx[...] = jnp.zeros_like(dwx)
    dwbc[...] = jnp.zeros_like(dwbc)
    dnumbers[...] = jnp.zeros_like(dnumbers)
    step_bias, rate_scale, skip = numbers[0], numbers[1], numbers[2]

    def fill(i, carry):
        start = pl.multiple_of(i * QUERY, QUERY)
        rows = pl.ds(start, QUERY)
        xz_pad[pl.ds(start + 8, QUERY), :] = xz[rows, :].astype(FULL)
        bc_pad[pl.ds(start + 8, QUERY), :] = bc[rows, :].astype(FULL)
        return carry

    lax.fori_loop(0, blocks, fill, 0)

    def slope(pre):
        s = jax.nn.sigmoid(pre)
        return s * (1.0 + pre * (1.0 - s))

    def total(v):
        return jnp.sum(jnp.sum(v, axis=1, keepdims=True), axis=0, keepdims=True)

    def conv_back(pad, start, dpre_pad, dpre, weight, dw):
        mark = marks[pl.ds(start, QUERY), :]
        window = pad[pl.ds(start, QUERY + 8), :]
        later = dpre_pad[pl.ds(start, QUERY + 8), :]
        later_marks = marks[pl.ds(start, QUERY + 8), :]
        out = weight[CONV - 1 :] * dpre
        dw[CONV - 1 : CONV, :] += jnp.sum(dpre * window[8:], axis=0, keepdims=True)
        dw[CONV : CONV + 1, :] += jnp.sum(dpre, axis=0, keepdims=True)
        for lag in range(1, CONV):
            tap = CONV - 1 - lag
            out = out + weight[tap : tap + 1] * (
                (later * later_marks[:, lag : lag + 1])[lag : lag + QUERY]
            )
            dw[tap : tap + 1, :] += jnp.sum(
                dpre * (window[8 - lag : 8 - lag + QUERY] * mark[:, lag : lag + 1]),
                axis=0,
                keepdims=True,
            )
        return out

    def block(k, carry):
        i = blocks - 1 - k
        start = pl.multiple_of(i * QUERY, QUERY)
        rows = pl.ds(start, QUERY)
        mark = marks[rows, :]
        pre_x = convolved(xz_pad[pl.ds(start, QUERY + 8), :], mark, wx[...], bx[...])
        pre = convolved(bc_pad[pl.ds(start, QUERY + 8), :], mark, wbc[...], bbc[...])
        act = jax.nn.silu(pre)
        x, b, c = jax.nn.silu(pre_x)[:, :HEAD_M], act[:, :STATE], act[:, STATE:]
        step = dt[rows, :]
        lower, delta, decay, begun, tail, kept = decays(mark, step, step_bias, rate_scale)
        held, dheld = states[i], dstate[...]
        z = xz[rows, :].astype(FULL)[:, HEAD_M:]
        du, y = du_in[rows, :].astype(FULL), y_in[rows, :]
        dy = du * jax.nn.silu(z)
        dz = du * y * slope(z)
        scores = nt(c, b, highest)
        reach = decay * delta.T
        dweight = nt(dy, x, highest)
        dscores = dweight * reach
        fed = x * (tail * delta)[:, :HEAD_M]
        begun_dy = dy * begun[:, :HEAD_M]
        dc = nn(dscores, b, highest) + nn(begun_dy, held, highest)
        db = tn(dscores, c, highest) + nn(fed, dheld, highest)
        dfed = nt(b, dheld, highest)
        dx = skip * dy + tn(scores * reach, dy, highest) + (tail * delta)[:, :HEAD_M] * dfed
        moved = dweight * scores * decay
        turned = moved.T
        ddelta = jnp.sum(turned, axis=1, keepdims=True)
        dtotal = jnp.sum(moved * delta.T, axis=1, keepdims=True) - ddelta * delta[:, :1]
        dtotal += jnp.sum(begun_dy * nt(c, held, highest), axis=1, keepdims=True)
        dtail = jnp.sum(dfed * x, axis=1, keepdims=True)
        ddelta += dtail * tail[:, :1]
        dtail = dtail * (tail * delta)[:, :1]
        dtotal -= dtail
        dlast = jnp.sum(dtail, axis=0, keepdims=True) + total(dheld * held * kept)
        dlog = tn(lower, jnp.broadcast_to(dtotal, (QUERY, QUERY)), highest)[:, :1] + dlast
        ddelta -= dlog * rate_scale
        dstep = ddelta * jax.nn.sigmoid(step + step_bias)
        ddt[rows, :] = dstep
        dnumbers[0:1, :] += jnp.broadcast_to(jnp.sum(dstep, axis=0, keepdims=True), (1, 128))
        dnumbers[1:2, :] -= jnp.broadcast_to(
            jnp.sum(dlog * delta[:, :1] * rate_scale, axis=0, keepdims=True), (1, 128)
        )
        dnumbers[2:3, :] += jnp.broadcast_to(total(dy * x), (1, 128))
        dstate[...] = dheld * kept + tn(begun_dy, c, highest)
        dpre_x = jnp.concatenate([dx, jnp.zeros_like(dx)], axis=1) * slope(pre_x)
        dpre = jnp.concatenate([db, dc], axis=1) * slope(pre)
        dx_pad[rows, :] = dpre_x
        dbc_pad[rows, :] = dpre
        dxr = conv_back(xz_pad, start, dx_pad, dpre_x, wx[...], dwx)
        dxz[rows, :] = jnp.concatenate([dxr[:, :HEAD_M], dz], axis=1).astype(dxz.dtype)
        dbc[rows, :] = conv_back(bc_pad, start, dbc_pad, dpre, wbc[...], dwbc).astype(dbc.dtype)
        return carry

    lax.fori_loop(0, blocks, block, 0)


def in_smem():
    return pl.BlockSpec(memory_space=pltpu.SMEM)


def in_vmem():
    return pl.BlockSpec(memory_space=pltpu.VMEM)


def mixer_forward(numbers, xz, bc, dt, marks, wx, bx, wbc, bbc):
    count = xz.shape[0]
    return pl.pallas_call(
        mixer_forward_kernel,
        out_shape=[
            jax.ShapeDtypeStruct((count, HEAD_M), FULL),
            jax.ShapeDtypeStruct((count, HEAD_M), FULL),
            jax.ShapeDtypeStruct((count // QUERY, HEAD_M, STATE), FULL),
        ],
        in_specs=[in_smem()] + [in_vmem()] * 8,
        out_specs=[in_vmem()] * 3,
        scratch_shapes=[
            pltpu.VMEM((count + 8, 2 * HEAD_M), FULL),
            pltpu.VMEM((count + 8, 2 * STATE), FULL),
            pltpu.VMEM((HEAD_M, STATE), FULL),
        ],
        compiler_params=pltpu.CompilerParams(vmem_limit_bytes=32 << 20),
        name="mixer_forward",
    )(numbers, xz, bc, dt, marks, wx, bx, wbc, bbc)


def mixer_backward(numbers, xz, bc, dt, marks, wx, bx, wbc, bbc, y, states, du):
    count = xz.shape[0]
    return pl.pallas_call(
        mixer_backward_kernel,
        out_shape=[
            jax.ShapeDtypeStruct((count, 2 * HEAD_M), LOW),
            jax.ShapeDtypeStruct((count, 2 * STATE), LOW),
            jax.ShapeDtypeStruct((count, 1), FULL),
            jax.ShapeDtypeStruct((8, 2 * HEAD_M), FULL),
            jax.ShapeDtypeStruct((8, 2 * STATE), FULL),
            jax.ShapeDtypeStruct((8, 128), FULL),
        ],
        in_specs=[in_smem()] + [in_vmem()] * 11,
        out_specs=[in_vmem()] * 6,
        scratch_shapes=[
            pltpu.VMEM((count + 8, 2 * HEAD_M), FULL),
            pltpu.VMEM((count + 8, 2 * STATE), FULL),
            pltpu.VMEM((count + 8, 2 * HEAD_M), FULL),
            pltpu.VMEM((count + 8, 2 * STATE), FULL),
            pltpu.VMEM((HEAD_M, STATE), FULL),
        ],
        compiler_params=pltpu.CompilerParams(vmem_limit_bytes=32 << 20),
        name="mixer_backward",
    )(numbers, xz, bc, dt, marks, wx, bx, wbc, bbc, y, states, du)


def patch_causal():
    row = lax.broadcasted_iota(jnp.int32, (BYTE_BLOCK, BYTE_BLOCK), 0)
    column = lax.broadcasted_iota(jnp.int32, (BYTE_BLOCK, BYTE_BLOCK), 1)
    return (lax.div(row, PATCH) == lax.div(column, PATCH)) & (row >= column)


def head_probs(q, k, causal):
    scores = jnp.where(causal, nt(q, k) * HEAD_A ** (-0.5), masked_score)
    grown = jnp.exp(scores - jnp.max(scores, axis=1, keepdims=True))
    return grown / jnp.sum(grown, axis=1, keepdims=True)


def of_head(block, half):
    lane = lax.broadcasted_iota(jnp.int32, block.shape, 1)
    return jnp.where(lax.div(lane, HEAD_A) == half, block, jnp.zeros_like(block))


def attend_kernel(q_ref, k_ref, v_ref, out):
    causal = patch_causal()
    for first in range(0, q_ref.shape[0], BYTE_BLOCK):
        rows = pl.ds(first, BYTE_BLOCK)
        q, k, v = q_ref[rows, :], k_ref[rows, :], v_ref[rows, :]
        mixed = jnp.zeros(q.shape, FULL)
        for half in range(2):
            probs = head_probs(of_head(q, half), k, causal)
            mixed += nn(probs.astype(LOW), of_head(v, half))
        out[rows, :] = mixed.astype(LOW)


def attend_back_kernel(q_ref, k_ref, v_ref, g_ref, dq_out, dk_out, dv_out):
    causal = patch_causal()
    scale = HEAD_A ** (-0.5)
    for first in range(0, q_ref.shape[0], BYTE_BLOCK):
        rows = pl.ds(first, BYTE_BLOCK)
        q, k, v, g = q_ref[rows, :], k_ref[rows, :], v_ref[rows, :], g_ref[rows, :]
        dq = jnp.zeros(q.shape, FULL)
        dk = jnp.zeros(q.shape, FULL)
        dv = jnp.zeros(q.shape, FULL)
        for half in range(2):
            own_q, own_k, own_g = of_head(q, half), of_head(k, half), of_head(g, half)
            probs = head_probs(own_q, k, causal)
            dprobs = nt(own_g, v)
            dv += tn(probs.astype(LOW), own_g)
            dscores = probs * (dprobs - jnp.sum(probs * dprobs, axis=1, keepdims=True))
            dscores = dscores.astype(LOW)
            dq += nn(dscores, own_k)
            dk += tn(dscores, own_q)
        dq_out[rows, :] = (dq * scale).astype(LOW)
        dk_out[rows, :] = (dk * scale).astype(LOW)
        dv_out[rows, :] = dv.astype(LOW)


def attend_heads(qkv):
    rows = qkv.shape[0]
    pairs = HEADS_A // 2

    def spec(offset):
        return pl.BlockSpec((rows, 2 * HEAD_A), lambda i: (0, i + offset))

    return pl.pallas_call(
        attend_kernel,
        grid=(pairs,),
        out_shape=jax.ShapeDtypeStruct((rows, D), LOW),
        in_specs=[spec(0), spec(pairs), spec(2 * pairs)],
        out_specs=spec(0),
        name="attend",
    )(qkv, qkv, qkv)


def attend_heads_back(qkv, heads_grad):
    rows = qkv.shape[0]
    pairs = HEADS_A // 2

    def spec(offset):
        return pl.BlockSpec((rows, 2 * HEAD_A), lambda i: (0, i + offset))

    return pl.pallas_call(
        attend_back_kernel,
        grid=(pairs,),
        out_shape=[jax.ShapeDtypeStruct((rows, D), LOW)] * 3,
        in_specs=[spec(0), spec(pairs), spec(2 * pairs), spec(0)],
        out_specs=[spec(0)] * 3,
        name="attend_back",
    )(qkv, qkv, qkv, heads_grad)


def per_device_heads(
    byte_ids,
    doc_patches,
    pad_bytes,
    byte_table,
    patch_weight,
    gain_mix,
    in_weight,
    conv_weight,
    conv_bias,
    step_bias,
    log_rate,
    skip_gain,
    gated_gain,
    out_weight,
    local_weight,
    gain_attn,
    query_weight,
    key_weight,
    value_weight,
    attn_weight,
    feed_gain,
    gate_weight,
    up_weight,
    down_weight,
    cotangent,
):
    narrow, wide = lax.axis_size("narrow"), lax.axis_size("wide")
    devices = narrow * wide
    device = lax.axis_index(BOTH)
    rows = byte_ids.shape[0]
    patches = rows // PATCH
    everything = devices * patches
    own_rows = patch_weight.shape[0]
    hidden_width = gate_weight.shape[1]
    share = hidden_width // narrow

    segment, _, keep_all = patch_layout(doc_patches, pad_bytes, 0, everything)
    keep_all = keep_all.reshape(everything, PATCH)
    place = jnp.arange(everything)
    mark_columns = [segment.astype(FULL)]
    for lag in range(1, CONV):
        earlier = jnp.concatenate([jnp.full((lag,), -1, jnp.int32), segment[:-lag]])
        mark_columns.append((earlier == segment).astype(FULL))
    by_block = segment.reshape(-1, QUERY)
    before = jnp.concatenate([jnp.full((1,), -1, jnp.int32), by_block[:-1, -1]])
    mark_columns.append((by_block == before[:, None]).astype(FULL).reshape(-1))
    mark_columns.append((by_block == by_block[:, -1:]).astype(FULL).reshape(-1))
    mark_columns.append(
        jnp.broadcast_to((by_block[:, -1:] == before[:, None]).astype(FULL), by_block.shape).reshape(-1)
    )
    mark_columns.append(jnp.zeros((everything,), FULL))
    marks = jnp.pad(jnp.stack(mark_columns, axis=1), ((0, 8), (0, 0)))
    keep_rows = lax.dynamic_slice_in_dim(keep_all, device * patches, patches).reshape(-1)

    ids_low = byte_ids.astype(LOW).reshape(patches, PATCH)
    bcdt_width = 2 * STATE + HEADS_M
    start_pack = jnp.concatenate(
        [
            patch_weight,
            jnp.pad(in_weight[:, 2 * DI :], ((0, 0), (0, 96))),
            jnp.pad(ids_low, ((0, 0), (0, 120))),
        ],
        axis=1,
    )
    xz_blocks = jnp.concatenate(
        [
            in_weight[:, DI : 2 * DI].reshape(own_rows, HEADS_M, HEAD_M),
            in_weight[:, :DI].reshape(own_rows, HEADS_M, HEAD_M),
        ],
        axis=2,
    ).transpose(1, 0, 2)
    xz_weight = exchange(xz_blocks, BOTH).reshape(D, 2 * HEAD_M)
    start_all, table_all = gather_all([start_pack, byte_table], 0)
    middle_pack = jnp.concatenate(
        [
            query_weight,
            key_weight,
            value_weight,
            attn_weight,
            out_weight[:own_rows],
            out_weight[own_rows:],
            local_weight.T,
        ],
        axis=1,
    )
    middle_all = lax.all_gather(middle_pack, BOTH, axis=0, tiled=True)
    feed_blocks = jnp.stack(
        [
            gate_weight.T.reshape(narrow, share, -1),
            up_weight.T.reshape(narrow, share, -1),
            down_weight.reshape(narrow, share, -1),
        ],
        axis=1,
    )
    feed_turned = exchange(feed_blocks, "narrow").transpose(1, 2, 0, 3).reshape(3, share, D)
    feed_all = lax.all_gather(feed_turned, "wide")
    in_all = lax.all_gather(in_weight, BOTH, axis=0, tiled=True)

    patch_all = start_all[:, :D]
    bcdt_weight = start_all[:, D : D + bcdt_width]
    ids_all = start_all[:, D + 384 : D + 384 + PATCH].astype(jnp.int32)

    vocabulary = jnp.arange(VOCAB, dtype=jnp.int32)
    onehot = (ids_all[:, :, None] == vocabulary).astype(LOW) * keep_all[:, :, None].astype(LOW)
    embedded = (
        jnp.dot(onehot.reshape(everything * PATCH, VOCAB), table_all, preferred_element_type=FULL)
        .astype(LOW)
        .reshape(everything, D)
    )
    mixed_all = jnp.dot(embedded, patch_all, preferred_element_type=FULL)
    normed_all = root_norm(mixed_all, gain_mix).astype(LOW)
    xz = jnp.dot(normed_all, xz_weight, preferred_element_type=FULL).astype(LOW)
    bcdt = jnp.dot(normed_all, bcdt_weight, preferred_element_type=FULL).astype(LOW)
    bc = bcdt[:, : 2 * STATE]
    dt = lax.dynamic_slice_in_dim(bcdt[:, 2 * STATE :], device, 1, axis=1).astype(FULL)
    mixed_in = lax.dynamic_slice_in_dim(mixed_all, device * patches, patches)

    conv_x = lax.dynamic_slice_in_dim(conv_weight, device * HEAD_M, HEAD_M, axis=1)
    bias_x = lax.dynamic_slice_in_dim(conv_bias, device * HEAD_M, HEAD_M)[None]
    conv_x = jnp.pad(conv_x, ((0, 0), (0, HEAD_M)))
    bias_x = jnp.pad(bias_x, ((0, 0), (0, HEAD_M)))
    conv_bc = conv_weight[:, DI:]
    bias_bc = conv_bias[None, DI:]

    def own(values):
        return lax.dynamic_index_in_dim(values, device, 0, False)

    numbers = jnp.stack([own(step_bias), jnp.exp(own(log_rate)), own(skip_gain)])
    mixer_args = (numbers, xz, bc, dt, marks, conv_x, bias_x, conv_bc, bias_bc)
    u, y, states = mixer_forward(*mixer_args)
    u_blocks = exchange(u.astype(LOW).reshape(devices, patches, HEAD_M), BOTH)
    gated_rows = u_blocks.transpose(1, 0, 2).reshape(patches, DI).astype(FULL)
    gated_scale = lax.rsqrt(jnp.mean(gated_rows * gated_rows, axis=-1, keepdims=True) + epsilon)
    gated_low = (gated_rows * gated_scale * gated_gain).astype(LOW)

    out_all = (
        middle_all[:, 4 * D : 6 * D]
        .reshape(devices, own_rows, 2, D)
        .transpose(0, 2, 1, 3)
        .reshape(DI, D)
    )
    local_all = middle_all[:, 6 * D :]
    qkv_all = middle_all[:, : 3 * D]
    attn_all = middle_all[:, 3 * D : 4 * D]
    global_out = mixed_in + jnp.dot(gated_low, out_all, preferred_element_type=FULL)

    local_rows = global_out.astype(LOW).reshape(rows, EMB)
    stream = nt(local_rows, local_all)
    normed_attn = root_norm(stream, gain_attn).astype(LOW)
    qkv = jnp.dot(normed_attn, qkv_all, preferred_element_type=FULL).astype(LOW)
    mixed_heads = attend_heads(qkv)
    after_attn = stream + jnp.dot(mixed_heads, attn_all, preferred_element_type=FULL)
    normed_feed = root_norm(after_attn, feed_gain).astype(LOW)
    out_grad = cotangent.astype(FULL) * keep_rows[:, None]
    feed_grad = out_grad.astype(LOW)

    feed_width = wide * share
    gate_up_all = feed_all[:, :2].reshape(wide, 2, share, D).transpose(1, 0, 2, 3)
    gate_up_all = gate_up_all.reshape(2 * feed_width, D)
    down_all = feed_all[:, 2].reshape(feed_width, D)

    def over_narrow(values):
        spread_out = jnp.broadcast_to(values[None], (narrow,) + values.shape)
        return exchange(spread_out, "narrow").reshape((-1,) + values.shape[1:])

    def back_over_narrow(values):
        blocks = exchange(values.astype(LOW).reshape(narrow, rows, D), "narrow")
        return jnp.sum(blocks.astype(FULL), axis=0)

    grid_grad = over_narrow(feed_grad)
    grid_in = over_narrow(normed_feed)
    gate_up = nt(grid_in, gate_up_all)
    gate, up = gate_up[:, :feed_width], gate_up[:, feed_width:]
    hidden = (jax.nn.silu(gate) * up).astype(LOW)
    feed_out = back_over_narrow(nn(hidden, down_all))
    hidden_grad = nt(grid_grad, down_all)
    gate_up_grad = silu_back(gate_up, hidden_grad, feed_width).astype(LOW)
    grad_gate_up = tn(gate_up_grad, grid_in).reshape(2, wide, share, D)
    grad_down_part = tn(hidden, grid_grad).reshape(1, wide, share, D)
    feed_in_grad = back_over_narrow(nn(gate_up_grad, gate_up_all))
    feed_grads = jnp.concatenate([grad_gate_up, grad_down_part]).transpose(1, 0, 2, 3).astype(LOW)
    feed_sums = lax.psum_scatter(
        feed_grads.reshape(-1, D), "wide", scatter_dimension=0, tiled=True
    )
    feed_sums = feed_sums.reshape(3, share, narrow, D // narrow).transpose(2, 0, 1, 3)
    feed_sums = exchange(feed_sums, "narrow").transpose(1, 0, 2, 3).astype(FULL)
    feed_sums = feed_sums.reshape(3, hidden_width, D // narrow)
    grad_gate, grad_up, grad_down = feed_sums[0].T, feed_sums[1].T, feed_sums[2]
    out_rows = ((after_attn + feed_out.astype(LOW).astype(FULL)) * keep_rows[:, None]).astype(LOW)

    _, feed_norm_back = jax.vjp(root_norm, after_attn, feed_gain)
    after_norm_grad, grad_feed_gain = feed_norm_back(feed_in_grad.astype(LOW).astype(FULL))
    after_grad = out_grad + after_norm_grad
    attn_grad = after_grad.astype(LOW)
    heads_grad = nt(attn_grad, attn_all).astype(LOW)
    query_grad, key_grad, value_grad = attend_heads_back(qkv, heads_grad)
    qkv_grad = jnp.concatenate([query_grad, key_grad, value_grad], axis=1)
    normed_grad = nt(qkv_grad, qkv_all)
    _, attn_norm_back = jax.vjp(root_norm, stream, gain_attn)
    stream_norm_grad, grad_gain_attn = attn_norm_back(normed_grad)
    stream_grad = (after_grad + stream_norm_grad).astype(LOW)
    middle_grads = jnp.concatenate(
        [tn(normed_attn, qkv_grad), tn(mixed_heads, attn_grad), tn(stream_grad, local_rows)], axis=1
    ).astype(LOW)
    middle_sums = lax.psum_scatter(middle_grads, BOTH, scatter_dimension=0, tiled=True).astype(FULL)
    global_grad = nn(stream_grad, local_all).reshape(patches, D)

    mix_grad = global_grad.astype(LOW)
    gated_grad = nt(mix_grad, out_all)
    _, gated_back = jax.vjp(root_norm, gated_rows, gated_gain)
    gated_rows_grad, grad_gated_gain = gated_back(gated_grad)
    du_blocks = gated_rows_grad.astype(LOW).reshape(patches, devices, HEAD_M).transpose(1, 0, 2)
    du = exchange(du_blocks, BOTH).reshape(everything, HEAD_M)
    dxz, dbc, ddt, dwx, dwbc, dnumbers = mixer_backward(*mixer_args, y, states, du)
    grad_xz = tn(normed_all, dxz).astype(LOW).reshape(devices, own_rows, 2 * HEAD_M)
    grad_xz = exchange(grad_xz, BOTH).astype(FULL).transpose(1, 0, 2)
    proj_blocks = jnp.concatenate(
        [dxz, dbc, jnp.pad(ddt.astype(LOW), ((0, 0), (0, 127)))], axis=1
    ).reshape(devices, patches, 4 * STATE)
    proj_blocks = exchange(proj_blocks, BOTH)
    xz_grad = proj_blocks[:, :, :STATE].transpose(1, 0, 2)
    bc_grad = jnp.sum(proj_blocks[:, :, STATE : 3 * STATE].astype(FULL), axis=0).astype(LOW)
    bcdt_grad = jnp.concatenate([bc_grad, proj_blocks[:, :, 3 * STATE].T], axis=1)
    proj_low = jnp.concatenate(
        [
            xz_grad[:, :, HEAD_M:].reshape(patches, DI),
            xz_grad[:, :, :HEAD_M].reshape(patches, DI),
            bcdt_grad,
        ],
        axis=1,
    )
    normed_mix_grad = nt(proj_low, in_all)
    _, mix_norm_back = jax.vjp(root_norm, mixed_in, gain_mix)
    mixed_norm_grad, grad_gain_mix = mix_norm_back(normed_mix_grad)
    embed_grad = (global_grad + mixed_norm_grad).astype(LOW)

    end_pack = jnp.concatenate(
        [
            embed_grad,
            mix_grad,
            jnp.pad(bcdt_grad, ((0, 0), (0, 96))),
            jnp.broadcast_to(gated_scale.astype(LOW), (patches, 128)),
        ],
        axis=1,
    )
    (end_all,) = gather_all([end_pack], 1)
    embed_grad_all = end_all[:, :D]
    mix_grad_all = end_all[:, D : 2 * D]
    bcdt_grad_all = end_all[:, 2 * D : 2 * D + bcdt_width]
    scale_all = end_all[:, 2 * D + 384 : 2 * D + 385].astype(FULL)
    gain_own = lax.dynamic_slice_in_dim(gated_gain, device * HEAD_M, HEAD_M)
    grad_out = tn((u * scale_all * gain_own).astype(LOW), mix_grad_all)
    normed_own = lax.dynamic_slice_in_dim(normed_all, device * own_rows, own_rows, axis=1)
    grad_bcdt = tn(normed_own, bcdt_grad_all)
    grad_in = jnp.concatenate(
        [
            grad_xz[:, :, HEAD_M:].reshape(own_rows, DI),
            grad_xz[:, :, :HEAD_M].reshape(own_rows, DI),
            grad_bcdt,
        ],
        axis=1,
    )
    embedded_own = lax.dynamic_slice_in_dim(embedded, device * own_rows, own_rows, axis=1)
    grad_patch = tn(embedded_own, embed_grad_all)
    own_words = byte_table.shape[0]
    words = device * own_words + jnp.arange(own_words, dtype=jnp.int32)
    chosen = (ids_all[:, :, None] == words).astype(LOW) * keep_all[:, :, None].astype(LOW)
    word_sums = tn(chosen.reshape(everything, PATCH * own_words), embed_grad_all)
    grad_table = jnp.einsum(
        "kvd,ked->ve",
        word_sums.reshape(PATCH, own_words, D),
        patch_all.astype(FULL).reshape(PATCH, EMB, D),
        precision=highest,
    )

    conv_grads = jnp.zeros((CONV + 1, DI + 2 * STATE), FULL)
    conv_grads = lax.dynamic_update_slice(
        conv_grads, dwx[: CONV + 1, :HEAD_M], (0, device * HEAD_M)
    )
    conv_grads = lax.dynamic_update_slice(conv_grads, dwbc[: CONV + 1], (0, DI))
    number_grads = jnp.where(
        jnp.arange(HEADS_M)[None, :] == device, dnumbers[:3, :1], 0.0
    )
    small = lax.psum(
        (conv_grads, number_grads, grad_gain_mix, grad_gated_gain, grad_gain_attn, grad_feed_gain),
        BOTH,
    )
    conv_grads, number_grads = small[:2]
    return (
        out_rows,
        grad_table,
        grad_patch,
        small[2],
        grad_in,
        conv_grads[:CONV],
        conv_grads[CONV],
        number_grads[0],
        number_grads[1],
        number_grads[2],
        small[3],
        grad_out,
        middle_sums[:, 4 * D :].T,
        small[4],
        middle_sums[:, :D],
        middle_sums[:, D : 2 * D],
        middle_sums[:, 2 * D : 3 * D],
        middle_sums[:, 3 * D : 4 * D],
        small[5],
        grad_gate,
        grad_up,
        grad_down,
    )


def solution(mesh):
    placed = (
        P(("narrow", "wide")),
        P(),
        P(),
        P(("narrow", "wide"), None),
        P(("narrow", "wide"), None),
        P(),
        P(("narrow", "wide"), None),
        P(),
        P(),
        P(),
        P(),
        P(),
        P(),
        P(("narrow", "wide"), None),
        P(None, ("narrow", "wide")),
        P(),
        P(("narrow", "wide"), None),
        P(("narrow", "wide"), None),
        P(("narrow", "wide"), None),
        P(("narrow", "wide"), None),
        P(),
        P("narrow", "wide"),
        P("narrow", "wide"),
        P("wide", "narrow"),
        P(("narrow", "wide"), None),
    )
    return jax.shard_map(
        per_device_heads if mesh.size == HEADS_M else per_device_rows,
        mesh=mesh,
        in_specs=placed,
        out_specs=(
            P(("narrow", "wide"), None),
            P(("narrow", "wide"), None),
            P(("narrow", "wide"), None),
            P(),
            P(("narrow", "wide"), None),
            P(),
            P(),
            P(),
            P(),
            P(),
            P(),
            P(("narrow", "wide"), None),
            P(None, ("narrow", "wide")),
            P(),
            P(("narrow", "wide"), None),
            P(("narrow", "wide"), None),
            P(("narrow", "wide"), None),
            P(("narrow", "wide"), None),
            P(),
            P("narrow", "wide"),
            P("narrow", "wide"),
            P("wide", "narrow"),
        ),
        check_vma=False,
    )
```

```python
from functools import partial

import jax
import jax.numpy as jnp
from jax import lax
from jax.experimental import pallas as pl
from jax.experimental.pallas import tpu as pltpu
from jax.sharding import PartitionSpec as P

D = 1024
PATCH = 8
EMB = 128
VOCAB = 256
HEADS_M = 32
HEAD_M = 64
DI = 2048
STATE = 128
CONV = 4
HEADS_A = 16
HEAD_A = 64


epsilon = 1e-05
highest = lax.Precision.HIGHEST
masked_score = -1e30


def running_sum(x):
    place = jnp.arange(x.shape[0])
    seen = place[:, None] >= place[None, :]
    if x.ndim == 1:
        return jnp.sum(jnp.where(seen, x[None, :], 0), axis=1).astype(x.dtype)
    return jnp.dot(seen.astype(x.dtype), x, precision=highest)


def passed_along(x, axis, by):
    peers = lax.axis_size(axis)
    pairs = [(i, i + by) for i in range(peers) if 0 <= i + by < peers]
    return lax.ppermute(x, axis, pairs)


def prefix_2(x, axis, join, neutral):
    place = lax.axis_index(axis)
    gathered = jax.tree.map(
        lambda a, kind: lax.all_gather(a.astype(kind), axis), x, (jnp.bfloat16, jnp.bfloat16)
    )
    state = jax.tree.map(lambda a, e: jnp.zeros_like(a) + jnp.asarray(e, a.dtype), x, neutral)

    def prefix_one(hop, state):
        return join(
            state,
            jax.tree.map(
                lambda a, own: lax.dynamic_index_in_dim(a, hop, 0, False).astype(own.dtype),
                gathered,
                x,
            ),
        )

    return lax.fori_loop(0, place, prefix_one, state)


def carried_in_2(x, axis, join, neutral):
    count = lax.axis_size(axis)
    place = lax.axis_index(axis)
    ahead = count - 1 - place
    gathered = jax.tree.map(
        lambda a, kind: lax.all_gather(a.astype(kind), axis),
        x,
        jax.tree.map(lambda a: jnp.bfloat16 if a.dtype == jnp.float32 else a.dtype, x),
    )
    state = jax.tree.map(lambda a, e: jnp.zeros_like(a) + jnp.asarray(e, a.dtype), x, neutral)

    def carried_one(hop, state):
        source = count - 1 - hop
        return join(
            state,
            jax.tree.map(
                lambda a, own: lax.dynamic_index_in_dim(a, source, 0, False).astype(own.dtype),
                gathered,
                x,
            ),
        )

    return lax.fori_loop(0, ahead, carried_one, state)


def root_norm(values, gain):
    return values * lax.rsqrt(jnp.mean(values * values, axis=-1, keepdims=True) + epsilon) * gain


def patch_layout(doc_patches, pad_bytes, first_index, patch_count):
    patch_index = first_index + jnp.arange(patch_count, dtype=jnp.int32)
    doc_ends = running_sum(doc_patches)
    doc_index = jnp.arange(doc_patches.shape[0], dtype=jnp.int32)
    segment = jnp.sum((patch_index[:, None] >= doc_ends[None, :]).astype(jnp.int32), axis=1)
    owner_mask = segment[:, None] == doc_index[None, :]
    last_end = jnp.sum(jnp.where(owner_mask, doc_ends[None, :] - 1, 0), axis=1)
    doc_starts = jnp.sum(jnp.where(owner_mask, (doc_ends - doc_patches)[None, :], 0), axis=1)
    pad_count = jnp.sum(jnp.where(owner_mask, pad_bytes[None, :], 0), axis=1)
    offset = jnp.arange(PATCH, dtype=jnp.int32)
    padded = (patch_index == last_end)[:, None] & (offset[None, :] >= PATCH - pad_count[:, None])
    keep_mask = 1.0 - padded.astype(jnp.float32).reshape(-1)
    return (segment, (patch_index == doc_starts).astype(jnp.int32), keep_mask)


def ssd_terms(layout, projected, rim_rows, small_params):
    conv_weight, conv_bias, step_bias, log_rate, skip_gain = small_params
    segment, rim_segment, first_patch = layout
    conv_in = projected[:, DI : 2 * DI + 2 * STATE]
    patch_count = conv_in.shape[0]
    padded = jnp.concatenate([rim_rows, conv_in], 0)
    padded_seg = jnp.concatenate([rim_segment, segment], 0)
    conv_sum = conv_bias
    for conv_tap in range(CONV):
        same_doc = (padded_seg[conv_tap : conv_tap + patch_count] == segment).astype(jnp.float32)[
            :, None
        ]
        conv_sum = (
            conv_sum + conv_weight[conv_tap] * padded[conv_tap : conv_tap + patch_count] * same_doc
        )
    activated = jax.nn.silu(conv_sum)
    values = activated[:, :DI].reshape(patch_count, HEADS_M, HEAD_M)
    input_map = activated[:, DI : DI + STATE]
    output_map = activated[:, DI + STATE :]
    time_steps = jax.nn.softplus(projected[:, 2 * DI + 2 * STATE :] + step_bias)
    cumulative = running_sum(-time_steps * jnp.exp(log_rate))
    no_reset = (running_sum(first_patch) == 0).astype(jnp.float32)
    return (values, input_map, output_map, time_steps, cumulative, no_reset)


def local_state(layout, projected, rim_rows, small_params):
    values, input_map, output_map, time_steps, cumulative, no_reset = ssd_terms(
        layout, projected, rim_rows, small_params
    )
    segment = layout[0]
    decay_tail = (
        jnp.exp(cumulative[-1][None, :] - cumulative)
        * (segment == segment[-1]).astype(jnp.float32)[:, None]
        * time_steps
    )
    state_local = jnp.einsum("sh,shp,sn->hpn", decay_tail, values, input_map, precision=highest)
    decay_total = jnp.exp(cumulative[-1]) * no_reset[-1]
    return (decay_total, state_local)


def mixer_output(layout, projected, rim_rows, small_params, incoming, gated_gain):
    values, input_map, output_map, time_steps, cumulative, no_reset = ssd_terms(
        layout, projected, rim_rows, small_params
    )
    segment = layout[0]
    patch_count = values.shape[0]
    position = jnp.arange(patch_count)
    visible = (segment[:, None] == segment[None, :]) & (position[:, None] >= position[None, :])
    log_gap = jnp.where(visible[:, :, None], cumulative[:, None, :] - cumulative[None, :, :], 0.0)
    inner = jnp.dot(output_map, input_map.T, precision=highest)
    weight = (
        jnp.exp(log_gap)
        * visible[:, :, None].astype(jnp.float32)
        * time_steps[None, :, :]
        * inner[:, :, None]
    )
    within = jnp.einsum("tsh,shp->thp", weight, values, precision=highest)
    carried_in = (
        jnp.einsum("tn,hpn->thp", output_map, incoming, precision=highest)
        * (jnp.exp(cumulative) * no_reset[:, None])[:, :, None]
    )
    result = (within + carried_in + small_params[4][None, :, None] * values).reshape(
        patch_count, DI
    )
    gated_rows = result * jax.nn.silu(projected[:, :DI])
    return root_norm(gated_rows, gated_gain)


def combine_states(earlier, following):
    return (earlier[0] * following[0], following[0][:, None, None] * earlier[1] + following[1])


def attend(stream, gain_attn, query_all, key_all, value_all):
    head_shape = (-1, PATCH, HEADS_A, HEAD_A)
    normed_attn = root_norm(stream, gain_attn).astype(jnp.bfloat16)
    queries = jnp.dot(normed_attn, query_all, preferred_element_type=jnp.float32).astype(
        jnp.bfloat16
    )
    key_rows = jnp.dot(normed_attn, key_all, preferred_element_type=jnp.float32).astype(
        jnp.bfloat16
    )
    value_rows = jnp.dot(normed_attn, value_all, preferred_element_type=jnp.float32).astype(
        jnp.bfloat16
    )
    scores = jnp.einsum(
        "pqhe,pkhe->phqk",
        queries.reshape(head_shape),
        key_rows.reshape(head_shape),
        preferred_element_type=jnp.float32,
    ) * HEAD_A ** (-0.5)
    position = jnp.arange(PATCH)
    causal = position[:, None] >= position[None, :]
    attn_probs = jax.nn.softmax(jnp.where(causal, scores, masked_score), axis=-1)
    mixed_heads = jnp.einsum(
        "phqk,pkhe->pqhe",
        attn_probs.astype(jnp.bfloat16),
        value_rows.reshape(head_shape),
        preferred_element_type=jnp.float32,
    )
    mixed_heads = mixed_heads.reshape(stream.shape[0], -1).astype(jnp.bfloat16)
    return (normed_attn, queries, key_rows, value_rows, attn_probs, mixed_heads)


def spread(values):
    by_rows = lax.all_to_all(values, "narrow", split_axis=1, concat_axis=0, tiled=True)
    return lax.all_gather(by_rows, "wide", axis=0, tiled=True)


def collect(term_fn, row_count):
    summed = lax.psum_scatter(
        term_fn(jnp.int32(0), row_count * lax.axis_size("wide")).astype(jnp.bfloat16),
        "wide",
        scatter_dimension=0,
        tiled=True,
    )
    return lax.all_to_all(summed, "narrow", split_axis=0, concat_axis=1, tiled=True)


def narrow_total(partial_rows):
    return lax.psum(partial_rows, "narrow").astype(jnp.float32)


def silu_back(gate_up, hidden_grad, hidden_width):
    gate_rows = gate_up[:, :hidden_width]
    up_rows = gate_up[:, hidden_width:]
    sigmoid = jax.nn.sigmoid(gate_rows)
    gate_grad = hidden_grad * up_rows * sigmoid * (1.0 + gate_rows * (1.0 - sigmoid))
    up_grad = hidden_grad * gate_rows * sigmoid
    return jnp.concatenate([gate_grad, up_grad], axis=1)


def per_device_rows(
    byte_ids,
    doc_patches,
    pad_bytes,
    byte_table,
    patch_weight,
    gain_mix,
    in_weight,
    conv_weight,
    conv_bias,
    step_bias,
    log_rate,
    skip_gain,
    gated_gain,
    out_weight,
    local_weight,
    gain_attn,
    query_weight,
    key_weight,
    value_weight,
    attn_weight,
    feed_gain,
    gate_weight,
    up_weight,
    down_weight,
    cotangent,
):
    byte_rows = byte_ids.shape[0]
    patches = byte_rows // PATCH
    device = lax.axis_index(("narrow", "wide"))
    wide_count = lax.axis_size("wide")
    segment, first_patch, keep_mask = patch_layout(
        doc_patches, pad_bytes, device * patches, patches
    )
    rim_segment = patch_layout(doc_patches, pad_bytes, device * patches - (CONV - 1), CONV - 1)[0]
    layout = (segment, rim_segment, first_patch)
    gathered = (
        lax.all_gather(byte_table, ("narrow", "wide"), axis=0, tiled=True),
        lax.all_gather(patch_weight, ("narrow", "wide"), axis=0, tiled=True),
        lax.all_gather(in_weight, ("narrow", "wide"), axis=0, tiled=True),
        lax.all_gather(out_weight, ("narrow", "wide"), axis=0, tiled=True),
        lax.all_gather(local_weight, ("narrow", "wide"), axis=1, tiled=True),
        lax.all_gather(query_weight, ("narrow", "wide"), axis=0, tiled=True),
        lax.all_gather(key_weight, ("narrow", "wide"), axis=0, tiled=True),
        lax.all_gather(value_weight, ("narrow", "wide"), axis=0, tiled=True),
        lax.all_gather(attn_weight, ("narrow", "wide"), axis=0, tiled=True),
    )
    table_all, patch_all, in_all, out_all, local_all, query_all, key_all, value_all, attn_all = (
        gathered
    )
    onehot = (byte_ids[:, None] == jnp.arange(VOCAB, dtype=jnp.int32)[None, :]).astype(jnp.bfloat16)
    embedded = (
        (jnp.dot(onehot, table_all, preferred_element_type=jnp.float32) * keep_mask[:, None])
        .astype(jnp.bfloat16)
        .reshape(patches, D)
    )
    mixed_in = jnp.dot(embedded, patch_all, preferred_element_type=jnp.float32)
    normed_mix = root_norm(mixed_in, gain_mix).astype(jnp.bfloat16)
    projected = jnp.dot(normed_mix, in_all, preferred_element_type=jnp.float32).astype(jnp.bfloat16)
    rim_rows = passed_along(
        projected[patches - (CONV - 1) :, DI : 2 * DI + 2 * STATE], ("narrow", "wide"), 1
    ).astype(jnp.float32)
    projected_f = projected.astype(jnp.float32)
    small_params = (conv_weight, conv_bias, step_bias, log_rate, skip_gain)
    (decay_total, state_local), state_back = jax.vjp(
        partial(local_state, layout), projected_f, rim_rows, small_params
    )
    prefix = prefix_2(
        (decay_total, state_local),
        ("narrow", "wide"),
        combine_states,
        (jnp.ones_like(decay_total), jnp.zeros_like(state_local)),
    )
    incoming = prefix[1]
    gated_norm, mixer_back = jax.vjp(
        partial(mixer_output, layout), projected_f, rim_rows, small_params, incoming, gated_gain
    )
    gated_low = gated_norm.astype(jnp.bfloat16)
    global_out = mixed_in + jnp.dot(gated_low, out_all, preferred_element_type=jnp.float32)
    local_rows = global_out.astype(jnp.bfloat16).reshape(byte_rows, EMB)
    stream = jnp.dot(local_rows, local_all, preferred_element_type=jnp.float32)
    normed_attn, queries, key_rows, value_rows, attn_probs, mixed_heads = attend(
        stream, gain_attn, query_all, key_all, value_all
    )
    after_attn = stream + jnp.dot(mixed_heads, attn_all, preferred_element_type=jnp.float32)
    normed_feed = root_norm(after_attn, feed_gain).astype(jnp.bfloat16)
    out_grad = cotangent.astype(jnp.float32) * keep_mask[:, None]
    feed_grad = out_grad.astype(jnp.bfloat16)
    grid_in = spread(normed_feed)
    both_weights = jnp.concatenate([gate_weight, up_weight], axis=1)
    hidden_width = gate_weight.shape[1]
    grid_share = grid_in.shape[0] // wide_count
    gate_up_part = jnp.dot(grid_in, both_weights, preferred_element_type=jnp.float32).astype(
        jnp.bfloat16
    )
    gate_up = narrow_total(gate_up_part)
    hidden = (jax.nn.silu(gate_up[:, :hidden_width]) * gate_up[:, hidden_width:]).astype(
        jnp.bfloat16
    )

    def down_term(first_row, row_count):
        return jnp.dot(hidden, down_weight, preferred_element_type=jnp.float32)

    feed_out = collect(down_term, grid_share)
    grid_grad = spread(feed_grad)
    grad_down = jnp.einsum("gf,gd->fd", hidden, grid_grad, preferred_element_type=jnp.float32)
    hidden_part = jnp.einsum(
        "gd,fd->gf", grid_grad, down_weight, preferred_element_type=jnp.float32
    ).astype(jnp.bfloat16)
    hidden_grad = narrow_total(hidden_part)
    gate_up_grad = silu_back(gate_up, hidden_grad, hidden_width).astype(jnp.bfloat16)
    grad_both = jnp.einsum("gd,gf->df", grid_in, gate_up_grad, preferred_element_type=jnp.float32)

    def back_term(first_row, row_count):
        return jnp.einsum(
            "gf,df->gd", gate_up_grad, both_weights, preferred_element_type=jnp.float32
        )

    feed_in_grad = collect(back_term, grid_share)
    grad_gate = grad_both[:, :hidden_width]
    grad_up = grad_both[:, hidden_width:]
    after_feed = after_attn + feed_out.astype(jnp.float32)
    out_rows = (after_feed * keep_mask[:, None]).astype(jnp.bfloat16)
    feed_normed, feed_norm_back = jax.vjp(root_norm, after_attn, feed_gain)
    after_norm_grad, grad_feed_gain = feed_norm_back(feed_in_grad.astype(jnp.float32))
    after_grad = out_grad + after_norm_grad
    head_shape = (-1, PATCH, HEADS_A, HEAD_A)
    score_scale = HEAD_A ** (-0.5)
    attn_grad = after_grad.astype(jnp.bfloat16)
    grad_attn = jnp.einsum("rd,re->de", mixed_heads, attn_grad, preferred_element_type=jnp.float32)
    heads_grad = (
        jnp.einsum("re,de->rd", attn_grad, attn_all, preferred_element_type=jnp.float32)
        .astype(jnp.bfloat16)
        .reshape(head_shape)
    )
    probs_grad = jnp.einsum(
        "pqhe,pkhe->phqk",
        heads_grad,
        value_rows.reshape(head_shape),
        preferred_element_type=jnp.float32,
    )
    value_grad = (
        jnp.einsum(
            "phqk,pqhe->pkhe",
            attn_probs.astype(jnp.bfloat16),
            heads_grad,
            preferred_element_type=jnp.float32,
        )
        .reshape(byte_rows, D)
        .astype(jnp.bfloat16)
    )
    score_grad = (
        attn_probs * (probs_grad - jnp.sum(attn_probs * probs_grad, axis=-1, keepdims=True))
    ).astype(jnp.bfloat16)
    query_grad = (
        (
            jnp.einsum(
                "phqk,pkhe->pqhe",
                score_grad,
                key_rows.reshape(head_shape),
                preferred_element_type=jnp.float32,
            )
            * score_scale
        )
        .reshape(byte_rows, D)
        .astype(jnp.bfloat16)
    )
    key_grad = (
        (
            jnp.einsum(
                "phqk,pqhe->pkhe",
                score_grad,
                queries.reshape(head_shape),
                preferred_element_type=jnp.float32,
            )
            * score_scale
        )
        .reshape(byte_rows, D)
        .astype(jnp.bfloat16)
    )
    grad_query = jnp.einsum(
        "rd,re->de", normed_attn, query_grad, preferred_element_type=jnp.float32
    )
    grad_key = jnp.einsum("rd,re->de", normed_attn, key_grad, preferred_element_type=jnp.float32)
    grad_value = jnp.einsum(
        "rd,re->de", normed_attn, value_grad, preferred_element_type=jnp.float32
    )
    normed_grad = jnp.einsum("re,de->rd", query_grad, query_all, preferred_element_type=jnp.float32)
    normed_grad = normed_grad + jnp.einsum(
        "re,de->rd", key_grad, key_all, preferred_element_type=jnp.float32
    )
    normed_grad = normed_grad + jnp.einsum(
        "re,de->rd", value_grad, value_all, preferred_element_type=jnp.float32
    )
    attn_normed, attn_norm_back = jax.vjp(root_norm, stream, gain_attn)
    stream_norm_grad, grad_gain_attn = attn_norm_back(normed_grad)
    stream_grad = (after_grad + stream_norm_grad).astype(jnp.bfloat16)
    grad_local = jnp.einsum(
        "re,rd->ed", local_rows, stream_grad, preferred_element_type=jnp.float32
    )
    global_grad = jnp.einsum(
        "rd,ed->re", stream_grad, local_all, preferred_element_type=jnp.float32
    ).reshape(patches, D)
    mix_grad = global_grad.astype(jnp.bfloat16)
    grad_out = jnp.einsum("pi,pd->id", gated_low, mix_grad, preferred_element_type=jnp.float32)
    gated_grad = jnp.einsum("pd,id->pi", mix_grad, out_all, preferred_element_type=jnp.float32)
    proj_grad_mix, rim_grad_mix, small_grad_mix, incoming_grad, grad_gated_gain = mixer_back(
        gated_grad
    )
    suffix = carried_in_2(
        (decay_total, incoming_grad),
        ("narrow", "wide"),
        combine_states,
        (jnp.ones_like(decay_total), jnp.zeros_like(incoming_grad)),
    )
    later_grad = suffix[1]
    decay_grad = jnp.sum(later_grad * incoming, axis=(1, 2))
    proj_grad_state, rim_grad_state, small_grad_state = state_back((decay_grad, later_grad))
    rim_from_next = passed_along(rim_grad_mix + rim_grad_state, ("narrow", "wide"), -1)
    proj_grad = proj_grad_mix + proj_grad_state
    proj_grad = proj_grad.at[patches - (CONV - 1) :, DI : 2 * DI + 2 * STATE].add(rim_from_next)
    proj_low = proj_grad.astype(jnp.bfloat16)
    grad_in = jnp.einsum("pd,pk->dk", normed_mix, proj_low, preferred_element_type=jnp.float32)
    normed_mix_grad = jnp.einsum("pk,dk->pd", proj_low, in_all, preferred_element_type=jnp.float32)
    mix_normed, mix_norm_back = jax.vjp(root_norm, mixed_in, gain_mix)
    mixed_norm_grad, grad_gain_mix = mix_norm_back(normed_mix_grad)
    embed_grad = (global_grad + mixed_norm_grad).astype(jnp.bfloat16)
    grad_patch = jnp.einsum("pi,pd->id", embedded, embed_grad, preferred_element_type=jnp.float32)
    byte_grad = (
        jnp.einsum("pd,id->pi", embed_grad, patch_all, preferred_element_type=jnp.float32).reshape(
            byte_rows, EMB
        )
        * keep_mask[:, None]
    )
    grad_table = jnp.dot(onehot.astype(jnp.float32).T, byte_grad, precision=highest)
    shared = (
        lax.psum_scatter(grad_table, ("narrow", "wide"), scatter_dimension=0, tiled=True),
        lax.psum_scatter(grad_patch, ("narrow", "wide"), scatter_dimension=0, tiled=True),
        lax.psum_scatter(grad_in, ("narrow", "wide"), scatter_dimension=0, tiled=True),
        lax.psum_scatter(grad_out, ("narrow", "wide"), scatter_dimension=0, tiled=True),
        lax.psum_scatter(grad_local, ("narrow", "wide"), scatter_dimension=1, tiled=True),
        lax.psum_scatter(grad_query, ("narrow", "wide"), scatter_dimension=0, tiled=True),
        lax.psum_scatter(grad_key, ("narrow", "wide"), scatter_dimension=0, tiled=True),
        lax.psum_scatter(grad_value, ("narrow", "wide"), scatter_dimension=0, tiled=True),
        lax.psum_scatter(grad_attn, ("narrow", "wide"), scatter_dimension=0, tiled=True),
    )
    small_sum = lax.psum(
        (
            small_grad_mix[0] + small_grad_state[0],
            small_grad_mix[1] + small_grad_state[1],
            small_grad_mix[2] + small_grad_state[2],
            small_grad_mix[3] + small_grad_state[3],
            small_grad_mix[4] + small_grad_state[4],
            grad_gain_mix,
            grad_gated_gain,
            grad_gain_attn,
            grad_feed_gain,
        ),
        ("narrow", "wide"),
    )
    return (
        out_rows,
        shared[0],
        shared[1],
        small_sum[5],
        shared[2],
        small_sum[0],
        small_sum[1],
        small_sum[2],
        small_sum[3],
        small_sum[4],
        small_sum[6],
        shared[3],
        shared[4],
        small_sum[7],
        shared[5],
        shared[6],
        shared[7],
        shared[8],
        small_sum[8],
        grad_gate,
        grad_up,
        grad_down,
    )


QUERY = 128
BYTE_BLOCK = 128
MESH = pl.DeviceIdType.MESH
LOW = jnp.bfloat16
FULL = jnp.float32
BOTH = ("narrow", "wide")


def nn(a, b, precision=None):
    return lax.dot_general(
        a, b, (((1,), (0,)), ((), ())), precision=precision, preferred_element_type=FULL
    )


def nt(a, b, precision=None):
    return lax.dot_general(
        a, b, (((1,), (1,)), ((), ())), precision=precision, preferred_element_type=FULL
    )


def tn(a, b, precision=None):
    return lax.dot_general(
        a, b, (((0,), (0,)), ((), ())), precision=precision, preferred_element_type=FULL
    )


def gather_kernel(count, narrow, depth, *refs):
    ins, outs = refs[:count], refs[count : 2 * count]
    local, z_send, z_recv, n_send, n_recv, c_send, c_recv = refs[2 * count :]
    n, w = lax.axis_index("narrow"), lax.axis_index("wide")
    z, c = lax.div(w, 2), lax.rem(w, 2)
    z_peers = [(n, lax.rem(z + k, depth) * 2 + c) for k in range(1, depth)]
    n_peers = [lax.rem(n + k, narrow) for k in range(1, narrow)]
    twin = (n, z * 2 + 1 - c)
    barrier = pltpu.get_barrier_semaphore()
    for peer in z_peers:
        pl.semaphore_signal(barrier, inc=1, device_id=peer, device_id_type=MESH)
    for m in n_peers:
        pl.semaphore_signal(barrier, inc=1, device_id=(m, w), device_id_type=MESH)
    pl.semaphore_signal(barrier, inc=1, device_id=twin, device_id_type=MESH)
    pl.semaphore_wait(barrier, len(z_peers) + len(n_peers) + 1)

    def remote(src, dst, send, recv, peer):
        return pltpu.make_async_remote_copy(
            src_ref=src, dst_ref=dst, send_sem=send, recv_sem=recv, device_id=peer, device_id_type=MESH
        )

    own = [pltpu.make_async_copy(ins[i], outs[i].at[n, z, c], local.at[i]) for i in range(count)]
    for i in range(count):
        own[i].start()
        for peer in z_peers:
            remote(ins[i], outs[i].at[n, z, c], z_send.at[i], z_recv.at[i], peer).start()
    for i in range(count):
        own[i].wait()
        part = outs[i].at[n, pl.ds(0, depth - 1), c]
        remote(part, part, z_send.at[i], z_recv.at[i], twin).wait_recv()
        mine = outs[i].at[n, :, c]
        for m in n_peers:
            remote(mine, mine, n_send.at[i], n_recv.at[i], (m, w)).start()
        remote(mine, mine, c_send.at[i], c_recv.at[i], twin).start()
    for i in range(count):
        part = outs[i].at[pl.ds(0, narrow - 1), :, c]
        remote(part, part, n_send.at[i], n_recv.at[i], twin).wait_recv()
        for m in n_peers:
            theirs = outs[i].at[m, :, c]
            remote(theirs, theirs, c_send.at[i], c_recv.at[i], twin).start()
    for i in range(count):
        half = outs[i].at[:, :, 1 - c]
        remote(half, half, c_send.at[i], c_recv.at[i], twin).wait()
        part = outs[i].at[n, pl.ds(0, depth - 1), c]
        remote(part, part, z_send.at[i], z_recv.at[i], twin).wait_send()
        part = outs[i].at[pl.ds(0, narrow - 1), :, c]
        remote(part, part, n_send.at[i], n_recv.at[i], twin).wait_send()


def gather_all(arrays, collective_id):
    narrow, wide = lax.axis_size("narrow"), lax.axis_size("wide")
    count = len(arrays)
    dma = pltpu.SemaphoreType.DMA((count,))
    outs = pl.pallas_call(
        partial(gather_kernel, count, narrow, wide // 2),
        out_shape=[
            jax.ShapeDtypeStruct((narrow, wide // 2, 2) + a.shape, a.dtype) for a in arrays
        ],
        in_specs=[pl.BlockSpec(memory_space=pl.ANY)] * count,
        out_specs=[pl.BlockSpec(memory_space=pl.ANY)] * count,
        scratch_shapes=[dma] * 7,
        compiler_params=pltpu.CompilerParams(collective_id=collective_id, has_side_effects=True),
        name="gather_all",
    )(*arrays)
    return [o.reshape((-1,) + a.shape[1:]) for o, a in zip(outs, arrays)]


def exchange(blocks, axis):
    return lax.all_to_all(blocks, axis, split_axis=0, concat_axis=0, tiled=True)


def softplus(v):
    return jnp.maximum(v, 0.0) + jnp.log1p(jnp.exp(-jnp.abs(v)))


def convolved(window, marks, weight, bias):
    pre = bias + weight[CONV - 1 :] * window[8:]
    for lag in range(1, CONV):
        pre = pre + weight[CONV - 1 - lag : CONV - lag] * (
            window[8 - lag : 8 - lag + QUERY] * marks[:, lag : lag + 1]
        )
    return pre


def decays(marks, dt, step_bias, rate_scale):
    shape = (QUERY, QUERY)
    row = lax.broadcasted_iota(jnp.int32, shape, 0)
    column = lax.broadcasted_iota(jnp.int32, shape, 1)
    lower = (row >= column).astype(FULL)
    segment = jnp.broadcast_to(marks[:, :1], shape)
    visible = (segment == segment.T) & (row >= column)
    delta = jnp.broadcast_to(softplus(dt + step_bias), shape)
    total = nn(lower, -delta * rate_scale, highest)
    gap = jnp.where(visible, total - total.T, 0.0)
    decay = jnp.where(visible, jnp.exp(gap), 0.0)
    last = total[QUERY - 1 :, :]
    begun = jnp.exp(total) * marks[:, 4:5]
    tail = jnp.exp(last - total) * marks[:, 5:6]
    kept = jnp.exp(last) * marks[:1, 6:7]
    return lower, delta, decay, begun, tail, kept


def mixer_forward_kernel(
    numbers, xz, bc, dt, marks, wx, bx, wbc, bbc, u_out, y_out, states, xz_pad, bc_pad, state
):
    count = xz.shape[0]
    xz_pad[pl.ds(0, 8), :] = jnp.zeros((8, xz_pad.shape[1]), FULL)
    bc_pad[pl.ds(0, 8), :] = jnp.zeros((8, bc_pad.shape[1]), FULL)
    state[...] = jnp.zeros_like(state)
    step_bias, rate_scale, skip = numbers[0], numbers[1], numbers[2]

    xz_pad[pl.ds(8, count), :] = xz[...].astype(FULL)
    bc_pad[pl.ds(8, count), :] = bc[...].astype(FULL)

    def block(i, carry):
        start = pl.multiple_of(i * QUERY, QUERY)
        rows = pl.ds(start, QUERY)
        mark = marks[rows, :]
        act_x = jax.nn.silu(convolved(xz_pad[pl.ds(start, QUERY + 8), :], mark, wx[...], bx[...]))
        act = jax.nn.silu(convolved(bc_pad[pl.ds(start, QUERY + 8), :], mark, wbc[...], bbc[...]))
        x, b, c = act_x[:, :HEAD_M], act[:, :STATE], act[:, STATE:]
        lower, delta, decay, begun, tail, kept = decays(mark, dt[rows, :], step_bias, rate_scale)
        weight = nt(c, b, highest) * decay * delta.T
        held = state[...]
        states[i] = held
        y = (
            nn(weight, x, highest)
            + nt(c, held, highest) * begun[:, :HEAD_M]
            + skip * x
        )
        state[...] = held * kept + tn(x * (tail * delta)[:, :HEAD_M], b, highest)
        z = xz[rows, :].astype(FULL)[:, HEAD_M:]
        y_out[rows, :] = y
        u_out[rows, :] = y * jax.nn.silu(z)
        return carry

    lax.fori_loop(0, count // QUERY, block, 0)


def mixer_backward_kernel(
    numbers,
    xz,
    bc,
    dt,
    marks,
    wx,
    bx,
    wbc,
    bbc,
    y_in,
    states,
    du_in,
    dxz,
    dbc,
    ddt,
    dwx,
    dwbc,
    dnumbers,
    xz_pad,
    bc_pad,
    dx_pad,
    dbc_pad,
    dstate,
):
    count = xz.shape[0]
    blocks = count // QUERY
    xz_pad[pl.ds(0, 8), :] = jnp.zeros((8, xz_pad.shape[1]), FULL)
    bc_pad[pl.ds(0, 8), :] = jnp.zeros((8, bc_pad.shape[1]), FULL)
    dx_pad[pl.ds(count, 8), :] = jnp.zeros((8, dx_pad.shape[1]), FULL)
    dbc_pad[pl.ds(count, 8), :] = jnp.zeros((8, dbc_pad.shape[1]), FULL)
    dstate[...] = jnp.zeros_like(dstate)
    dwx[...] = jnp.zeros_like(dwx)
    dwbc[...] = jnp.zeros_like(dwbc)
    dnumbers[...] = jnp.zeros_like(dnumbers)
    step_bias, rate_scale, skip = numbers[0], numbers[1], numbers[2]

    def fill(i, carry):
        start = pl.multiple_of(i * QUERY, QUERY)
        rows = pl.ds(start, QUERY)
        xz_pad[pl.ds(start + 8, QUERY), :] = xz[rows, :].astype(FULL)
        bc_pad[pl.ds(start + 8, QUERY), :] = bc[rows, :].astype(FULL)
        return carry

    lax.fori_loop(0, blocks, fill, 0)

    def slope(pre):
        s = jax.nn.sigmoid(pre)
        return s * (1.0 + pre * (1.0 - s))

    def total(v):
        return jnp.sum(jnp.sum(v, axis=1, keepdims=True), axis=0, keepdims=True)

    def conv_back(pad, start, dpre_pad, dpre, weight, dw):
        mark = marks[pl.ds(start, QUERY), :]
        window = pad[pl.ds(start, QUERY + 8), :]
        later = dpre_pad[pl.ds(start, QUERY + 8), :]
        later_marks = marks[pl.ds(start, QUERY + 8), :]
        out = weight[CONV - 1 :] * dpre
        dw[CONV - 1 : CONV, :] += jnp.sum(dpre * window[8:], axis=0, keepdims=True)
        dw[CONV : CONV + 1, :] += jnp.sum(dpre, axis=0, keepdims=True)
        for lag in range(1, CONV):
            tap = CONV - 1 - lag
            out = out + weight[tap : tap + 1] * (
                (later * later_marks[:, lag : lag + 1])[lag : lag + QUERY]
            )
            dw[tap : tap + 1, :] += jnp.sum(
                dpre * (window[8 - lag : 8 - lag + QUERY] * mark[:, lag : lag + 1]),
                axis=0,
                keepdims=True,
            )
        return out

    def block(k, carry):
        i = blocks - 1 - k
        start = pl.multiple_of(i * QUERY, QUERY)
        rows = pl.ds(start, QUERY)
        mark = marks[rows, :]
        pre_x = convolved(xz_pad[pl.ds(start, QUERY + 8), :], mark, wx[...], bx[...])
        pre = convolved(bc_pad[pl.ds(start, QUERY + 8), :], mark, wbc[...], bbc[...])
        act = jax.nn.silu(pre)
        x, b, c = jax.nn.silu(pre_x)[:, :HEAD_M], act[:, :STATE], act[:, STATE:]
        step = dt[rows, :]
        lower, delta, decay, begun, tail, kept = decays(mark, step, step_bias, rate_scale)
        held, dheld = states[i], dstate[...]
        z = xz[rows, :].astype(FULL)[:, HEAD_M:]
        du, y = du_in[rows, :].astype(FULL), y_in[rows, :]
        dy = du * jax.nn.silu(z)
        dz = du * y * slope(z)
        scores = nt(c, b, highest)
        reach = decay * delta.T
        dweight = nt(dy, x, highest)
        dscores = dweight * reach
        fed = x * (tail * delta)[:, :HEAD_M]
        begun_dy = dy * begun[:, :HEAD_M]
        dc = nn(dscores, b, highest) + nn(begun_dy, held, highest)
        db = tn(dscores, c, highest) + nn(fed, dheld, highest)
        dfed = nt(b, dheld, highest)
        dx = skip * dy + tn(scores * reach, dy, highest) + (tail * delta)[:, :HEAD_M] * dfed
        moved = dweight * scores * decay
        turned = moved.T
        ddelta = jnp.sum(turned, axis=1, keepdims=True)
        dtotal = jnp.sum(moved * delta.T, axis=1, keepdims=True) - ddelta * delta[:, :1]
        dtotal += jnp.sum(begun_dy * nt(c, held, highest), axis=1, keepdims=True)
        dtail = jnp.sum(dfed * x, axis=1, keepdims=True)
        ddelta += dtail * tail[:, :1]
        dtail = dtail * (tail * delta)[:, :1]
        dtotal -= dtail
        dlast = jnp.sum(dtail, axis=0, keepdims=True) + total(dheld * held * kept)
        dlog = tn(lower, jnp.broadcast_to(dtotal, (QUERY, QUERY)), highest)[:, :1] + dlast
        ddelta -= dlog * rate_scale
        dstep = ddelta * jax.nn.sigmoid(step + step_bias)
        ddt[rows, :] = dstep
        dnumbers[0:1, :] += jnp.broadcast_to(jnp.sum(dstep, axis=0, keepdims=True), (1, 128))
        dnumbers[1:2, :] -= jnp.broadcast_to(
            jnp.sum(dlog * delta[:, :1] * rate_scale, axis=0, keepdims=True), (1, 128)
        )
        dnumbers[2:3, :] += jnp.broadcast_to(total(dy * x), (1, 128))
        dstate[...] = dheld * kept + tn(begun_dy, c, highest)
        dpre_x = jnp.concatenate([dx, jnp.zeros_like(dx)], axis=1) * slope(pre_x)
        dpre = jnp.concatenate([db, dc], axis=1) * slope(pre)
        dx_pad[rows, :] = dpre_x
        dbc_pad[rows, :] = dpre
        dxr = conv_back(xz_pad, start, dx_pad, dpre_x, wx[...], dwx)
        dxz[rows, :] = jnp.concatenate([dxr[:, :HEAD_M], dz], axis=1).astype(dxz.dtype)
        dbc[rows, :] = conv_back(bc_pad, start, dbc_pad, dpre, wbc[...], dwbc).astype(dbc.dtype)
        return carry

    lax.fori_loop(0, blocks, block, 0)


def in_smem():
    return pl.BlockSpec(memory_space=pltpu.SMEM)


def in_vmem():
    return pl.BlockSpec(memory_space=pltpu.VMEM)


def mixer_forward(numbers, xz, bc, dt, marks, wx, bx, wbc, bbc):
    count = xz.shape[0]
    return pl.pallas_call(
        mixer_forward_kernel,
        out_shape=[
            jax.ShapeDtypeStruct((count, HEAD_M), FULL),
            jax.ShapeDtypeStruct((count, HEAD_M), FULL),
            jax.ShapeDtypeStruct((count // QUERY, HEAD_M, STATE), FULL),
        ],
        in_specs=[in_smem()] + [in_vmem()] * 8,
        out_specs=[in_vmem()] * 3,
        scratch_shapes=[
            pltpu.VMEM((count + 8, 2 * HEAD_M), FULL),
            pltpu.VMEM((count + 8, 2 * STATE), FULL),
            pltpu.VMEM((HEAD_M, STATE), FULL),
        ],
        compiler_params=pltpu.CompilerParams(vmem_limit_bytes=32 << 20),
        name="mixer_forward",
    )(numbers, xz, bc, dt, marks, wx, bx, wbc, bbc)


def mixer_backward(numbers, xz, bc, dt, marks, wx, bx, wbc, bbc, y, states, du):
    count = xz.shape[0]
    return pl.pallas_call(
        mixer_backward_kernel,
        out_shape=[
            jax.ShapeDtypeStruct((count, 2 * HEAD_M), LOW),
            jax.ShapeDtypeStruct((count, 2 * STATE), LOW),
            jax.ShapeDtypeStruct((count, 1), FULL),
            jax.ShapeDtypeStruct((8, 2 * HEAD_M), FULL),
            jax.ShapeDtypeStruct((8, 2 * STATE), FULL),
            jax.ShapeDtypeStruct((8, 128), FULL),
        ],
        in_specs=[in_smem()] + [in_vmem()] * 11,
        out_specs=[in_vmem()] * 6,
        scratch_shapes=[
            pltpu.VMEM((count + 8, 2 * HEAD_M), FULL),
            pltpu.VMEM((count + 8, 2 * STATE), FULL),
            pltpu.VMEM((count + 8, 2 * HEAD_M), FULL),
            pltpu.VMEM((count + 8, 2 * STATE), FULL),
            pltpu.VMEM((HEAD_M, STATE), FULL),
        ],
        compiler_params=pltpu.CompilerParams(vmem_limit_bytes=32 << 20),
        name="mixer_backward",
    )(numbers, xz, bc, dt, marks, wx, bx, wbc, bbc, y, states, du)


def patch_causal():
    row = lax.broadcasted_iota(jnp.int32, (BYTE_BLOCK, BYTE_BLOCK), 0)
    column = lax.broadcasted_iota(jnp.int32, (BYTE_BLOCK, BYTE_BLOCK), 1)
    return (lax.div(row, PATCH) == lax.div(column, PATCH)) & (row >= column)


def head_probs(q, k, causal):
    scores = jnp.where(causal, nt(q, k) * HEAD_A ** (-0.5), masked_score)
    grown = jnp.exp(scores - jnp.max(scores, axis=1, keepdims=True))
    return grown / jnp.sum(grown, axis=1, keepdims=True)


def of_head(block, half):
    lane = lax.broadcasted_iota(jnp.int32, block.shape, 1)
    return jnp.where(lax.div(lane, HEAD_A) == half, block, jnp.zeros_like(block))


def attend_kernel(q_ref, k_ref, v_ref, out):
    causal = patch_causal()
    for first in range(0, q_ref.shape[0], BYTE_BLOCK):
        rows = pl.ds(first, BYTE_BLOCK)
        q, k, v = q_ref[rows, :], k_ref[rows, :], v_ref[rows, :]
        mixed = jnp.zeros(q.shape, FULL)
        for half in range(2):
            probs = head_probs(of_head(q, half), k, causal)
            mixed += nn(probs.astype(LOW), of_head(v, half))
        out[rows, :] = mixed.astype(LOW)


def attend_back_kernel(q_ref, k_ref, v_ref, g_ref, dq_out, dk_out, dv_out):
    causal = patch_causal()
    scale = HEAD_A ** (-0.5)
    for first in range(0, q_ref.shape[0], BYTE_BLOCK):
        rows = pl.ds(first, BYTE_BLOCK)
        q, k, v, g = q_ref[rows, :], k_ref[rows, :], v_ref[rows, :], g_ref[rows, :]
        dq = jnp.zeros(q.shape, FULL)
        dk = jnp.zeros(q.shape, FULL)
        dv = jnp.zeros(q.shape, FULL)
        for half in range(2):
            own_q, own_k, own_g = of_head(q, half), of_head(k, half), of_head(g, half)
            probs = head_probs(own_q, k, causal)
            dprobs = nt(own_g, v)
            dv += tn(probs.astype(LOW), own_g)
            dscores = probs * (dprobs - jnp.sum(probs * dprobs, axis=1, keepdims=True))
            dscores = dscores.astype(LOW)
            dq += nn(dscores, own_k)
            dk += tn(dscores, own_q)
        dq_out[rows, :] = (dq * scale).astype(LOW)
        dk_out[rows, :] = (dk * scale).astype(LOW)
        dv_out[rows, :] = dv.astype(LOW)


def attend_heads(qkv):
    rows = qkv.shape[0]
    pairs = HEADS_A // 2

    def spec(offset):
        return pl.BlockSpec((rows, 2 * HEAD_A), lambda i: (0, i + offset))

    return pl.pallas_call(
        attend_kernel,
        grid=(pairs,),
        out_shape=jax.ShapeDtypeStruct((rows, D), LOW),
        in_specs=[spec(0), spec(pairs), spec(2 * pairs)],
        out_specs=spec(0),
        name="attend",
    )(qkv, qkv, qkv)


def attend_heads_back(qkv, heads_grad):
    rows = qkv.shape[0]
    pairs = HEADS_A // 2

    def spec(offset):
        return pl.BlockSpec((rows, 2 * HEAD_A), lambda i: (0, i + offset))

    return pl.pallas_call(
        attend_back_kernel,
        grid=(pairs,),
        out_shape=[jax.ShapeDtypeStruct((rows, D), LOW)] * 3,
        in_specs=[spec(0), spec(pairs), spec(2 * pairs), spec(0)],
        out_specs=[spec(0)] * 3,
        name="attend_back",
    )(qkv, qkv, qkv, heads_grad)


def feed_kernel(
    narrow,
    x_in,
    *refs,
):
    g_ins = refs[:narrow]
    w_in, f_out, gx_out, grads, w, x, g, hid, gg, gu, sent, got = refs[narrow : narrow + 12]
    w_sem, g_sem, x_sem, x_send, x_recv, r_send, r_recv = refs[narrow + 12 :]
    n, wide_place = lax.axis_index("narrow"), lax.axis_index("wide")
    barrier = pltpu.get_barrier_semaphore()
    for k in range(1, narrow):
        peer = (lax.rem(n + k, narrow), wide_place)
        pl.semaphore_signal(barrier, inc=1, device_id=peer, device_id_type=MESH)
    own_x = pltpu.make_async_copy(x_in, x.at[0], x_sem)
    own_x.start()
    g_copies = [pltpu.make_async_copy(g_ins[k], g.at[k], g_sem.at[k]) for k in range(narrow)]
    w_copies = [pltpu.make_async_copy(w_in.at[:, i], w.at[i], w_sem.at[i]) for i in range(3)]
    g_copies[0].start()
    for copy in w_copies:
        copy.start()
    for copy in g_copies[1:]:
        copy.start()
    pl.semaphore_wait(barrier, narrow - 1)

    def x_copy(k):
        return pltpu.make_async_remote_copy(
            src_ref=x_in,
            dst_ref=x.at[k],
            send_sem=x_send.at[k - 1],
            recv_sem=x_recv.at[k - 1],
            device_id=(lax.rem(n + narrow - k, narrow), wide_place),
            device_id_type=MESH,
        )

    def r_copy(k):
        return pltpu.make_async_remote_copy(
            src_ref=sent.at[k - 1],
            dst_ref=got.at[k - 1],
            send_sem=r_send.at[k - 1],
            recv_sem=r_recv.at[k - 1],
            device_id=(lax.rem(n + k, narrow), wide_place),
            device_id_type=MESH,
        )

    for k in range(1, narrow):
        x_copy(k).start()
    own_x.wait()
    for copy in w_copies:
        copy.wait()
    for copy in g_copies:
        copy.wait()
    rows, width = x_in.shape
    places, share = w.shape[1], w.shape[2]
    hidden = places * share
    chunk = 2 * share

    def weights(i, start):
        return w[i, pl.ds(start, 2)].reshape(chunk, width)

    def columns(i, first):
        return w[i, :, :, first : first + chunk].reshape(hidden, chunk)

    def block(k, carry):
        @pl.when(k > 0)
        def _():
            x_copy(k).wait_recv()

        xk, gk = x[k], g[k]
        for place in range(0, places, 2):
            units = slice(place * share, place * share + chunk)
            gate = nt(xk, weights(0, place))
            up = nt(xk, weights(1, place))
            dhid = nt(gk, weights(2, place))
            s = jax.nn.sigmoid(gate)
            act = gate * s
            hid[k, :, units] = (act * up).astype(LOW)
            gg[k, :, units] = (dhid * up * s * (1.0 + gate * (1.0 - s))).astype(LOW)
            gu[k, :, units] = (dhid * act).astype(LOW)
        ggk, guk, hidk = gg[k], gu[k], hid[k]
        for first in range(0, width, chunk):
            gx = nn(ggk, columns(0, first)) + nn(guk, columns(1, first))

            @pl.when(k == 0)
            def _():
                gx_out[:, first : first + chunk] = gx

            @pl.when(k > 0)
            def _():
                sent[k - 1, :, first : first + chunk] = gx.astype(LOW)

        @pl.when(k > 0)
        def _():
            r_copy(k).start()

        for first in range(0, width, chunk):
            f_out[k, :, first : first + chunk] = nn(hidk, columns(2, first)).astype(LOW)
        return carry

    lax.fori_loop(0, narrow, block, 0)

    def weight_grads(place, carry):
        units = pl.ds(pl.multiple_of(place * share, share), share)
        for i, (left, right) in enumerate(((gg, x), (gu, x), (hid, g))):
            lhs = left[:, :, units].reshape(narrow * rows, share)
            for first in range(0, width, 2 * chunk):
                rhs = right[:, :, first : first + 2 * chunk].reshape(narrow * rows, 2 * chunk)
                grads[place, i, :, first : first + 2 * chunk] = tn(lhs, rhs).astype(LOW)
        return carry

    lax.fori_loop(0, places, weight_grads, 0)
    for k in range(1, narrow):
        r_copy(k).wait_recv()
        gx_out[...] += got[k - 1].astype(FULL)
    for k in range(1, narrow):
        x_copy(k).wait_send()
        r_copy(k).wait_send()


def feed_forward_back(x_own, g_blocks, feed_all, collective_id):
    narrow = len(g_blocks)
    rows, width = x_own.shape
    places, _, share, _ = feed_all.shape
    dma = pltpu.SemaphoreType.DMA
    anywhere = pl.BlockSpec(memory_space=pl.ANY)

    def rows_scratch(count, columns):
        return pltpu.VMEM((count, rows, columns), LOW)

    hidden = places * share
    return pl.pallas_call(
        partial(feed_kernel, narrow),
        out_shape=[
            jax.ShapeDtypeStruct((narrow, rows, width), LOW),
            jax.ShapeDtypeStruct((rows, width), FULL),
            jax.ShapeDtypeStruct(feed_all.shape, LOW),
        ],
        in_specs=[anywhere] * (narrow + 2),
        out_specs=[in_vmem()] * 3,
        scratch_shapes=[
            pltpu.VMEM((3, places, share, width), LOW),
            rows_scratch(narrow, width),
            rows_scratch(narrow, width),
            rows_scratch(narrow, hidden),
            rows_scratch(narrow, hidden),
            rows_scratch(narrow, hidden),
            rows_scratch(narrow - 1, width),
            rows_scratch(narrow - 1, width),
            dma((3,)),
            dma((narrow,)),
            dma,
            dma((narrow - 1,)),
            dma((narrow - 1,)),
            dma((narrow - 1,)),
            dma((narrow - 1,)),
        ],
        compiler_params=pltpu.CompilerParams(
            collective_id=collective_id, has_side_effects=True, vmem_limit_bytes=56 << 20
        ),
        name="feed",
    )(x_own, *g_blocks, feed_all)


def per_device_heads(
    byte_ids,
    doc_patches,
    pad_bytes,
    byte_table,
    patch_weight,
    gain_mix,
    in_weight,
    conv_weight,
    conv_bias,
    step_bias,
    log_rate,
    skip_gain,
    gated_gain,
    out_weight,
    local_weight,
    gain_attn,
    query_weight,
    key_weight,
    value_weight,
    attn_weight,
    feed_gain,
    gate_weight,
    up_weight,
    down_weight,
    cotangent,
):
    narrow, wide = lax.axis_size("narrow"), lax.axis_size("wide")
    devices = narrow * wide
    device = lax.axis_index(BOTH)
    rows = byte_ids.shape[0]
    patches = rows // PATCH
    everything = devices * patches
    own_rows = patch_weight.shape[0]
    hidden_width = gate_weight.shape[1]
    share = hidden_width // narrow

    segment, _, keep_all = patch_layout(doc_patches, pad_bytes, 0, everything)
    keep_all = keep_all.reshape(everything, PATCH)
    place = jnp.arange(everything)
    mark_columns = [segment.astype(FULL)]
    for lag in range(1, CONV):
        earlier = jnp.concatenate([jnp.full((lag,), -1, jnp.int32), segment[:-lag]])
        mark_columns.append((earlier == segment).astype(FULL))
    by_block = segment.reshape(-1, QUERY)
    before = jnp.concatenate([jnp.full((1,), -1, jnp.int32), by_block[:-1, -1]])
    mark_columns.append((by_block == before[:, None]).astype(FULL).reshape(-1))
    mark_columns.append((by_block == by_block[:, -1:]).astype(FULL).reshape(-1))
    mark_columns.append(
        jnp.broadcast_to((by_block[:, -1:] == before[:, None]).astype(FULL), by_block.shape).reshape(-1)
    )
    mark_columns.append(jnp.zeros((everything,), FULL))
    marks = jnp.pad(jnp.stack(mark_columns, axis=1), ((0, 8), (0, 0)))
    keep_rows = lax.dynamic_slice_in_dim(keep_all, device * patches, patches).reshape(-1)

    ids_low = byte_ids.astype(LOW).reshape(patches, PATCH)
    bcdt_width = 2 * STATE + HEADS_M
    start_pack = jnp.concatenate(
        [
            patch_weight,
            jnp.pad(in_weight[:, 2 * DI :], ((0, 0), (0, 96))),
            jnp.pad(ids_low, ((0, 0), (0, 120))),
        ],
        axis=1,
    )
    xz_blocks = jnp.concatenate(
        [
            in_weight[:, DI : 2 * DI].reshape(own_rows, HEADS_M, HEAD_M),
            in_weight[:, :DI].reshape(own_rows, HEADS_M, HEAD_M),
        ],
        axis=2,
    ).transpose(1, 0, 2)
    xz_weight = exchange(xz_blocks, BOTH).reshape(D, 2 * HEAD_M)
    start_all, table_all = gather_all([start_pack, byte_table], 0)
    middle_pack = jnp.concatenate(
        [
            query_weight,
            key_weight,
            value_weight,
            attn_weight,
            out_weight[:own_rows],
            out_weight[own_rows:],
            local_weight.T,
        ],
        axis=1,
    )
    middle_all = lax.all_gather(middle_pack, BOTH, axis=0, tiled=True)
    feed_blocks = jnp.stack(
        [
            gate_weight.T.reshape(narrow, share, -1),
            up_weight.T.reshape(narrow, share, -1),
            down_weight.reshape(narrow, share, -1),
        ],
        axis=1,
    )
    feed_turned = exchange(feed_blocks, "narrow").transpose(1, 2, 0, 3).reshape(3, share, D)
    feed_all = lax.all_gather(feed_turned, "wide")
    in_all = lax.all_gather(in_weight, BOTH, axis=0, tiled=True)

    patch_all = start_all[:, :D]
    bcdt_weight = start_all[:, D : D + bcdt_width]
    ids_all = start_all[:, D + 384 : D + 384 + PATCH].astype(jnp.int32)

    vocabulary = jnp.arange(VOCAB, dtype=jnp.int32)
    onehot = (ids_all[:, :, None] == vocabulary).astype(LOW) * keep_all[:, :, None].astype(LOW)
    embedded = (
        jnp.dot(onehot.reshape(everything * PATCH, VOCAB), table_all, preferred_element_type=FULL)
        .astype(LOW)
        .reshape(everything, D)
    )
    mixed_all = jnp.dot(embedded, patch_all, preferred_element_type=FULL)
    normed_all = root_norm(mixed_all, gain_mix).astype(LOW)
    xz = jnp.dot(normed_all, xz_weight, preferred_element_type=FULL).astype(LOW)
    bcdt = jnp.dot(normed_all, bcdt_weight, preferred_element_type=FULL).astype(LOW)
    bc = bcdt[:, : 2 * STATE]
    dt = lax.dynamic_slice_in_dim(bcdt[:, 2 * STATE :], device, 1, axis=1).astype(FULL)
    mixed_in = lax.dynamic_slice_in_dim(mixed_all, device * patches, patches)

    conv_x = lax.dynamic_slice_in_dim(conv_weight, device * HEAD_M, HEAD_M, axis=1)
    bias_x = lax.dynamic_slice_in_dim(conv_bias, device * HEAD_M, HEAD_M)[None]
    conv_x = jnp.pad(conv_x, ((0, 0), (0, HEAD_M)))
    bias_x = jnp.pad(bias_x, ((0, 0), (0, HEAD_M)))
    conv_bc = conv_weight[:, DI:]
    bias_bc = conv_bias[None, DI:]

    def own(values):
        return lax.dynamic_index_in_dim(values, device, 0, False)

    numbers = jnp.stack([own(step_bias), jnp.exp(own(log_rate)), own(skip_gain)])
    mixer_args = (numbers, xz, bc, dt, marks, conv_x, bias_x, conv_bc, bias_bc)
    u, y, states = mixer_forward(*mixer_args)
    u_blocks = exchange(u.astype(LOW).reshape(devices, patches, HEAD_M), BOTH)
    gated_rows = u_blocks.transpose(1, 0, 2).reshape(patches, DI).astype(FULL)
    gated_scale = lax.rsqrt(jnp.mean(gated_rows * gated_rows, axis=-1, keepdims=True) + epsilon)
    gated_low = (gated_rows * gated_scale * gated_gain).astype(LOW)

    out_all = (
        middle_all[:, 4 * D : 6 * D]
        .reshape(devices, own_rows, 2, D)
        .transpose(0, 2, 1, 3)
        .reshape(DI, D)
    )
    local_all = middle_all[:, 6 * D :]
    qkv_all = middle_all[:, : 3 * D]
    attn_all = middle_all[:, 3 * D : 4 * D]
    global_out = mixed_in + jnp.dot(gated_low, out_all, preferred_element_type=FULL)

    local_rows = global_out.astype(LOW).reshape(rows, EMB)
    stream = nt(local_rows, local_all)
    normed_attn = root_norm(stream, gain_attn).astype(LOW)
    qkv = jnp.dot(normed_attn, qkv_all, preferred_element_type=FULL).astype(LOW)
    mixed_heads = attend_heads(qkv)
    after_attn = stream + jnp.dot(mixed_heads, attn_all, preferred_element_type=FULL)
    normed_feed = root_norm(after_attn, feed_gain).astype(LOW)
    out_grad = cotangent.astype(FULL) * keep_rows[:, None]
    feed_grad = out_grad.astype(LOW)

    def passed_narrow(values, by):
        pairs = [(i, (i + by) % narrow) for i in range(narrow)]
        return lax.ppermute(values, "narrow", pairs)

    g_blocks = [feed_grad] + [passed_narrow(feed_grad, narrow - k) for k in range(1, narrow)]
    feed_parts, feed_in_grad, feed_grads = feed_forward_back(normed_feed, g_blocks, feed_all, 2)
    feed_out = feed_parts[0].astype(FULL)
    for k in range(1, narrow):
        feed_out = feed_out + passed_narrow(feed_parts[k], k).astype(FULL)
    feed_sums = lax.psum_scatter(
        feed_grads.reshape(-1, D), "wide", scatter_dimension=0, tiled=True
    )
    feed_sums = feed_sums.reshape(3, share, narrow, D // narrow).transpose(2, 0, 1, 3)
    feed_sums = exchange(feed_sums, "narrow").transpose(1, 0, 2, 3).astype(FULL)
    feed_sums = feed_sums.reshape(3, hidden_width, D // narrow)
    grad_gate, grad_up, grad_down = feed_sums[0].T, feed_sums[1].T, feed_sums[2]
    out_rows = ((after_attn + feed_out.astype(LOW).astype(FULL)) * keep_rows[:, None]).astype(LOW)

    _, feed_norm_back = jax.vjp(root_norm, after_attn, feed_gain)
    after_norm_grad, grad_feed_gain = feed_norm_back(feed_in_grad.astype(LOW).astype(FULL))
    after_grad = out_grad + after_norm_grad
    attn_grad = after_grad.astype(LOW)
    heads_grad = nt(attn_grad, attn_all).astype(LOW)
    query_grad, key_grad, value_grad = attend_heads_back(qkv, heads_grad)
    qkv_grad = jnp.concatenate([query_grad, key_grad, value_grad], axis=1)
    normed_grad = nt(qkv_grad, qkv_all)
    _, attn_norm_back = jax.vjp(root_norm, stream, gain_attn)
    stream_norm_grad, grad_gain_attn = attn_norm_back(normed_grad)
    stream_grad = (after_grad + stream_norm_grad).astype(LOW)
    middle_grads = jnp.concatenate(
        [tn(normed_attn, qkv_grad), tn(mixed_heads, attn_grad), tn(stream_grad, local_rows)], axis=1
    ).astype(LOW)
    middle_sums = lax.psum_scatter(middle_grads, BOTH, scatter_dimension=0, tiled=True).astype(FULL)
    global_grad = nn(stream_grad, local_all).reshape(patches, D)

    mix_grad = global_grad.astype(LOW)
    gated_grad = nt(mix_grad, out_all)
    _, gated_back = jax.vjp(root_norm, gated_rows, gated_gain)
    gated_rows_grad, grad_gated_gain = gated_back(gated_grad)
    du_blocks = gated_rows_grad.astype(LOW).reshape(patches, devices, HEAD_M).transpose(1, 0, 2)
    du = exchange(du_blocks, BOTH).reshape(everything, HEAD_M)
    dxz, dbc, ddt, dwx, dwbc, dnumbers = mixer_backward(*mixer_args, y, states, du)
    grad_xz = tn(normed_all, dxz).astype(LOW).reshape(devices, own_rows, 2 * HEAD_M)
    grad_xz = exchange(grad_xz, BOTH).astype(FULL).transpose(1, 0, 2)
    proj_blocks = jnp.concatenate(
        [dxz, dbc, jnp.pad(ddt.astype(LOW), ((0, 0), (0, 127)))], axis=1
    ).reshape(devices, patches, 4 * STATE)
    proj_blocks = exchange(proj_blocks, BOTH)
    xz_grad = proj_blocks[:, :, :STATE].transpose(1, 0, 2)
    bc_grad = jnp.sum(proj_blocks[:, :, STATE : 3 * STATE].astype(FULL), axis=0).astype(LOW)
    bcdt_grad = jnp.concatenate([bc_grad, proj_blocks[:, :, 3 * STATE].T], axis=1)
    proj_low = jnp.concatenate(
        [
            xz_grad[:, :, HEAD_M:].reshape(patches, DI),
            xz_grad[:, :, :HEAD_M].reshape(patches, DI),
            bcdt_grad,
        ],
        axis=1,
    )
    normed_mix_grad = nt(proj_low, in_all)
    _, mix_norm_back = jax.vjp(root_norm, mixed_in, gain_mix)
    mixed_norm_grad, grad_gain_mix = mix_norm_back(normed_mix_grad)
    embed_grad = (global_grad + mixed_norm_grad).astype(LOW)

    end_pack = jnp.concatenate(
        [
            embed_grad,
            mix_grad,
            jnp.pad(bcdt_grad, ((0, 0), (0, 96))),
            jnp.broadcast_to(gated_scale.astype(LOW), (patches, 128)),
        ],
        axis=1,
    )
    sums_pack = jnp.concatenate(
        [
            grad_gain_mix,
            grad_gated_gain,
            grad_gain_attn,
            grad_feed_gain,
            dwbc[: CONV + 1].reshape(-1),
            dwx[: CONV + 1, :HEAD_M].reshape(-1),
            dnumbers[:3, 0],
        ]
    )
    sums_width = -(-sums_pack.shape[0] // 1024) * 1024
    sums_pack = jnp.pad(sums_pack, (0, sums_width - sums_pack.shape[0])).reshape(-1, 128)
    end_all, sums_all = gather_all([end_pack, sums_pack], 1)
    sums_all = sums_all.reshape(devices, sums_width)
    embed_grad_all = end_all[:, :D]
    mix_grad_all = end_all[:, D : 2 * D]
    bcdt_grad_all = end_all[:, 2 * D : 2 * D + bcdt_width]
    scale_all = end_all[:, 2 * D + 384 : 2 * D + 385].astype(FULL)
    gain_own = lax.dynamic_slice_in_dim(gated_gain, device * HEAD_M, HEAD_M)
    grad_out = tn((u * scale_all * gain_own).astype(LOW), mix_grad_all)
    normed_own = lax.dynamic_slice_in_dim(normed_all, device * own_rows, own_rows, axis=1)
    grad_bcdt = tn(normed_own, bcdt_grad_all)
    grad_in = jnp.concatenate(
        [
            grad_xz[:, :, HEAD_M:].reshape(own_rows, DI),
            grad_xz[:, :, :HEAD_M].reshape(own_rows, DI),
            grad_bcdt,
        ],
        axis=1,
    )
    embedded_own = lax.dynamic_slice_in_dim(embedded, device * own_rows, own_rows, axis=1)
    grad_patch = tn(embedded_own, embed_grad_all)
    own_words = byte_table.shape[0]
    words = device * own_words + jnp.arange(own_words, dtype=jnp.int32)
    chosen = (ids_all[:, :, None] == words).astype(LOW) * keep_all[:, :, None].astype(LOW)
    word_sums = tn(chosen.reshape(everything, PATCH * own_words), embed_grad_all)
    grad_table = jnp.einsum(
        "kvd,ked->ve",
        word_sums.reshape(PATCH, own_words, D),
        patch_all.astype(FULL).reshape(PATCH, EMB, D),
        precision=highest,
    )

    owned = 3 * D + DI + (CONV + 1) * 2 * STATE
    small = jnp.sum(sums_all[:, :owned], axis=0)
    gain_grads = jnp.split(small[: 3 * D + DI], [D, D + DI, 2 * D + DI])
    conv_own = sums_all[:, owned : owned + (CONV + 1) * HEAD_M].reshape(devices, CONV + 1, HEAD_M)
    conv_grads = jnp.concatenate(
        [
            conv_own.transpose(1, 0, 2).reshape(CONV + 1, DI),
            small[3 * D + DI :].reshape(CONV + 1, 2 * STATE),
        ],
        axis=1,
    )
    number_grads = sums_all[:, owned + (CONV + 1) * HEAD_M : owned + (CONV + 1) * HEAD_M + 3].T
    return (
        out_rows,
        grad_table,
        grad_patch,
        gain_grads[0],
        grad_in,
        conv_grads[:CONV],
        conv_grads[CONV],
        number_grads[0],
        number_grads[1],
        number_grads[2],
        gain_grads[1],
        grad_out,
        middle_sums[:, 4 * D :].T,
        gain_grads[2],
        middle_sums[:, :D],
        middle_sums[:, D : 2 * D],
        middle_sums[:, 2 * D : 3 * D],
        middle_sums[:, 3 * D : 4 * D],
        gain_grads[3],
        grad_gate,
        grad_up,
        grad_down,
    )


def solution(mesh):
    placed = (
        P(("narrow", "wide")),
        P(),
        P(),
        P(("narrow", "wide"), None),
        P(("narrow", "wide"), None),
        P(),
        P(("narrow", "wide"), None),
        P(),
        P(),
        P(),
        P(),
        P(),
        P(),
        P(("narrow", "wide"), None),
        P(None, ("narrow", "wide")),
        P(),
        P(("narrow", "wide"), None),
        P(("narrow", "wide"), None),
        P(("narrow", "wide"), None),
        P(("narrow", "wide"), None),
        P(),
        P("narrow", "wide"),
        P("narrow", "wide"),
        P("wide", "narrow"),
        P(("narrow", "wide"), None),
    )
    return jax.shard_map(
        per_device_heads if mesh.size == HEADS_M else per_device_rows,
        mesh=mesh,
        in_specs=placed,
        out_specs=(
            P(("narrow", "wide"), None),
            P(("narrow", "wide"), None),
            P(("narrow", "wide"), None),
            P(),
            P(("narrow", "wide"), None),
            P(),
            P(),
            P(),
            P(),
            P(),
            P(),
            P(("narrow", "wide"), None),
            P(None, ("narrow", "wide")),
            P(),
            P(("narrow", "wide"), None),
            P(("narrow", "wide"), None),
            P(("narrow", "wide"), None),
            P(("narrow", "wide"), None),
            P(),
            P("narrow", "wide"),
            P("narrow", "wide"),
            P("wide", "narrow"),
        ),
        check_vma=False,
    )
```

```python
from functools import partial

import jax
import jax.numpy as jnp
from jax import lax
from jax.experimental import pallas as pl
from jax.experimental.pallas import tpu as pltpu
from jax.sharding import PartitionSpec as P

NARROW = "narrow"
WIDE = "wide"
D = 1024
PATCH = 8
EMB = 128
VOCAB = 256
HEADS_M = 32
HEAD_M = 64
DI = 2048
STATE = 128
CONV = 4
HEADS_A = 16
HEAD_A = 64


epsilon = 1e-05
highest = lax.Precision.HIGHEST
masked_score = -1e30


def running_sum(x):
    place = jnp.arange(x.shape[0])
    seen = place[:, None] >= place[None, :]
    if x.ndim == 1:
        return jnp.sum(jnp.where(seen, x[None, :], 0), axis=1).astype(x.dtype)
    return jnp.dot(seen.astype(x.dtype), x, precision=highest)


def passed_along(x, axis, by):
    peers = lax.axis_size(axis)
    pairs = [(i, i + by) for i in range(peers) if 0 <= i + by < peers]
    return lax.ppermute(x, axis, pairs)


def prefix_2(x, axis, join, neutral):
    place = lax.axis_index(axis)
    gathered = jax.tree.map(
        lambda a, kind: lax.all_gather(a.astype(kind), axis), x, (jnp.bfloat16, jnp.bfloat16)
    )
    state = jax.tree.map(lambda a, e: jnp.zeros_like(a) + jnp.asarray(e, a.dtype), x, neutral)

    def prefix_one(hop, state):
        return join(
            state,
            jax.tree.map(
                lambda a, own: lax.dynamic_index_in_dim(a, hop, 0, False).astype(own.dtype),
                gathered,
                x,
            ),
        )

    return lax.fori_loop(0, place, prefix_one, state)


def carried_in_2(x, axis, join, neutral):
    count = lax.axis_size(axis)
    place = lax.axis_index(axis)
    ahead = count - 1 - place
    gathered = jax.tree.map(
        lambda a, kind: lax.all_gather(a.astype(kind), axis),
        x,
        jax.tree.map(lambda a: jnp.bfloat16 if a.dtype == jnp.float32 else a.dtype, x),
    )
    state = jax.tree.map(lambda a, e: jnp.zeros_like(a) + jnp.asarray(e, a.dtype), x, neutral)

    def carried_one(hop, state):
        source = count - 1 - hop
        return join(
            state,
            jax.tree.map(
                lambda a, own: lax.dynamic_index_in_dim(a, source, 0, False).astype(own.dtype),
                gathered,
                x,
            ),
        )

    return lax.fori_loop(0, ahead, carried_one, state)


def root_norm(values, gain):
    return values * lax.rsqrt(jnp.mean(values * values, axis=-1, keepdims=True) + epsilon) * gain


def patch_layout(doc_patches, pad_bytes, first_index, patch_count):
    patch_index = first_index + jnp.arange(patch_count, dtype=jnp.int32)
    doc_ends = running_sum(doc_patches)
    doc_index = jnp.arange(doc_patches.shape[0], dtype=jnp.int32)
    segment = jnp.sum((patch_index[:, None] >= doc_ends[None, :]).astype(jnp.int32), axis=1)
    owner_mask = segment[:, None] == doc_index[None, :]
    last_end = jnp.sum(jnp.where(owner_mask, doc_ends[None, :] - 1, 0), axis=1)
    doc_starts = jnp.sum(jnp.where(owner_mask, (doc_ends - doc_patches)[None, :], 0), axis=1)
    pad_count = jnp.sum(jnp.where(owner_mask, pad_bytes[None, :], 0), axis=1)
    offset = jnp.arange(PATCH, dtype=jnp.int32)
    padded = (patch_index == last_end)[:, None] & (offset[None, :] >= PATCH - pad_count[:, None])
    keep_mask = 1.0 - padded.astype(jnp.float32).reshape(-1)
    return (segment, (patch_index == doc_starts).astype(jnp.int32), keep_mask)


def ssd_terms(layout, projected, rim_rows, small_params):
    conv_weight, conv_bias, step_bias, log_rate, skip_gain = small_params
    segment, rim_segment, first_patch = layout
    conv_in = projected[:, DI : 2 * DI + 2 * STATE]
    patch_count = conv_in.shape[0]
    padded = jnp.concatenate([rim_rows, conv_in], 0)
    padded_seg = jnp.concatenate([rim_segment, segment], 0)
    conv_sum = conv_bias
    for conv_tap in range(CONV):
        same_doc = (padded_seg[conv_tap : conv_tap + patch_count] == segment).astype(jnp.float32)[
            :, None
        ]
        conv_sum = (
            conv_sum + conv_weight[conv_tap] * padded[conv_tap : conv_tap + patch_count] * same_doc
        )
    activated = jax.nn.silu(conv_sum)
    values = activated[:, :DI].reshape(patch_count, HEADS_M, HEAD_M)
    input_map = activated[:, DI : DI + STATE]
    output_map = activated[:, DI + STATE :]
    time_steps = jax.nn.softplus(projected[:, 2 * DI + 2 * STATE :] + step_bias)
    cumulative = running_sum(-time_steps * jnp.exp(log_rate))
    no_reset = (running_sum(first_patch) == 0).astype(jnp.float32)
    return (values, input_map, output_map, time_steps, cumulative, no_reset)


def local_state(layout, projected, rim_rows, small_params):
    values, input_map, output_map, time_steps, cumulative, no_reset = ssd_terms(
        layout, projected, rim_rows, small_params
    )
    segment = layout[0]
    decay_tail = (
        jnp.exp(cumulative[-1][None, :] - cumulative)
        * (segment == segment[-1]).astype(jnp.float32)[:, None]
        * time_steps
    )
    state_local = jnp.einsum("sh,shp,sn->hpn", decay_tail, values, input_map, precision=highest)
    decay_total = jnp.exp(cumulative[-1]) * no_reset[-1]
    return (decay_total, state_local)


def mixer_output(layout, projected, rim_rows, small_params, incoming, gated_gain):
    values, input_map, output_map, time_steps, cumulative, no_reset = ssd_terms(
        layout, projected, rim_rows, small_params
    )
    segment = layout[0]
    patch_count = values.shape[0]
    position = jnp.arange(patch_count)
    visible = (segment[:, None] == segment[None, :]) & (position[:, None] >= position[None, :])
    log_gap = jnp.where(visible[:, :, None], cumulative[:, None, :] - cumulative[None, :, :], 0.0)
    inner = jnp.dot(output_map, input_map.T, precision=highest)
    weight = (
        jnp.exp(log_gap)
        * visible[:, :, None].astype(jnp.float32)
        * time_steps[None, :, :]
        * inner[:, :, None]
    )
    within = jnp.einsum("tsh,shp->thp", weight, values, precision=highest)
    carried_in = (
        jnp.einsum("tn,hpn->thp", output_map, incoming, precision=highest)
        * (jnp.exp(cumulative) * no_reset[:, None])[:, :, None]
    )
    result = (within + carried_in + small_params[4][None, :, None] * values).reshape(
        patch_count, DI
    )
    gated_rows = result * jax.nn.silu(projected[:, :DI])
    return root_norm(gated_rows, gated_gain)


def combine_states(earlier, following):
    return (earlier[0] * following[0], following[0][:, None, None] * earlier[1] + following[1])


def attend(stream, gain_attn, query_all, key_all, value_all):
    head_shape = (-1, PATCH, HEADS_A, HEAD_A)
    normed_attn = root_norm(stream, gain_attn).astype(jnp.bfloat16)
    queries = jnp.dot(normed_attn, query_all, preferred_element_type=jnp.float32).astype(
        jnp.bfloat16
    )
    key_rows = jnp.dot(normed_attn, key_all, preferred_element_type=jnp.float32).astype(
        jnp.bfloat16
    )
    value_rows = jnp.dot(normed_attn, value_all, preferred_element_type=jnp.float32).astype(
        jnp.bfloat16
    )
    scores = jnp.einsum(
        "pqhe,pkhe->phqk",
        queries.reshape(head_shape),
        key_rows.reshape(head_shape),
        preferred_element_type=jnp.float32,
    ) * HEAD_A ** (-0.5)
    position = jnp.arange(PATCH)
    causal = position[:, None] >= position[None, :]
    attn_probs = jax.nn.softmax(jnp.where(causal, scores, masked_score), axis=-1)
    mixed_heads = jnp.einsum(
        "phqk,pkhe->pqhe",
        attn_probs.astype(jnp.bfloat16),
        value_rows.reshape(head_shape),
        preferred_element_type=jnp.float32,
    )
    mixed_heads = mixed_heads.reshape(stream.shape[0], -1).astype(jnp.bfloat16)
    return (normed_attn, queries, key_rows, value_rows, attn_probs, mixed_heads)


def spread(values):
    by_rows = lax.all_to_all(values, NARROW, split_axis=1, concat_axis=0, tiled=True)
    return lax.all_gather(by_rows, WIDE, axis=0, tiled=True)


def collect(term_fn, row_count):
    summed = lax.psum_scatter(
        term_fn(jnp.int32(0), row_count * lax.axis_size(WIDE)).astype(jnp.bfloat16),
        WIDE,
        scatter_dimension=0,
        tiled=True,
    )
    return lax.all_to_all(summed, NARROW, split_axis=0, concat_axis=1, tiled=True)


def narrow_total(partial_rows):
    return lax.psum(partial_rows, NARROW).astype(jnp.float32)


def silu_back(gate_up, hidden_grad, hidden_width):
    gate_rows = gate_up[:, :hidden_width]
    up_rows = gate_up[:, hidden_width:]
    sigmoid = jax.nn.sigmoid(gate_rows)
    gate_grad = hidden_grad * up_rows * sigmoid * (1.0 + gate_rows * (1.0 - sigmoid))
    up_grad = hidden_grad * gate_rows * sigmoid
    return jnp.concatenate([gate_grad, up_grad], axis=1)


def per_device_rows(
    byte_ids,
    doc_patches,
    pad_bytes,
    byte_table,
    patch_weight,
    gain_mix,
    in_weight,
    conv_weight,
    conv_bias,
    step_bias,
    log_rate,
    skip_gain,
    gated_gain,
    out_weight,
    local_weight,
    gain_attn,
    query_weight,
    key_weight,
    value_weight,
    attn_weight,
    feed_gain,
    gate_weight,
    up_weight,
    down_weight,
    cotangent,
):
    byte_rows = byte_ids.shape[0]
    patches = byte_rows // PATCH
    device = lax.axis_index((NARROW, WIDE))
    wide_count = lax.axis_size(WIDE)
    segment, first_patch, keep_mask = patch_layout(
        doc_patches, pad_bytes, device * patches, patches
    )
    rim_segment = patch_layout(doc_patches, pad_bytes, device * patches - (CONV - 1), CONV - 1)[0]
    layout = (segment, rim_segment, first_patch)
    gathered = (
        lax.all_gather(byte_table, (NARROW, WIDE), axis=0, tiled=True),
        lax.all_gather(patch_weight, (NARROW, WIDE), axis=0, tiled=True),
        lax.all_gather(in_weight, (NARROW, WIDE), axis=0, tiled=True),
        lax.all_gather(out_weight, (NARROW, WIDE), axis=0, tiled=True),
        lax.all_gather(local_weight, (NARROW, WIDE), axis=1, tiled=True),
        lax.all_gather(query_weight, (NARROW, WIDE), axis=0, tiled=True),
        lax.all_gather(key_weight, (NARROW, WIDE), axis=0, tiled=True),
        lax.all_gather(value_weight, (NARROW, WIDE), axis=0, tiled=True),
        lax.all_gather(attn_weight, (NARROW, WIDE), axis=0, tiled=True),
    )
    table_all, patch_all, in_all, out_all, local_all, query_all, key_all, value_all, attn_all = (
        gathered
    )
    onehot = (byte_ids[:, None] == jnp.arange(VOCAB, dtype=jnp.int32)[None, :]).astype(jnp.bfloat16)
    embedded = (
        (jnp.dot(onehot, table_all, preferred_element_type=jnp.float32) * keep_mask[:, None])
        .astype(jnp.bfloat16)
        .reshape(patches, D)
    )
    mixed_in = jnp.dot(embedded, patch_all, preferred_element_type=jnp.float32)
    normed_mix = root_norm(mixed_in, gain_mix).astype(jnp.bfloat16)
    projected = jnp.dot(normed_mix, in_all, preferred_element_type=jnp.float32).astype(jnp.bfloat16)
    rim_rows = passed_along(
        projected[patches - (CONV - 1) :, DI : 2 * DI + 2 * STATE], (NARROW, WIDE), 1
    ).astype(jnp.float32)
    projected_f = projected.astype(jnp.float32)
    small_params = (conv_weight, conv_bias, step_bias, log_rate, skip_gain)
    (decay_total, state_local), state_back = jax.vjp(
        partial(local_state, layout), projected_f, rim_rows, small_params
    )
    prefix = prefix_2(
        (decay_total, state_local),
        (NARROW, WIDE),
        combine_states,
        (jnp.ones_like(decay_total), jnp.zeros_like(state_local)),
    )
    incoming = prefix[1]
    gated_norm, mixer_back = jax.vjp(
        partial(mixer_output, layout), projected_f, rim_rows, small_params, incoming, gated_gain
    )
    gated_low = gated_norm.astype(jnp.bfloat16)
    global_out = mixed_in + jnp.dot(gated_low, out_all, preferred_element_type=jnp.float32)
    local_rows = global_out.astype(jnp.bfloat16).reshape(byte_rows, EMB)
    stream = jnp.dot(local_rows, local_all, preferred_element_type=jnp.float32)
    normed_attn, queries, key_rows, value_rows, attn_probs, mixed_heads = attend(
        stream, gain_attn, query_all, key_all, value_all
    )
    after_attn = stream + jnp.dot(mixed_heads, attn_all, preferred_element_type=jnp.float32)
    normed_feed = root_norm(after_attn, feed_gain).astype(jnp.bfloat16)
    out_grad = cotangent.astype(jnp.float32) * keep_mask[:, None]
    feed_grad = out_grad.astype(jnp.bfloat16)
    grid_in = spread(normed_feed)
    both_weights = jnp.concatenate([gate_weight, up_weight], axis=1)
    hidden_width = gate_weight.shape[1]
    grid_share = grid_in.shape[0] // wide_count
    gate_up_part = jnp.dot(grid_in, both_weights, preferred_element_type=jnp.float32).astype(
        jnp.bfloat16
    )
    gate_up = narrow_total(gate_up_part)
    hidden = (jax.nn.silu(gate_up[:, :hidden_width]) * gate_up[:, hidden_width:]).astype(
        jnp.bfloat16
    )

    def down_term(first_row, row_count):
        return jnp.dot(hidden, down_weight, preferred_element_type=jnp.float32)

    feed_out = collect(down_term, grid_share)
    grid_grad = spread(feed_grad)
    grad_down = jnp.einsum("gf,gd->fd", hidden, grid_grad, preferred_element_type=jnp.float32)
    hidden_part = jnp.einsum(
        "gd,fd->gf", grid_grad, down_weight, preferred_element_type=jnp.float32
    ).astype(jnp.bfloat16)
    hidden_grad = narrow_total(hidden_part)
    gate_up_grad = silu_back(gate_up, hidden_grad, hidden_width).astype(jnp.bfloat16)
    grad_both = jnp.einsum("gd,gf->df", grid_in, gate_up_grad, preferred_element_type=jnp.float32)

    def back_term(first_row, row_count):
        return jnp.einsum(
            "gf,df->gd", gate_up_grad, both_weights, preferred_element_type=jnp.float32
        )

    feed_in_grad = collect(back_term, grid_share)
    grad_gate = grad_both[:, :hidden_width]
    grad_up = grad_both[:, hidden_width:]
    after_feed = after_attn + feed_out.astype(jnp.float32)
    out_rows = (after_feed * keep_mask[:, None]).astype(jnp.bfloat16)
    feed_normed, feed_norm_back = jax.vjp(root_norm, after_attn, feed_gain)
    after_norm_grad, grad_feed_gain = feed_norm_back(feed_in_grad.astype(jnp.float32))
    after_grad = out_grad + after_norm_grad
    head_shape = (-1, PATCH, HEADS_A, HEAD_A)
    score_scale = HEAD_A ** (-0.5)
    attn_grad = after_grad.astype(jnp.bfloat16)
    grad_attn = jnp.einsum("rd,re->de", mixed_heads, attn_grad, preferred_element_type=jnp.float32)
    heads_grad = (
        jnp.einsum("re,de->rd", attn_grad, attn_all, preferred_element_type=jnp.float32)
        .astype(jnp.bfloat16)
        .reshape(head_shape)
    )
    probs_grad = jnp.einsum(
        "pqhe,pkhe->phqk",
        heads_grad,
        value_rows.reshape(head_shape),
        preferred_element_type=jnp.float32,
    )
    value_grad = (
        jnp.einsum(
            "phqk,pqhe->pkhe",
            attn_probs.astype(jnp.bfloat16),
            heads_grad,
            preferred_element_type=jnp.float32,
        )
        .reshape(byte_rows, D)
        .astype(jnp.bfloat16)
    )
    score_grad = (
        attn_probs * (probs_grad - jnp.sum(attn_probs * probs_grad, axis=-1, keepdims=True))
    ).astype(jnp.bfloat16)
    query_grad = (
        (
            jnp.einsum(
                "phqk,pkhe->pqhe",
                score_grad,
                key_rows.reshape(head_shape),
                preferred_element_type=jnp.float32,
            )
            * score_scale
        )
        .reshape(byte_rows, D)
        .astype(jnp.bfloat16)
    )
    key_grad = (
        (
            jnp.einsum(
                "phqk,pqhe->pkhe",
                score_grad,
                queries.reshape(head_shape),
                preferred_element_type=jnp.float32,
            )
            * score_scale
        )
        .reshape(byte_rows, D)
        .astype(jnp.bfloat16)
    )
    grad_query = jnp.einsum(
        "rd,re->de", normed_attn, query_grad, preferred_element_type=jnp.float32
    )
    grad_key = jnp.einsum("rd,re->de", normed_attn, key_grad, preferred_element_type=jnp.float32)
    grad_value = jnp.einsum(
        "rd,re->de", normed_attn, value_grad, preferred_element_type=jnp.float32
    )
    normed_grad = jnp.einsum("re,de->rd", query_grad, query_all, preferred_element_type=jnp.float32)
    normed_grad = normed_grad + jnp.einsum(
        "re,de->rd", key_grad, key_all, preferred_element_type=jnp.float32
    )
    normed_grad = normed_grad + jnp.einsum(
        "re,de->rd", value_grad, value_all, preferred_element_type=jnp.float32
    )
    attn_normed, attn_norm_back = jax.vjp(root_norm, stream, gain_attn)
    stream_norm_grad, grad_gain_attn = attn_norm_back(normed_grad)
    stream_grad = (after_grad + stream_norm_grad).astype(jnp.bfloat16)
    grad_local = jnp.einsum(
        "re,rd->ed", local_rows, stream_grad, preferred_element_type=jnp.float32
    )
    global_grad = jnp.einsum(
        "rd,ed->re", stream_grad, local_all, preferred_element_type=jnp.float32
    ).reshape(patches, D)
    mix_grad = global_grad.astype(jnp.bfloat16)
    grad_out = jnp.einsum("pi,pd->id", gated_low, mix_grad, preferred_element_type=jnp.float32)
    gated_grad = jnp.einsum("pd,id->pi", mix_grad, out_all, preferred_element_type=jnp.float32)
    proj_grad_mix, rim_grad_mix, small_grad_mix, incoming_grad, grad_gated_gain = mixer_back(
        gated_grad
    )
    suffix = carried_in_2(
        (decay_total, incoming_grad),
        (NARROW, WIDE),
        combine_states,
        (jnp.ones_like(decay_total), jnp.zeros_like(incoming_grad)),
    )
    later_grad = suffix[1]
    decay_grad = jnp.sum(later_grad * incoming, axis=(1, 2))
    proj_grad_state, rim_grad_state, small_grad_state = state_back((decay_grad, later_grad))
    rim_from_next = passed_along(rim_grad_mix + rim_grad_state, (NARROW, WIDE), -1)
    proj_grad = proj_grad_mix + proj_grad_state
    proj_grad = proj_grad.at[patches - (CONV - 1) :, DI : 2 * DI + 2 * STATE].add(rim_from_next)
    proj_low = proj_grad.astype(jnp.bfloat16)
    grad_in = jnp.einsum("pd,pk->dk", normed_mix, proj_low, preferred_element_type=jnp.float32)
    normed_mix_grad = jnp.einsum("pk,dk->pd", proj_low, in_all, preferred_element_type=jnp.float32)
    mix_normed, mix_norm_back = jax.vjp(root_norm, mixed_in, gain_mix)
    mixed_norm_grad, grad_gain_mix = mix_norm_back(normed_mix_grad)
    embed_grad = (global_grad + mixed_norm_grad).astype(jnp.bfloat16)
    grad_patch = jnp.einsum("pi,pd->id", embedded, embed_grad, preferred_element_type=jnp.float32)
    byte_grad = (
        jnp.einsum("pd,id->pi", embed_grad, patch_all, preferred_element_type=jnp.float32).reshape(
            byte_rows, EMB
        )
        * keep_mask[:, None]
    )
    grad_table = jnp.dot(onehot.astype(jnp.float32).T, byte_grad, precision=highest)
    shared = (
        lax.psum_scatter(grad_table, (NARROW, WIDE), scatter_dimension=0, tiled=True),
        lax.psum_scatter(grad_patch, (NARROW, WIDE), scatter_dimension=0, tiled=True),
        lax.psum_scatter(grad_in, (NARROW, WIDE), scatter_dimension=0, tiled=True),
        lax.psum_scatter(grad_out, (NARROW, WIDE), scatter_dimension=0, tiled=True),
        lax.psum_scatter(grad_local, (NARROW, WIDE), scatter_dimension=1, tiled=True),
        lax.psum_scatter(grad_query, (NARROW, WIDE), scatter_dimension=0, tiled=True),
        lax.psum_scatter(grad_key, (NARROW, WIDE), scatter_dimension=0, tiled=True),
        lax.psum_scatter(grad_value, (NARROW, WIDE), scatter_dimension=0, tiled=True),
        lax.psum_scatter(grad_attn, (NARROW, WIDE), scatter_dimension=0, tiled=True),
    )
    small_sum = lax.psum(
        (
            small_grad_mix[0] + small_grad_state[0],
            small_grad_mix[1] + small_grad_state[1],
            small_grad_mix[2] + small_grad_state[2],
            small_grad_mix[3] + small_grad_state[3],
            small_grad_mix[4] + small_grad_state[4],
            grad_gain_mix,
            grad_gated_gain,
            grad_gain_attn,
            grad_feed_gain,
        ),
        (NARROW, WIDE),
    )
    return (
        out_rows,
        shared[0],
        shared[1],
        small_sum[5],
        shared[2],
        small_sum[0],
        small_sum[1],
        small_sum[2],
        small_sum[3],
        small_sum[4],
        small_sum[6],
        shared[3],
        shared[4],
        small_sum[7],
        shared[5],
        shared[6],
        shared[7],
        shared[8],
        small_sum[8],
        grad_gate,
        grad_up,
        grad_down,
    )


QUERY = 128
BYTE_BLOCK = 128
MESH = pl.DeviceIdType.MESH
LOW = jnp.bfloat16
FULL = jnp.float32
BOTH = (NARROW, WIDE)


def nn(a, b, precision=None):
    return lax.dot_general(
        a, b, (((1,), (0,)), ((), ())), precision=precision, preferred_element_type=FULL
    )


def nt(a, b, precision=None):
    return lax.dot_general(
        a, b, (((1,), (1,)), ((), ())), precision=precision, preferred_element_type=FULL
    )


def tn(a, b, precision=None):
    return lax.dot_general(
        a, b, (((0,), (0,)), ((), ())), precision=precision, preferred_element_type=FULL
    )


def device_at(place, wide):
    return (lax.div(place, wide), lax.rem(place, wide))


def remote(src, dst, send, recv, peer):
    return pltpu.make_async_remote_copy(
        src_ref=src, dst_ref=dst, send_sem=send, recv_sem=recv, device_id=peer, device_id_type=MESH
    )


def greet_all(devices, wide):
    me = lax.axis_index(NARROW) * wide + lax.axis_index(WIDE)
    barrier = pltpu.get_barrier_semaphore()

    def greet(k, carry):
        peer = device_at(lax.rem(me + k, devices), wide)
        pl.semaphore_signal(barrier, inc=1, device_id=peer, device_id_type=MESH)
        return carry

    lax.fori_loop(1, devices, greet, 0)
    return me, lambda: pl.semaphore_wait(barrier, devices - 1)


def send_blocks(me, devices, wide, src, dst, send, recv):
    def one(k, carry):
        place = lax.rem(me + k, devices)
        remote(src.at[place], dst.at[me], send, recv, device_at(place, wide)).start()
        return carry

    lax.fori_loop(1, devices, one, 0)


def wait_blocks(me, devices, wide, dst, send, recv):
    part = dst.at[pl.ds(0, devices - 1)]
    remote(part, part, send, recv, device_at(me, wide)).wait()


def gather_kernel(count, narrow, depth, last, *refs):
    if last:
        middle, feed = refs[count : count + 2]
        middle_out, feed_got = refs[2 * count + 2 : 2 * count + 4]
        middle_got, m_send, m_recv, m_sem, f_send, f_recv, f_sem = refs[-7:]
        refs = refs[:count] + refs[count + 2 : 2 * count + 2] + refs[2 * count + 4 : -7]
    ins, outs = refs[:count], refs[count : 2 * count]
    local, z_send, z_recv, n_send, n_recv, c_send, c_recv = refs[2 * count :]
    n, w = lax.axis_index(NARROW), lax.axis_index(WIDE)
    z, c = lax.div(w, 2), lax.rem(w, 2)
    z_peers = [(n, lax.rem(z + k, depth) * 2 + c) for k in range(1, depth)]
    n_peers = [lax.rem(n + k, narrow) for k in range(1, narrow)]
    twin = (n, z * 2 + 1 - c)
    barrier = pltpu.get_barrier_semaphore()
    for peer in z_peers:
        pl.semaphore_signal(barrier, inc=1, device_id=peer, device_id_type=MESH)
    for m in n_peers:
        pl.semaphore_signal(barrier, inc=1, device_id=(m, w), device_id_type=MESH)
    pl.semaphore_signal(barrier, inc=1, device_id=twin, device_id_type=MESH)
    pl.semaphore_wait(barrier, len(z_peers) + len(n_peers) + 1)

    own = [pltpu.make_async_copy(ins[i], outs[i].at[n, z, c], local.at[i]) for i in range(count)]
    for i in range(count):
        own[i].start()
        for peer in z_peers:
            remote(ins[i], outs[i].at[n, z, c], z_send.at[i], z_recv.at[i], peer).start()
    if last:
        middle_copies, feed_copies = [], []
        for k in range(1, depth):
            place = lax.rem(z + k, depth)
            middle_copies.append(
                remote(
                    middle.at[place],
                    middle_got.at[k],
                    m_send.at[k - 1],
                    m_recv.at[k - 1],
                    (n, place * 2 + c),
                )
            )
        for k in range(1, narrow):
            m = lax.rem(n + k, narrow)
            feed_copies.append(
                remote(feed.at[m], feed_got.at[n], f_send.at[k - 1], f_recv.at[k - 1], (m, w))
            )
        for copy in middle_copies + feed_copies:
            copy.start()
        own += [
            pltpu.make_async_copy(middle.at[z], middle_got.at[0], m_sem),
            pltpu.make_async_copy(feed.at[n], feed_got.at[n], f_sem),
        ]
        own[count].start()
        own[count + 1].start()
    for i in range(count):
        own[i].wait()
        part = outs[i].at[n, pl.ds(0, depth - 1), c]
        remote(part, part, z_send.at[i], z_recv.at[i], twin).wait_recv()
        mine = outs[i].at[n, :, c]
        for m in n_peers:
            remote(mine, mine, n_send.at[i], n_recv.at[i], (m, w)).start()
        remote(mine, mine, c_send.at[i], c_recv.at[i], twin).start()
    for i in range(count):
        part = outs[i].at[pl.ds(0, narrow - 1), :, c]
        remote(part, part, n_send.at[i], n_recv.at[i], twin).wait_recv()
        for m in n_peers:
            theirs = outs[i].at[m, :, c]
            remote(theirs, theirs, c_send.at[i], c_recv.at[i], twin).start()
    for i in range(count):
        half = outs[i].at[:, :, 1 - c]
        remote(half, half, c_send.at[i], c_recv.at[i], twin).wait()
        part = outs[i].at[n, pl.ds(0, depth - 1), c]
        remote(part, part, z_send.at[i], z_recv.at[i], twin).wait_send()
        part = outs[i].at[pl.ds(0, narrow - 1), :, c]
        remote(part, part, n_send.at[i], n_recv.at[i], twin).wait_send()
    if last:
        own[count].wait()
        own[count + 1].wait()
        for copy in middle_copies:
            copy.wait()
        total = middle_got[0].astype(FULL)
        for k in range(1, depth):
            total += middle_got[k].astype(FULL)
        middle_out[...] = total
        for copy in feed_copies:
            copy.wait()


def gather_all(arrays, collective_id, middle=None, feed=None):
    narrow, wide = lax.axis_size(NARROW), lax.axis_size(WIDE)
    count = len(arrays)
    dma = pltpu.SemaphoreType.DMA
    anywhere = pl.BlockSpec(memory_space=pl.ANY)
    outs = [jax.ShapeDtypeStruct((narrow, wide // 2, 2) + a.shape, a.dtype) for a in arrays]
    out_specs = [anywhere] * count
    scratch = [dma((count,))] * 7
    last = middle is not None
    if last:
        outs += [
            jax.ShapeDtypeStruct(middle.shape[1:], FULL),
            jax.ShapeDtypeStruct(feed.shape, feed.dtype),
        ]
        out_specs += [in_vmem(), anywhere]
        scratch += [pltpu.VMEM(middle.shape, middle.dtype)]
        scratch += [dma((wide // 2 - 1,))] * 2 + [dma] + [dma((narrow - 1,))] * 2 + [dma]
    outs = pl.pallas_call(
        partial(gather_kernel, count, narrow, wide // 2, last),
        out_shape=outs,
        in_specs=[anywhere] * (count + 2 * last),
        out_specs=out_specs,
        scratch_shapes=scratch,
        compiler_params=pltpu.CompilerParams(
            collective_id=collective_id, has_side_effects=True, vmem_limit_bytes=32 << 20
        ),
        name="gather_all",
    )(*arrays, *((middle, feed) if last else ()))
    gathered = [o.reshape((-1,) + a.shape[1:]) for o, a in zip(outs, arrays)]
    return gathered + list(outs[count:])


def exchange(blocks, axis):
    return lax.all_to_all(blocks, axis, split_axis=0, concat_axis=0, tiled=True)


def softplus(v):
    return jnp.maximum(v, 0.0) + jnp.log1p(jnp.exp(-jnp.abs(v)))


def convolved(window, marks, weight, bias):
    pre = bias + weight[CONV - 1 :] * window[8:]
    for lag in range(1, CONV):
        pre = pre + weight[CONV - 1 - lag : CONV - lag] * (
            window[8 - lag : 8 - lag + QUERY] * marks[:, lag : lag + 1]
        )
    return pre


def decays(marks, dt, step_bias, rate_scale):
    shape = (QUERY, QUERY)
    row = lax.broadcasted_iota(jnp.int32, shape, 0)
    column = lax.broadcasted_iota(jnp.int32, shape, 1)
    lower = (row >= column).astype(FULL)
    segment = jnp.broadcast_to(marks[:, :1], shape)
    visible = (segment == segment.T) & (row >= column)
    delta = jnp.broadcast_to(softplus(dt + step_bias), shape)
    total = nn(lower, -delta * rate_scale, highest)
    gap = jnp.where(visible, total - total.T, 0.0)
    decay = jnp.where(visible, jnp.exp(gap), 0.0)
    last = total[QUERY - 1 :, :]
    begun = jnp.exp(total) * marks[:, 4:5]
    tail = jnp.exp(last - total) * marks[:, 5:6]
    kept = jnp.exp(last) * marks[:1, 6:7]
    return lower, delta, decay, begun, tail, kept


def mixer_forward_kernel(
    numbers, xz, bc, dt, marks, wx, bx, wbc, bbc, u_out, y_out, states, xz_pad, bc_pad, state
):
    count = xz.shape[0]
    xz_pad[pl.ds(0, 8), :] = jnp.zeros((8, xz_pad.shape[1]), FULL)
    bc_pad[pl.ds(0, 8), :] = jnp.zeros((8, bc_pad.shape[1]), FULL)
    state[...] = jnp.zeros_like(state)
    step_bias, rate_scale, skip = numbers[0], numbers[1], numbers[2]

    xz_pad[pl.ds(8, count), :] = xz[...].astype(FULL)
    bc_pad[pl.ds(8, count), :] = bc[...].astype(FULL)

    def block(i, carry):
        start = pl.multiple_of(i * QUERY, QUERY)
        rows = pl.ds(start, QUERY)
        mark = marks[rows, :]
        act_x = jax.nn.silu(convolved(xz_pad[pl.ds(start, QUERY + 8), :], mark, wx[...], bx[...]))
        act = jax.nn.silu(convolved(bc_pad[pl.ds(start, QUERY + 8), :], mark, wbc[...], bbc[...]))
        x, b, c = act_x[:, :HEAD_M], act[:, :STATE], act[:, STATE:]
        lower, delta, decay, begun, tail, kept = decays(mark, dt[rows, :], step_bias, rate_scale)
        weight = nt(c, b, highest) * decay * delta.T
        held = state[...]
        states[i] = held
        y = (
            nn(weight, x, highest)
            + nt(c, held, highest) * begun[:, :HEAD_M]
            + skip * x
        )
        state[...] = held * kept + tn(x * (tail * delta)[:, :HEAD_M], b, highest)
        z = xz[rows, :].astype(FULL)[:, HEAD_M:]
        y_out[rows, :] = y
        u_out[rows, :] = y * jax.nn.silu(z)
        return carry

    lax.fori_loop(0, count // QUERY, block, 0)


def mixer_backward_kernel(
    narrow,
    wide,
    numbers,
    xz,
    bc,
    dt,
    marks,
    wx,
    bx,
    wbc,
    bbc,
    y_in,
    states,
    normed,
    w_xz,
    w_bcdt,
    du_blocks,
    feed_parts,
    middle_parts,
    dwx,
    dwbc,
    dnumbers,
    rows_grad,
    xz_grads,
    feed_sums,
    middle_sums,
    xz_pad,
    bc_pad,
    dx_pad,
    dbc_pad,
    dstate,
    du_got,
    dxz,
    dbcdt,
    partial_rows,
    core_got,
    narrow_got,
    z_rows,
    z_got,
    grads,
    grads_got,
    feed_got,
    middle_got,
    du_send,
    du_recv,
    core_send,
    core_recv,
    narrow_send,
    narrow_recv,
    z_send,
    z_recv,
    grads_send,
    grads_recv,
    feed_send,
    feed_recv,
    feed_sem,
    middle_send,
    middle_recv,
    middle_sem,
):
    devices = narrow * wide
    depth = wide // 2
    me, arrived = greet_all(devices, wide)
    n, w = lax.axis_index(NARROW), lax.axis_index(WIDE)
    z_place, core = lax.div(w, 2), lax.rem(w, 2)
    twin = (n, z_place * 2 + 1 - core)
    count = xz.shape[0]
    blocks = count // QUERY
    xz_pad[pl.ds(0, 8), :] = jnp.zeros((8, xz_pad.shape[1]), FULL)
    bc_pad[pl.ds(0, 8), :] = jnp.zeros((8, bc_pad.shape[1]), FULL)
    dx_pad[pl.ds(count, 8), :] = jnp.zeros((8, dx_pad.shape[1]), FULL)
    dbc_pad[pl.ds(count, 8), :] = jnp.zeros((8, dbc_pad.shape[1]), FULL)
    dstate[...] = jnp.zeros_like(dstate)
    dwx[...] = jnp.zeros_like(dwx)
    dwbc[...] = jnp.zeros_like(dwbc)
    dnumbers[...] = jnp.zeros_like(dnumbers)
    step_bias, rate_scale, skip = numbers[0], numbers[1], numbers[2]

    def fill(i, carry):
        start = pl.multiple_of(i * QUERY, QUERY)
        rows = pl.ds(start, QUERY)
        xz_pad[pl.ds(start + 8, QUERY), :] = xz[rows, :].astype(FULL)
        bc_pad[pl.ds(start + 8, QUERY), :] = bc[rows, :].astype(FULL)
        return carry

    arrived()
    send_blocks(me, devices, wide, du_blocks, du_got, du_send, du_recv)
    own_feed = pltpu.make_async_copy(feed_parts.at[z_place], feed_got.at[0], feed_sem)
    own_feed.start()

    def feed_copy(k):
        place = lax.rem(z_place + k, depth)
        return remote(
            feed_parts.at[place],
            feed_got.at[k],
            feed_send.at[k - 1],
            feed_recv.at[k - 1],
            (n, place * 2 + core),
        )

    own_middle = pltpu.make_async_copy(middle_parts.at[n], middle_got.at[0], middle_sem)
    own_middle.start()

    def middle_copy(k):
        m = lax.rem(n + k, narrow)
        return remote(
            middle_parts.at[m], middle_got.at[k], middle_send.at[k - 1], middle_recv.at[k - 1], (m, w)
        )

    for k in range(1, depth):
        feed_copy(k).start()
    for k in range(1, narrow):
        middle_copy(k).start()
    du_got[me] = du_blocks[me]
    lax.fori_loop(0, blocks, fill, 0)
    wait_blocks(me, devices, wide, du_got, du_send, du_recv)
    patches = du_blocks.shape[1]
    group = QUERY // patches
    own_lane = lax.broadcasted_iota(jnp.int32, (QUERY, STATE), 1) == me

    def slope(pre):
        s = jax.nn.sigmoid(pre)
        return s * (1.0 + pre * (1.0 - s))

    def total(v):
        return jnp.sum(jnp.sum(v, axis=1, keepdims=True), axis=0, keepdims=True)

    def conv_back(pad, start, dpre_pad, dpre, weight, dw):
        mark = marks[pl.ds(start, QUERY), :]
        window = pad[pl.ds(start, QUERY + 8), :]
        later = dpre_pad[pl.ds(start, QUERY + 8), :]
        later_marks = marks[pl.ds(start, QUERY + 8), :]
        out = weight[CONV - 1 :] * dpre
        dw[CONV - 1 : CONV, :] += jnp.sum(dpre * window[8:], axis=0, keepdims=True)
        dw[CONV : CONV + 1, :] += jnp.sum(dpre, axis=0, keepdims=True)
        for lag in range(1, CONV):
            tap = CONV - 1 - lag
            out = out + weight[tap : tap + 1] * (
                (later * later_marks[:, lag : lag + 1])[lag : lag + QUERY]
            )
            dw[tap : tap + 1, :] += jnp.sum(
                dpre * (window[8 - lag : 8 - lag + QUERY] * mark[:, lag : lag + 1]),
                axis=0,
                keepdims=True,
            )
        return out

    def block(k, carry):
        i = blocks - 1 - k
        start = pl.multiple_of(i * QUERY, QUERY)
        rows = pl.ds(start, QUERY)
        mark = marks[rows, :]
        pre_x = convolved(xz_pad[pl.ds(start, QUERY + 8), :], mark, wx[...], bx[...])
        pre = convolved(bc_pad[pl.ds(start, QUERY + 8), :], mark, wbc[...], bbc[...])
        act = jax.nn.silu(pre)
        x, b, c = jax.nn.silu(pre_x)[:, :HEAD_M], act[:, :STATE], act[:, STATE:]
        step = dt[rows, :]
        lower, delta, decay, begun, tail, kept = decays(mark, step, step_bias, rate_scale)
        held, dheld = states[i], dstate[...]
        z = xz[rows, :].astype(FULL)[:, HEAD_M:]
        du = du_got[pl.ds(i * group, group)].astype(FULL).reshape(QUERY, HEAD_M)
        y = y_in[rows, :]
        dy = du * jax.nn.silu(z)
        dz = du * y * slope(z)
        scores = nt(c, b, highest)
        reach = decay * delta.T
        dweight = nt(dy, x, highest)
        dscores = dweight * reach
        fed = x * (tail * delta)[:, :HEAD_M]
        begun_dy = dy * begun[:, :HEAD_M]
        dc = nn(dscores, b, highest) + nn(begun_dy, held, highest)
        db = tn(dscores, c, highest) + nn(fed, dheld, highest)
        dfed = nt(b, dheld, highest)
        dx = skip * dy + tn(scores * reach, dy, highest) + (tail * delta)[:, :HEAD_M] * dfed
        moved = dweight * scores * decay
        turned = moved.T
        ddelta = jnp.sum(turned, axis=1, keepdims=True)
        dtotal = jnp.sum(moved * delta.T, axis=1, keepdims=True) - ddelta * delta[:, :1]
        dtotal += jnp.sum(begun_dy * nt(c, held, highest), axis=1, keepdims=True)
        dtail = jnp.sum(dfed * x, axis=1, keepdims=True)
        ddelta += dtail * tail[:, :1]
        dtail = dtail * (tail * delta)[:, :1]
        dtotal -= dtail
        dlast = jnp.sum(dtail, axis=0, keepdims=True) + total(dheld * held * kept)
        dlog = tn(lower, jnp.broadcast_to(dtotal, (QUERY, QUERY)), highest)[:, :1] + dlast
        ddelta -= dlog * rate_scale
        dstep = ddelta * jax.nn.sigmoid(step + step_bias)
        dbcdt[rows, 2 * STATE :] = jnp.where(own_lane, dstep, 0.0).astype(LOW)
        dnumbers[0:1, :] += jnp.broadcast_to(jnp.sum(dstep, axis=0, keepdims=True), (1, 128))
        dnumbers[1:2, :] -= jnp.broadcast_to(
            jnp.sum(dlog * delta[:, :1] * rate_scale, axis=0, keepdims=True), (1, 128)
        )
        dnumbers[2:3, :] += jnp.broadcast_to(total(dy * x), (1, 128))
        dstate[...] = dheld * kept + tn(begun_dy, c, highest)
        dpre_x = jnp.concatenate([dx, jnp.zeros_like(dx)], axis=1) * slope(pre_x)
        dpre = jnp.concatenate([db, dc], axis=1) * slope(pre)
        dx_pad[rows, :] = dpre_x
        dbc_pad[rows, :] = dpre
        dxz[rows, :] = jnp.concatenate([dz, dz], axis=1).astype(LOW)
        return carry

    lax.fori_loop(0, blocks, block, 0)

    def unconvolve(i, carry):
        start = pl.multiple_of(i * QUERY, QUERY)
        rows = pl.ds(start, QUERY)
        dxr = conv_back(xz_pad, start, dx_pad, dx_pad[rows, :], wx[...], dwx)
        left = lax.broadcasted_iota(jnp.int32, dxr.shape, 1) < HEAD_M
        dxz[rows, :] = jnp.where(left, dxr, dxz[rows, :].astype(FULL)).astype(LOW)
        dbcdt[rows, : 2 * STATE] = conv_back(
            bc_pad, start, dbc_pad, dbc_pad[rows, :], wbc[...], dwbc
        ).astype(LOW)
        return carry

    lax.fori_loop(0, blocks, unconvolve, 0)

    width = normed.shape[1]
    own_rows = xz_grads.shape[1]

    def rows_of(m, carry):
        for z in range(depth):
            start = (m * depth + z) * 2 * patches
            rows = pl.ds(pl.multiple_of(start, 2 * patches), 2 * patches)
            values = nt(dxz[rows, :], w_xz[...]) + nt(dbcdt[rows, :], w_bcdt[...])
            partial_rows[m, z, :, :, :width] = values.astype(LOW).reshape(2, patches, width)
        return carry

    lax.fori_loop(0, narrow, rows_of, 0)

    def weight_grads(m, carry):
        span = width // narrow
        columns = pl.ds(pl.multiple_of(m * span, span), span)
        lhs = normed[:, columns]
        grads[pl.ds(m * 2 * depth, 2 * depth)] = (
            tn(lhs, dxz[...]).astype(LOW).reshape(2 * depth, own_rows, 2 * HEAD_M)
        )
        partial_rows[m, :, :, :, width:] = (
            tn(lhs, dbcdt[...]).astype(LOW).reshape(depth, 2, own_rows, 3 * STATE)
        )
        return carry

    lax.fori_loop(0, narrow, weight_grads, 0)
    to_twin = remote(partial_rows.at[:, :, 1 - core], core_got, core_send, core_recv, twin)
    to_twin.start()
    to_twin.wait_recv()
    for m in range(narrow):
        for z in range(depth):
            core_got[m, z] = (
                core_got[m, z].astype(FULL) + partial_rows[m, z, core].astype(FULL)
            ).astype(LOW)
    for k in range(1, narrow):
        m = lax.rem(n + k, narrow)
        remote(core_got.at[m], narrow_got.at[k - 1], narrow_send.at[k - 1], narrow_recv.at[k - 1], (m, w)).start()
    for k in range(1, narrow):
        remote(
            core_got.at[n], narrow_got.at[k - 1], narrow_send.at[k - 1], narrow_recv.at[k - 1], twin
        ).wait_recv()
    for z in range(depth):
        total_rows = core_got[n, z].astype(FULL)
        for k in range(1, narrow):
            total_rows += narrow_got[k - 1, z].astype(FULL)
        z_rows[z] = total_rows.astype(LOW)
    for k in range(1, depth):
        place = lax.rem(z_place + k, depth)
        remote(
            z_rows.at[place],
            z_got.at[k - 1],
            z_send.at[k - 1],
            z_recv.at[k - 1],
            (n, place * 2 + core),
        ).start()
    send_blocks(me, devices, wide, grads, grads_got, grads_send, grads_recv)
    grads_got[me] = grads[me]
    total_rows = z_rows[z_place].astype(FULL)
    for k in range(1, depth):
        remote(
            z_rows.at[z_place], z_got.at[k - 1], z_send.at[k - 1], z_recv.at[k - 1], twin
        ).wait_recv()
        total_rows += z_got[k - 1].astype(FULL)
    rows_grad[...] = total_rows
    wait_blocks(me, devices, wide, grads_got, grads_send, grads_recv)
    xz_grads[...] = grads_got[...]
    own_middle.wait()
    for k in range(1, narrow):
        middle_copy(k).wait_recv()
    for z in range(depth):
        middle_total = middle_got[0, z].astype(FULL)
        for k in range(1, narrow):
            middle_total += middle_got[k, z].astype(FULL)
        middle_sums[z] = middle_total.astype(LOW)
    own_feed.wait()
    for k in range(1, depth):
        feed_copy(k).wait_recv()
    for i in range(3):
        feed_total = feed_got[0, i].astype(FULL)
        for k in range(1, depth):
            feed_total += feed_got[k, i].astype(FULL)
        feed_sums[i] = feed_total.astype(LOW)
    for k in range(1, depth):
        feed_copy(k).wait_send()
    for k in range(1, narrow):
        middle_copy(k).wait_send()
    to_twin.wait_send()
    for k in range(1, narrow):
        remote(
            core_got.at[n], narrow_got.at[k - 1], narrow_send.at[k - 1], narrow_recv.at[k - 1], twin
        ).wait_send()
    for k in range(1, depth):
        remote(
            z_rows.at[z_place], z_got.at[k - 1], z_send.at[k - 1], z_recv.at[k - 1], twin
        ).wait_send()


def in_smem():
    return pl.BlockSpec(memory_space=pltpu.SMEM)


def in_vmem():
    return pl.BlockSpec(memory_space=pltpu.VMEM)


def mixer_forward(numbers, xz, bc, dt, marks, wx, bx, wbc, bbc):
    count = xz.shape[0]
    return pl.pallas_call(
        mixer_forward_kernel,
        out_shape=[
            jax.ShapeDtypeStruct((count, HEAD_M), FULL),
            jax.ShapeDtypeStruct((count, HEAD_M), FULL),
            jax.ShapeDtypeStruct((count // QUERY, HEAD_M, STATE), FULL),
        ],
        in_specs=[in_smem()] + [in_vmem()] * 8,
        out_specs=[in_vmem()] * 3,
        scratch_shapes=[
            pltpu.VMEM((count + 8, 2 * HEAD_M), FULL),
            pltpu.VMEM((count + 8, 2 * STATE), FULL),
            pltpu.VMEM((HEAD_M, STATE), FULL),
        ],
        compiler_params=pltpu.CompilerParams(vmem_limit_bytes=32 << 20),
        name="mixer_forward",
    )(numbers, xz, bc, dt, marks, wx, bx, wbc, bbc)


def mixer_backward(
    numbers, xz, bc, dt, marks, wx, bx, wbc, bbc, y, states, normed, w_xz, w_bcdt, du_blocks, feed_parts, middle_parts, collective_id
):
    narrow, wide = lax.axis_size(NARROW), lax.axis_size(WIDE)
    devices = narrow * wide
    count, width = normed.shape
    patches = count // devices
    own_rows = width // devices
    dma = pltpu.SemaphoreType.DMA
    low = partial(pltpu.VMEM, dtype=LOW)
    every = width + w_bcdt.shape[1]
    return pl.pallas_call(
        partial(mixer_backward_kernel, narrow, wide),
        out_shape=[
            jax.ShapeDtypeStruct((8, 2 * HEAD_M), FULL),
            jax.ShapeDtypeStruct((8, 2 * STATE), FULL),
            jax.ShapeDtypeStruct((8, 128), FULL),
            jax.ShapeDtypeStruct((patches, every), FULL),
            jax.ShapeDtypeStruct((devices, own_rows, 2 * HEAD_M), LOW),
            jax.ShapeDtypeStruct(feed_parts.shape[1:], LOW),
            jax.ShapeDtypeStruct(middle_parts.shape[1:], LOW),
        ],
        in_specs=[in_smem()] + [in_vmem()] * 14 + [pl.BlockSpec(memory_space=pl.ANY)] * 2,
        out_specs=[in_vmem()] * 7,
        scratch_shapes=[
            pltpu.VMEM((count + 8, 2 * HEAD_M), FULL),
            pltpu.VMEM((count + 8, 2 * STATE), FULL),
            pltpu.VMEM((count + 8, 2 * HEAD_M), FULL),
            pltpu.VMEM((count + 8, 2 * STATE), FULL),
            pltpu.VMEM((HEAD_M, STATE), FULL),
            low((devices, patches, HEAD_M)),
            low((count, 2 * HEAD_M)),
            low((count, 3 * STATE)),
            low((narrow, wide // 2, 2, patches, every)),
            low((narrow, wide // 2, patches, every)),
            low((narrow - 1, wide // 2, patches, every)),
            low((wide // 2, patches, every)),
            low((wide // 2 - 1, patches, every)),
            low((devices, own_rows, 2 * HEAD_M)),
            low((devices, own_rows, 2 * HEAD_M)),
            low(feed_parts.shape),
            low(middle_parts.shape),
            dma,
            dma,
            dma,
            dma,
            dma((narrow - 1,)),
            dma((narrow - 1,)),
            dma((wide // 2 - 1,)),
            dma((wide // 2 - 1,)),
            dma,
            dma,
            dma((wide // 2 - 1,)),
            dma((wide // 2 - 1,)),
            dma,
            dma((narrow - 1,)),
            dma((narrow - 1,)),
            dma,
        ],
        compiler_params=pltpu.CompilerParams(
            collective_id=collective_id, has_side_effects=True, vmem_limit_bytes=56 << 20
        ),
        name="mixer_backward",
    )(
        numbers,
        xz,
        bc,
        dt,
        marks,
        wx,
        bx,
        wbc,
        bbc,
        y,
        states,
        normed,
        w_xz,
        w_bcdt,
        du_blocks,
        feed_parts,
        middle_parts,
    )


def patch_causal():
    row = lax.broadcasted_iota(jnp.int32, (BYTE_BLOCK, BYTE_BLOCK), 0)
    column = lax.broadcasted_iota(jnp.int32, (BYTE_BLOCK, BYTE_BLOCK), 1)
    return (lax.div(row, PATCH) == lax.div(column, PATCH)) & (row >= column)


def head_probs(q, k, causal):
    scores = jnp.where(causal, nt(q, k) * HEAD_A ** (-0.5), masked_score)
    grown = jnp.exp(scores - jnp.max(scores, axis=1, keepdims=True))
    return grown / jnp.sum(grown, axis=1, keepdims=True)


def of_head(block, half):
    lane = lax.broadcasted_iota(jnp.int32, block.shape, 1)
    return jnp.where(lax.div(lane, HEAD_A) == half, block, jnp.zeros_like(block))


def fetched(pack, places, blocks, sems):
    copies = []
    for i, place in enumerate(places):
        width = place.shape[1]
        start = blocks[i]
        copies.append(
            pltpu.make_async_copy(pack.at[:, pl.ds(start, width)], place, sems.at[i])
        )
        copies[-1].start()
    return [copy.wait for copy in copies]


def unit_rows(values):
    scale = lax.rsqrt(jnp.mean(values * values, axis=1, keepdims=True) + epsilon)
    return values * scale, scale


def norm_back(grad, gain, unit, scale):
    scaled = grad * gain
    return scale * (scaled - unit * jnp.mean(scaled * unit, axis=1, keepdims=True))


WEIGHT_STEP = 256


def attend_pairs(qkv, mixed):
    causal = patch_causal()
    blocks = qkv.shape[0] // BYTE_BLOCK

    def pair(i, carry):
        def lanes(part):
            start = part * D + i * (2 * HEAD_A)
            return pl.ds(pl.multiple_of(start, 2 * HEAD_A), 2 * HEAD_A)

        for block in range(blocks):
            rows = pl.ds(block * BYTE_BLOCK, BYTE_BLOCK)
            q, k, v = qkv[rows, lanes(0)], qkv[rows, lanes(1)], qkv[rows, lanes(2)]
            total = jnp.zeros(q.shape, FULL)
            for half in range(2):
                probs = head_probs(of_head(q, half), k, causal)
                total += nn(probs.astype(LOW), of_head(v, half))
            mixed[rows, lanes(0)] = total.astype(LOW)
        return carry

    lax.fori_loop(0, HEADS_A // 2, pair, 0)


def attend_pairs_back(qkv, heads_grad, qkv_grad):
    causal = patch_causal()
    blocks = qkv.shape[0] // BYTE_BLOCK
    scale = HEAD_A ** (-0.5)

    def pair(i, carry):
        def lanes(part):
            start = part * D + i * (2 * HEAD_A)
            return pl.ds(pl.multiple_of(start, 2 * HEAD_A), 2 * HEAD_A)

        for block in range(blocks):
            rows = pl.ds(block * BYTE_BLOCK, BYTE_BLOCK)
            q, k, v = qkv[rows, lanes(0)], qkv[rows, lanes(1)], qkv[rows, lanes(2)]
            g = heads_grad[rows, lanes(0)]
            dq = jnp.zeros(q.shape, FULL)
            dk = jnp.zeros(q.shape, FULL)
            dv = jnp.zeros(q.shape, FULL)
            for half in range(2):
                own_q, own_k, own_g = of_head(q, half), of_head(k, half), of_head(g, half)
                probs = head_probs(own_q, k, causal)
                dprobs = nt(own_g, v)
                dv += tn(probs.astype(LOW), own_g)
                dscores = probs * (dprobs - jnp.sum(probs * dprobs, axis=1, keepdims=True))
                dscores = dscores.astype(LOW)
                dq += nn(dscores, own_k)
                dk += tn(dscores, own_q)
            qkv_grad[rows, lanes(0)] = (dq * scale).astype(LOW)
            qkv_grad[rows, lanes(1)] = (dk * scale).astype(LOW)
            qkv_grad[rows, lanes(2)] = dv.astype(LOW)
        return carry

    lax.fori_loop(0, HEADS_A // 2, pair, 0)


def bytes_forward_kernel(
    u_blocks,
    mixed_in,
    gains,
    gated_gain,
    pack,
    gated_out,
    local_out,
    stream_out,
    normed_out,
    qkv,
    mixed,
    after_out,
    feed_out,
    w_out0,
    w_out1,
    w_local,
    w_q,
    w_k,
    w_v,
    w_attn,
    pieces,
    sems,
):
    places = (w_out0, w_out1, w_local, w_q, w_k, w_v, w_attn)
    blocks = [4 * D, 5 * D, 6 * D, 0, D, 2 * D, 3 * D]
    waits = fetched(pack, places, blocks, sems)
    patches = mixed_in.shape[0]
    half = HEAD_M // 2
    for i in range(2):
        for first in range(0, HEADS_M, 4):
            gated_out[i, :, first * half : (first + 4) * half] = jnp.concatenate(
                [
                    u_blocks[first + j].astype(FULL)[:, i * half : (i + 1) * half]
                    for j in range(4)
                ],
                axis=1,
            )
    held = [gated_out[0], gated_out[1]]
    square = sum(jnp.sum(v * v, axis=1, keepdims=True) for v in held)
    scale = lax.rsqrt(square / (2 * D) + epsilon)
    gated = [(held[i] * scale * gated_gain[i : i + 1, :]).astype(LOW) for i in range(2)]
    waits[0]()
    waits[1]()
    joined = mixed_in[...] + nn(gated[0], w_out0[...]) + nn(gated[1], w_out1[...])
    for k in range(PATCH):
        pieces[pl.ds(k, patches, stride=PATCH), :] = joined[:, k * EMB : (k + 1) * EMB]
    local = pieces[...].astype(LOW)
    local_out[...] = local
    waits[2]()
    stream = nt(local, w_local[...])
    stream_out[...] = stream
    normed = (unit_rows(stream)[0] * gains[0:1, :]).astype(LOW)
    normed_out[...] = normed
    for i, weight in enumerate((w_q, w_k, w_v)):
        waits[3 + i]()
        for first in range(0, D, WEIGHT_STEP):
            qkv[:, i * D + first : i * D + first + WEIGHT_STEP] = nn(
                normed, weight[:, first : first + WEIGHT_STEP]
            ).astype(LOW)
    attend_pairs(qkv, mixed)
    waits[6]()
    heads = mixed[...]
    for first in range(0, D, WEIGHT_STEP):
        columns = slice(first, first + WEIGHT_STEP)
        after_out[:, columns] = stream_out[:, columns] + nn(heads, w_attn[:, columns])
    feed_out[...] = (unit_rows(after_out[...])[0] * gains[1:2, :]).astype(LOW)


def bytes_forward(u_blocks, mixed_in, gains, gated_gain, pack):
    patches = mixed_in.shape[0]
    rows = patches * PATCH

    def full(shape, kind):
        return jax.ShapeDtypeStruct(shape, kind)

    return pl.pallas_call(
        bytes_forward_kernel,
        out_shape=[
            full((2, patches, D), FULL),
            full((rows, EMB), LOW),
            full((rows, D), FULL),
            full((rows, D), LOW),
            full((rows, 3 * D), LOW),
            full((rows, D), LOW),
            full((rows, D), FULL),
            full((rows, D), LOW),
        ],
        in_specs=[in_vmem()] * 4 + [pl.BlockSpec(memory_space=pl.ANY)],
        out_specs=[in_vmem()] * 8,
        scratch_shapes=[pltpu.VMEM((D, D), LOW)] * 2
        + [pltpu.VMEM((D, EMB), LOW)]
        + [pltpu.VMEM((D, D), LOW)] * 4
        + [pltpu.VMEM((rows, EMB), FULL), pltpu.SemaphoreType.DMA((7,))],
        compiler_params=pltpu.CompilerParams(vmem_limit_bytes=48 << 20),
        name="bytes_forward",
    )(u_blocks, mixed_in, gains, gated_gain, pack)


def bytes_backward_kernel(
    narrow,
    feed_in_grad,
    cotangent,
    keep,
    after,
    stream_in,
    normed_in,
    qkv,
    mixed,
    local_in,
    gated_rows,
    gains,
    gated_gain,
    pack,
    feed_parts,
    global_out,
    scale_out,
    sums,
    gain_grads,
    gated_gain_grads,
    du_blocks,
    rows_out,
    w_attn,
    w_q,
    w_k,
    w_v,
    w_local,
    w_out0,
    w_out1,
    after_grad,
    heads_grad,
    qkv_grad,
    pieces,
    parts_got,
    grads,
    grads_got,
    sems,
    p_send,
    p_recv,
    t_send,
    t_recv,
):
    n, wide_place = lax.axis_index(NARROW), lax.axis_index(WIDE)
    core = lax.rem(wide_place, 2)
    twin = (n, wide_place + 1 - 2 * core)
    barrier = pltpu.get_barrier_semaphore()
    pl.semaphore_signal(barrier, inc=1, device_id=twin, device_id_type=MESH)
    for k in range(1, narrow):
        peer = (lax.rem(n + k, narrow), wide_place)
        pl.semaphore_signal(barrier, inc=1, device_id=peer, device_id_type=MESH)

    def twin_copy(i, columns):
        return remote(
            grads.at[:, 1 - core, :, columns],
            grads_got.at[:, :, columns],
            t_send.at[i],
            t_recv.at[i],
            twin,
        )

    def give(i, columns, part):
        grads[:, :, :, columns] = part.astype(LOW).reshape(grads.shape[:3] + part.shape[1:])
        twin_copy(i, columns).start()

    def part_copy(k):
        peer = (lax.rem(n + k, narrow), wide_place)
        return remote(feed_parts.at[k], parts_got.at[k], p_send.at[k - 1], p_recv.at[k - 1], peer)

    own_part = pltpu.make_async_copy(feed_parts.at[0], parts_got.at[0], sems.at[7])
    own_part.start()
    places = (w_attn, w_q, w_k, w_v, w_local, w_out0, w_out1)
    blocks = [3 * D, 0, D, 2 * D, 6 * D, 4 * D, 5 * D]
    waits = fetched(pack, places, blocks, sems)
    pl.semaphore_wait(barrier, narrow)
    for k in range(1, narrow):
        part_copy(k).start()
    patches = global_out.shape[0]
    unit, scale = unit_rows(after[...])
    grad = feed_in_grad[...].astype(LOW).astype(FULL)
    gain_grads[1:2, :] = jnp.sum(grad * unit, axis=0, keepdims=True)
    after_grad[...] = cotangent[...].astype(FULL) * keep[...] + norm_back(
        grad, gains[1:2, :], unit, scale
    )
    attn_grad = after_grad[...].astype(LOW)
    waits[0]()
    for first in range(0, D, WEIGHT_STEP):
        columns = slice(first, first + WEIGHT_STEP)
        heads_grad[:, columns] = nt(attn_grad, w_attn[columns, :]).astype(LOW)
        give(
            (3 * D + first) // WEIGHT_STEP,
            pl.ds(3 * D + first, WEIGHT_STEP),
            tn(mixed[...], attn_grad[:, columns]),
        )
    attend_pairs_back(qkv, heads_grad, qkv_grad)
    normed_grad = jnp.zeros(after_grad.shape, FULL)
    for i, weight in enumerate((w_q, w_k, w_v)):
        waits[1 + i]()
        normed_grad += nt(qkv_grad[:, i * D : (i + 1) * D], weight[...])
    unit, scale = unit_rows(stream_in[...])
    gain_grads[0:1, :] = jnp.sum(normed_grad * unit, axis=0, keepdims=True)
    stream_grad = (after_grad[...] + norm_back(normed_grad, gains[0:1, :], unit, scale)).astype(LOW)
    waits[4]()
    pieces[...] = nn(stream_grad, w_local[...])
    for k in range(PATCH):
        global_out[:, k * EMB : (k + 1) * EMB] = pieces[pl.ds(k, patches, stride=PATCH), :]
    mix_grad = global_out[...].astype(LOW)
    waits[5]()
    waits[6]()
    inner = [nt(mix_grad, w_out0[...]), nt(mix_grad, w_out1[...])]
    held = [gated_rows[0], gated_rows[1]]
    square = sum(jnp.sum(v * v, axis=1, keepdims=True) for v in held)
    scale = lax.rsqrt(square / (2 * D) + epsilon)
    units = [v * scale for v in held]
    scaled = [inner[i] * gated_gain[i : i + 1, :] for i in range(2)]
    mean = sum(jnp.sum(scaled[i] * units[i], axis=1, keepdims=True) for i in range(2)) / (2 * D)
    for i in range(2):
        gated_gain_grads[i : i + 1, :] = jnp.sum(inner[i] * units[i], axis=0, keepdims=True)
    scale_out[...] = jnp.broadcast_to(scale, scale_out.shape)
    rows_grads = [scale * (scaled[i] - units[i] * mean) for i in range(2)]
    half = HEAD_M // 2
    for head in range(HEADS_M):
        lanes = slice(head * half, (head + 1) * half)
        du_blocks[head] = jnp.concatenate([part[:, lanes] for part in rows_grads], axis=1).astype(LOW)
    give(4 * D // WEIGHT_STEP, pl.ds(4 * D, EMB), tn(stream_grad, local_in[...]))

    def weight_grads(i, carry):
        columns = pl.ds(pl.multiple_of(i * WEIGHT_STEP, WEIGHT_STEP), WEIGHT_STEP)
        give(i, columns, tn(normed_in[...], qkv_grad[:, columns]))
        return carry

    lax.fori_loop(0, 3 * D // WEIGHT_STEP, weight_grads, 0)
    own_part.wait()
    for k in range(1, narrow):
        part_copy(k).wait_recv()
    for first in range(0, D, WEIGHT_STEP):
        columns = slice(first, first + WEIGHT_STEP)
        feed = parts_got[0, :, columns].astype(FULL)
        for k in range(1, narrow):
            feed += parts_got[k, :, columns].astype(FULL)
        feed = feed.astype(LOW).astype(FULL)
        rows_out[:, columns] = ((after[:, columns] + feed) * keep[...]).astype(LOW)

    def add_twin(i, columns):
        twin_copy(i, columns).wait_recv()
        sums[:, :, columns] = (
            grads[:, core, :, columns].astype(FULL) + grads_got[:, :, columns].astype(FULL)
        ).astype(LOW)

    def add_one(i, carry):
        add_twin(i, pl.ds(pl.multiple_of(i * WEIGHT_STEP, WEIGHT_STEP), WEIGHT_STEP))
        return carry

    def end_one(i, carry):
        twin_copy(i, pl.ds(pl.multiple_of(i * WEIGHT_STEP, WEIGHT_STEP), WEIGHT_STEP)).wait_send()
        return carry

    steps = 4 * D // WEIGHT_STEP
    add_twin(steps, pl.ds(4 * D, EMB))
    lax.fori_loop(0, steps, add_one, 0)
    twin_copy(steps, pl.ds(4 * D, EMB)).wait_send()
    lax.fori_loop(0, steps, end_one, 0)
    for k in range(1, narrow):
        part_copy(k).wait_send()


def bytes_backward(
    feed_in_grad,
    cotangent,
    keep,
    after,
    stream,
    normed,
    qkv,
    mixed,
    local,
    gated_rows,
    gains,
    gated_gain,
    pack,
    feed_parts,
    collective_id,
):
    narrow = feed_parts.shape[0]
    every = 4 * D + EMB
    rows = after.shape[0]
    patches = rows // PATCH

    def full(shape, kind):
        return jax.ShapeDtypeStruct(shape, kind)

    return pl.pallas_call(
        partial(bytes_backward_kernel, narrow),
        out_shape=[
            full((patches, D), FULL),
            full((patches, 128), FULL),
            full((HEADS_M // 2, D // HEADS_M, every), LOW),
            full((2, D), FULL),
            full((2, D), FULL),
            full((HEADS_M, patches, HEAD_M), LOW),
            full((rows, D), LOW),
        ],
        in_specs=[in_vmem()] * 12 + [pl.BlockSpec(memory_space=pl.ANY)] * 2,
        out_specs=[in_vmem()] * 7,
        scratch_shapes=[pltpu.VMEM((D, D), LOW)] * 4
        + [pltpu.VMEM((D, EMB), LOW)]
        + [pltpu.VMEM((D, D), LOW)] * 2
        + [
            pltpu.VMEM((rows, D), FULL),
            pltpu.VMEM((rows, D), LOW),
            pltpu.VMEM((rows, 3 * D), LOW),
            pltpu.VMEM((rows, EMB), FULL),
            pltpu.VMEM((narrow, rows, D), LOW),
            pltpu.VMEM((HEADS_M // 2, 2, D // HEADS_M, every), LOW),
            pltpu.VMEM((HEADS_M // 2, D // HEADS_M, every), LOW),
            pltpu.SemaphoreType.DMA((8,)),
            pltpu.SemaphoreType.DMA((narrow - 1,)),
            pltpu.SemaphoreType.DMA((narrow - 1,)),
            pltpu.SemaphoreType.DMA((4 * D // WEIGHT_STEP + 1,)),
            pltpu.SemaphoreType.DMA((4 * D // WEIGHT_STEP + 1,)),
        ],
        compiler_params=pltpu.CompilerParams(
            collective_id=collective_id, has_side_effects=True, vmem_limit_bytes=56 << 20
        ),
        name="bytes_backward",
    )(
        feed_in_grad,
        cotangent,
        keep,
        after,
        stream,
        normed,
        qkv,
        mixed,
        local,
        gated_rows,
        gains,
        gated_gain,
        pack,
        feed_parts,
    )


def feed_kernel(
    narrow,
    x_in,
    *refs,
):
    g_ins = refs[:narrow]
    w_in, f_out, gx_out, grads, w, x, g, hid, gg, gu, sent, got = refs[narrow : narrow + 12]
    twin_out, twin_got = refs[narrow + 12 : narrow + 14]
    w_sem, g_sem, x_sem, x_send, x_recv, r_send, r_recv, t_send, t_recv = refs[narrow + 14 :]
    n, wide_place = lax.axis_index(NARROW), lax.axis_index(WIDE)
    core = lax.rem(wide_place, 2)
    twin = (n, wide_place + 1 - 2 * core)
    barrier = pltpu.get_barrier_semaphore()
    pl.semaphore_signal(barrier, inc=1, device_id=twin, device_id_type=MESH)
    for k in range(1, narrow):
        peer = (lax.rem(n + k, narrow), wide_place)
        pl.semaphore_signal(barrier, inc=1, device_id=peer, device_id_type=MESH)
    own_x = pltpu.make_async_copy(x_in, x.at[0], x_sem)
    own_x.start()
    g_copies = [pltpu.make_async_copy(g_ins[k], g.at[k], g_sem.at[k]) for k in range(narrow)]
    w_copies = [pltpu.make_async_copy(w_in.at[:, i], w.at[i], w_sem.at[i]) for i in range(3)]
    g_copies[0].start()
    for copy in w_copies:
        copy.start()
    for copy in g_copies[1:]:
        copy.start()
    pl.semaphore_wait(barrier, narrow)

    def x_copy(k):
        return pltpu.make_async_remote_copy(
            src_ref=x_in,
            dst_ref=x.at[k],
            send_sem=x_send.at[k - 1],
            recv_sem=x_recv.at[k - 1],
            device_id=(lax.rem(n + narrow - k, narrow), wide_place),
            device_id_type=MESH,
        )

    def r_copy(k):
        return pltpu.make_async_remote_copy(
            src_ref=sent.at[k - 1],
            dst_ref=got.at[k - 1],
            send_sem=r_send.at[k - 1],
            recv_sem=r_recv.at[k - 1],
            device_id=(lax.rem(n + k, narrow), wide_place),
            device_id_type=MESH,
        )

    for k in range(1, narrow):
        x_copy(k).start()
    own_x.wait()
    for copy in w_copies:
        copy.wait()
    for copy in g_copies:
        copy.wait()
    rows, width = x_in.shape
    places, share = w.shape[1], w.shape[2]
    hidden = places * share
    chunk = 2 * share

    def weights(i, start):
        return w[i, pl.ds(start, 2)].reshape(chunk, width)

    def columns(i, first):
        return w[i, :, :, first : first + chunk].reshape(hidden, chunk)

    def block(k, carry):
        @pl.when(k > 0)
        def _():
            x_copy(k).wait_recv()

        xk, gk = x[k], g[k]
        for place in range(0, places, 2):
            units = slice(place * share, place * share + chunk)
            gate = nt(xk, weights(0, place))
            up = nt(xk, weights(1, place))
            dhid = nt(gk, weights(2, place))
            s = jax.nn.sigmoid(gate)
            act = gate * s
            hid[k, :, units] = (act * up).astype(LOW)
            gg[k, :, units] = (dhid * up * s * (1.0 + gate * (1.0 - s))).astype(LOW)
            gu[k, :, units] = (dhid * act).astype(LOW)
        ggk, guk, hidk = gg[k], gu[k], hid[k]
        for first in range(0, width, chunk):
            gx = nn(ggk, columns(0, first)) + nn(guk, columns(1, first))

            @pl.when(k == 0)
            def _():
                gx_out[:, first : first + chunk] = gx

            @pl.when(k > 0)
            def _():
                sent[k - 1, :, first : first + chunk] = gx.astype(LOW)

        @pl.when(k > 0)
        def _():
            r_copy(k).start()

        for first in range(0, width, chunk):
            f_out[k, :, first : first + chunk] = nn(hidk, columns(2, first)).astype(LOW)
        return carry

    lax.fori_loop(0, narrow, block, 0)

    depth = places // 2

    def weight_grads(place, i, first, columns):
        left, right = ((gg, x), (gu, x), (hid, g))[i]
        units = pl.ds(pl.multiple_of(place * share, share), share)
        lhs = left[:, :, units].reshape(narrow * rows, share)
        rhs = right[:, :, first : first + columns].reshape(narrow * rows, columns)
        return tn(lhs, rhs)

    def t_copy(j):
        return remote(twin_out.at[j], twin_got.at[j], t_send.at[j], t_recv.at[j], twin)

    def for_twin(j, carry):
        for i in range(3):
            for first in range(0, width, 2 * chunk):
                twin_out[j, i, :, first : first + 2 * chunk] = weight_grads(
                    2 * j + 1 - core, i, first, 2 * chunk
                ).astype(LOW)
        t_copy(j).start()
        return carry

    def for_own(j, carry):
        t_copy(j).wait_recv()
        for i in range(3):
            for first in range(0, width, 2 * chunk):
                columns = slice(first, first + 2 * chunk)
                part = weight_grads(2 * j + core, i, first, 2 * chunk)
                grads[j, i, :, columns] = (
                    part + twin_got[j, i, :, columns].astype(FULL)
                ).astype(LOW)
        return carry

    lax.fori_loop(0, depth, for_twin, 0)
    lax.fori_loop(0, depth, for_own, 0)
    for k in range(1, narrow):
        r_copy(k).wait_recv()
        gx_out[...] += got[k - 1].astype(FULL)
    for k in range(1, narrow):
        x_copy(k).wait_send()
        r_copy(k).wait_send()
    for j in range(depth):
        t_copy(j).wait_send()


def feed_forward_back(x_own, g_blocks, feed_all, collective_id):
    narrow = len(g_blocks)
    rows, width = x_own.shape
    places, _, share, _ = feed_all.shape
    dma = pltpu.SemaphoreType.DMA
    anywhere = pl.BlockSpec(memory_space=pl.ANY)

    def rows_scratch(count, columns):
        return pltpu.VMEM((count, rows, columns), LOW)

    hidden = places * share
    return pl.pallas_call(
        partial(feed_kernel, narrow),
        out_shape=[
            jax.ShapeDtypeStruct((narrow, rows, width), LOW),
            jax.ShapeDtypeStruct((rows, width), FULL),
            jax.ShapeDtypeStruct((places // 2,) + feed_all.shape[1:], LOW),
        ],
        in_specs=[anywhere] * (narrow + 2),
        out_specs=[in_vmem()] * 3,
        scratch_shapes=[
            pltpu.VMEM((3, places, share, width), LOW),
            rows_scratch(narrow, width),
            rows_scratch(narrow, width),
            rows_scratch(narrow, hidden),
            rows_scratch(narrow, hidden),
            rows_scratch(narrow, hidden),
            rows_scratch(narrow - 1, width),
            rows_scratch(narrow - 1, width),
            pltpu.VMEM((places // 2,) + feed_all.shape[1:], LOW),
            pltpu.VMEM((places // 2,) + feed_all.shape[1:], LOW),
            dma((3,)),
            dma((narrow,)),
            dma,
            dma((narrow - 1,)),
            dma((narrow - 1,)),
            dma((narrow - 1,)),
            dma((narrow - 1,)),
            dma((places // 2,)),
            dma((places // 2,)),
        ],
        compiler_params=pltpu.CompilerParams(
            collective_id=collective_id, has_side_effects=True, vmem_limit_bytes=58 << 20
        ),
        name="feed",
    )(x_own, *g_blocks, feed_all)


def per_device_heads(
    byte_ids,
    doc_patches,
    pad_bytes,
    byte_table,
    patch_weight,
    gain_mix,
    in_weight,
    conv_weight,
    conv_bias,
    step_bias,
    log_rate,
    skip_gain,
    gated_gain,
    out_weight,
    local_weight,
    gain_attn,
    query_weight,
    key_weight,
    value_weight,
    attn_weight,
    feed_gain,
    gate_weight,
    up_weight,
    down_weight,
    cotangent,
):
    narrow, wide = lax.axis_size(NARROW), lax.axis_size(WIDE)
    devices = narrow * wide
    device = lax.axis_index(BOTH)
    rows = byte_ids.shape[0]
    patches = rows // PATCH
    everything = devices * patches
    own_rows = patch_weight.shape[0]
    hidden_width = gate_weight.shape[1]
    share = hidden_width // narrow

    segment, _, keep_all = patch_layout(doc_patches, pad_bytes, 0, everything)
    keep_all = keep_all.reshape(everything, PATCH)
    place = jnp.arange(everything)
    mark_columns = [segment.astype(FULL)]
    for lag in range(1, CONV):
        earlier = jnp.concatenate([jnp.full((lag,), -1, jnp.int32), segment[:-lag]])
        mark_columns.append((earlier == segment).astype(FULL))
    by_block = segment.reshape(-1, QUERY)
    before = jnp.concatenate([jnp.full((1,), -1, jnp.int32), by_block[:-1, -1]])
    mark_columns.append((by_block == before[:, None]).astype(FULL).reshape(-1))
    mark_columns.append((by_block == by_block[:, -1:]).astype(FULL).reshape(-1))
    mark_columns.append(
        jnp.broadcast_to((by_block[:, -1:] == before[:, None]).astype(FULL), by_block.shape).reshape(-1)
    )
    mark_columns.append(jnp.zeros((everything,), FULL))
    marks = jnp.pad(jnp.stack(mark_columns, axis=1), ((0, 8), (0, 0)))
    keep_rows = lax.dynamic_slice_in_dim(keep_all, device * patches, patches).reshape(-1)

    ids_low = byte_ids.astype(LOW).reshape(patches, PATCH)
    bcdt_width = 2 * STATE + HEADS_M
    start_pack = jnp.concatenate(
        [
            patch_weight,
            jnp.pad(in_weight[:, 2 * DI :], ((0, 0), (0, 96))),
            jnp.pad(ids_low, ((0, 0), (0, 120))),
        ],
        axis=1,
    )
    xz_blocks = jnp.concatenate(
        [
            in_weight[:, DI : 2 * DI].reshape(own_rows, HEADS_M, HEAD_M),
            in_weight[:, :DI].reshape(own_rows, HEADS_M, HEAD_M),
        ],
        axis=2,
    ).transpose(1, 0, 2)
    xz_weight = exchange(xz_blocks, BOTH).reshape(D, 2 * HEAD_M)
    start_all, table_all = gather_all([start_pack, byte_table], 0)
    middle_pack = jnp.concatenate(
        [
            query_weight,
            key_weight,
            value_weight,
            attn_weight,
            out_weight[:own_rows],
            out_weight[own_rows:],
            local_weight.T,
        ],
        axis=1,
    )
    middle_all = lax.all_gather(middle_pack, BOTH, axis=0, tiled=True)
    feed_blocks = jnp.stack(
        [
            gate_weight.T.reshape(narrow, share, -1),
            up_weight.T.reshape(narrow, share, -1),
            down_weight.reshape(narrow, share, -1),
        ],
        axis=1,
    )
    feed_turned = exchange(feed_blocks, NARROW).transpose(1, 2, 0, 3).reshape(3, share, D)
    feed_all = lax.all_gather(feed_turned, WIDE)

    patch_all = start_all[:, :D]
    bcdt_weight = start_all[:, D : D + bcdt_width]
    ids_all = start_all[:, D + 384 : D + 384 + PATCH].astype(jnp.int32)

    vocabulary = jnp.arange(VOCAB, dtype=jnp.int32)
    onehot = (ids_all[:, :, None] == vocabulary).astype(LOW) * keep_all[:, :, None].astype(LOW)
    embedded = (
        jnp.dot(onehot.reshape(everything * PATCH, VOCAB), table_all, preferred_element_type=FULL)
        .astype(LOW)
        .reshape(everything, D)
    )
    mixed_all = jnp.dot(embedded, patch_all, preferred_element_type=FULL)
    normed_all = root_norm(mixed_all, gain_mix).astype(LOW)
    xz = jnp.dot(normed_all, xz_weight, preferred_element_type=FULL).astype(LOW)
    bcdt = jnp.dot(normed_all, bcdt_weight, preferred_element_type=FULL).astype(LOW)
    bc = bcdt[:, : 2 * STATE]
    dt = lax.dynamic_slice_in_dim(bcdt[:, 2 * STATE :], device, 1, axis=1).astype(FULL)
    mixed_in = lax.dynamic_slice_in_dim(mixed_all, device * patches, patches)

    conv_x = lax.dynamic_slice_in_dim(conv_weight, device * HEAD_M, HEAD_M, axis=1)
    bias_x = lax.dynamic_slice_in_dim(conv_bias, device * HEAD_M, HEAD_M)[None]
    conv_x = jnp.pad(conv_x, ((0, 0), (0, HEAD_M)))
    bias_x = jnp.pad(bias_x, ((0, 0), (0, HEAD_M)))
    conv_bc = conv_weight[:, DI:]
    bias_bc = conv_bias[None, DI:]

    def own(values):
        return lax.dynamic_index_in_dim(values, device, 0, False)

    numbers = jnp.stack([own(step_bias), jnp.exp(own(log_rate)), own(skip_gain)])
    mixer_args = (numbers, xz, bc, dt, marks, conv_x, bias_x, conv_bc, bias_bc)
    u, y, states = mixer_forward(*mixer_args)
    u_blocks = exchange(u.astype(LOW).reshape(devices, patches, HEAD_M), BOTH)
    half = HEAD_M // 2
    gated_gain_split = gated_gain.reshape(devices, 2, half).transpose(1, 0, 2).reshape(2, D)

    byte_gains = jnp.stack([gain_attn, feed_gain])
    (
        gated_rows,
        local_rows,
        stream,
        normed_attn,
        qkv,
        mixed_heads,
        after_attn,
        normed_feed,
    ) = bytes_forward(u_blocks, mixed_in, byte_gains, gated_gain_split, middle_all)
    feed_grad = (cotangent.astype(FULL) * keep_rows[:, None]).astype(LOW)

    def passed_narrow(values, by):
        pairs = [(i, (i + by) % narrow) for i in range(narrow)]
        return lax.ppermute(values, NARROW, pairs)

    g_blocks = [feed_grad] + [passed_narrow(feed_grad, narrow - k) for k in range(1, narrow)]
    feed_parts, feed_in_grad, feed_grads = feed_forward_back(normed_feed, g_blocks, feed_all, 2)

    (
        global_grad,
        gated_scale,
        middle_parts,
        byte_gain_grads,
        gated_gain_grads,
        du_blocks,
        out_rows,
    ) = bytes_backward(
        feed_in_grad,
        cotangent,
        keep_rows[:, None],
        after_attn,
        stream,
        normed_attn,
        qkv,
        mixed_heads,
        local_rows,
        gated_rows,
        byte_gains,
        gated_gain_split,
        middle_all,
        feed_parts,
        4,
    )
    middle_parts = middle_parts.reshape(narrow, wide // 2, own_rows, -1)
    grad_gated_gain = gated_gain_grads.reshape(2, devices, half).transpose(1, 0, 2).reshape(DI)
    grad_gain_attn, grad_feed_gain = byte_gain_grads[0], byte_gain_grads[1]

    mix_grad = global_grad.astype(LOW)
    bcdt_padded = start_all[:, D : D + 3 * STATE]
    dwx, dwbc, dnumbers, rows_grad, xz_grads, feed_sums, middle_sums = mixer_backward(
        *mixer_args,
        y,
        states,
        normed_all,
        xz_weight,
        bcdt_padded,
        du_blocks,
        feed_grads,
        middle_parts,
        3,
    )
    normed_mix_grad, bcdt_grads = rows_grad[:, :D], rows_grad[:, D:]
    feed_sums = feed_sums.reshape(3, share, narrow, D // narrow).transpose(2, 0, 1, 3)
    grad_xz = xz_grads.astype(FULL).transpose(1, 0, 2)
    _, mix_norm_back = jax.vjp(root_norm, mixed_in, gain_mix)
    mixed_norm_grad, grad_gain_mix = mix_norm_back(normed_mix_grad)
    embed_grad = (global_grad + mixed_norm_grad).astype(LOW)

    end_pack = jnp.concatenate(
        [
            embed_grad,
            mix_grad,
            gated_scale.astype(LOW),
        ],
        axis=1,
    )
    sums_pack = jnp.concatenate(
        [
            grad_gain_mix,
            grad_gated_gain,
            grad_gain_attn,
            grad_feed_gain,
            dwbc[: CONV + 1].reshape(-1),
            dwx[: CONV + 1, :HEAD_M].reshape(-1),
            dnumbers[:3, 0],
        ]
    )
    sums_width = -(-sums_pack.shape[0] // 1024) * 1024
    sums_pack = jnp.pad(sums_pack, (0, sums_width - sums_pack.shape[0])).reshape(-1, 128)
    end_all, sums_all, middle_sums, feed_sums = gather_all(
        [end_pack, sums_pack], 1, middle_sums, feed_sums
    )
    feed_sums = feed_sums.transpose(1, 0, 2, 3).astype(FULL).reshape(3, hidden_width, D // narrow)
    grad_gate, grad_up, grad_down = feed_sums[0].T, feed_sums[1].T, feed_sums[2]
    sums_all = sums_all.reshape(devices, sums_width)
    embed_grad_all = end_all[:, :D]
    mix_grad_all = end_all[:, D : 2 * D]
    scale_all = end_all[:, 2 * D : 2 * D + 1].astype(FULL)
    gain_own = lax.dynamic_slice_in_dim(gated_gain, device * HEAD_M, HEAD_M)
    grad_out = tn((u * scale_all * gain_own).astype(LOW), mix_grad_all)
    grad_in = jnp.concatenate(
        [
            grad_xz[:, :, HEAD_M:].reshape(own_rows, DI),
            grad_xz[:, :, :HEAD_M].reshape(own_rows, DI),
            bcdt_grads[:, :bcdt_width],
        ],
        axis=1,
    )
    embedded_own = lax.dynamic_slice_in_dim(embedded, device * own_rows, own_rows, axis=1)
    grad_patch = tn(embedded_own, embed_grad_all)
    own_words = byte_table.shape[0]
    words = device * own_words + jnp.arange(own_words, dtype=jnp.int32)
    chosen = (ids_all[:, :, None] == words).astype(LOW) * keep_all[:, :, None].astype(LOW)
    word_sums = tn(chosen.reshape(everything, PATCH * own_words), embed_grad_all)
    grad_table = jnp.einsum(
        "kvd,ked->ve",
        word_sums.reshape(PATCH, own_words, D),
        patch_all.astype(FULL).reshape(PATCH, EMB, D),
        precision=highest,
    )

    owned = 3 * D + DI + (CONV + 1) * 2 * STATE
    small = jnp.sum(sums_all[:, :owned], axis=0)
    gain_grads = jnp.split(small[: 3 * D + DI], [D, D + DI, 2 * D + DI])
    conv_own = sums_all[:, owned : owned + (CONV + 1) * HEAD_M].reshape(devices, CONV + 1, HEAD_M)
    conv_grads = jnp.concatenate(
        [
            conv_own.transpose(1, 0, 2).reshape(CONV + 1, DI),
            small[3 * D + DI :].reshape(CONV + 1, 2 * STATE),
        ],
        axis=1,
    )
    number_grads = sums_all[:, owned + (CONV + 1) * HEAD_M : owned + (CONV + 1) * HEAD_M + 3].T
    return (
        out_rows,
        grad_table,
        grad_patch,
        gain_grads[0],
        grad_in,
        conv_grads[:CONV],
        conv_grads[CONV],
        number_grads[0],
        number_grads[1],
        number_grads[2],
        gain_grads[1],
        grad_out,
        middle_sums[:, 4 * D :].T,
        gain_grads[2],
        middle_sums[:, :D],
        middle_sums[:, D : 2 * D],
        middle_sums[:, 2 * D : 3 * D],
        middle_sums[:, 3 * D : 4 * D],
        gain_grads[3],
        grad_gate,
        grad_up,
        grad_down,
    )


def solution(mesh):
    placed = (
        P((NARROW, WIDE)),
        P(),
        P(),
        P((NARROW, WIDE), None),
        P((NARROW, WIDE), None),
        P(),
        P((NARROW, WIDE), None),
        P(),
        P(),
        P(),
        P(),
        P(),
        P(),
        P((NARROW, WIDE), None),
        P(None, (NARROW, WIDE)),
        P(),
        P((NARROW, WIDE), None),
        P((NARROW, WIDE), None),
        P((NARROW, WIDE), None),
        P((NARROW, WIDE), None),
        P(),
        P(NARROW, WIDE),
        P(NARROW, WIDE),
        P(WIDE, NARROW),
        P((NARROW, WIDE), None),
    )
    return jax.shard_map(
        per_device_heads if mesh.size == HEADS_M else per_device_rows,
        mesh=mesh,
        in_specs=placed,
        out_specs=(
            P((NARROW, WIDE), None),
            P((NARROW, WIDE), None),
            P((NARROW, WIDE), None),
            P(),
            P((NARROW, WIDE), None),
            P(),
            P(),
            P(),
            P(),
            P(),
            P(),
            P((NARROW, WIDE), None),
            P(None, (NARROW, WIDE)),
            P(),
            P((NARROW, WIDE), None),
            P((NARROW, WIDE), None),
            P((NARROW, WIDE), None),
            P((NARROW, WIDE), None),
            P(),
            P(NARROW, WIDE),
            P(NARROW, WIDE),
            P(WIDE, NARROW),
        ),
        check_vma=False,
    )
```

```python
from functools import partial

import jax
import jax.numpy as jnp
from jax import lax
from jax.experimental import pallas as pl
from jax.experimental.pallas import tpu as pltpu
from jax.sharding import PartitionSpec as P

NARROW = "narrow"
WIDE = "wide"
D = 1024
PATCH = 8
EMB = 128
VOCAB = 256
HEADS_M = 32
HEAD_M = 64
DI = 2048
STATE = 128
CONV = 4
HEADS_A = 16
HEAD_A = 64


epsilon = 1e-05
highest = lax.Precision.HIGHEST
masked_score = -1e30


def running_sum(x):
    place = jnp.arange(x.shape[0])
    seen = place[:, None] >= place[None, :]
    if x.ndim == 1:
        return jnp.sum(jnp.where(seen, x[None, :], 0), axis=1).astype(x.dtype)
    return jnp.dot(seen.astype(x.dtype), x, precision=highest)


def passed_along(x, axis, by):
    peers = lax.axis_size(axis)
    pairs = [(i, i + by) for i in range(peers) if 0 <= i + by < peers]
    return lax.ppermute(x, axis, pairs)


def prefix_2(x, axis, join, neutral):
    place = lax.axis_index(axis)
    gathered = jax.tree.map(
        lambda a, kind: lax.all_gather(a.astype(kind), axis), x, (jnp.bfloat16, jnp.bfloat16)
    )
    state = jax.tree.map(lambda a, e: jnp.zeros_like(a) + jnp.asarray(e, a.dtype), x, neutral)

    def prefix_one(hop, state):
        return join(
            state,
            jax.tree.map(
                lambda a, own: lax.dynamic_index_in_dim(a, hop, 0, False).astype(own.dtype),
                gathered,
                x,
            ),
        )

    return lax.fori_loop(0, place, prefix_one, state)


def carried_in_2(x, axis, join, neutral):
    count = lax.axis_size(axis)
    place = lax.axis_index(axis)
    ahead = count - 1 - place
    gathered = jax.tree.map(
        lambda a, kind: lax.all_gather(a.astype(kind), axis),
        x,
        jax.tree.map(lambda a: jnp.bfloat16 if a.dtype == jnp.float32 else a.dtype, x),
    )
    state = jax.tree.map(lambda a, e: jnp.zeros_like(a) + jnp.asarray(e, a.dtype), x, neutral)

    def carried_one(hop, state):
        source = count - 1 - hop
        return join(
            state,
            jax.tree.map(
                lambda a, own: lax.dynamic_index_in_dim(a, source, 0, False).astype(own.dtype),
                gathered,
                x,
            ),
        )

    return lax.fori_loop(0, ahead, carried_one, state)


def root_norm(values, gain):
    return values * lax.rsqrt(jnp.mean(values * values, axis=-1, keepdims=True) + epsilon) * gain


def patch_layout(doc_patches, pad_bytes, first_index, patch_count):
    patch_index = first_index + jnp.arange(patch_count, dtype=jnp.int32)
    doc_ends = running_sum(doc_patches)
    doc_index = jnp.arange(doc_patches.shape[0], dtype=jnp.int32)
    segment = jnp.sum((patch_index[:, None] >= doc_ends[None, :]).astype(jnp.int32), axis=1)
    owner_mask = segment[:, None] == doc_index[None, :]
    last_end = jnp.sum(jnp.where(owner_mask, doc_ends[None, :] - 1, 0), axis=1)
    doc_starts = jnp.sum(jnp.where(owner_mask, (doc_ends - doc_patches)[None, :], 0), axis=1)
    pad_count = jnp.sum(jnp.where(owner_mask, pad_bytes[None, :], 0), axis=1)
    offset = jnp.arange(PATCH, dtype=jnp.int32)
    padded = (patch_index == last_end)[:, None] & (offset[None, :] >= PATCH - pad_count[:, None])
    keep_mask = 1.0 - padded.astype(jnp.float32).reshape(-1)
    return (segment, (patch_index == doc_starts).astype(jnp.int32), keep_mask)


def ssd_terms(layout, projected, rim_rows, small_params):
    conv_weight, conv_bias, step_bias, log_rate, skip_gain = small_params
    segment, rim_segment, first_patch = layout
    conv_in = projected[:, DI : 2 * DI + 2 * STATE]
    patch_count = conv_in.shape[0]
    padded = jnp.concatenate([rim_rows, conv_in], 0)
    padded_seg = jnp.concatenate([rim_segment, segment], 0)
    conv_sum = conv_bias
    for conv_tap in range(CONV):
        same_doc = (padded_seg[conv_tap : conv_tap + patch_count] == segment).astype(jnp.float32)[
            :, None
        ]
        conv_sum = (
            conv_sum + conv_weight[conv_tap] * padded[conv_tap : conv_tap + patch_count] * same_doc
        )
    activated = jax.nn.silu(conv_sum)
    values = activated[:, :DI].reshape(patch_count, HEADS_M, HEAD_M)
    input_map = activated[:, DI : DI + STATE]
    output_map = activated[:, DI + STATE :]
    time_steps = jax.nn.softplus(projected[:, 2 * DI + 2 * STATE :] + step_bias)
    cumulative = running_sum(-time_steps * jnp.exp(log_rate))
    no_reset = (running_sum(first_patch) == 0).astype(jnp.float32)
    return (values, input_map, output_map, time_steps, cumulative, no_reset)


def local_state(layout, projected, rim_rows, small_params):
    values, input_map, output_map, time_steps, cumulative, no_reset = ssd_terms(
        layout, projected, rim_rows, small_params
    )
    segment = layout[0]
    decay_tail = (
        jnp.exp(cumulative[-1][None, :] - cumulative)
        * (segment == segment[-1]).astype(jnp.float32)[:, None]
        * time_steps
    )
    state_local = jnp.einsum("sh,shp,sn->hpn", decay_tail, values, input_map, precision=highest)
    decay_total = jnp.exp(cumulative[-1]) * no_reset[-1]
    return (decay_total, state_local)


def mixer_output(layout, projected, rim_rows, small_params, incoming, gated_gain):
    values, input_map, output_map, time_steps, cumulative, no_reset = ssd_terms(
        layout, projected, rim_rows, small_params
    )
    segment = layout[0]
    patch_count = values.shape[0]
    position = jnp.arange(patch_count)
    visible = (segment[:, None] == segment[None, :]) & (position[:, None] >= position[None, :])
    log_gap = jnp.where(visible[:, :, None], cumulative[:, None, :] - cumulative[None, :, :], 0.0)
    inner = jnp.dot(output_map, input_map.T, precision=highest)
    weight = (
        jnp.exp(log_gap)
        * visible[:, :, None].astype(jnp.float32)
        * time_steps[None, :, :]
        * inner[:, :, None]
    )
    within = jnp.einsum("tsh,shp->thp", weight, values, precision=highest)
    carried_in = (
        jnp.einsum("tn,hpn->thp", output_map, incoming, precision=highest)
        * (jnp.exp(cumulative) * no_reset[:, None])[:, :, None]
    )
    result = (within + carried_in + small_params[4][None, :, None] * values).reshape(
        patch_count, DI
    )
    gated_rows = result * jax.nn.silu(projected[:, :DI])
    return root_norm(gated_rows, gated_gain)


def combine_states(earlier, following):
    return (earlier[0] * following[0], following[0][:, None, None] * earlier[1] + following[1])


def attend(stream, gain_attn, query_all, key_all, value_all):
    head_shape = (-1, PATCH, HEADS_A, HEAD_A)
    normed_attn = root_norm(stream, gain_attn).astype(jnp.bfloat16)
    queries = jnp.dot(normed_attn, query_all, preferred_element_type=jnp.float32).astype(
        jnp.bfloat16
    )
    key_rows = jnp.dot(normed_attn, key_all, preferred_element_type=jnp.float32).astype(
        jnp.bfloat16
    )
    value_rows = jnp.dot(normed_attn, value_all, preferred_element_type=jnp.float32).astype(
        jnp.bfloat16
    )
    scores = jnp.einsum(
        "pqhe,pkhe->phqk",
        queries.reshape(head_shape),
        key_rows.reshape(head_shape),
        preferred_element_type=jnp.float32,
    ) * HEAD_A ** (-0.5)
    position = jnp.arange(PATCH)
    causal = position[:, None] >= position[None, :]
    attn_probs = jax.nn.softmax(jnp.where(causal, scores, masked_score), axis=-1)
    mixed_heads = jnp.einsum(
        "phqk,pkhe->pqhe",
        attn_probs.astype(jnp.bfloat16),
        value_rows.reshape(head_shape),
        preferred_element_type=jnp.float32,
    )
    mixed_heads = mixed_heads.reshape(stream.shape[0], -1).astype(jnp.bfloat16)
    return (normed_attn, queries, key_rows, value_rows, attn_probs, mixed_heads)


def spread(values):
    by_rows = lax.all_to_all(values, NARROW, split_axis=1, concat_axis=0, tiled=True)
    return lax.all_gather(by_rows, WIDE, axis=0, tiled=True)


def collect(term_fn, row_count):
    summed = lax.psum_scatter(
        term_fn(jnp.int32(0), row_count * lax.axis_size(WIDE)).astype(jnp.bfloat16),
        WIDE,
        scatter_dimension=0,
        tiled=True,
    )
    return lax.all_to_all(summed, NARROW, split_axis=0, concat_axis=1, tiled=True)


def narrow_total(partial_rows):
    return lax.psum(partial_rows, NARROW).astype(jnp.float32)


def silu_back(gate_up, hidden_grad, hidden_width):
    gate_rows = gate_up[:, :hidden_width]
    up_rows = gate_up[:, hidden_width:]
    sigmoid = jax.nn.sigmoid(gate_rows)
    gate_grad = hidden_grad * up_rows * sigmoid * (1.0 + gate_rows * (1.0 - sigmoid))
    up_grad = hidden_grad * gate_rows * sigmoid
    return jnp.concatenate([gate_grad, up_grad], axis=1)


def per_device_rows(
    byte_ids,
    doc_patches,
    pad_bytes,
    byte_table,
    patch_weight,
    gain_mix,
    in_weight,
    conv_weight,
    conv_bias,
    step_bias,
    log_rate,
    skip_gain,
    gated_gain,
    out_weight,
    local_weight,
    gain_attn,
    query_weight,
    key_weight,
    value_weight,
    attn_weight,
    feed_gain,
    gate_weight,
    up_weight,
    down_weight,
    cotangent,
):
    byte_rows = byte_ids.shape[0]
    patches = byte_rows // PATCH
    device = lax.axis_index((NARROW, WIDE))
    wide_count = lax.axis_size(WIDE)
    segment, first_patch, keep_mask = patch_layout(
        doc_patches, pad_bytes, device * patches, patches
    )
    rim_segment = patch_layout(doc_patches, pad_bytes, device * patches - (CONV - 1), CONV - 1)[0]
    layout = (segment, rim_segment, first_patch)
    gathered = (
        lax.all_gather(byte_table, (NARROW, WIDE), axis=0, tiled=True),
        lax.all_gather(patch_weight, (NARROW, WIDE), axis=0, tiled=True),
        lax.all_gather(in_weight, (NARROW, WIDE), axis=0, tiled=True),
        lax.all_gather(out_weight, (NARROW, WIDE), axis=0, tiled=True),
        lax.all_gather(local_weight, (NARROW, WIDE), axis=1, tiled=True),
        lax.all_gather(query_weight, (NARROW, WIDE), axis=0, tiled=True),
        lax.all_gather(key_weight, (NARROW, WIDE), axis=0, tiled=True),
        lax.all_gather(value_weight, (NARROW, WIDE), axis=0, tiled=True),
        lax.all_gather(attn_weight, (NARROW, WIDE), axis=0, tiled=True),
    )
    table_all, patch_all, in_all, out_all, local_all, query_all, key_all, value_all, attn_all = (
        gathered
    )
    onehot = (byte_ids[:, None] == jnp.arange(VOCAB, dtype=jnp.int32)[None, :]).astype(jnp.bfloat16)
    embedded = (
        (jnp.dot(onehot, table_all, preferred_element_type=jnp.float32) * keep_mask[:, None])
        .astype(jnp.bfloat16)
        .reshape(patches, D)
    )
    mixed_in = jnp.dot(embedded, patch_all, preferred_element_type=jnp.float32)
    normed_mix = root_norm(mixed_in, gain_mix).astype(jnp.bfloat16)
    projected = jnp.dot(normed_mix, in_all, preferred_element_type=jnp.float32).astype(jnp.bfloat16)
    rim_rows = passed_along(
        projected[patches - (CONV - 1) :, DI : 2 * DI + 2 * STATE], (NARROW, WIDE), 1
    ).astype(jnp.float32)
    projected_f = projected.astype(jnp.float32)
    small_params = (conv_weight, conv_bias, step_bias, log_rate, skip_gain)
    (decay_total, state_local), state_back = jax.vjp(
        partial(local_state, layout), projected_f, rim_rows, small_params
    )
    prefix = prefix_2(
        (decay_total, state_local),
        (NARROW, WIDE),
        combine_states,
        (jnp.ones_like(decay_total), jnp.zeros_like(state_local)),
    )
    incoming = prefix[1]
    gated_norm, mixer_back = jax.vjp(
        partial(mixer_output, layout), projected_f, rim_rows, small_params, incoming, gated_gain
    )
    gated_low = gated_norm.astype(jnp.bfloat16)
    global_out = mixed_in + jnp.dot(gated_low, out_all, preferred_element_type=jnp.float32)
    local_rows = global_out.astype(jnp.bfloat16).reshape(byte_rows, EMB)
    stream = jnp.dot(local_rows, local_all, preferred_element_type=jnp.float32)
    normed_attn, queries, key_rows, value_rows, attn_probs, mixed_heads = attend(
        stream, gain_attn, query_all, key_all, value_all
    )
    after_attn = stream + jnp.dot(mixed_heads, attn_all, preferred_element_type=jnp.float32)
    normed_feed = root_norm(after_attn, feed_gain).astype(jnp.bfloat16)
    out_grad = cotangent.astype(jnp.float32) * keep_mask[:, None]
    feed_grad = out_grad.astype(jnp.bfloat16)
    grid_in = spread(normed_feed)
    both_weights = jnp.concatenate([gate_weight, up_weight], axis=1)
    hidden_width = gate_weight.shape[1]
    grid_share = grid_in.shape[0] // wide_count
    gate_up_part = jnp.dot(grid_in, both_weights, preferred_element_type=jnp.float32).astype(
        jnp.bfloat16
    )
    gate_up = narrow_total(gate_up_part)
    hidden = (jax.nn.silu(gate_up[:, :hidden_width]) * gate_up[:, hidden_width:]).astype(
        jnp.bfloat16
    )

    def down_term(first_row, row_count):
        return jnp.dot(hidden, down_weight, preferred_element_type=jnp.float32)

    feed_out = collect(down_term, grid_share)
    grid_grad = spread(feed_grad)
    grad_down = jnp.einsum("gf,gd->fd", hidden, grid_grad, preferred_element_type=jnp.float32)
    hidden_part = jnp.einsum(
        "gd,fd->gf", grid_grad, down_weight, preferred_element_type=jnp.float32
    ).astype(jnp.bfloat16)
    hidden_grad = narrow_total(hidden_part)
    gate_up_grad = silu_back(gate_up, hidden_grad, hidden_width).astype(jnp.bfloat16)
    grad_both = jnp.einsum("gd,gf->df", grid_in, gate_up_grad, preferred_element_type=jnp.float32)

    def back_term(first_row, row_count):
        return jnp.einsum(
            "gf,df->gd", gate_up_grad, both_weights, preferred_element_type=jnp.float32
        )

    feed_in_grad = collect(back_term, grid_share)
    grad_gate = grad_both[:, :hidden_width]
    grad_up = grad_both[:, hidden_width:]
    after_feed = after_attn + feed_out.astype(jnp.float32)
    out_rows = (after_feed * keep_mask[:, None]).astype(jnp.bfloat16)
    feed_normed, feed_norm_back = jax.vjp(root_norm, after_attn, feed_gain)
    after_norm_grad, grad_feed_gain = feed_norm_back(feed_in_grad.astype(jnp.float32))
    after_grad = out_grad + after_norm_grad
    head_shape = (-1, PATCH, HEADS_A, HEAD_A)
    score_scale = HEAD_A ** (-0.5)
    attn_grad = after_grad.astype(jnp.bfloat16)
    grad_attn = jnp.einsum("rd,re->de", mixed_heads, attn_grad, preferred_element_type=jnp.float32)
    heads_grad = (
        jnp.einsum("re,de->rd", attn_grad, attn_all, preferred_element_type=jnp.float32)
        .astype(jnp.bfloat16)
        .reshape(head_shape)
    )
    probs_grad = jnp.einsum(
        "pqhe,pkhe->phqk",
        heads_grad,
        value_rows.reshape(head_shape),
        preferred_element_type=jnp.float32,
    )
    value_grad = (
        jnp.einsum(
            "phqk,pqhe->pkhe",
            attn_probs.astype(jnp.bfloat16),
            heads_grad,
            preferred_element_type=jnp.float32,
        )
        .reshape(byte_rows, D)
        .astype(jnp.bfloat16)
    )
    score_grad = (
        attn_probs * (probs_grad - jnp.sum(attn_probs * probs_grad, axis=-1, keepdims=True))
    ).astype(jnp.bfloat16)
    query_grad = (
        (
            jnp.einsum(
                "phqk,pkhe->pqhe",
                score_grad,
                key_rows.reshape(head_shape),
                preferred_element_type=jnp.float32,
            )
            * score_scale
        )
        .reshape(byte_rows, D)
        .astype(jnp.bfloat16)
    )
    key_grad = (
        (
            jnp.einsum(
                "phqk,pqhe->pkhe",
                score_grad,
                queries.reshape(head_shape),
                preferred_element_type=jnp.float32,
            )
            * score_scale
        )
        .reshape(byte_rows, D)
        .astype(jnp.bfloat16)
    )
    grad_query = jnp.einsum(
        "rd,re->de", normed_attn, query_grad, preferred_element_type=jnp.float32
    )
    grad_key = jnp.einsum("rd,re->de", normed_attn, key_grad, preferred_element_type=jnp.float32)
    grad_value = jnp.einsum(
        "rd,re->de", normed_attn, value_grad, preferred_element_type=jnp.float32
    )
    normed_grad = jnp.einsum("re,de->rd", query_grad, query_all, preferred_element_type=jnp.float32)
    normed_grad = normed_grad + jnp.einsum(
        "re,de->rd", key_grad, key_all, preferred_element_type=jnp.float32
    )
    normed_grad = normed_grad + jnp.einsum(
        "re,de->rd", value_grad, value_all, preferred_element_type=jnp.float32
    )
    attn_normed, attn_norm_back = jax.vjp(root_norm, stream, gain_attn)
    stream_norm_grad, grad_gain_attn = attn_norm_back(normed_grad)
    stream_grad = (after_grad + stream_norm_grad).astype(jnp.bfloat16)
    grad_local = jnp.einsum(
        "re,rd->ed", local_rows, stream_grad, preferred_element_type=jnp.float32
    )
    global_grad = jnp.einsum(
        "rd,ed->re", stream_grad, local_all, preferred_element_type=jnp.float32
    ).reshape(patches, D)
    mix_grad = global_grad.astype(jnp.bfloat16)
    grad_out = jnp.einsum("pi,pd->id", gated_low, mix_grad, preferred_element_type=jnp.float32)
    gated_grad = jnp.einsum("pd,id->pi", mix_grad, out_all, preferred_element_type=jnp.float32)
    proj_grad_mix, rim_grad_mix, small_grad_mix, incoming_grad, grad_gated_gain = mixer_back(
        gated_grad
    )
    suffix = carried_in_2(
        (decay_total, incoming_grad),
        (NARROW, WIDE),
        combine_states,
        (jnp.ones_like(decay_total), jnp.zeros_like(incoming_grad)),
    )
    later_grad = suffix[1]
    decay_grad = jnp.sum(later_grad * incoming, axis=(1, 2))
    proj_grad_state, rim_grad_state, small_grad_state = state_back((decay_grad, later_grad))
    rim_from_next = passed_along(rim_grad_mix + rim_grad_state, (NARROW, WIDE), -1)
    proj_grad = proj_grad_mix + proj_grad_state
    proj_grad = proj_grad.at[patches - (CONV - 1) :, DI : 2 * DI + 2 * STATE].add(rim_from_next)
    proj_low = proj_grad.astype(jnp.bfloat16)
    grad_in = jnp.einsum("pd,pk->dk", normed_mix, proj_low, preferred_element_type=jnp.float32)
    normed_mix_grad = jnp.einsum("pk,dk->pd", proj_low, in_all, preferred_element_type=jnp.float32)
    mix_normed, mix_norm_back = jax.vjp(root_norm, mixed_in, gain_mix)
    mixed_norm_grad, grad_gain_mix = mix_norm_back(normed_mix_grad)
    embed_grad = (global_grad + mixed_norm_grad).astype(jnp.bfloat16)
    grad_patch = jnp.einsum("pi,pd->id", embedded, embed_grad, preferred_element_type=jnp.float32)
    byte_grad = (
        jnp.einsum("pd,id->pi", embed_grad, patch_all, preferred_element_type=jnp.float32).reshape(
            byte_rows, EMB
        )
        * keep_mask[:, None]
    )
    grad_table = jnp.dot(onehot.astype(jnp.float32).T, byte_grad, precision=highest)
    shared = (
        lax.psum_scatter(grad_table, (NARROW, WIDE), scatter_dimension=0, tiled=True),
        lax.psum_scatter(grad_patch, (NARROW, WIDE), scatter_dimension=0, tiled=True),
        lax.psum_scatter(grad_in, (NARROW, WIDE), scatter_dimension=0, tiled=True),
        lax.psum_scatter(grad_out, (NARROW, WIDE), scatter_dimension=0, tiled=True),
        lax.psum_scatter(grad_local, (NARROW, WIDE), scatter_dimension=1, tiled=True),
        lax.psum_scatter(grad_query, (NARROW, WIDE), scatter_dimension=0, tiled=True),
        lax.psum_scatter(grad_key, (NARROW, WIDE), scatter_dimension=0, tiled=True),
        lax.psum_scatter(grad_value, (NARROW, WIDE), scatter_dimension=0, tiled=True),
        lax.psum_scatter(grad_attn, (NARROW, WIDE), scatter_dimension=0, tiled=True),
    )
    small_sum = lax.psum(
        (
            small_grad_mix[0] + small_grad_state[0],
            small_grad_mix[1] + small_grad_state[1],
            small_grad_mix[2] + small_grad_state[2],
            small_grad_mix[3] + small_grad_state[3],
            small_grad_mix[4] + small_grad_state[4],
            grad_gain_mix,
            grad_gated_gain,
            grad_gain_attn,
            grad_feed_gain,
        ),
        (NARROW, WIDE),
    )
    return (
        out_rows,
        shared[0],
        shared[1],
        small_sum[5],
        shared[2],
        small_sum[0],
        small_sum[1],
        small_sum[2],
        small_sum[3],
        small_sum[4],
        small_sum[6],
        shared[3],
        shared[4],
        small_sum[7],
        shared[5],
        shared[6],
        shared[7],
        shared[8],
        small_sum[8],
        grad_gate,
        grad_up,
        grad_down,
    )


QUERY = 128
BYTE_BLOCK = 128
MESH = pl.DeviceIdType.MESH
SUM_ROWS = (3 * D + DI + (CONV + 1) * 2 * STATE) // 128
LOW = jnp.bfloat16
FULL = jnp.float32
BOTH = (NARROW, WIDE)


def nn(a, b, precision=None):
    return lax.dot_general(
        a, b, (((1,), (0,)), ((), ())), precision=precision, preferred_element_type=FULL
    )


def nt(a, b, precision=None):
    return lax.dot_general(
        a, b, (((1,), (1,)), ((), ())), precision=precision, preferred_element_type=FULL
    )


def tn(a, b, precision=None):
    return lax.dot_general(
        a, b, (((0,), (0,)), ((), ())), precision=precision, preferred_element_type=FULL
    )


def device_at(place, wide):
    return (lax.div(place, wide), lax.rem(place, wide))


def remote(src, dst, send, recv, peer):
    return pltpu.make_async_remote_copy(
        src_ref=src, dst_ref=dst, send_sem=send, recv_sem=recv, device_id=peer, device_id_type=MESH
    )


def greet_all(devices, wide):
    me = lax.axis_index(NARROW) * wide + lax.axis_index(WIDE)
    barrier = pltpu.get_barrier_semaphore()

    def greet(k, carry):
        peer = device_at(lax.rem(me + k, devices), wide)
        pl.semaphore_signal(barrier, inc=1, device_id=peer, device_id_type=MESH)
        return carry

    lax.fori_loop(1, devices, greet, 0)
    return me, lambda: pl.semaphore_wait(barrier, devices - 1)


def send_blocks(me, devices, wide, src, dst, send, recv):
    def one(k, carry):
        place = lax.rem(me + k, devices)
        remote(src.at[place], dst.at[me], send, recv, device_at(place, wide)).start()
        return carry

    lax.fori_loop(1, devices, one, 0)


def wait_blocks(me, devices, wide, dst, send, recv):
    part = dst.at[pl.ds(0, devices - 1)]
    remote(part, part, send, recv, device_at(me, wide)).wait()


class StagedGather:
    def __init__(self, block, out, sems, narrow, depth):
        n, w = lax.axis_index(NARROW), lax.axis_index(WIDE)
        z, c = lax.div(w, 2), lax.rem(w, 2)
        self.out, self.narrow, self.depth = out, narrow, depth
        self.n, self.c = n, c
        self.sems = [sems.at[i] for i in range(7)]
        self.twin = (n, z * 2 + 1 - c)
        self.n_peers = [lax.rem(n + k, narrow) for k in range(1, narrow)]
        self.w = w
        self.own = pltpu.make_async_copy(block, out.at[n, z, c], self.sems[0])
        self.first = [
            remote(
                block,
                out.at[n, z, c],
                self.sems[1],
                self.sems[2],
                (n, lax.rem(z + k, depth) * 2 + c),
            )
            for k in range(1, depth)
        ]

    def wait_for(self, part, i):
        return remote(part, part, self.sems[i], self.sems[i + 1], self.twin)

    def z_part(self):
        return self.wait_for(self.out.at[self.n, pl.ds(0, self.depth - 1), self.c], 1)

    def n_part(self):
        return self.wait_for(self.out.at[pl.ds(0, self.narrow - 1), :, self.c], 3)

    def start(self):
        self.own.start()
        for copy in self.first:
            copy.start()

    def spread(self):
        self.own.wait()
        self.z_part().wait_recv()
        mine = self.out.at[self.n, :, self.c]
        for m in self.n_peers:
            remote(mine, mine, self.sems[3], self.sems[4], (m, self.w)).start()
        self.wait_for(mine, 5).start()

    def cross(self):
        self.n_part().wait_recv()
        for m in self.n_peers:
            self.wait_for(self.out.at[m, :, self.c], 5).start()

    def finish(self):
        self.wait_for(self.out.at[:, :, 1 - self.c], 5).wait()
        self.z_part().wait_send()
        self.n_part().wait_send()


def greet_lines(narrow, depth):
    n, w = lax.axis_index(NARROW), lax.axis_index(WIDE)
    z, c = lax.div(w, 2), lax.rem(w, 2)
    peers = [(n, lax.rem(z + k, depth) * 2 + c) for k in range(1, depth)]
    peers += [(lax.rem(n + k, narrow), w) for k in range(1, narrow)]
    peers += [(n, z * 2 + 1 - c)]
    barrier = pltpu.get_barrier_semaphore()
    for peer in peers:
        pl.semaphore_signal(barrier, inc=1, device_id=peer, device_id_type=MESH)
    pl.semaphore_wait(barrier, len(peers))


class LineSum:
    def __init__(self, parts, got, sems, place, length, peer_of):
        self.got, self.length = got, length
        self.own = pltpu.make_async_copy(parts.at[place], got.at[0], sems.at[0])
        self.copies = []
        for k in range(1, length):
            there = lax.rem(place + k, length)
            self.copies.append(
                remote(
                    parts.at[there], got.at[k], sems.at[2 * k - 1], sems.at[2 * k], peer_of(there)
                )
            )

    def start(self):
        self.own.start()
        for copy in self.copies:
            copy.start()

    def arrive(self):
        self.own.wait()
        for copy in self.copies:
            copy.wait_recv()

    def total(self, *index):
        summed = self.got[(0,) + index].astype(FULL)
        for k in range(1, self.length):
            summed += self.got[(k,) + index].astype(FULL)
        return summed

    def finish(self):
        for copy in self.copies:
            copy.wait_send()


def start_kernel(
    narrow,
    wide,
    pack,
    table,
    xz_blocks,
    gate,
    up,
    down,
    middle,
    cotangent,
    pack_all,
    table_all,
    xz_all,
    gate_turned,
    up_turned,
    down_turned,
    middle_line,
    others,
    pack_sems,
    table_sems,
    xz_sems,
    turn_send,
    turn_recv,
    own_sems,
    line_send,
    line_recv,
    other_send,
    other_recv,
):
    devices, depth = narrow * wide, wide // 2
    me, arrived = greet_all(devices, wide)
    n, w = lax.axis_index(NARROW), lax.axis_index(WIDE)
    z, c = lax.div(w, 2), lax.rem(w, 2)
    twin = (n, z * 2 + 1 - c)
    rows, units = gate.shape[0], gate.shape[1] // narrow
    columns = down.shape[1]
    gathers = [
        StagedGather(pack, pack_all, pack_sems, narrow, depth),
        StagedGather(table, table_all, table_sems, narrow, depth),
    ]

    def pieces(m):
        mine = pl.ds(m * units, units)
        return (gate.at[:, mine], up.at[:, mine], down.at[mine, :])

    landing = (
        gate_turned.at[pl.ds(n * rows, rows), :],
        up_turned.at[pl.ds(n * rows, rows), :],
        down_turned.at[:, pl.ds(n * columns, columns)],
    )
    turns = []
    for k in range(1, narrow):
        m = lax.rem(n + k, narrow)
        for i, piece in enumerate(pieces(m)):
            turns.append(
                remote(piece, landing[i], turn_send.at[k - 1, i], turn_recv.at[k - 1, i], (m, w))
            )
    own = [
        pltpu.make_async_copy(piece, landing[i], own_sems.at[i])
        for i, piece in enumerate(pieces(n))
    ]
    own.append(pltpu.make_async_copy(xz_blocks.at[me], xz_all.at[me], own_sems.at[3]))
    own.append(pltpu.make_async_copy(middle, middle_line.at[z], own_sems.at[4]))
    lines = [
        remote(middle, middle_line.at[z], line_send, line_recv, (n, lax.rem(z + k, depth) * 2 + c))
        for k in range(1, depth)
    ]
    for k in range(1, narrow):
        peer = (lax.rem(n + narrow - k, narrow), w)
        turns.append(
            remote(cotangent, others.at[k - 1], other_send.at[k - 1], other_recv.at[k - 1], peer)
        )
    arrived()
    for gather in gathers:
        gather.start()
    for copy in turns + own:
        copy.start()
    send_blocks(me, devices, wide, xz_blocks, xz_all, xz_sems.at[0], xz_sems.at[1])
    for copy in lines:
        copy.start()
    for gather in gathers:
        gather.spread()
    for gather in gathers:
        gather.cross()
    for copy in own:
        copy.wait()
    for copy in turns:
        copy.wait()
    for gather in gathers:
        gather.finish()
    wait_blocks(me, devices, wide, xz_all, xz_sems.at[0], xz_sems.at[1])
    part = middle_line.at[pl.ds(0, depth - 1)]
    remote(part, part, line_send, line_recv, twin).wait()


def start_weights(pack, table, xz_blocks, gate, up, down, middle, cotangent, collective_id):
    narrow, wide = lax.axis_size(NARROW), lax.axis_size(WIDE)
    depth = wide // 2
    units = gate.shape[1] // narrow
    dma = pltpu.SemaphoreType.DMA
    anywhere = pl.BlockSpec(memory_space=pl.ANY)

    def low(*shape):
        return jax.ShapeDtypeStruct(shape, LOW)

    outs = pl.pallas_call(
        partial(start_kernel, narrow, wide),
        out_shape=[
            low(narrow, depth, 2, *pack.shape),
            low(narrow, depth, 2, *table.shape),
            low(*xz_blocks.shape),
            low(D, units),
            low(D, units),
            low(units, D),
            low(depth, *middle.shape),
            low(narrow - 1, *cotangent.shape),
        ],
        in_specs=[anywhere] * 8,
        out_specs=[anywhere] * 8,
        scratch_shapes=[
            dma((7,)),
            dma((7,)),
            dma((2,)),
            dma((narrow - 1, 3)),
            dma((narrow - 1, 3)),
            dma((5,)),
            dma,
            dma,
            dma((narrow - 1,)),
            dma((narrow - 1,)),
        ],
        compiler_params=pltpu.CompilerParams(collective_id=collective_id, has_side_effects=True),
        name="start_weights",
    )(pack, table, xz_blocks, gate, up, down, middle, cotangent)
    return (
        outs[0].reshape(-1, pack.shape[1]),
        outs[1].reshape(-1, table.shape[1]),
        outs[2].reshape(D, -1),
    ) + tuple(outs[3:])


def end_kernel(
    narrow,
    depth,
    pack,
    sums,
    middle,
    down_sum,
    pack_all,
    sums_all,
    middle_out,
    down_out,
    middle_got,
    down_got,
    pack_sems,
    sums_sems,
    middle_sems,
    down_send,
    down_recv,
    down_own,
):
    n, w = lax.axis_index(NARROW), lax.axis_index(WIDE)
    z, c = lax.div(w, 2), lax.rem(w, 2)
    greet_lines(narrow, depth)
    gathers = [
        StagedGather(pack, pack_all, pack_sems, narrow, depth),
        StagedGather(sums, sums_all, sums_sems, narrow, depth),
    ]
    line = LineSum(middle, middle_got, middle_sems, z, depth, lambda there: (n, there * 2 + c))
    back = Returned(down_sum, down_got, down_send, down_recv, down_own, n, w, narrow, 1)
    for gather in gathers:
        gather.start()
    line.start()
    back.start()
    for gather in gathers:
        gather.spread()
    line.arrive()
    middle_out[...] = line.total()
    for gather in gathers:
        gather.cross()
    back.arrive()
    down_out[...] = down_got[...].astype(FULL)
    for gather in gathers:
        gather.finish()
    line.finish()
    back.finish()


class Returned:
    def __init__(self, values, got, send, recv, own, n, w, narrow, axis):
        span = values.shape[axis] // narrow
        other = values.shape[1 - axis]

        def block(m):
            mine = pl.ds(m * span, span)
            return values.at[mine, :] if axis == 0 else values.at[:, mine]

        there = pl.ds(n * other, other)
        landing = got.at[:, there] if axis == 0 else got.at[there, :]
        self.own = pltpu.make_async_copy(block(n), landing, own)
        self.copies = []
        for k in range(1, narrow):
            m = lax.rem(n + k, narrow)
            self.copies.append(
                remote(block(m), landing, send.at[k - 1], recv.at[k - 1], (m, w))
            )

    def start(self):
        self.own.start()
        for copy in self.copies:
            copy.start()

    def arrive(self):
        self.own.wait()
        for copy in self.copies:
            copy.wait_recv()

    def finish(self):
        for copy in self.copies:
            copy.wait_send()


def end_gather(pack, sums, middle, down_sum, collective_id):
    narrow, wide = lax.axis_size(NARROW), lax.axis_size(WIDE)
    depth = wide // 2
    dma = pltpu.SemaphoreType.DMA
    anywhere = pl.BlockSpec(memory_space=pl.ANY)
    down_shape = (down_sum.shape[0] * narrow, down_sum.shape[1] // narrow)
    outs = pl.pallas_call(
        partial(end_kernel, narrow, depth),
        out_shape=[
            jax.ShapeDtypeStruct((narrow, depth, 2) + pack.shape, pack.dtype),
            jax.ShapeDtypeStruct((narrow, depth, 2) + sums.shape, sums.dtype),
            jax.ShapeDtypeStruct(middle.shape[1:], FULL),
            jax.ShapeDtypeStruct(down_shape, FULL),
        ],
        in_specs=[anywhere] * 4,
        out_specs=[anywhere] * 2 + [in_vmem()] * 2,
        scratch_shapes=[
            pltpu.VMEM(middle.shape, middle.dtype),
            pltpu.VMEM(down_shape, LOW),
            dma((7,)),
            dma((7,)),
            dma((2 * depth,)),
            dma((narrow - 1,)),
            dma((narrow - 1,)),
            dma,
        ],
        compiler_params=pltpu.CompilerParams(
            collective_id=collective_id, has_side_effects=True, vmem_limit_bytes=32 << 20
        ),
        name="end_gather",
    )(pack, sums, middle, down_sum)
    return [
        outs[0].reshape(-1, pack.shape[1]),
        outs[1].reshape((-1,) + sums.shape),
        outs[2],
        outs[3],
    ]


def softplus(v):
    return jnp.maximum(v, 0.0) + jnp.log1p(jnp.exp(-jnp.abs(v)))


def convolved(window, marks, weight, bias):
    pre = bias + weight[CONV - 1 :] * window[8:]
    for lag in range(1, CONV):
        pre = pre + weight[CONV - 1 - lag : CONV - lag] * (
            window[8 - lag : 8 - lag + QUERY] * marks[:, lag : lag + 1]
        )
    return pre


def decays(marks, dt, step_bias, rate_scale):
    shape = (QUERY, QUERY)
    row = lax.broadcasted_iota(jnp.int32, shape, 0)
    column = lax.broadcasted_iota(jnp.int32, shape, 1)
    lower = (row >= column).astype(FULL)
    segment = jnp.broadcast_to(marks[:, :1], shape)
    visible = (segment == segment.T) & (row >= column)
    delta = jnp.broadcast_to(softplus(dt + step_bias), shape)
    total = nn(lower, -delta * rate_scale, highest)
    gap = jnp.where(visible, total - total.T, 0.0)
    decay = jnp.where(visible, jnp.exp(gap), 0.0)
    last = total[QUERY - 1 :, :]
    begun = jnp.exp(total) * marks[:, 4:5]
    tail = jnp.exp(last - total) * marks[:, 5:6]
    kept = jnp.exp(last) * marks[:1, 6:7]
    return lower, delta, decay, begun, tail, kept


def head_numbers(step_bias, log_rate, skip_gain, me):
    return step_bias[me], jnp.exp(jnp.full((1, QUERY), log_rate[me], FULL)), skip_gain[me]


def head_columns(values, me):
    start = pl.multiple_of(lax.div(me, 2) * 2 * HEAD_M, 2 * HEAD_M)
    pair = values[:, pl.ds(start, 2 * HEAD_M)]
    lane = lax.broadcasted_iota(jnp.int32, pair.shape, 1)
    moved = jnp.concatenate([pair[:, HEAD_M:], pair[:, :HEAD_M]], axis=1)
    odd = jnp.full(pair.shape, lax.rem(me, 2), jnp.int32) == 1
    return jnp.where(lane < HEAD_M, jnp.where(odd, moved, pair), 0.0)


def documents(doc_patches, pad_bytes):
    ends, end = [], 0
    for d in range(doc_patches.shape[0]):
        end = end + doc_patches[d]
        ends.append(end)

    def document(place):
        return sum((place >= end).astype(jnp.int32) for end in ends)

    def kept(place, offset):
        padded = [
            ((place == end - 1) & (offset >= PATCH - pad_bytes[d])).astype(FULL)
            for d, end in enumerate(ends)
        ]
        return 1.0 - sum(padded)

    return document, kept


def patch_marks(document, first, count):
    place = first + lax.broadcasted_iota(jnp.int32, (count, 8), 0)
    kind = lax.broadcasted_iota(jnp.int32, (count, 8), 1)
    opening = lax.div(place, QUERY) * QUERY
    block_mark = jnp.where(kind == CONV, opening - 1, opening + QUERY - 1)
    ahead = jnp.where(kind < CONV, place - kind, block_mark)
    facing = jnp.where(kind == CONV + 2, opening - 1, place)
    same = (document(ahead) == document(facing)) & (ahead >= 0) & (facing >= 0)
    return jnp.where(kind == 0, document(place).astype(FULL), same.astype(FULL))


def mixer_front_kernel(
    narrow,
    wide,
    doc_patches,
    pad_bytes,
    step_biases,
    log_rates,
    skip_gains,
    start,
    table,
    w_xz,
    gain,
    conv_weight,
    conv_bias,
    gate,
    up,
    down,
    middle,
    embedded,
    normed,
    xz,
    bc,
    dt,
    u_out,
    y_out,
    states,
    mixed_in,
    u_got,
    marks,
    keep_rows,
    keep_all,
    gate_all,
    up_all,
    down_all,
    middle_all,
    mixed_all,
    xz_pad,
    bc_pad,
    state,
    u_blocks,
    u_send,
    u_recv,
    own_sems,
    line_send,
    line_recv,
    cross_send,
    cross_recv,
    middle_sems,
):
    devices, depth = narrow * wide, wide // 2
    me, arrived = greet_all(devices, wide)
    n, w = lax.axis_index(NARROW), lax.axis_index(WIDE)
    z, c = lax.div(w, 2), lax.rem(w, 2)
    twin = (n, z * 2 + 1 - c)
    turned = (gate, up, down)
    results = (gate_all, up_all, down_all)
    own = [pltpu.make_async_copy(turned[i], results[i].at[z, c], own_sems.at[i]) for i in range(3)]
    own.append(pltpu.make_async_copy(middle, middle_all.at[n, :, c], own_sems.at[3]))
    for copy in own:
        copy.start()
    beside = n + 1 - 2 * lax.rem(n, 2)
    across = n + 2 - 4 * lax.div(n, 2)
    corner = narrow - 1 - n
    arrived()

    def middle_copy(j, way, owner, src=None):
        there = middle_all.at[owner, j, c]
        peer = twin if way >= 4 else ((beside if way in (0, 3) else across), w)
        return remote(
            there if src is None else src, there, middle_sems.at[0, way, j], middle_sems.at[1, way, j], peer
        )

    for j in range(depth):
        middle_copy(j, 0, n, middle.at[j]).start()
        middle_copy(j, 1, n, middle.at[j]).start()

    def line_copy(i, source, step, src=None):
        there = results[i].at[source, c]
        return remote(
            there if src is None else src,
            there,
            line_send.at[i, source, max(step, 0)],
            line_recv.at[i, source],
            (n, (z + step) * 2 + c),
        )

    def along(i, source, step, src=None):
        @pl.when((z + step >= 0) & (z + step < depth))
        def _():
            line_copy(i, source, step, src).start()

    for i in range(3):
        along(i, z, 1, turned[i])
        along(i, z, -1, turned[i])
    own_middle = remote(
        middle, middle_all.at[n, :, c], middle_sems.at[0, 7, 0], middle_sems.at[1, 7, 0], twin
    )
    own_middle.start()

    def middle_on(j):
        middle_copy(j, 0, beside).wait_recv()
        if j % 2 == 0:
            middle_copy(j, 2, beside).start()
        middle_copy(j, 4, beside).start()
        middle_copy(j, 1, across).wait_recv()
        if j % 2 == 1:
            middle_copy(j, 3, across).start()
        middle_copy(j, 5, across).start()

    def line_on(distance):
        for step in (1, -1):
            source = z - step * distance

            @pl.when((source >= 0) & (source < depth))
            def _():
                for i in range(3):
                    line_copy(i, source, step).wait_recv()
                    along(i, source, step)
                    theirs = results[i].at[source, c]
                    remote(theirs, theirs, cross_send.at[i], cross_recv.at[i], twin).start()

    count = embedded.shape[0]
    patches = u_blocks.shape[1]
    block_rows = 2 * QUERY
    xz_pad[pl.ds(0, 8), :] = jnp.zeros((8, xz_pad.shape[1]), FULL)
    bc_pad[pl.ds(0, 8), :] = jnp.zeros((8, bc_pad.shape[1]), FULL)
    state[...] = jnp.zeros_like(state)
    step_bias, rate_scale, skip = head_numbers(step_biases, log_rates, skip_gains, me)
    document, kept_bytes = documents(doc_patches, pad_bytes)
    for first in range(0, count + 8, (count + 8) // 3):
        part = (count + 8) // 3
        marks[first : first + part, :] = patch_marks(document, first, part)
    byte = lax.broadcasted_iota(jnp.int32, keep_rows.shape[1:], 0)
    for k in range(narrow):
        there = (lax.rem(n + k, narrow) * wide + w) * patches
        keep_rows[k] = kept_bytes(there + lax.div(byte, PATCH), lax.rem(byte, PATCH))
    wx, bx = head_columns(conv_weight, me), head_columns(conv_bias, me)
    wbc, bbc = conv_weight[:, DI:], conv_bias[:, DI:]
    words = lax.broadcasted_iota(jnp.int32, (block_rows, VOCAB), 1).astype(FULL)
    own_lane = lax.broadcasted_iota(jnp.int32, (block_rows, STATE), 1) == me

    def project(i, carry):
        rows = pl.ds(pl.multiple_of(i * block_rows, block_rows), block_rows)
        ids = start[rows, 3 * STATE : 4 * STATE].astype(FULL)
        place = i * block_rows + lax.broadcasted_iota(jnp.int32, (block_rows, PATCH), 0)
        kept = kept_bytes(place, lax.broadcasted_iota(jnp.int32, (block_rows, PATCH), 1))
        keep_all[rows, :] = kept
        for k in range(PATCH):
            chosen = jnp.where(ids[:, k : k + 1] == words, kept[:, k : k + 1], 0.0).astype(LOW)
            embedded[rows, k * EMB : (k + 1) * EMB] = nn(chosen, table[...]).astype(LOW)
        row_embedded = embedded[rows, :]
        for first in range(0, D, WEIGHT_STEP):
            columns = slice(first, first + WEIGHT_STEP)
            weight = start[:, 4 * STATE + first : 4 * STATE + first + WEIGHT_STEP]
            mixed_all[rows, columns] = nn(row_embedded, weight)
        row_normed = (unit_rows(mixed_all[rows, :])[0] * gain[...]).astype(LOW)
        normed[rows, :] = row_normed
        row_xz = nn(row_normed, w_xz[...]).astype(LOW)
        row_bcdt = nn(row_normed, start[:, : 3 * STATE]).astype(LOW)
        xz[rows, :] = row_xz
        bc[rows, :] = row_bcdt[:, : 2 * STATE]
        own_dt = jnp.where(own_lane, row_bcdt[:, 2 * STATE :].astype(FULL), 0.0)
        dt[rows, :] = jnp.sum(own_dt, axis=1, keepdims=True)
        padded = pl.ds(pl.multiple_of(i * block_rows + 8, 8), block_rows)
        xz_pad[padded, :] = row_xz.astype(FULL)
        bc_pad[padded, :] = row_bcdt[:, : 2 * STATE].astype(FULL)
        return carry

    lax.fori_loop(0, count // block_rows, project, 0)
    middle_on(0)
    mixed_in[...] = mixed_all[pl.ds(pl.multiple_of(me * patches, patches), patches), :]
    group = QUERY // patches

    def block(i, carry):
        first = pl.multiple_of(i * QUERY, QUERY)
        rows = pl.ds(first, QUERY)
        mark = marks[rows, :]
        act_x = jax.nn.silu(convolved(xz_pad[pl.ds(first, QUERY + 8), :], mark, wx, bx))
        act = jax.nn.silu(convolved(bc_pad[pl.ds(first, QUERY + 8), :], mark, wbc, bbc))
        x, b, c = act_x[:, :HEAD_M], act[:, :STATE], act[:, STATE:]
        lower, delta, decay, begun, tail, kept = decays(mark, dt[rows, :], step_bias, rate_scale)
        weight = nt(c, b, highest) * decay * delta.T
        held = state[...]
        states[i] = held
        y = (
            nn(weight, x, highest)
            + nt(c, held, highest) * begun[:, :HEAD_M]
            + skip * x
        )
        state[...] = held * kept + tn(x * (tail * delta)[:, :HEAD_M], b, highest)
        z = xz[rows, :].astype(FULL)[:, HEAD_M:]
        u = y * jax.nn.silu(z)
        y_out[rows, :] = y
        u_out[rows, :] = u
        u_blocks[pl.ds(i * group, group)] = u.astype(LOW).reshape(group, patches, HEAD_M)
        return carry

    lax.fori_loop(0, count // QUERY, block, 0)
    send_blocks(me, devices, wide, u_blocks, u_got, u_send, u_recv)
    u_got[me] = u_blocks[me]
    line_on(1)
    middle_on(1)
    for copy in own:
        copy.wait()
    for i in range(3):
        mine = results[i].at[z, c]
        remote(mine, mine, cross_send.at[i], cross_recv.at[i], twin).start()
    middle_on(2)
    line_on(2)
    middle_on(3)
    for j in range(depth):
        middle_copy(j, 2 + j % 2, corner).wait_recv()
        middle_copy(j, 6, corner).start()
    line_on(3)
    wait_blocks(me, devices, wide, u_got, u_send, u_recv)
    for i in range(3):
        theirs = results[i].at[:, 1 - c]
        remote(theirs, theirs, cross_send.at[i], cross_recv.at[i], twin).wait()
    own_middle.wait()
    for j in range(depth):
        for way, owner in ((4, beside), (5, across), (6, corner)):
            middle_copy(j, way, owner).wait()
        middle_copy(j, 0, n, middle.at[j]).wait_send()
        middle_copy(j, 1, n, middle.at[j]).wait_send()
        middle_copy(j, 2 + j % 2, n).wait_send()
    for i in range(3):
        for source in range(depth):
            for step in (1, -1):

                @pl.when((step * (z - source) >= 0) & (z + step >= 0) & (z + step < depth))
                def _():
                    line_copy(i, source, step).wait_send()


def mixer_backward_kernel(
    narrow,
    wide,
    step_biases,
    log_rates,
    skip_gains,
    xz,
    bc,
    dt,
    marks,
    conv_weight,
    conv_bias,
    y_in,
    states,
    normed,
    w_xz,
    start,
    mixed_in,
    global_grad,
    gain,
    gated_scale,
    gain_grads,
    gated_gain_grads,
    du_blocks,
    down_parts,
    middle_parts,
    gate_sum,
    up_sum,
    mix_grad,
    end_pack,
    sums,
    bcdt_grads,
    xz_grads,
    down_sum,
    middle_sums,
    gate_out,
    up_out,
    mix_all,
    w_bcdt,
    w_sem,
    dwx,
    dwbc,
    dnumbers,
    xz_pad,
    bc_pad,
    dx_pad,
    dbc_pad,
    dstate,
    du_got,
    dxz,
    dbcdt,
    partial_rows,
    core_got,
    narrow_got,
    z_rows,
    z_got,
    grads,
    grads_got,
    down_got,
    middle_got,
    gate_got,
    up_got,
    du_send,
    du_recv,
    core_send,
    core_recv,
    narrow_send,
    narrow_recv,
    z_send,
    z_recv,
    grads_send,
    grads_recv,
    down_sems,
    middle_sems,
    back_send,
    back_recv,
    back_own,
    mix_sems,
):
    devices = narrow * wide
    depth = wide // 2
    me, arrived = greet_all(devices, wide)
    n, w = lax.axis_index(NARROW), lax.axis_index(WIDE)
    z_place, core = lax.div(w, 2), lax.rem(w, 2)
    twin = (n, z_place * 2 + 1 - core)
    count = xz.shape[0]
    blocks = count // QUERY
    xz_pad[pl.ds(0, 8), :] = jnp.zeros((8, xz_pad.shape[1]), FULL)
    bc_pad[pl.ds(0, 8), :] = jnp.zeros((8, bc_pad.shape[1]), FULL)
    dx_pad[pl.ds(count, 8), :] = jnp.zeros((8, dx_pad.shape[1]), FULL)
    dbc_pad[pl.ds(count, 8), :] = jnp.zeros((8, dbc_pad.shape[1]), FULL)
    dstate[...] = jnp.zeros_like(dstate)
    dwx[...] = jnp.zeros_like(dwx)
    dwbc[...] = jnp.zeros_like(dwbc)
    dnumbers[...] = jnp.zeros_like(dnumbers)
    step_bias, rate_scale, skip = head_numbers(step_biases, log_rates, skip_gains, me)
    wx, bx = head_columns(conv_weight, me), head_columns(conv_bias, me)
    wbc, bbc = conv_weight[:, DI:], conv_bias[:, DI:]
    weight_copy = pltpu.make_async_copy(start.at[:, pl.ds(0, 3 * STATE)], w_bcdt, w_sem)
    weight_copy.start()

    def fill(i, carry):
        first = pl.multiple_of(i * QUERY, QUERY)
        rows = pl.ds(first, QUERY)
        xz_pad[pl.ds(first + 8, QUERY), :] = xz[rows, :].astype(FULL)
        bc_pad[pl.ds(first + 8, QUERY), :] = bc[rows, :].astype(FULL)
        return carry

    arrived()
    send_blocks(me, devices, wide, du_blocks, du_got, du_send, du_recv)
    down_line = LineSum(
        down_parts, down_got, down_sems, z_place, depth, lambda there: (n, there * 2 + core)
    )
    middle_line = LineSum(middle_parts, middle_got, middle_sems, n, narrow, lambda there: (there, w))
    backs = [
        Returned(
            values, landed, back_send.at[i], back_recv.at[i], back_own.at[i], n, w, narrow, 0
        )
        for i, (values, landed) in enumerate(((gate_sum, gate_got), (up_sum, up_got)))
    ]
    mix_gather = StagedGather(mix_grad, mix_all, mix_sems, narrow, depth)
    mix_gather.start()
    for back in backs:
        back.start()
    middle_line.start()
    down_line.start()
    du_got[me] = du_blocks[me]
    lax.fori_loop(0, blocks, fill, 0)
    wait_blocks(me, devices, wide, du_got, du_send, du_recv)
    patches = du_blocks.shape[1]
    group = QUERY // patches
    own_lane = lax.broadcasted_iota(jnp.int32, (QUERY, STATE), 1) == me

    def slope(pre):
        s = jax.nn.sigmoid(pre)
        return s * (1.0 + pre * (1.0 - s))

    def total(v):
        return jnp.sum(jnp.sum(v, axis=1, keepdims=True), axis=0, keepdims=True)

    def conv_back(pad, first, dpre_pad, dpre, weight, dw):
        mark = marks[pl.ds(first, QUERY), :]
        window = pad[pl.ds(first, QUERY + 8), :]
        later = dpre_pad[pl.ds(first, QUERY + 8), :]
        later_marks = marks[pl.ds(first, QUERY + 8), :]
        out = weight[CONV - 1 :] * dpre
        dw[CONV - 1 : CONV, :] += jnp.sum(dpre * window[8:], axis=0, keepdims=True)
        dw[CONV : CONV + 1, :] += jnp.sum(dpre, axis=0, keepdims=True)
        for lag in range(1, CONV):
            tap = CONV - 1 - lag
            out = out + weight[tap : tap + 1] * (
                (later * later_marks[:, lag : lag + 1])[lag : lag + QUERY]
            )
            dw[tap : tap + 1, :] += jnp.sum(
                dpre * (window[8 - lag : 8 - lag + QUERY] * mark[:, lag : lag + 1]),
                axis=0,
                keepdims=True,
            )
        return out

    def block(k, carry):
        i = blocks - 1 - k
        first = pl.multiple_of(i * QUERY, QUERY)
        rows = pl.ds(first, QUERY)
        mark = marks[rows, :]
        pre_x = convolved(xz_pad[pl.ds(first, QUERY + 8), :], mark, wx, bx)
        pre = convolved(bc_pad[pl.ds(first, QUERY + 8), :], mark, wbc, bbc)
        act = jax.nn.silu(pre)
        x, b, c = jax.nn.silu(pre_x)[:, :HEAD_M], act[:, :STATE], act[:, STATE:]
        step = dt[rows, :]
        lower, delta, decay, begun, tail, kept = decays(mark, step, step_bias, rate_scale)
        held, dheld = states[i], dstate[...]
        z = xz[rows, :].astype(FULL)[:, HEAD_M:]
        du = du_got[pl.ds(i * group, group)].astype(FULL).reshape(QUERY, HEAD_M)
        y = y_in[rows, :]
        dy = du * jax.nn.silu(z)
        dz = du * y * slope(z)
        scores = nt(c, b, highest)
        reach = decay * delta.T
        dweight = nt(dy, x, highest)
        dscores = dweight * reach
        fed = x * (tail * delta)[:, :HEAD_M]
        begun_dy = dy * begun[:, :HEAD_M]
        dc = nn(dscores, b, highest) + nn(begun_dy, held, highest)
        db = tn(dscores, c, highest) + nn(fed, dheld, highest)
        dfed = nt(b, dheld, highest)
        dx = skip * dy + tn(scores * reach, dy, highest) + (tail * delta)[:, :HEAD_M] * dfed
        moved = dweight * scores * decay
        turned = moved.T
        ddelta = jnp.sum(turned, axis=1, keepdims=True)
        dtotal = jnp.sum(moved * delta.T, axis=1, keepdims=True) - ddelta * delta[:, :1]
        dtotal += jnp.sum(begun_dy * nt(c, held, highest), axis=1, keepdims=True)
        dtail = jnp.sum(dfed * x, axis=1, keepdims=True)
        ddelta += dtail * tail[:, :1]
        dtail = dtail * (tail * delta)[:, :1]
        dtotal -= dtail
        dlast = jnp.sum(dtail, axis=0, keepdims=True) + total(dheld * held * kept)
        dlog = tn(lower, jnp.broadcast_to(dtotal, (QUERY, QUERY)), highest)[:, :1] + dlast
        ddelta -= dlog * rate_scale[:, :1]
        dstep = ddelta * jax.nn.sigmoid(step + step_bias)
        dbcdt[rows, 2 * STATE :] = jnp.where(own_lane, dstep, 0.0).astype(LOW)
        dnumbers[0:1, :] += jnp.broadcast_to(jnp.sum(dstep, axis=0, keepdims=True), (1, 128))
        dnumbers[1:2, :] -= jnp.broadcast_to(
            jnp.sum(dlog * delta[:, :1] * rate_scale[:, :1], axis=0, keepdims=True), (1, 128)
        )
        dnumbers[2:3, :] += jnp.broadcast_to(total(dy * x), (1, 128))
        dstate[...] = dheld * kept + tn(begun_dy, c, highest)
        dpre_x = jnp.concatenate([dx, jnp.zeros_like(dx)], axis=1) * slope(pre_x)
        dpre = jnp.concatenate([db, dc], axis=1) * slope(pre)
        dx_pad[rows, :] = dpre_x
        dbc_pad[rows, :] = dpre
        dxz[rows, :] = jnp.concatenate([dz, dz], axis=1).astype(LOW)
        return carry

    lax.fori_loop(0, blocks, block, 0)

    def unconvolve(i, carry):
        first = pl.multiple_of(i * QUERY, QUERY)
        rows = pl.ds(first, QUERY)
        dxr = conv_back(xz_pad, first, dx_pad, dx_pad[rows, :], wx, dwx)
        left = lax.broadcasted_iota(jnp.int32, dxr.shape, 1) < HEAD_M
        dxz[rows, :] = jnp.where(left, dxr, dxz[rows, :].astype(FULL)).astype(LOW)
        dbcdt[rows, : 2 * STATE] = conv_back(
            bc_pad, first, dbc_pad, dbc_pad[rows, :], wbc, dwbc
        ).astype(LOW)
        return carry

    mix_gather.spread()
    lax.fori_loop(0, blocks, unconvolve, 0)

    width = normed.shape[1]
    own_rows = xz_grads.shape[1]

    weight_copy.wait()

    def rows_of(m, carry):
        for z in range(depth):
            first = (m * depth + z) * 2 * patches
            rows = pl.ds(pl.multiple_of(first, 2 * patches), 2 * patches)
            values = nt(dxz[rows, :], w_xz[...]) + nt(dbcdt[rows, :], w_bcdt[...])
            partial_rows[m, z, :, :, :width] = values.astype(LOW).reshape(2, patches, width)
        return carry

    lax.fori_loop(0, narrow, rows_of, 0)

    def weight_grads(m, carry):
        span = width // narrow
        columns = pl.ds(pl.multiple_of(m * span, span), span)
        lhs = normed[:, columns]
        grads[pl.ds(m * 2 * depth, 2 * depth)] = (
            tn(lhs, dxz[...]).astype(LOW).reshape(2 * depth, own_rows, 2 * HEAD_M)
        )
        partial_rows[m, :, :, :, width:] = (
            tn(lhs, dbcdt[...]).astype(LOW).reshape(depth, 2, own_rows, 3 * STATE)
        )
        return carry

    lax.fori_loop(0, narrow, weight_grads, 0)
    to_twin = remote(partial_rows.at[:, :, 1 - core], core_got, core_send, core_recv, twin)
    to_twin.start()
    send_blocks(me, devices, wide, grads, grads_got, grads_send, grads_recv)
    grads_got[me] = grads[me]
    for back, landed, out in zip(backs, (gate_got, up_got), (gate_out, up_out)):
        back.arrive()
        out[...] = landed[...].astype(FULL)
    to_twin.wait_recv()

    def narrow_copy(k, m):
        return remote(
            core_got.at[m], narrow_got.at[k - 1], narrow_send.at[k - 1], narrow_recv.at[k - 1], (m, w)
        )

    for k in range(1, narrow):
        m = lax.rem(n + k, narrow)
        for z in range(depth):
            core_got[m, z] = (
                core_got[m, z].astype(FULL) + partial_rows[m, z, core].astype(FULL)
            ).astype(LOW)
        narrow_copy(k, m).start()
    mix_gather.cross()
    middle_line.arrive()
    for z in range(depth):
        middle_sums[z] = middle_line.total(z).astype(LOW)
    for k in range(1, narrow):
        narrow_copy(k, n).wait_recv()
    for z in range(depth):
        total_rows = core_got[n, z].astype(FULL) + partial_rows[n, z, core].astype(FULL)
        for k in range(1, narrow):
            total_rows += narrow_got[k - 1, z].astype(FULL)
        z_rows[z] = total_rows.astype(LOW)

    def z_copy(k, place):
        return remote(
            z_rows.at[place], z_got.at[k - 1], z_send.at[k - 1], z_recv.at[k - 1], (n, place * 2 + core)
        )

    for k in range(1, depth):
        z_copy(k, lax.rem(z_place + k, depth)).start()
    down_line.arrive()
    down_sum[...] = down_line.total().astype(LOW)
    wait_blocks(me, devices, wide, grads_got, grads_send, grads_recv)
    xz_grads[...] = grads_got[...]
    total_rows = z_rows[z_place].astype(FULL)
    for k in range(1, depth):
        z_copy(k, z_place).wait_recv()
        total_rows += z_got[k - 1].astype(FULL)
    bcdt_grads[...] = total_rows[:, width:]
    unit, scale = unit_rows(mixed_in[...])
    normed_grad = total_rows[:, :width]
    embed_grad = global_grad[...] + norm_back(normed_grad, gain[...], unit, scale)
    end_pack[:, :width] = embed_grad.astype(LOW)
    end_pack[:, width:] = gated_scale[...].astype(LOW)
    gain_mix_grad = jnp.sum(normed_grad * unit, axis=0, keepdims=True)
    wide_rows = [gain_mix_grad] + [gated_gain_grads[i : i + 1, :] for i in range(2)]
    wide_rows += [gain_grads[i : i + 1, :] for i in range(2)]
    wide_rows += [dwbc[i : i + 1, :] for i in range(CONV + 1)]
    wide_rows += [dwx[i : i + 1, :] for i in range(CONV + 1)]
    row = 0
    for values in wide_rows:
        for first in range(0, values.shape[1], 128):
            sums[row : row + 1, :] = values[:, first : first + 128]
            row += 1
    lane = lax.broadcasted_iota(jnp.int32, (1, 128), 1)
    sums[row : row + 1, :] = sum(
        jnp.where(lane == i, dnumbers[i : i + 1, :], 0.0) for i in range(3)
    )
    mix_gather.finish()
    down_line.finish()
    middle_line.finish()
    for back in backs:
        back.finish()
    to_twin.wait_send()
    for k in range(1, narrow):
        narrow_copy(k, n).wait_send()
    for k in range(1, depth):
        z_copy(k, z_place).wait_send()


def in_smem():
    return pl.BlockSpec(memory_space=pltpu.SMEM)


def in_vmem():
    return pl.BlockSpec(memory_space=pltpu.VMEM)


def mixer_front(scalars, start, table, w_xz, gain, conv_weight, conv_bias, turned, middle, collective_id):
    narrow, wide = lax.axis_size(NARROW), lax.axis_size(WIDE)
    devices = narrow * wide
    count = start.shape[0]
    patches = count // devices
    dma = pltpu.SemaphoreType.DMA

    def full(*shape):
        return jax.ShapeDtypeStruct(shape, FULL)

    def low(*shape):
        return jax.ShapeDtypeStruct(shape, LOW)

    depth = wide // 2
    anywhere = pl.BlockSpec(memory_space=pl.ANY)
    outs = pl.pallas_call(
        partial(mixer_front_kernel, narrow, wide),
        out_shape=[
            low(count, D),
            low(count, D),
            low(count, 2 * HEAD_M),
            low(count, 2 * STATE),
            full(count, 1),
            full(count, HEAD_M),
            full(count, HEAD_M),
            full(count // QUERY, HEAD_M, STATE),
            full(patches, D),
            low(devices, patches, HEAD_M),
            full(count + 8, 8),
            full(narrow, patches * PATCH, 1),
            full(count, PATCH),
        ]
        + [low(depth, 2, *part.shape) for part in turned]
        + [low(narrow, depth, 2, *middle.shape[1:])],
        in_specs=[in_smem()] * 5 + [in_vmem()] * 6 + [anywhere] * 4,
        out_specs=[in_vmem()] * 13 + [anywhere] * 4,
        scratch_shapes=[
            pltpu.VMEM((count, D), FULL),
            pltpu.VMEM((count + 8, 2 * HEAD_M), FULL),
            pltpu.VMEM((count + 8, 2 * STATE), FULL),
            pltpu.VMEM((HEAD_M, STATE), FULL),
            pltpu.VMEM((devices, patches, HEAD_M), LOW),
            dma,
            dma,
            dma((4,)),
            dma((3, depth, 2)),
            dma((3, depth)),
            dma((3,)),
            dma((3,)),
            dma((2, 8, depth)),
        ],
        compiler_params=pltpu.CompilerParams(
            collective_id=collective_id, has_side_effects=True, vmem_limit_bytes=48 << 20
        ),
        name="mixer_front",
    )(*scalars, start, table, w_xz, gain, conv_weight, conv_bias, *turned, middle)
    gate_all, up_all, down_all, middle_all = outs[13:]
    return (
        outs[:13],
        gate_all.reshape(wide, D, -1),
        up_all.reshape(wide, D, -1),
        down_all.reshape(-1, D),
        middle_all.reshape(D, -1),
    )


def mixer_backward(
    scalars,
    xz,
    bc,
    dt,
    marks,
    conv_weight,
    conv_bias,
    y,
    states,
    normed,
    w_xz,
    start,
    mixed_in,
    global_grad,
    gain,
    gated_scale,
    gain_grads,
    gated_gain_grads,
    du_blocks,
    down_parts,
    middle_parts,
    gate_sum,
    up_sum,
    mix_grad,
    collective_id,
):
    narrow, wide = lax.axis_size(NARROW), lax.axis_size(WIDE)
    devices = narrow * wide
    count, width = normed.shape
    patches = count // devices
    own_rows = width // devices
    dma = pltpu.SemaphoreType.DMA
    low = partial(pltpu.VMEM, dtype=LOW)
    every = width + 3 * STATE
    back_shape = (gate_sum.shape[0] // narrow, gate_sum.shape[1] * narrow)
    anywhere = pl.BlockSpec(memory_space=pl.ANY)
    return pl.pallas_call(
        partial(mixer_backward_kernel, narrow, wide),
        out_shape=[
            jax.ShapeDtypeStruct((patches, width + 128), LOW),
            jax.ShapeDtypeStruct((SUM_ROWS + CONV + 2, 128), FULL),
            jax.ShapeDtypeStruct((own_rows, 3 * STATE), FULL),
            jax.ShapeDtypeStruct((devices, own_rows, 2 * HEAD_M), LOW),
            jax.ShapeDtypeStruct(down_parts.shape[1:], LOW),
            jax.ShapeDtypeStruct(middle_parts.shape[1:], LOW),
            jax.ShapeDtypeStruct(back_shape, FULL),
            jax.ShapeDtypeStruct(back_shape, FULL),
            jax.ShapeDtypeStruct((narrow, wide // 2, 2) + mix_grad.shape, LOW),
        ],
        in_specs=[in_smem()] * 3
        + [in_vmem()] * 10
        + [anywhere]
        + [in_vmem()] * 7
        + [anywhere] * 5,
        out_specs=[in_vmem()] * 8 + [anywhere],
        scratch_shapes=[
            low((width, 3 * STATE)),
            dma,
            pltpu.VMEM((8, 2 * HEAD_M), FULL),
            pltpu.VMEM((8, 2 * STATE), FULL),
            pltpu.VMEM((8, 128), FULL),
            pltpu.VMEM((count + 8, 2 * HEAD_M), FULL),
            pltpu.VMEM((count + 8, 2 * STATE), FULL),
            pltpu.VMEM((count + 8, 2 * HEAD_M), FULL),
            pltpu.VMEM((count + 8, 2 * STATE), FULL),
            pltpu.VMEM((HEAD_M, STATE), FULL),
            low((devices, patches, HEAD_M)),
            low((count, 2 * HEAD_M)),
            low((count, 3 * STATE)),
            low((narrow, wide // 2, 2, patches, every)),
            low((narrow, wide // 2, patches, every)),
            low((narrow - 1, wide // 2, patches, every)),
            low((wide // 2, patches, every)),
            low((wide // 2 - 1, patches, every)),
            low((devices, own_rows, 2 * HEAD_M)),
            low((devices, own_rows, 2 * HEAD_M)),
            low(down_parts.shape),
            low(middle_parts.shape),
            low(back_shape),
            low(back_shape),
            dma,
            dma,
            dma,
            dma,
            dma((narrow - 1,)),
            dma((narrow - 1,)),
            dma((wide // 2 - 1,)),
            dma((wide // 2 - 1,)),
            dma,
            dma,
            dma((wide,)),
            dma((2 * narrow,)),
            dma((2, narrow - 1)),
            dma((2, narrow - 1)),
            dma((2,)),
            dma((7,)),
        ],
        compiler_params=pltpu.CompilerParams(
            collective_id=collective_id, has_side_effects=True, vmem_limit_bytes=56 << 20
        ),
        name="mixer_backward",
    )(
        *scalars,
        xz,
        bc,
        dt,
        marks,
        conv_weight,
        conv_bias,
        y,
        states,
        normed,
        w_xz,
        start,
        mixed_in,
        global_grad,
        gain,
        gated_scale,
        gain_grads,
        gated_gain_grads,
        du_blocks,
        down_parts,
        middle_parts,
        gate_sum,
        up_sum,
        mix_grad,
    )


def finish_kernel(
    pack_all,
    mix_all,
    u,
    keep,
    middle,
    xz_grads,
    bcdt_grads,
    gated_gain,
    embedded,
    start,
    table_out,
    patch_out,
    in_out,
    out_out,
    local_out,
    query_out,
    key_out,
    value_out,
    attn_out,
    embedded_own,
    ids_all,
    patch_all,
    rows_of_four,
    sems,
):
    me = lax.axis_index(NARROW) * lax.axis_size(WIDE) + lax.axis_index(WIDE)
    own_rows = patch_out.shape[0]
    group = 128 // own_rows
    columns = pl.ds(pl.multiple_of(lax.div(me, group) * 128, 128), 128)
    copies = [
        pltpu.make_async_copy(embedded.at[:, columns], embedded_own, sems.at[0]),
        pltpu.make_async_copy(start.at[:, pl.ds(3 * STATE, 128)], ids_all, sems.at[1]),
        pltpu.make_async_copy(start.at[:, pl.ds(4 * STATE, D)], patch_all, sems.at[2]),
    ]
    for copy in copies:
        copy.start()
    for i, out in enumerate((query_out, key_out, value_out, attn_out)):
        out[...] = middle[:, i * D : (i + 1) * D]
    local_out[...] = middle[:, 4 * D :].T
    for pair in range(0, HEADS_M, 2):
        both = [xz_grads[pair + i].astype(FULL) for i in range(2)]
        first = pair * HEAD_M
        in_out[:, first : first + 128] = jnp.concatenate([v[:, HEAD_M:] for v in both], axis=1)
        in_out[:, DI + first : DI + first + 128] = jnp.concatenate(
            [v[:, :HEAD_M] for v in both], axis=1
        )
    in_out[:, 2 * DI : 2 * DI + 2 * STATE] = bcdt_grads[:, : 2 * STATE]
    in_out[:, 2 * DI + 2 * STATE :] = bcdt_grads[:, 2 * STATE : 2 * STATE + HEADS_M]
    scale = pack_all[:, D:].astype(FULL)[:, :HEAD_M]
    gain = head_columns(gated_gain, me)[:, :HEAD_M]
    gated = (u[...] * scale * gain).astype(LOW)
    out_out[...] = tn(gated, mix_all[...])
    copies[0].wait()
    copies[1].wait()
    grads = pack_all[:, :D]
    rows_of_four[...] = tn(embedded_own[...], grads)
    patch_out[...] = rows_of_four[pl.ds(pl.multiple_of(lax.rem(me, group) * own_rows, own_rows), own_rows), :]
    own_words = table_out.shape[0]
    count = pack_all.shape[0]
    lane = lax.broadcasted_iota(jnp.int32, (count, PATCH * own_words), 1)
    ids = jnp.zeros((count, PATCH * own_words), FULL)
    kept = jnp.zeros((count, PATCH * own_words), FULL)
    values = ids_all[...].astype(FULL)
    for k in range(PATCH):
        here = lax.div(lane, own_words) == k
        ids = jnp.where(here, values[:, k : k + 1], ids)
        kept = jnp.where(here, keep[:, k : k + 1], kept)
    words = (me * own_words + lax.rem(lane, own_words)).astype(FULL)
    sums = tn(jnp.where(ids == words, kept, 0.0).astype(LOW), grads)
    high = sums.astype(LOW)
    rest = (sums - high.astype(FULL)).astype(LOW)
    copies[2].wait()
    table = jnp.zeros(table_out.shape, FULL)
    for k in range(PATCH):
        rows = slice(k * own_words, (k + 1) * own_words)
        weight = patch_all[k * EMB : (k + 1) * EMB, :]
        table += nt(high[rows], weight) + nt(rest[rows], weight)
    table_out[...] = table


def finish(pack_all, mix_all, u, keep, middle, xz_grads, bcdt_grads, gated_gain, embedded, start):
    count = pack_all.shape[0]
    devices, own_rows = xz_grads.shape[:2]
    anywhere = pl.BlockSpec(memory_space=pl.ANY)

    def full(*shape):
        return jax.ShapeDtypeStruct(shape, FULL)

    return pl.pallas_call(
        finish_kernel,
        out_shape=[
            full(VOCAB // devices, EMB),
            full(own_rows, D),
            full(own_rows, 2 * DI + 2 * STATE + HEADS_M),
            full(DI // devices, D),
            full(EMB, own_rows),
        ]
        + [full(own_rows, D)] * 4,
        in_specs=[in_vmem()] * 8 + [anywhere] * 2,
        out_specs=[in_vmem()] * 9,
        scratch_shapes=[
            pltpu.VMEM((count, 128), LOW),
            pltpu.VMEM((count, 128), LOW),
            pltpu.VMEM((D, D), LOW),
            pltpu.VMEM((128, D), FULL),
            pltpu.SemaphoreType.DMA((3,)),
        ],
        compiler_params=pltpu.CompilerParams(vmem_limit_bytes=40 << 20),
        name="finish",
    )(pack_all, mix_all, u, keep, middle, xz_grads, bcdt_grads, gated_gain, embedded, start)


def patch_causal():
    row = lax.broadcasted_iota(jnp.int32, (BYTE_BLOCK, BYTE_BLOCK), 0)
    column = lax.broadcasted_iota(jnp.int32, (BYTE_BLOCK, BYTE_BLOCK), 1)
    return (lax.div(row, PATCH) == lax.div(column, PATCH)) & (row >= column)


def head_probs(q, k, causal):
    scores = jnp.where(causal, nt(q, k) * HEAD_A ** (-0.5), masked_score)
    grown = jnp.exp(scores - jnp.max(scores, axis=1, keepdims=True))
    return grown / jnp.sum(grown, axis=1, keepdims=True)


def of_head(block, half):
    lane = lax.broadcasted_iota(jnp.int32, block.shape, 1)
    return jnp.where(lax.div(lane, HEAD_A) == half, block, jnp.zeros_like(block))


def fetched(pack, places, blocks, sems):
    copies = []
    for i, place in enumerate(places):
        width = place.shape[1]
        start = blocks[i]
        copies.append(
            pltpu.make_async_copy(pack.at[:, pl.ds(start, width)], place, sems.at[i])
        )
        copies[-1].start()
    return [copy.wait for copy in copies]


def unit_rows(values):
    scale = lax.rsqrt(jnp.mean(values * values, axis=1, keepdims=True) + epsilon)
    return values * scale, scale


def norm_back(grad, gain, unit, scale):
    scaled = grad * gain
    return scale * (scaled - unit * jnp.mean(scaled * unit, axis=1, keepdims=True))


WEIGHT_STEP = 256


def attend_pairs(qkv, mixed):
    causal = patch_causal()
    blocks = qkv.shape[0] // BYTE_BLOCK

    def pair(i, carry):
        def lanes(part):
            start = part * D + i * (2 * HEAD_A)
            return pl.ds(pl.multiple_of(start, 2 * HEAD_A), 2 * HEAD_A)

        for block in range(blocks):
            rows = pl.ds(block * BYTE_BLOCK, BYTE_BLOCK)
            q, k, v = qkv[rows, lanes(0)], qkv[rows, lanes(1)], qkv[rows, lanes(2)]
            total = jnp.zeros(q.shape, FULL)
            for half in range(2):
                probs = head_probs(of_head(q, half), k, causal)
                total += nn(probs.astype(LOW), of_head(v, half))
            mixed[rows, lanes(0)] = total.astype(LOW)
        return carry

    lax.fori_loop(0, HEADS_A // 2, pair, 0)


def attend_pairs_back(qkv, heads_grad, qkv_grad):
    causal = patch_causal()
    blocks = qkv.shape[0] // BYTE_BLOCK
    scale = HEAD_A ** (-0.5)

    def pair(i, carry):
        def lanes(part):
            start = part * D + i * (2 * HEAD_A)
            return pl.ds(pl.multiple_of(start, 2 * HEAD_A), 2 * HEAD_A)

        for block in range(blocks):
            rows = pl.ds(block * BYTE_BLOCK, BYTE_BLOCK)
            q, k, v = qkv[rows, lanes(0)], qkv[rows, lanes(1)], qkv[rows, lanes(2)]
            g = heads_grad[rows, lanes(0)]
            dq = jnp.zeros(q.shape, FULL)
            dk = jnp.zeros(q.shape, FULL)
            dv = jnp.zeros(q.shape, FULL)
            for half in range(2):
                own_q, own_k, own_g = of_head(q, half), of_head(k, half), of_head(g, half)
                probs = head_probs(own_q, k, causal)
                dprobs = nt(own_g, v)
                dv += tn(probs.astype(LOW), own_g)
                dscores = probs * (dprobs - jnp.sum(probs * dprobs, axis=1, keepdims=True))
                dscores = dscores.astype(LOW)
                dq += nn(dscores, own_k)
                dk += tn(dscores, own_q)
            qkv_grad[rows, lanes(0)] = (dq * scale).astype(LOW)
            qkv_grad[rows, lanes(1)] = (dk * scale).astype(LOW)
            qkv_grad[rows, lanes(2)] = dv.astype(LOW)
        return carry

    lax.fori_loop(0, HEADS_A // 2, pair, 0)


def bytes_forward_kernel(
    u_blocks,
    mixed_in,
    gains,
    gated_gain,
    pack,
    gated_out,
    local_out,
    stream_out,
    normed_out,
    qkv,
    mixed,
    after_out,
    feed_out,
    w_out0,
    w_out1,
    w_local,
    w_q,
    w_k,
    w_v,
    w_attn,
    pieces,
    sems,
):
    places = (w_out0, w_out1, w_local, w_q, w_k, w_v, w_attn)
    blocks = [4 * D, 5 * D, 6 * D, 0, D, 2 * D, 3 * D]
    waits = fetched(pack, places, blocks, sems)
    patches = mixed_in.shape[0]
    half = HEAD_M // 2
    for i in range(2):
        for first in range(0, HEADS_M, 4):
            gated_out[i, :, first * half : (first + 4) * half] = jnp.concatenate(
                [
                    u_blocks[first + j].astype(FULL)[:, i * half : (i + 1) * half]
                    for j in range(4)
                ],
                axis=1,
            )
    held = [gated_out[0], gated_out[1]]
    square = sum(jnp.sum(v * v, axis=1, keepdims=True) for v in held)
    scale = lax.rsqrt(square / (2 * D) + epsilon)
    gated = [(held[i] * scale * gated_gain[i : i + 1, :]).astype(LOW) for i in range(2)]
    waits[0]()
    waits[1]()
    joined = mixed_in[...] + nn(gated[0], w_out0[...]) + nn(gated[1], w_out1[...])
    for k in range(PATCH):
        pieces[pl.ds(k, patches, stride=PATCH), :] = joined[:, k * EMB : (k + 1) * EMB]
    local = pieces[...].astype(LOW)
    local_out[...] = local
    waits[2]()
    stream = nt(local, w_local[...])
    stream_out[...] = stream
    normed = (unit_rows(stream)[0] * gains[0:1, :]).astype(LOW)
    normed_out[...] = normed
    for i, weight in enumerate((w_q, w_k, w_v)):
        waits[3 + i]()
        for first in range(0, D, WEIGHT_STEP):
            qkv[:, i * D + first : i * D + first + WEIGHT_STEP] = nn(
                normed, weight[:, first : first + WEIGHT_STEP]
            ).astype(LOW)
    attend_pairs(qkv, mixed)
    waits[6]()
    heads = mixed[...]
    for first in range(0, D, WEIGHT_STEP):
        columns = slice(first, first + WEIGHT_STEP)
        after_out[:, columns] = stream_out[:, columns] + nn(heads, w_attn[:, columns])
    feed_out[...] = (unit_rows(after_out[...])[0] * gains[1:2, :]).astype(LOW)


def bytes_forward(u_blocks, mixed_in, gains, gated_gain, pack):
    patches = mixed_in.shape[0]
    rows = patches * PATCH

    def full(shape, kind):
        return jax.ShapeDtypeStruct(shape, kind)

    return pl.pallas_call(
        bytes_forward_kernel,
        out_shape=[
            full((2, patches, D), FULL),
            full((rows, EMB), LOW),
            full((rows, D), FULL),
            full((rows, D), LOW),
            full((rows, 3 * D), LOW),
            full((rows, D), LOW),
            full((rows, D), FULL),
            full((rows, D), LOW),
        ],
        in_specs=[in_vmem()] * 4 + [pl.BlockSpec(memory_space=pl.ANY)],
        out_specs=[in_vmem()] * 8,
        scratch_shapes=[pltpu.VMEM((D, D), LOW)] * 2
        + [pltpu.VMEM((D, EMB), LOW)]
        + [pltpu.VMEM((D, D), LOW)] * 4
        + [pltpu.VMEM((rows, EMB), FULL), pltpu.SemaphoreType.DMA((7,))],
        compiler_params=pltpu.CompilerParams(vmem_limit_bytes=48 << 20),
        name="bytes_forward",
    )(u_blocks, mixed_in, gains, gated_gain, pack)


def bytes_backward_kernel(
    narrow,
    feed_in_grad,
    cotangent,
    keep,
    after,
    stream_in,
    normed_in,
    qkv,
    mixed,
    local_in,
    gated_rows,
    gains,
    gated_gain,
    pack,
    feed_parts,
    gate_parts,
    up_parts,
    global_out,
    mix_out,
    scale_out,
    sums,
    gain_grads,
    gated_gain_grads,
    du_blocks,
    rows_out,
    gate_out,
    up_out,
    w_attn,
    w_q,
    w_k,
    w_v,
    w_local,
    w_out0,
    w_out1,
    after_grad,
    heads_grad,
    qkv_grad,
    pieces,
    parts_got,
    grads,
    grads_got,
    gate_got,
    up_got,
    sems,
    p_send,
    p_recv,
    t_send,
    t_recv,
    gate_sems,
    up_sems,
):
    n, wide_place = lax.axis_index(NARROW), lax.axis_index(WIDE)
    core = lax.rem(wide_place, 2)
    twin = (n, wide_place + 1 - 2 * core)
    depth = gate_parts.shape[0]
    z_place = lax.div(wide_place, 2)
    lines = [
        LineSum(parts, landed, line_sems, z_place, depth, lambda there: (n, there * 2 + core))
        for parts, landed, line_sems in (
            (gate_parts, gate_got, gate_sems),
            (up_parts, up_got, up_sems),
        )
    ]

    def twin_copy(i, columns):
        return remote(
            grads.at[:, 1 - core, :, columns],
            grads_got.at[:, :, columns],
            t_send.at[i],
            t_recv.at[i],
            twin,
        )

    def give(i, columns, part):
        grads[:, :, :, columns] = part.astype(LOW).reshape(grads.shape[:3] + part.shape[1:])
        twin_copy(i, columns).start()

    def part_copy(k):
        peer = (lax.rem(n + k, narrow), wide_place)
        return remote(feed_parts.at[k], parts_got.at[k], p_send.at[k - 1], p_recv.at[k - 1], peer)

    own_part = pltpu.make_async_copy(feed_parts.at[0], parts_got.at[0], sems.at[7])
    own_part.start()
    places = (w_attn, w_q, w_k, w_v, w_local, w_out0, w_out1)
    blocks = [3 * D, 0, D, 2 * D, 6 * D, 4 * D, 5 * D]
    waits = fetched(pack, places, blocks, sems)
    greet_lines(narrow, depth)
    for line in lines:
        line.start()
    for k in range(1, narrow):
        part_copy(k).start()
    patches = global_out.shape[0]
    unit, scale = unit_rows(after[...])
    grad = feed_in_grad[...].astype(LOW).astype(FULL)
    gain_grads[1:2, :] = jnp.sum(grad * unit, axis=0, keepdims=True)
    after_grad[...] = cotangent[...].astype(FULL) * keep[0] + norm_back(
        grad, gains[1:2, :], unit, scale
    )
    attn_grad = after_grad[...].astype(LOW)
    waits[0]()
    for first in range(0, D, WEIGHT_STEP):
        columns = slice(first, first + WEIGHT_STEP)
        heads_grad[:, columns] = nt(attn_grad, w_attn[columns, :]).astype(LOW)
        give(
            (3 * D + first) // WEIGHT_STEP,
            pl.ds(3 * D + first, WEIGHT_STEP),
            tn(mixed[...], attn_grad[:, columns]),
        )
    attend_pairs_back(qkv, heads_grad, qkv_grad)
    normed_grad = jnp.zeros(after_grad.shape, FULL)
    for i, weight in enumerate((w_q, w_k, w_v)):
        waits[1 + i]()
        normed_grad += nt(qkv_grad[:, i * D : (i + 1) * D], weight[...])
    unit, scale = unit_rows(stream_in[...])
    gain_grads[0:1, :] = jnp.sum(normed_grad * unit, axis=0, keepdims=True)
    stream_grad = (after_grad[...] + norm_back(normed_grad, gains[0:1, :], unit, scale)).astype(LOW)
    waits[4]()
    pieces[...] = nn(stream_grad, w_local[...])
    for k in range(PATCH):
        global_out[:, k * EMB : (k + 1) * EMB] = pieces[pl.ds(k, patches, stride=PATCH), :]
    mix_grad = global_out[...].astype(LOW)
    mix_out[...] = mix_grad
    waits[5]()
    waits[6]()
    inner = [nt(mix_grad, w_out0[...]), nt(mix_grad, w_out1[...])]
    held = [gated_rows[0], gated_rows[1]]
    square = sum(jnp.sum(v * v, axis=1, keepdims=True) for v in held)
    scale = lax.rsqrt(square / (2 * D) + epsilon)
    units = [v * scale for v in held]
    scaled = [inner[i] * gated_gain[i : i + 1, :] for i in range(2)]
    mean = sum(jnp.sum(scaled[i] * units[i], axis=1, keepdims=True) for i in range(2)) / (2 * D)
    for i in range(2):
        gated_gain_grads[i : i + 1, :] = jnp.sum(inner[i] * units[i], axis=0, keepdims=True)
    scale_out[...] = jnp.broadcast_to(scale, scale_out.shape)
    rows_grads = [scale * (scaled[i] - units[i] * mean) for i in range(2)]
    half = HEAD_M // 2
    for head in range(HEADS_M):
        lanes = slice(head * half, (head + 1) * half)
        du_blocks[head] = jnp.concatenate([part[:, lanes] for part in rows_grads], axis=1).astype(LOW)
    give(4 * D // WEIGHT_STEP, pl.ds(4 * D, EMB), tn(stream_grad, local_in[...]))

    def weight_grads(i, carry):
        columns = pl.ds(pl.multiple_of(i * WEIGHT_STEP, WEIGHT_STEP), WEIGHT_STEP)
        give(i, columns, tn(normed_in[...], qkv_grad[:, columns]))
        return carry

    lax.fori_loop(0, 3 * D // WEIGHT_STEP, weight_grads, 0)
    own_part.wait()
    for k in range(1, narrow):
        part_copy(k).wait_recv()
    for first in range(0, D, WEIGHT_STEP):
        columns = slice(first, first + WEIGHT_STEP)
        feed = parts_got[0, :, columns].astype(FULL)
        for k in range(1, narrow):
            feed += parts_got[k, :, columns].astype(FULL)
        feed = feed.astype(LOW).astype(FULL)
        rows_out[:, columns] = ((after[:, columns] + feed) * keep[0]).astype(LOW)

    def add_twin(i, columns):
        twin_copy(i, columns).wait_recv()
        sums[:, :, columns] = (
            grads[:, core, :, columns].astype(FULL) + grads_got[:, :, columns].astype(FULL)
        ).astype(LOW)

    def add_one(i, carry):
        add_twin(i, pl.ds(pl.multiple_of(i * WEIGHT_STEP, WEIGHT_STEP), WEIGHT_STEP))
        return carry

    def end_one(i, carry):
        twin_copy(i, pl.ds(pl.multiple_of(i * WEIGHT_STEP, WEIGHT_STEP), WEIGHT_STEP)).wait_send()
        return carry

    steps = 4 * D // WEIGHT_STEP
    add_twin(steps, pl.ds(4 * D, EMB))
    lax.fori_loop(0, steps, add_one, 0)
    for line, out in zip(lines, (gate_out, up_out)):
        line.arrive()
        out[...] = line.total().astype(LOW)
        line.finish()
    twin_copy(steps, pl.ds(4 * D, EMB)).wait_send()
    lax.fori_loop(0, steps, end_one, 0)
    for k in range(1, narrow):
        part_copy(k).wait_send()


def bytes_backward(
    feed_in_grad,
    cotangent,
    keep,
    after,
    stream,
    normed,
    qkv,
    mixed,
    local,
    gated_rows,
    gains,
    gated_gain,
    pack,
    feed_parts,
    gate_parts,
    up_parts,
    collective_id,
):
    narrow = feed_parts.shape[0]
    every = 4 * D + EMB
    rows = after.shape[0]
    patches = rows // PATCH

    def full(shape, kind):
        return jax.ShapeDtypeStruct(shape, kind)

    return pl.pallas_call(
        partial(bytes_backward_kernel, narrow),
        out_shape=[
            full((patches, D), FULL),
            full((patches, D), LOW),
            full((patches, 128), FULL),
            full((HEADS_M // 2, D // HEADS_M, every), LOW),
            full((2, D), FULL),
            full((2, D), FULL),
            full((HEADS_M, patches, HEAD_M), LOW),
            full((rows, D), LOW),
            full(gate_parts.shape[1:], LOW),
            full(up_parts.shape[1:], LOW),
        ],
        in_specs=[in_vmem()] * 12 + [pl.BlockSpec(memory_space=pl.ANY)] * 4,
        out_specs=[in_vmem()] * 10,
        scratch_shapes=[pltpu.VMEM((D, D), LOW)] * 4
        + [pltpu.VMEM((D, EMB), LOW)]
        + [pltpu.VMEM((D, D), LOW)] * 2
        + [
            pltpu.VMEM((rows, D), FULL),
            pltpu.VMEM((rows, D), LOW),
            pltpu.VMEM((rows, 3 * D), LOW),
            pltpu.VMEM((rows, EMB), FULL),
            pltpu.VMEM((narrow, rows, D), LOW),
            pltpu.VMEM((HEADS_M // 2, 2, D // HEADS_M, every), LOW),
            pltpu.VMEM((HEADS_M // 2, D // HEADS_M, every), LOW),
            pltpu.VMEM(gate_parts.shape, LOW),
            pltpu.VMEM(up_parts.shape, LOW),
            pltpu.SemaphoreType.DMA((8,)),
            pltpu.SemaphoreType.DMA((narrow - 1,)),
            pltpu.SemaphoreType.DMA((narrow - 1,)),
            pltpu.SemaphoreType.DMA((4 * D // WEIGHT_STEP + 1,)),
            pltpu.SemaphoreType.DMA((4 * D // WEIGHT_STEP + 1,)),
            pltpu.SemaphoreType.DMA((2 * gate_parts.shape[0],)),
            pltpu.SemaphoreType.DMA((2 * gate_parts.shape[0],)),
        ],
        compiler_params=pltpu.CompilerParams(
            collective_id=collective_id, has_side_effects=True, vmem_limit_bytes=60 << 20
        ),
        name="bytes_backward",
    )(
        feed_in_grad,
        cotangent,
        keep,
        after,
        stream,
        normed,
        qkv,
        mixed,
        local,
        gated_rows,
        gains,
        gated_gain,
        pack,
        feed_parts,
        gate_parts,
        up_parts,
    )


def feed_kernel(narrow, x_in, g_own, g_others, keep, *refs):
    gate_in, up_in, down_in, f_out, gx_out, gate_sum, up_sum, down_sum = refs[:8]
    wg, wu, wd, x, xt, g, hid, gg, gu, sent, got = refs[8:19]
    gate_twin, up_twin, down_twin, gate_got, up_got, down_got = refs[19:25]
    w_sem, g_sem, x_sem, x_send, x_recv, r_send, r_recv, t_send, t_recv = refs[25:]
    n, wide_place = lax.axis_index(NARROW), lax.axis_index(WIDE)
    core = lax.rem(wide_place, 2)
    twin = (n, wide_place + 1 - 2 * core)
    barrier = pltpu.get_barrier_semaphore()
    pl.semaphore_signal(barrier, inc=1, device_id=twin, device_id_type=MESH)
    for k in range(1, narrow):
        peer = (lax.rem(n + k, narrow), wide_place)
        pl.semaphore_signal(barrier, inc=1, device_id=peer, device_id_type=MESH)
    places, width, share = gate_in.shape
    rows = x_in.shape[0]
    hidden = places * share
    depth = places // 2
    chunk = 2 * share
    own_x = pltpu.make_async_copy(x_in, x.at[0], x_sem)
    own_x.start()
    g_copies = [
        pltpu.make_async_copy(g_own, g.at[0], g_sem.at[0]),
        pltpu.make_async_copy(g_others, g.at[pl.ds(1, narrow - 1)], g_sem.at[1]),
    ]
    w_copies = [pltpu.make_async_copy(down_in, wd, w_sem.at[2 * places])]
    for place in range(places):
        units = slice(place * share, (place + 1) * share)
        w_copies.append(pltpu.make_async_copy(gate_in.at[place], wg.at[:, units], w_sem.at[place]))
        w_copies.append(
            pltpu.make_async_copy(up_in.at[place], wu.at[:, units], w_sem.at[places + place])
        )
    g_copies[0].start()
    for copy in w_copies:
        copy.start()
    for copy in g_copies[1:]:
        copy.start()
    pl.semaphore_wait(barrier, narrow)

    def x_copy(k):
        peer = (lax.rem(n + narrow - k, narrow), wide_place)
        return remote(x_in, x.at[k], x_send.at[k - 1], x_recv.at[k - 1], peer)

    def r_copy(k):
        peer = (lax.rem(n + k, narrow), wide_place)
        return remote(sent.at[k - 1], got.at[k - 1], r_send.at[k - 1], r_recv.at[k - 1], peer)

    for k in range(1, narrow):
        x_copy(k).start()
    own_x.wait()
    for copy in w_copies:
        copy.wait()
    for copy in g_copies:
        copy.wait()

    def block(k, carry):
        @pl.when(k > 0)
        def _():
            x_copy(k).wait_recv()

        xk = x[k]
        gk = (g[k].astype(FULL) * keep[k]).astype(LOW)
        g[k] = gk
        xt[k] = xk.T
        for first in range(0, hidden, chunk):
            units = slice(first, first + chunk)
            gate = nn(xk, wg[:, units])
            up = nn(xk, wu[:, units])
            dhid = nt(gk, wd[units, :])
            s = jax.nn.sigmoid(gate)
            act = gate * s
            hid[k, :, units] = (act * up).astype(LOW)
            gg[k, :, units] = (dhid * up * s * (1.0 + gate * (1.0 - s))).astype(LOW)
            gu[k, :, units] = (dhid * act).astype(LOW)
        ggk, guk, hidk = gg[k], gu[k], hid[k]
        for first in range(0, width, chunk):
            columns = slice(first, first + chunk)
            gx = nt(ggk, wg[columns, :]) + nt(guk, wu[columns, :])

            @pl.when(k == 0)
            def _():
                gx_out[:, columns] = gx

            @pl.when(k > 0)
            def _():
                sent[k - 1, :, columns] = gx.astype(LOW)

        @pl.when(k > 0)
        def _():
            r_copy(k).start()

        for first in range(0, width, chunk):
            columns = slice(first, first + chunk)
            f_out[k, :, columns] = nn(hidk, wd[:, columns]).astype(LOW)
        return carry

    lax.fori_loop(0, narrow, block, 0)

    def units_of(j, of_core):
        start = (2 * j + of_core) * share
        return pl.ds(pl.multiple_of(start, share), share)

    def columns_grads(left, j, of_core):
        total = jnp.zeros((width, chunk), FULL)
        for k in range(narrow):
            pair = [left[k, :, units_of(2 * j + i, of_core)] for i in range(2)]
            total += nn(xt[k], jnp.concatenate(pair, axis=1))
        return total[:, :share], total[:, share:]

    def rows_grads(j, of_core):
        lhs = hid[:, :, units_of(j, of_core)].reshape(narrow * rows, share)
        return tn(lhs, g[...].reshape(narrow * rows, width))

    outs = (gate_twin, up_twin, down_twin)
    ins = (gate_got, up_got, down_got)

    def t_copy(i, j):
        return remote(outs[i].at[j], ins[i].at[j], t_send.at[i, j], t_recv.at[i, j], twin)

    def for_twin(j, carry):
        for i, left in enumerate((gg, gu)):
            for half, part in enumerate(columns_grads(left, j, 1 - core)):
                outs[i][2 * j + half] = part.astype(LOW)
                t_copy(i, 2 * j + half).start()
        for half in range(2):
            outs[2][2 * j + half] = rows_grads(2 * j + half, 1 - core).astype(LOW)
            t_copy(2, 2 * j + half).start()
        return carry

    def for_own(j, carry):
        for i, (left, total) in enumerate(((gg, gate_sum), (gu, up_sum))):
            for half, part in enumerate(columns_grads(left, j, core)):
                t_copy(i, 2 * j + half).wait_recv()
                total[2 * j + half] = (part + ins[i][2 * j + half].astype(FULL)).astype(LOW)
        for half in range(2):
            part = rows_grads(2 * j + half, core)
            t_copy(2, 2 * j + half).wait_recv()
            down_sum[2 * j + half] = (part + ins[2][2 * j + half].astype(FULL)).astype(LOW)
        return carry

    lax.fori_loop(0, depth // 2, for_twin, 0)
    lax.fori_loop(0, depth // 2, for_own, 0)
    for k in range(1, narrow):
        r_copy(k).wait_recv()
        gx_out[...] += got[k - 1].astype(FULL)
    for k in range(1, narrow):
        x_copy(k).wait_send()
        r_copy(k).wait_send()
    for i in range(3):
        for j in range(depth):
            t_copy(i, j).wait_send()


def feed_forward_back(x_own, g_own, g_others, keep, gate_all, up_all, down_all, collective_id):
    narrow = keep.shape[0]
    rows, width = x_own.shape
    places, _, share = gate_all.shape
    hidden, depth = places * share, places // 2
    dma = pltpu.SemaphoreType.DMA
    anywhere = pl.BlockSpec(memory_space=pl.ANY)

    def low(*shape):
        return pltpu.VMEM(shape, LOW)

    sums = [(depth, width, share), (depth, width, share), (depth, share, width)]
    return pl.pallas_call(
        partial(feed_kernel, narrow),
        out_shape=[
            jax.ShapeDtypeStruct((narrow, rows, width), LOW),
            jax.ShapeDtypeStruct((rows, width), FULL),
        ]
        + [jax.ShapeDtypeStruct(shape, LOW) for shape in sums],
        in_specs=[anywhere] * 3 + [in_vmem()] + [anywhere] * 3,
        out_specs=[in_vmem()] * 5,
        scratch_shapes=[
            low(width, hidden),
            low(width, hidden),
            low(hidden, width),
            low(narrow, rows, width),
            low(narrow, width, rows),
            low(narrow, rows, width),
            low(narrow, rows, hidden),
            low(narrow, rows, hidden),
            low(narrow, rows, hidden),
            low(narrow - 1, rows, width),
            low(narrow - 1, rows, width),
        ]
        + [low(*shape) for shape in sums + sums]
        + [
            dma((2 * places + 1,)),
            dma((2,)),
            dma,
            dma((narrow - 1,)),
            dma((narrow - 1,)),
            dma((narrow - 1,)),
            dma((narrow - 1,)),
            dma((3, depth)),
            dma((3, depth)),
        ],
        compiler_params=pltpu.CompilerParams(
            collective_id=collective_id, has_side_effects=True, vmem_limit_bytes=44 << 20
        ),
        name="feed",
    )(x_own, g_own, g_others, keep, gate_all, up_all, down_all)


def per_device_heads(
    byte_ids,
    doc_patches,
    pad_bytes,
    byte_table,
    patch_weight,
    gain_mix,
    in_weight,
    conv_weight,
    conv_bias,
    step_bias,
    log_rate,
    skip_gain,
    gated_gain,
    out_weight,
    local_weight,
    gain_attn,
    query_weight,
    key_weight,
    value_weight,
    attn_weight,
    feed_gain,
    gate_weight,
    up_weight,
    down_weight,
    cotangent,
):
    narrow, wide = lax.axis_size(NARROW), lax.axis_size(WIDE)
    devices = narrow * wide
    device = lax.axis_index(BOTH)
    rows = byte_ids.shape[0]
    patches = rows // PATCH
    everything = devices * patches
    own_rows = patch_weight.shape[0]
    hidden_width = gate_weight.shape[1]
    share = hidden_width // narrow

    ids_low = byte_ids.astype(LOW).reshape(patches, PATCH)
    bcdt_width = 2 * STATE + HEADS_M
    start_pack = jnp.concatenate(
        [
            jnp.pad(in_weight[:, 2 * DI :], ((0, 0), (0, 96))),
            jnp.pad(ids_low, ((0, 0), (0, 120))),
            patch_weight,
        ],
        axis=1,
    )
    xz_blocks = jnp.concatenate(
        [
            in_weight[:, DI : 2 * DI].reshape(own_rows, HEADS_M, HEAD_M),
            in_weight[:, :DI].reshape(own_rows, HEADS_M, HEAD_M),
        ],
        axis=2,
    ).transpose(1, 0, 2)
    middle_pack = jnp.concatenate(
        [
            query_weight,
            key_weight,
            value_weight,
            attn_weight,
            out_weight[:own_rows],
            out_weight[own_rows:],
            local_weight.T,
        ],
        axis=1,
    )
    start_all, table_all, xz_weight, *turned, middle_line, others = start_weights(
        start_pack,
        byte_table,
        xz_blocks,
        gate_weight,
        up_weight,
        down_weight,
        middle_pack,
        cotangent,
        0,
    )
    numbers = (step_bias, log_rate, skip_gain)
    conv = (conv_weight, conv_bias[None])
    front, gate_all, up_all, down_all, middle_all = mixer_front(
        (doc_patches, pad_bytes) + numbers,
        start_all,
        table_all,
        xz_weight,
        gain_mix[None],
        *conv,
        turned,
        middle_line,
        5,
    )
    embedded, normed_all, xz, bc, dt, u, y, states, mixed_in, u_blocks, marks, keep_rows, keep_all = front
    half = HEAD_M // 2
    gated_gain_split = gated_gain.reshape(devices, 2, half).transpose(1, 0, 2).reshape(2, D)

    byte_gains = jnp.stack([gain_attn, feed_gain])
    (
        gated_rows,
        local_rows,
        stream,
        normed_attn,
        qkv,
        mixed_heads,
        after_attn,
        normed_feed,
    ) = bytes_forward(u_blocks, mixed_in, byte_gains, gated_gain_split, middle_all)
    feed_parts, feed_in_grad, gate_parts, up_parts, down_parts = feed_forward_back(
        normed_feed, cotangent, others, keep_rows, gate_all, up_all, down_all, 2
    )

    (
        global_grad,
        mix_grad,
        gated_scale,
        middle_parts,
        byte_gain_grads,
        gated_gain_grads,
        du_blocks,
        out_rows,
        gate_sum,
        up_sum,
    ) = bytes_backward(
        feed_in_grad,
        cotangent,
        keep_rows,
        after_attn,
        stream,
        normed_attn,
        qkv,
        mixed_heads,
        local_rows,
        gated_rows,
        byte_gains,
        gated_gain_split,
        middle_all,
        feed_parts,
        gate_parts,
        up_parts,
        4,
    )
    middle_parts = middle_parts.reshape(narrow, wide // 2, own_rows, -1)

    (
        end_pack,
        sums_pack,
        bcdt_grads,
        xz_grads,
        down_sum,
        middle_sums,
        grad_gate,
        grad_up,
        mix_grad_all,
    ) = mixer_backward(
        numbers,
        xz,
        bc,
        dt,
        marks,
        *conv,
        y,
        states,
        normed_all,
        xz_weight,
        start_all,
        mixed_in,
        global_grad,
        gain_mix[None],
        gated_scale,
        byte_gain_grads,
        gated_gain_grads,
        du_blocks,
        down_parts,
        middle_parts,
        gate_sum,
        up_sum,
        mix_grad,
        3,
    )
    mix_grad_all = mix_grad_all.reshape(everything, D)

    end_all, sums_all, middle_sums, grad_down = end_gather(
        end_pack, sums_pack, middle_sums, down_sum, 1
    )
    (
        grad_table,
        grad_patch,
        grad_in,
        grad_out,
        grad_local,
        grad_query,
        grad_key,
        grad_value,
        grad_attn,
    ) = finish(
        end_all,
        mix_grad_all,
        u,
        keep_all,
        middle_sums,
        xz_grads,
        bcdt_grads,
        gated_gain[None],
        embedded,
        start_all,
    )
    small = jnp.sum(sums_all[:, :SUM_ROWS], axis=0).reshape(-1)
    gain_grads = jnp.split(small[: 3 * D + DI], [D, D + DI, 2 * D + DI])
    gain_grads[1] = gain_grads[1].reshape(2, devices, half).transpose(1, 0, 2).reshape(DI)
    conv_own = sums_all[:, SUM_ROWS : SUM_ROWS + CONV + 1, :HEAD_M].transpose(1, 0, 2)
    conv_grads = jnp.concatenate(
        [conv_own.reshape(CONV + 1, DI), small[3 * D + DI :].reshape(CONV + 1, 2 * STATE)], axis=1
    )
    number_grads = sums_all[:, SUM_ROWS + CONV + 1, :3].T
    return (
        out_rows,
        grad_table,
        grad_patch,
        gain_grads[0],
        grad_in,
        conv_grads[:CONV],
        conv_grads[CONV],
        number_grads[0],
        number_grads[1],
        number_grads[2],
        gain_grads[1],
        grad_out,
        grad_local,
        gain_grads[2],
        grad_query,
        grad_key,
        grad_value,
        grad_attn,
        gain_grads[3],
        grad_gate,
        grad_up,
        grad_down,
    )


def solution(mesh):
    placed = (
        P((NARROW, WIDE)),
        P(),
        P(),
        P((NARROW, WIDE), None),
        P((NARROW, WIDE), None),
        P(),
        P((NARROW, WIDE), None),
        P(),
        P(),
        P(),
        P(),
        P(),
        P(),
        P((NARROW, WIDE), None),
        P(None, (NARROW, WIDE)),
        P(),
        P((NARROW, WIDE), None),
        P((NARROW, WIDE), None),
        P((NARROW, WIDE), None),
        P((NARROW, WIDE), None),
        P(),
        P(NARROW, WIDE),
        P(NARROW, WIDE),
        P(WIDE, NARROW),
        P((NARROW, WIDE), None),
    )
    return jax.shard_map(
        per_device_heads if mesh.size == HEADS_M else per_device_rows,
        mesh=mesh,
        in_specs=placed,
        out_specs=(
            P((NARROW, WIDE), None),
            P((NARROW, WIDE), None),
            P((NARROW, WIDE), None),
            P(),
            P((NARROW, WIDE), None),
            P(),
            P(),
            P(),
            P(),
            P(),
            P(),
            P((NARROW, WIDE), None),
            P(None, (NARROW, WIDE)),
            P(),
            P((NARROW, WIDE), None),
            P((NARROW, WIDE), None),
            P((NARROW, WIDE), None),
            P((NARROW, WIDE), None),
            P(),
            P(NARROW, WIDE),
            P(NARROW, WIDE),
            P(WIDE, NARROW),
        ),
        check_vma=False,
    )
```

```python
from functools import partial

import jax
import jax.numpy as jnp
from jax import lax
from jax.experimental import pallas as pl
from jax.experimental.pallas import tpu as pltpu
from jax.sharding import PartitionSpec as P

NARROW = "narrow"
WIDE = "wide"
D = 1024
PATCH = 8
EMB = 128
VOCAB = 256
HEADS_M = 32
HEAD_M = 64
DI = 2048
STATE = 128
CONV = 4
HEADS_A = 16
HEAD_A = 64


epsilon = 1e-05
highest = lax.Precision.HIGHEST
masked_score = -1e30


def running_sum(x):
    place = jnp.arange(x.shape[0])
    seen = place[:, None] >= place[None, :]
    if x.ndim == 1:
        return jnp.sum(jnp.where(seen, x[None, :], 0), axis=1).astype(x.dtype)
    return jnp.dot(seen.astype(x.dtype), x, precision=highest)


def passed_along(x, axis, by):
    peers = lax.axis_size(axis)
    pairs = [(i, i + by) for i in range(peers) if 0 <= i + by < peers]
    return lax.ppermute(x, axis, pairs)


def prefix_2(x, axis, join, neutral):
    place = lax.axis_index(axis)
    gathered = jax.tree.map(
        lambda a, kind: lax.all_gather(a.astype(kind), axis), x, (jnp.bfloat16, jnp.bfloat16)
    )
    state = jax.tree.map(lambda a, e: jnp.zeros_like(a) + jnp.asarray(e, a.dtype), x, neutral)

    def prefix_one(hop, state):
        return join(
            state,
            jax.tree.map(
                lambda a, own: lax.dynamic_index_in_dim(a, hop, 0, False).astype(own.dtype),
                gathered,
                x,
            ),
        )

    return lax.fori_loop(0, place, prefix_one, state)


def carried_in_2(x, axis, join, neutral):
    count = lax.axis_size(axis)
    place = lax.axis_index(axis)
    ahead = count - 1 - place
    gathered = jax.tree.map(
        lambda a, kind: lax.all_gather(a.astype(kind), axis),
        x,
        jax.tree.map(lambda a: jnp.bfloat16 if a.dtype == jnp.float32 else a.dtype, x),
    )
    state = jax.tree.map(lambda a, e: jnp.zeros_like(a) + jnp.asarray(e, a.dtype), x, neutral)

    def carried_one(hop, state):
        source = count - 1 - hop
        return join(
            state,
            jax.tree.map(
                lambda a, own: lax.dynamic_index_in_dim(a, source, 0, False).astype(own.dtype),
                gathered,
                x,
            ),
        )

    return lax.fori_loop(0, ahead, carried_one, state)


def root_norm(values, gain):
    return values * lax.rsqrt(jnp.mean(values * values, axis=-1, keepdims=True) + epsilon) * gain


def patch_layout(doc_patches, pad_bytes, first_index, patch_count):
    patch_index = first_index + jnp.arange(patch_count, dtype=jnp.int32)
    doc_ends = running_sum(doc_patches)
    doc_index = jnp.arange(doc_patches.shape[0], dtype=jnp.int32)
    segment = jnp.sum((patch_index[:, None] >= doc_ends[None, :]).astype(jnp.int32), axis=1)
    owner_mask = segment[:, None] == doc_index[None, :]
    last_end = jnp.sum(jnp.where(owner_mask, doc_ends[None, :] - 1, 0), axis=1)
    doc_starts = jnp.sum(jnp.where(owner_mask, (doc_ends - doc_patches)[None, :], 0), axis=1)
    pad_count = jnp.sum(jnp.where(owner_mask, pad_bytes[None, :], 0), axis=1)
    offset = jnp.arange(PATCH, dtype=jnp.int32)
    padded = (patch_index == last_end)[:, None] & (offset[None, :] >= PATCH - pad_count[:, None])
    keep_mask = 1.0 - padded.astype(jnp.float32).reshape(-1)
    return (segment, (patch_index == doc_starts).astype(jnp.int32), keep_mask)


def ssd_terms(layout, projected, rim_rows, small_params):
    conv_weight, conv_bias, step_bias, log_rate, skip_gain = small_params
    segment, rim_segment, first_patch = layout
    conv_in = projected[:, DI : 2 * DI + 2 * STATE]
    patch_count = conv_in.shape[0]
    padded = jnp.concatenate([rim_rows, conv_in], 0)
    padded_seg = jnp.concatenate([rim_segment, segment], 0)
    conv_sum = conv_bias
    for conv_tap in range(CONV):
        same_doc = (padded_seg[conv_tap : conv_tap + patch_count] == segment).astype(jnp.float32)[
            :, None
        ]
        conv_sum = (
            conv_sum + conv_weight[conv_tap] * padded[conv_tap : conv_tap + patch_count] * same_doc
        )
    activated = jax.nn.silu(conv_sum)
    values = activated[:, :DI].reshape(patch_count, HEADS_M, HEAD_M)
    input_map = activated[:, DI : DI + STATE]
    output_map = activated[:, DI + STATE :]
    time_steps = jax.nn.softplus(projected[:, 2 * DI + 2 * STATE :] + step_bias)
    cumulative = running_sum(-time_steps * jnp.exp(log_rate))
    no_reset = (running_sum(first_patch) == 0).astype(jnp.float32)
    return (values, input_map, output_map, time_steps, cumulative, no_reset)


def local_state(layout, projected, rim_rows, small_params):
    values, input_map, output_map, time_steps, cumulative, no_reset = ssd_terms(
        layout, projected, rim_rows, small_params
    )
    segment = layout[0]
    decay_tail = (
        jnp.exp(cumulative[-1][None, :] - cumulative)
        * (segment == segment[-1]).astype(jnp.float32)[:, None]
        * time_steps
    )
    state_local = jnp.einsum("sh,shp,sn->hpn", decay_tail, values, input_map, precision=highest)
    decay_total = jnp.exp(cumulative[-1]) * no_reset[-1]
    return (decay_total, state_local)


def mixer_output(layout, projected, rim_rows, small_params, incoming, gated_gain):
    values, input_map, output_map, time_steps, cumulative, no_reset = ssd_terms(
        layout, projected, rim_rows, small_params
    )
    segment = layout[0]
    patch_count = values.shape[0]
    position = jnp.arange(patch_count)
    visible = (segment[:, None] == segment[None, :]) & (position[:, None] >= position[None, :])
    log_gap = jnp.where(visible[:, :, None], cumulative[:, None, :] - cumulative[None, :, :], 0.0)
    inner = jnp.dot(output_map, input_map.T, precision=highest)
    weight = (
        jnp.exp(log_gap)
        * visible[:, :, None].astype(jnp.float32)
        * time_steps[None, :, :]
        * inner[:, :, None]
    )
    within = jnp.einsum("tsh,shp->thp", weight, values, precision=highest)
    carried_in = (
        jnp.einsum("tn,hpn->thp", output_map, incoming, precision=highest)
        * (jnp.exp(cumulative) * no_reset[:, None])[:, :, None]
    )
    result = (within + carried_in + small_params[4][None, :, None] * values).reshape(
        patch_count, DI
    )
    gated_rows = result * jax.nn.silu(projected[:, :DI])
    return root_norm(gated_rows, gated_gain)


def combine_states(earlier, following):
    return (earlier[0] * following[0], following[0][:, None, None] * earlier[1] + following[1])


def attend(stream, gain_attn, query_all, key_all, value_all):
    head_shape = (-1, PATCH, HEADS_A, HEAD_A)
    normed_attn = root_norm(stream, gain_attn).astype(jnp.bfloat16)
    queries = jnp.dot(normed_attn, query_all, preferred_element_type=jnp.float32).astype(
        jnp.bfloat16
    )
    key_rows = jnp.dot(normed_attn, key_all, preferred_element_type=jnp.float32).astype(
        jnp.bfloat16
    )
    value_rows = jnp.dot(normed_attn, value_all, preferred_element_type=jnp.float32).astype(
        jnp.bfloat16
    )
    scores = jnp.einsum(
        "pqhe,pkhe->phqk",
        queries.reshape(head_shape),
        key_rows.reshape(head_shape),
        preferred_element_type=jnp.float32,
    ) * HEAD_A ** (-0.5)
    position = jnp.arange(PATCH)
    causal = position[:, None] >= position[None, :]
    attn_probs = jax.nn.softmax(jnp.where(causal, scores, masked_score), axis=-1)
    mixed_heads = jnp.einsum(
        "phqk,pkhe->pqhe",
        attn_probs.astype(jnp.bfloat16),
        value_rows.reshape(head_shape),
        preferred_element_type=jnp.float32,
    )
    mixed_heads = mixed_heads.reshape(stream.shape[0], -1).astype(jnp.bfloat16)
    return (normed_attn, queries, key_rows, value_rows, attn_probs, mixed_heads)


def spread(values):
    by_rows = lax.all_to_all(values, NARROW, split_axis=1, concat_axis=0, tiled=True)
    return lax.all_gather(by_rows, WIDE, axis=0, tiled=True)


def collect(term_fn, row_count):
    summed = lax.psum_scatter(
        term_fn(jnp.int32(0), row_count * lax.axis_size(WIDE)).astype(jnp.bfloat16),
        WIDE,
        scatter_dimension=0,
        tiled=True,
    )
    return lax.all_to_all(summed, NARROW, split_axis=0, concat_axis=1, tiled=True)


def narrow_total(partial_rows):
    return lax.psum(partial_rows, NARROW).astype(jnp.float32)


def silu_back(gate_up, hidden_grad, hidden_width):
    gate_rows = gate_up[:, :hidden_width]
    up_rows = gate_up[:, hidden_width:]
    sigmoid = jax.nn.sigmoid(gate_rows)
    gate_grad = hidden_grad * up_rows * sigmoid * (1.0 + gate_rows * (1.0 - sigmoid))
    up_grad = hidden_grad * gate_rows * sigmoid
    return jnp.concatenate([gate_grad, up_grad], axis=1)


def per_device_rows(
    byte_ids,
    doc_patches,
    pad_bytes,
    byte_table,
    patch_weight,
    gain_mix,
    in_weight,
    conv_weight,
    conv_bias,
    step_bias,
    log_rate,
    skip_gain,
    gated_gain,
    out_weight,
    local_weight,
    gain_attn,
    query_weight,
    key_weight,
    value_weight,
    attn_weight,
    feed_gain,
    gate_weight,
    up_weight,
    down_weight,
    cotangent,
):
    byte_rows = byte_ids.shape[0]
    patches = byte_rows // PATCH
    device = lax.axis_index((NARROW, WIDE))
    wide_count = lax.axis_size(WIDE)
    segment, first_patch, keep_mask = patch_layout(
        doc_patches, pad_bytes, device * patches, patches
    )
    rim_segment = patch_layout(doc_patches, pad_bytes, device * patches - (CONV - 1), CONV - 1)[0]
    layout = (segment, rim_segment, first_patch)
    gathered = (
        lax.all_gather(byte_table, (NARROW, WIDE), axis=0, tiled=True),
        lax.all_gather(patch_weight, (NARROW, WIDE), axis=0, tiled=True),
        lax.all_gather(in_weight, (NARROW, WIDE), axis=0, tiled=True),
        lax.all_gather(out_weight, (NARROW, WIDE), axis=0, tiled=True),
        lax.all_gather(local_weight, (NARROW, WIDE), axis=1, tiled=True),
        lax.all_gather(query_weight, (NARROW, WIDE), axis=0, tiled=True),
        lax.all_gather(key_weight, (NARROW, WIDE), axis=0, tiled=True),
        lax.all_gather(value_weight, (NARROW, WIDE), axis=0, tiled=True),
        lax.all_gather(attn_weight, (NARROW, WIDE), axis=0, tiled=True),
    )
    table_all, patch_all, in_all, out_all, local_all, query_all, key_all, value_all, attn_all = (
        gathered
    )
    onehot = (byte_ids[:, None] == jnp.arange(VOCAB, dtype=jnp.int32)[None, :]).astype(jnp.bfloat16)
    embedded = (
        (jnp.dot(onehot, table_all, preferred_element_type=jnp.float32) * keep_mask[:, None])
        .astype(jnp.bfloat16)
        .reshape(patches, D)
    )
    mixed_in = jnp.dot(embedded, patch_all, preferred_element_type=jnp.float32)
    normed_mix = root_norm(mixed_in, gain_mix).astype(jnp.bfloat16)
    projected = jnp.dot(normed_mix, in_all, preferred_element_type=jnp.float32).astype(jnp.bfloat16)
    rim_rows = passed_along(
        projected[patches - (CONV - 1) :, DI : 2 * DI + 2 * STATE], (NARROW, WIDE), 1
    ).astype(jnp.float32)
    projected_f = projected.astype(jnp.float32)
    small_params = (conv_weight, conv_bias, step_bias, log_rate, skip_gain)
    (decay_total, state_local), state_back = jax.vjp(
        partial(local_state, layout), projected_f, rim_rows, small_params
    )
    prefix = prefix_2(
        (decay_total, state_local),
        (NARROW, WIDE),
        combine_states,
        (jnp.ones_like(decay_total), jnp.zeros_like(state_local)),
    )
    incoming = prefix[1]
    gated_norm, mixer_back = jax.vjp(
        partial(mixer_output, layout), projected_f, rim_rows, small_params, incoming, gated_gain
    )
    gated_low = gated_norm.astype(jnp.bfloat16)
    global_out = mixed_in + jnp.dot(gated_low, out_all, preferred_element_type=jnp.float32)
    local_rows = global_out.astype(jnp.bfloat16).reshape(byte_rows, EMB)
    stream = jnp.dot(local_rows, local_all, preferred_element_type=jnp.float32)
    normed_attn, queries, key_rows, value_rows, attn_probs, mixed_heads = attend(
        stream, gain_attn, query_all, key_all, value_all
    )
    after_attn = stream + jnp.dot(mixed_heads, attn_all, preferred_element_type=jnp.float32)
    normed_feed = root_norm(after_attn, feed_gain).astype(jnp.bfloat16)
    out_grad = cotangent.astype(jnp.float32) * keep_mask[:, None]
    feed_grad = out_grad.astype(jnp.bfloat16)
    grid_in = spread(normed_feed)
    both_weights = jnp.concatenate([gate_weight, up_weight], axis=1)
    hidden_width = gate_weight.shape[1]
    grid_share = grid_in.shape[0] // wide_count
    gate_up_part = jnp.dot(grid_in, both_weights, preferred_element_type=jnp.float32).astype(
        jnp.bfloat16
    )
    gate_up = narrow_total(gate_up_part)
    hidden = (jax.nn.silu(gate_up[:, :hidden_width]) * gate_up[:, hidden_width:]).astype(
        jnp.bfloat16
    )

    def down_term(first_row, row_count):
        return jnp.dot(hidden, down_weight, preferred_element_type=jnp.float32)

    feed_out = collect(down_term, grid_share)
    grid_grad = spread(feed_grad)
    grad_down = jnp.einsum("gf,gd->fd", hidden, grid_grad, preferred_element_type=jnp.float32)
    hidden_part = jnp.einsum(
        "gd,fd->gf", grid_grad, down_weight, preferred_element_type=jnp.float32
    ).astype(jnp.bfloat16)
    hidden_grad = narrow_total(hidden_part)
    gate_up_grad = silu_back(gate_up, hidden_grad, hidden_width).astype(jnp.bfloat16)
    grad_both = jnp.einsum("gd,gf->df", grid_in, gate_up_grad, preferred_element_type=jnp.float32)

    def back_term(first_row, row_count):
        return jnp.einsum(
            "gf,df->gd", gate_up_grad, both_weights, preferred_element_type=jnp.float32
        )

    feed_in_grad = collect(back_term, grid_share)
    grad_gate = grad_both[:, :hidden_width]
    grad_up = grad_both[:, hidden_width:]
    after_feed = after_attn + feed_out.astype(jnp.float32)
    out_rows = (after_feed * keep_mask[:, None]).astype(jnp.bfloat16)
    feed_normed, feed_norm_back = jax.vjp(root_norm, after_attn, feed_gain)
    after_norm_grad, grad_feed_gain = feed_norm_back(feed_in_grad.astype(jnp.float32))
    after_grad = out_grad + after_norm_grad
    head_shape = (-1, PATCH, HEADS_A, HEAD_A)
    score_scale = HEAD_A ** (-0.5)
    attn_grad = after_grad.astype(jnp.bfloat16)
    grad_attn = jnp.einsum("rd,re->de", mixed_heads, attn_grad, preferred_element_type=jnp.float32)
    heads_grad = (
        jnp.einsum("re,de->rd", attn_grad, attn_all, preferred_element_type=jnp.float32)
        .astype(jnp.bfloat16)
        .reshape(head_shape)
    )
    probs_grad = jnp.einsum(
        "pqhe,pkhe->phqk",
        heads_grad,
        value_rows.reshape(head_shape),
        preferred_element_type=jnp.float32,
    )
    value_grad = (
        jnp.einsum(
            "phqk,pqhe->pkhe",
            attn_probs.astype(jnp.bfloat16),
            heads_grad,
            preferred_element_type=jnp.float32,
        )
        .reshape(byte_rows, D)
        .astype(jnp.bfloat16)
    )
    score_grad = (
        attn_probs * (probs_grad - jnp.sum(attn_probs * probs_grad, axis=-1, keepdims=True))
    ).astype(jnp.bfloat16)
    query_grad = (
        (
            jnp.einsum(
                "phqk,pkhe->pqhe",
                score_grad,
                key_rows.reshape(head_shape),
                preferred_element_type=jnp.float32,
            )
            * score_scale
        )
        .reshape(byte_rows, D)
        .astype(jnp.bfloat16)
    )
    key_grad = (
        (
            jnp.einsum(
                "phqk,pqhe->pkhe",
                score_grad,
                queries.reshape(head_shape),
                preferred_element_type=jnp.float32,
            )
            * score_scale
        )
        .reshape(byte_rows, D)
        .astype(jnp.bfloat16)
    )
    grad_query = jnp.einsum(
        "rd,re->de", normed_attn, query_grad, preferred_element_type=jnp.float32
    )
    grad_key = jnp.einsum("rd,re->de", normed_attn, key_grad, preferred_element_type=jnp.float32)
    grad_value = jnp.einsum(
        "rd,re->de", normed_attn, value_grad, preferred_element_type=jnp.float32
    )
    normed_grad = jnp.einsum("re,de->rd", query_grad, query_all, preferred_element_type=jnp.float32)
    normed_grad = normed_grad + jnp.einsum(
        "re,de->rd", key_grad, key_all, preferred_element_type=jnp.float32
    )
    normed_grad = normed_grad + jnp.einsum(
        "re,de->rd", value_grad, value_all, preferred_element_type=jnp.float32
    )
    attn_normed, attn_norm_back = jax.vjp(root_norm, stream, gain_attn)
    stream_norm_grad, grad_gain_attn = attn_norm_back(normed_grad)
    stream_grad = (after_grad + stream_norm_grad).astype(jnp.bfloat16)
    grad_local = jnp.einsum(
        "re,rd->ed", local_rows, stream_grad, preferred_element_type=jnp.float32
    )
    global_grad = jnp.einsum(
        "rd,ed->re", stream_grad, local_all, preferred_element_type=jnp.float32
    ).reshape(patches, D)
    mix_grad = global_grad.astype(jnp.bfloat16)
    grad_out = jnp.einsum("pi,pd->id", gated_low, mix_grad, preferred_element_type=jnp.float32)
    gated_grad = jnp.einsum("pd,id->pi", mix_grad, out_all, preferred_element_type=jnp.float32)
    proj_grad_mix, rim_grad_mix, small_grad_mix, incoming_grad, grad_gated_gain = mixer_back(
        gated_grad
    )
    suffix = carried_in_2(
        (decay_total, incoming_grad),
        (NARROW, WIDE),
        combine_states,
        (jnp.ones_like(decay_total), jnp.zeros_like(incoming_grad)),
    )
    later_grad = suffix[1]
    decay_grad = jnp.sum(later_grad * incoming, axis=(1, 2))
    proj_grad_state, rim_grad_state, small_grad_state = state_back((decay_grad, later_grad))
    rim_from_next = passed_along(rim_grad_mix + rim_grad_state, (NARROW, WIDE), -1)
    proj_grad = proj_grad_mix + proj_grad_state
    proj_grad = proj_grad.at[patches - (CONV - 1) :, DI : 2 * DI + 2 * STATE].add(rim_from_next)
    proj_low = proj_grad.astype(jnp.bfloat16)
    grad_in = jnp.einsum("pd,pk->dk", normed_mix, proj_low, preferred_element_type=jnp.float32)
    normed_mix_grad = jnp.einsum("pk,dk->pd", proj_low, in_all, preferred_element_type=jnp.float32)
    mix_normed, mix_norm_back = jax.vjp(root_norm, mixed_in, gain_mix)
    mixed_norm_grad, grad_gain_mix = mix_norm_back(normed_mix_grad)
    embed_grad = (global_grad + mixed_norm_grad).astype(jnp.bfloat16)
    grad_patch = jnp.einsum("pi,pd->id", embedded, embed_grad, preferred_element_type=jnp.float32)
    byte_grad = (
        jnp.einsum("pd,id->pi", embed_grad, patch_all, preferred_element_type=jnp.float32).reshape(
            byte_rows, EMB
        )
        * keep_mask[:, None]
    )
    grad_table = jnp.dot(onehot.astype(jnp.float32).T, byte_grad, precision=highest)
    shared = (
        lax.psum_scatter(grad_table, (NARROW, WIDE), scatter_dimension=0, tiled=True),
        lax.psum_scatter(grad_patch, (NARROW, WIDE), scatter_dimension=0, tiled=True),
        lax.psum_scatter(grad_in, (NARROW, WIDE), scatter_dimension=0, tiled=True),
        lax.psum_scatter(grad_out, (NARROW, WIDE), scatter_dimension=0, tiled=True),
        lax.psum_scatter(grad_local, (NARROW, WIDE), scatter_dimension=1, tiled=True),
        lax.psum_scatter(grad_query, (NARROW, WIDE), scatter_dimension=0, tiled=True),
        lax.psum_scatter(grad_key, (NARROW, WIDE), scatter_dimension=0, tiled=True),
        lax.psum_scatter(grad_value, (NARROW, WIDE), scatter_dimension=0, tiled=True),
        lax.psum_scatter(grad_attn, (NARROW, WIDE), scatter_dimension=0, tiled=True),
    )
    small_sum = lax.psum(
        (
            small_grad_mix[0] + small_grad_state[0],
            small_grad_mix[1] + small_grad_state[1],
            small_grad_mix[2] + small_grad_state[2],
            small_grad_mix[3] + small_grad_state[3],
            small_grad_mix[4] + small_grad_state[4],
            grad_gain_mix,
            grad_gated_gain,
            grad_gain_attn,
            grad_feed_gain,
        ),
        (NARROW, WIDE),
    )
    return (
        out_rows,
        shared[0],
        shared[1],
        small_sum[5],
        shared[2],
        small_sum[0],
        small_sum[1],
        small_sum[2],
        small_sum[3],
        small_sum[4],
        small_sum[6],
        shared[3],
        shared[4],
        small_sum[7],
        shared[5],
        shared[6],
        shared[7],
        shared[8],
        small_sum[8],
        grad_gate,
        grad_up,
        grad_down,
    )


QUERY = 128
BYTE_BLOCK = 128
MESH = pl.DeviceIdType.MESH
SUM_ROWS = (3 * D + DI + (CONV + 1) * 2 * STATE) // 128
LOW = jnp.bfloat16
FULL = jnp.float32
BOTH = (NARROW, WIDE)


def nn(a, b, precision=None):
    return lax.dot_general(
        a, b, (((1,), (0,)), ((), ())), precision=precision, preferred_element_type=FULL
    )


def nt(a, b, precision=None):
    return lax.dot_general(
        a, b, (((1,), (1,)), ((), ())), precision=precision, preferred_element_type=FULL
    )


def tn(a, b, precision=None):
    return lax.dot_general(
        a, b, (((0,), (0,)), ((), ())), precision=precision, preferred_element_type=FULL
    )


def device_at(place, wide):
    return (lax.div(place, wide), lax.rem(place, wide))


def remote(src, dst, send, recv, peer):
    return pltpu.make_async_remote_copy(
        src_ref=src, dst_ref=dst, send_sem=send, recv_sem=recv, device_id=peer, device_id_type=MESH
    )


def greet_all(devices, wide):
    me = lax.axis_index(NARROW) * wide + lax.axis_index(WIDE)
    barrier = pltpu.get_barrier_semaphore()

    def greet(k, carry):
        peer = device_at(lax.rem(me + k, devices), wide)
        pl.semaphore_signal(barrier, inc=1, device_id=peer, device_id_type=MESH)
        return carry

    lax.fori_loop(1, devices, greet, 0)
    return me, lambda: pl.semaphore_wait(barrier, devices - 1)


def send_blocks(me, devices, wide, src, dst, send, recv):
    def one(k, carry):
        place = lax.rem(me + k, devices)
        remote(src.at[place], dst.at[me], send, recv, device_at(place, wide)).start()
        return carry

    lax.fori_loop(1, devices, one, 0)


def wait_blocks(me, devices, wide, dst, send, recv):
    part = dst.at[pl.ds(0, devices - 1)]
    remote(part, part, send, recv, device_at(me, wide)).wait()


class StagedGather:
    def __init__(self, block, out, sems, narrow, depth):
        n, w = lax.axis_index(NARROW), lax.axis_index(WIDE)
        z, c = lax.div(w, 2), lax.rem(w, 2)
        self.out, self.narrow, self.depth = out, narrow, depth
        self.n, self.c = n, c
        self.sems = [sems.at[i] for i in range(7)]
        self.twin = (n, z * 2 + 1 - c)
        self.n_peers = [lax.rem(n + k, narrow) for k in range(1, narrow)]
        self.w = w
        self.own = pltpu.make_async_copy(block, out.at[n, z, c], self.sems[0])
        self.first = [
            remote(
                block,
                out.at[n, z, c],
                self.sems[1],
                self.sems[2],
                (n, lax.rem(z + k, depth) * 2 + c),
            )
            for k in range(1, depth)
        ]

    def wait_for(self, part, i):
        return remote(part, part, self.sems[i], self.sems[i + 1], self.twin)

    def z_part(self):
        return self.wait_for(self.out.at[self.n, pl.ds(0, self.depth - 1), self.c], 1)

    def n_part(self):
        return self.wait_for(self.out.at[pl.ds(0, self.narrow - 1), :, self.c], 3)

    def start(self):
        self.own.start()
        for copy in self.first:
            copy.start()

    def spread(self):
        self.own.wait()
        self.z_part().wait_recv()
        mine = self.out.at[self.n, :, self.c]
        for m in self.n_peers:
            remote(mine, mine, self.sems[3], self.sems[4], (m, self.w)).start()
        self.wait_for(mine, 5).start()

    def cross(self):
        self.n_part().wait_recv()
        for m in self.n_peers:
            self.wait_for(self.out.at[m, :, self.c], 5).start()

    def finish(self):
        self.wait_for(self.out.at[:, :, 1 - self.c], 5).wait()
        self.z_part().wait_send()
        self.n_part().wait_send()


def greet_lines(narrow, depth):
    n, w = lax.axis_index(NARROW), lax.axis_index(WIDE)
    z, c = lax.div(w, 2), lax.rem(w, 2)
    peers = [(n, lax.rem(z + k, depth) * 2 + c) for k in range(1, depth)]
    peers += [(lax.rem(n + k, narrow), w) for k in range(1, narrow)]
    peers += [(n, z * 2 + 1 - c)]
    barrier = pltpu.get_barrier_semaphore()
    for peer in peers:
        pl.semaphore_signal(barrier, inc=1, device_id=peer, device_id_type=MESH)
    pl.semaphore_wait(barrier, len(peers))


class LineSum:
    def __init__(self, parts, got, sems, place, length, peer_of):
        self.got, self.length = got, length
        self.own = pltpu.make_async_copy(parts.at[place], got.at[0], sems.at[0])
        self.copies = []
        for k in range(1, length):
            there = lax.rem(place + k, length)
            self.copies.append(
                remote(
                    parts.at[there], got.at[k], sems.at[2 * k - 1], sems.at[2 * k], peer_of(there)
                )
            )

    def start(self):
        self.own.start()
        for copy in self.copies:
            copy.start()

    def arrive(self):
        self.own.wait()
        for copy in self.copies:
            copy.wait_recv()

    def total(self, *index):
        summed = self.got[(0,) + index].astype(FULL)
        for k in range(1, self.length):
            summed += self.got[(k,) + index].astype(FULL)
        return summed

    def finish(self):
        for copy in self.copies:
            copy.wait_send()


def square_of(n, narrow):
    return n + 1 - 2 * lax.rem(n, 2), n + 2 - 4 * lax.div(n, 2), narrow - 1 - n


class SquareSum:
    def __init__(self, parts, own, held, got, sems, n, w, narrow):
        beside, across, corner = square_of(n, narrow)
        self.own, self.held, self.got = own, held, got
        self.half = half = parts.shape[1] // 2
        low, high = pl.ds(0, half), pl.ds(half, half)
        self.local = [
            pltpu.make_async_copy(parts.at[n], own, sems.at[0, 6]),
            pltpu.make_async_copy(parts.at[across, low], held.at[0], sems.at[0, 7]),
            pltpu.make_async_copy(parts.at[beside, high], held.at[1], sems.at[1, 6]),
        ]

        def send(i, src, peer):
            return remote(src, got.at[i], sems.at[0, i], sems.at[1, i], (peer, w))

        self.copies = [
            send(0, parts.at[corner, low], beside),
            send(1, parts.at[corner, high], across),
            send(2, parts.at[beside, low], beside),
            send(3, parts.at[across, high], across),
            send(4, held.at[1], beside),
            send(5, held.at[0], across),
        ]

    def start(self):
        for copy in self.local + self.copies[:4]:
            copy.start()

    def relay(self):
        for i in range(2):
            self.local[1 + i].wait()
            self.copies[i].wait_recv()
            for j in range(self.half):
                self.held[i, j] = (
                    self.held[i, j].astype(FULL) + self.got[i, j].astype(FULL)
                ).astype(LOW)
            self.copies[5 - i].start()

    def arrive(self):
        self.local[0].wait()
        for copy in self.copies[2:]:
            copy.wait_recv()

    def total(self, j):
        first, second = (2, 5) if j < self.half else (4, 3)
        summed = self.own[j].astype(FULL)
        for i in (first, second):
            summed += self.got[i, j % self.half].astype(FULL)
        return summed

    def finish(self):
        for copy in self.copies:
            copy.wait_send()


def start_kernel(
    narrow,
    wide,
    pack,
    table,
    xz_blocks,
    gate,
    up,
    down,
    middle,
    cotangent,
    pack_all,
    table_all,
    xz_all,
    gate_turned,
    up_turned,
    down_turned,
    middle_line,
    others,
    pack_sems,
    table_sems,
    xz_sems,
    turn_send,
    turn_recv,
    own_sems,
    line_send,
    line_recv,
    other_send,
    other_recv,
):
    devices, depth = narrow * wide, wide // 2
    me, arrived = greet_all(devices, wide)
    n, w = lax.axis_index(NARROW), lax.axis_index(WIDE)
    z, c = lax.div(w, 2), lax.rem(w, 2)
    twin = (n, z * 2 + 1 - c)
    rows, units = gate.shape[0], gate.shape[1] // narrow
    columns = down.shape[1]
    gathers = [
        StagedGather(pack, pack_all, pack_sems, narrow, depth),
        StagedGather(table, table_all, table_sems, narrow, depth),
    ]

    def pieces(m):
        mine = pl.ds(m * units, units)
        return (gate.at[:, mine], up.at[:, mine], down.at[mine, :])

    landing = (
        gate_turned.at[pl.ds(n * rows, rows), :],
        up_turned.at[pl.ds(n * rows, rows), :],
        down_turned.at[:, pl.ds(n * columns, columns)],
    )
    turns = []
    for k in range(1, narrow):
        m = lax.rem(n + k, narrow)
        for i, piece in enumerate(pieces(m)):
            turns.append(
                remote(piece, landing[i], turn_send.at[k - 1, i], turn_recv.at[k - 1, i], (m, w))
            )
    own = [
        pltpu.make_async_copy(piece, landing[i], own_sems.at[i])
        for i, piece in enumerate(pieces(n))
    ]
    own.append(pltpu.make_async_copy(xz_blocks.at[me], xz_all.at[me], own_sems.at[3]))
    own.append(pltpu.make_async_copy(middle, middle_line.at[z], own_sems.at[4]))
    lines = [
        remote(middle, middle_line.at[z], line_send, line_recv, (n, lax.rem(z + k, depth) * 2 + c))
        for k in range(1, depth)
    ]
    for k in range(1, narrow):
        peer = (lax.rem(n + narrow - k, narrow), w)
        turns.append(
            remote(cotangent, others.at[k - 1], other_send.at[k - 1], other_recv.at[k - 1], peer)
        )
    arrived()
    for gather in gathers:
        gather.start()
    for copy in turns + own:
        copy.start()
    send_blocks(me, devices, wide, xz_blocks, xz_all, xz_sems.at[0], xz_sems.at[1])
    for copy in lines:
        copy.start()
    for gather in gathers:
        gather.spread()
    for gather in gathers:
        gather.cross()
    for copy in own:
        copy.wait()
    for copy in turns:
        copy.wait()
    for gather in gathers:
        gather.finish()
    wait_blocks(me, devices, wide, xz_all, xz_sems.at[0], xz_sems.at[1])
    part = middle_line.at[pl.ds(0, depth - 1)]
    remote(part, part, line_send, line_recv, twin).wait()


def start_weights(pack, table, xz_blocks, gate, up, down, middle, cotangent, collective_id):
    narrow, wide = lax.axis_size(NARROW), lax.axis_size(WIDE)
    depth = wide // 2
    units = gate.shape[1] // narrow
    dma = pltpu.SemaphoreType.DMA
    anywhere = pl.BlockSpec(memory_space=pl.ANY)

    def low(*shape):
        return jax.ShapeDtypeStruct(shape, LOW)

    outs = pl.pallas_call(
        partial(start_kernel, narrow, wide),
        out_shape=[
            low(narrow, depth, 2, *pack.shape),
            low(narrow, depth, 2, *table.shape),
            low(*xz_blocks.shape),
            low(D, units),
            low(D, units),
            low(units, D),
            low(depth, *middle.shape),
            low(narrow - 1, *cotangent.shape),
        ],
        in_specs=[anywhere] * 8,
        out_specs=[anywhere] * 8,
        scratch_shapes=[
            dma((7,)),
            dma((7,)),
            dma((2,)),
            dma((narrow - 1, 3)),
            dma((narrow - 1, 3)),
            dma((5,)),
            dma,
            dma,
            dma((narrow - 1,)),
            dma((narrow - 1,)),
        ],
        compiler_params=pltpu.CompilerParams(collective_id=collective_id, has_side_effects=True),
        name="start_weights",
    )(pack, table, xz_blocks, gate, up, down, middle, cotangent)
    return (
        outs[0].reshape(-1, pack.shape[1]),
        outs[1].reshape(-1, table.shape[1]),
        outs[2].reshape(D, -1),
    ) + tuple(outs[3:])


def end_kernel(
    narrow,
    depth,
    pack,
    sums,
    middle,
    up_sum,
    down_sum,
    pack_all,
    sums_all,
    middle_out,
    up_out,
    down_out,
    middle_got,
    up_got,
    down_got,
    pack_sems,
    sums_sems,
    middle_sems,
    back_send,
    back_recv,
    back_own,
):
    n, w = lax.axis_index(NARROW), lax.axis_index(WIDE)
    z, c = lax.div(w, 2), lax.rem(w, 2)
    greet_lines(narrow, depth)
    gathers = [
        StagedGather(pack, pack_all, pack_sems, narrow, depth),
        StagedGather(sums, sums_all, sums_sems, narrow, depth),
    ]
    line = LineSum(middle, middle_got, middle_sems, z, depth, lambda there: (n, there * 2 + c))
    backs = [
        Returned(
            values, landed, back_send.at[i], back_recv.at[i], back_own.at[i], n, w, narrow, i
        )
        for i, (values, landed) in enumerate(((up_sum, up_got), (down_sum, down_got)))
    ]
    for gather in gathers:
        gather.start()
    line.start()
    for back in backs:
        back.start()
    for gather in gathers:
        gather.spread()
    line.arrive()
    middle_out[...] = line.total()
    for gather in gathers:
        gather.cross()
    for back, landed, out in zip(backs, (up_got, down_got), (up_out, down_out)):
        back.arrive()
        out[...] = landed[...].astype(FULL)
    for gather in gathers:
        gather.finish()
    line.finish()
    for back in backs:
        back.finish()


class Returned:
    def __init__(self, values, got, send, recv, own, n, w, narrow, axis):
        span = values.shape[axis] // narrow
        other = values.shape[1 - axis]

        def block(m):
            mine = pl.ds(m * span, span)
            return values.at[mine, :] if axis == 0 else values.at[:, mine]

        there = pl.ds(n * other, other)
        landing = got.at[:, there] if axis == 0 else got.at[there, :]
        self.own = pltpu.make_async_copy(block(n), landing, own)
        self.copies = []
        for k in range(1, narrow):
            m = lax.rem(n + k, narrow)
            self.copies.append(
                remote(block(m), landing, send.at[k - 1], recv.at[k - 1], (m, w))
            )

    def start(self):
        self.own.start()
        for copy in self.copies:
            copy.start()

    def arrive(self):
        self.own.wait()
        for copy in self.copies:
            copy.wait_recv()

    def finish(self):
        for copy in self.copies:
            copy.wait_send()


def end_gather(pack, sums, middle, up_sum, down_sum, collective_id):
    narrow, wide = lax.axis_size(NARROW), lax.axis_size(WIDE)
    depth = wide // 2
    dma = pltpu.SemaphoreType.DMA
    anywhere = pl.BlockSpec(memory_space=pl.ANY)
    up_shape = (up_sum.shape[0] // narrow, up_sum.shape[1] * narrow)
    down_shape = (down_sum.shape[0] * narrow, down_sum.shape[1] // narrow)
    outs = pl.pallas_call(
        partial(end_kernel, narrow, depth),
        out_shape=[
            jax.ShapeDtypeStruct((narrow, depth, 2) + pack.shape, pack.dtype),
            jax.ShapeDtypeStruct((narrow, depth, 2) + sums.shape, sums.dtype),
            jax.ShapeDtypeStruct(middle.shape[1:], FULL),
            jax.ShapeDtypeStruct(up_shape, FULL),
            jax.ShapeDtypeStruct(down_shape, FULL),
        ],
        in_specs=[anywhere] * 5,
        out_specs=[anywhere] * 2 + [in_vmem()] * 3,
        scratch_shapes=[
            pltpu.VMEM(middle.shape, middle.dtype),
            pltpu.VMEM(up_shape, LOW),
            pltpu.VMEM(down_shape, LOW),
            dma((7,)),
            dma((7,)),
            dma((2 * depth,)),
            dma((2, narrow - 1)),
            dma((2, narrow - 1)),
            dma((2,)),
        ],
        compiler_params=pltpu.CompilerParams(
            collective_id=collective_id, has_side_effects=True, vmem_limit_bytes=32 << 20
        ),
        name="end_gather",
    )(pack, sums, middle, up_sum, down_sum)
    return [
        outs[0].reshape(-1, pack.shape[1]),
        outs[1].reshape((-1,) + sums.shape),
    ] + list(outs[2:])


def softplus(v):
    return jnp.maximum(v, 0.0) + jnp.log1p(jnp.exp(-jnp.abs(v)))


def convolved(window, marks, weight, bias):
    pre = bias + weight[CONV - 1 :] * window[8:]
    for lag in range(1, CONV):
        pre = pre + weight[CONV - 1 - lag : CONV - lag] * (
            window[8 - lag : 8 - lag + QUERY] * marks[:, lag : lag + 1]
        )
    return pre


def decays(marks, dt, step_bias, rate_scale):
    shape = (QUERY, QUERY)
    row = lax.broadcasted_iota(jnp.int32, shape, 0)
    column = lax.broadcasted_iota(jnp.int32, shape, 1)
    lower = (row >= column).astype(FULL)
    segment = jnp.broadcast_to(marks[:, :1], shape)
    visible = (segment == segment.T) & (row >= column)
    delta = jnp.broadcast_to(softplus(dt + step_bias), shape)
    total = nn(lower, -delta * rate_scale, highest)
    gap = jnp.where(visible, total - total.T, 0.0)
    decay = jnp.where(visible, jnp.exp(gap), 0.0)
    last = total[QUERY - 1 :, :]
    begun = jnp.exp(total) * marks[:, 4:5]
    tail = jnp.exp(last - total) * marks[:, 5:6]
    kept = jnp.exp(last) * marks[:1, 6:7]
    return lower, delta, decay, begun, tail, kept


def head_numbers(step_bias, log_rate, skip_gain, me):
    return step_bias[me], jnp.exp(jnp.full((1, QUERY), log_rate[me], FULL)), skip_gain[me]


def head_columns(values, me):
    start = pl.multiple_of(lax.div(me, 2) * 2 * HEAD_M, 2 * HEAD_M)
    pair = values[:, pl.ds(start, 2 * HEAD_M)]
    lane = lax.broadcasted_iota(jnp.int32, pair.shape, 1)
    moved = jnp.concatenate([pair[:, HEAD_M:], pair[:, :HEAD_M]], axis=1)
    odd = jnp.full(pair.shape, lax.rem(me, 2), jnp.int32) == 1
    return jnp.where(lane < HEAD_M, jnp.where(odd, moved, pair), 0.0)


def documents(doc_patches, pad_bytes):
    ends, end = [], 0
    for d in range(doc_patches.shape[0]):
        end = end + doc_patches[d]
        ends.append(end)

    def document(place):
        return sum((place >= end).astype(jnp.int32) for end in ends)

    def kept(place, offset):
        padded = [
            ((place == end - 1) & (offset >= PATCH - pad_bytes[d])).astype(FULL)
            for d, end in enumerate(ends)
        ]
        return 1.0 - sum(padded)

    return document, kept


def patch_marks(document, first, count):
    place = first + lax.broadcasted_iota(jnp.int32, (count, 8), 0)
    kind = lax.broadcasted_iota(jnp.int32, (count, 8), 1)
    opening = lax.div(place, QUERY) * QUERY
    block_mark = jnp.where(kind == CONV, opening - 1, opening + QUERY - 1)
    ahead = jnp.where(kind < CONV, place - kind, block_mark)
    facing = jnp.where(kind == CONV + 2, opening - 1, place)
    same = (document(ahead) == document(facing)) & (ahead >= 0) & (facing >= 0)
    return jnp.where(kind == 0, document(place).astype(FULL), same.astype(FULL))


def mixer_front_kernel(
    narrow,
    wide,
    doc_patches,
    pad_bytes,
    step_biases,
    log_rates,
    skip_gains,
    start,
    table,
    w_xz,
    gain,
    conv_weight,
    conv_bias,
    gate,
    up,
    down,
    middle,
    embedded,
    normed,
    xz,
    bc,
    dt,
    u_out,
    y_out,
    states,
    mixed_in,
    u_got,
    marks,
    keep_rows,
    keep_all,
    gate_all,
    up_all,
    down_all,
    middle_all,
    mixed_all,
    xz_pad,
    bc_pad,
    state,
    u_blocks,
    u_send,
    u_recv,
    own_sems,
    line_send,
    line_recv,
    cross_send,
    cross_recv,
    middle_sems,
):
    devices, depth = narrow * wide, wide // 2
    me, arrived = greet_all(devices, wide)
    n, w = lax.axis_index(NARROW), lax.axis_index(WIDE)
    z, c = lax.div(w, 2), lax.rem(w, 2)
    twin = (n, z * 2 + 1 - c)
    turned = (gate, up, down)
    results = (gate_all, up_all, down_all)
    own = [pltpu.make_async_copy(turned[i], results[i].at[z, c], own_sems.at[i]) for i in range(3)]
    own.append(pltpu.make_async_copy(middle, middle_all.at[n, :, c], own_sems.at[3]))
    for copy in own:
        copy.start()
    beside, across, corner = square_of(n, narrow)
    arrived()

    def middle_copy(j, way, owner, src=None):
        there = middle_all.at[owner, j, c]
        peer = twin if way >= 4 else ((beside if way in (0, 3) else across), w)
        return remote(
            there if src is None else src, there, middle_sems.at[0, way, j], middle_sems.at[1, way, j], peer
        )

    for j in range(depth):
        middle_copy(j, 0, n, middle.at[j]).start()
        middle_copy(j, 1, n, middle.at[j]).start()

    def line_copy(i, source, step, src=None):
        there = results[i].at[source, c]
        return remote(
            there if src is None else src,
            there,
            line_send.at[i, source, max(step, 0)],
            line_recv.at[i, source],
            (n, (z + step) * 2 + c),
        )

    def along(i, source, step, src=None):
        @pl.when((z + step >= 0) & (z + step < depth))
        def _():
            line_copy(i, source, step, src).start()

    for i in range(3):
        along(i, z, 1, turned[i])
        along(i, z, -1, turned[i])
    own_middle = remote(
        middle, middle_all.at[n, :, c], middle_sems.at[0, 7, 0], middle_sems.at[1, 7, 0], twin
    )
    own_middle.start()

    def middle_on(j):
        middle_copy(j, 0, beside).wait_recv()
        if j % 2 == 0:
            middle_copy(j, 2, beside).start()
        middle_copy(j, 4, beside).start()
        middle_copy(j, 1, across).wait_recv()
        if j % 2 == 1:
            middle_copy(j, 3, across).start()
        middle_copy(j, 5, across).start()

    def line_on(distance):
        for step in (1, -1):
            source = z - step * distance

            @pl.when((source >= 0) & (source < depth))
            def _():
                for i in range(3):
                    line_copy(i, source, step).wait_recv()
                    along(i, source, step)
                    theirs = results[i].at[source, c]
                    remote(theirs, theirs, cross_send.at[i], cross_recv.at[i], twin).start()

    count = embedded.shape[0]
    patches = u_blocks.shape[1]
    block_rows = 2 * QUERY
    xz_pad[pl.ds(0, 8), :] = jnp.zeros((8, xz_pad.shape[1]), FULL)
    bc_pad[pl.ds(0, 8), :] = jnp.zeros((8, bc_pad.shape[1]), FULL)
    state[...] = jnp.zeros_like(state)
    step_bias, rate_scale, skip = head_numbers(step_biases, log_rates, skip_gains, me)
    document, kept_bytes = documents(doc_patches, pad_bytes)
    for first in range(0, count + 8, (count + 8) // 3):
        part = (count + 8) // 3
        marks[first : first + part, :] = patch_marks(document, first, part)
    byte = lax.broadcasted_iota(jnp.int32, keep_rows.shape[1:], 0)
    for k in range(narrow):
        there = (lax.rem(n + k, narrow) * wide + w) * patches
        keep_rows[k] = kept_bytes(there + lax.div(byte, PATCH), lax.rem(byte, PATCH))
    wx, bx = head_columns(conv_weight, me), head_columns(conv_bias, me)
    wbc, bbc = conv_weight[:, DI:], conv_bias[:, DI:]
    words = lax.broadcasted_iota(jnp.int32, (block_rows, VOCAB), 1).astype(FULL)
    own_lane = lax.broadcasted_iota(jnp.int32, (block_rows, STATE), 1) == me

    def project(i, carry):
        rows = pl.ds(pl.multiple_of(i * block_rows, block_rows), block_rows)
        ids = start[rows, 3 * STATE : 4 * STATE].astype(FULL)
        place = i * block_rows + lax.broadcasted_iota(jnp.int32, (block_rows, PATCH), 0)
        kept = kept_bytes(place, lax.broadcasted_iota(jnp.int32, (block_rows, PATCH), 1))
        keep_all[rows, :] = kept
        for k in range(PATCH):
            chosen = jnp.where(ids[:, k : k + 1] == words, kept[:, k : k + 1], 0.0).astype(LOW)
            embedded[rows, k * EMB : (k + 1) * EMB] = nn(chosen, table[...]).astype(LOW)
        row_embedded = embedded[rows, :]
        for first in range(0, D, WEIGHT_STEP):
            columns = slice(first, first + WEIGHT_STEP)
            weight = start[:, 4 * STATE + first : 4 * STATE + first + WEIGHT_STEP]
            mixed_all[rows, columns] = nn(row_embedded, weight)
        row_normed = (unit_rows(mixed_all[rows, :])[0] * gain[...]).astype(LOW)
        normed[rows, :] = row_normed
        row_xz = nn(row_normed, w_xz[...]).astype(LOW)
        row_bcdt = nn(row_normed, start[:, : 3 * STATE]).astype(LOW)
        xz[rows, :] = row_xz
        bc[rows, :] = row_bcdt[:, : 2 * STATE]
        own_dt = jnp.where(own_lane, row_bcdt[:, 2 * STATE :].astype(FULL), 0.0)
        dt[rows, :] = jnp.sum(own_dt, axis=1, keepdims=True)
        padded = pl.ds(pl.multiple_of(i * block_rows + 8, 8), block_rows)
        xz_pad[padded, :] = row_xz.astype(FULL)
        bc_pad[padded, :] = row_bcdt[:, : 2 * STATE].astype(FULL)
        return carry

    lax.fori_loop(0, count // block_rows, project, 0)
    middle_on(0)
    mixed_in[...] = mixed_all[pl.ds(pl.multiple_of(me * patches, patches), patches), :]
    group = QUERY // patches

    def block(i, carry):
        first = pl.multiple_of(i * QUERY, QUERY)
        rows = pl.ds(first, QUERY)
        mark = marks[rows, :]
        act_x = jax.nn.silu(convolved(xz_pad[pl.ds(first, QUERY + 8), :], mark, wx, bx))
        act = jax.nn.silu(convolved(bc_pad[pl.ds(first, QUERY + 8), :], mark, wbc, bbc))
        x, b, c = act_x[:, :HEAD_M], act[:, :STATE], act[:, STATE:]
        lower, delta, decay, begun, tail, kept = decays(mark, dt[rows, :], step_bias, rate_scale)
        weight = nt(c, b, highest) * decay * delta.T
        held = state[...]
        states[i] = held
        y = (
            nn(weight, x, highest)
            + nt(c, held, highest) * begun[:, :HEAD_M]
            + skip * x
        )
        state[...] = held * kept + tn(x * (tail * delta)[:, :HEAD_M], b, highest)
        z = xz[rows, :].astype(FULL)[:, HEAD_M:]
        u = y * jax.nn.silu(z)
        y_out[rows, :] = y
        u_out[rows, :] = u
        u_blocks[pl.ds(i * group, group)] = u.astype(LOW).reshape(group, patches, HEAD_M)
        return carry

    lax.fori_loop(0, count // QUERY, block, 0)
    send_blocks(me, devices, wide, u_blocks, u_got, u_send, u_recv)
    u_got[me] = u_blocks[me]
    line_on(1)
    middle_on(1)
    for copy in own:
        copy.wait()
    for i in range(3):
        mine = results[i].at[z, c]
        remote(mine, mine, cross_send.at[i], cross_recv.at[i], twin).start()
    middle_on(2)
    line_on(2)
    middle_on(3)
    for j in range(depth):
        middle_copy(j, 2 + j % 2, corner).wait_recv()
        middle_copy(j, 6, corner).start()
    line_on(3)
    wait_blocks(me, devices, wide, u_got, u_send, u_recv)
    for i in range(3):
        theirs = results[i].at[:, 1 - c]
        remote(theirs, theirs, cross_send.at[i], cross_recv.at[i], twin).wait()
    own_middle.wait()
    for j in range(depth):
        for way, owner in ((4, beside), (5, across), (6, corner)):
            middle_copy(j, way, owner).wait()
        middle_copy(j, 0, n, middle.at[j]).wait_send()
        middle_copy(j, 1, n, middle.at[j]).wait_send()
        middle_copy(j, 2 + j % 2, n).wait_send()
    for i in range(3):
        for source in range(depth):
            for step in (1, -1):

                @pl.when((step * (z - source) >= 0) & (z + step >= 0) & (z + step < depth))
                def _():
                    line_copy(i, source, step).wait_send()


def mixer_backward_kernel(
    narrow,
    wide,
    step_biases,
    log_rates,
    skip_gains,
    xz,
    bc,
    dt,
    marks,
    conv_weight,
    conv_bias,
    y_in,
    states,
    normed,
    w_xz,
    start,
    mixed_in,
    global_grad,
    gain,
    gated_scale,
    gain_grads,
    gated_gain_grads,
    du_blocks,
    up_parts,
    down_parts,
    middle_parts,
    gate_sum,
    mix_grad,
    end_pack,
    sums,
    bcdt_grads,
    xz_grads,
    up_sum,
    down_sum,
    middle_sums,
    gate_out,
    mix_all,
    w_bcdt,
    w_sem,
    dwx,
    dwbc,
    dnumbers,
    xz_pad,
    bc_pad,
    dx_pad,
    dbc_pad,
    dstate,
    du_got,
    dxz,
    dbcdt,
    partial_rows,
    core_got,
    narrow_got,
    z_rows,
    z_got,
    grads,
    grads_got,
    up_got,
    down_got,
    middle_own,
    middle_held,
    middle_got,
    gate_got,
    du_send,
    du_recv,
    core_send,
    core_recv,
    narrow_send,
    narrow_recv,
    z_send,
    z_recv,
    grads_send,
    grads_recv,
    up_sems,
    down_sems,
    middle_sems,
    back_send,
    back_recv,
    back_own,
    mix_sems,
):
    devices = narrow * wide
    depth = wide // 2
    me, arrived = greet_all(devices, wide)
    n, w = lax.axis_index(NARROW), lax.axis_index(WIDE)
    z_place, core = lax.div(w, 2), lax.rem(w, 2)
    twin = (n, z_place * 2 + 1 - core)
    count = xz.shape[0]
    blocks = count // QUERY
    xz_pad[pl.ds(0, 8), :] = jnp.zeros((8, xz_pad.shape[1]), FULL)
    bc_pad[pl.ds(0, 8), :] = jnp.zeros((8, bc_pad.shape[1]), FULL)
    dx_pad[pl.ds(count, 8), :] = jnp.zeros((8, dx_pad.shape[1]), FULL)
    dbc_pad[pl.ds(count, 8), :] = jnp.zeros((8, dbc_pad.shape[1]), FULL)
    dstate[...] = jnp.zeros_like(dstate)
    dwx[...] = jnp.zeros_like(dwx)
    dwbc[...] = jnp.zeros_like(dwbc)
    dnumbers[...] = jnp.zeros_like(dnumbers)
    step_bias, rate_scale, skip = head_numbers(step_biases, log_rates, skip_gains, me)
    wx, bx = head_columns(conv_weight, me), head_columns(conv_bias, me)
    wbc, bbc = conv_weight[:, DI:], conv_bias[:, DI:]
    weight_copy = pltpu.make_async_copy(start.at[:, pl.ds(0, 3 * STATE)], w_bcdt, w_sem)
    weight_copy.start()

    def fill(i, carry):
        first = pl.multiple_of(i * QUERY, QUERY)
        rows = pl.ds(first, QUERY)
        xz_pad[pl.ds(first + 8, QUERY), :] = xz[rows, :].astype(FULL)
        bc_pad[pl.ds(first + 8, QUERY), :] = bc[rows, :].astype(FULL)
        return carry

    arrived()
    send_blocks(me, devices, wide, du_blocks, du_got, du_send, du_recv)
    lines = [
        LineSum(parts, landed, line_sems, z_place, depth, lambda there: (n, there * 2 + core))
        for parts, landed, line_sems in (
            (down_parts, down_got, down_sems),
            (up_parts, up_got, up_sems),
        )
    ]
    middle_line = SquareSum(
        middle_parts, middle_own, middle_held, middle_got, middle_sems, n, w, narrow
    )
    back = Returned(gate_sum, gate_got, back_send, back_recv, back_own, n, w, narrow, 0)
    mix_gather = StagedGather(mix_grad, mix_all, mix_sems, narrow, depth)
    middle_line.start()
    mix_gather.start()
    for line in lines:
        line.start()
    back.start()
    du_got[me] = du_blocks[me]
    lax.fori_loop(0, blocks, fill, 0)
    wait_blocks(me, devices, wide, du_got, du_send, du_recv)
    patches = du_blocks.shape[1]
    group = QUERY // patches
    own_lane = lax.broadcasted_iota(jnp.int32, (QUERY, STATE), 1) == me

    def slope(pre):
        s = jax.nn.sigmoid(pre)
        return s * (1.0 + pre * (1.0 - s))

    def total(v):
        return jnp.sum(jnp.sum(v, axis=1, keepdims=True), axis=0, keepdims=True)

    def conv_back(pad, first, dpre_pad, dpre, weight, dw):
        mark = marks[pl.ds(first, QUERY), :]
        window = pad[pl.ds(first, QUERY + 8), :]
        later = dpre_pad[pl.ds(first, QUERY + 8), :]
        later_marks = marks[pl.ds(first, QUERY + 8), :]
        out = weight[CONV - 1 :] * dpre
        dw[CONV - 1 : CONV, :] += jnp.sum(dpre * window[8:], axis=0, keepdims=True)
        dw[CONV : CONV + 1, :] += jnp.sum(dpre, axis=0, keepdims=True)
        for lag in range(1, CONV):
            tap = CONV - 1 - lag
            out = out + weight[tap : tap + 1] * (
                (later * later_marks[:, lag : lag + 1])[lag : lag + QUERY]
            )
            dw[tap : tap + 1, :] += jnp.sum(
                dpre * (window[8 - lag : 8 - lag + QUERY] * mark[:, lag : lag + 1]),
                axis=0,
                keepdims=True,
            )
        return out

    def block(k, carry):
        i = blocks - 1 - k
        first = pl.multiple_of(i * QUERY, QUERY)
        rows = pl.ds(first, QUERY)
        mark = marks[rows, :]
        pre_x = convolved(xz_pad[pl.ds(first, QUERY + 8), :], mark, wx, bx)
        pre = convolved(bc_pad[pl.ds(first, QUERY + 8), :], mark, wbc, bbc)
        act = jax.nn.silu(pre)
        x, b, c = jax.nn.silu(pre_x)[:, :HEAD_M], act[:, :STATE], act[:, STATE:]
        step = dt[rows, :]
        lower, delta, decay, begun, tail, kept = decays(mark, step, step_bias, rate_scale)
        held, dheld = states[i], dstate[...]
        z = xz[rows, :].astype(FULL)[:, HEAD_M:]
        du = du_got[pl.ds(i * group, group)].astype(FULL).reshape(QUERY, HEAD_M)
        y = y_in[rows, :]
        dy = du * jax.nn.silu(z)
        dz = du * y * slope(z)
        scores = nt(c, b, highest)
        reach = decay * delta.T
        dweight = nt(dy, x, highest)
        dscores = dweight * reach
        fed = x * (tail * delta)[:, :HEAD_M]
        begun_dy = dy * begun[:, :HEAD_M]
        dc = nn(dscores, b, highest) + nn(begun_dy, held, highest)
        db = tn(dscores, c, highest) + nn(fed, dheld, highest)
        dfed = nt(b, dheld, highest)
        dx = skip * dy + tn(scores * reach, dy, highest) + (tail * delta)[:, :HEAD_M] * dfed
        moved = dweight * scores * decay
        turned = moved.T
        ddelta = jnp.sum(turned, axis=1, keepdims=True)
        dtotal = jnp.sum(moved * delta.T, axis=1, keepdims=True) - ddelta * delta[:, :1]
        dtotal += jnp.sum(begun_dy * nt(c, held, highest), axis=1, keepdims=True)
        dtail = jnp.sum(dfed * x, axis=1, keepdims=True)
        ddelta += dtail * tail[:, :1]
        dtail = dtail * (tail * delta)[:, :1]
        dtotal -= dtail
        dlast = jnp.sum(dtail, axis=0, keepdims=True) + total(dheld * held * kept)
        dlog = tn(lower, jnp.broadcast_to(dtotal, (QUERY, QUERY)), highest)[:, :1] + dlast
        ddelta -= dlog * rate_scale[:, :1]
        dstep = ddelta * jax.nn.sigmoid(step + step_bias)
        dbcdt[rows, 2 * STATE :] = jnp.where(own_lane, dstep, 0.0).astype(LOW)
        dnumbers[0:1, :] += jnp.broadcast_to(jnp.sum(dstep, axis=0, keepdims=True), (1, 128))
        dnumbers[1:2, :] -= jnp.broadcast_to(
            jnp.sum(dlog * delta[:, :1] * rate_scale[:, :1], axis=0, keepdims=True), (1, 128)
        )
        dnumbers[2:3, :] += jnp.broadcast_to(total(dy * x), (1, 128))
        dstate[...] = dheld * kept + tn(begun_dy, c, highest)
        dpre_x = jnp.concatenate([dx, jnp.zeros_like(dx)], axis=1) * slope(pre_x)
        dpre = jnp.concatenate([db, dc], axis=1) * slope(pre)
        dx_pad[rows, :] = dpre_x
        dbc_pad[rows, :] = dpre
        dxz[rows, :] = jnp.concatenate([dz, dz], axis=1).astype(LOW)
        return carry

    lax.fori_loop(0, blocks, block, 0)

    def unconvolve(i, carry):
        first = pl.multiple_of(i * QUERY, QUERY)
        rows = pl.ds(first, QUERY)
        dxr = conv_back(xz_pad, first, dx_pad, dx_pad[rows, :], wx, dwx)
        left = lax.broadcasted_iota(jnp.int32, dxr.shape, 1) < HEAD_M
        dxz[rows, :] = jnp.where(left, dxr, dxz[rows, :].astype(FULL)).astype(LOW)
        dbcdt[rows, : 2 * STATE] = conv_back(
            bc_pad, first, dbc_pad, dbc_pad[rows, :], wbc, dwbc
        ).astype(LOW)
        return carry

    middle_line.relay()
    mix_gather.spread()
    lax.fori_loop(0, blocks, unconvolve, 0)

    width = normed.shape[1]
    own_rows = xz_grads.shape[1]

    weight_copy.wait()

    def rows_of(m, carry):
        for z in range(depth):
            first = (m * depth + z) * 2 * patches
            rows = pl.ds(pl.multiple_of(first, 2 * patches), 2 * patches)
            values = nt(dxz[rows, :], w_xz[...]) + nt(dbcdt[rows, :], w_bcdt[...])
            partial_rows[m, z, :, :, :width] = values.astype(LOW).reshape(2, patches, width)
        return carry

    lax.fori_loop(0, narrow, rows_of, 0)

    def weight_grads(m, carry):
        span = width // narrow
        columns = pl.ds(pl.multiple_of(m * span, span), span)
        lhs = normed[:, columns]
        grads[pl.ds(m * 2 * depth, 2 * depth)] = (
            tn(lhs, dxz[...]).astype(LOW).reshape(2 * depth, own_rows, 2 * HEAD_M)
        )
        partial_rows[m, :, :, :, width:] = (
            tn(lhs, dbcdt[...]).astype(LOW).reshape(depth, 2, own_rows, 3 * STATE)
        )
        return carry

    lax.fori_loop(0, narrow, weight_grads, 0)
    to_twin = remote(partial_rows.at[:, :, 1 - core], core_got, core_send, core_recv, twin)
    to_twin.start()
    send_blocks(me, devices, wide, grads, grads_got, grads_send, grads_recv)
    grads_got[me] = grads[me]
    back.arrive()
    gate_out[...] = gate_got[...].astype(FULL)
    to_twin.wait_recv()

    def narrow_copy(k, m):
        return remote(
            core_got.at[m], narrow_got.at[k - 1], narrow_send.at[k - 1], narrow_recv.at[k - 1], (m, w)
        )

    for k in range(1, narrow):
        m = lax.rem(n + k, narrow)
        for z in range(depth):
            core_got[m, z] = (
                core_got[m, z].astype(FULL) + partial_rows[m, z, core].astype(FULL)
            ).astype(LOW)
        narrow_copy(k, m).start()
    mix_gather.cross()
    middle_line.arrive()
    for z in range(depth):
        middle_sums[z] = middle_line.total(z).astype(LOW)
    for k in range(1, narrow):
        narrow_copy(k, n).wait_recv()
    for z in range(depth):
        total_rows = core_got[n, z].astype(FULL) + partial_rows[n, z, core].astype(FULL)
        for k in range(1, narrow):
            total_rows += narrow_got[k - 1, z].astype(FULL)
        z_rows[z] = total_rows.astype(LOW)

    def z_copy(k, place):
        return remote(
            z_rows.at[place], z_got.at[k - 1], z_send.at[k - 1], z_recv.at[k - 1], (n, place * 2 + core)
        )

    for k in range(1, depth):
        z_copy(k, lax.rem(z_place + k, depth)).start()
    for line, out in zip(lines, (down_sum, up_sum)):
        line.arrive()
        out[...] = line.total().astype(LOW)
    wait_blocks(me, devices, wide, grads_got, grads_send, grads_recv)
    xz_grads[...] = grads_got[...]
    total_rows = z_rows[z_place].astype(FULL)
    for k in range(1, depth):
        z_copy(k, z_place).wait_recv()
        total_rows += z_got[k - 1].astype(FULL)
    bcdt_grads[...] = total_rows[:, width:]
    unit, scale = unit_rows(mixed_in[...])
    normed_grad = total_rows[:, :width]
    embed_grad = global_grad[...] + norm_back(normed_grad, gain[...], unit, scale)
    end_pack[:, :width] = embed_grad.astype(LOW)
    end_pack[:, width:] = gated_scale[...].astype(LOW)
    gain_mix_grad = jnp.sum(normed_grad * unit, axis=0, keepdims=True)
    wide_rows = [gain_mix_grad] + [gated_gain_grads[i : i + 1, :] for i in range(2)]
    wide_rows += [gain_grads[i : i + 1, :] for i in range(2)]
    wide_rows += [dwbc[i : i + 1, :] for i in range(CONV + 1)]
    wide_rows += [dwx[i : i + 1, :] for i in range(CONV + 1)]
    row = 0
    for values in wide_rows:
        for first in range(0, values.shape[1], 128):
            sums[row : row + 1, :] = values[:, first : first + 128]
            row += 1
    lane = lax.broadcasted_iota(jnp.int32, (1, 128), 1)
    sums[row : row + 1, :] = sum(
        jnp.where(lane == i, dnumbers[i : i + 1, :], 0.0) for i in range(3)
    )
    mix_gather.finish()
    for line in lines:
        line.finish()
    middle_line.finish()
    back.finish()
    to_twin.wait_send()
    for k in range(1, narrow):
        narrow_copy(k, n).wait_send()
    for k in range(1, depth):
        z_copy(k, z_place).wait_send()


def in_smem():
    return pl.BlockSpec(memory_space=pltpu.SMEM)


def in_vmem():
    return pl.BlockSpec(memory_space=pltpu.VMEM)


def mixer_front(scalars, start, table, w_xz, gain, conv_weight, conv_bias, turned, middle, collective_id):
    narrow, wide = lax.axis_size(NARROW), lax.axis_size(WIDE)
    devices = narrow * wide
    count = start.shape[0]
    patches = count // devices
    dma = pltpu.SemaphoreType.DMA

    def full(*shape):
        return jax.ShapeDtypeStruct(shape, FULL)

    def low(*shape):
        return jax.ShapeDtypeStruct(shape, LOW)

    depth = wide // 2
    anywhere = pl.BlockSpec(memory_space=pl.ANY)
    outs = pl.pallas_call(
        partial(mixer_front_kernel, narrow, wide),
        out_shape=[
            low(count, D),
            low(count, D),
            low(count, 2 * HEAD_M),
            low(count, 2 * STATE),
            full(count, 1),
            full(count, HEAD_M),
            full(count, HEAD_M),
            full(count // QUERY, HEAD_M, STATE),
            full(patches, D),
            low(devices, patches, HEAD_M),
            full(count + 8, 8),
            full(narrow, patches * PATCH, 1),
            full(count, PATCH),
        ]
        + [low(depth, 2, *part.shape) for part in turned]
        + [low(narrow, depth, 2, *middle.shape[1:])],
        in_specs=[in_smem()] * 5 + [in_vmem()] * 6 + [anywhere] * 4,
        out_specs=[in_vmem()] * 13 + [anywhere] * 4,
        scratch_shapes=[
            pltpu.VMEM((count, D), FULL),
            pltpu.VMEM((count + 8, 2 * HEAD_M), FULL),
            pltpu.VMEM((count + 8, 2 * STATE), FULL),
            pltpu.VMEM((HEAD_M, STATE), FULL),
            pltpu.VMEM((devices, patches, HEAD_M), LOW),
            dma,
            dma,
            dma((4,)),
            dma((3, depth, 2)),
            dma((3, depth)),
            dma((3,)),
            dma((3,)),
            dma((2, 8, depth)),
        ],
        compiler_params=pltpu.CompilerParams(
            collective_id=collective_id, has_side_effects=True, vmem_limit_bytes=48 << 20
        ),
        name="mixer_front",
    )(*scalars, start, table, w_xz, gain, conv_weight, conv_bias, *turned, middle)
    gate_all, up_all, down_all, middle_all = outs[13:]
    return (
        outs[:13],
        gate_all.reshape(wide, D, -1),
        up_all.reshape(wide, D, -1),
        down_all.reshape(-1, D),
        middle_all.reshape(D, -1),
    )


def mixer_backward(
    scalars,
    xz,
    bc,
    dt,
    marks,
    conv_weight,
    conv_bias,
    y,
    states,
    normed,
    w_xz,
    start,
    mixed_in,
    global_grad,
    gain,
    gated_scale,
    gain_grads,
    gated_gain_grads,
    du_blocks,
    up_parts,
    down_parts,
    middle_parts,
    gate_sum,
    mix_grad,
    collective_id,
):
    narrow, wide = lax.axis_size(NARROW), lax.axis_size(WIDE)
    devices = narrow * wide
    count, width = normed.shape
    patches = count // devices
    own_rows = width // devices
    dma = pltpu.SemaphoreType.DMA
    low = partial(pltpu.VMEM, dtype=LOW)
    every = width + 3 * STATE
    back_shape = (gate_sum.shape[0] // narrow, gate_sum.shape[1] * narrow)
    anywhere = pl.BlockSpec(memory_space=pl.ANY)
    return pl.pallas_call(
        partial(mixer_backward_kernel, narrow, wide),
        out_shape=[
            jax.ShapeDtypeStruct((patches, width + 128), LOW),
            jax.ShapeDtypeStruct((SUM_ROWS + CONV + 2, 128), FULL),
            jax.ShapeDtypeStruct((own_rows, 3 * STATE), FULL),
            jax.ShapeDtypeStruct((devices, own_rows, 2 * HEAD_M), LOW),
            jax.ShapeDtypeStruct(up_parts.shape[1:], LOW),
            jax.ShapeDtypeStruct(down_parts.shape[1:], LOW),
            jax.ShapeDtypeStruct(middle_parts.shape[1:], LOW),
            jax.ShapeDtypeStruct(back_shape, FULL),
            jax.ShapeDtypeStruct((narrow, wide // 2, 2) + mix_grad.shape, LOW),
        ],
        in_specs=[in_smem()] * 3
        + [in_vmem()] * 10
        + [anywhere]
        + [in_vmem()] * 7
        + [anywhere] * 5,
        out_specs=[in_vmem()] * 8 + [anywhere],
        scratch_shapes=[
            low((width, 3 * STATE)),
            dma,
            pltpu.VMEM((8, 2 * HEAD_M), FULL),
            pltpu.VMEM((8, 2 * STATE), FULL),
            pltpu.VMEM((8, 128), FULL),
            pltpu.VMEM((count + 8, 2 * HEAD_M), FULL),
            pltpu.VMEM((count + 8, 2 * STATE), FULL),
            pltpu.VMEM((count + 8, 2 * HEAD_M), FULL),
            pltpu.VMEM((count + 8, 2 * STATE), FULL),
            pltpu.VMEM((HEAD_M, STATE), FULL),
            low((devices, patches, HEAD_M)),
            low((count, 2 * HEAD_M)),
            low((count, 3 * STATE)),
            low((narrow, wide // 2, 2, patches, every)),
            low((narrow, wide // 2, patches, every)),
            low((narrow - 1, wide // 2, patches, every)),
            low((wide // 2, patches, every)),
            low((wide // 2 - 1, patches, every)),
            low((devices, own_rows, 2 * HEAD_M)),
            low((devices, own_rows, 2 * HEAD_M)),
            low(up_parts.shape),
            low(down_parts.shape),
            low(middle_parts.shape[1:]),
            low((2, wide // 4) + middle_parts.shape[2:]),
            low((6, wide // 4) + middle_parts.shape[2:]),
            low(back_shape),
            dma,
            dma,
            dma,
            dma,
            dma((narrow - 1,)),
            dma((narrow - 1,)),
            dma((wide // 2 - 1,)),
            dma((wide // 2 - 1,)),
            dma,
            dma,
            dma((wide,)),
            dma((wide,)),
            dma((2, 8)),
            dma((narrow - 1,)),
            dma((narrow - 1,)),
            dma,
            dma((7,)),
        ],
        compiler_params=pltpu.CompilerParams(
            collective_id=collective_id, has_side_effects=True, vmem_limit_bytes=56 << 20
        ),
        name="mixer_backward",
    )(
        *scalars,
        xz,
        bc,
        dt,
        marks,
        conv_weight,
        conv_bias,
        y,
        states,
        normed,
        w_xz,
        start,
        mixed_in,
        global_grad,
        gain,
        gated_scale,
        gain_grads,
        gated_gain_grads,
        du_blocks,
        up_parts,
        down_parts,
        middle_parts,
        gate_sum,
        mix_grad,
    )


def finish_kernel(
    pack_all,
    mix_all,
    u,
    keep,
    middle,
    xz_grads,
    bcdt_grads,
    gated_gain,
    embedded,
    start,
    table_out,
    patch_out,
    in_out,
    out_out,
    local_out,
    query_out,
    key_out,
    value_out,
    attn_out,
    embedded_own,
    ids_all,
    patch_all,
    rows_of_four,
    sems,
):
    me = lax.axis_index(NARROW) * lax.axis_size(WIDE) + lax.axis_index(WIDE)
    own_rows = patch_out.shape[0]
    group = 128 // own_rows
    columns = pl.ds(pl.multiple_of(lax.div(me, group) * 128, 128), 128)
    copies = [
        pltpu.make_async_copy(embedded.at[:, columns], embedded_own, sems.at[0]),
        pltpu.make_async_copy(start.at[:, pl.ds(3 * STATE, 128)], ids_all, sems.at[1]),
        pltpu.make_async_copy(start.at[:, pl.ds(4 * STATE, D)], patch_all, sems.at[2]),
    ]
    for copy in copies:
        copy.start()
    for i, out in enumerate((query_out, key_out, value_out, attn_out)):
        out[...] = middle[:, i * D : (i + 1) * D]
    local_out[...] = middle[:, 4 * D :].T
    for pair in range(0, HEADS_M, 2):
        both = [xz_grads[pair + i].astype(FULL) for i in range(2)]
        first = pair * HEAD_M
        in_out[:, first : first + 128] = jnp.concatenate([v[:, HEAD_M:] for v in both], axis=1)
        in_out[:, DI + first : DI + first + 128] = jnp.concatenate(
            [v[:, :HEAD_M] for v in both], axis=1
        )
    in_out[:, 2 * DI : 2 * DI + 2 * STATE] = bcdt_grads[:, : 2 * STATE]
    in_out[:, 2 * DI + 2 * STATE :] = bcdt_grads[:, 2 * STATE : 2 * STATE + HEADS_M]
    scale = pack_all[:, D:].astype(FULL)[:, :HEAD_M]
    gain = head_columns(gated_gain, me)[:, :HEAD_M]
    gated = (u[...] * scale * gain).astype(LOW)
    out_out[...] = tn(gated, mix_all[...])
    copies[0].wait()
    copies[1].wait()
    grads = pack_all[:, :D]
    rows_of_four[...] = tn(embedded_own[...], grads)
    patch_out[...] = rows_of_four[pl.ds(pl.multiple_of(lax.rem(me, group) * own_rows, own_rows), own_rows), :]
    own_words = table_out.shape[0]
    count = pack_all.shape[0]
    lane = lax.broadcasted_iota(jnp.int32, (count, PATCH * own_words), 1)
    ids = jnp.zeros((count, PATCH * own_words), FULL)
    kept = jnp.zeros((count, PATCH * own_words), FULL)
    values = ids_all[...].astype(FULL)
    for k in range(PATCH):
        here = lax.div(lane, own_words) == k
        ids = jnp.where(here, values[:, k : k + 1], ids)
        kept = jnp.where(here, keep[:, k : k + 1], kept)
    words = (me * own_words + lax.rem(lane, own_words)).astype(FULL)
    sums = tn(jnp.where(ids == words, kept, 0.0).astype(LOW), grads)
    high = sums.astype(LOW)
    rest = (sums - high.astype(FULL)).astype(LOW)
    copies[2].wait()
    table = jnp.zeros(table_out.shape, FULL)
    for k in range(PATCH):
        rows = slice(k * own_words, (k + 1) * own_words)
        weight = patch_all[k * EMB : (k + 1) * EMB, :]
        table += nt(high[rows], weight) + nt(rest[rows], weight)
    table_out[...] = table


def finish(pack_all, mix_all, u, keep, middle, xz_grads, bcdt_grads, gated_gain, embedded, start):
    count = pack_all.shape[0]
    devices, own_rows = xz_grads.shape[:2]
    anywhere = pl.BlockSpec(memory_space=pl.ANY)

    def full(*shape):
        return jax.ShapeDtypeStruct(shape, FULL)

    return pl.pallas_call(
        finish_kernel,
        out_shape=[
            full(VOCAB // devices, EMB),
            full(own_rows, D),
            full(own_rows, 2 * DI + 2 * STATE + HEADS_M),
            full(DI // devices, D),
            full(EMB, own_rows),
        ]
        + [full(own_rows, D)] * 4,
        in_specs=[in_vmem()] * 8 + [anywhere] * 2,
        out_specs=[in_vmem()] * 9,
        scratch_shapes=[
            pltpu.VMEM((count, 128), LOW),
            pltpu.VMEM((count, 128), LOW),
            pltpu.VMEM((D, D), LOW),
            pltpu.VMEM((128, D), FULL),
            pltpu.SemaphoreType.DMA((3,)),
        ],
        compiler_params=pltpu.CompilerParams(vmem_limit_bytes=40 << 20),
        name="finish",
    )(pack_all, mix_all, u, keep, middle, xz_grads, bcdt_grads, gated_gain, embedded, start)


def patch_causal():
    row = lax.broadcasted_iota(jnp.int32, (BYTE_BLOCK, BYTE_BLOCK), 0)
    column = lax.broadcasted_iota(jnp.int32, (BYTE_BLOCK, BYTE_BLOCK), 1)
    return (lax.div(row, PATCH) == lax.div(column, PATCH)) & (row >= column)


def head_probs(q, k, causal):
    scores = jnp.where(causal, nt(q, k) * HEAD_A ** (-0.5), masked_score)
    grown = jnp.exp(scores - jnp.max(scores, axis=1, keepdims=True))
    return grown / jnp.sum(grown, axis=1, keepdims=True)


def of_head(block, half):
    lane = lax.broadcasted_iota(jnp.int32, block.shape, 1)
    return jnp.where(lax.div(lane, HEAD_A) == half, block, jnp.zeros_like(block))


def fetched(pack, places, blocks, sems):
    copies = []
    for i, place in enumerate(places):
        width = place.shape[1]
        start = blocks[i]
        copies.append(
            pltpu.make_async_copy(pack.at[:, pl.ds(start, width)], place, sems.at[i])
        )
        copies[-1].start()
    return [copy.wait for copy in copies]


def unit_rows(values):
    scale = lax.rsqrt(jnp.mean(values * values, axis=1, keepdims=True) + epsilon)
    return values * scale, scale


def norm_back(grad, gain, unit, scale):
    scaled = grad * gain
    return scale * (scaled - unit * jnp.mean(scaled * unit, axis=1, keepdims=True))


WEIGHT_STEP = 256


def attend_pairs(qkv, mixed):
    causal = patch_causal()
    blocks = qkv.shape[0] // BYTE_BLOCK

    def pair(i, carry):
        def lanes(part):
            start = part * D + i * (2 * HEAD_A)
            return pl.ds(pl.multiple_of(start, 2 * HEAD_A), 2 * HEAD_A)

        for block in range(blocks):
            rows = pl.ds(block * BYTE_BLOCK, BYTE_BLOCK)
            q, k, v = qkv[rows, lanes(0)], qkv[rows, lanes(1)], qkv[rows, lanes(2)]
            total = jnp.zeros(q.shape, FULL)
            for half in range(2):
                probs = head_probs(of_head(q, half), k, causal)
                total += nn(probs.astype(LOW), of_head(v, half))
            mixed[rows, lanes(0)] = total.astype(LOW)
        return carry

    lax.fori_loop(0, HEADS_A // 2, pair, 0)


def attend_pairs_back(qkv, heads_grad, qkv_grad):
    causal = patch_causal()
    blocks = qkv.shape[0] // BYTE_BLOCK
    scale = HEAD_A ** (-0.5)

    def pair(i, carry):
        def lanes(part):
            start = part * D + i * (2 * HEAD_A)
            return pl.ds(pl.multiple_of(start, 2 * HEAD_A), 2 * HEAD_A)

        for block in range(blocks):
            rows = pl.ds(block * BYTE_BLOCK, BYTE_BLOCK)
            q, k, v = qkv[rows, lanes(0)], qkv[rows, lanes(1)], qkv[rows, lanes(2)]
            g = heads_grad[rows, lanes(0)]
            dq = jnp.zeros(q.shape, FULL)
            dk = jnp.zeros(q.shape, FULL)
            dv = jnp.zeros(q.shape, FULL)
            for half in range(2):
                own_q, own_k, own_g = of_head(q, half), of_head(k, half), of_head(g, half)
                probs = head_probs(own_q, k, causal)
                dprobs = nt(own_g, v)
                dv += tn(probs.astype(LOW), own_g)
                dscores = probs * (dprobs - jnp.sum(probs * dprobs, axis=1, keepdims=True))
                dscores = dscores.astype(LOW)
                dq += nn(dscores, own_k)
                dk += tn(dscores, own_q)
            qkv_grad[rows, lanes(0)] = (dq * scale).astype(LOW)
            qkv_grad[rows, lanes(1)] = (dk * scale).astype(LOW)
            qkv_grad[rows, lanes(2)] = dv.astype(LOW)
        return carry

    lax.fori_loop(0, HEADS_A // 2, pair, 0)


def bytes_forward_kernel(
    u_blocks,
    mixed_in,
    gains,
    gated_gain,
    pack,
    gated_out,
    local_out,
    stream_out,
    normed_out,
    qkv,
    mixed,
    after_out,
    feed_out,
    w_out0,
    w_out1,
    w_local,
    w_q,
    w_k,
    w_v,
    w_attn,
    pieces,
    sems,
):
    places = (w_out0, w_out1, w_local, w_q, w_k, w_v, w_attn)
    blocks = [4 * D, 5 * D, 6 * D, 0, D, 2 * D, 3 * D]
    waits = fetched(pack, places, blocks, sems)
    patches = mixed_in.shape[0]
    half = HEAD_M // 2
    for i in range(2):
        for first in range(0, HEADS_M, 4):
            gated_out[i, :, first * half : (first + 4) * half] = jnp.concatenate(
                [
                    u_blocks[first + j].astype(FULL)[:, i * half : (i + 1) * half]
                    for j in range(4)
                ],
                axis=1,
            )
    held = [gated_out[0], gated_out[1]]
    square = sum(jnp.sum(v * v, axis=1, keepdims=True) for v in held)
    scale = lax.rsqrt(square / (2 * D) + epsilon)
    gated = [(held[i] * scale * gated_gain[i : i + 1, :]).astype(LOW) for i in range(2)]
    waits[0]()
    waits[1]()
    joined = mixed_in[...] + nn(gated[0], w_out0[...]) + nn(gated[1], w_out1[...])
    for k in range(PATCH):
        pieces[pl.ds(k, patches, stride=PATCH), :] = joined[:, k * EMB : (k + 1) * EMB]
    local = pieces[...].astype(LOW)
    local_out[...] = local
    waits[2]()
    stream = nt(local, w_local[...])
    stream_out[...] = stream
    normed = (unit_rows(stream)[0] * gains[0:1, :]).astype(LOW)
    normed_out[...] = normed
    for i, weight in enumerate((w_q, w_k, w_v)):
        waits[3 + i]()
        for first in range(0, D, WEIGHT_STEP):
            qkv[:, i * D + first : i * D + first + WEIGHT_STEP] = nn(
                normed, weight[:, first : first + WEIGHT_STEP]
            ).astype(LOW)
    attend_pairs(qkv, mixed)
    waits[6]()
    heads = mixed[...]
    for first in range(0, D, WEIGHT_STEP):
        columns = slice(first, first + WEIGHT_STEP)
        after_out[:, columns] = stream_out[:, columns] + nn(heads, w_attn[:, columns])
    feed_out[...] = (unit_rows(after_out[...])[0] * gains[1:2, :]).astype(LOW)


def bytes_forward(u_blocks, mixed_in, gains, gated_gain, pack):
    patches = mixed_in.shape[0]
    rows = patches * PATCH

    def full(shape, kind):
        return jax.ShapeDtypeStruct(shape, kind)

    return pl.pallas_call(
        bytes_forward_kernel,
        out_shape=[
            full((2, patches, D), FULL),
            full((rows, EMB), LOW),
            full((rows, D), FULL),
            full((rows, D), LOW),
            full((rows, 3 * D), LOW),
            full((rows, D), LOW),
            full((rows, D), FULL),
            full((rows, D), LOW),
        ],
        in_specs=[in_vmem()] * 4 + [pl.BlockSpec(memory_space=pl.ANY)],
        out_specs=[in_vmem()] * 8,
        scratch_shapes=[pltpu.VMEM((D, D), LOW)] * 2
        + [pltpu.VMEM((D, EMB), LOW)]
        + [pltpu.VMEM((D, D), LOW)] * 4
        + [pltpu.VMEM((rows, EMB), FULL), pltpu.SemaphoreType.DMA((7,))],
        compiler_params=pltpu.CompilerParams(vmem_limit_bytes=48 << 20),
        name="bytes_forward",
    )(u_blocks, mixed_in, gains, gated_gain, pack)


def bytes_backward_kernel(
    narrow,
    feed_in_grad,
    cotangent,
    keep,
    after,
    stream_in,
    normed_in,
    qkv,
    mixed,
    local_in,
    gated_rows,
    gains,
    gated_gain,
    pack,
    feed_parts,
    gate_parts,
    global_out,
    mix_out,
    scale_out,
    sums,
    gain_grads,
    gated_gain_grads,
    du_blocks,
    rows_out,
    gate_out,
    w_attn,
    w_q,
    w_k,
    w_v,
    w_local,
    w_out0,
    w_out1,
    after_grad,
    heads_grad,
    qkv_grad,
    pieces,
    parts_got,
    grads,
    grads_got,
    gate_got,
    sems,
    p_send,
    p_recv,
    t_send,
    t_recv,
    gate_sems,
):
    n, wide_place = lax.axis_index(NARROW), lax.axis_index(WIDE)
    core = lax.rem(wide_place, 2)
    twin = (n, wide_place + 1 - 2 * core)
    depth = gate_parts.shape[0]
    z_place = lax.div(wide_place, 2)
    line = LineSum(
        gate_parts, gate_got, gate_sems, z_place, depth, lambda there: (n, there * 2 + core)
    )

    def twin_copy(i, columns):
        return remote(
            grads.at[:, 1 - core, :, columns],
            grads_got.at[:, :, columns],
            t_send.at[i],
            t_recv.at[i],
            twin,
        )

    def give(i, columns, part):
        grads[:, :, :, columns] = part.astype(LOW).reshape(grads.shape[:3] + part.shape[1:])
        twin_copy(i, columns).start()

    def part_copy(k):
        peer = (lax.rem(n + k, narrow), wide_place)
        return remote(feed_parts.at[k], parts_got.at[k], p_send.at[k - 1], p_recv.at[k - 1], peer)

    own_part = pltpu.make_async_copy(feed_parts.at[0], parts_got.at[0], sems.at[7])
    own_part.start()
    places = (w_attn, w_q, w_k, w_v, w_local, w_out0, w_out1)
    blocks = [3 * D, 0, D, 2 * D, 6 * D, 4 * D, 5 * D]
    waits = fetched(pack, places, blocks, sems)
    greet_lines(narrow, depth)
    line.start()
    for k in range(1, narrow):
        part_copy(k).start()
    patches = global_out.shape[0]
    unit, scale = unit_rows(after[...])
    grad = feed_in_grad[...].astype(LOW).astype(FULL)
    gain_grads[1:2, :] = jnp.sum(grad * unit, axis=0, keepdims=True)
    after_grad[...] = cotangent[...].astype(FULL) * keep[0] + norm_back(
        grad, gains[1:2, :], unit, scale
    )
    attn_grad = after_grad[...].astype(LOW)
    waits[0]()
    for first in range(0, D, WEIGHT_STEP):
        columns = slice(first, first + WEIGHT_STEP)
        heads_grad[:, columns] = nt(attn_grad, w_attn[columns, :]).astype(LOW)
        give(
            (3 * D + first) // WEIGHT_STEP,
            pl.ds(3 * D + first, WEIGHT_STEP),
            tn(mixed[...], attn_grad[:, columns]),
        )
    attend_pairs_back(qkv, heads_grad, qkv_grad)
    normed_grad = jnp.zeros(after_grad.shape, FULL)
    for i, weight in enumerate((w_q, w_k, w_v)):
        waits[1 + i]()
        normed_grad += nt(qkv_grad[:, i * D : (i + 1) * D], weight[...])
    unit, scale = unit_rows(stream_in[...])
    gain_grads[0:1, :] = jnp.sum(normed_grad * unit, axis=0, keepdims=True)
    stream_grad = (after_grad[...] + norm_back(normed_grad, gains[0:1, :], unit, scale)).astype(LOW)
    waits[4]()
    pieces[...] = nn(stream_grad, w_local[...])
    for k in range(PATCH):
        global_out[:, k * EMB : (k + 1) * EMB] = pieces[pl.ds(k, patches, stride=PATCH), :]
    mix_grad = global_out[...].astype(LOW)
    mix_out[...] = mix_grad
    waits[5]()
    waits[6]()
    inner = [nt(mix_grad, w_out0[...]), nt(mix_grad, w_out1[...])]
    held = [gated_rows[0], gated_rows[1]]
    square = sum(jnp.sum(v * v, axis=1, keepdims=True) for v in held)
    scale = lax.rsqrt(square / (2 * D) + epsilon)
    units = [v * scale for v in held]
    scaled = [inner[i] * gated_gain[i : i + 1, :] for i in range(2)]
    mean = sum(jnp.sum(scaled[i] * units[i], axis=1, keepdims=True) for i in range(2)) / (2 * D)
    for i in range(2):
        gated_gain_grads[i : i + 1, :] = jnp.sum(inner[i] * units[i], axis=0, keepdims=True)
    scale_out[...] = jnp.broadcast_to(scale, scale_out.shape)
    rows_grads = [scale * (scaled[i] - units[i] * mean) for i in range(2)]
    half = HEAD_M // 2
    for head in range(HEADS_M):
        lanes = slice(head * half, (head + 1) * half)
        du_blocks[head] = jnp.concatenate([part[:, lanes] for part in rows_grads], axis=1).astype(LOW)
    give(4 * D // WEIGHT_STEP, pl.ds(4 * D, EMB), tn(stream_grad, local_in[...]))

    def weight_grads(i, carry):
        columns = pl.ds(pl.multiple_of(i * WEIGHT_STEP, WEIGHT_STEP), WEIGHT_STEP)
        give(i, columns, tn(normed_in[...], qkv_grad[:, columns]))
        return carry

    lax.fori_loop(0, 3 * D // WEIGHT_STEP, weight_grads, 0)
    own_part.wait()
    for k in range(1, narrow):
        part_copy(k).wait_recv()
    for first in range(0, D, WEIGHT_STEP):
        columns = slice(first, first + WEIGHT_STEP)
        feed = parts_got[0, :, columns].astype(FULL)
        for k in range(1, narrow):
            feed += parts_got[k, :, columns].astype(FULL)
        feed = feed.astype(LOW).astype(FULL)
        rows_out[:, columns] = ((after[:, columns] + feed) * keep[0]).astype(LOW)

    def add_twin(i, columns):
        twin_copy(i, columns).wait_recv()
        sums[:, :, columns] = (
            grads[:, core, :, columns].astype(FULL) + grads_got[:, :, columns].astype(FULL)
        ).astype(LOW)

    def add_one(i, carry):
        add_twin(i, pl.ds(pl.multiple_of(i * WEIGHT_STEP, WEIGHT_STEP), WEIGHT_STEP))
        return carry

    def end_one(i, carry):
        twin_copy(i, pl.ds(pl.multiple_of(i * WEIGHT_STEP, WEIGHT_STEP), WEIGHT_STEP)).wait_send()
        return carry

    steps = 4 * D // WEIGHT_STEP
    add_twin(steps, pl.ds(4 * D, EMB))
    lax.fori_loop(0, steps, add_one, 0)
    line.arrive()
    gate_out[...] = line.total().astype(LOW)
    line.finish()
    twin_copy(steps, pl.ds(4 * D, EMB)).wait_send()
    lax.fori_loop(0, steps, end_one, 0)
    for k in range(1, narrow):
        part_copy(k).wait_send()


def bytes_backward(
    feed_in_grad,
    cotangent,
    keep,
    after,
    stream,
    normed,
    qkv,
    mixed,
    local,
    gated_rows,
    gains,
    gated_gain,
    pack,
    feed_parts,
    gate_parts,
    collective_id,
):
    narrow = feed_parts.shape[0]
    every = 4 * D + EMB
    rows = after.shape[0]
    patches = rows // PATCH

    def full(shape, kind):
        return jax.ShapeDtypeStruct(shape, kind)

    return pl.pallas_call(
        partial(bytes_backward_kernel, narrow),
        out_shape=[
            full((patches, D), FULL),
            full((patches, D), LOW),
            full((patches, 128), FULL),
            full((HEADS_M // 2, D // HEADS_M, every), LOW),
            full((2, D), FULL),
            full((2, D), FULL),
            full((HEADS_M, patches, HEAD_M), LOW),
            full((rows, D), LOW),
            full(gate_parts.shape[1:], LOW),
        ],
        in_specs=[in_vmem()] * 12 + [pl.BlockSpec(memory_space=pl.ANY)] * 3,
        out_specs=[in_vmem()] * 9,
        scratch_shapes=[pltpu.VMEM((D, D), LOW)] * 4
        + [pltpu.VMEM((D, EMB), LOW)]
        + [pltpu.VMEM((D, D), LOW)] * 2
        + [
            pltpu.VMEM((rows, D), FULL),
            pltpu.VMEM((rows, D), LOW),
            pltpu.VMEM((rows, 3 * D), LOW),
            pltpu.VMEM((rows, EMB), FULL),
            pltpu.VMEM((narrow, rows, D), LOW),
            pltpu.VMEM((HEADS_M // 2, 2, D // HEADS_M, every), LOW),
            pltpu.VMEM((HEADS_M // 2, D // HEADS_M, every), LOW),
            pltpu.VMEM(gate_parts.shape, LOW),
            pltpu.SemaphoreType.DMA((8,)),
            pltpu.SemaphoreType.DMA((narrow - 1,)),
            pltpu.SemaphoreType.DMA((narrow - 1,)),
            pltpu.SemaphoreType.DMA((4 * D // WEIGHT_STEP + 1,)),
            pltpu.SemaphoreType.DMA((4 * D // WEIGHT_STEP + 1,)),
            pltpu.SemaphoreType.DMA((2 * gate_parts.shape[0],)),
        ],
        compiler_params=pltpu.CompilerParams(
            collective_id=collective_id, has_side_effects=True, vmem_limit_bytes=60 << 20
        ),
        name="bytes_backward",
    )(
        feed_in_grad,
        cotangent,
        keep,
        after,
        stream,
        normed,
        qkv,
        mixed,
        local,
        gated_rows,
        gains,
        gated_gain,
        pack,
        feed_parts,
        gate_parts,
    )


def feed_kernel(narrow, x_in, g_own, g_others, keep, *refs):
    gate_in, up_in, down_in, f_out, gx_out, gate_sum, up_sum, down_sum = refs[:8]
    wg, wu, wd, x, xt, g, hid, gg, gu, sent, got = refs[8:19]
    gate_twin, up_twin, down_twin, gate_got, up_got, down_got = refs[19:25]
    w_sem, g_sem, x_sem, x_send, x_recv, r_send, r_recv, t_send, t_recv = refs[25:]
    n, wide_place = lax.axis_index(NARROW), lax.axis_index(WIDE)
    core = lax.rem(wide_place, 2)
    twin = (n, wide_place + 1 - 2 * core)
    barrier = pltpu.get_barrier_semaphore()
    pl.semaphore_signal(barrier, inc=1, device_id=twin, device_id_type=MESH)
    for k in range(1, narrow):
        peer = (lax.rem(n + k, narrow), wide_place)
        pl.semaphore_signal(barrier, inc=1, device_id=peer, device_id_type=MESH)
    places, width, share = gate_in.shape
    rows = x_in.shape[0]
    hidden = places * share
    depth = places // 2
    chunk = 2 * share
    own_x = pltpu.make_async_copy(x_in, x.at[0], x_sem)
    own_x.start()
    g_copies = [
        pltpu.make_async_copy(g_own, g.at[0], g_sem.at[0]),
        pltpu.make_async_copy(g_others, g.at[pl.ds(1, narrow - 1)], g_sem.at[1]),
    ]
    w_copies = [pltpu.make_async_copy(down_in, wd, w_sem.at[2 * places])]
    for place in range(places):
        units = slice(place * share, (place + 1) * share)
        w_copies.append(pltpu.make_async_copy(gate_in.at[place], wg.at[:, units], w_sem.at[place]))
        w_copies.append(
            pltpu.make_async_copy(up_in.at[place], wu.at[:, units], w_sem.at[places + place])
        )
    g_copies[0].start()
    for copy in w_copies:
        copy.start()
    for copy in g_copies[1:]:
        copy.start()
    pl.semaphore_wait(barrier, narrow)

    def x_copy(k):
        peer = (lax.rem(n + narrow - k, narrow), wide_place)
        return remote(x_in, x.at[k], x_send.at[k - 1], x_recv.at[k - 1], peer)

    def r_copy(k):
        peer = (lax.rem(n + k, narrow), wide_place)
        return remote(sent.at[k - 1], got.at[k - 1], r_send.at[k - 1], r_recv.at[k - 1], peer)

    for k in range(1, narrow):
        x_copy(k).start()
    own_x.wait()
    for copy in w_copies:
        copy.wait()
    for copy in g_copies:
        copy.wait()

    def block(k, carry):
        @pl.when(k > 0)
        def _():
            x_copy(k).wait_recv()

        xk = x[k]
        gk = (g[k].astype(FULL) * keep[k]).astype(LOW)
        g[k] = gk
        xt[k] = xk.T
        for first in range(0, hidden, chunk):
            units = slice(first, first + chunk)
            gate = nn(xk, wg[:, units])
            up = nn(xk, wu[:, units])
            dhid = nt(gk, wd[units, :])
            s = jax.nn.sigmoid(gate)
            act = gate * s
            hid[k, :, units] = (act * up).astype(LOW)
            gg[k, :, units] = (dhid * up * s * (1.0 + gate * (1.0 - s))).astype(LOW)
            gu[k, :, units] = (dhid * act).astype(LOW)
        ggk, guk, hidk = gg[k], gu[k], hid[k]
        for first in range(0, width, chunk):
            columns = slice(first, first + chunk)
            gx = nt(ggk, wg[columns, :]) + nt(guk, wu[columns, :])

            @pl.when(k == 0)
            def _():
                gx_out[:, columns] = gx

            @pl.when(k > 0)
            def _():
                sent[k - 1, :, columns] = gx.astype(LOW)

        @pl.when(k > 0)
        def _():
            r_copy(k).start()

        for first in range(0, width, chunk):
            columns = slice(first, first + chunk)
            f_out[k, :, columns] = nn(hidk, wd[:, columns]).astype(LOW)
        return carry

    lax.fori_loop(0, narrow, block, 0)

    def units_of(j, of_core):
        start = (2 * j + of_core) * share
        return pl.ds(pl.multiple_of(start, share), share)

    def columns_grads(left, j, of_core):
        total = jnp.zeros((width, chunk), FULL)
        for k in range(narrow):
            pair = [left[k, :, units_of(2 * j + i, of_core)] for i in range(2)]
            total += nn(xt[k], jnp.concatenate(pair, axis=1))
        return total[:, :share], total[:, share:]

    def rows_grads(j, of_core):
        lhs = hid[:, :, units_of(j, of_core)].reshape(narrow * rows, share)
        return tn(lhs, g[...].reshape(narrow * rows, width))

    outs = (gate_twin, up_twin, down_twin)
    ins = (gate_got, up_got, down_got)

    def t_copy(i, j):
        return remote(outs[i].at[j], ins[i].at[j], t_send.at[i, j], t_recv.at[i, j], twin)

    def for_twin(j, carry):
        for i, left in enumerate((gg, gu)):
            for half, part in enumerate(columns_grads(left, j, 1 - core)):
                outs[i][2 * j + half] = part.astype(LOW)
                t_copy(i, 2 * j + half).start()
        for half in range(2):
            outs[2][2 * j + half] = rows_grads(2 * j + half, 1 - core).astype(LOW)
            t_copy(2, 2 * j + half).start()
        return carry

    def for_own(j, carry):
        for i, (left, total) in enumerate(((gg, gate_sum), (gu, up_sum))):
            for half, part in enumerate(columns_grads(left, j, core)):
                t_copy(i, 2 * j + half).wait_recv()
                total[2 * j + half] = (part + ins[i][2 * j + half].astype(FULL)).astype(LOW)
        for half in range(2):
            part = rows_grads(2 * j + half, core)
            t_copy(2, 2 * j + half).wait_recv()
            down_sum[2 * j + half] = (part + ins[2][2 * j + half].astype(FULL)).astype(LOW)
        return carry

    lax.fori_loop(0, depth // 2, for_twin, 0)
    lax.fori_loop(0, depth // 2, for_own, 0)
    for k in range(1, narrow):
        r_copy(k).wait_recv()
        gx_out[...] += got[k - 1].astype(FULL)
    for k in range(1, narrow):
        x_copy(k).wait_send()
        r_copy(k).wait_send()
    for i in range(3):
        for j in range(depth):
            t_copy(i, j).wait_send()


def feed_forward_back(x_own, g_own, g_others, keep, gate_all, up_all, down_all, collective_id):
    narrow = keep.shape[0]
    rows, width = x_own.shape
    places, _, share = gate_all.shape
    hidden, depth = places * share, places // 2
    dma = pltpu.SemaphoreType.DMA
    anywhere = pl.BlockSpec(memory_space=pl.ANY)

    def low(*shape):
        return pltpu.VMEM(shape, LOW)

    sums = [(depth, width, share), (depth, width, share), (depth, share, width)]
    return pl.pallas_call(
        partial(feed_kernel, narrow),
        out_shape=[
            jax.ShapeDtypeStruct((narrow, rows, width), LOW),
            jax.ShapeDtypeStruct((rows, width), FULL),
        ]
        + [jax.ShapeDtypeStruct(shape, LOW) for shape in sums],
        in_specs=[anywhere] * 3 + [in_vmem()] + [anywhere] * 3,
        out_specs=[in_vmem()] * 5,
        scratch_shapes=[
            low(width, hidden),
            low(width, hidden),
            low(hidden, width),
            low(narrow, rows, width),
            low(narrow, width, rows),
            low(narrow, rows, width),
            low(narrow, rows, hidden),
            low(narrow, rows, hidden),
            low(narrow, rows, hidden),
            low(narrow - 1, rows, width),
            low(narrow - 1, rows, width),
        ]
        + [low(*shape) for shape in sums + sums]
        + [
            dma((2 * places + 1,)),
            dma((2,)),
            dma,
            dma((narrow - 1,)),
            dma((narrow - 1,)),
            dma((narrow - 1,)),
            dma((narrow - 1,)),
            dma((3, depth)),
            dma((3, depth)),
        ],
        compiler_params=pltpu.CompilerParams(
            collective_id=collective_id, has_side_effects=True, vmem_limit_bytes=44 << 20
        ),
        name="feed",
    )(x_own, g_own, g_others, keep, gate_all, up_all, down_all)


def per_device_heads(
    byte_ids,
    doc_patches,
    pad_bytes,
    byte_table,
    patch_weight,
    gain_mix,
    in_weight,
    conv_weight,
    conv_bias,
    step_bias,
    log_rate,
    skip_gain,
    gated_gain,
    out_weight,
    local_weight,
    gain_attn,
    query_weight,
    key_weight,
    value_weight,
    attn_weight,
    feed_gain,
    gate_weight,
    up_weight,
    down_weight,
    cotangent,
):
    narrow, wide = lax.axis_size(NARROW), lax.axis_size(WIDE)
    devices = narrow * wide
    device = lax.axis_index(BOTH)
    rows = byte_ids.shape[0]
    patches = rows // PATCH
    everything = devices * patches
    own_rows = patch_weight.shape[0]
    hidden_width = gate_weight.shape[1]
    share = hidden_width // narrow

    ids_low = byte_ids.astype(LOW).reshape(patches, PATCH)
    bcdt_width = 2 * STATE + HEADS_M
    start_pack = jnp.concatenate(
        [
            jnp.pad(in_weight[:, 2 * DI :], ((0, 0), (0, 96))),
            jnp.pad(ids_low, ((0, 0), (0, 120))),
            patch_weight,
        ],
        axis=1,
    )
    xz_blocks = jnp.concatenate(
        [
            in_weight[:, DI : 2 * DI].reshape(own_rows, HEADS_M, HEAD_M),
            in_weight[:, :DI].reshape(own_rows, HEADS_M, HEAD_M),
        ],
        axis=2,
    ).transpose(1, 0, 2)
    middle_pack = jnp.concatenate(
        [
            query_weight,
            key_weight,
            value_weight,
            attn_weight,
            out_weight[:own_rows],
            out_weight[own_rows:],
            local_weight.T,
        ],
        axis=1,
    )
    start_all, table_all, xz_weight, *turned, middle_line, others = start_weights(
        start_pack,
        byte_table,
        xz_blocks,
        gate_weight,
        up_weight,
        down_weight,
        middle_pack,
        cotangent,
        0,
    )
    numbers = (step_bias, log_rate, skip_gain)
    conv = (conv_weight, conv_bias[None])
    front, gate_all, up_all, down_all, middle_all = mixer_front(
        (doc_patches, pad_bytes) + numbers,
        start_all,
        table_all,
        xz_weight,
        gain_mix[None],
        *conv,
        turned,
        middle_line,
        5,
    )
    embedded, normed_all, xz, bc, dt, u, y, states, mixed_in, u_blocks, marks, keep_rows, keep_all = front
    half = HEAD_M // 2
    gated_gain_split = gated_gain.reshape(devices, 2, half).transpose(1, 0, 2).reshape(2, D)

    byte_gains = jnp.stack([gain_attn, feed_gain])
    (
        gated_rows,
        local_rows,
        stream,
        normed_attn,
        qkv,
        mixed_heads,
        after_attn,
        normed_feed,
    ) = bytes_forward(u_blocks, mixed_in, byte_gains, gated_gain_split, middle_all)
    feed_parts, feed_in_grad, gate_parts, up_parts, down_parts = feed_forward_back(
        normed_feed, cotangent, others, keep_rows, gate_all, up_all, down_all, 2
    )

    (
        global_grad,
        mix_grad,
        gated_scale,
        middle_parts,
        byte_gain_grads,
        gated_gain_grads,
        du_blocks,
        out_rows,
        gate_sum,
    ) = bytes_backward(
        feed_in_grad,
        cotangent,
        keep_rows,
        after_attn,
        stream,
        normed_attn,
        qkv,
        mixed_heads,
        local_rows,
        gated_rows,
        byte_gains,
        gated_gain_split,
        middle_all,
        feed_parts,
        gate_parts,
        4,
    )
    middle_parts = middle_parts.reshape(narrow, wide // 2, own_rows, -1)

    (
        end_pack,
        sums_pack,
        bcdt_grads,
        xz_grads,
        up_sum,
        down_sum,
        middle_sums,
        grad_gate,
        mix_grad_all,
    ) = mixer_backward(
        numbers,
        xz,
        bc,
        dt,
        marks,
        *conv,
        y,
        states,
        normed_all,
        xz_weight,
        start_all,
        mixed_in,
        global_grad,
        gain_mix[None],
        gated_scale,
        byte_gain_grads,
        gated_gain_grads,
        du_blocks,
        up_parts,
        down_parts,
        middle_parts,
        gate_sum,
        mix_grad,
        3,
    )
    mix_grad_all = mix_grad_all.reshape(everything, D)

    end_all, sums_all, middle_sums, grad_up, grad_down = end_gather(
        end_pack, sums_pack, middle_sums, up_sum, down_sum, 1
    )
    (
        grad_table,
        grad_patch,
        grad_in,
        grad_out,
        grad_local,
        grad_query,
        grad_key,
        grad_value,
        grad_attn,
    ) = finish(
        end_all,
        mix_grad_all,
        u,
        keep_all,
        middle_sums,
        xz_grads,
        bcdt_grads,
        gated_gain[None],
        embedded,
        start_all,
    )
    small = jnp.sum(sums_all[:, :SUM_ROWS], axis=0).reshape(-1)
    gain_grads = jnp.split(small[: 3 * D + DI], [D, D + DI, 2 * D + DI])
    gain_grads[1] = gain_grads[1].reshape(2, devices, half).transpose(1, 0, 2).reshape(DI)
    conv_own = sums_all[:, SUM_ROWS : SUM_ROWS + CONV + 1, :HEAD_M].transpose(1, 0, 2)
    conv_grads = jnp.concatenate(
        [conv_own.reshape(CONV + 1, DI), small[3 * D + DI :].reshape(CONV + 1, 2 * STATE)], axis=1
    )
    number_grads = sums_all[:, SUM_ROWS + CONV + 1, :3].T
    return (
        out_rows,
        grad_table,
        grad_patch,
        gain_grads[0],
        grad_in,
        conv_grads[:CONV],
        conv_grads[CONV],
        number_grads[0],
        number_grads[1],
        number_grads[2],
        gain_grads[1],
        grad_out,
        grad_local,
        gain_grads[2],
        grad_query,
        grad_key,
        grad_value,
        grad_attn,
        gain_grads[3],
        grad_gate,
        grad_up,
        grad_down,
    )


def solution(mesh):
    placed = (
        P((NARROW, WIDE)),
        P(),
        P(),
        P((NARROW, WIDE), None),
        P((NARROW, WIDE), None),
        P(),
        P((NARROW, WIDE), None),
        P(),
        P(),
        P(),
        P(),
        P(),
        P(),
        P((NARROW, WIDE), None),
        P(None, (NARROW, WIDE)),
        P(),
        P((NARROW, WIDE), None),
        P((NARROW, WIDE), None),
        P((NARROW, WIDE), None),
        P((NARROW, WIDE), None),
        P(),
        P(NARROW, WIDE),
        P(NARROW, WIDE),
        P(WIDE, NARROW),
        P((NARROW, WIDE), None),
    )
    return jax.shard_map(
        per_device_heads if mesh.size == HEADS_M else per_device_rows,
        mesh=mesh,
        in_specs=placed,
        out_specs=(
            P((NARROW, WIDE), None),
            P((NARROW, WIDE), None),
            P((NARROW, WIDE), None),
            P(),
            P((NARROW, WIDE), None),
            P(),
            P(),
            P(),
            P(),
            P(),
            P(),
            P((NARROW, WIDE), None),
            P(None, (NARROW, WIDE)),
            P(),
            P((NARROW, WIDE), None),
            P((NARROW, WIDE), None),
            P((NARROW, WIDE), None),
            P((NARROW, WIDE), None),
            P(),
            P(NARROW, WIDE),
            P(NARROW, WIDE),
            P(WIDE, NARROW),
        ),
        check_vma=False,
    )
```

```python
from functools import partial

import jax
import jax.numpy as jnp
from jax import lax
from jax.experimental import pallas as pl
from jax.experimental.pallas import tpu as pltpu
from jax.sharding import PartitionSpec as P

NARROW = "narrow"
WIDE = "wide"
D = 1024
PATCH = 8
EMB = 128
VOCAB = 256
HEADS_M = 32
HEAD_M = 64
DI = 2048
STATE = 128
CONV = 4
HEADS_A = 16
HEAD_A = 64


epsilon = 1e-05
highest = lax.Precision.HIGHEST
masked_score = -1e30


def running_sum(x):
    place = jnp.arange(x.shape[0])
    seen = place[:, None] >= place[None, :]
    if x.ndim == 1:
        return jnp.sum(jnp.where(seen, x[None, :], 0), axis=1).astype(x.dtype)
    return jnp.dot(seen.astype(x.dtype), x, precision=highest)


def passed_along(x, axis, by):
    peers = lax.axis_size(axis)
    pairs = [(i, i + by) for i in range(peers) if 0 <= i + by < peers]
    return lax.ppermute(x, axis, pairs)


def prefix_2(x, axis, join, neutral):
    place = lax.axis_index(axis)
    gathered = jax.tree.map(
        lambda a, kind: lax.all_gather(a.astype(kind), axis), x, (jnp.bfloat16, jnp.bfloat16)
    )
    state = jax.tree.map(lambda a, e: jnp.zeros_like(a) + jnp.asarray(e, a.dtype), x, neutral)

    def prefix_one(hop, state):
        return join(
            state,
            jax.tree.map(
                lambda a, own: lax.dynamic_index_in_dim(a, hop, 0, False).astype(own.dtype),
                gathered,
                x,
            ),
        )

    return lax.fori_loop(0, place, prefix_one, state)


def carried_in_2(x, axis, join, neutral):
    count = lax.axis_size(axis)
    place = lax.axis_index(axis)
    ahead = count - 1 - place
    gathered = jax.tree.map(
        lambda a, kind: lax.all_gather(a.astype(kind), axis),
        x,
        jax.tree.map(lambda a: jnp.bfloat16 if a.dtype == jnp.float32 else a.dtype, x),
    )
    state = jax.tree.map(lambda a, e: jnp.zeros_like(a) + jnp.asarray(e, a.dtype), x, neutral)

    def carried_one(hop, state):
        source = count - 1 - hop
        return join(
            state,
            jax.tree.map(
                lambda a, own: lax.dynamic_index_in_dim(a, source, 0, False).astype(own.dtype),
                gathered,
                x,
            ),
        )

    return lax.fori_loop(0, ahead, carried_one, state)


def root_norm(values, gain):
    return values * lax.rsqrt(jnp.mean(values * values, axis=-1, keepdims=True) + epsilon) * gain


def patch_layout(doc_patches, pad_bytes, first_index, patch_count):
    patch_index = first_index + jnp.arange(patch_count, dtype=jnp.int32)
    doc_ends = running_sum(doc_patches)
    doc_index = jnp.arange(doc_patches.shape[0], dtype=jnp.int32)
    segment = jnp.sum((patch_index[:, None] >= doc_ends[None, :]).astype(jnp.int32), axis=1)
    owner_mask = segment[:, None] == doc_index[None, :]
    last_end = jnp.sum(jnp.where(owner_mask, doc_ends[None, :] - 1, 0), axis=1)
    doc_starts = jnp.sum(jnp.where(owner_mask, (doc_ends - doc_patches)[None, :], 0), axis=1)
    pad_count = jnp.sum(jnp.where(owner_mask, pad_bytes[None, :], 0), axis=1)
    offset = jnp.arange(PATCH, dtype=jnp.int32)
    padded = (patch_index == last_end)[:, None] & (offset[None, :] >= PATCH - pad_count[:, None])
    keep_mask = 1.0 - padded.astype(jnp.float32).reshape(-1)
    return (segment, (patch_index == doc_starts).astype(jnp.int32), keep_mask)


def ssd_terms(layout, projected, rim_rows, small_params):
    conv_weight, conv_bias, step_bias, log_rate, skip_gain = small_params
    segment, rim_segment, first_patch = layout
    conv_in = projected[:, DI : 2 * DI + 2 * STATE]
    patch_count = conv_in.shape[0]
    padded = jnp.concatenate([rim_rows, conv_in], 0)
    padded_seg = jnp.concatenate([rim_segment, segment], 0)
    conv_sum = conv_bias
    for conv_tap in range(CONV):
        same_doc = (padded_seg[conv_tap : conv_tap + patch_count] == segment).astype(jnp.float32)[
            :, None
        ]
        conv_sum = (
            conv_sum + conv_weight[conv_tap] * padded[conv_tap : conv_tap + patch_count] * same_doc
        )
    activated = jax.nn.silu(conv_sum)
    values = activated[:, :DI].reshape(patch_count, HEADS_M, HEAD_M)
    input_map = activated[:, DI : DI + STATE]
    output_map = activated[:, DI + STATE :]
    time_steps = jax.nn.softplus(projected[:, 2 * DI + 2 * STATE :] + step_bias)
    cumulative = running_sum(-time_steps * jnp.exp(log_rate))
    no_reset = (running_sum(first_patch) == 0).astype(jnp.float32)
    return (values, input_map, output_map, time_steps, cumulative, no_reset)


def local_state(layout, projected, rim_rows, small_params):
    values, input_map, output_map, time_steps, cumulative, no_reset = ssd_terms(
        layout, projected, rim_rows, small_params
    )
    segment = layout[0]
    decay_tail = (
        jnp.exp(cumulative[-1][None, :] - cumulative)
        * (segment == segment[-1]).astype(jnp.float32)[:, None]
        * time_steps
    )
    state_local = jnp.einsum("sh,shp,sn->hpn", decay_tail, values, input_map, precision=highest)
    decay_total = jnp.exp(cumulative[-1]) * no_reset[-1]
    return (decay_total, state_local)


def mixer_output(layout, projected, rim_rows, small_params, incoming, gated_gain):
    values, input_map, output_map, time_steps, cumulative, no_reset = ssd_terms(
        layout, projected, rim_rows, small_params
    )
    segment = layout[0]
    patch_count = values.shape[0]
    position = jnp.arange(patch_count)
    visible = (segment[:, None] == segment[None, :]) & (position[:, None] >= position[None, :])
    log_gap = jnp.where(visible[:, :, None], cumulative[:, None, :] - cumulative[None, :, :], 0.0)
    inner = jnp.dot(output_map, input_map.T, precision=highest)
    weight = (
        jnp.exp(log_gap)
        * visible[:, :, None].astype(jnp.float32)
        * time_steps[None, :, :]
        * inner[:, :, None]
    )
    within = jnp.einsum("tsh,shp->thp", weight, values, precision=highest)
    carried_in = (
        jnp.einsum("tn,hpn->thp", output_map, incoming, precision=highest)
        * (jnp.exp(cumulative) * no_reset[:, None])[:, :, None]
    )
    result = (within + carried_in + small_params[4][None, :, None] * values).reshape(
        patch_count, DI
    )
    gated_rows = result * jax.nn.silu(projected[:, :DI])
    return root_norm(gated_rows, gated_gain)


def combine_states(earlier, following):
    return (earlier[0] * following[0], following[0][:, None, None] * earlier[1] + following[1])


def attend(stream, gain_attn, query_all, key_all, value_all):
    head_shape = (-1, PATCH, HEADS_A, HEAD_A)
    normed_attn = root_norm(stream, gain_attn).astype(jnp.bfloat16)
    queries = jnp.dot(normed_attn, query_all, preferred_element_type=jnp.float32).astype(
        jnp.bfloat16
    )
    key_rows = jnp.dot(normed_attn, key_all, preferred_element_type=jnp.float32).astype(
        jnp.bfloat16
    )
    value_rows = jnp.dot(normed_attn, value_all, preferred_element_type=jnp.float32).astype(
        jnp.bfloat16
    )
    scores = jnp.einsum(
        "pqhe,pkhe->phqk",
        queries.reshape(head_shape),
        key_rows.reshape(head_shape),
        preferred_element_type=jnp.float32,
    ) * HEAD_A ** (-0.5)
    position = jnp.arange(PATCH)
    causal = position[:, None] >= position[None, :]
    attn_probs = jax.nn.softmax(jnp.where(causal, scores, masked_score), axis=-1)
    mixed_heads = jnp.einsum(
        "phqk,pkhe->pqhe",
        attn_probs.astype(jnp.bfloat16),
        value_rows.reshape(head_shape),
        preferred_element_type=jnp.float32,
    )
    mixed_heads = mixed_heads.reshape(stream.shape[0], -1).astype(jnp.bfloat16)
    return (normed_attn, queries, key_rows, value_rows, attn_probs, mixed_heads)


def spread(values):
    by_rows = lax.all_to_all(values, NARROW, split_axis=1, concat_axis=0, tiled=True)
    return lax.all_gather(by_rows, WIDE, axis=0, tiled=True)


def collect(term_fn, row_count):
    summed = lax.psum_scatter(
        term_fn(jnp.int32(0), row_count * lax.axis_size(WIDE)).astype(jnp.bfloat16),
        WIDE,
        scatter_dimension=0,
        tiled=True,
    )
    return lax.all_to_all(summed, NARROW, split_axis=0, concat_axis=1, tiled=True)


def narrow_total(partial_rows):
    return lax.psum(partial_rows, NARROW).astype(jnp.float32)


def silu_back(gate_up, hidden_grad, hidden_width):
    gate_rows = gate_up[:, :hidden_width]
    up_rows = gate_up[:, hidden_width:]
    sigmoid = jax.nn.sigmoid(gate_rows)
    gate_grad = hidden_grad * up_rows * sigmoid * (1.0 + gate_rows * (1.0 - sigmoid))
    up_grad = hidden_grad * gate_rows * sigmoid
    return jnp.concatenate([gate_grad, up_grad], axis=1)


def per_device_rows(
    byte_ids,
    doc_patches,
    pad_bytes,
    byte_table,
    patch_weight,
    gain_mix,
    in_weight,
    conv_weight,
    conv_bias,
    step_bias,
    log_rate,
    skip_gain,
    gated_gain,
    out_weight,
    local_weight,
    gain_attn,
    query_weight,
    key_weight,
    value_weight,
    attn_weight,
    feed_gain,
    gate_weight,
    up_weight,
    down_weight,
    cotangent,
):
    byte_rows = byte_ids.shape[0]
    patches = byte_rows // PATCH
    device = lax.axis_index((NARROW, WIDE))
    wide_count = lax.axis_size(WIDE)
    segment, first_patch, keep_mask = patch_layout(
        doc_patches, pad_bytes, device * patches, patches
    )
    rim_segment = patch_layout(doc_patches, pad_bytes, device * patches - (CONV - 1), CONV - 1)[0]
    layout = (segment, rim_segment, first_patch)
    gathered = (
        lax.all_gather(byte_table, (NARROW, WIDE), axis=0, tiled=True),
        lax.all_gather(patch_weight, (NARROW, WIDE), axis=0, tiled=True),
        lax.all_gather(in_weight, (NARROW, WIDE), axis=0, tiled=True),
        lax.all_gather(out_weight, (NARROW, WIDE), axis=0, tiled=True),
        lax.all_gather(local_weight, (NARROW, WIDE), axis=1, tiled=True),
        lax.all_gather(query_weight, (NARROW, WIDE), axis=0, tiled=True),
        lax.all_gather(key_weight, (NARROW, WIDE), axis=0, tiled=True),
        lax.all_gather(value_weight, (NARROW, WIDE), axis=0, tiled=True),
        lax.all_gather(attn_weight, (NARROW, WIDE), axis=0, tiled=True),
    )
    table_all, patch_all, in_all, out_all, local_all, query_all, key_all, value_all, attn_all = (
        gathered
    )
    onehot = (byte_ids[:, None] == jnp.arange(VOCAB, dtype=jnp.int32)[None, :]).astype(jnp.bfloat16)
    embedded = (
        (jnp.dot(onehot, table_all, preferred_element_type=jnp.float32) * keep_mask[:, None])
        .astype(jnp.bfloat16)
        .reshape(patches, D)
    )
    mixed_in = jnp.dot(embedded, patch_all, preferred_element_type=jnp.float32)
    normed_mix = root_norm(mixed_in, gain_mix).astype(jnp.bfloat16)
    projected = jnp.dot(normed_mix, in_all, preferred_element_type=jnp.float32).astype(jnp.bfloat16)
    rim_rows = passed_along(
        projected[patches - (CONV - 1) :, DI : 2 * DI + 2 * STATE], (NARROW, WIDE), 1
    ).astype(jnp.float32)
    projected_f = projected.astype(jnp.float32)
    small_params = (conv_weight, conv_bias, step_bias, log_rate, skip_gain)
    (decay_total, state_local), state_back = jax.vjp(
        partial(local_state, layout), projected_f, rim_rows, small_params
    )
    prefix = prefix_2(
        (decay_total, state_local),
        (NARROW, WIDE),
        combine_states,
        (jnp.ones_like(decay_total), jnp.zeros_like(state_local)),
    )
    incoming = prefix[1]
    gated_norm, mixer_back = jax.vjp(
        partial(mixer_output, layout), projected_f, rim_rows, small_params, incoming, gated_gain
    )
    gated_low = gated_norm.astype(jnp.bfloat16)
    global_out = mixed_in + jnp.dot(gated_low, out_all, preferred_element_type=jnp.float32)
    local_rows = global_out.astype(jnp.bfloat16).reshape(byte_rows, EMB)
    stream = jnp.dot(local_rows, local_all, preferred_element_type=jnp.float32)
    normed_attn, queries, key_rows, value_rows, attn_probs, mixed_heads = attend(
        stream, gain_attn, query_all, key_all, value_all
    )
    after_attn = stream + jnp.dot(mixed_heads, attn_all, preferred_element_type=jnp.float32)
    normed_feed = root_norm(after_attn, feed_gain).astype(jnp.bfloat16)
    out_grad = cotangent.astype(jnp.float32) * keep_mask[:, None]
    feed_grad = out_grad.astype(jnp.bfloat16)
    grid_in = spread(normed_feed)
    both_weights = jnp.concatenate([gate_weight, up_weight], axis=1)
    hidden_width = gate_weight.shape[1]
    grid_share = grid_in.shape[0] // wide_count
    gate_up_part = jnp.dot(grid_in, both_weights, preferred_element_type=jnp.float32).astype(
        jnp.bfloat16
    )
    gate_up = narrow_total(gate_up_part)
    hidden = (jax.nn.silu(gate_up[:, :hidden_width]) * gate_up[:, hidden_width:]).astype(
        jnp.bfloat16
    )

    def down_term(first_row, row_count):
        return jnp.dot(hidden, down_weight, preferred_element_type=jnp.float32)

    feed_out = collect(down_term, grid_share)
    grid_grad = spread(feed_grad)
    grad_down = jnp.einsum("gf,gd->fd", hidden, grid_grad, preferred_element_type=jnp.float32)
    hidden_part = jnp.einsum(
        "gd,fd->gf", grid_grad, down_weight, preferred_element_type=jnp.float32
    ).astype(jnp.bfloat16)
    hidden_grad = narrow_total(hidden_part)
    gate_up_grad = silu_back(gate_up, hidden_grad, hidden_width).astype(jnp.bfloat16)
    grad_both = jnp.einsum("gd,gf->df", grid_in, gate_up_grad, preferred_element_type=jnp.float32)

    def back_term(first_row, row_count):
        return jnp.einsum(
            "gf,df->gd", gate_up_grad, both_weights, preferred_element_type=jnp.float32
        )

    feed_in_grad = collect(back_term, grid_share)
    grad_gate = grad_both[:, :hidden_width]
    grad_up = grad_both[:, hidden_width:]
    after_feed = after_attn + feed_out.astype(jnp.float32)
    out_rows = (after_feed * keep_mask[:, None]).astype(jnp.bfloat16)
    feed_normed, feed_norm_back = jax.vjp(root_norm, after_attn, feed_gain)
    after_norm_grad, grad_feed_gain = feed_norm_back(feed_in_grad.astype(jnp.float32))
    after_grad = out_grad + after_norm_grad
    head_shape = (-1, PATCH, HEADS_A, HEAD_A)
    score_scale = HEAD_A ** (-0.5)
    attn_grad = after_grad.astype(jnp.bfloat16)
    grad_attn = jnp.einsum("rd,re->de", mixed_heads, attn_grad, preferred_element_type=jnp.float32)
    heads_grad = (
        jnp.einsum("re,de->rd", attn_grad, attn_all, preferred_element_type=jnp.float32)
        .astype(jnp.bfloat16)
        .reshape(head_shape)
    )
    probs_grad = jnp.einsum(
        "pqhe,pkhe->phqk",
        heads_grad,
        value_rows.reshape(head_shape),
        preferred_element_type=jnp.float32,
    )
    value_grad = (
        jnp.einsum(
            "phqk,pqhe->pkhe",
            attn_probs.astype(jnp.bfloat16),
            heads_grad,
            preferred_element_type=jnp.float32,
        )
        .reshape(byte_rows, D)
        .astype(jnp.bfloat16)
    )
    score_grad = (
        attn_probs * (probs_grad - jnp.sum(attn_probs * probs_grad, axis=-1, keepdims=True))
    ).astype(jnp.bfloat16)
    query_grad = (
        (
            jnp.einsum(
                "phqk,pkhe->pqhe",
                score_grad,
                key_rows.reshape(head_shape),
                preferred_element_type=jnp.float32,
            )
            * score_scale
        )
        .reshape(byte_rows, D)
        .astype(jnp.bfloat16)
    )
    key_grad = (
        (
            jnp.einsum(
                "phqk,pqhe->pkhe",
                score_grad,
                queries.reshape(head_shape),
                preferred_element_type=jnp.float32,
            )
            * score_scale
        )
        .reshape(byte_rows, D)
        .astype(jnp.bfloat16)
    )
    grad_query = jnp.einsum(
        "rd,re->de", normed_attn, query_grad, preferred_element_type=jnp.float32
    )
    grad_key = jnp.einsum("rd,re->de", normed_attn, key_grad, preferred_element_type=jnp.float32)
    grad_value = jnp.einsum(
        "rd,re->de", normed_attn, value_grad, preferred_element_type=jnp.float32
    )
    normed_grad = jnp.einsum("re,de->rd", query_grad, query_all, preferred_element_type=jnp.float32)
    normed_grad = normed_grad + jnp.einsum(
        "re,de->rd", key_grad, key_all, preferred_element_type=jnp.float32
    )
    normed_grad = normed_grad + jnp.einsum(
        "re,de->rd", value_grad, value_all, preferred_element_type=jnp.float32
    )
    attn_normed, attn_norm_back = jax.vjp(root_norm, stream, gain_attn)
    stream_norm_grad, grad_gain_attn = attn_norm_back(normed_grad)
    stream_grad = (after_grad + stream_norm_grad).astype(jnp.bfloat16)
    grad_local = jnp.einsum(
        "re,rd->ed", local_rows, stream_grad, preferred_element_type=jnp.float32
    )
    global_grad = jnp.einsum(
        "rd,ed->re", stream_grad, local_all, preferred_element_type=jnp.float32
    ).reshape(patches, D)
    mix_grad = global_grad.astype(jnp.bfloat16)
    grad_out = jnp.einsum("pi,pd->id", gated_low, mix_grad, preferred_element_type=jnp.float32)
    gated_grad = jnp.einsum("pd,id->pi", mix_grad, out_all, preferred_element_type=jnp.float32)
    proj_grad_mix, rim_grad_mix, small_grad_mix, incoming_grad, grad_gated_gain = mixer_back(
        gated_grad
    )
    suffix = carried_in_2(
        (decay_total, incoming_grad),
        (NARROW, WIDE),
        combine_states,
        (jnp.ones_like(decay_total), jnp.zeros_like(incoming_grad)),
    )
    later_grad = suffix[1]
    decay_grad = jnp.sum(later_grad * incoming, axis=(1, 2))
    proj_grad_state, rim_grad_state, small_grad_state = state_back((decay_grad, later_grad))
    rim_from_next = passed_along(rim_grad_mix + rim_grad_state, (NARROW, WIDE), -1)
    proj_grad = proj_grad_mix + proj_grad_state
    proj_grad = proj_grad.at[patches - (CONV - 1) :, DI : 2 * DI + 2 * STATE].add(rim_from_next)
    proj_low = proj_grad.astype(jnp.bfloat16)
    grad_in = jnp.einsum("pd,pk->dk", normed_mix, proj_low, preferred_element_type=jnp.float32)
    normed_mix_grad = jnp.einsum("pk,dk->pd", proj_low, in_all, preferred_element_type=jnp.float32)
    mix_normed, mix_norm_back = jax.vjp(root_norm, mixed_in, gain_mix)
    mixed_norm_grad, grad_gain_mix = mix_norm_back(normed_mix_grad)
    embed_grad = (global_grad + mixed_norm_grad).astype(jnp.bfloat16)
    grad_patch = jnp.einsum("pi,pd->id", embedded, embed_grad, preferred_element_type=jnp.float32)
    byte_grad = (
        jnp.einsum("pd,id->pi", embed_grad, patch_all, preferred_element_type=jnp.float32).reshape(
            byte_rows, EMB
        )
        * keep_mask[:, None]
    )
    grad_table = jnp.dot(onehot.astype(jnp.float32).T, byte_grad, precision=highest)
    shared = (
        lax.psum_scatter(grad_table, (NARROW, WIDE), scatter_dimension=0, tiled=True),
        lax.psum_scatter(grad_patch, (NARROW, WIDE), scatter_dimension=0, tiled=True),
        lax.psum_scatter(grad_in, (NARROW, WIDE), scatter_dimension=0, tiled=True),
        lax.psum_scatter(grad_out, (NARROW, WIDE), scatter_dimension=0, tiled=True),
        lax.psum_scatter(grad_local, (NARROW, WIDE), scatter_dimension=1, tiled=True),
        lax.psum_scatter(grad_query, (NARROW, WIDE), scatter_dimension=0, tiled=True),
        lax.psum_scatter(grad_key, (NARROW, WIDE), scatter_dimension=0, tiled=True),
        lax.psum_scatter(grad_value, (NARROW, WIDE), scatter_dimension=0, tiled=True),
        lax.psum_scatter(grad_attn, (NARROW, WIDE), scatter_dimension=0, tiled=True),
    )
    small_sum = lax.psum(
        (
            small_grad_mix[0] + small_grad_state[0],
            small_grad_mix[1] + small_grad_state[1],
            small_grad_mix[2] + small_grad_state[2],
            small_grad_mix[3] + small_grad_state[3],
            small_grad_mix[4] + small_grad_state[4],
            grad_gain_mix,
            grad_gated_gain,
            grad_gain_attn,
            grad_feed_gain,
        ),
        (NARROW, WIDE),
    )
    return (
        out_rows,
        shared[0],
        shared[1],
        small_sum[5],
        shared[2],
        small_sum[0],
        small_sum[1],
        small_sum[2],
        small_sum[3],
        small_sum[4],
        small_sum[6],
        shared[3],
        shared[4],
        small_sum[7],
        shared[5],
        shared[6],
        shared[7],
        shared[8],
        small_sum[8],
        grad_gate,
        grad_up,
        grad_down,
    )


QUERY = 128
BYTE_BLOCK = 128
MESH = pl.DeviceIdType.MESH
SUM_ROWS = (3 * D + DI + (CONV + 1) * 2 * STATE) // 128
LOW = jnp.bfloat16
FULL = jnp.float32
BOTH = (NARROW, WIDE)


def nn(a, b, precision=None):
    return lax.dot_general(
        a, b, (((1,), (0,)), ((), ())), precision=precision, preferred_element_type=FULL
    )


def nt(a, b, precision=None):
    return lax.dot_general(
        a, b, (((1,), (1,)), ((), ())), precision=precision, preferred_element_type=FULL
    )


def tn(a, b, precision=None):
    return lax.dot_general(
        a, b, (((0,), (0,)), ((), ())), precision=precision, preferred_element_type=FULL
    )


def device_at(place, wide):
    return (lax.div(place, wide), lax.rem(place, wide))


def remote(src, dst, send, recv, peer):
    return pltpu.make_async_remote_copy(
        src_ref=src, dst_ref=dst, send_sem=send, recv_sem=recv, device_id=peer, device_id_type=MESH
    )


def greet_all(devices, wide):
    me = lax.axis_index(NARROW) * wide + lax.axis_index(WIDE)
    barrier = pltpu.get_barrier_semaphore()

    def greet(k, carry):
        peer = device_at(lax.rem(me + k, devices), wide)
        pl.semaphore_signal(barrier, inc=1, device_id=peer, device_id_type=MESH)
        return carry

    lax.fori_loop(1, devices, greet, 0)
    return me, lambda: pl.semaphore_wait(barrier, devices - 1)


def send_blocks(me, devices, wide, src, dst, send, recv):
    def one(k, carry):
        place = lax.rem(me + k, devices)
        remote(src.at[place], dst.at[me], send, recv, device_at(place, wide)).start()
        return carry

    lax.fori_loop(1, devices, one, 0)


def wait_blocks(me, devices, wide, dst, send, recv):
    part = dst.at[pl.ds(0, devices - 1)]
    remote(part, part, send, recv, device_at(me, wide)).wait()


class StagedGather:
    def __init__(self, block, out, sems, narrow, depth):
        n, w = lax.axis_index(NARROW), lax.axis_index(WIDE)
        z, c = lax.div(w, 2), lax.rem(w, 2)
        self.out, self.narrow, self.depth = out, narrow, depth
        self.n, self.c = n, c
        self.sems = [sems.at[i] for i in range(7)]
        self.twin = (n, z * 2 + 1 - c)
        self.n_peers = [lax.rem(n + k, narrow) for k in range(1, narrow)]
        self.w = w
        self.own = pltpu.make_async_copy(block, out.at[n, z, c], self.sems[0])
        self.first = [
            remote(
                block,
                out.at[n, z, c],
                self.sems[1],
                self.sems[2],
                (n, lax.rem(z + k, depth) * 2 + c),
            )
            for k in range(1, depth)
        ]

    def wait_for(self, part, i):
        return remote(part, part, self.sems[i], self.sems[i + 1], self.twin)

    def z_part(self):
        return self.wait_for(self.out.at[self.n, pl.ds(0, self.depth - 1), self.c], 1)

    def n_part(self):
        return self.wait_for(self.out.at[pl.ds(0, self.narrow - 1), :, self.c], 3)

    def start(self):
        self.own.start()
        for copy in self.first:
            copy.start()

    def spread(self):
        self.own.wait()
        self.z_part().wait_recv()
        mine = self.out.at[self.n, :, self.c]
        for m in self.n_peers:
            remote(mine, mine, self.sems[3], self.sems[4], (m, self.w)).start()
        self.wait_for(mine, 5).start()

    def cross(self):
        self.n_part().wait_recv()
        for m in self.n_peers:
            self.wait_for(self.out.at[m, :, self.c], 5).start()

    def finish(self):
        self.wait_for(self.out.at[:, :, 1 - self.c], 5).wait()
        self.z_part().wait_send()
        self.n_part().wait_send()


def greet_lines(narrow, depth):
    n, w = lax.axis_index(NARROW), lax.axis_index(WIDE)
    z, c = lax.div(w, 2), lax.rem(w, 2)
    peers = [(n, lax.rem(z + k, depth) * 2 + c) for k in range(1, depth)]
    peers += [(lax.rem(n + k, narrow), w) for k in range(1, narrow)]
    peers += [(n, z * 2 + 1 - c)]
    barrier = pltpu.get_barrier_semaphore()
    for peer in peers:
        pl.semaphore_signal(barrier, inc=1, device_id=peer, device_id_type=MESH)
    pl.semaphore_wait(barrier, len(peers))


class LineSum:
    def __init__(self, parts, got, sems, place, length, peer_of):
        self.got, self.length = got, length
        self.own = pltpu.make_async_copy(parts.at[place], got.at[0], sems.at[0])
        self.copies = []
        for k in range(1, length):
            there = lax.rem(place + k, length)
            self.copies.append(
                remote(
                    parts.at[there], got.at[k], sems.at[2 * k - 1], sems.at[2 * k], peer_of(there)
                )
            )

    def start(self):
        self.own.start()
        for copy in self.copies:
            copy.start()

    def arrive(self):
        self.own.wait()
        for copy in self.copies:
            copy.wait_recv()

    def total(self, *index):
        summed = self.got[(0,) + index].astype(FULL)
        for k in range(1, self.length):
            summed += self.got[(k,) + index].astype(FULL)
        return summed

    def finish(self):
        for copy in self.copies:
            copy.wait_send()


def square_peer(n, k):
    x, y, kx, ky = lax.rem(n, 2), lax.div(n, 2), lax.rem(k, 2), lax.div(k, 2)
    return 2 * (y + ky - 2 * y * ky) + x + kx - 2 * x * kx


class SquareShare:
    def __init__(self, rows, got, send, recv, n, w):
        self.half = half = rows.shape[0] // 2
        low, high = pl.ds(0, half), pl.ds(half, half)
        beside, across = (square_peer(n, 1), w), (square_peer(n, 2), w)
        self.first = [
            remote(rows, got.at[1], send.at[1], recv.at[1], beside),
            remote(rows, got.at[2], send.at[2], recv.at[2], across),
        ]
        self.second = [
            remote(got.at[1, low], got.at[3, low], send.at[0], recv.at[0], across),
            remote(got.at[2, high], got.at[3, high], send.at[3], recv.at[3], beside),
        ]

    def start(self):
        for copy in self.first:
            copy.start()

    def relay(self, i):
        self.first[i].wait_recv()
        self.second[i].start()

    def arrive(self):
        for copy in self.second:
            copy.wait_recv()

    def finish(self):
        for copy in self.first + self.second:
            copy.wait_send()


def square_of(n, narrow):
    return n + 1 - 2 * lax.rem(n, 2), n + 2 - 4 * lax.div(n, 2), narrow - 1 - n


class SquareSum:
    def __init__(self, parts, own, held, got, sems, n, w, narrow):
        beside, across, corner = square_of(n, narrow)
        self.own, self.held, self.got = own, held, got
        self.half = half = parts.shape[1] // 2
        low, high = pl.ds(0, half), pl.ds(half, half)
        self.local = [
            pltpu.make_async_copy(parts.at[n], own, sems.at[0, 6]),
            pltpu.make_async_copy(parts.at[across, low], held.at[0], sems.at[0, 7]),
            pltpu.make_async_copy(parts.at[beside, high], held.at[1], sems.at[1, 6]),
        ]

        def send(i, src, peer):
            return remote(src, got.at[i], sems.at[0, i], sems.at[1, i], (peer, w))

        self.copies = [
            send(0, parts.at[corner, low], beside),
            send(1, parts.at[corner, high], across),
            send(2, parts.at[beside, low], beside),
            send(3, parts.at[across, high], across),
            send(4, held.at[1], beside),
            send(5, held.at[0], across),
        ]

    def start(self):
        for copy in self.local + self.copies[:4]:
            copy.start()

    def relay(self):
        for i in range(2):
            self.local[1 + i].wait()
            self.copies[i].wait_recv()
            for j in range(self.half):
                self.held[i, j] = (
                    self.held[i, j].astype(FULL) + self.got[i, j].astype(FULL)
                ).astype(LOW)
            self.copies[5 - i].start()

    def arrive(self):
        self.local[0].wait()
        for copy in self.copies[2:]:
            copy.wait_recv()

    def total(self, j):
        first, second = (2, 5) if j < self.half else (4, 3)
        summed = self.own[j].astype(FULL)
        for i in (first, second):
            summed += self.got[i, j % self.half].astype(FULL)
        return summed

    def finish(self):
        for copy in self.copies:
            copy.wait_send()


def end_kernel(
    narrow,
    depth,
    pack,
    sums,
    middle,
    up_sum,
    down_sum,
    pack_all,
    sums_all,
    middle_out,
    up_out,
    down_out,
    middle_got,
    up_got,
    down_got,
    pack_sems,
    sums_sems,
    middle_sems,
    back_send,
    back_recv,
    back_own,
):
    n, w = lax.axis_index(NARROW), lax.axis_index(WIDE)
    z, c = lax.div(w, 2), lax.rem(w, 2)
    greet_lines(narrow, depth)
    gathers = [
        StagedGather(pack, pack_all, pack_sems, narrow, depth),
        StagedGather(sums, sums_all, sums_sems, narrow, depth),
    ]
    line = LineSum(middle, middle_got, middle_sems, z, depth, lambda there: (n, there * 2 + c))
    backs = [
        Returned(
            values, landed, back_send.at[i], back_recv.at[i], back_own.at[i], n, w, narrow, i
        )
        for i, (values, landed) in enumerate(((up_sum, up_got), (down_sum, down_got)))
    ]
    for gather in gathers:
        gather.start()
    line.start()
    for back in backs:
        back.start()
    for gather in gathers:
        gather.spread()
    line.arrive()
    middle_out[...] = line.total()
    for gather in gathers:
        gather.cross()
    for back, landed, out in zip(backs, (up_got, down_got), (up_out, down_out)):
        back.arrive()
        out[...] = landed[...].astype(FULL)
    for gather in gathers:
        gather.finish()
    line.finish()
    for back in backs:
        back.finish()


class Returned:
    def __init__(self, values, got, send, recv, own, n, w, narrow, axis):
        span = values.shape[axis] // narrow
        other = values.shape[1 - axis]

        def block(m):
            mine = pl.ds(m * span, span)
            return values.at[mine, :] if axis == 0 else values.at[:, mine]

        there = pl.ds(n * other, other)
        landing = got.at[:, there] if axis == 0 else got.at[there, :]
        self.own = pltpu.make_async_copy(block(n), landing, own)
        self.copies = []
        for k in range(1, narrow):
            m = lax.rem(n + k, narrow)
            self.copies.append(
                remote(block(m), landing, send.at[k - 1], recv.at[k - 1], (m, w))
            )

    def start(self):
        self.own.start()
        for copy in self.copies:
            copy.start()

    def arrive(self):
        self.own.wait()
        for copy in self.copies:
            copy.wait_recv()

    def finish(self):
        for copy in self.copies:
            copy.wait_send()


def end_gather(pack, sums, middle, up_sum, down_sum, collective_id):
    narrow, wide = lax.axis_size(NARROW), lax.axis_size(WIDE)
    depth = wide // 2
    dma = pltpu.SemaphoreType.DMA
    anywhere = pl.BlockSpec(memory_space=pl.ANY)
    up_shape = (up_sum.shape[0] // narrow, up_sum.shape[1] * narrow)
    down_shape = (down_sum.shape[0] * narrow, down_sum.shape[1] // narrow)
    outs = pl.pallas_call(
        partial(end_kernel, narrow, depth),
        out_shape=[
            jax.ShapeDtypeStruct((narrow, depth, 2) + pack.shape, pack.dtype),
            jax.ShapeDtypeStruct((narrow, depth, 2) + sums.shape, sums.dtype),
            jax.ShapeDtypeStruct(middle.shape[1:], FULL),
            jax.ShapeDtypeStruct(up_shape, FULL),
            jax.ShapeDtypeStruct(down_shape, FULL),
        ],
        in_specs=[anywhere] * 5,
        out_specs=[anywhere] * 2 + [in_vmem()] * 3,
        scratch_shapes=[
            pltpu.VMEM(middle.shape, middle.dtype),
            pltpu.VMEM(up_shape, LOW),
            pltpu.VMEM(down_shape, LOW),
            dma((7,)),
            dma((7,)),
            dma((2 * depth,)),
            dma((2, narrow - 1)),
            dma((2, narrow - 1)),
            dma((2,)),
        ],
        compiler_params=pltpu.CompilerParams(
            collective_id=collective_id, has_side_effects=True, vmem_limit_bytes=32 << 20
        ),
        name="end_gather",
    )(pack, sums, middle, up_sum, down_sum)
    return [
        outs[0].reshape(-1, pack.shape[1]),
        outs[1].reshape((-1,) + sums.shape),
    ] + list(outs[2:])


def softplus(v):
    return jnp.maximum(v, 0.0) + jnp.log1p(jnp.exp(-jnp.abs(v)))


def convolved(window, marks, weight, bias):
    pre = bias + weight[CONV - 1 :] * window[8:]
    for lag in range(1, CONV):
        pre = pre + weight[CONV - 1 - lag : CONV - lag] * (
            window[8 - lag : 8 - lag + QUERY] * marks[:, lag : lag + 1]
        )
    return pre


def decays(marks, dt, step_bias, rate_scale):
    shape = (QUERY, QUERY)
    row = lax.broadcasted_iota(jnp.int32, shape, 0)
    column = lax.broadcasted_iota(jnp.int32, shape, 1)
    lower = (row >= column).astype(FULL)
    segment = jnp.broadcast_to(marks[:, :1], shape)
    visible = (segment == segment.T) & (row >= column)
    delta = jnp.broadcast_to(softplus(dt + step_bias), shape)
    total = nn(lower, -delta * rate_scale, highest)
    gap = jnp.where(visible, total - total.T, 0.0)
    decay = jnp.where(visible, jnp.exp(gap), 0.0)
    last = total[QUERY - 1 :, :]
    begun = jnp.exp(total) * marks[:, 4:5]
    tail = jnp.exp(last - total) * marks[:, 5:6]
    kept = jnp.exp(last) * marks[:1, 6:7]
    return lower, delta, decay, begun, tail, kept


def head_numbers(step_bias, log_rate, skip_gain, me):
    return step_bias[me], jnp.exp(jnp.full((1, QUERY), log_rate[me], FULL)), skip_gain[me]


def head_columns(values, me):
    start = pl.multiple_of(lax.div(me, 2) * 2 * HEAD_M, 2 * HEAD_M)
    pair = values[:, pl.ds(start, 2 * HEAD_M)]
    lane = lax.broadcasted_iota(jnp.int32, pair.shape, 1)
    moved = jnp.concatenate([pair[:, HEAD_M:], pair[:, :HEAD_M]], axis=1)
    odd = jnp.full(pair.shape, lax.rem(me, 2), jnp.int32) == 1
    return jnp.where(lane < HEAD_M, jnp.where(odd, moved, pair), 0.0)


def documents(doc_patches, pad_bytes):
    ends, end = [], 0
    for d in range(doc_patches.shape[0]):
        end = end + doc_patches[d]
        ends.append(end)

    def document(place):
        return sum((place >= end).astype(jnp.int32) for end in ends)

    def kept(place, offset):
        padded = [
            ((place == end - 1) & (offset >= PATCH - pad_bytes[d])).astype(FULL)
            for d, end in enumerate(ends)
        ]
        return 1.0 - sum(padded)

    return document, kept


def patch_marks(document, first, count):
    place = first + lax.broadcasted_iota(jnp.int32, (count, 8), 0)
    kind = lax.broadcasted_iota(jnp.int32, (count, 8), 1)
    opening = lax.div(place, QUERY) * QUERY
    block_mark = jnp.where(kind == CONV, opening - 1, opening + QUERY - 1)
    ahead = jnp.where(kind < CONV, place - kind, block_mark)
    facing = jnp.where(kind == CONV + 2, opening - 1, place)
    same = (document(ahead) == document(facing)) & (ahead >= 0) & (facing >= 0)
    return jnp.where(kind == 0, document(place).astype(FULL), same.astype(FULL))


def mixer_front_kernel(
    narrow,
    wide,
    doc_patches,
    pad_bytes,
    step_biases,
    log_rates,
    skip_gains,
    gain,
    conv_weight,
    conv_bias,
    pack,
    table,
    xz_blocks,
    gate,
    up,
    down,
    middle,
    cotangent,
    embedded,
    normed,
    xz,
    bc,
    dt,
    u_out,
    y_out,
    states,
    mixed_in,
    u_got,
    marks,
    keep_rows,
    keep_all,
    start,
    w_xz,
    gate_all,
    up_all,
    down_all,
    middle_all,
    others,
    table_all,
    gate_turned,
    up_turned,
    down_turned,
    mixed_all,
    xz_pad,
    bc_pad,
    state,
    u_blocks,
    u_send,
    u_recv,
    pack_sems,
    table_sems,
    xz_sems,
    turn_send,
    turn_recv,
    start_sems,
    depth_send,
    depth_recv,
    other_send,
    other_recv,
    own_sems,
    line_send,
    line_recv,
    cross_send,
    cross_recv,
    middle_sems,
):
    devices, depth = narrow * wide, wide // 2
    me, arrived = greet_all(devices, wide)
    n, w = lax.axis_index(NARROW), lax.axis_index(WIDE)
    z, c = lax.div(w, 2), lax.rem(w, 2)
    twin = (n, z * 2 + 1 - c)
    rows_in, units_in = gate.shape[0], gate.shape[1] // narrow
    columns_in = down.shape[1]
    gathers = [
        StagedGather(pack, start, pack_sems, narrow, depth),
        StagedGather(table, table_all, table_sems, narrow, depth),
    ]

    def pieces(m):
        mine = pl.ds(m * units_in, units_in)
        return (gate.at[:, mine], up.at[:, mine], down.at[mine, :])

    turned = (gate_turned, up_turned, down_turned)
    landing = (
        gate_turned.at[pl.ds(n * rows_in, rows_in), :],
        up_turned.at[pl.ds(n * rows_in, rows_in), :],
        down_turned.at[:, pl.ds(n * columns_in, columns_in)],
    )
    turns = []
    for k in range(1, narrow):
        m = lax.rem(n + k, narrow)
        for i, piece in enumerate(pieces(m)):
            turns.append(
                remote(piece, landing[i], turn_send.at[k - 1, i], turn_recv.at[k - 1, i], (m, w))
            )
    first_own = [
        pltpu.make_async_copy(piece, landing[i], start_sems.at[i])
        for i, piece in enumerate(pieces(n))
    ]
    own_xz = pltpu.make_async_copy(xz_blocks.at[me], w_xz.at[me], start_sems.at[3])
    own_middle = pltpu.make_async_copy(middle, middle_all.at[n, z, c], start_sems.at[4])

    def depth_copy(source, target):
        return remote(
            middle,
            middle_all.at[n, source, c],
            depth_send.at[target],
            depth_recv.at[source],
            (n, target * 2 + c),
        )

    share = SquareShare(cotangent, others, other_send, other_recv, n, w)
    results = (gate_all, up_all, down_all)
    own = [pltpu.make_async_copy(turned[i], results[i].at[z, c], own_sems.at[i]) for i in range(3)]
    beside, across, corner = square_of(n, narrow)

    def middle_copy(j, way, owner):
        there = middle_all.at[owner, j, c]
        peer = twin if way >= 4 else ((beside if way in (0, 3) else across), w)
        return remote(there, there, middle_sems.at[0, way, j], middle_sems.at[1, way, j], peer)

    def line_copy(i, source, step, src=None):
        there = results[i].at[source, c]
        return remote(
            there if src is None else src,
            there,
            line_send.at[i, source, max(step, 0)],
            line_recv.at[i, source],
            (n, (z + step) * 2 + c),
        )

    def along(i, source, step, src=None):
        @pl.when((z + step >= 0) & (z + step < depth))
        def _():
            line_copy(i, source, step, src).start()

    def middle_begin(j):
        @pl.when(z == j)
        def _():
            own_middle.wait()

        @pl.when(z != j)
        def _():
            depth_copy(j, z).wait_recv()

        for way in (0, 1, 7):
            middle_copy(j, way, n).start()

    def middle_on(j):
        middle_copy(j, 0, beside).wait_recv()
        if j % 2 == 0:
            middle_copy(j, 2, beside).start()
        middle_copy(j, 4, beside).start()
        middle_copy(j, 1, across).wait_recv()
        if j % 2 == 1:
            middle_copy(j, 3, across).start()
        middle_copy(j, 5, across).start()

    def line_side(distance, step):
        source = z - step * distance

        @pl.when((source >= 0) & (source < depth))
        def _():
            for i in range(3):
                line_copy(i, source, step).wait_recv()
                along(i, source, step)
                theirs = results[i].at[source, c]
                remote(theirs, theirs, cross_send.at[i], cross_recv.at[i], twin).start()

    def line_on(distance):
        @pl.when(2 * z < depth)
        def _():
            line_side(distance, 1)
            line_side(distance, -1)

        @pl.when(2 * z >= depth)
        def _():
            line_side(distance, -1)
            line_side(distance, 1)

    arrived()
    for gather in gathers:
        gather.start()
    for copy in turns + first_own + [own_xz, own_middle]:
        copy.start()
    send_blocks(me, devices, wide, xz_blocks, w_xz, xz_sems.at[0], xz_sems.at[1])
    for distance in range(1, depth):
        for target in (z + distance, z - distance):

            @pl.when((target >= 0) & (target < depth))
            def _():
                depth_copy(z, target).start()

    for gather in gathers:
        gather.spread()
    for copy in first_own[:3]:
        copy.wait()
    for copy in turns:
        copy.wait_recv()
    for i in range(3):
        along(i, z, 1, turned[i])
        along(i, z, -1, turned[i])
    for copy in own:
        copy.start()
    for gather in gathers:
        gather.cross()
    share.start()

    count = embedded.shape[0]
    patches = u_blocks.shape[1]
    block_rows = 2 * QUERY
    xz_pad[pl.ds(0, 8), :] = jnp.zeros((8, xz_pad.shape[1]), FULL)
    bc_pad[pl.ds(0, 8), :] = jnp.zeros((8, bc_pad.shape[1]), FULL)
    state[...] = jnp.zeros_like(state)
    step_bias, rate_scale, skip = head_numbers(step_biases, log_rates, skip_gains, me)
    document, kept_bytes = documents(doc_patches, pad_bytes)
    for first in range(0, count + 8, (count + 8) // 3):
        part = (count + 8) // 3
        marks[first : first + part, :] = patch_marks(document, first, part)
    byte = lax.broadcasted_iota(jnp.int32, keep_rows.shape[1:], 0)
    for k in range(narrow):
        there = (square_peer(n, k) * wide + w) * patches
        keep_rows[k] = kept_bytes(there + lax.div(byte, PATCH), lax.rem(byte, PATCH))
    wx, bx = head_columns(conv_weight, me), head_columns(conv_bias, me)
    wbc, bbc = conv_weight[:, DI:], conv_bias[:, DI:]
    for gather in gathers:
        gather.finish()
    own_xz.wait()
    wait_blocks(me, devices, wide, w_xz, xz_sems.at[0], xz_sems.at[1])
    words = lax.broadcasted_iota(jnp.int32, (block_rows, VOCAB), 1).astype(FULL)
    own_lane = lax.broadcasted_iota(jnp.int32, (block_rows, STATE), 1) == me

    word_rows = table_all[...].reshape(VOCAB, EMB).astype(LOW)

    def project(i, carry):
        rows = pl.ds(pl.multiple_of(i * block_rows, block_rows), block_rows)
        ids = start[i, :, :, :, 3 * STATE : 4 * STATE].reshape(block_rows, STATE).astype(FULL)
        place = i * block_rows + lax.broadcasted_iota(jnp.int32, (block_rows, PATCH), 0)
        kept = kept_bytes(place, lax.broadcasted_iota(jnp.int32, (block_rows, PATCH), 1))
        keep_all[rows, :] = kept
        for k in range(PATCH):
            chosen = jnp.where(ids[:, k : k + 1] == words, kept[:, k : k + 1], 0.0).astype(LOW)
            embedded[rows, k * EMB : (k + 1) * EMB] = nn(chosen, word_rows).astype(LOW)
        row_embedded = embedded[rows, :]
        for first in range(0, D, WEIGHT_STEP):
            columns = slice(first, first + WEIGHT_STEP)
            there = slice(4 * STATE + first, 4 * STATE + first + WEIGHT_STEP)
            weight = start[:, :, :, :, there].reshape(D, WEIGHT_STEP)
            mixed_all[rows, columns] = nn(row_embedded, weight)
        row_normed = (unit_rows(mixed_all[rows, :])[0] * gain[...]).astype(LOW)
        normed[rows, :] = row_normed
        row_xz = nn(row_normed, w_xz[...].reshape(D, 2 * HEAD_M)).astype(LOW)
        weight = start[:, :, :, :, : 3 * STATE].reshape(D, 3 * STATE)
        row_bcdt = nn(row_normed, weight).astype(LOW)
        xz[rows, :] = row_xz
        bc[rows, :] = row_bcdt[:, : 2 * STATE]
        own_dt = jnp.where(own_lane, row_bcdt[:, 2 * STATE :].astype(FULL), 0.0)
        dt[rows, :] = jnp.sum(own_dt, axis=1, keepdims=True)
        padded = pl.ds(pl.multiple_of(i * block_rows + 8, 8), block_rows)
        xz_pad[padded, :] = row_xz.astype(FULL)
        bc_pad[padded, :] = row_bcdt[:, : 2 * STATE].astype(FULL)
        return carry

    lax.fori_loop(0, count // block_rows, project, 0)
    for j in range(depth):
        middle_begin(j)
    for i in range(2):
        share.relay(i)
    mixed_in[...] = mixed_all[pl.ds(pl.multiple_of(me * patches, patches), patches), :]
    group = QUERY // patches

    def block(i, carry):
        first = pl.multiple_of(i * QUERY, QUERY)
        rows = pl.ds(first, QUERY)
        mark = marks[rows, :]
        act_x = jax.nn.silu(convolved(xz_pad[pl.ds(first, QUERY + 8), :], mark, wx, bx))
        act = jax.nn.silu(convolved(bc_pad[pl.ds(first, QUERY + 8), :], mark, wbc, bbc))
        x, b, c = act_x[:, :HEAD_M], act[:, :STATE], act[:, STATE:]
        lower, delta, decay, begun, tail, kept = decays(mark, dt[rows, :], step_bias, rate_scale)
        weight = nt(c, b, highest) * decay * delta.T
        held = state[...]
        states[i] = held
        y = (
            nn(weight, x, highest)
            + nt(c, held, highest) * begun[:, :HEAD_M]
            + skip * x
        )
        state[...] = held * kept + tn(x * (tail * delta)[:, :HEAD_M], b, highest)
        z = xz[rows, :].astype(FULL)[:, HEAD_M:]
        u = y * jax.nn.silu(z)
        y_out[rows, :] = y
        u_out[rows, :] = u
        u_blocks[pl.ds(i * group, group)] = u.astype(LOW).reshape(group, patches, HEAD_M)
        return carry

    lax.fori_loop(0, count // QUERY, block, 0)
    send_blocks(me, devices, wide, u_blocks, u_got, u_send, u_recv)
    u_got[me] = u_blocks[me]
    line_on(1)
    for copy in own:
        copy.wait()
    for i in range(3):
        mine = results[i].at[z, c]
        remote(mine, mine, cross_send.at[i], cross_recv.at[i], twin).start()
    middle_on(0)
    middle_on(1)
    line_on(2)
    middle_on(2)
    middle_on(3)
    for j in range(depth):
        middle_copy(j, 2 + j % 2, corner).wait_recv()
        middle_copy(j, 6, corner).start()
    line_on(3)
    wait_blocks(me, devices, wide, u_got, u_send, u_recv)
    share.arrive()
    share.finish()
    for copy in turns:
        copy.wait_send()
    for target in range(depth):

        @pl.when(target != z)
        def _():
            depth_copy(z, target).wait_send()

    for i in range(3):
        theirs = results[i].at[:, 1 - c]
        remote(theirs, theirs, cross_send.at[i], cross_recv.at[i], twin).wait()
    for j in range(depth):
        for way, owner in ((4, beside), (5, across), (6, corner), (7, n)):
            middle_copy(j, way, owner).wait()
        for way in (0, 1, 2 + j % 2):
            middle_copy(j, way, n).wait_send()
    for i in range(3):
        for source in range(depth):
            for step in (1, -1):

                @pl.when((step * (z - source) >= 0) & (z + step >= 0) & (z + step < depth))
                def _():
                    line_copy(i, source, step).wait_send()


def mixer_backward_kernel(
    narrow,
    wide,
    step_biases,
    log_rates,
    skip_gains,
    xz,
    bc,
    dt,
    marks,
    conv_weight,
    conv_bias,
    y_in,
    states,
    normed,
    w_xz,
    start,
    mixed_in,
    global_grad,
    gain,
    gated_scale,
    gain_grads,
    gated_gain_grads,
    du_blocks,
    up_parts,
    down_parts,
    middle_parts,
    gate_sum,
    mix_grad,
    end_pack,
    sums,
    bcdt_grads,
    xz_grads,
    up_sum,
    down_sum,
    middle_sums,
    gate_out,
    mix_all,
    w_bcdt,
    w_sem,
    dwx,
    dwbc,
    dnumbers,
    xz_pad,
    bc_pad,
    dx_pad,
    dbc_pad,
    dstate,
    du_got,
    dxz,
    dbcdt,
    partial_rows,
    core_got,
    narrow_got,
    z_rows,
    z_got,
    grads,
    grads_got,
    up_got,
    down_got,
    middle_own,
    middle_held,
    middle_got,
    gate_got,
    du_send,
    du_recv,
    core_send,
    core_recv,
    narrow_send,
    narrow_recv,
    z_send,
    z_recv,
    grads_send,
    grads_recv,
    up_sems,
    down_sems,
    middle_sems,
    back_send,
    back_recv,
    back_own,
    mix_sems,
):
    devices = narrow * wide
    depth = wide // 2
    me, arrived = greet_all(devices, wide)
    n, w = lax.axis_index(NARROW), lax.axis_index(WIDE)
    z_place, core = lax.div(w, 2), lax.rem(w, 2)
    twin = (n, z_place * 2 + 1 - core)
    count = xz.shape[0]
    blocks = count // QUERY
    xz_pad[pl.ds(0, 8), :] = jnp.zeros((8, xz_pad.shape[1]), FULL)
    bc_pad[pl.ds(0, 8), :] = jnp.zeros((8, bc_pad.shape[1]), FULL)
    dx_pad[pl.ds(count, 8), :] = jnp.zeros((8, dx_pad.shape[1]), FULL)
    dbc_pad[pl.ds(count, 8), :] = jnp.zeros((8, dbc_pad.shape[1]), FULL)
    dstate[...] = jnp.zeros_like(dstate)
    dwx[...] = jnp.zeros_like(dwx)
    dwbc[...] = jnp.zeros_like(dwbc)
    dnumbers[...] = jnp.zeros_like(dnumbers)
    step_bias, rate_scale, skip = head_numbers(step_biases, log_rates, skip_gains, me)
    wx, bx = head_columns(conv_weight, me), head_columns(conv_bias, me)
    wbc, bbc = conv_weight[:, DI:], conv_bias[:, DI:]
    weight_copy = pltpu.make_async_copy(start.at[:, pl.ds(0, 3 * STATE)], w_bcdt, w_sem)
    weight_copy.start()

    def fill(i, carry):
        first = pl.multiple_of(i * QUERY, QUERY)
        rows = pl.ds(first, QUERY)
        xz_pad[pl.ds(first + 8, QUERY), :] = xz[rows, :].astype(FULL)
        bc_pad[pl.ds(first + 8, QUERY), :] = bc[rows, :].astype(FULL)
        return carry

    arrived()
    send_blocks(me, devices, wide, du_blocks, du_got, du_send, du_recv)
    lines = [
        LineSum(parts, landed, line_sems, z_place, depth, lambda there: (n, there * 2 + core))
        for parts, landed, line_sems in (
            (down_parts, down_got, down_sems),
            (up_parts, up_got, up_sems),
        )
    ]
    middle_line = SquareSum(
        middle_parts, middle_own, middle_held, middle_got, middle_sems, n, w, narrow
    )
    back = Returned(gate_sum, gate_got, back_send, back_recv, back_own, n, w, narrow, 0)
    mix_gather = StagedGather(mix_grad, mix_all, mix_sems, narrow, depth)
    middle_line.start()
    mix_gather.start()
    for line in lines:
        line.start()
    back.start()
    du_got[me] = du_blocks[me]
    lax.fori_loop(0, blocks, fill, 0)
    wait_blocks(me, devices, wide, du_got, du_send, du_recv)
    patches = du_blocks.shape[1]
    group = QUERY // patches
    own_lane = lax.broadcasted_iota(jnp.int32, (QUERY, STATE), 1) == me

    def slope(pre):
        s = jax.nn.sigmoid(pre)
        return s * (1.0 + pre * (1.0 - s))

    def total(v):
        return jnp.sum(jnp.sum(v, axis=1, keepdims=True), axis=0, keepdims=True)

    def conv_back(pad, first, dpre_pad, dpre, weight, dw):
        mark = marks[pl.ds(first, QUERY), :]
        window = pad[pl.ds(first, QUERY + 8), :]
        later = dpre_pad[pl.ds(first, QUERY + 8), :]
        later_marks = marks[pl.ds(first, QUERY + 8), :]
        out = weight[CONV - 1 :] * dpre
        dw[CONV - 1 : CONV, :] += jnp.sum(dpre * window[8:], axis=0, keepdims=True)
        dw[CONV : CONV + 1, :] += jnp.sum(dpre, axis=0, keepdims=True)
        for lag in range(1, CONV):
            tap = CONV - 1 - lag
            out = out + weight[tap : tap + 1] * (
                (later * later_marks[:, lag : lag + 1])[lag : lag + QUERY]
            )
            dw[tap : tap + 1, :] += jnp.sum(
                dpre * (window[8 - lag : 8 - lag + QUERY] * mark[:, lag : lag + 1]),
                axis=0,
                keepdims=True,
            )
        return out

    def block(k, carry):
        i = blocks - 1 - k
        first = pl.multiple_of(i * QUERY, QUERY)
        rows = pl.ds(first, QUERY)
        mark = marks[rows, :]
        pre_x = convolved(xz_pad[pl.ds(first, QUERY + 8), :], mark, wx, bx)
        pre = convolved(bc_pad[pl.ds(first, QUERY + 8), :], mark, wbc, bbc)
        act = jax.nn.silu(pre)
        x, b, c = jax.nn.silu(pre_x)[:, :HEAD_M], act[:, :STATE], act[:, STATE:]
        step = dt[rows, :]
        lower, delta, decay, begun, tail, kept = decays(mark, step, step_bias, rate_scale)
        held, dheld = states[i], dstate[...]
        z = xz[rows, :].astype(FULL)[:, HEAD_M:]
        du = du_got[pl.ds(i * group, group)].astype(FULL).reshape(QUERY, HEAD_M)
        y = y_in[rows, :]
        dy = du * jax.nn.silu(z)
        dz = du * y * slope(z)
        scores = nt(c, b, highest)
        reach = decay * delta.T
        dweight = nt(dy, x, highest)
        dscores = dweight * reach
        fed = x * (tail * delta)[:, :HEAD_M]
        begun_dy = dy * begun[:, :HEAD_M]
        dc = nn(dscores, b, highest) + nn(begun_dy, held, highest)
        db = tn(dscores, c, highest) + nn(fed, dheld, highest)
        dfed = nt(b, dheld, highest)
        dx = skip * dy + tn(scores * reach, dy, highest) + (tail * delta)[:, :HEAD_M] * dfed
        moved = dweight * scores * decay
        turned = moved.T
        ddelta = jnp.sum(turned, axis=1, keepdims=True)
        dtotal = jnp.sum(moved * delta.T, axis=1, keepdims=True) - ddelta * delta[:, :1]
        dtotal += jnp.sum(begun_dy * nt(c, held, highest), axis=1, keepdims=True)
        dtail = jnp.sum(dfed * x, axis=1, keepdims=True)
        ddelta += dtail * tail[:, :1]
        dtail = dtail * (tail * delta)[:, :1]
        dtotal -= dtail
        dlast = jnp.sum(dtail, axis=0, keepdims=True) + total(dheld * held * kept)
        dlog = tn(lower, jnp.broadcast_to(dtotal, (QUERY, QUERY)), highest)[:, :1] + dlast
        ddelta -= dlog * rate_scale[:, :1]
        dstep = ddelta * jax.nn.sigmoid(step + step_bias)
        dbcdt[rows, 2 * STATE :] = jnp.where(own_lane, dstep, 0.0).astype(LOW)
        dnumbers[0:1, :] += jnp.broadcast_to(jnp.sum(dstep, axis=0, keepdims=True), (1, 128))
        dnumbers[1:2, :] -= jnp.broadcast_to(
            jnp.sum(dlog * delta[:, :1] * rate_scale[:, :1], axis=0, keepdims=True), (1, 128)
        )
        dnumbers[2:3, :] += jnp.broadcast_to(total(dy * x), (1, 128))
        dstate[...] = dheld * kept + tn(begun_dy, c, highest)
        dpre_x = jnp.concatenate([dx, jnp.zeros_like(dx)], axis=1) * slope(pre_x)
        dpre = jnp.concatenate([db, dc], axis=1) * slope(pre)
        dx_pad[rows, :] = dpre_x
        dbc_pad[rows, :] = dpre
        dxz[rows, :] = jnp.concatenate([dz, dz], axis=1).astype(LOW)
        return carry

    lax.fori_loop(0, blocks, block, 0)

    def unconvolve(i, carry):
        first = pl.multiple_of(i * QUERY, QUERY)
        rows = pl.ds(first, QUERY)
        dxr = conv_back(xz_pad, first, dx_pad, dx_pad[rows, :], wx, dwx)
        left = lax.broadcasted_iota(jnp.int32, dxr.shape, 1) < HEAD_M
        dxz[rows, :] = jnp.where(left, dxr, dxz[rows, :].astype(FULL)).astype(LOW)
        dbcdt[rows, : 2 * STATE] = conv_back(
            bc_pad, first, dbc_pad, dbc_pad[rows, :], wbc, dwbc
        ).astype(LOW)
        return carry

    middle_line.relay()
    mix_gather.spread()
    lax.fori_loop(0, blocks, unconvolve, 0)

    width = normed.shape[1]
    own_rows = xz_grads.shape[1]

    weight_copy.wait()

    def rows_of(m, carry):
        for z in range(depth):
            first = (m * depth + z) * 2 * patches
            rows = pl.ds(pl.multiple_of(first, 2 * patches), 2 * patches)
            values = nt(dxz[rows, :], w_xz[...]) + nt(dbcdt[rows, :], w_bcdt[...])
            partial_rows[m, z, :, :, :width] = values.astype(LOW).reshape(2, patches, width)
        return carry

    lax.fori_loop(0, narrow, rows_of, 0)

    def weight_grads(m, carry):
        span = width // narrow
        columns = pl.ds(pl.multiple_of(m * span, span), span)
        lhs = normed[:, columns]
        grads[pl.ds(m * 2 * depth, 2 * depth)] = (
            tn(lhs, dxz[...]).astype(LOW).reshape(2 * depth, own_rows, 2 * HEAD_M)
        )
        partial_rows[m, :, :, :, width:] = (
            tn(lhs, dbcdt[...]).astype(LOW).reshape(depth, 2, own_rows, 3 * STATE)
        )
        return carry

    lax.fori_loop(0, narrow, weight_grads, 0)
    to_twin = remote(partial_rows.at[:, :, 1 - core], core_got, core_send, core_recv, twin)
    to_twin.start()
    send_blocks(me, devices, wide, grads, grads_got, grads_send, grads_recv)
    grads_got[me] = grads[me]
    back.arrive()
    gate_out[...] = gate_got[...].astype(FULL)
    to_twin.wait_recv()

    def narrow_copy(k, m):
        return remote(
            core_got.at[m], narrow_got.at[k - 1], narrow_send.at[k - 1], narrow_recv.at[k - 1], (m, w)
        )

    for k in range(1, narrow):
        m = lax.rem(n + k, narrow)
        for z in range(depth):
            core_got[m, z] = (
                core_got[m, z].astype(FULL) + partial_rows[m, z, core].astype(FULL)
            ).astype(LOW)
        narrow_copy(k, m).start()
    mix_gather.cross()
    middle_line.arrive()
    for z in range(depth):
        middle_sums[z] = middle_line.total(z).astype(LOW)
    for k in range(1, narrow):
        narrow_copy(k, n).wait_recv()
    for z in range(depth):
        total_rows = core_got[n, z].astype(FULL) + partial_rows[n, z, core].astype(FULL)
        for k in range(1, narrow):
            total_rows += narrow_got[k - 1, z].astype(FULL)
        z_rows[z] = total_rows.astype(LOW)

    def z_copy(k, place):
        return remote(
            z_rows.at[place], z_got.at[k - 1], z_send.at[k - 1], z_recv.at[k - 1], (n, place * 2 + core)
        )

    for k in range(1, depth):
        z_copy(k, lax.rem(z_place + k, depth)).start()
    for line, out in zip(lines, (down_sum, up_sum)):
        line.arrive()
        out[...] = line.total().astype(LOW)
    wait_blocks(me, devices, wide, grads_got, grads_send, grads_recv)
    xz_grads[...] = grads_got[...]
    total_rows = z_rows[z_place].astype(FULL)
    for k in range(1, depth):
        z_copy(k, z_place).wait_recv()
        total_rows += z_got[k - 1].astype(FULL)
    bcdt_grads[...] = total_rows[:, width:]
    unit, scale = unit_rows(mixed_in[...])
    normed_grad = total_rows[:, :width]
    embed_grad = global_grad[...] + norm_back(normed_grad, gain[...], unit, scale)
    end_pack[:, :width] = embed_grad.astype(LOW)
    end_pack[:, width:] = gated_scale[...].astype(LOW)
    gain_mix_grad = jnp.sum(normed_grad * unit, axis=0, keepdims=True)
    wide_rows = [gain_mix_grad] + [gated_gain_grads[i : i + 1, :] for i in range(2)]
    wide_rows += [gain_grads[i : i + 1, :] for i in range(2)]
    wide_rows += [dwbc[i : i + 1, :] for i in range(CONV + 1)]
    wide_rows += [dwx[i : i + 1, :] for i in range(CONV + 1)]
    row = 0
    for values in wide_rows:
        for first in range(0, values.shape[1], 128):
            sums[row : row + 1, :] = values[:, first : first + 128]
            row += 1
    lane = lax.broadcasted_iota(jnp.int32, (1, 128), 1)
    sums[row : row + 1, :] = sum(
        jnp.where(lane == i, dnumbers[i : i + 1, :], 0.0) for i in range(3)
    )
    mix_gather.finish()
    for line in lines:
        line.finish()
    middle_line.finish()
    back.finish()
    to_twin.wait_send()
    for k in range(1, narrow):
        narrow_copy(k, n).wait_send()
    for k in range(1, depth):
        z_copy(k, z_place).wait_send()


def in_smem():
    return pl.BlockSpec(memory_space=pltpu.SMEM)


def in_vmem():
    return pl.BlockSpec(memory_space=pltpu.VMEM)


def mixer_front(scalars, gain, conv_weight, conv_bias, arrays, collective_id):
    narrow, wide = lax.axis_size(NARROW), lax.axis_size(WIDE)
    devices, depth = narrow * wide, wide // 2
    pack, table, xz_blocks, gate, up, down, middle, cotangent = arrays
    patches = cotangent.shape[0] // PATCH
    count = devices * patches
    units = gate.shape[1] // narrow
    dma = pltpu.SemaphoreType.DMA
    anywhere = pl.BlockSpec(memory_space=pl.ANY)

    def full(*shape):
        return jax.ShapeDtypeStruct(shape, FULL)

    def low(*shape):
        return jax.ShapeDtypeStruct(shape, LOW)

    outs = pl.pallas_call(
        partial(mixer_front_kernel, narrow, wide),
        out_shape=[
            low(count, D),
            low(count, D),
            low(count, 2 * HEAD_M),
            low(count, 2 * STATE),
            full(count, 1),
            full(count, HEAD_M),
            full(count, HEAD_M),
            full(count // QUERY, HEAD_M, STATE),
            full(patches, D),
            low(devices, patches, HEAD_M),
            full(count + 8, 8),
            full(narrow, patches * PATCH, 1),
            full(count, PATCH),
            low(narrow, depth, 2, *pack.shape),
            low(*xz_blocks.shape),
            low(depth, 2, D, units),
            low(depth, 2, D, units),
            low(depth, 2, units, D),
            low(narrow, depth, 2, *middle.shape),
            low(narrow, *cotangent.shape),
        ],
        in_specs=[in_smem()] * 5 + [in_vmem()] * 3 + [anywhere] * 8,
        out_specs=[in_vmem()] * 15 + [anywhere] * 5,
        scratch_shapes=[
            pltpu.VMEM((narrow, depth, 2) + table.shape, FULL),
            pltpu.VMEM((D, units), LOW),
            pltpu.VMEM((D, units), LOW),
            pltpu.VMEM((units, D), LOW),
            pltpu.VMEM((count, D), FULL),
            pltpu.VMEM((count + 8, 2 * HEAD_M), FULL),
            pltpu.VMEM((count + 8, 2 * STATE), FULL),
            pltpu.VMEM((HEAD_M, STATE), FULL),
            pltpu.VMEM((devices, patches, HEAD_M), LOW),
            dma,
            dma,
            dma((7,)),
            dma((7,)),
            dma((2,)),
            dma((narrow - 1, 3)),
            dma((narrow - 1, 3)),
            dma((5,)),
            dma((depth,)),
            dma((depth,)),
            dma((narrow,)),
            dma((narrow,)),
            dma((3,)),
            dma((3, depth, 2)),
            dma((3, depth)),
            dma((3,)),
            dma((3,)),
            dma((2, 8, depth)),
        ],
        compiler_params=pltpu.CompilerParams(
            collective_id=collective_id, has_side_effects=True, vmem_limit_bytes=48 << 20
        ),
        name="mixer_front",
    )(*scalars, gain, conv_weight, conv_bias, *arrays)
    start, w_xz, gate_all, up_all, down_all, middle_all, others = outs[13:]
    return (
        outs[:13],
        start.reshape(D, -1),
        w_xz.reshape(D, -1),
        gate_all.reshape(wide, D, -1),
        up_all.reshape(wide, D, -1),
        down_all.reshape(-1, D),
        middle_all.reshape(D, -1),
        others,
    )


def mixer_backward(
    scalars,
    xz,
    bc,
    dt,
    marks,
    conv_weight,
    conv_bias,
    y,
    states,
    normed,
    w_xz,
    start,
    mixed_in,
    global_grad,
    gain,
    gated_scale,
    gain_grads,
    gated_gain_grads,
    du_blocks,
    up_parts,
    down_parts,
    middle_parts,
    gate_sum,
    mix_grad,
    collective_id,
):
    narrow, wide = lax.axis_size(NARROW), lax.axis_size(WIDE)
    devices = narrow * wide
    count, width = normed.shape
    patches = count // devices
    own_rows = width // devices
    dma = pltpu.SemaphoreType.DMA
    low = partial(pltpu.VMEM, dtype=LOW)
    every = width + 3 * STATE
    back_shape = (gate_sum.shape[0] // narrow, gate_sum.shape[1] * narrow)
    anywhere = pl.BlockSpec(memory_space=pl.ANY)
    return pl.pallas_call(
        partial(mixer_backward_kernel, narrow, wide),
        out_shape=[
            jax.ShapeDtypeStruct((patches, width + 128), LOW),
            jax.ShapeDtypeStruct((SUM_ROWS + CONV + 2, 128), FULL),
            jax.ShapeDtypeStruct((own_rows, 3 * STATE), FULL),
            jax.ShapeDtypeStruct((devices, own_rows, 2 * HEAD_M), LOW),
            jax.ShapeDtypeStruct(up_parts.shape[1:], LOW),
            jax.ShapeDtypeStruct(down_parts.shape[1:], LOW),
            jax.ShapeDtypeStruct(middle_parts.shape[1:], LOW),
            jax.ShapeDtypeStruct(back_shape, FULL),
            jax.ShapeDtypeStruct((narrow, wide // 2, 2) + mix_grad.shape, LOW),
        ],
        in_specs=[in_smem()] * 3
        + [in_vmem()] * 10
        + [anywhere]
        + [in_vmem()] * 7
        + [anywhere] * 5,
        out_specs=[in_vmem()] * 8 + [anywhere],
        scratch_shapes=[
            low((width, 3 * STATE)),
            dma,
            pltpu.VMEM((8, 2 * HEAD_M), FULL),
            pltpu.VMEM((8, 2 * STATE), FULL),
            pltpu.VMEM((8, 128), FULL),
            pltpu.VMEM((count + 8, 2 * HEAD_M), FULL),
            pltpu.VMEM((count + 8, 2 * STATE), FULL),
            pltpu.VMEM((count + 8, 2 * HEAD_M), FULL),
            pltpu.VMEM((count + 8, 2 * STATE), FULL),
            pltpu.VMEM((HEAD_M, STATE), FULL),
            low((devices, patches, HEAD_M)),
            low((count, 2 * HEAD_M)),
            low((count, 3 * STATE)),
            low((narrow, wide // 2, 2, patches, every)),
            low((narrow, wide // 2, patches, every)),
            low((narrow - 1, wide // 2, patches, every)),
            low((wide // 2, patches, every)),
            low((wide // 2 - 1, patches, every)),
            low((devices, own_rows, 2 * HEAD_M)),
            low((devices, own_rows, 2 * HEAD_M)),
            low(up_parts.shape),
            low(down_parts.shape),
            low(middle_parts.shape[1:]),
            low((2, wide // 4) + middle_parts.shape[2:]),
            low((6, wide // 4) + middle_parts.shape[2:]),
            low(back_shape),
            dma,
            dma,
            dma,
            dma,
            dma((narrow - 1,)),
            dma((narrow - 1,)),
            dma((wide // 2 - 1,)),
            dma((wide // 2 - 1,)),
            dma,
            dma,
            dma((wide,)),
            dma((wide,)),
            dma((2, 8)),
            dma((narrow - 1,)),
            dma((narrow - 1,)),
            dma,
            dma((7,)),
        ],
        compiler_params=pltpu.CompilerParams(
            collective_id=collective_id, has_side_effects=True, vmem_limit_bytes=56 << 20
        ),
        name="mixer_backward",
    )(
        *scalars,
        xz,
        bc,
        dt,
        marks,
        conv_weight,
        conv_bias,
        y,
        states,
        normed,
        w_xz,
        start,
        mixed_in,
        global_grad,
        gain,
        gated_scale,
        gain_grads,
        gated_gain_grads,
        du_blocks,
        up_parts,
        down_parts,
        middle_parts,
        gate_sum,
        mix_grad,
    )


def finish_kernel(
    pack_all,
    mix_all,
    u,
    keep,
    middle,
    xz_grads,
    bcdt_grads,
    gated_gain,
    embedded,
    start,
    table_out,
    patch_out,
    in_out,
    out_out,
    local_out,
    query_out,
    key_out,
    value_out,
    attn_out,
    embedded_own,
    ids_all,
    patch_all,
    rows_of_four,
    sems,
):
    me = lax.axis_index(NARROW) * lax.axis_size(WIDE) + lax.axis_index(WIDE)
    own_rows = patch_out.shape[0]
    group = 128 // own_rows
    columns = pl.ds(pl.multiple_of(lax.div(me, group) * 128, 128), 128)
    copies = [
        pltpu.make_async_copy(embedded.at[:, columns], embedded_own, sems.at[0]),
        pltpu.make_async_copy(start.at[:, pl.ds(3 * STATE, 128)], ids_all, sems.at[1]),
        pltpu.make_async_copy(start.at[:, pl.ds(4 * STATE, D)], patch_all, sems.at[2]),
    ]
    for copy in copies:
        copy.start()
    for i, out in enumerate((query_out, key_out, value_out, attn_out)):
        out[...] = middle[:, i * D : (i + 1) * D]
    local_out[...] = middle[:, 4 * D :].T
    for pair in range(0, HEADS_M, 2):
        both = [xz_grads[pair + i].astype(FULL) for i in range(2)]
        first = pair * HEAD_M
        in_out[:, first : first + 128] = jnp.concatenate([v[:, HEAD_M:] for v in both], axis=1)
        in_out[:, DI + first : DI + first + 128] = jnp.concatenate(
            [v[:, :HEAD_M] for v in both], axis=1
        )
    in_out[:, 2 * DI : 2 * DI + 2 * STATE] = bcdt_grads[:, : 2 * STATE]
    in_out[:, 2 * DI + 2 * STATE :] = bcdt_grads[:, 2 * STATE : 2 * STATE + HEADS_M]
    scale = pack_all[:, D:].astype(FULL)[:, :HEAD_M]
    gain = head_columns(gated_gain, me)[:, :HEAD_M]
    gated = (u[...] * scale * gain).astype(LOW)
    out_out[...] = tn(gated, mix_all[...])
    copies[0].wait()
    copies[1].wait()
    grads = pack_all[:, :D]
    rows_of_four[...] = tn(embedded_own[...], grads)
    patch_out[...] = rows_of_four[pl.ds(pl.multiple_of(lax.rem(me, group) * own_rows, own_rows), own_rows), :]
    own_words = table_out.shape[0]
    count = pack_all.shape[0]
    lane = lax.broadcasted_iota(jnp.int32, (count, PATCH * own_words), 1)
    ids = jnp.zeros((count, PATCH * own_words), FULL)
    kept = jnp.zeros((count, PATCH * own_words), FULL)
    values = ids_all[...].astype(FULL)
    for k in range(PATCH):
        here = lax.div(lane, own_words) == k
        ids = jnp.where(here, values[:, k : k + 1], ids)
        kept = jnp.where(here, keep[:, k : k + 1], kept)
    words = (me * own_words + lax.rem(lane, own_words)).astype(FULL)
    sums = tn(jnp.where(ids == words, kept, 0.0).astype(LOW), grads)
    high = sums.astype(LOW)
    rest = (sums - high.astype(FULL)).astype(LOW)
    copies[2].wait()
    table = jnp.zeros(table_out.shape, FULL)
    for k in range(PATCH):
        rows = slice(k * own_words, (k + 1) * own_words)
        weight = patch_all[k * EMB : (k + 1) * EMB, :]
        table += nt(high[rows], weight) + nt(rest[rows], weight)
    table_out[...] = table


def finish(pack_all, mix_all, u, keep, middle, xz_grads, bcdt_grads, gated_gain, embedded, start):
    count = pack_all.shape[0]
    devices, own_rows = xz_grads.shape[:2]
    anywhere = pl.BlockSpec(memory_space=pl.ANY)

    def full(*shape):
        return jax.ShapeDtypeStruct(shape, FULL)

    return pl.pallas_call(
        finish_kernel,
        out_shape=[
            full(VOCAB // devices, EMB),
            full(own_rows, D),
            full(own_rows, 2 * DI + 2 * STATE + HEADS_M),
            full(DI // devices, D),
            full(EMB, own_rows),
        ]
        + [full(own_rows, D)] * 4,
        in_specs=[in_vmem()] * 8 + [anywhere] * 2,
        out_specs=[in_vmem()] * 9,
        scratch_shapes=[
            pltpu.VMEM((count, 128), LOW),
            pltpu.VMEM((count, 128), LOW),
            pltpu.VMEM((D, D), LOW),
            pltpu.VMEM((128, D), FULL),
            pltpu.SemaphoreType.DMA((3,)),
        ],
        compiler_params=pltpu.CompilerParams(vmem_limit_bytes=40 << 20),
        name="finish",
    )(pack_all, mix_all, u, keep, middle, xz_grads, bcdt_grads, gated_gain, embedded, start)


def patch_causal():
    row = lax.broadcasted_iota(jnp.int32, (BYTE_BLOCK, BYTE_BLOCK), 0)
    column = lax.broadcasted_iota(jnp.int32, (BYTE_BLOCK, BYTE_BLOCK), 1)
    return (lax.div(row, PATCH) == lax.div(column, PATCH)) & (row >= column)


def head_probs(q, k, causal):
    scores = jnp.where(causal, nt(q, k) * HEAD_A ** (-0.5), masked_score)
    grown = jnp.exp(scores - jnp.max(scores, axis=1, keepdims=True))
    return grown / jnp.sum(grown, axis=1, keepdims=True)


def of_head(block, half):
    lane = lax.broadcasted_iota(jnp.int32, block.shape, 1)
    return jnp.where(lax.div(lane, HEAD_A) == half, block, jnp.zeros_like(block))


def fetched(pack, places, blocks, sems):
    copies = []
    for i, place in enumerate(places):
        width = place.shape[1]
        start = blocks[i]
        copies.append(
            pltpu.make_async_copy(pack.at[:, pl.ds(start, width)], place, sems.at[i])
        )
        copies[-1].start()
    return [copy.wait for copy in copies]


def unit_rows(values):
    scale = lax.rsqrt(jnp.mean(values * values, axis=1, keepdims=True) + epsilon)
    return values * scale, scale


def norm_back(grad, gain, unit, scale):
    scaled = grad * gain
    return scale * (scaled - unit * jnp.mean(scaled * unit, axis=1, keepdims=True))


WEIGHT_STEP = 256


def attend_pairs(qkv, mixed):
    causal = patch_causal()
    blocks = qkv.shape[0] // BYTE_BLOCK

    def pair(i, carry):
        def lanes(part):
            start = part * D + i * (2 * HEAD_A)
            return pl.ds(pl.multiple_of(start, 2 * HEAD_A), 2 * HEAD_A)

        for block in range(blocks):
            rows = pl.ds(block * BYTE_BLOCK, BYTE_BLOCK)
            q, k, v = qkv[rows, lanes(0)], qkv[rows, lanes(1)], qkv[rows, lanes(2)]
            total = jnp.zeros(q.shape, FULL)
            for half in range(2):
                probs = head_probs(of_head(q, half), k, causal)
                total += nn(probs.astype(LOW), of_head(v, half))
            mixed[rows, lanes(0)] = total.astype(LOW)
        return carry

    lax.fori_loop(0, HEADS_A // 2, pair, 0)


def attend_pairs_back(qkv, heads_grad, qkv_grad):
    causal = patch_causal()
    blocks = qkv.shape[0] // BYTE_BLOCK
    scale = HEAD_A ** (-0.5)

    def pair(i, carry):
        def lanes(part):
            start = part * D + i * (2 * HEAD_A)
            return pl.ds(pl.multiple_of(start, 2 * HEAD_A), 2 * HEAD_A)

        for block in range(blocks):
            rows = pl.ds(block * BYTE_BLOCK, BYTE_BLOCK)
            q, k, v = qkv[rows, lanes(0)], qkv[rows, lanes(1)], qkv[rows, lanes(2)]
            g = heads_grad[rows, lanes(0)]
            dq = jnp.zeros(q.shape, FULL)
            dk = jnp.zeros(q.shape, FULL)
            dv = jnp.zeros(q.shape, FULL)
            for half in range(2):
                own_q, own_k, own_g = of_head(q, half), of_head(k, half), of_head(g, half)
                probs = head_probs(own_q, k, causal)
                dprobs = nt(own_g, v)
                dv += tn(probs.astype(LOW), own_g)
                dscores = probs * (dprobs - jnp.sum(probs * dprobs, axis=1, keepdims=True))
                dscores = dscores.astype(LOW)
                dq += nn(dscores, own_k)
                dk += tn(dscores, own_q)
            qkv_grad[rows, lanes(0)] = (dq * scale).astype(LOW)
            qkv_grad[rows, lanes(1)] = (dk * scale).astype(LOW)
            qkv_grad[rows, lanes(2)] = dv.astype(LOW)
        return carry

    lax.fori_loop(0, HEADS_A // 2, pair, 0)


def bytes_forward_kernel(
    u_blocks,
    mixed_in,
    gains,
    gated_gain,
    pack,
    gated_out,
    local_out,
    stream_out,
    normed_out,
    qkv,
    mixed,
    after_out,
    feed_out,
    w_out0,
    w_out1,
    w_local,
    w_q,
    w_k,
    w_v,
    w_attn,
    pieces,
    sems,
):
    places = (w_out0, w_out1, w_local, w_q, w_k, w_v, w_attn)
    blocks = [4 * D, 5 * D, 6 * D, 0, D, 2 * D, 3 * D]
    waits = fetched(pack, places, blocks, sems)
    patches = mixed_in.shape[0]
    half = HEAD_M // 2
    for i in range(2):
        for first in range(0, HEADS_M, 4):
            gated_out[i, :, first * half : (first + 4) * half] = jnp.concatenate(
                [
                    u_blocks[first + j].astype(FULL)[:, i * half : (i + 1) * half]
                    for j in range(4)
                ],
                axis=1,
            )
    held = [gated_out[0], gated_out[1]]
    square = sum(jnp.sum(v * v, axis=1, keepdims=True) for v in held)
    scale = lax.rsqrt(square / (2 * D) + epsilon)
    gated = [(held[i] * scale * gated_gain[i : i + 1, :]).astype(LOW) for i in range(2)]
    waits[0]()
    waits[1]()
    joined = mixed_in[...] + nn(gated[0], w_out0[...]) + nn(gated[1], w_out1[...])
    for k in range(PATCH):
        pieces[pl.ds(k, patches, stride=PATCH), :] = joined[:, k * EMB : (k + 1) * EMB]
    local = pieces[...].astype(LOW)
    local_out[...] = local
    waits[2]()
    stream = nt(local, w_local[...])
    stream_out[...] = stream
    normed = (unit_rows(stream)[0] * gains[0:1, :]).astype(LOW)
    normed_out[...] = normed
    for i, weight in enumerate((w_q, w_k, w_v)):
        waits[3 + i]()
        for first in range(0, D, WEIGHT_STEP):
            qkv[:, i * D + first : i * D + first + WEIGHT_STEP] = nn(
                normed, weight[:, first : first + WEIGHT_STEP]
            ).astype(LOW)
    attend_pairs(qkv, mixed)
    waits[6]()
    heads = mixed[...]
    for first in range(0, D, WEIGHT_STEP):
        columns = slice(first, first + WEIGHT_STEP)
        after_out[:, columns] = stream_out[:, columns] + nn(heads, w_attn[:, columns])
    feed_out[...] = (unit_rows(after_out[...])[0] * gains[1:2, :]).astype(LOW)


def bytes_forward(u_blocks, mixed_in, gains, gated_gain, pack):
    patches = mixed_in.shape[0]
    rows = patches * PATCH

    def full(shape, kind):
        return jax.ShapeDtypeStruct(shape, kind)

    return pl.pallas_call(
        bytes_forward_kernel,
        out_shape=[
            full((2, patches, D), FULL),
            full((rows, EMB), LOW),
            full((rows, D), FULL),
            full((rows, D), LOW),
            full((rows, 3 * D), LOW),
            full((rows, D), LOW),
            full((rows, D), FULL),
            full((rows, D), LOW),
        ],
        in_specs=[in_vmem()] * 4 + [pl.BlockSpec(memory_space=pl.ANY)],
        out_specs=[in_vmem()] * 8,
        scratch_shapes=[pltpu.VMEM((D, D), LOW)] * 2
        + [pltpu.VMEM((D, EMB), LOW)]
        + [pltpu.VMEM((D, D), LOW)] * 4
        + [pltpu.VMEM((rows, EMB), FULL), pltpu.SemaphoreType.DMA((7,))],
        compiler_params=pltpu.CompilerParams(vmem_limit_bytes=48 << 20),
        name="bytes_forward",
    )(u_blocks, mixed_in, gains, gated_gain, pack)


def bytes_backward_kernel(
    narrow,
    feed_in_grad,
    cotangent,
    keep,
    after,
    stream_in,
    normed_in,
    qkv,
    mixed,
    local_in,
    gated_rows,
    gains,
    gated_gain,
    pack,
    feed_parts,
    gate_parts,
    global_out,
    mix_out,
    scale_out,
    sums,
    gain_grads,
    gated_gain_grads,
    du_blocks,
    rows_out,
    gate_out,
    w_attn,
    w_q,
    w_k,
    w_v,
    w_local,
    w_out0,
    w_out1,
    after_grad,
    heads_grad,
    qkv_grad,
    pieces,
    parts_got,
    grads,
    grads_got,
    gate_got,
    sems,
    p_send,
    p_recv,
    t_send,
    t_recv,
    gate_sems,
):
    n, wide_place = lax.axis_index(NARROW), lax.axis_index(WIDE)
    core = lax.rem(wide_place, 2)
    twin = (n, wide_place + 1 - 2 * core)
    depth = gate_parts.shape[0]
    z_place = lax.div(wide_place, 2)
    line = LineSum(
        gate_parts, gate_got, gate_sems, z_place, depth, lambda there: (n, there * 2 + core)
    )

    def twin_copy(i, columns):
        return remote(
            grads.at[:, 1 - core, :, columns],
            grads_got.at[:, :, columns],
            t_send.at[i],
            t_recv.at[i],
            twin,
        )

    def give(i, columns, part):
        grads[:, :, :, columns] = part.astype(LOW).reshape(grads.shape[:3] + part.shape[1:])
        twin_copy(i, columns).start()

    def part_copy(k):
        peer = (square_peer(n, k), wide_place)
        return remote(feed_parts.at[k], parts_got.at[k], p_send.at[k - 1], p_recv.at[k - 1], peer)

    own_part = pltpu.make_async_copy(feed_parts.at[0], parts_got.at[0], sems.at[7])
    own_part.start()
    places = (w_attn, w_q, w_k, w_v, w_local, w_out0, w_out1)
    blocks = [3 * D, 0, D, 2 * D, 6 * D, 4 * D, 5 * D]
    waits = fetched(pack, places, blocks, sems)
    greet_lines(narrow, depth)
    line.start()
    for k in range(1, narrow):
        part_copy(k).start()
    patches = global_out.shape[0]
    unit, scale = unit_rows(after[...])
    grad = feed_in_grad[...].astype(LOW).astype(FULL)
    gain_grads[1:2, :] = jnp.sum(grad * unit, axis=0, keepdims=True)
    after_grad[...] = cotangent[...].astype(FULL) * keep[0] + norm_back(
        grad, gains[1:2, :], unit, scale
    )
    attn_grad = after_grad[...].astype(LOW)
    waits[0]()
    for first in range(0, D, WEIGHT_STEP):
        columns = slice(first, first + WEIGHT_STEP)
        heads_grad[:, columns] = nt(attn_grad, w_attn[columns, :]).astype(LOW)
        give(
            (3 * D + first) // WEIGHT_STEP,
            pl.ds(3 * D + first, WEIGHT_STEP),
            tn(mixed[...], attn_grad[:, columns]),
        )
    attend_pairs_back(qkv, heads_grad, qkv_grad)
    normed_grad = jnp.zeros(after_grad.shape, FULL)
    for i, weight in enumerate((w_q, w_k, w_v)):
        waits[1 + i]()
        normed_grad += nt(qkv_grad[:, i * D : (i + 1) * D], weight[...])
    unit, scale = unit_rows(stream_in[...])
    gain_grads[0:1, :] = jnp.sum(normed_grad * unit, axis=0, keepdims=True)
    stream_grad = (after_grad[...] + norm_back(normed_grad, gains[0:1, :], unit, scale)).astype(LOW)
    waits[4]()
    pieces[...] = nn(stream_grad, w_local[...])
    for k in range(PATCH):
        global_out[:, k * EMB : (k + 1) * EMB] = pieces[pl.ds(k, patches, stride=PATCH), :]
    mix_grad = global_out[...].astype(LOW)
    mix_out[...] = mix_grad
    waits[5]()
    waits[6]()
    inner = [nt(mix_grad, w_out0[...]), nt(mix_grad, w_out1[...])]
    held = [gated_rows[0], gated_rows[1]]
    square = sum(jnp.sum(v * v, axis=1, keepdims=True) for v in held)
    scale = lax.rsqrt(square / (2 * D) + epsilon)
    units = [v * scale for v in held]
    scaled = [inner[i] * gated_gain[i : i + 1, :] for i in range(2)]
    mean = sum(jnp.sum(scaled[i] * units[i], axis=1, keepdims=True) for i in range(2)) / (2 * D)
    for i in range(2):
        gated_gain_grads[i : i + 1, :] = jnp.sum(inner[i] * units[i], axis=0, keepdims=True)
    scale_out[...] = jnp.broadcast_to(scale, scale_out.shape)
    rows_grads = [scale * (scaled[i] - units[i] * mean) for i in range(2)]
    half = HEAD_M // 2
    for head in range(HEADS_M):
        lanes = slice(head * half, (head + 1) * half)
        du_blocks[head] = jnp.concatenate([part[:, lanes] for part in rows_grads], axis=1).astype(LOW)
    give(4 * D // WEIGHT_STEP, pl.ds(4 * D, EMB), tn(stream_grad, local_in[...]))

    def weight_grads(i, carry):
        columns = pl.ds(pl.multiple_of(i * WEIGHT_STEP, WEIGHT_STEP), WEIGHT_STEP)
        give(i, columns, tn(normed_in[...], qkv_grad[:, columns]))
        return carry

    lax.fori_loop(0, 3 * D // WEIGHT_STEP, weight_grads, 0)
    own_part.wait()
    for k in range(1, narrow):
        part_copy(k).wait_recv()
    for first in range(0, D, WEIGHT_STEP):
        columns = slice(first, first + WEIGHT_STEP)
        feed = parts_got[0, :, columns].astype(FULL)
        for k in range(1, narrow):
            feed += parts_got[k, :, columns].astype(FULL)
        feed = feed.astype(LOW).astype(FULL)
        rows_out[:, columns] = ((after[:, columns] + feed) * keep[0]).astype(LOW)

    def add_twin(i, columns):
        twin_copy(i, columns).wait_recv()
        sums[:, :, columns] = (
            grads[:, core, :, columns].astype(FULL) + grads_got[:, :, columns].astype(FULL)
        ).astype(LOW)

    def add_one(i, carry):
        add_twin(i, pl.ds(pl.multiple_of(i * WEIGHT_STEP, WEIGHT_STEP), WEIGHT_STEP))
        return carry

    def end_one(i, carry):
        twin_copy(i, pl.ds(pl.multiple_of(i * WEIGHT_STEP, WEIGHT_STEP), WEIGHT_STEP)).wait_send()
        return carry

    steps = 4 * D // WEIGHT_STEP
    add_twin(steps, pl.ds(4 * D, EMB))
    lax.fori_loop(0, steps, add_one, 0)
    line.arrive()
    gate_out[...] = line.total().astype(LOW)
    line.finish()
    twin_copy(steps, pl.ds(4 * D, EMB)).wait_send()
    lax.fori_loop(0, steps, end_one, 0)
    for k in range(1, narrow):
        part_copy(k).wait_send()


def bytes_backward(
    feed_in_grad,
    cotangent,
    keep,
    after,
    stream,
    normed,
    qkv,
    mixed,
    local,
    gated_rows,
    gains,
    gated_gain,
    pack,
    feed_parts,
    gate_parts,
    collective_id,
):
    narrow = feed_parts.shape[0]
    every = 4 * D + EMB
    rows = after.shape[0]
    patches = rows // PATCH

    def full(shape, kind):
        return jax.ShapeDtypeStruct(shape, kind)

    return pl.pallas_call(
        partial(bytes_backward_kernel, narrow),
        out_shape=[
            full((patches, D), FULL),
            full((patches, D), LOW),
            full((patches, 128), FULL),
            full((HEADS_M // 2, D // HEADS_M, every), LOW),
            full((2, D), FULL),
            full((2, D), FULL),
            full((HEADS_M, patches, HEAD_M), LOW),
            full((rows, D), LOW),
            full(gate_parts.shape[1:], LOW),
        ],
        in_specs=[in_vmem()] * 12 + [pl.BlockSpec(memory_space=pl.ANY)] * 3,
        out_specs=[in_vmem()] * 9,
        scratch_shapes=[pltpu.VMEM((D, D), LOW)] * 4
        + [pltpu.VMEM((D, EMB), LOW)]
        + [pltpu.VMEM((D, D), LOW)] * 2
        + [
            pltpu.VMEM((rows, D), FULL),
            pltpu.VMEM((rows, D), LOW),
            pltpu.VMEM((rows, 3 * D), LOW),
            pltpu.VMEM((rows, EMB), FULL),
            pltpu.VMEM((narrow, rows, D), LOW),
            pltpu.VMEM((HEADS_M // 2, 2, D // HEADS_M, every), LOW),
            pltpu.VMEM((HEADS_M // 2, D // HEADS_M, every), LOW),
            pltpu.VMEM(gate_parts.shape, LOW),
            pltpu.SemaphoreType.DMA((8,)),
            pltpu.SemaphoreType.DMA((narrow - 1,)),
            pltpu.SemaphoreType.DMA((narrow - 1,)),
            pltpu.SemaphoreType.DMA((4 * D // WEIGHT_STEP + 1,)),
            pltpu.SemaphoreType.DMA((4 * D // WEIGHT_STEP + 1,)),
            pltpu.SemaphoreType.DMA((2 * gate_parts.shape[0],)),
        ],
        compiler_params=pltpu.CompilerParams(
            collective_id=collective_id, has_side_effects=True, vmem_limit_bytes=60 << 20
        ),
        name="bytes_backward",
    )(
        feed_in_grad,
        cotangent,
        keep,
        after,
        stream,
        normed,
        qkv,
        mixed,
        local,
        gated_rows,
        gains,
        gated_gain,
        pack,
        feed_parts,
        gate_parts,
    )


def feed_kernel(narrow, x_in, g_own, g_others, keep, *refs):
    gate_in, up_in, down_in, f_out, gx_out, gate_sum, up_sum, down_sum = refs[:8]
    wg, wu, wd, x, xt, g, hid, gg, gu, sent, got = refs[8:19]
    gate_twin, up_twin, down_twin, gate_got, up_got, down_got = refs[19:25]
    w_sem, g_sem, x_sem, x_send, x_recv, r_send, r_recv, t_send, t_recv = refs[25:]
    n, wide_place = lax.axis_index(NARROW), lax.axis_index(WIDE)
    core = lax.rem(wide_place, 2)
    twin = (n, wide_place + 1 - 2 * core)
    barrier = pltpu.get_barrier_semaphore()
    pl.semaphore_signal(barrier, inc=1, device_id=twin, device_id_type=MESH)
    for k in range(1, narrow):
        peer = (lax.rem(n + k, narrow), wide_place)
        pl.semaphore_signal(barrier, inc=1, device_id=peer, device_id_type=MESH)
    places, width, share = gate_in.shape
    rows = x_in.shape[0]
    hidden = places * share
    depth = places // 2
    chunk = 2 * share
    own_x = pltpu.make_async_copy(x_in, x.at[0], x_sem)
    own_x.start()
    g_copies = [
        pltpu.make_async_copy(g_own, g.at[0], g_sem.at[0]),
        pltpu.make_async_copy(
            g_others.at[pl.ds(1, narrow - 1)], g.at[pl.ds(1, narrow - 1)], g_sem.at[1]
        ),
    ]
    w_copies = [pltpu.make_async_copy(down_in, wd, w_sem.at[2 * places])]
    for place in range(places):
        units = slice(place * share, (place + 1) * share)
        w_copies.append(pltpu.make_async_copy(gate_in.at[place], wg.at[:, units], w_sem.at[place]))
        w_copies.append(
            pltpu.make_async_copy(up_in.at[place], wu.at[:, units], w_sem.at[places + place])
        )
    g_copies[0].start()
    for copy in w_copies:
        copy.start()
    for copy in g_copies[1:]:
        copy.start()
    pl.semaphore_wait(barrier, narrow)

    share_x = SquareShare(x_in, x, x_send, x_recv, n, wide_place)

    def r_copy(k):
        peer = (square_peer(n, k), wide_place)
        return remote(sent.at[k - 1], got.at[k - 1], r_send.at[k - 1], r_recv.at[k - 1], peer)

    share_x.start()
    own_x.wait()
    for copy in w_copies:
        copy.wait()
    for copy in g_copies:
        copy.wait()

    def block(k, carry):
        @pl.when(k == 1)
        def _():
            share_x.relay(0)
            share_x.relay(1)

        @pl.when(k == narrow - 1)
        def _():
            share_x.arrive()

        xk = x[k]
        gk = (g[k].astype(FULL) * keep[k]).astype(LOW)
        g[k] = gk
        xt[:, pl.ds(pl.multiple_of(k * rows, rows), rows)] = xk.T
        for first in range(0, hidden, chunk):
            units = slice(first, first + chunk)
            gate = nn(xk, wg[:, units])
            up = nn(xk, wu[:, units])
            dhid = nt(gk, wd[units, :])
            s = jax.nn.sigmoid(gate)
            act = gate * s
            hid[k, :, units] = (act * up).astype(LOW)
            gg[k, :, units] = (dhid * up * s * (1.0 + gate * (1.0 - s))).astype(LOW)
            gu[k, :, units] = (dhid * act).astype(LOW)
        ggk, guk, hidk = gg[k], gu[k], hid[k]
        for first in range(0, width, chunk):
            columns = slice(first, first + chunk)
            gx = nt(ggk, wg[columns, :]) + nt(guk, wu[columns, :])

            @pl.when(k == 0)
            def _():
                gx_out[:, columns] = gx

            @pl.when(k > 0)
            def _():
                sent[k - 1, :, columns] = gx.astype(LOW)

        @pl.when(k > 0)
        def _():
            r_copy(k).start()

        for first in range(0, width, chunk):
            columns = slice(first, first + chunk)
            f_out[k, :, columns] = nn(hidk, wd[:, columns]).astype(LOW)
        return carry

    lax.fori_loop(0, narrow, block, 0)

    def units_of(j, of_core):
        start = (2 * j + of_core) * share
        return pl.ds(pl.multiple_of(start, share), share)

    def two_places(left, j, of_core):
        pair = [left[:, :, units_of(2 * j + i, of_core)] for i in range(2)]
        return jnp.concatenate(pair, axis=2).reshape(narrow * rows, chunk)

    def columns_grads(left, j, of_core):
        total = nn(xt[...], two_places(left, j, of_core))
        return total[:, :share], total[:, share:]

    def rows_grads(j, of_core):
        total = tn(two_places(hid, j, of_core), g[...].reshape(narrow * rows, width))
        return total[:share], total[share:]

    outs = (gate_twin, up_twin, down_twin)
    ins = (gate_got, up_got, down_got)

    def t_copy(i, j):
        return remote(outs[i].at[j], ins[i].at[j], t_send.at[i, j], t_recv.at[i, j], twin)

    def for_twin(j, carry):
        for i, left in enumerate((gg, gu)):
            for half, part in enumerate(columns_grads(left, j, 1 - core)):
                outs[i][2 * j + half] = part.astype(LOW)
                t_copy(i, 2 * j + half).start()
        for half, part in enumerate(rows_grads(j, 1 - core)):
            outs[2][2 * j + half] = part.astype(LOW)
            t_copy(2, 2 * j + half).start()
        return carry

    def for_own(j, carry):
        for i, (left, total) in enumerate(((gg, gate_sum), (gu, up_sum))):
            for half, part in enumerate(columns_grads(left, j, core)):
                t_copy(i, 2 * j + half).wait_recv()
                total[2 * j + half] = (part + ins[i][2 * j + half].astype(FULL)).astype(LOW)
        for half, part in enumerate(rows_grads(j, core)):
            t_copy(2, 2 * j + half).wait_recv()
            down_sum[2 * j + half] = (part + ins[2][2 * j + half].astype(FULL)).astype(LOW)
        return carry

    lax.fori_loop(0, depth // 2, for_twin, 0)
    lax.fori_loop(0, depth // 2, for_own, 0)
    for k in range(1, narrow):
        r_copy(k).wait_recv()
        gx_out[...] += got[k - 1].astype(FULL)
    share_x.finish()
    for k in range(1, narrow):
        r_copy(k).wait_send()
    for i in range(3):
        for j in range(depth):
            t_copy(i, j).wait_send()


def feed_forward_back(x_own, g_own, g_others, keep, gate_all, up_all, down_all, collective_id):
    narrow = keep.shape[0]
    rows, width = x_own.shape
    places, _, share = gate_all.shape
    hidden, depth = places * share, places // 2
    dma = pltpu.SemaphoreType.DMA
    anywhere = pl.BlockSpec(memory_space=pl.ANY)

    def low(*shape):
        return pltpu.VMEM(shape, LOW)

    sums = [(depth, width, share), (depth, width, share), (depth, share, width)]
    return pl.pallas_call(
        partial(feed_kernel, narrow),
        out_shape=[
            jax.ShapeDtypeStruct((narrow, rows, width), LOW),
            jax.ShapeDtypeStruct((rows, width), FULL),
        ]
        + [jax.ShapeDtypeStruct(shape, LOW) for shape in sums],
        in_specs=[anywhere] * 3 + [in_vmem()] + [anywhere] * 3,
        out_specs=[in_vmem()] * 5,
        scratch_shapes=[
            low(width, hidden),
            low(width, hidden),
            low(hidden, width),
            low(narrow, rows, width),
            low(width, narrow * rows),
            low(narrow, rows, width),
            low(narrow, rows, hidden),
            low(narrow, rows, hidden),
            low(narrow, rows, hidden),
            low(narrow - 1, rows, width),
            low(narrow - 1, rows, width),
        ]
        + [low(*shape) for shape in sums + sums]
        + [
            dma((2 * places + 1,)),
            dma((2,)),
            dma,
            dma((narrow,)),
            dma((narrow,)),
            dma((narrow - 1,)),
            dma((narrow - 1,)),
            dma((3, depth)),
            dma((3, depth)),
        ],
        compiler_params=pltpu.CompilerParams(
            collective_id=collective_id, has_side_effects=True, vmem_limit_bytes=44 << 20
        ),
        name="feed",
    )(x_own, g_own, g_others, keep, gate_all, up_all, down_all)


def per_device_heads(
    byte_ids,
    doc_patches,
    pad_bytes,
    byte_table,
    patch_weight,
    gain_mix,
    in_weight,
    conv_weight,
    conv_bias,
    step_bias,
    log_rate,
    skip_gain,
    gated_gain,
    out_weight,
    local_weight,
    gain_attn,
    query_weight,
    key_weight,
    value_weight,
    attn_weight,
    feed_gain,
    gate_weight,
    up_weight,
    down_weight,
    cotangent,
):
    narrow, wide = lax.axis_size(NARROW), lax.axis_size(WIDE)
    devices = narrow * wide
    device = lax.axis_index(BOTH)
    rows = byte_ids.shape[0]
    patches = rows // PATCH
    everything = devices * patches
    own_rows = patch_weight.shape[0]
    hidden_width = gate_weight.shape[1]
    share = hidden_width // narrow

    ids_low = byte_ids.astype(LOW).reshape(patches, PATCH)
    bcdt_width = 2 * STATE + HEADS_M
    start_pack = jnp.concatenate(
        [
            jnp.pad(in_weight[:, 2 * DI :], ((0, 0), (0, 96))),
            jnp.pad(ids_low, ((0, 0), (0, 120))),
            patch_weight,
        ],
        axis=1,
    )
    xz_blocks = jnp.concatenate(
        [
            in_weight[:, DI : 2 * DI].reshape(own_rows, HEADS_M, HEAD_M),
            in_weight[:, :DI].reshape(own_rows, HEADS_M, HEAD_M),
        ],
        axis=2,
    ).transpose(1, 0, 2)
    middle_pack = jnp.concatenate(
        [
            query_weight,
            key_weight,
            value_weight,
            attn_weight,
            out_weight[:own_rows],
            out_weight[own_rows:],
            local_weight.T,
        ],
        axis=1,
    )
    numbers = (step_bias, log_rate, skip_gain)
    conv = (conv_weight, conv_bias[None])
    front, start_all, xz_weight, gate_all, up_all, down_all, middle_all, others = mixer_front(
        (doc_patches, pad_bytes) + numbers,
        gain_mix[None],
        *conv,
        (
            start_pack,
            byte_table.astype(FULL),
            xz_blocks,
            gate_weight,
            up_weight,
            down_weight,
            middle_pack,
            cotangent,
        ),
        5,
    )
    embedded, normed_all, xz, bc, dt, u, y, states, mixed_in, u_blocks, marks, keep_rows, keep_all = front
    half = HEAD_M // 2
    gated_gain_split = gated_gain.reshape(devices, 2, half).transpose(1, 0, 2).reshape(2, D)

    byte_gains = jnp.stack([gain_attn, feed_gain])
    (
        gated_rows,
        local_rows,
        stream,
        normed_attn,
        qkv,
        mixed_heads,
        after_attn,
        normed_feed,
    ) = bytes_forward(u_blocks, mixed_in, byte_gains, gated_gain_split, middle_all)
    feed_parts, feed_in_grad, gate_parts, up_parts, down_parts = feed_forward_back(
        normed_feed, cotangent, others, keep_rows, gate_all, up_all, down_all, 2
    )

    (
        global_grad,
        mix_grad,
        gated_scale,
        middle_parts,
        byte_gain_grads,
        gated_gain_grads,
        du_blocks,
        out_rows,
        gate_sum,
    ) = bytes_backward(
        feed_in_grad,
        cotangent,
        keep_rows,
        after_attn,
        stream,
        normed_attn,
        qkv,
        mixed_heads,
        local_rows,
        gated_rows,
        byte_gains,
        gated_gain_split,
        middle_all,
        feed_parts,
        gate_parts,
        4,
    )
    middle_parts = middle_parts.reshape(narrow, wide // 2, own_rows, -1)

    (
        end_pack,
        sums_pack,
        bcdt_grads,
        xz_grads,
        up_sum,
        down_sum,
        middle_sums,
        grad_gate,
        mix_grad_all,
    ) = mixer_backward(
        numbers,
        xz,
        bc,
        dt,
        marks,
        *conv,
        y,
        states,
        normed_all,
        xz_weight,
        start_all,
        mixed_in,
        global_grad,
        gain_mix[None],
        gated_scale,
        byte_gain_grads,
        gated_gain_grads,
        du_blocks,
        up_parts,
        down_parts,
        middle_parts,
        gate_sum,
        mix_grad,
        3,
    )
    mix_grad_all = mix_grad_all.reshape(everything, D)

    end_all, sums_all, middle_sums, grad_up, grad_down = end_gather(
        end_pack, sums_pack, middle_sums, up_sum, down_sum, 1
    )
    (
        grad_table,
        grad_patch,
        grad_in,
        grad_out,
        grad_local,
        grad_query,
        grad_key,
        grad_value,
        grad_attn,
    ) = finish(
        end_all,
        mix_grad_all,
        u,
        keep_all,
        middle_sums,
        xz_grads,
        bcdt_grads,
        gated_gain[None],
        embedded,
        start_all,
    )
    small = jnp.sum(sums_all[:, :SUM_ROWS], axis=0).reshape(-1)
    gain_grads = jnp.split(small[: 3 * D + DI], [D, D + DI, 2 * D + DI])
    gain_grads[1] = gain_grads[1].reshape(2, devices, half).transpose(1, 0, 2).reshape(DI)
    conv_own = sums_all[:, SUM_ROWS : SUM_ROWS + CONV + 1, :HEAD_M].transpose(1, 0, 2)
    conv_grads = jnp.concatenate(
        [conv_own.reshape(CONV + 1, DI), small[3 * D + DI :].reshape(CONV + 1, 2 * STATE)], axis=1
    )
    number_grads = sums_all[:, SUM_ROWS + CONV + 1, :3].T
    return (
        out_rows,
        grad_table,
        grad_patch,
        gain_grads[0],
        grad_in,
        conv_grads[:CONV],
        conv_grads[CONV],
        number_grads[0],
        number_grads[1],
        number_grads[2],
        gain_grads[1],
        grad_out,
        grad_local,
        gain_grads[2],
        grad_query,
        grad_key,
        grad_value,
        grad_attn,
        gain_grads[3],
        grad_gate,
        grad_up,
        grad_down,
    )


def solution(mesh):
    placed = (
        P((NARROW, WIDE)),
        P(),
        P(),
        P((NARROW, WIDE), None),
        P((NARROW, WIDE), None),
        P(),
        P((NARROW, WIDE), None),
        P(),
        P(),
        P(),
        P(),
        P(),
        P(),
        P((NARROW, WIDE), None),
        P(None, (NARROW, WIDE)),
        P(),
        P((NARROW, WIDE), None),
        P((NARROW, WIDE), None),
        P((NARROW, WIDE), None),
        P((NARROW, WIDE), None),
        P(),
        P(NARROW, WIDE),
        P(NARROW, WIDE),
        P(WIDE, NARROW),
        P((NARROW, WIDE), None),
    )
    return jax.shard_map(
        per_device_heads if mesh.size == HEADS_M else per_device_rows,
        mesh=mesh,
        in_specs=placed,
        out_specs=(
            P((NARROW, WIDE), None),
            P((NARROW, WIDE), None),
            P((NARROW, WIDE), None),
            P(),
            P((NARROW, WIDE), None),
            P(),
            P(),
            P(),
            P(),
            P(),
            P(),
            P((NARROW, WIDE), None),
            P(None, (NARROW, WIDE)),
            P(),
            P((NARROW, WIDE), None),
            P((NARROW, WIDE), None),
            P((NARROW, WIDE), None),
            P((NARROW, WIDE), None),
            P(),
            P(NARROW, WIDE),
            P(NARROW, WIDE),
            P(WIDE, NARROW),
        ),
        check_vma=False,
    )
```

```python
from functools import partial

import jax
import jax.numpy as jnp
from jax import lax
from jax.experimental import pallas as pl
from jax.experimental.pallas import tpu as pltpu
from jax.sharding import PartitionSpec as P

NARROW = "narrow"
WIDE = "wide"
D = 1024
PATCH = 8
EMB = 128
VOCAB = 256
HEADS_M = 32
HEAD_M = 64
DI = 2048
STATE = 128
CONV = 4
HEADS_A = 16
HEAD_A = 64


epsilon = 1e-05
highest = lax.Precision.HIGHEST
masked_score = -1e30


def running_sum(x):
    place = jnp.arange(x.shape[0])
    seen = place[:, None] >= place[None, :]
    if x.ndim == 1:
        return jnp.sum(jnp.where(seen, x[None, :], 0), axis=1).astype(x.dtype)
    return jnp.dot(seen.astype(x.dtype), x, precision=highest)


def passed_along(x, axis, by):
    peers = lax.axis_size(axis)
    pairs = [(i, i + by) for i in range(peers) if 0 <= i + by < peers]
    return lax.ppermute(x, axis, pairs)


def prefix_2(x, axis, join, neutral):
    place = lax.axis_index(axis)
    gathered = jax.tree.map(
        lambda a, kind: lax.all_gather(a.astype(kind), axis), x, (jnp.bfloat16, jnp.bfloat16)
    )
    state = jax.tree.map(lambda a, e: jnp.zeros_like(a) + jnp.asarray(e, a.dtype), x, neutral)

    def prefix_one(hop, state):
        return join(
            state,
            jax.tree.map(
                lambda a, own: lax.dynamic_index_in_dim(a, hop, 0, False).astype(own.dtype),
                gathered,
                x,
            ),
        )

    return lax.fori_loop(0, place, prefix_one, state)


def carried_in_2(x, axis, join, neutral):
    count = lax.axis_size(axis)
    place = lax.axis_index(axis)
    ahead = count - 1 - place
    gathered = jax.tree.map(
        lambda a, kind: lax.all_gather(a.astype(kind), axis),
        x,
        jax.tree.map(lambda a: jnp.bfloat16 if a.dtype == jnp.float32 else a.dtype, x),
    )
    state = jax.tree.map(lambda a, e: jnp.zeros_like(a) + jnp.asarray(e, a.dtype), x, neutral)

    def carried_one(hop, state):
        source = count - 1 - hop
        return join(
            state,
            jax.tree.map(
                lambda a, own: lax.dynamic_index_in_dim(a, source, 0, False).astype(own.dtype),
                gathered,
                x,
            ),
        )

    return lax.fori_loop(0, ahead, carried_one, state)


def root_norm(values, gain):
    return values * lax.rsqrt(jnp.mean(values * values, axis=-1, keepdims=True) + epsilon) * gain


def patch_layout(doc_patches, pad_bytes, first_index, patch_count):
    patch_index = first_index + jnp.arange(patch_count, dtype=jnp.int32)
    doc_ends = running_sum(doc_patches)
    doc_index = jnp.arange(doc_patches.shape[0], dtype=jnp.int32)
    segment = jnp.sum((patch_index[:, None] >= doc_ends[None, :]).astype(jnp.int32), axis=1)
    owner_mask = segment[:, None] == doc_index[None, :]
    last_end = jnp.sum(jnp.where(owner_mask, doc_ends[None, :] - 1, 0), axis=1)
    doc_starts = jnp.sum(jnp.where(owner_mask, (doc_ends - doc_patches)[None, :], 0), axis=1)
    pad_count = jnp.sum(jnp.where(owner_mask, pad_bytes[None, :], 0), axis=1)
    offset = jnp.arange(PATCH, dtype=jnp.int32)
    padded = (patch_index == last_end)[:, None] & (offset[None, :] >= PATCH - pad_count[:, None])
    keep_mask = 1.0 - padded.astype(jnp.float32).reshape(-1)
    return (segment, (patch_index == doc_starts).astype(jnp.int32), keep_mask)


def ssd_terms(layout, projected, rim_rows, small_params):
    conv_weight, conv_bias, step_bias, log_rate, skip_gain = small_params
    segment, rim_segment, first_patch = layout
    conv_in = projected[:, DI : 2 * DI + 2 * STATE]
    patch_count = conv_in.shape[0]
    padded = jnp.concatenate([rim_rows, conv_in], 0)
    padded_seg = jnp.concatenate([rim_segment, segment], 0)
    conv_sum = conv_bias
    for conv_tap in range(CONV):
        same_doc = (padded_seg[conv_tap : conv_tap + patch_count] == segment).astype(jnp.float32)[
            :, None
        ]
        conv_sum = (
            conv_sum + conv_weight[conv_tap] * padded[conv_tap : conv_tap + patch_count] * same_doc
        )
    activated = jax.nn.silu(conv_sum)
    values = activated[:, :DI].reshape(patch_count, HEADS_M, HEAD_M)
    input_map = activated[:, DI : DI + STATE]
    output_map = activated[:, DI + STATE :]
    time_steps = jax.nn.softplus(projected[:, 2 * DI + 2 * STATE :] + step_bias)
    cumulative = running_sum(-time_steps * jnp.exp(log_rate))
    no_reset = (running_sum(first_patch) == 0).astype(jnp.float32)
    return (values, input_map, output_map, time_steps, cumulative, no_reset)


def local_state(layout, projected, rim_rows, small_params):
    values, input_map, output_map, time_steps, cumulative, no_reset = ssd_terms(
        layout, projected, rim_rows, small_params
    )
    segment = layout[0]
    decay_tail = (
        jnp.exp(cumulative[-1][None, :] - cumulative)
        * (segment == segment[-1]).astype(jnp.float32)[:, None]
        * time_steps
    )
    state_local = jnp.einsum("sh,shp,sn->hpn", decay_tail, values, input_map, precision=highest)
    decay_total = jnp.exp(cumulative[-1]) * no_reset[-1]
    return (decay_total, state_local)


def mixer_output(layout, projected, rim_rows, small_params, incoming, gated_gain):
    values, input_map, output_map, time_steps, cumulative, no_reset = ssd_terms(
        layout, projected, rim_rows, small_params
    )
    segment = layout[0]
    patch_count = values.shape[0]
    position = jnp.arange(patch_count)
    visible = (segment[:, None] == segment[None, :]) & (position[:, None] >= position[None, :])
    log_gap = jnp.where(visible[:, :, None], cumulative[:, None, :] - cumulative[None, :, :], 0.0)
    inner = jnp.dot(output_map, input_map.T, precision=highest)
    weight = (
        jnp.exp(log_gap)
        * visible[:, :, None].astype(jnp.float32)
        * time_steps[None, :, :]
        * inner[:, :, None]
    )
    within = jnp.einsum("tsh,shp->thp", weight, values, precision=highest)
    carried_in = (
        jnp.einsum("tn,hpn->thp", output_map, incoming, precision=highest)
        * (jnp.exp(cumulative) * no_reset[:, None])[:, :, None]
    )
    result = (within + carried_in + small_params[4][None, :, None] * values).reshape(
        patch_count, DI
    )
    gated_rows = result * jax.nn.silu(projected[:, :DI])
    return root_norm(gated_rows, gated_gain)


def combine_states(earlier, following):
    return (earlier[0] * following[0], following[0][:, None, None] * earlier[1] + following[1])


def attend(stream, gain_attn, query_all, key_all, value_all):
    head_shape = (-1, PATCH, HEADS_A, HEAD_A)
    normed_attn = root_norm(stream, gain_attn).astype(jnp.bfloat16)
    queries = jnp.dot(normed_attn, query_all, preferred_element_type=jnp.float32).astype(
        jnp.bfloat16
    )
    key_rows = jnp.dot(normed_attn, key_all, preferred_element_type=jnp.float32).astype(
        jnp.bfloat16
    )
    value_rows = jnp.dot(normed_attn, value_all, preferred_element_type=jnp.float32).astype(
        jnp.bfloat16
    )
    scores = jnp.einsum(
        "pqhe,pkhe->phqk",
        queries.reshape(head_shape),
        key_rows.reshape(head_shape),
        preferred_element_type=jnp.float32,
    ) * HEAD_A ** (-0.5)
    position = jnp.arange(PATCH)
    causal = position[:, None] >= position[None, :]
    attn_probs = jax.nn.softmax(jnp.where(causal, scores, masked_score), axis=-1)
    mixed_heads = jnp.einsum(
        "phqk,pkhe->pqhe",
        attn_probs.astype(jnp.bfloat16),
        value_rows.reshape(head_shape),
        preferred_element_type=jnp.float32,
    )
    mixed_heads = mixed_heads.reshape(stream.shape[0], -1).astype(jnp.bfloat16)
    return (normed_attn, queries, key_rows, value_rows, attn_probs, mixed_heads)


def spread(values):
    by_rows = lax.all_to_all(values, NARROW, split_axis=1, concat_axis=0, tiled=True)
    return lax.all_gather(by_rows, WIDE, axis=0, tiled=True)


def collect(term_fn, row_count):
    summed = lax.psum_scatter(
        term_fn(jnp.int32(0), row_count * lax.axis_size(WIDE)).astype(jnp.bfloat16),
        WIDE,
        scatter_dimension=0,
        tiled=True,
    )
    return lax.all_to_all(summed, NARROW, split_axis=0, concat_axis=1, tiled=True)


def narrow_total(partial_rows):
    return lax.psum(partial_rows, NARROW).astype(jnp.float32)


def silu_back(gate_up, hidden_grad, hidden_width):
    gate_rows = gate_up[:, :hidden_width]
    up_rows = gate_up[:, hidden_width:]
    sigmoid = jax.nn.sigmoid(gate_rows)
    gate_grad = hidden_grad * up_rows * sigmoid * (1.0 + gate_rows * (1.0 - sigmoid))
    up_grad = hidden_grad * gate_rows * sigmoid
    return jnp.concatenate([gate_grad, up_grad], axis=1)


def per_device_rows(
    byte_ids,
    doc_patches,
    pad_bytes,
    byte_table,
    patch_weight,
    gain_mix,
    in_weight,
    conv_weight,
    conv_bias,
    step_bias,
    log_rate,
    skip_gain,
    gated_gain,
    out_weight,
    local_weight,
    gain_attn,
    query_weight,
    key_weight,
    value_weight,
    attn_weight,
    feed_gain,
    gate_weight,
    up_weight,
    down_weight,
    cotangent,
):
    byte_rows = byte_ids.shape[0]
    patches = byte_rows // PATCH
    device = lax.axis_index((NARROW, WIDE))
    wide_count = lax.axis_size(WIDE)
    segment, first_patch, keep_mask = patch_layout(
        doc_patches, pad_bytes, device * patches, patches
    )
    rim_segment = patch_layout(doc_patches, pad_bytes, device * patches - (CONV - 1), CONV - 1)[0]
    layout = (segment, rim_segment, first_patch)
    gathered = (
        lax.all_gather(byte_table, (NARROW, WIDE), axis=0, tiled=True),
        lax.all_gather(patch_weight, (NARROW, WIDE), axis=0, tiled=True),
        lax.all_gather(in_weight, (NARROW, WIDE), axis=0, tiled=True),
        lax.all_gather(out_weight, (NARROW, WIDE), axis=0, tiled=True),
        lax.all_gather(local_weight, (NARROW, WIDE), axis=1, tiled=True),
        lax.all_gather(query_weight, (NARROW, WIDE), axis=0, tiled=True),
        lax.all_gather(key_weight, (NARROW, WIDE), axis=0, tiled=True),
        lax.all_gather(value_weight, (NARROW, WIDE), axis=0, tiled=True),
        lax.all_gather(attn_weight, (NARROW, WIDE), axis=0, tiled=True),
    )
    table_all, patch_all, in_all, out_all, local_all, query_all, key_all, value_all, attn_all = (
        gathered
    )
    onehot = (byte_ids[:, None] == jnp.arange(VOCAB, dtype=jnp.int32)[None, :]).astype(jnp.bfloat16)
    embedded = (
        (jnp.dot(onehot, table_all, preferred_element_type=jnp.float32) * keep_mask[:, None])
        .astype(jnp.bfloat16)
        .reshape(patches, D)
    )
    mixed_in = jnp.dot(embedded, patch_all, preferred_element_type=jnp.float32)
    normed_mix = root_norm(mixed_in, gain_mix).astype(jnp.bfloat16)
    projected = jnp.dot(normed_mix, in_all, preferred_element_type=jnp.float32).astype(jnp.bfloat16)
    rim_rows = passed_along(
        projected[patches - (CONV - 1) :, DI : 2 * DI + 2 * STATE], (NARROW, WIDE), 1
    ).astype(jnp.float32)
    projected_f = projected.astype(jnp.float32)
    small_params = (conv_weight, conv_bias, step_bias, log_rate, skip_gain)
    (decay_total, state_local), state_back = jax.vjp(
        partial(local_state, layout), projected_f, rim_rows, small_params
    )
    prefix = prefix_2(
        (decay_total, state_local),
        (NARROW, WIDE),
        combine_states,
        (jnp.ones_like(decay_total), jnp.zeros_like(state_local)),
    )
    incoming = prefix[1]
    gated_norm, mixer_back = jax.vjp(
        partial(mixer_output, layout), projected_f, rim_rows, small_params, incoming, gated_gain
    )
    gated_low = gated_norm.astype(jnp.bfloat16)
    global_out = mixed_in + jnp.dot(gated_low, out_all, preferred_element_type=jnp.float32)
    local_rows = global_out.astype(jnp.bfloat16).reshape(byte_rows, EMB)
    stream = jnp.dot(local_rows, local_all, preferred_element_type=jnp.float32)
    normed_attn, queries, key_rows, value_rows, attn_probs, mixed_heads = attend(
        stream, gain_attn, query_all, key_all, value_all
    )
    after_attn = stream + jnp.dot(mixed_heads, attn_all, preferred_element_type=jnp.float32)
    normed_feed = root_norm(after_attn, feed_gain).astype(jnp.bfloat16)
    out_grad = cotangent.astype(jnp.float32) * keep_mask[:, None]
    feed_grad = out_grad.astype(jnp.bfloat16)
    grid_in = spread(normed_feed)
    both_weights = jnp.concatenate([gate_weight, up_weight], axis=1)
    hidden_width = gate_weight.shape[1]
    grid_share = grid_in.shape[0] // wide_count
    gate_up_part = jnp.dot(grid_in, both_weights, preferred_element_type=jnp.float32).astype(
        jnp.bfloat16
    )
    gate_up = narrow_total(gate_up_part)
    hidden = (jax.nn.silu(gate_up[:, :hidden_width]) * gate_up[:, hidden_width:]).astype(
        jnp.bfloat16
    )

    def down_term(first_row, row_count):
        return jnp.dot(hidden, down_weight, preferred_element_type=jnp.float32)

    feed_out = collect(down_term, grid_share)
    grid_grad = spread(feed_grad)
    grad_down = jnp.einsum("gf,gd->fd", hidden, grid_grad, preferred_element_type=jnp.float32)
    hidden_part = jnp.einsum(
        "gd,fd->gf", grid_grad, down_weight, preferred_element_type=jnp.float32
    ).astype(jnp.bfloat16)
    hidden_grad = narrow_total(hidden_part)
    gate_up_grad = silu_back(gate_up, hidden_grad, hidden_width).astype(jnp.bfloat16)
    grad_both = jnp.einsum("gd,gf->df", grid_in, gate_up_grad, preferred_element_type=jnp.float32)

    def back_term(first_row, row_count):
        return jnp.einsum(
            "gf,df->gd", gate_up_grad, both_weights, preferred_element_type=jnp.float32
        )

    feed_in_grad = collect(back_term, grid_share)
    grad_gate = grad_both[:, :hidden_width]
    grad_up = grad_both[:, hidden_width:]
    after_feed = after_attn + feed_out.astype(jnp.float32)
    out_rows = (after_feed * keep_mask[:, None]).astype(jnp.bfloat16)
    feed_normed, feed_norm_back = jax.vjp(root_norm, after_attn, feed_gain)
    after_norm_grad, grad_feed_gain = feed_norm_back(feed_in_grad.astype(jnp.float32))
    after_grad = out_grad + after_norm_grad
    head_shape = (-1, PATCH, HEADS_A, HEAD_A)
    score_scale = HEAD_A ** (-0.5)
    attn_grad = after_grad.astype(jnp.bfloat16)
    grad_attn = jnp.einsum("rd,re->de", mixed_heads, attn_grad, preferred_element_type=jnp.float32)
    heads_grad = (
        jnp.einsum("re,de->rd", attn_grad, attn_all, preferred_element_type=jnp.float32)
        .astype(jnp.bfloat16)
        .reshape(head_shape)
    )
    probs_grad = jnp.einsum(
        "pqhe,pkhe->phqk",
        heads_grad,
        value_rows.reshape(head_shape),
        preferred_element_type=jnp.float32,
    )
    value_grad = (
        jnp.einsum(
            "phqk,pqhe->pkhe",
            attn_probs.astype(jnp.bfloat16),
            heads_grad,
            preferred_element_type=jnp.float32,
        )
        .reshape(byte_rows, D)
        .astype(jnp.bfloat16)
    )
    score_grad = (
        attn_probs * (probs_grad - jnp.sum(attn_probs * probs_grad, axis=-1, keepdims=True))
    ).astype(jnp.bfloat16)
    query_grad = (
        (
            jnp.einsum(
                "phqk,pkhe->pqhe",
                score_grad,
                key_rows.reshape(head_shape),
                preferred_element_type=jnp.float32,
            )
            * score_scale
        )
        .reshape(byte_rows, D)
        .astype(jnp.bfloat16)
    )
    key_grad = (
        (
            jnp.einsum(
                "phqk,pqhe->pkhe",
                score_grad,
                queries.reshape(head_shape),
                preferred_element_type=jnp.float32,
            )
            * score_scale
        )
        .reshape(byte_rows, D)
        .astype(jnp.bfloat16)
    )
    grad_query = jnp.einsum(
        "rd,re->de", normed_attn, query_grad, preferred_element_type=jnp.float32
    )
    grad_key = jnp.einsum("rd,re->de", normed_attn, key_grad, preferred_element_type=jnp.float32)
    grad_value = jnp.einsum(
        "rd,re->de", normed_attn, value_grad, preferred_element_type=jnp.float32
    )
    normed_grad = jnp.einsum("re,de->rd", query_grad, query_all, preferred_element_type=jnp.float32)
    normed_grad = normed_grad + jnp.einsum(
        "re,de->rd", key_grad, key_all, preferred_element_type=jnp.float32
    )
    normed_grad = normed_grad + jnp.einsum(
        "re,de->rd", value_grad, value_all, preferred_element_type=jnp.float32
    )
    attn_normed, attn_norm_back = jax.vjp(root_norm, stream, gain_attn)
    stream_norm_grad, grad_gain_attn = attn_norm_back(normed_grad)
    stream_grad = (after_grad + stream_norm_grad).astype(jnp.bfloat16)
    grad_local = jnp.einsum(
        "re,rd->ed", local_rows, stream_grad, preferred_element_type=jnp.float32
    )
    global_grad = jnp.einsum(
        "rd,ed->re", stream_grad, local_all, preferred_element_type=jnp.float32
    ).reshape(patches, D)
    mix_grad = global_grad.astype(jnp.bfloat16)
    grad_out = jnp.einsum("pi,pd->id", gated_low, mix_grad, preferred_element_type=jnp.float32)
    gated_grad = jnp.einsum("pd,id->pi", mix_grad, out_all, preferred_element_type=jnp.float32)
    proj_grad_mix, rim_grad_mix, small_grad_mix, incoming_grad, grad_gated_gain = mixer_back(
        gated_grad
    )
    suffix = carried_in_2(
        (decay_total, incoming_grad),
        (NARROW, WIDE),
        combine_states,
        (jnp.ones_like(decay_total), jnp.zeros_like(incoming_grad)),
    )
    later_grad = suffix[1]
    decay_grad = jnp.sum(later_grad * incoming, axis=(1, 2))
    proj_grad_state, rim_grad_state, small_grad_state = state_back((decay_grad, later_grad))
    rim_from_next = passed_along(rim_grad_mix + rim_grad_state, (NARROW, WIDE), -1)
    proj_grad = proj_grad_mix + proj_grad_state
    proj_grad = proj_grad.at[patches - (CONV - 1) :, DI : 2 * DI + 2 * STATE].add(rim_from_next)
    proj_low = proj_grad.astype(jnp.bfloat16)
    grad_in = jnp.einsum("pd,pk->dk", normed_mix, proj_low, preferred_element_type=jnp.float32)
    normed_mix_grad = jnp.einsum("pk,dk->pd", proj_low, in_all, preferred_element_type=jnp.float32)
    mix_normed, mix_norm_back = jax.vjp(root_norm, mixed_in, gain_mix)
    mixed_norm_grad, grad_gain_mix = mix_norm_back(normed_mix_grad)
    embed_grad = (global_grad + mixed_norm_grad).astype(jnp.bfloat16)
    grad_patch = jnp.einsum("pi,pd->id", embedded, embed_grad, preferred_element_type=jnp.float32)
    byte_grad = (
        jnp.einsum("pd,id->pi", embed_grad, patch_all, preferred_element_type=jnp.float32).reshape(
            byte_rows, EMB
        )
        * keep_mask[:, None]
    )
    grad_table = jnp.dot(onehot.astype(jnp.float32).T, byte_grad, precision=highest)
    shared = (
        lax.psum_scatter(grad_table, (NARROW, WIDE), scatter_dimension=0, tiled=True),
        lax.psum_scatter(grad_patch, (NARROW, WIDE), scatter_dimension=0, tiled=True),
        lax.psum_scatter(grad_in, (NARROW, WIDE), scatter_dimension=0, tiled=True),
        lax.psum_scatter(grad_out, (NARROW, WIDE), scatter_dimension=0, tiled=True),
        lax.psum_scatter(grad_local, (NARROW, WIDE), scatter_dimension=1, tiled=True),
        lax.psum_scatter(grad_query, (NARROW, WIDE), scatter_dimension=0, tiled=True),
        lax.psum_scatter(grad_key, (NARROW, WIDE), scatter_dimension=0, tiled=True),
        lax.psum_scatter(grad_value, (NARROW, WIDE), scatter_dimension=0, tiled=True),
        lax.psum_scatter(grad_attn, (NARROW, WIDE), scatter_dimension=0, tiled=True),
    )
    small_sum = lax.psum(
        (
            small_grad_mix[0] + small_grad_state[0],
            small_grad_mix[1] + small_grad_state[1],
            small_grad_mix[2] + small_grad_state[2],
            small_grad_mix[3] + small_grad_state[3],
            small_grad_mix[4] + small_grad_state[4],
            grad_gain_mix,
            grad_gated_gain,
            grad_gain_attn,
            grad_feed_gain,
        ),
        (NARROW, WIDE),
    )
    return (
        out_rows,
        shared[0],
        shared[1],
        small_sum[5],
        shared[2],
        small_sum[0],
        small_sum[1],
        small_sum[2],
        small_sum[3],
        small_sum[4],
        small_sum[6],
        shared[3],
        shared[4],
        small_sum[7],
        shared[5],
        shared[6],
        shared[7],
        shared[8],
        small_sum[8],
        grad_gate,
        grad_up,
        grad_down,
    )


QUERY = 128
BYTE_BLOCK = 128
MESH = pl.DeviceIdType.MESH
SUM_ROWS = (3 * D + DI + (CONV + 1) * 2 * STATE) // 128
LOW = jnp.bfloat16
FULL = jnp.float32
BOTH = (NARROW, WIDE)


def nn(a, b, precision=None):
    return lax.dot_general(
        a, b, (((1,), (0,)), ((), ())), precision=precision, preferred_element_type=FULL
    )


def nt(a, b, precision=None):
    return lax.dot_general(
        a, b, (((1,), (1,)), ((), ())), precision=precision, preferred_element_type=FULL
    )


def tn(a, b, precision=None):
    return lax.dot_general(
        a, b, (((0,), (0,)), ((), ())), precision=precision, preferred_element_type=FULL
    )


def device_at(place, wide):
    return (lax.div(place, wide), lax.rem(place, wide))


def remote(src, dst, send, recv, peer):
    return pltpu.make_async_remote_copy(
        src_ref=src, dst_ref=dst, send_sem=send, recv_sem=recv, device_id=peer, device_id_type=MESH
    )


def greet_all(devices, wide):
    me = lax.axis_index(NARROW) * wide + lax.axis_index(WIDE)
    barrier = pltpu.get_barrier_semaphore()

    def greet(k, carry):
        peer = device_at(lax.rem(me + k, devices), wide)
        pl.semaphore_signal(barrier, inc=1, device_id=peer, device_id_type=MESH)
        return carry

    lax.fori_loop(1, devices, greet, 0)
    return me, lambda: pl.semaphore_wait(barrier, devices - 1)


def send_blocks(me, devices, wide, src, dst, send, recv):
    def one(k, carry):
        place = lax.rem(me + k, devices)
        remote(src.at[place], dst.at[me], send, recv, device_at(place, wide)).start()
        return carry

    lax.fori_loop(1, devices, one, 0)


def wait_blocks(me, devices, wide, dst, send, recv):
    part = dst.at[pl.ds(0, devices - 1)]
    remote(part, part, send, recv, device_at(me, wide)).wait()


class StagedGather:
    def __init__(self, block, out, sems, narrow, depth):
        n, w = lax.axis_index(NARROW), lax.axis_index(WIDE)
        z, c = lax.div(w, 2), lax.rem(w, 2)
        self.out, self.narrow, self.depth = out, narrow, depth
        self.n, self.c = n, c
        self.sems = [sems.at[i] for i in range(7)]
        self.twin = (n, z * 2 + 1 - c)
        self.n_peers = [lax.rem(n + k, narrow) for k in range(1, narrow)]
        self.w = w
        self.own = pltpu.make_async_copy(block, out.at[n, z, c], self.sems[0])
        self.first = [
            remote(
                block,
                out.at[n, z, c],
                self.sems[1],
                self.sems[2],
                (n, lax.rem(z + k, depth) * 2 + c),
            )
            for k in range(1, depth)
        ]

    def wait_for(self, part, i):
        return remote(part, part, self.sems[i], self.sems[i + 1], self.twin)

    def z_part(self):
        return self.wait_for(self.out.at[self.n, pl.ds(0, self.depth - 1), self.c], 1)

    def n_part(self):
        return self.wait_for(self.out.at[pl.ds(0, self.narrow - 1), :, self.c], 3)

    def start(self):
        self.own.start()
        for copy in self.first:
            copy.start()

    def spread(self):
        self.own.wait()
        self.z_part().wait_recv()
        mine = self.out.at[self.n, :, self.c]
        for m in self.n_peers:
            remote(mine, mine, self.sems[3], self.sems[4], (m, self.w)).start()
        self.wait_for(mine, 5).start()

    def cross(self):
        self.n_part().wait_recv()
        for m in self.n_peers:
            self.wait_for(self.out.at[m, :, self.c], 5).start()

    def finish(self):
        self.wait_for(self.out.at[:, :, 1 - self.c], 5).wait()
        self.z_part().wait_send()
        self.n_part().wait_send()


def greet_lines(narrow, depth):
    n, w = lax.axis_index(NARROW), lax.axis_index(WIDE)
    z, c = lax.div(w, 2), lax.rem(w, 2)
    peers = [(n, lax.rem(z + k, depth) * 2 + c) for k in range(1, depth)]
    peers += [(lax.rem(n + k, narrow), w) for k in range(1, narrow)]
    peers += [(n, z * 2 + 1 - c)]
    barrier = pltpu.get_barrier_semaphore()
    for peer in peers:
        pl.semaphore_signal(barrier, inc=1, device_id=peer, device_id_type=MESH)
    pl.semaphore_wait(barrier, len(peers))


class LineSum:
    def __init__(self, parts, got, sems, place, length, peer_of):
        self.got, self.length = got, length
        self.own = pltpu.make_async_copy(parts.at[place], got.at[0], sems.at[0])
        self.copies = []
        for k in range(1, length):
            there = lax.rem(place + k, length)
            self.copies.append(
                remote(
                    parts.at[there], got.at[k], sems.at[2 * k - 1], sems.at[2 * k], peer_of(there)
                )
            )

    def start(self):
        self.own.start()
        for copy in self.copies:
            copy.start()

    def arrive(self):
        self.own.wait()
        for copy in self.copies:
            copy.wait_recv()

    def total(self, *index):
        summed = self.got[(0,) + index].astype(FULL)
        for k in range(1, self.length):
            summed += self.got[(k,) + index].astype(FULL)
        return summed

    def finish(self):
        for copy in self.copies:
            copy.wait_send()


def square_peer(n, k):
    x, y, kx, ky = lax.rem(n, 2), lax.div(n, 2), lax.rem(k, 2), lax.div(k, 2)
    return 2 * (y + ky - 2 * y * ky) + x + kx - 2 * x * kx


class SquareShare:
    def __init__(self, rows, got, send, recv, n, w):
        self.half = half = rows.shape[0] // 2
        low, high = pl.ds(0, half), pl.ds(half, half)
        beside, across = (square_peer(n, 1), w), (square_peer(n, 2), w)
        self.first = [
            remote(rows, got.at[1], send.at[1], recv.at[1], beside),
            remote(rows, got.at[2], send.at[2], recv.at[2], across),
        ]
        self.second = [
            remote(got.at[1, low], got.at[3, low], send.at[0], recv.at[0], across),
            remote(got.at[2, high], got.at[3, high], send.at[3], recv.at[3], beside),
        ]

    def start(self):
        for copy in self.first:
            copy.start()

    def relay(self, i):
        self.first[i].wait_recv()
        self.second[i].start()

    def arrive(self):
        for copy in self.second:
            copy.wait_recv()

    def finish(self):
        for copy in self.first + self.second:
            copy.wait_send()


def square_of(n, narrow):
    return n + 1 - 2 * lax.rem(n, 2), n + 2 - 4 * lax.div(n, 2), narrow - 1 - n


class SquareSum:
    def __init__(self, parts, own, held, got, sems, n, w, narrow):
        beside, across, corner = square_of(n, narrow)
        self.own, self.held, self.got = own, held, got
        self.half = half = parts.shape[1] // 2
        low, high = pl.ds(0, half), pl.ds(half, half)
        self.local = [
            pltpu.make_async_copy(parts.at[n], own, sems.at[0, 6]),
            pltpu.make_async_copy(parts.at[across, low], held.at[0], sems.at[0, 7]),
            pltpu.make_async_copy(parts.at[beside, high], held.at[1], sems.at[1, 6]),
        ]

        def send(i, src, peer):
            return remote(src, got.at[i], sems.at[0, i], sems.at[1, i], (peer, w))

        self.copies = [
            send(0, parts.at[corner, low], beside),
            send(1, parts.at[corner, high], across),
            send(2, parts.at[beside, low], beside),
            send(3, parts.at[across, high], across),
            send(4, held.at[1], beside),
            send(5, held.at[0], across),
        ]

    def start(self):
        for copy in self.local + self.copies[:4]:
            copy.start()

    def relay(self):
        for i in range(2):
            self.local[1 + i].wait()
            self.copies[i].wait_recv()
            for j in range(self.half):
                self.held[i, j] = (
                    self.held[i, j].astype(FULL) + self.got[i, j].astype(FULL)
                ).astype(LOW)
            self.copies[5 - i].start()

    def arrive(self):
        self.local[0].wait()
        for copy in self.copies[2:]:
            copy.wait_recv()

    def total(self, j):
        first, second = (2, 5) if j < self.half else (4, 3)
        summed = self.own[j].astype(FULL)
        for i in (first, second):
            summed += self.got[i, j % self.half].astype(FULL)
        return summed

    def finish(self):
        for copy in self.copies:
            copy.wait_send()


def end_kernel(
    narrow,
    depth,
    pack,
    sums,
    middle,
    up_sum,
    down_sum,
    pack_all,
    sums_all,
    middle_out,
    up_out,
    down_out,
    middle_got,
    up_got,
    down_got,
    pack_sems,
    sums_sems,
    middle_sems,
    back_send,
    back_recv,
    back_own,
):
    n, w = lax.axis_index(NARROW), lax.axis_index(WIDE)
    z, c = lax.div(w, 2), lax.rem(w, 2)
    greet_lines(narrow, depth)
    gathers = [
        StagedGather(pack, pack_all, pack_sems, narrow, depth),
        StagedGather(sums, sums_all, sums_sems, narrow, depth),
    ]
    line = LineSum(middle, middle_got, middle_sems, z, depth, lambda there: (n, there * 2 + c))
    backs = [
        Returned(
            values, landed, back_send.at[i], back_recv.at[i], back_own.at[i], n, w, narrow, i
        )
        for i, (values, landed) in enumerate(((up_sum, up_got), (down_sum, down_got)))
    ]
    for gather in gathers:
        gather.start()
    line.start()
    for back in backs:
        back.start()
    for gather in gathers:
        gather.spread()
    line.arrive()
    middle_out[...] = line.total()
    for gather in gathers:
        gather.cross()
    for back, landed, out in zip(backs, (up_got, down_got), (up_out, down_out)):
        back.arrive()
        out[...] = landed[...].astype(FULL)
    for gather in gathers:
        gather.finish()
    line.finish()
    for back in backs:
        back.finish()


class Returned:
    def __init__(self, values, got, send, recv, own, n, w, narrow, axis):
        span = values.shape[axis] // narrow
        other = values.shape[1 - axis]

        def block(m):
            mine = pl.ds(m * span, span)
            return values.at[mine, :] if axis == 0 else values.at[:, mine]

        there = pl.ds(n * other, other)
        landing = got.at[:, there] if axis == 0 else got.at[there, :]
        self.own = pltpu.make_async_copy(block(n), landing, own)
        self.copies = []
        for k in range(1, narrow):
            m = lax.rem(n + k, narrow)
            self.copies.append(
                remote(block(m), landing, send.at[k - 1], recv.at[k - 1], (m, w))
            )

    def start(self):
        self.own.start()
        for copy in self.copies:
            copy.start()

    def arrive(self):
        self.own.wait()
        for copy in self.copies:
            copy.wait_recv()

    def finish(self):
        for copy in self.copies:
            copy.wait_send()


def end_gather(pack, sums, middle, up_sum, down_sum, collective_id):
    narrow, wide = lax.axis_size(NARROW), lax.axis_size(WIDE)
    depth = wide // 2
    dma = pltpu.SemaphoreType.DMA
    anywhere = pl.BlockSpec(memory_space=pl.ANY)
    up_shape = (up_sum.shape[0] // narrow, up_sum.shape[1] * narrow)
    down_shape = (down_sum.shape[0] * narrow, down_sum.shape[1] // narrow)
    outs = pl.pallas_call(
        partial(end_kernel, narrow, depth),
        out_shape=[
            jax.ShapeDtypeStruct((narrow, depth, 2) + pack.shape, pack.dtype),
            jax.ShapeDtypeStruct((narrow, depth, 2) + sums.shape, sums.dtype),
            jax.ShapeDtypeStruct(middle.shape[1:], FULL),
            jax.ShapeDtypeStruct(up_shape, FULL),
            jax.ShapeDtypeStruct(down_shape, FULL),
        ],
        in_specs=[anywhere] * 5,
        out_specs=[anywhere] * 2 + [in_vmem()] * 3,
        scratch_shapes=[
            pltpu.VMEM(middle.shape, middle.dtype),
            pltpu.VMEM(up_shape, LOW),
            pltpu.VMEM(down_shape, LOW),
            dma((7,)),
            dma((7,)),
            dma((2 * depth,)),
            dma((2, narrow - 1)),
            dma((2, narrow - 1)),
            dma((2,)),
        ],
        compiler_params=pltpu.CompilerParams(
            collective_id=collective_id, has_side_effects=True, vmem_limit_bytes=10 << 20
        ),
        name="end_gather",
    )(pack, sums, middle, up_sum, down_sum)
    return [
        outs[0].reshape(-1, pack.shape[1]),
        outs[1].reshape((-1,) + sums.shape),
    ] + list(outs[2:])


def softplus(v):
    return jnp.maximum(v, 0.0) + jnp.log1p(jnp.exp(-jnp.abs(v)))


def convolved(window, marks, weight, bias):
    pre = bias + weight[CONV - 1 :] * window[8:]
    for lag in range(1, CONV):
        pre = pre + weight[CONV - 1 - lag : CONV - lag] * (
            window[8 - lag : 8 - lag + QUERY] * marks[:, lag : lag + 1]
        )
    return pre


def decays(marks, dt, step_bias, rate_scale):
    shape = (QUERY, QUERY)
    row = lax.broadcasted_iota(jnp.int32, shape, 0)
    column = lax.broadcasted_iota(jnp.int32, shape, 1)
    lower = (row >= column).astype(FULL)
    segment = jnp.broadcast_to(marks[:, :1], shape)
    visible = (segment == segment.T) & (row >= column)
    delta = jnp.broadcast_to(softplus(dt + step_bias), shape)
    total = nn(lower, -delta * rate_scale, highest)
    gap = jnp.where(visible, total - total.T, 0.0)
    decay = jnp.where(visible, jnp.exp(gap), 0.0)
    last = total[QUERY - 1 :, :]
    begun = jnp.exp(total) * marks[:, 4:5]
    tail = jnp.exp(last - total) * marks[:, 5:6]
    kept = jnp.exp(last) * marks[:1, 6:7]
    return lower, delta, decay, begun, tail, kept


def head_numbers(step_bias, log_rate, skip_gain, me):
    return step_bias[me], jnp.exp(jnp.full((1, QUERY), log_rate[me], FULL)), skip_gain[me]


def head_columns(values, me):
    start = pl.multiple_of(lax.div(me, 2) * 2 * HEAD_M, 2 * HEAD_M)
    pair = values[:, pl.ds(start, 2 * HEAD_M)]
    lane = lax.broadcasted_iota(jnp.int32, pair.shape, 1)
    moved = jnp.concatenate([pair[:, HEAD_M:], pair[:, :HEAD_M]], axis=1)
    odd = jnp.full(pair.shape, lax.rem(me, 2), jnp.int32) == 1
    return jnp.where(lane < HEAD_M, jnp.where(odd, moved, pair), 0.0)


def documents(doc_patches, pad_bytes):
    ends, end = [], 0
    for d in range(doc_patches.shape[0]):
        end = end + doc_patches[d]
        ends.append(end)

    def document(place):
        return sum((place >= end).astype(jnp.int32) for end in ends)

    def kept(place, offset):
        padded = [
            ((place == end - 1) & (offset >= PATCH - pad_bytes[d])).astype(FULL)
            for d, end in enumerate(ends)
        ]
        return 1.0 - sum(padded)

    return document, kept


def patch_marks(document, first, count):
    place = first + lax.broadcasted_iota(jnp.int32, (count, 8), 0)
    kind = lax.broadcasted_iota(jnp.int32, (count, 8), 1)
    opening = lax.div(place, QUERY) * QUERY
    block_mark = jnp.where(kind == CONV, opening - 1, opening + QUERY - 1)
    ahead = jnp.where(kind < CONV, place - kind, block_mark)
    facing = jnp.where(kind == CONV + 2, opening - 1, place)
    same = (document(ahead) == document(facing)) & (ahead >= 0) & (facing >= 0)
    return jnp.where(kind == 0, document(place).astype(FULL), same.astype(FULL))


def mixer_front_kernel(
    narrow,
    wide,
    doc_patches,
    pad_bytes,
    step_biases,
    log_rates,
    skip_gains,
    gain,
    conv_weight,
    conv_bias,
    pack,
    table,
    xz_blocks,
    gate,
    up,
    down,
    middle,
    cotangent,
    embedded,
    normed,
    xz,
    bc,
    dt,
    u_out,
    y_out,
    states,
    mixed_in,
    u_got,
    marks,
    keep_rows,
    keep_all,
    start,
    w_xz,
    gate_all,
    up_all,
    down_all,
    middle_all,
    others,
    table_all,
    gate_turned,
    up_turned,
    down_turned,
    mixed_all,
    xz_pad,
    bc_pad,
    state,
    u_blocks,
    u_send,
    u_recv,
    pack_sems,
    table_sems,
    xz_sems,
    turn_send,
    turn_recv,
    start_sems,
    depth_send,
    depth_recv,
    other_send,
    other_recv,
    own_sems,
    line_send,
    line_recv,
    cross_send,
    cross_recv,
    middle_sems,
):
    devices, depth = narrow * wide, wide // 2
    me, arrived = greet_all(devices, wide)
    n, w = lax.axis_index(NARROW), lax.axis_index(WIDE)
    z, c = lax.div(w, 2), lax.rem(w, 2)
    twin = (n, z * 2 + 1 - c)
    rows_in, units_in = gate.shape[0], gate.shape[1] // narrow
    columns_in = down.shape[1]
    gathers = [
        StagedGather(pack, start, pack_sems, narrow, depth),
        StagedGather(table, table_all, table_sems, narrow, depth),
    ]

    def pieces(m):
        mine = pl.ds(m * units_in, units_in)
        return (gate.at[:, mine], up.at[:, mine], down.at[mine, :])

    turned = (gate_turned, up_turned, down_turned)
    landing = (
        gate_turned.at[pl.ds(n * rows_in, rows_in), :],
        up_turned.at[pl.ds(n * rows_in, rows_in), :],
        down_turned.at[:, pl.ds(n * columns_in, columns_in)],
    )
    turns = []
    for k in range(1, narrow):
        m = lax.rem(n + k, narrow)
        for i, piece in enumerate(pieces(m)):
            turns.append(
                remote(piece, landing[i], turn_send.at[k - 1, i], turn_recv.at[k - 1, i], (m, w))
            )
    first_own = [
        pltpu.make_async_copy(piece, landing[i], start_sems.at[i])
        for i, piece in enumerate(pieces(n))
    ]
    own_xz = pltpu.make_async_copy(xz_blocks.at[me], w_xz.at[me], start_sems.at[3])
    own_middle = pltpu.make_async_copy(middle, middle_all.at[n, z, c], start_sems.at[4])

    def depth_copy(source, target):
        return remote(
            middle,
            middle_all.at[n, source, c],
            depth_send.at[target],
            depth_recv.at[source],
            (n, target * 2 + c),
        )

    share = SquareShare(cotangent, others, other_send, other_recv, n, w)
    results = (gate_all, up_all, down_all)
    own = [pltpu.make_async_copy(turned[i], results[i].at[z, c], own_sems.at[i]) for i in range(3)]
    beside, across, corner = square_of(n, narrow)

    def middle_copy(j, way, owner):
        there = middle_all.at[owner, j, c]
        peer = twin if way >= 4 else ((beside if way in (0, 3) else across), w)
        return remote(there, there, middle_sems.at[0, way, j], middle_sems.at[1, way, j], peer)

    def line_copy(i, source, step, src=None):
        there = results[i].at[source, c]
        return remote(
            there if src is None else src,
            there,
            line_send.at[i, source, max(step, 0)],
            line_recv.at[i, source],
            (n, (z + step) * 2 + c),
        )

    def along(i, source, step, src=None):
        @pl.when((z + step >= 0) & (z + step < depth))
        def _():
            line_copy(i, source, step, src).start()

    def middle_begin(j):
        @pl.when(z == j)
        def _():
            own_middle.wait()

        @pl.when(z != j)
        def _():
            depth_copy(j, z).wait_recv()

        for way in (0, 1, 7):
            middle_copy(j, way, n).start()

    def middle_on(j):
        middle_copy(j, 0, beside).wait_recv()
        if j % 2 == 0:
            middle_copy(j, 2, beside).start()
        middle_copy(j, 4, beside).start()
        middle_copy(j, 1, across).wait_recv()
        if j % 2 == 1:
            middle_copy(j, 3, across).start()
        middle_copy(j, 5, across).start()

    def line_side(distance, step):
        source = z - step * distance

        @pl.when((source >= 0) & (source < depth))
        def _():
            for i in range(3):
                line_copy(i, source, step).wait_recv()
                along(i, source, step)
                theirs = results[i].at[source, c]
                remote(theirs, theirs, cross_send.at[i], cross_recv.at[i], twin).start()

    def line_on(distance):
        @pl.when(2 * z < depth)
        def _():
            line_side(distance, 1)
            line_side(distance, -1)

        @pl.when(2 * z >= depth)
        def _():
            line_side(distance, -1)
            line_side(distance, 1)

    arrived()
    for gather in gathers:
        gather.start()
    for copy in turns + first_own + [own_xz, own_middle]:
        copy.start()
    send_blocks(me, devices, wide, xz_blocks, w_xz, xz_sems.at[0], xz_sems.at[1])
    for distance in range(1, depth):
        for target in (z + distance, z - distance):

            @pl.when((target >= 0) & (target < depth))
            def _():
                depth_copy(z, target).start()

    for gather in gathers:
        gather.spread()
    for copy in first_own[:3]:
        copy.wait()
    for copy in turns:
        copy.wait_recv()
    for i in range(3):
        along(i, z, 1, turned[i])
        along(i, z, -1, turned[i])
    for copy in own:
        copy.start()
    for gather in gathers:
        gather.cross()
    share.start()

    count = embedded.shape[0]
    patches = u_blocks.shape[1]
    block_rows = 2 * QUERY
    xz_pad[pl.ds(0, 8), :] = jnp.zeros((8, xz_pad.shape[1]), FULL)
    bc_pad[pl.ds(0, 8), :] = jnp.zeros((8, bc_pad.shape[1]), FULL)
    state[...] = jnp.zeros_like(state)
    step_bias, rate_scale, skip = head_numbers(step_biases, log_rates, skip_gains, me)
    document, kept_bytes = documents(doc_patches, pad_bytes)
    for first in range(0, count + 8, (count + 8) // 3):
        part = (count + 8) // 3
        marks[first : first + part, :] = patch_marks(document, first, part)
    byte = lax.broadcasted_iota(jnp.int32, keep_rows.shape[1:], 0)
    for k in range(narrow):
        there = (square_peer(n, k) * wide + w) * patches
        keep_rows[k] = kept_bytes(there + lax.div(byte, PATCH), lax.rem(byte, PATCH))
    wx, bx = head_columns(conv_weight, me), head_columns(conv_bias, me)
    wbc, bbc = conv_weight[:, DI:], conv_bias[:, DI:]
    for gather in gathers:
        gather.finish()
    own_xz.wait()
    wait_blocks(me, devices, wide, w_xz, xz_sems.at[0], xz_sems.at[1])
    words = lax.broadcasted_iota(jnp.int32, (block_rows, VOCAB), 1).astype(FULL)
    own_lane = lax.broadcasted_iota(jnp.int32, (block_rows, STATE), 1) == me

    word_rows = table_all[...].reshape(VOCAB, EMB).astype(LOW)

    def project(i, carry):
        rows = pl.ds(pl.multiple_of(i * block_rows, block_rows), block_rows)
        ids = start[i, :, :, :, 3 * STATE : 4 * STATE].reshape(block_rows, STATE).astype(FULL)
        place = i * block_rows + lax.broadcasted_iota(jnp.int32, (block_rows, PATCH), 0)
        kept = kept_bytes(place, lax.broadcasted_iota(jnp.int32, (block_rows, PATCH), 1))
        keep_all[rows, :] = kept
        for k in range(PATCH):
            chosen = jnp.where(ids[:, k : k + 1] == words, kept[:, k : k + 1], 0.0).astype(LOW)
            embedded[rows, k * EMB : (k + 1) * EMB] = nn(chosen, word_rows).astype(LOW)
        row_embedded = embedded[rows, :]
        for first in range(0, D, WEIGHT_STEP):
            columns = slice(first, first + WEIGHT_STEP)
            there = slice(4 * STATE + first, 4 * STATE + first + WEIGHT_STEP)
            weight = start[:, :, :, :, there].reshape(D, WEIGHT_STEP)
            mixed_all[rows, columns] = nn(row_embedded, weight)
        row_normed = (unit_rows(mixed_all[rows, :])[0] * gain[...]).astype(LOW)
        normed[rows, :] = row_normed
        row_xz = nn(row_normed, w_xz[...].reshape(D, 2 * HEAD_M)).astype(LOW)
        weight = start[:, :, :, :, : 3 * STATE].reshape(D, 3 * STATE)
        row_bcdt = nn(row_normed, weight).astype(LOW)
        xz[rows, :] = row_xz
        bc[rows, :] = row_bcdt[:, : 2 * STATE]
        own_dt = jnp.where(own_lane, row_bcdt[:, 2 * STATE :].astype(FULL), 0.0)
        dt[rows, :] = jnp.sum(own_dt, axis=1, keepdims=True)
        padded = pl.ds(pl.multiple_of(i * block_rows + 8, 8), block_rows)
        xz_pad[padded, :] = row_xz.astype(FULL)
        bc_pad[padded, :] = row_bcdt[:, : 2 * STATE].astype(FULL)
        return carry

    lax.fori_loop(0, count // block_rows, project, 0)
    for j in range(depth):
        middle_begin(j)
    for i in range(2):
        share.relay(i)
    mixed_in[...] = mixed_all[pl.ds(pl.multiple_of(me * patches, patches), patches), :]
    group = QUERY // patches

    def block(i, carry):
        first = pl.multiple_of(i * QUERY, QUERY)
        rows = pl.ds(first, QUERY)
        mark = marks[rows, :]
        act_x = jax.nn.silu(convolved(xz_pad[pl.ds(first, QUERY + 8), :], mark, wx, bx))
        act = jax.nn.silu(convolved(bc_pad[pl.ds(first, QUERY + 8), :], mark, wbc, bbc))
        x, b, c = act_x[:, :HEAD_M], act[:, :STATE], act[:, STATE:]
        lower, delta, decay, begun, tail, kept = decays(mark, dt[rows, :], step_bias, rate_scale)
        weight = nt(c, b, highest) * decay * delta.T
        held = state[...]
        states[i] = held
        y = (
            nn(weight, x, highest)
            + nt(c, held, highest) * begun[:, :HEAD_M]
            + skip * x
        )
        state[...] = held * kept + tn(x * (tail * delta)[:, :HEAD_M], b, highest)
        z = xz[rows, :].astype(FULL)[:, HEAD_M:]
        u = y * jax.nn.silu(z)
        y_out[rows, :] = y
        u_out[rows, :] = u
        u_blocks[pl.ds(i * group, group)] = u.astype(LOW).reshape(group, patches, HEAD_M)
        return carry

    lax.fori_loop(0, count // QUERY, block, 0)
    send_blocks(me, devices, wide, u_blocks, u_got, u_send, u_recv)
    u_got[me] = u_blocks[me]
    line_on(1)
    for copy in own:
        copy.wait()
    for i in range(3):
        mine = results[i].at[z, c]
        remote(mine, mine, cross_send.at[i], cross_recv.at[i], twin).start()
    middle_on(0)
    middle_on(1)
    line_on(2)
    middle_on(2)
    middle_on(3)
    for j in range(depth):
        middle_copy(j, 2 + j % 2, corner).wait_recv()
        middle_copy(j, 6, corner).start()
    line_on(3)
    wait_blocks(me, devices, wide, u_got, u_send, u_recv)
    share.arrive()
    share.finish()
    for copy in turns:
        copy.wait_send()
    for target in range(depth):

        @pl.when(target != z)
        def _():
            depth_copy(z, target).wait_send()

    for i in range(3):
        theirs = results[i].at[:, 1 - c]
        remote(theirs, theirs, cross_send.at[i], cross_recv.at[i], twin).wait()
    for j in range(depth):
        for way, owner in ((4, beside), (5, across), (6, corner), (7, n)):
            middle_copy(j, way, owner).wait()
        for way in (0, 1, 2 + j % 2):
            middle_copy(j, way, n).wait_send()
    for i in range(3):
        for source in range(depth):
            for step in (1, -1):

                @pl.when((step * (z - source) >= 0) & (z + step >= 0) & (z + step < depth))
                def _():
                    line_copy(i, source, step).wait_send()


def mixer_backward_kernel(
    narrow,
    wide,
    step_biases,
    log_rates,
    skip_gains,
    xz,
    bc,
    dt,
    marks,
    conv_weight,
    conv_bias,
    y_in,
    states,
    normed,
    w_xz,
    start,
    mixed_in,
    global_grad,
    gain,
    gated_scale,
    gain_grads,
    gated_gain_grads,
    du_blocks,
    up_parts,
    down_parts,
    middle_parts,
    gate_sum,
    mix_grad,
    end_pack,
    sums,
    bcdt_grads,
    xz_grads,
    up_sum,
    down_sum,
    middle_sums,
    gate_out,
    mix_all,
    w_bcdt,
    w_sem,
    dwx,
    dwbc,
    dnumbers,
    xz_pad,
    bc_pad,
    dx_pad,
    dbc_pad,
    dstate,
    du_got,
    dxz,
    dbcdt,
    partial_rows,
    core_got,
    narrow_got,
    z_rows,
    z_got,
    grads,
    grads_got,
    up_got,
    down_got,
    middle_own,
    middle_held,
    middle_got,
    gate_got,
    du_send,
    du_recv,
    core_send,
    core_recv,
    narrow_send,
    narrow_recv,
    z_send,
    z_recv,
    grads_send,
    grads_recv,
    up_sems,
    down_sems,
    middle_sems,
    back_send,
    back_recv,
    back_own,
    mix_sems,
):
    devices = narrow * wide
    depth = wide // 2
    me, arrived = greet_all(devices, wide)
    n, w = lax.axis_index(NARROW), lax.axis_index(WIDE)
    z_place, core = lax.div(w, 2), lax.rem(w, 2)
    twin = (n, z_place * 2 + 1 - core)
    count = xz.shape[0]
    blocks = count // QUERY
    xz_pad[pl.ds(0, 8), :] = jnp.zeros((8, xz_pad.shape[1]), FULL)
    bc_pad[pl.ds(0, 8), :] = jnp.zeros((8, bc_pad.shape[1]), FULL)
    dx_pad[pl.ds(count, 8), :] = jnp.zeros((8, dx_pad.shape[1]), FULL)
    dbc_pad[pl.ds(count, 8), :] = jnp.zeros((8, dbc_pad.shape[1]), FULL)
    dstate[...] = jnp.zeros_like(dstate)
    dwx[...] = jnp.zeros_like(dwx)
    dwbc[...] = jnp.zeros_like(dwbc)
    dnumbers[...] = jnp.zeros_like(dnumbers)
    step_bias, rate_scale, skip = head_numbers(step_biases, log_rates, skip_gains, me)
    wx, bx = head_columns(conv_weight, me), head_columns(conv_bias, me)
    wbc, bbc = conv_weight[:, DI:], conv_bias[:, DI:]
    weight_copy = pltpu.make_async_copy(start.at[:, pl.ds(0, 3 * STATE)], w_bcdt, w_sem)
    weight_copy.start()

    def fill(i, carry):
        first = pl.multiple_of(i * QUERY, QUERY)
        rows = pl.ds(first, QUERY)
        xz_pad[pl.ds(first + 8, QUERY), :] = xz[rows, :].astype(FULL)
        bc_pad[pl.ds(first + 8, QUERY), :] = bc[rows, :].astype(FULL)
        return carry

    arrived()
    send_blocks(me, devices, wide, du_blocks, du_got, du_send, du_recv)
    lines = [
        LineSum(parts, landed, line_sems, z_place, depth, lambda there: (n, there * 2 + core))
        for parts, landed, line_sems in (
            (down_parts, down_got, down_sems),
            (up_parts, up_got, up_sems),
        )
    ]
    middle_line = SquareSum(
        middle_parts, middle_own, middle_held, middle_got, middle_sems, n, w, narrow
    )
    back = Returned(gate_sum, gate_got, back_send, back_recv, back_own, n, w, narrow, 0)
    mix_gather = StagedGather(mix_grad, mix_all, mix_sems, narrow, depth)
    middle_line.start()
    mix_gather.start()
    for line in lines:
        line.start()
    back.start()
    du_got[me] = du_blocks[me]
    lax.fori_loop(0, blocks, fill, 0)
    wait_blocks(me, devices, wide, du_got, du_send, du_recv)
    patches = du_blocks.shape[1]
    group = QUERY // patches
    own_lane = lax.broadcasted_iota(jnp.int32, (QUERY, STATE), 1) == me

    def slope(pre):
        s = jax.nn.sigmoid(pre)
        return s * (1.0 + pre * (1.0 - s))

    def total(v):
        return jnp.sum(jnp.sum(v, axis=1, keepdims=True), axis=0, keepdims=True)

    def conv_back(pad, first, dpre_pad, dpre, weight, dw):
        mark = marks[pl.ds(first, QUERY), :]
        window = pad[pl.ds(first, QUERY + 8), :]
        later = dpre_pad[pl.ds(first, QUERY + 8), :]
        later_marks = marks[pl.ds(first, QUERY + 8), :]
        out = weight[CONV - 1 :] * dpre
        dw[CONV - 1 : CONV, :] += jnp.sum(dpre * window[8:], axis=0, keepdims=True)
        dw[CONV : CONV + 1, :] += jnp.sum(dpre, axis=0, keepdims=True)
        for lag in range(1, CONV):
            tap = CONV - 1 - lag
            out = out + weight[tap : tap + 1] * (
                (later * later_marks[:, lag : lag + 1])[lag : lag + QUERY]
            )
            dw[tap : tap + 1, :] += jnp.sum(
                dpre * (window[8 - lag : 8 - lag + QUERY] * mark[:, lag : lag + 1]),
                axis=0,
                keepdims=True,
            )
        return out

    def block(k, carry):
        i = blocks - 1 - k
        first = pl.multiple_of(i * QUERY, QUERY)
        rows = pl.ds(first, QUERY)
        mark = marks[rows, :]
        pre_x = convolved(xz_pad[pl.ds(first, QUERY + 8), :], mark, wx, bx)
        pre = convolved(bc_pad[pl.ds(first, QUERY + 8), :], mark, wbc, bbc)
        act = jax.nn.silu(pre)
        x, b, c = jax.nn.silu(pre_x)[:, :HEAD_M], act[:, :STATE], act[:, STATE:]
        step = dt[rows, :]
        lower, delta, decay, begun, tail, kept = decays(mark, step, step_bias, rate_scale)
        held, dheld = states[i], dstate[...]
        z = xz[rows, :].astype(FULL)[:, HEAD_M:]
        du = du_got[pl.ds(i * group, group)].astype(FULL).reshape(QUERY, HEAD_M)
        y = y_in[rows, :]
        dy = du * jax.nn.silu(z)
        dz = du * y * slope(z)
        scores = nt(c, b, highest)
        reach = decay * delta.T
        dweight = nt(dy, x, highest)
        dscores = dweight * reach
        fed = x * (tail * delta)[:, :HEAD_M]
        begun_dy = dy * begun[:, :HEAD_M]
        dc = nn(dscores, b, highest) + nn(begun_dy, held, highest)
        db = tn(dscores, c, highest) + nn(fed, dheld, highest)
        dfed = nt(b, dheld, highest)
        dx = skip * dy + tn(scores * reach, dy, highest) + (tail * delta)[:, :HEAD_M] * dfed
        moved = dweight * scores * decay
        turned = moved.T
        ddelta = jnp.sum(turned, axis=1, keepdims=True)
        dtotal = jnp.sum(moved * delta.T, axis=1, keepdims=True) - ddelta * delta[:, :1]
        dtotal += jnp.sum(begun_dy * nt(c, held, highest), axis=1, keepdims=True)
        dtail = jnp.sum(dfed * x, axis=1, keepdims=True)
        ddelta += dtail * tail[:, :1]
        dtail = dtail * (tail * delta)[:, :1]
        dtotal -= dtail
        dlast = jnp.sum(dtail, axis=0, keepdims=True) + total(dheld * held * kept)
        dlog = tn(lower, jnp.broadcast_to(dtotal, (QUERY, QUERY)), highest)[:, :1] + dlast
        ddelta -= dlog * rate_scale[:, :1]
        dstep = ddelta * jax.nn.sigmoid(step + step_bias)
        dbcdt[rows, 2 * STATE :] = jnp.where(own_lane, dstep, 0.0).astype(LOW)
        dnumbers[0:1, :] += jnp.broadcast_to(jnp.sum(dstep, axis=0, keepdims=True), (1, 128))
        dnumbers[1:2, :] -= jnp.broadcast_to(
            jnp.sum(dlog * delta[:, :1] * rate_scale[:, :1], axis=0, keepdims=True), (1, 128)
        )
        dnumbers[2:3, :] += jnp.broadcast_to(total(dy * x), (1, 128))
        dstate[...] = dheld * kept + tn(begun_dy, c, highest)
        dpre_x = jnp.concatenate([dx, jnp.zeros_like(dx)], axis=1) * slope(pre_x)
        dpre = jnp.concatenate([db, dc], axis=1) * slope(pre)
        dx_pad[rows, :] = dpre_x
        dbc_pad[rows, :] = dpre
        dxz[rows, :] = jnp.concatenate([dz, dz], axis=1).astype(LOW)
        return carry

    lax.fori_loop(0, blocks, block, 0)

    def unconvolve(i, carry):
        first = pl.multiple_of(i * QUERY, QUERY)
        rows = pl.ds(first, QUERY)
        dxr = conv_back(xz_pad, first, dx_pad, dx_pad[rows, :], wx, dwx)
        left = lax.broadcasted_iota(jnp.int32, dxr.shape, 1) < HEAD_M
        dxz[rows, :] = jnp.where(left, dxr, dxz[rows, :].astype(FULL)).astype(LOW)
        dbcdt[rows, : 2 * STATE] = conv_back(
            bc_pad, first, dbc_pad, dbc_pad[rows, :], wbc, dwbc
        ).astype(LOW)
        return carry

    middle_line.relay()
    mix_gather.spread()
    lax.fori_loop(0, blocks, unconvolve, 0)

    width = normed.shape[1]
    own_rows = xz_grads.shape[1]

    weight_copy.wait()

    def rows_of(m, carry):
        for z in range(depth):
            first = (m * depth + z) * 2 * patches
            rows = pl.ds(pl.multiple_of(first, 2 * patches), 2 * patches)
            values = nt(dxz[rows, :], w_xz[...]) + nt(dbcdt[rows, :], w_bcdt[...])
            partial_rows[m, z, :, :, :width] = values.astype(LOW).reshape(2, patches, width)
        return carry

    lax.fori_loop(0, narrow, rows_of, 0)

    def weight_grads(m, carry):
        span = width // narrow
        columns = pl.ds(pl.multiple_of(m * span, span), span)
        lhs = normed[:, columns]
        grads[pl.ds(m * 2 * depth, 2 * depth)] = (
            tn(lhs, dxz[...]).astype(LOW).reshape(2 * depth, own_rows, 2 * HEAD_M)
        )
        partial_rows[m, :, :, :, width:] = (
            tn(lhs, dbcdt[...]).astype(LOW).reshape(depth, 2, own_rows, 3 * STATE)
        )
        return carry

    lax.fori_loop(0, narrow, weight_grads, 0)
    to_twin = remote(partial_rows.at[:, :, 1 - core], core_got, core_send, core_recv, twin)
    to_twin.start()
    send_blocks(me, devices, wide, grads, grads_got, grads_send, grads_recv)
    grads_got[me] = grads[me]
    back.arrive()
    gate_out[...] = gate_got[...].astype(FULL)
    to_twin.wait_recv()

    def narrow_copy(k, m):
        return remote(
            core_got.at[m], narrow_got.at[k - 1], narrow_send.at[k - 1], narrow_recv.at[k - 1], (m, w)
        )

    for k in range(1, narrow):
        m = lax.rem(n + k, narrow)
        for z in range(depth):
            core_got[m, z] = (
                core_got[m, z].astype(FULL) + partial_rows[m, z, core].astype(FULL)
            ).astype(LOW)
        narrow_copy(k, m).start()
    mix_gather.cross()
    middle_line.arrive()
    for z in range(depth):
        middle_sums[z] = middle_line.total(z).astype(LOW)
    for k in range(1, narrow):
        narrow_copy(k, n).wait_recv()
    for z in range(depth):
        total_rows = core_got[n, z].astype(FULL) + partial_rows[n, z, core].astype(FULL)
        for k in range(1, narrow):
            total_rows += narrow_got[k - 1, z].astype(FULL)
        z_rows[z] = total_rows.astype(LOW)

    def z_copy(k, place):
        return remote(
            z_rows.at[place], z_got.at[k - 1], z_send.at[k - 1], z_recv.at[k - 1], (n, place * 2 + core)
        )

    for k in range(1, depth):
        z_copy(k, lax.rem(z_place + k, depth)).start()
    for line, out in zip(lines, (down_sum, up_sum)):
        line.arrive()
        out[...] = line.total().astype(LOW)
    wait_blocks(me, devices, wide, grads_got, grads_send, grads_recv)
    xz_grads[...] = grads_got[...]
    total_rows = z_rows[z_place].astype(FULL)
    for k in range(1, depth):
        z_copy(k, z_place).wait_recv()
        total_rows += z_got[k - 1].astype(FULL)
    bcdt_grads[...] = total_rows[:, width:]
    unit, scale = unit_rows(mixed_in[...])
    normed_grad = total_rows[:, :width]
    embed_grad = global_grad[...] + norm_back(normed_grad, gain[...], unit, scale)
    end_pack[:, :width] = embed_grad.astype(LOW)
    end_pack[:, width:] = gated_scale[...].astype(LOW)
    gain_mix_grad = jnp.sum(normed_grad * unit, axis=0, keepdims=True)
    wide_rows = [gain_mix_grad] + [gated_gain_grads[i : i + 1, :] for i in range(2)]
    wide_rows += [gain_grads[i : i + 1, :] for i in range(2)]
    wide_rows += [dwbc[i : i + 1, :] for i in range(CONV + 1)]
    wide_rows += [dwx[i : i + 1, :] for i in range(CONV + 1)]
    row = 0
    for values in wide_rows:
        for first in range(0, values.shape[1], 128):
            sums[row : row + 1, :] = values[:, first : first + 128]
            row += 1
    lane = lax.broadcasted_iota(jnp.int32, (1, 128), 1)
    sums[row : row + 1, :] = sum(
        jnp.where(lane == i, dnumbers[i : i + 1, :], 0.0) for i in range(3)
    )
    mix_gather.finish()
    for line in lines:
        line.finish()
    middle_line.finish()
    back.finish()
    to_twin.wait_send()
    for k in range(1, narrow):
        narrow_copy(k, n).wait_send()
    for k in range(1, depth):
        z_copy(k, z_place).wait_send()


def in_smem():
    return pl.BlockSpec(memory_space=pltpu.SMEM)


def in_vmem():
    return pl.BlockSpec(memory_space=pltpu.VMEM)


def mixer_front(scalars, gain, conv_weight, conv_bias, arrays, collective_id):
    narrow, wide = lax.axis_size(NARROW), lax.axis_size(WIDE)
    devices, depth = narrow * wide, wide // 2
    pack, table, xz_blocks, gate, up, down, middle, cotangent = arrays
    patches = cotangent.shape[0] // PATCH
    count = devices * patches
    units = gate.shape[1] // narrow
    dma = pltpu.SemaphoreType.DMA
    anywhere = pl.BlockSpec(memory_space=pl.ANY)

    def full(*shape):
        return jax.ShapeDtypeStruct(shape, FULL)

    def low(*shape):
        return jax.ShapeDtypeStruct(shape, LOW)

    outs = pl.pallas_call(
        partial(mixer_front_kernel, narrow, wide),
        out_shape=[
            low(count, D),
            low(count, D),
            low(count, 2 * HEAD_M),
            low(count, 2 * STATE),
            full(count, 1),
            full(count, HEAD_M),
            full(count, HEAD_M),
            full(count // QUERY, HEAD_M, STATE),
            full(patches, D),
            low(devices, patches, HEAD_M),
            full(count + 8, 8),
            full(narrow, patches * PATCH, 1),
            full(count, PATCH),
            low(narrow, depth, 2, *pack.shape),
            low(*xz_blocks.shape),
            low(depth, 2, D, units),
            low(depth, 2, D, units),
            low(depth, 2, units, D),
            low(narrow, depth, 2, *middle.shape),
            low(narrow, *cotangent.shape),
        ],
        in_specs=[in_smem()] * 5 + [in_vmem()] * 3 + [anywhere] * 8,
        out_specs=[in_vmem()] * 15 + [anywhere] * 5,
        scratch_shapes=[
            pltpu.VMEM((narrow, depth, 2) + table.shape, FULL),
            pltpu.VMEM((D, units), LOW),
            pltpu.VMEM((D, units), LOW),
            pltpu.VMEM((units, D), LOW),
            pltpu.VMEM((count, D), FULL),
            pltpu.VMEM((count + 8, 2 * HEAD_M), FULL),
            pltpu.VMEM((count + 8, 2 * STATE), FULL),
            pltpu.VMEM((HEAD_M, STATE), FULL),
            pltpu.VMEM((devices, patches, HEAD_M), LOW),
            dma,
            dma,
            dma((7,)),
            dma((7,)),
            dma((2,)),
            dma((narrow - 1, 3)),
            dma((narrow - 1, 3)),
            dma((5,)),
            dma((depth,)),
            dma((depth,)),
            dma((narrow,)),
            dma((narrow,)),
            dma((3,)),
            dma((3, depth, 2)),
            dma((3, depth)),
            dma((3,)),
            dma((3,)),
            dma((2, 8, depth)),
        ],
        compiler_params=pltpu.CompilerParams(
            collective_id=collective_id, has_side_effects=True, vmem_limit_bytes=52 << 20
        ),
        name="mixer_front",
    )(*scalars, gain, conv_weight, conv_bias, *arrays)
    start, w_xz, gate_all, up_all, down_all, middle_all, others = outs[13:]
    return (
        outs[:13],
        start.reshape(D, -1),
        w_xz.reshape(D, -1),
        gate_all.reshape(wide, D, -1),
        up_all.reshape(wide, D, -1),
        down_all.reshape(-1, D),
        middle_all.reshape(D, -1),
        others,
    )


def mixer_backward(
    scalars,
    xz,
    bc,
    dt,
    marks,
    conv_weight,
    conv_bias,
    y,
    states,
    normed,
    w_xz,
    start,
    mixed_in,
    global_grad,
    gain,
    gated_scale,
    gain_grads,
    gated_gain_grads,
    du_blocks,
    up_parts,
    down_parts,
    middle_parts,
    gate_sum,
    mix_grad,
    collective_id,
):
    narrow, wide = lax.axis_size(NARROW), lax.axis_size(WIDE)
    devices = narrow * wide
    count, width = normed.shape
    patches = count // devices
    own_rows = width // devices
    dma = pltpu.SemaphoreType.DMA
    low = partial(pltpu.VMEM, dtype=LOW)
    every = width + 3 * STATE
    back_shape = (gate_sum.shape[0] // narrow, gate_sum.shape[1] * narrow)
    anywhere = pl.BlockSpec(memory_space=pl.ANY)
    return pl.pallas_call(
        partial(mixer_backward_kernel, narrow, wide),
        out_shape=[
            jax.ShapeDtypeStruct((patches, width + 128), LOW),
            jax.ShapeDtypeStruct((SUM_ROWS + CONV + 2, 128), FULL),
            jax.ShapeDtypeStruct((own_rows, 3 * STATE), FULL),
            jax.ShapeDtypeStruct((devices, own_rows, 2 * HEAD_M), LOW),
            jax.ShapeDtypeStruct(up_parts.shape[1:], LOW),
            jax.ShapeDtypeStruct(down_parts.shape[1:], LOW),
            jax.ShapeDtypeStruct(middle_parts.shape[1:], LOW),
            jax.ShapeDtypeStruct(back_shape, FULL),
            jax.ShapeDtypeStruct((narrow, wide // 2, 2) + mix_grad.shape, LOW),
        ],
        in_specs=[in_smem()] * 3
        + [in_vmem()] * 10
        + [anywhere]
        + [in_vmem()] * 7
        + [anywhere] * 5,
        out_specs=[in_vmem()] * 8 + [anywhere],
        scratch_shapes=[
            low((width, 3 * STATE)),
            dma,
            pltpu.VMEM((8, 2 * HEAD_M), FULL),
            pltpu.VMEM((8, 2 * STATE), FULL),
            pltpu.VMEM((8, 128), FULL),
            pltpu.VMEM((count + 8, 2 * HEAD_M), FULL),
            pltpu.VMEM((count + 8, 2 * STATE), FULL),
            pltpu.VMEM((count + 8, 2 * HEAD_M), FULL),
            pltpu.VMEM((count + 8, 2 * STATE), FULL),
            pltpu.VMEM((HEAD_M, STATE), FULL),
            low((devices, patches, HEAD_M)),
            low((count, 2 * HEAD_M)),
            low((count, 3 * STATE)),
            low((narrow, wide // 2, 2, patches, every)),
            low((narrow, wide // 2, patches, every)),
            low((narrow - 1, wide // 2, patches, every)),
            low((wide // 2, patches, every)),
            low((wide // 2 - 1, patches, every)),
            low((devices, own_rows, 2 * HEAD_M)),
            low((devices, own_rows, 2 * HEAD_M)),
            low(up_parts.shape),
            low(down_parts.shape),
            low(middle_parts.shape[1:]),
            low((2, wide // 4) + middle_parts.shape[2:]),
            low((6, wide // 4) + middle_parts.shape[2:]),
            low(back_shape),
            dma,
            dma,
            dma,
            dma,
            dma((narrow - 1,)),
            dma((narrow - 1,)),
            dma((wide // 2 - 1,)),
            dma((wide // 2 - 1,)),
            dma,
            dma,
            dma((wide,)),
            dma((wide,)),
            dma((2, 8)),
            dma((narrow - 1,)),
            dma((narrow - 1,)),
            dma,
            dma((7,)),
        ],
        compiler_params=pltpu.CompilerParams(
            collective_id=collective_id, has_side_effects=True, vmem_limit_bytes=36 << 20
        ),
        name="mixer_backward",
    )(
        *scalars,
        xz,
        bc,
        dt,
        marks,
        conv_weight,
        conv_bias,
        y,
        states,
        normed,
        w_xz,
        start,
        mixed_in,
        global_grad,
        gain,
        gated_scale,
        gain_grads,
        gated_gain_grads,
        du_blocks,
        up_parts,
        down_parts,
        middle_parts,
        gate_sum,
        mix_grad,
    )


def finish_kernel(
    pack_all,
    mix_all,
    u,
    keep,
    middle,
    xz_grads,
    bcdt_grads,
    gated_gain,
    embedded,
    start,
    table_out,
    patch_out,
    in_out,
    out_out,
    local_out,
    query_out,
    key_out,
    value_out,
    attn_out,
    embedded_own,
    ids_all,
    patch_all,
    rows_of_four,
    sems,
):
    me = lax.axis_index(NARROW) * lax.axis_size(WIDE) + lax.axis_index(WIDE)
    own_rows = patch_out.shape[0]
    group = 128 // own_rows
    columns = pl.ds(pl.multiple_of(lax.div(me, group) * 128, 128), 128)
    copies = [
        pltpu.make_async_copy(embedded.at[:, columns], embedded_own, sems.at[0]),
        pltpu.make_async_copy(start.at[:, pl.ds(3 * STATE, 128)], ids_all, sems.at[1]),
        pltpu.make_async_copy(start.at[:, pl.ds(4 * STATE, D)], patch_all, sems.at[2]),
    ]
    for copy in copies:
        copy.start()
    for i, out in enumerate((query_out, key_out, value_out, attn_out)):
        out[...] = middle[:, i * D : (i + 1) * D]
    local_out[...] = middle[:, 4 * D :].T
    for pair in range(0, HEADS_M, 2):
        both = [xz_grads[pair + i].astype(FULL) for i in range(2)]
        first = pair * HEAD_M
        in_out[:, first : first + 128] = jnp.concatenate([v[:, HEAD_M:] for v in both], axis=1)
        in_out[:, DI + first : DI + first + 128] = jnp.concatenate(
            [v[:, :HEAD_M] for v in both], axis=1
        )
    in_out[:, 2 * DI : 2 * DI + 2 * STATE] = bcdt_grads[:, : 2 * STATE]
    in_out[:, 2 * DI + 2 * STATE :] = bcdt_grads[:, 2 * STATE : 2 * STATE + HEADS_M]
    scale = pack_all[:, D:].astype(FULL)[:, :HEAD_M]
    gain = head_columns(gated_gain, me)[:, :HEAD_M]
    gated = (u[...] * scale * gain).astype(LOW)
    out_out[...] = tn(gated, mix_all[...])
    copies[0].wait()
    copies[1].wait()
    grads = pack_all[:, :D]
    rows_of_four[...] = tn(embedded_own[...], grads)
    patch_out[...] = rows_of_four[pl.ds(pl.multiple_of(lax.rem(me, group) * own_rows, own_rows), own_rows), :]
    own_words = table_out.shape[0]
    count = pack_all.shape[0]
    lane = lax.broadcasted_iota(jnp.int32, (count, PATCH * own_words), 1)
    ids = jnp.zeros((count, PATCH * own_words), FULL)
    kept = jnp.zeros((count, PATCH * own_words), FULL)
    values = ids_all[...].astype(FULL)
    for k in range(PATCH):
        here = lax.div(lane, own_words) == k
        ids = jnp.where(here, values[:, k : k + 1], ids)
        kept = jnp.where(here, keep[:, k : k + 1], kept)
    words = (me * own_words + lax.rem(lane, own_words)).astype(FULL)
    sums = tn(jnp.where(ids == words, kept, 0.0).astype(LOW), grads)
    high = sums.astype(LOW)
    rest = (sums - high.astype(FULL)).astype(LOW)
    copies[2].wait()
    table = jnp.zeros(table_out.shape, FULL)
    for k in range(PATCH):
        rows = slice(k * own_words, (k + 1) * own_words)
        weight = patch_all[k * EMB : (k + 1) * EMB, :]
        table += nt(high[rows], weight) + nt(rest[rows], weight)
    table_out[...] = table


def finish(pack_all, mix_all, u, keep, middle, xz_grads, bcdt_grads, gated_gain, embedded, start):
    count = pack_all.shape[0]
    devices, own_rows = xz_grads.shape[:2]
    anywhere = pl.BlockSpec(memory_space=pl.ANY)

    def full(*shape):
        return jax.ShapeDtypeStruct(shape, FULL)

    return pl.pallas_call(
        finish_kernel,
        out_shape=[
            full(VOCAB // devices, EMB),
            full(own_rows, D),
            full(own_rows, 2 * DI + 2 * STATE + HEADS_M),
            full(DI // devices, D),
            full(EMB, own_rows),
        ]
        + [full(own_rows, D)] * 4,
        in_specs=[in_vmem()] * 8 + [anywhere] * 2,
        out_specs=[in_vmem()] * 9,
        scratch_shapes=[
            pltpu.VMEM((count, 128), LOW),
            pltpu.VMEM((count, 128), LOW),
            pltpu.VMEM((D, D), LOW),
            pltpu.VMEM((128, D), FULL),
            pltpu.SemaphoreType.DMA((3,)),
        ],
        compiler_params=pltpu.CompilerParams(vmem_limit_bytes=20 << 20),
        name="finish",
    )(pack_all, mix_all, u, keep, middle, xz_grads, bcdt_grads, gated_gain, embedded, start)


def patch_causal():
    row = lax.broadcasted_iota(jnp.int32, (BYTE_BLOCK, BYTE_BLOCK), 0)
    column = lax.broadcasted_iota(jnp.int32, (BYTE_BLOCK, BYTE_BLOCK), 1)
    return (lax.div(row, PATCH) == lax.div(column, PATCH)) & (row >= column)


def head_probs(q, k, causal):
    scores = jnp.where(causal, nt(q, k) * HEAD_A ** (-0.5), masked_score)
    grown = jnp.exp(scores - jnp.max(scores, axis=1, keepdims=True))
    return grown / jnp.sum(grown, axis=1, keepdims=True)


def of_head(block, half):
    lane = lax.broadcasted_iota(jnp.int32, block.shape, 1)
    return jnp.where(lax.div(lane, HEAD_A) == half, block, jnp.zeros_like(block))


def fetched(pack, places, blocks, sems):
    copies = []
    for i, place in enumerate(places):
        width = place.shape[1]
        start = blocks[i]
        copies.append(
            pltpu.make_async_copy(pack.at[:, pl.ds(start, width)], place, sems.at[i])
        )
        copies[-1].start()
    return [copy.wait for copy in copies]


def unit_rows(values):
    scale = lax.rsqrt(jnp.mean(values * values, axis=1, keepdims=True) + epsilon)
    return values * scale, scale


def norm_back(grad, gain, unit, scale):
    scaled = grad * gain
    return scale * (scaled - unit * jnp.mean(scaled * unit, axis=1, keepdims=True))


WEIGHT_STEP = 256


def attend_pairs(qkv, mixed):
    causal = patch_causal()
    blocks = qkv.shape[0] // BYTE_BLOCK

    def pair(i, carry):
        def lanes(part):
            start = part * D + i * (2 * HEAD_A)
            return pl.ds(pl.multiple_of(start, 2 * HEAD_A), 2 * HEAD_A)

        for block in range(blocks):
            rows = pl.ds(block * BYTE_BLOCK, BYTE_BLOCK)
            q, k, v = qkv[rows, lanes(0)], qkv[rows, lanes(1)], qkv[rows, lanes(2)]
            total = jnp.zeros(q.shape, FULL)
            for half in range(2):
                probs = head_probs(of_head(q, half), k, causal)
                total += nn(probs.astype(LOW), of_head(v, half))
            mixed[rows, lanes(0)] = total.astype(LOW)
        return carry

    lax.fori_loop(0, HEADS_A // 2, pair, 0)


def attend_pairs_back(qkv, heads_grad, qkv_grad):
    causal = patch_causal()
    blocks = qkv.shape[0] // BYTE_BLOCK
    scale = HEAD_A ** (-0.5)

    def pair(i, carry):
        def lanes(part):
            start = part * D + i * (2 * HEAD_A)
            return pl.ds(pl.multiple_of(start, 2 * HEAD_A), 2 * HEAD_A)

        for block in range(blocks):
            rows = pl.ds(block * BYTE_BLOCK, BYTE_BLOCK)
            q, k, v = qkv[rows, lanes(0)], qkv[rows, lanes(1)], qkv[rows, lanes(2)]
            g = heads_grad[rows, lanes(0)]
            dq = jnp.zeros(q.shape, FULL)
            dk = jnp.zeros(q.shape, FULL)
            dv = jnp.zeros(q.shape, FULL)
            for half in range(2):
                own_q, own_k, own_g = of_head(q, half), of_head(k, half), of_head(g, half)
                probs = head_probs(own_q, k, causal)
                dprobs = nt(own_g, v)
                dv += tn(probs.astype(LOW), own_g)
                dscores = probs * (dprobs - jnp.sum(probs * dprobs, axis=1, keepdims=True))
                dscores = dscores.astype(LOW)
                dq += nn(dscores, own_k)
                dk += tn(dscores, own_q)
            qkv_grad[rows, lanes(0)] = (dq * scale).astype(LOW)
            qkv_grad[rows, lanes(1)] = (dk * scale).astype(LOW)
            qkv_grad[rows, lanes(2)] = dv.astype(LOW)
        return carry

    lax.fori_loop(0, HEADS_A // 2, pair, 0)


def bytes_forward_kernel(
    u_blocks,
    mixed_in,
    gains,
    gated_gain,
    pack,
    gated_out,
    local_out,
    stream_out,
    normed_out,
    qkv,
    mixed,
    after_out,
    feed_out,
    w_out0,
    w_out1,
    w_local,
    w_q,
    w_k,
    w_v,
    w_attn,
    pieces,
    sems,
):
    places = (w_out0, w_out1, w_local, w_q, w_k, w_v, w_attn)
    blocks = [4 * D, 5 * D, 6 * D, 0, D, 2 * D, 3 * D]
    waits = fetched(pack, places, blocks, sems)
    patches = mixed_in.shape[0]
    half = HEAD_M // 2
    for i in range(2):
        for first in range(0, HEADS_M, 4):
            gated_out[i, :, first * half : (first + 4) * half] = jnp.concatenate(
                [
                    u_blocks[first + j].astype(FULL)[:, i * half : (i + 1) * half]
                    for j in range(4)
                ],
                axis=1,
            )
    held = [gated_out[0], gated_out[1]]
    square = sum(jnp.sum(v * v, axis=1, keepdims=True) for v in held)
    scale = lax.rsqrt(square / (2 * D) + epsilon)
    gated = [(held[i] * scale * gated_gain[i : i + 1, :]).astype(LOW) for i in range(2)]
    waits[0]()
    waits[1]()
    joined = mixed_in[...] + nn(gated[0], w_out0[...]) + nn(gated[1], w_out1[...])
    for k in range(PATCH):
        pieces[pl.ds(k, patches, stride=PATCH), :] = joined[:, k * EMB : (k + 1) * EMB]
    local = pieces[...].astype(LOW)
    local_out[...] = local
    waits[2]()
    stream = nt(local, w_local[...])
    stream_out[...] = stream
    normed = (unit_rows(stream)[0] * gains[0:1, :]).astype(LOW)
    normed_out[...] = normed
    for i, weight in enumerate((w_q, w_k, w_v)):
        waits[3 + i]()
        for first in range(0, D, WEIGHT_STEP):
            qkv[:, i * D + first : i * D + first + WEIGHT_STEP] = nn(
                normed, weight[:, first : first + WEIGHT_STEP]
            ).astype(LOW)
    attend_pairs(qkv, mixed)
    waits[6]()
    heads = mixed[...]
    for first in range(0, D, WEIGHT_STEP):
        columns = slice(first, first + WEIGHT_STEP)
        after_out[:, columns] = stream_out[:, columns] + nn(heads, w_attn[:, columns])
    feed_out[...] = (unit_rows(after_out[...])[0] * gains[1:2, :]).astype(LOW)


def bytes_forward(u_blocks, mixed_in, gains, gated_gain, pack):
    patches = mixed_in.shape[0]
    rows = patches * PATCH

    def full(shape, kind):
        return jax.ShapeDtypeStruct(shape, kind)

    return pl.pallas_call(
        bytes_forward_kernel,
        out_shape=[
            full((2, patches, D), FULL),
            full((rows, EMB), LOW),
            full((rows, D), FULL),
            full((rows, D), LOW),
            full((rows, 3 * D), LOW),
            full((rows, D), LOW),
            full((rows, D), FULL),
            full((rows, D), LOW),
        ],
        in_specs=[in_vmem()] * 4 + [pl.BlockSpec(memory_space=pl.ANY)],
        out_specs=[in_vmem()] * 8,
        scratch_shapes=[pltpu.VMEM((D, D), LOW)] * 2
        + [pltpu.VMEM((D, EMB), LOW)]
        + [pltpu.VMEM((D, D), LOW)] * 4
        + [pltpu.VMEM((rows, EMB), FULL), pltpu.SemaphoreType.DMA((7,))],
        compiler_params=pltpu.CompilerParams(vmem_limit_bytes=48 << 20),
        name="bytes_forward",
    )(u_blocks, mixed_in, gains, gated_gain, pack)


def bytes_backward_kernel(
    narrow,
    feed_in_grad,
    cotangent,
    keep,
    after,
    stream_in,
    normed_in,
    qkv,
    mixed,
    local_in,
    gated_rows,
    gains,
    gated_gain,
    pack,
    feed_parts,
    gate_parts,
    global_out,
    mix_out,
    scale_out,
    sums,
    gain_grads,
    gated_gain_grads,
    du_blocks,
    rows_out,
    gate_out,
    w_attn,
    w_q,
    w_k,
    w_v,
    w_local,
    w_out0,
    w_out1,
    after_grad,
    heads_grad,
    qkv_grad,
    pieces,
    parts_got,
    grads,
    grads_got,
    gate_got,
    sems,
    p_send,
    p_recv,
    t_send,
    t_recv,
    gate_sems,
):
    n, wide_place = lax.axis_index(NARROW), lax.axis_index(WIDE)
    core = lax.rem(wide_place, 2)
    twin = (n, wide_place + 1 - 2 * core)
    depth = gate_parts.shape[0]
    z_place = lax.div(wide_place, 2)
    line = LineSum(
        gate_parts, gate_got, gate_sems, z_place, depth, lambda there: (n, there * 2 + core)
    )

    def twin_copy(i, columns):
        return remote(
            grads.at[:, 1 - core, :, columns],
            grads_got.at[:, :, columns],
            t_send.at[i],
            t_recv.at[i],
            twin,
        )

    def give(i, columns, part):
        grads[:, :, :, columns] = part.astype(LOW).reshape(grads.shape[:3] + part.shape[1:])
        twin_copy(i, columns).start()

    def part_copy(k):
        peer = (square_peer(n, k), wide_place)
        return remote(feed_parts.at[k], parts_got.at[k], p_send.at[k - 1], p_recv.at[k - 1], peer)

    own_part = pltpu.make_async_copy(feed_parts.at[0], parts_got.at[0], sems.at[7])
    own_part.start()
    places = (w_attn, w_q, w_k, w_v, w_local, w_out0, w_out1)
    blocks = [3 * D, 0, D, 2 * D, 6 * D, 4 * D, 5 * D]
    waits = fetched(pack, places, blocks, sems)
    greet_lines(narrow, depth)
    line.start()
    for k in range(1, narrow):
        part_copy(k).start()
    patches = global_out.shape[0]
    unit, scale = unit_rows(after[...])
    grad = feed_in_grad[...].astype(LOW).astype(FULL)
    gain_grads[1:2, :] = jnp.sum(grad * unit, axis=0, keepdims=True)
    after_grad[...] = cotangent[...].astype(FULL) * keep[0] + norm_back(
        grad, gains[1:2, :], unit, scale
    )
    attn_grad = after_grad[...].astype(LOW)
    waits[0]()
    for first in range(0, D, WEIGHT_STEP):
        columns = slice(first, first + WEIGHT_STEP)
        heads_grad[:, columns] = nt(attn_grad, w_attn[columns, :]).astype(LOW)
        give(
            (3 * D + first) // WEIGHT_STEP,
            pl.ds(3 * D + first, WEIGHT_STEP),
            tn(mixed[...], attn_grad[:, columns]),
        )
    attend_pairs_back(qkv, heads_grad, qkv_grad)
    normed_grad = jnp.zeros(after_grad.shape, FULL)
    for i, weight in enumerate((w_q, w_k, w_v)):
        waits[1 + i]()
        normed_grad += nt(qkv_grad[:, i * D : (i + 1) * D], weight[...])
    unit, scale = unit_rows(stream_in[...])
    gain_grads[0:1, :] = jnp.sum(normed_grad * unit, axis=0, keepdims=True)
    stream_grad = (after_grad[...] + norm_back(normed_grad, gains[0:1, :], unit, scale)).astype(LOW)
    waits[4]()
    pieces[...] = nn(stream_grad, w_local[...])
    for k in range(PATCH):
        global_out[:, k * EMB : (k + 1) * EMB] = pieces[pl.ds(k, patches, stride=PATCH), :]
    mix_grad = global_out[...].astype(LOW)
    mix_out[...] = mix_grad
    waits[5]()
    waits[6]()
    inner = [nt(mix_grad, w_out0[...]), nt(mix_grad, w_out1[...])]
    held = [gated_rows[0], gated_rows[1]]
    square = sum(jnp.sum(v * v, axis=1, keepdims=True) for v in held)
    scale = lax.rsqrt(square / (2 * D) + epsilon)
    units = [v * scale for v in held]
    scaled = [inner[i] * gated_gain[i : i + 1, :] for i in range(2)]
    mean = sum(jnp.sum(scaled[i] * units[i], axis=1, keepdims=True) for i in range(2)) / (2 * D)
    for i in range(2):
        gated_gain_grads[i : i + 1, :] = jnp.sum(inner[i] * units[i], axis=0, keepdims=True)
    scale_out[...] = jnp.broadcast_to(scale, scale_out.shape)
    rows_grads = [scale * (scaled[i] - units[i] * mean) for i in range(2)]
    half = HEAD_M // 2
    for head in range(HEADS_M):
        lanes = slice(head * half, (head + 1) * half)
        du_blocks[head] = jnp.concatenate([part[:, lanes] for part in rows_grads], axis=1).astype(LOW)
    give(4 * D // WEIGHT_STEP, pl.ds(4 * D, EMB), tn(stream_grad, local_in[...]))

    def weight_grads(i, carry):
        columns = pl.ds(pl.multiple_of(i * WEIGHT_STEP, WEIGHT_STEP), WEIGHT_STEP)
        give(i, columns, tn(normed_in[...], qkv_grad[:, columns]))
        return carry

    lax.fori_loop(0, 3 * D // WEIGHT_STEP, weight_grads, 0)
    own_part.wait()
    for k in range(1, narrow):
        part_copy(k).wait_recv()
    for first in range(0, D, WEIGHT_STEP):
        columns = slice(first, first + WEIGHT_STEP)
        feed = parts_got[0, :, columns].astype(FULL)
        for k in range(1, narrow):
            feed += parts_got[k, :, columns].astype(FULL)
        feed = feed.astype(LOW).astype(FULL)
        rows_out[:, columns] = ((after[:, columns] + feed) * keep[0]).astype(LOW)

    def add_twin(i, columns):
        twin_copy(i, columns).wait_recv()
        sums[:, :, columns] = (
            grads[:, core, :, columns].astype(FULL) + grads_got[:, :, columns].astype(FULL)
        ).astype(LOW)

    def add_one(i, carry):
        add_twin(i, pl.ds(pl.multiple_of(i * WEIGHT_STEP, WEIGHT_STEP), WEIGHT_STEP))
        return carry

    def end_one(i, carry):
        twin_copy(i, pl.ds(pl.multiple_of(i * WEIGHT_STEP, WEIGHT_STEP), WEIGHT_STEP)).wait_send()
        return carry

    steps = 4 * D // WEIGHT_STEP
    add_twin(steps, pl.ds(4 * D, EMB))
    lax.fori_loop(0, steps, add_one, 0)
    line.arrive()
    gate_out[...] = line.total().astype(LOW)
    line.finish()
    twin_copy(steps, pl.ds(4 * D, EMB)).wait_send()
    lax.fori_loop(0, steps, end_one, 0)
    for k in range(1, narrow):
        part_copy(k).wait_send()


def bytes_backward(
    feed_in_grad,
    cotangent,
    keep,
    after,
    stream,
    normed,
    qkv,
    mixed,
    local,
    gated_rows,
    gains,
    gated_gain,
    pack,
    feed_parts,
    gate_parts,
    collective_id,
):
    narrow = feed_parts.shape[0]
    every = 4 * D + EMB
    rows = after.shape[0]
    patches = rows // PATCH

    def full(shape, kind):
        return jax.ShapeDtypeStruct(shape, kind)

    return pl.pallas_call(
        partial(bytes_backward_kernel, narrow),
        out_shape=[
            full((patches, D), FULL),
            full((patches, D), LOW),
            full((patches, 128), FULL),
            full((HEADS_M // 2, D // HEADS_M, every), LOW),
            full((2, D), FULL),
            full((2, D), FULL),
            full((HEADS_M, patches, HEAD_M), LOW),
            full((rows, D), LOW),
            full(gate_parts.shape[1:], LOW),
        ],
        in_specs=[in_vmem()] * 12 + [pl.BlockSpec(memory_space=pl.ANY)] * 3,
        out_specs=[in_vmem()] * 9,
        scratch_shapes=[pltpu.VMEM((D, D), LOW)] * 4
        + [pltpu.VMEM((D, EMB), LOW)]
        + [pltpu.VMEM((D, D), LOW)] * 2
        + [
            pltpu.VMEM((rows, D), FULL),
            pltpu.VMEM((rows, D), LOW),
            pltpu.VMEM((rows, 3 * D), LOW),
            pltpu.VMEM((rows, EMB), FULL),
            pltpu.VMEM((narrow, rows, D), LOW),
            pltpu.VMEM((HEADS_M // 2, 2, D // HEADS_M, every), LOW),
            pltpu.VMEM((HEADS_M // 2, D // HEADS_M, every), LOW),
            pltpu.VMEM(gate_parts.shape, LOW),
            pltpu.SemaphoreType.DMA((8,)),
            pltpu.SemaphoreType.DMA((narrow - 1,)),
            pltpu.SemaphoreType.DMA((narrow - 1,)),
            pltpu.SemaphoreType.DMA((4 * D // WEIGHT_STEP + 1,)),
            pltpu.SemaphoreType.DMA((4 * D // WEIGHT_STEP + 1,)),
            pltpu.SemaphoreType.DMA((2 * gate_parts.shape[0],)),
        ],
        compiler_params=pltpu.CompilerParams(
            collective_id=collective_id, has_side_effects=True, vmem_limit_bytes=44 << 20
        ),
        name="bytes_backward",
    )(
        feed_in_grad,
        cotangent,
        keep,
        after,
        stream,
        normed,
        qkv,
        mixed,
        local,
        gated_rows,
        gains,
        gated_gain,
        pack,
        feed_parts,
        gate_parts,
    )


def feed_kernel(narrow, x_in, g_own, g_others, keep, *refs):
    gate_in, up_in, down_in, f_out, gx_out, gate_sum, up_sum, down_sum = refs[:8]
    wg, wu, wd, x, xt, g, hid, gg, gu, sent, got = refs[8:19]
    gate_twin, up_twin, down_twin, gate_got, up_got, down_got = refs[19:25]
    w_sem, g_sem, x_sem, x_send, x_recv, r_send, r_recv, t_send, t_recv = refs[25:]
    n, wide_place = lax.axis_index(NARROW), lax.axis_index(WIDE)
    core = lax.rem(wide_place, 2)
    twin = (n, wide_place + 1 - 2 * core)
    barrier = pltpu.get_barrier_semaphore()
    pl.semaphore_signal(barrier, inc=1, device_id=twin, device_id_type=MESH)
    for k in range(1, narrow):
        peer = (lax.rem(n + k, narrow), wide_place)
        pl.semaphore_signal(barrier, inc=1, device_id=peer, device_id_type=MESH)
    places, width, share = gate_in.shape
    rows = x_in.shape[0]
    hidden = places * share
    depth = places // 2
    chunk = 2 * share
    own_x = pltpu.make_async_copy(x_in, x.at[0], x_sem)
    own_x.start()
    g_copies = [
        pltpu.make_async_copy(g_own, g.at[0], g_sem.at[0]),
        pltpu.make_async_copy(
            g_others.at[pl.ds(1, narrow - 1)], g.at[pl.ds(1, narrow - 1)], g_sem.at[1]
        ),
    ]
    w_copies = [pltpu.make_async_copy(down_in, wd, w_sem.at[2 * places])]
    for place in range(places):
        units = slice(place * share, (place + 1) * share)
        w_copies.append(pltpu.make_async_copy(gate_in.at[place], wg.at[:, units], w_sem.at[place]))
        w_copies.append(
            pltpu.make_async_copy(up_in.at[place], wu.at[:, units], w_sem.at[places + place])
        )
    g_copies[0].start()
    for copy in w_copies:
        copy.start()
    for copy in g_copies[1:]:
        copy.start()
    pl.semaphore_wait(barrier, narrow)

    share_x = SquareShare(x_in, x, x_send, x_recv, n, wide_place)

    def r_copy(k):
        peer = (square_peer(n, k), wide_place)
        return remote(sent.at[k - 1], got.at[k - 1], r_send.at[k - 1], r_recv.at[k - 1], peer)

    share_x.start()
    own_x.wait()
    for copy in w_copies:
        copy.wait()
    for copy in g_copies:
        copy.wait()

    def block(k, carry):
        @pl.when(k == 1)
        def _():
            share_x.relay(0)
            share_x.relay(1)

        @pl.when(k == narrow - 1)
        def _():
            share_x.arrive()

        xk = x[k]
        gk = (g[k].astype(FULL) * keep[k]).astype(LOW)
        g[k] = gk
        xt[:, pl.ds(pl.multiple_of(k * rows, rows), rows)] = xk.T
        for first in range(0, hidden, chunk):
            units = slice(first, first + chunk)
            gate = nn(xk, wg[:, units])
            up = nn(xk, wu[:, units])
            dhid = nt(gk, wd[units, :])
            s = jax.nn.sigmoid(gate)
            act = gate * s
            hid[k, :, units] = (act * up).astype(LOW)
            gg[k, :, units] = (dhid * up * s * (1.0 + gate * (1.0 - s))).astype(LOW)
            gu[k, :, units] = (dhid * act).astype(LOW)
        ggk, guk, hidk = gg[k], gu[k], hid[k]
        for first in range(0, width, chunk):
            columns = slice(first, first + chunk)
            gx = nt(ggk, wg[columns, :]) + nt(guk, wu[columns, :])

            @pl.when(k == 0)
            def _():
                gx_out[:, columns] = gx

            @pl.when(k > 0)
            def _():
                sent[k - 1, :, columns] = gx.astype(LOW)

        @pl.when(k > 0)
        def _():
            r_copy(k).start()

        for first in range(0, width, chunk):
            columns = slice(first, first + chunk)
            f_out[k, :, columns] = nn(hidk, wd[:, columns]).astype(LOW)
        return carry

    lax.fori_loop(0, narrow, block, 0)

    def units_of(j, of_core):
        start = (2 * j + of_core) * share
        return pl.ds(pl.multiple_of(start, share), share)

    def two_places(left, j, of_core):
        pair = [left[:, :, units_of(2 * j + i, of_core)] for i in range(2)]
        return jnp.concatenate(pair, axis=2).reshape(narrow * rows, chunk)

    def columns_grads(left, j, of_core):
        total = nn(xt[...], two_places(left, j, of_core))
        return total[:, :share], total[:, share:]

    def rows_grads(j, of_core):
        total = tn(two_places(hid, j, of_core), g[...].reshape(narrow * rows, width))
        return total[:share], total[share:]

    outs = (gate_twin, up_twin, down_twin)
    ins = (gate_got, up_got, down_got)

    def t_copy(i, j):
        return remote(outs[i].at[j], ins[i].at[j], t_send.at[i, j], t_recv.at[i, j], twin)

    def for_twin(j, carry):
        for i, left in enumerate((gg, gu)):
            for half, part in enumerate(columns_grads(left, j, 1 - core)):
                outs[i][2 * j + half] = part.astype(LOW)
                t_copy(i, 2 * j + half).start()
        for half, part in enumerate(rows_grads(j, 1 - core)):
            outs[2][2 * j + half] = part.astype(LOW)
            t_copy(2, 2 * j + half).start()
        return carry

    def for_own(j, carry):
        for i, (left, total) in enumerate(((gg, gate_sum), (gu, up_sum))):
            for half, part in enumerate(columns_grads(left, j, core)):
                t_copy(i, 2 * j + half).wait_recv()
                total[2 * j + half] = (part + ins[i][2 * j + half].astype(FULL)).astype(LOW)
        for half, part in enumerate(rows_grads(j, core)):
            t_copy(2, 2 * j + half).wait_recv()
            down_sum[2 * j + half] = (part + ins[2][2 * j + half].astype(FULL)).astype(LOW)
        return carry

    lax.fori_loop(0, depth // 2, for_twin, 0)
    lax.fori_loop(0, depth // 2, for_own, 0)
    for k in range(1, narrow):
        r_copy(k).wait_recv()
        gx_out[...] += got[k - 1].astype(FULL)
    share_x.finish()
    for k in range(1, narrow):
        r_copy(k).wait_send()
    for i in range(3):
        for j in range(depth):
            t_copy(i, j).wait_send()


def feed_forward_back(x_own, g_own, g_others, keep, gate_all, up_all, down_all, collective_id):
    narrow = keep.shape[0]
    rows, width = x_own.shape
    places, _, share = gate_all.shape
    hidden, depth = places * share, places // 2
    dma = pltpu.SemaphoreType.DMA
    anywhere = pl.BlockSpec(memory_space=pl.ANY)

    def low(*shape):
        return pltpu.VMEM(shape, LOW)

    sums = [(depth, width, share), (depth, width, share), (depth, share, width)]
    return pl.pallas_call(
        partial(feed_kernel, narrow),
        out_shape=[
            jax.ShapeDtypeStruct((narrow, rows, width), LOW),
            jax.ShapeDtypeStruct((rows, width), FULL),
        ]
        + [jax.ShapeDtypeStruct(shape, LOW) for shape in sums],
        in_specs=[anywhere] * 3 + [in_vmem()] + [anywhere] * 3,
        out_specs=[in_vmem()] * 5,
        scratch_shapes=[
            low(width, hidden),
            low(width, hidden),
            low(hidden, width),
            low(narrow, rows, width),
            low(width, narrow * rows),
            low(narrow, rows, width),
            low(narrow, rows, hidden),
            low(narrow, rows, hidden),
            low(narrow, rows, hidden),
            low(narrow - 1, rows, width),
            low(narrow - 1, rows, width),
        ]
        + [low(*shape) for shape in sums + sums]
        + [
            dma((2 * places + 1,)),
            dma((2,)),
            dma,
            dma((narrow,)),
            dma((narrow,)),
            dma((narrow - 1,)),
            dma((narrow - 1,)),
            dma((3, depth)),
            dma((3, depth)),
        ],
        compiler_params=pltpu.CompilerParams(
            collective_id=collective_id, has_side_effects=True, vmem_limit_bytes=36 << 20
        ),
        name="feed",
    )(x_own, g_own, g_others, keep, gate_all, up_all, down_all)


def per_device_heads(
    byte_ids,
    doc_patches,
    pad_bytes,
    byte_table,
    patch_weight,
    gain_mix,
    in_weight,
    conv_weight,
    conv_bias,
    step_bias,
    log_rate,
    skip_gain,
    gated_gain,
    out_weight,
    local_weight,
    gain_attn,
    query_weight,
    key_weight,
    value_weight,
    attn_weight,
    feed_gain,
    gate_weight,
    up_weight,
    down_weight,
    cotangent,
):
    narrow, wide = lax.axis_size(NARROW), lax.axis_size(WIDE)
    devices = narrow * wide
    device = lax.axis_index(BOTH)
    rows = byte_ids.shape[0]
    patches = rows // PATCH
    everything = devices * patches
    own_rows = patch_weight.shape[0]
    hidden_width = gate_weight.shape[1]
    share = hidden_width // narrow

    ids_low = byte_ids.astype(LOW).reshape(patches, PATCH)
    bcdt_width = 2 * STATE + HEADS_M
    start_pack = jnp.concatenate(
        [
            jnp.pad(in_weight[:, 2 * DI :], ((0, 0), (0, 96))),
            jnp.pad(ids_low, ((0, 0), (0, 120))),
            patch_weight,
        ],
        axis=1,
    )
    xz_blocks = jnp.concatenate(
        [
            in_weight[:, DI : 2 * DI].reshape(own_rows, HEADS_M, HEAD_M),
            in_weight[:, :DI].reshape(own_rows, HEADS_M, HEAD_M),
        ],
        axis=2,
    ).transpose(1, 0, 2)
    middle_pack = jnp.concatenate(
        [
            query_weight,
            key_weight,
            value_weight,
            attn_weight,
            out_weight[:own_rows],
            out_weight[own_rows:],
            local_weight.T,
        ],
        axis=1,
    )
    numbers = (step_bias, log_rate, skip_gain)
    conv = (conv_weight, conv_bias[None])
    front, start_all, xz_weight, gate_all, up_all, down_all, middle_all, others = mixer_front(
        (doc_patches, pad_bytes) + numbers,
        gain_mix[None],
        *conv,
        (
            start_pack,
            byte_table.astype(FULL),
            xz_blocks,
            gate_weight,
            up_weight,
            down_weight,
            middle_pack,
            cotangent,
        ),
        5,
    )
    embedded, normed_all, xz, bc, dt, u, y, states, mixed_in, u_blocks, marks, keep_rows, keep_all = front
    half = HEAD_M // 2
    gated_gain_split = gated_gain.reshape(devices, 2, half).transpose(1, 0, 2).reshape(2, D)

    byte_gains = jnp.stack([gain_attn, feed_gain])
    (
        gated_rows,
        local_rows,
        stream,
        normed_attn,
        qkv,
        mixed_heads,
        after_attn,
        normed_feed,
    ) = bytes_forward(u_blocks, mixed_in, byte_gains, gated_gain_split, middle_all)
    feed_parts, feed_in_grad, gate_parts, up_parts, down_parts = feed_forward_back(
        normed_feed, cotangent, others, keep_rows, gate_all, up_all, down_all, 2
    )

    (
        global_grad,
        mix_grad,
        gated_scale,
        middle_parts,
        byte_gain_grads,
        gated_gain_grads,
        du_blocks,
        out_rows,
        gate_sum,
    ) = bytes_backward(
        feed_in_grad,
        cotangent,
        keep_rows,
        after_attn,
        stream,
        normed_attn,
        qkv,
        mixed_heads,
        local_rows,
        gated_rows,
        byte_gains,
        gated_gain_split,
        middle_all,
        feed_parts,
        gate_parts,
        4,
    )
    middle_parts = middle_parts.reshape(narrow, wide // 2, own_rows, -1)

    (
        end_pack,
        sums_pack,
        bcdt_grads,
        xz_grads,
        up_sum,
        down_sum,
        middle_sums,
        grad_gate,
        mix_grad_all,
    ) = mixer_backward(
        numbers,
        xz,
        bc,
        dt,
        marks,
        *conv,
        y,
        states,
        normed_all,
        xz_weight,
        start_all,
        mixed_in,
        global_grad,
        gain_mix[None],
        gated_scale,
        byte_gain_grads,
        gated_gain_grads,
        du_blocks,
        up_parts,
        down_parts,
        middle_parts,
        gate_sum,
        mix_grad,
        3,
    )
    mix_grad_all = mix_grad_all.reshape(everything, D)

    end_all, sums_all, middle_sums, grad_up, grad_down = end_gather(
        end_pack, sums_pack, middle_sums, up_sum, down_sum, 1
    )
    (
        grad_table,
        grad_patch,
        grad_in,
        grad_out,
        grad_local,
        grad_query,
        grad_key,
        grad_value,
        grad_attn,
    ) = finish(
        end_all,
        mix_grad_all,
        u,
        keep_all,
        middle_sums,
        xz_grads,
        bcdt_grads,
        gated_gain[None],
        embedded,
        start_all,
    )
    small = jnp.sum(sums_all[:, :SUM_ROWS], axis=0).reshape(-1)
    gain_grads = jnp.split(small[: 3 * D + DI], [D, D + DI, 2 * D + DI])
    gain_grads[1] = gain_grads[1].reshape(2, devices, half).transpose(1, 0, 2).reshape(DI)
    conv_own = sums_all[:, SUM_ROWS : SUM_ROWS + CONV + 1, :HEAD_M].transpose(1, 0, 2)
    conv_grads = jnp.concatenate(
        [conv_own.reshape(CONV + 1, DI), small[3 * D + DI :].reshape(CONV + 1, 2 * STATE)], axis=1
    )
    number_grads = sums_all[:, SUM_ROWS + CONV + 1, :3].T
    return (
        out_rows,
        grad_table,
        grad_patch,
        gain_grads[0],
        grad_in,
        conv_grads[:CONV],
        conv_grads[CONV],
        number_grads[0],
        number_grads[1],
        number_grads[2],
        gain_grads[1],
        grad_out,
        grad_local,
        gain_grads[2],
        grad_query,
        grad_key,
        grad_value,
        grad_attn,
        gain_grads[3],
        grad_gate,
        grad_up,
        grad_down,
    )


def solution(mesh):
    placed = (
        P((NARROW, WIDE)),
        P(),
        P(),
        P((NARROW, WIDE), None),
        P((NARROW, WIDE), None),
        P(),
        P((NARROW, WIDE), None),
        P(),
        P(),
        P(),
        P(),
        P(),
        P(),
        P((NARROW, WIDE), None),
        P(None, (NARROW, WIDE)),
        P(),
        P((NARROW, WIDE), None),
        P((NARROW, WIDE), None),
        P((NARROW, WIDE), None),
        P((NARROW, WIDE), None),
        P(),
        P(NARROW, WIDE),
        P(NARROW, WIDE),
        P(WIDE, NARROW),
        P((NARROW, WIDE), None),
    )
    return jax.shard_map(
        per_device_heads if mesh.size == HEADS_M else per_device_rows,
        mesh=mesh,
        in_specs=placed,
        out_specs=(
            P((NARROW, WIDE), None),
            P((NARROW, WIDE), None),
            P((NARROW, WIDE), None),
            P(),
            P((NARROW, WIDE), None),
            P(),
            P(),
            P(),
            P(),
            P(),
            P(),
            P((NARROW, WIDE), None),
            P(None, (NARROW, WIDE)),
            P(),
            P((NARROW, WIDE), None),
            P((NARROW, WIDE), None),
            P((NARROW, WIDE), None),
            P((NARROW, WIDE), None),
            P(),
            P(NARROW, WIDE),
            P(NARROW, WIDE),
            P(WIDE, NARROW),
        ),
        check_vma=False,
    )
```

```python
from functools import partial

import jax
import jax.numpy as jnp
from jax import lax
from jax.experimental import pallas as pl
from jax.experimental.pallas import tpu as pltpu
from jax.sharding import PartitionSpec as P

NARROW = "narrow"
WIDE = "wide"
D = 1024
PATCH = 8
EMB = 128
VOCAB = 256
HEADS_M = 32
HEAD_M = 64
DI = 2048
STATE = 128
CONV = 4
HEADS_A = 16
HEAD_A = 64


epsilon = 1e-05
highest = lax.Precision.HIGHEST
masked_score = -1e30


def running_sum(x):
    place = jnp.arange(x.shape[0])
    seen = place[:, None] >= place[None, :]
    if x.ndim == 1:
        return jnp.sum(jnp.where(seen, x[None, :], 0), axis=1).astype(x.dtype)
    return jnp.dot(seen.astype(x.dtype), x, precision=highest)


def passed_along(x, axis, by):
    peers = lax.axis_size(axis)
    pairs = [(i, i + by) for i in range(peers) if 0 <= i + by < peers]
    return lax.ppermute(x, axis, pairs)


def prefix_2(x, axis, join, neutral):
    place = lax.axis_index(axis)
    gathered = jax.tree.map(
        lambda a, kind: lax.all_gather(a.astype(kind), axis), x, (jnp.bfloat16, jnp.bfloat16)
    )
    state = jax.tree.map(lambda a, e: jnp.zeros_like(a) + jnp.asarray(e, a.dtype), x, neutral)

    def prefix_one(hop, state):
        return join(
            state,
            jax.tree.map(
                lambda a, own: lax.dynamic_index_in_dim(a, hop, 0, False).astype(own.dtype),
                gathered,
                x,
            ),
        )

    return lax.fori_loop(0, place, prefix_one, state)


def carried_in_2(x, axis, join, neutral):
    count = lax.axis_size(axis)
    place = lax.axis_index(axis)
    ahead = count - 1 - place
    gathered = jax.tree.map(
        lambda a, kind: lax.all_gather(a.astype(kind), axis),
        x,
        jax.tree.map(lambda a: jnp.bfloat16 if a.dtype == jnp.float32 else a.dtype, x),
    )
    state = jax.tree.map(lambda a, e: jnp.zeros_like(a) + jnp.asarray(e, a.dtype), x, neutral)

    def carried_one(hop, state):
        source = count - 1 - hop
        return join(
            state,
            jax.tree.map(
                lambda a, own: lax.dynamic_index_in_dim(a, source, 0, False).astype(own.dtype),
                gathered,
                x,
            ),
        )

    return lax.fori_loop(0, ahead, carried_one, state)


def root_norm(values, gain):
    return values * lax.rsqrt(jnp.mean(values * values, axis=-1, keepdims=True) + epsilon) * gain


def patch_layout(doc_patches, pad_bytes, first_index, patch_count):
    patch_index = first_index + jnp.arange(patch_count, dtype=jnp.int32)
    doc_ends = running_sum(doc_patches)
    doc_index = jnp.arange(doc_patches.shape[0], dtype=jnp.int32)
    segment = jnp.sum((patch_index[:, None] >= doc_ends[None, :]).astype(jnp.int32), axis=1)
    owner_mask = segment[:, None] == doc_index[None, :]
    last_end = jnp.sum(jnp.where(owner_mask, doc_ends[None, :] - 1, 0), axis=1)
    doc_starts = jnp.sum(jnp.where(owner_mask, (doc_ends - doc_patches)[None, :], 0), axis=1)
    pad_count = jnp.sum(jnp.where(owner_mask, pad_bytes[None, :], 0), axis=1)
    offset = jnp.arange(PATCH, dtype=jnp.int32)
    padded = (patch_index == last_end)[:, None] & (offset[None, :] >= PATCH - pad_count[:, None])
    keep_mask = 1.0 - padded.astype(jnp.float32).reshape(-1)
    return (segment, (patch_index == doc_starts).astype(jnp.int32), keep_mask)


def ssd_terms(layout, projected, rim_rows, small_params):
    conv_weight, conv_bias, step_bias, log_rate, skip_gain = small_params
    segment, rim_segment, first_patch = layout
    conv_in = projected[:, DI : 2 * DI + 2 * STATE]
    patch_count = conv_in.shape[0]
    padded = jnp.concatenate([rim_rows, conv_in], 0)
    padded_seg = jnp.concatenate([rim_segment, segment], 0)
    conv_sum = conv_bias
    for conv_tap in range(CONV):
        same_doc = (padded_seg[conv_tap : conv_tap + patch_count] == segment).astype(jnp.float32)[
            :, None
        ]
        conv_sum = (
            conv_sum + conv_weight[conv_tap] * padded[conv_tap : conv_tap + patch_count] * same_doc
        )
    activated = jax.nn.silu(conv_sum)
    values = activated[:, :DI].reshape(patch_count, HEADS_M, HEAD_M)
    input_map = activated[:, DI : DI + STATE]
    output_map = activated[:, DI + STATE :]
    time_steps = jax.nn.softplus(projected[:, 2 * DI + 2 * STATE :] + step_bias)
    cumulative = running_sum(-time_steps * jnp.exp(log_rate))
    no_reset = (running_sum(first_patch) == 0).astype(jnp.float32)
    return (values, input_map, output_map, time_steps, cumulative, no_reset)


def local_state(layout, projected, rim_rows, small_params):
    values, input_map, output_map, time_steps, cumulative, no_reset = ssd_terms(
        layout, projected, rim_rows, small_params
    )
    segment = layout[0]
    decay_tail = (
        jnp.exp(cumulative[-1][None, :] - cumulative)
        * (segment == segment[-1]).astype(jnp.float32)[:, None]
        * time_steps
    )
    state_local = jnp.einsum("sh,shp,sn->hpn", decay_tail, values, input_map, precision=highest)
    decay_total = jnp.exp(cumulative[-1]) * no_reset[-1]
    return (decay_total, state_local)


def mixer_output(layout, projected, rim_rows, small_params, incoming, gated_gain):
    values, input_map, output_map, time_steps, cumulative, no_reset = ssd_terms(
        layout, projected, rim_rows, small_params
    )
    segment = layout[0]
    patch_count = values.shape[0]
    position = jnp.arange(patch_count)
    visible = (segment[:, None] == segment[None, :]) & (position[:, None] >= position[None, :])
    log_gap = jnp.where(visible[:, :, None], cumulative[:, None, :] - cumulative[None, :, :], 0.0)
    inner = jnp.dot(output_map, input_map.T, precision=highest)
    weight = (
        jnp.exp(log_gap)
        * visible[:, :, None].astype(jnp.float32)
        * time_steps[None, :, :]
        * inner[:, :, None]
    )
    within = jnp.einsum("tsh,shp->thp", weight, values, precision=highest)
    carried_in = (
        jnp.einsum("tn,hpn->thp", output_map, incoming, precision=highest)
        * (jnp.exp(cumulative) * no_reset[:, None])[:, :, None]
    )
    result = (within + carried_in + small_params[4][None, :, None] * values).reshape(
        patch_count, DI
    )
    gated_rows = result * jax.nn.silu(projected[:, :DI])
    return root_norm(gated_rows, gated_gain)


def combine_states(earlier, following):
    return (earlier[0] * following[0], following[0][:, None, None] * earlier[1] + following[1])


def attend(stream, gain_attn, query_all, key_all, value_all):
    head_shape = (-1, PATCH, HEADS_A, HEAD_A)
    normed_attn = root_norm(stream, gain_attn).astype(jnp.bfloat16)
    queries = jnp.dot(normed_attn, query_all, preferred_element_type=jnp.float32).astype(
        jnp.bfloat16
    )
    key_rows = jnp.dot(normed_attn, key_all, preferred_element_type=jnp.float32).astype(
        jnp.bfloat16
    )
    value_rows = jnp.dot(normed_attn, value_all, preferred_element_type=jnp.float32).astype(
        jnp.bfloat16
    )
    scores = jnp.einsum(
        "pqhe,pkhe->phqk",
        queries.reshape(head_shape),
        key_rows.reshape(head_shape),
        preferred_element_type=jnp.float32,
    ) * HEAD_A ** (-0.5)
    position = jnp.arange(PATCH)
    causal = position[:, None] >= position[None, :]
    attn_probs = jax.nn.softmax(jnp.where(causal, scores, masked_score), axis=-1)
    mixed_heads = jnp.einsum(
        "phqk,pkhe->pqhe",
        attn_probs.astype(jnp.bfloat16),
        value_rows.reshape(head_shape),
        preferred_element_type=jnp.float32,
    )
    mixed_heads = mixed_heads.reshape(stream.shape[0], -1).astype(jnp.bfloat16)
    return (normed_attn, queries, key_rows, value_rows, attn_probs, mixed_heads)


def spread(values):
    by_rows = lax.all_to_all(values, NARROW, split_axis=1, concat_axis=0, tiled=True)
    return lax.all_gather(by_rows, WIDE, axis=0, tiled=True)


def collect(term_fn, row_count):
    summed = lax.psum_scatter(
        term_fn(jnp.int32(0), row_count * lax.axis_size(WIDE)).astype(jnp.bfloat16),
        WIDE,
        scatter_dimension=0,
        tiled=True,
    )
    return lax.all_to_all(summed, NARROW, split_axis=0, concat_axis=1, tiled=True)


def narrow_total(partial_rows):
    return lax.psum(partial_rows, NARROW).astype(jnp.float32)


def silu_back(gate_up, hidden_grad, hidden_width):
    gate_rows = gate_up[:, :hidden_width]
    up_rows = gate_up[:, hidden_width:]
    sigmoid = jax.nn.sigmoid(gate_rows)
    gate_grad = hidden_grad * up_rows * sigmoid * (1.0 + gate_rows * (1.0 - sigmoid))
    up_grad = hidden_grad * gate_rows * sigmoid
    return jnp.concatenate([gate_grad, up_grad], axis=1)


def per_device_rows(
    byte_ids,
    doc_patches,
    pad_bytes,
    byte_table,
    patch_weight,
    gain_mix,
    in_weight,
    conv_weight,
    conv_bias,
    step_bias,
    log_rate,
    skip_gain,
    gated_gain,
    out_weight,
    local_weight,
    gain_attn,
    query_weight,
    key_weight,
    value_weight,
    attn_weight,
    feed_gain,
    gate_weight,
    up_weight,
    down_weight,
    cotangent,
):
    byte_rows = byte_ids.shape[0]
    patches = byte_rows // PATCH
    device = lax.axis_index((NARROW, WIDE))
    wide_count = lax.axis_size(WIDE)
    segment, first_patch, keep_mask = patch_layout(
        doc_patches, pad_bytes, device * patches, patches
    )
    rim_segment = patch_layout(doc_patches, pad_bytes, device * patches - (CONV - 1), CONV - 1)[0]
    layout = (segment, rim_segment, first_patch)
    gathered = (
        lax.all_gather(byte_table, (NARROW, WIDE), axis=0, tiled=True),
        lax.all_gather(patch_weight, (NARROW, WIDE), axis=0, tiled=True),
        lax.all_gather(in_weight, (NARROW, WIDE), axis=0, tiled=True),
        lax.all_gather(out_weight, (NARROW, WIDE), axis=0, tiled=True),
        lax.all_gather(local_weight, (NARROW, WIDE), axis=1, tiled=True),
        lax.all_gather(query_weight, (NARROW, WIDE), axis=0, tiled=True),
        lax.all_gather(key_weight, (NARROW, WIDE), axis=0, tiled=True),
        lax.all_gather(value_weight, (NARROW, WIDE), axis=0, tiled=True),
        lax.all_gather(attn_weight, (NARROW, WIDE), axis=0, tiled=True),
    )
    table_all, patch_all, in_all, out_all, local_all, query_all, key_all, value_all, attn_all = (
        gathered
    )
    onehot = (byte_ids[:, None] == jnp.arange(VOCAB, dtype=jnp.int32)[None, :]).astype(jnp.bfloat16)
    embedded = (
        (jnp.dot(onehot, table_all, preferred_element_type=jnp.float32) * keep_mask[:, None])
        .astype(jnp.bfloat16)
        .reshape(patches, D)
    )
    mixed_in = jnp.dot(embedded, patch_all, preferred_element_type=jnp.float32)
    normed_mix = root_norm(mixed_in, gain_mix).astype(jnp.bfloat16)
    projected = jnp.dot(normed_mix, in_all, preferred_element_type=jnp.float32).astype(jnp.bfloat16)
    rim_rows = passed_along(
        projected[patches - (CONV - 1) :, DI : 2 * DI + 2 * STATE], (NARROW, WIDE), 1
    ).astype(jnp.float32)
    projected_f = projected.astype(jnp.float32)
    small_params = (conv_weight, conv_bias, step_bias, log_rate, skip_gain)
    (decay_total, state_local), state_back = jax.vjp(
        partial(local_state, layout), projected_f, rim_rows, small_params
    )
    prefix = prefix_2(
        (decay_total, state_local),
        (NARROW, WIDE),
        combine_states,
        (jnp.ones_like(decay_total), jnp.zeros_like(state_local)),
    )
    incoming = prefix[1]
    gated_norm, mixer_back = jax.vjp(
        partial(mixer_output, layout), projected_f, rim_rows, small_params, incoming, gated_gain
    )
    gated_low = gated_norm.astype(jnp.bfloat16)
    global_out = mixed_in + jnp.dot(gated_low, out_all, preferred_element_type=jnp.float32)
    local_rows = global_out.astype(jnp.bfloat16).reshape(byte_rows, EMB)
    stream = jnp.dot(local_rows, local_all, preferred_element_type=jnp.float32)
    normed_attn, queries, key_rows, value_rows, attn_probs, mixed_heads = attend(
        stream, gain_attn, query_all, key_all, value_all
    )
    after_attn = stream + jnp.dot(mixed_heads, attn_all, preferred_element_type=jnp.float32)
    normed_feed = root_norm(after_attn, feed_gain).astype(jnp.bfloat16)
    out_grad = cotangent.astype(jnp.float32) * keep_mask[:, None]
    feed_grad = out_grad.astype(jnp.bfloat16)
    grid_in = spread(normed_feed)
    both_weights = jnp.concatenate([gate_weight, up_weight], axis=1)
    hidden_width = gate_weight.shape[1]
    grid_share = grid_in.shape[0] // wide_count
    gate_up_part = jnp.dot(grid_in, both_weights, preferred_element_type=jnp.float32).astype(
        jnp.bfloat16
    )
    gate_up = narrow_total(gate_up_part)
    hidden = (jax.nn.silu(gate_up[:, :hidden_width]) * gate_up[:, hidden_width:]).astype(
        jnp.bfloat16
    )

    def down_term(first_row, row_count):
        return jnp.dot(hidden, down_weight, preferred_element_type=jnp.float32)

    feed_out = collect(down_term, grid_share)
    grid_grad = spread(feed_grad)
    grad_down = jnp.einsum("gf,gd->fd", hidden, grid_grad, preferred_element_type=jnp.float32)
    hidden_part = jnp.einsum(
        "gd,fd->gf", grid_grad, down_weight, preferred_element_type=jnp.float32
    ).astype(jnp.bfloat16)
    hidden_grad = narrow_total(hidden_part)
    gate_up_grad = silu_back(gate_up, hidden_grad, hidden_width).astype(jnp.bfloat16)
    grad_both = jnp.einsum("gd,gf->df", grid_in, gate_up_grad, preferred_element_type=jnp.float32)

    def back_term(first_row, row_count):
        return jnp.einsum(
            "gf,df->gd", gate_up_grad, both_weights, preferred_element_type=jnp.float32
        )

    feed_in_grad = collect(back_term, grid_share)
    grad_gate = grad_both[:, :hidden_width]
    grad_up = grad_both[:, hidden_width:]
    after_feed = after_attn + feed_out.astype(jnp.float32)
    out_rows = (after_feed * keep_mask[:, None]).astype(jnp.bfloat16)
    feed_normed, feed_norm_back = jax.vjp(root_norm, after_attn, feed_gain)
    after_norm_grad, grad_feed_gain = feed_norm_back(feed_in_grad.astype(jnp.float32))
    after_grad = out_grad + after_norm_grad
    head_shape = (-1, PATCH, HEADS_A, HEAD_A)
    score_scale = HEAD_A ** (-0.5)
    attn_grad = after_grad.astype(jnp.bfloat16)
    grad_attn = jnp.einsum("rd,re->de", mixed_heads, attn_grad, preferred_element_type=jnp.float32)
    heads_grad = (
        jnp.einsum("re,de->rd", attn_grad, attn_all, preferred_element_type=jnp.float32)
        .astype(jnp.bfloat16)
        .reshape(head_shape)
    )
    probs_grad = jnp.einsum(
        "pqhe,pkhe->phqk",
        heads_grad,
        value_rows.reshape(head_shape),
        preferred_element_type=jnp.float32,
    )
    value_grad = (
        jnp.einsum(
            "phqk,pqhe->pkhe",
            attn_probs.astype(jnp.bfloat16),
            heads_grad,
            preferred_element_type=jnp.float32,
        )
        .reshape(byte_rows, D)
        .astype(jnp.bfloat16)
    )
    score_grad = (
        attn_probs * (probs_grad - jnp.sum(attn_probs * probs_grad, axis=-1, keepdims=True))
    ).astype(jnp.bfloat16)
    query_grad = (
        (
            jnp.einsum(
                "phqk,pkhe->pqhe",
                score_grad,
                key_rows.reshape(head_shape),
                preferred_element_type=jnp.float32,
            )
            * score_scale
        )
        .reshape(byte_rows, D)
        .astype(jnp.bfloat16)
    )
    key_grad = (
        (
            jnp.einsum(
                "phqk,pqhe->pkhe",
                score_grad,
                queries.reshape(head_shape),
                preferred_element_type=jnp.float32,
            )
            * score_scale
        )
        .reshape(byte_rows, D)
        .astype(jnp.bfloat16)
    )
    grad_query = jnp.einsum(
        "rd,re->de", normed_attn, query_grad, preferred_element_type=jnp.float32
    )
    grad_key = jnp.einsum("rd,re->de", normed_attn, key_grad, preferred_element_type=jnp.float32)
    grad_value = jnp.einsum(
        "rd,re->de", normed_attn, value_grad, preferred_element_type=jnp.float32
    )
    normed_grad = jnp.einsum("re,de->rd", query_grad, query_all, preferred_element_type=jnp.float32)
    normed_grad = normed_grad + jnp.einsum(
        "re,de->rd", key_grad, key_all, preferred_element_type=jnp.float32
    )
    normed_grad = normed_grad + jnp.einsum(
        "re,de->rd", value_grad, value_all, preferred_element_type=jnp.float32
    )
    attn_normed, attn_norm_back = jax.vjp(root_norm, stream, gain_attn)
    stream_norm_grad, grad_gain_attn = attn_norm_back(normed_grad)
    stream_grad = (after_grad + stream_norm_grad).astype(jnp.bfloat16)
    grad_local = jnp.einsum(
        "re,rd->ed", local_rows, stream_grad, preferred_element_type=jnp.float32
    )
    global_grad = jnp.einsum(
        "rd,ed->re", stream_grad, local_all, preferred_element_type=jnp.float32
    ).reshape(patches, D)
    mix_grad = global_grad.astype(jnp.bfloat16)
    grad_out = jnp.einsum("pi,pd->id", gated_low, mix_grad, preferred_element_type=jnp.float32)
    gated_grad = jnp.einsum("pd,id->pi", mix_grad, out_all, preferred_element_type=jnp.float32)
    proj_grad_mix, rim_grad_mix, small_grad_mix, incoming_grad, grad_gated_gain = mixer_back(
        gated_grad
    )
    suffix = carried_in_2(
        (decay_total, incoming_grad),
        (NARROW, WIDE),
        combine_states,
        (jnp.ones_like(decay_total), jnp.zeros_like(incoming_grad)),
    )
    later_grad = suffix[1]
    decay_grad = jnp.sum(later_grad * incoming, axis=(1, 2))
    proj_grad_state, rim_grad_state, small_grad_state = state_back((decay_grad, later_grad))
    rim_from_next = passed_along(rim_grad_mix + rim_grad_state, (NARROW, WIDE), -1)
    proj_grad = proj_grad_mix + proj_grad_state
    proj_grad = proj_grad.at[patches - (CONV - 1) :, DI : 2 * DI + 2 * STATE].add(rim_from_next)
    proj_low = proj_grad.astype(jnp.bfloat16)
    grad_in = jnp.einsum("pd,pk->dk", normed_mix, proj_low, preferred_element_type=jnp.float32)
    normed_mix_grad = jnp.einsum("pk,dk->pd", proj_low, in_all, preferred_element_type=jnp.float32)
    mix_normed, mix_norm_back = jax.vjp(root_norm, mixed_in, gain_mix)
    mixed_norm_grad, grad_gain_mix = mix_norm_back(normed_mix_grad)
    embed_grad = (global_grad + mixed_norm_grad).astype(jnp.bfloat16)
    grad_patch = jnp.einsum("pi,pd->id", embedded, embed_grad, preferred_element_type=jnp.float32)
    byte_grad = (
        jnp.einsum("pd,id->pi", embed_grad, patch_all, preferred_element_type=jnp.float32).reshape(
            byte_rows, EMB
        )
        * keep_mask[:, None]
    )
    grad_table = jnp.dot(onehot.astype(jnp.float32).T, byte_grad, precision=highest)
    shared = (
        lax.psum_scatter(grad_table, (NARROW, WIDE), scatter_dimension=0, tiled=True),
        lax.psum_scatter(grad_patch, (NARROW, WIDE), scatter_dimension=0, tiled=True),
        lax.psum_scatter(grad_in, (NARROW, WIDE), scatter_dimension=0, tiled=True),
        lax.psum_scatter(grad_out, (NARROW, WIDE), scatter_dimension=0, tiled=True),
        lax.psum_scatter(grad_local, (NARROW, WIDE), scatter_dimension=1, tiled=True),
        lax.psum_scatter(grad_query, (NARROW, WIDE), scatter_dimension=0, tiled=True),
        lax.psum_scatter(grad_key, (NARROW, WIDE), scatter_dimension=0, tiled=True),
        lax.psum_scatter(grad_value, (NARROW, WIDE), scatter_dimension=0, tiled=True),
        lax.psum_scatter(grad_attn, (NARROW, WIDE), scatter_dimension=0, tiled=True),
    )
    small_sum = lax.psum(
        (
            small_grad_mix[0] + small_grad_state[0],
            small_grad_mix[1] + small_grad_state[1],
            small_grad_mix[2] + small_grad_state[2],
            small_grad_mix[3] + small_grad_state[3],
            small_grad_mix[4] + small_grad_state[4],
            grad_gain_mix,
            grad_gated_gain,
            grad_gain_attn,
            grad_feed_gain,
        ),
        (NARROW, WIDE),
    )
    return (
        out_rows,
        shared[0],
        shared[1],
        small_sum[5],
        shared[2],
        small_sum[0],
        small_sum[1],
        small_sum[2],
        small_sum[3],
        small_sum[4],
        small_sum[6],
        shared[3],
        shared[4],
        small_sum[7],
        shared[5],
        shared[6],
        shared[7],
        shared[8],
        small_sum[8],
        grad_gate,
        grad_up,
        grad_down,
    )


QUERY = 128
BYTE_BLOCK = 128
MESH = pl.DeviceIdType.MESH
SUM_ROWS = (3 * D + DI + (CONV + 1) * 2 * STATE) // 128
LOW = jnp.bfloat16
FULL = jnp.float32
BOTH = (NARROW, WIDE)


def nn(a, b, precision=None):
    return lax.dot_general(
        a, b, (((1,), (0,)), ((), ())), precision=precision, preferred_element_type=FULL
    )


def nt(a, b, precision=None):
    return lax.dot_general(
        a, b, (((1,), (1,)), ((), ())), precision=precision, preferred_element_type=FULL
    )


def tn(a, b, precision=None):
    return lax.dot_general(
        a, b, (((0,), (0,)), ((), ())), precision=precision, preferred_element_type=FULL
    )


def device_at(place, wide):
    return (lax.div(place, wide), lax.rem(place, wide))


def remote(src, dst, send, recv, peer):
    return pltpu.make_async_remote_copy(
        src_ref=src, dst_ref=dst, send_sem=send, recv_sem=recv, device_id=peer, device_id_type=MESH
    )


def greet_all(devices, wide):
    me = lax.axis_index(NARROW) * wide + lax.axis_index(WIDE)
    barrier = pltpu.get_barrier_semaphore()

    def greet(k, carry):
        peer = device_at(lax.rem(me + k, devices), wide)
        pl.semaphore_signal(barrier, inc=1, device_id=peer, device_id_type=MESH)
        return carry

    lax.fori_loop(1, devices, greet, 0)
    return me, lambda: pl.semaphore_wait(barrier, devices - 1)


def send_blocks(me, devices, wide, src, dst, send, recv):
    def one(k, carry):
        place = lax.rem(me + k, devices)
        remote(src.at[place], dst.at[me], send, recv, device_at(place, wide)).start()
        return carry

    lax.fori_loop(1, devices, one, 0)


def wait_blocks(me, devices, wide, dst, send, recv):
    part = dst.at[pl.ds(0, devices - 1)]
    remote(part, part, send, recv, device_at(me, wide)).wait()


class StagedGather:
    def __init__(self, block, out, sems, narrow, depth):
        n, w = lax.axis_index(NARROW), lax.axis_index(WIDE)
        z, c = lax.div(w, 2), lax.rem(w, 2)
        self.out, self.narrow, self.depth = out, narrow, depth
        self.n, self.c = n, c
        self.sems = [sems.at[i] for i in range(7)]
        self.twin = (n, z * 2 + 1 - c)
        self.n_peers = [lax.rem(n + k, narrow) for k in range(1, narrow)]
        self.w = w
        self.own = pltpu.make_async_copy(block, out.at[n, z, c], self.sems[0])
        self.first = [
            remote(
                block,
                out.at[n, z, c],
                self.sems[1],
                self.sems[2],
                (n, lax.rem(z + k, depth) * 2 + c),
            )
            for k in range(1, depth)
        ]

    def wait_for(self, part, i):
        return remote(part, part, self.sems[i], self.sems[i + 1], self.twin)

    def z_part(self):
        return self.wait_for(self.out.at[self.n, pl.ds(0, self.depth - 1), self.c], 1)

    def n_part(self):
        return self.wait_for(self.out.at[pl.ds(0, self.narrow - 1), :, self.c], 3)

    def start(self):
        self.own.start()
        for copy in self.first:
            copy.start()

    def spread(self):
        self.own.wait()
        self.z_part().wait_recv()
        mine = self.out.at[self.n, :, self.c]
        for m in self.n_peers:
            remote(mine, mine, self.sems[3], self.sems[4], (m, self.w)).start()
        self.wait_for(mine, 5).start()

    def cross(self):
        self.n_part().wait_recv()
        for m in self.n_peers:
            self.wait_for(self.out.at[m, :, self.c], 5).start()

    def finish(self):
        self.wait_for(self.out.at[:, :, 1 - self.c], 5).wait()
        self.z_part().wait_send()
        self.n_part().wait_send()


def greet_lines(narrow, depth):
    n, w = lax.axis_index(NARROW), lax.axis_index(WIDE)
    z, c = lax.div(w, 2), lax.rem(w, 2)
    peers = [(n, lax.rem(z + k, depth) * 2 + c) for k in range(1, depth)]
    peers += [(lax.rem(n + k, narrow), w) for k in range(1, narrow)]
    peers += [(n, z * 2 + 1 - c)]
    barrier = pltpu.get_barrier_semaphore()
    for peer in peers:
        pl.semaphore_signal(barrier, inc=1, device_id=peer, device_id_type=MESH)
    pl.semaphore_wait(barrier, len(peers))


class LineSum:
    def __init__(self, parts, got, sems, place, length, peer_of):
        self.got, self.length = got, length
        self.own = pltpu.make_async_copy(parts.at[place], got.at[0], sems.at[0])
        self.copies = []
        for k in range(1, length):
            there = lax.rem(place + k, length)
            self.copies.append(
                remote(
                    parts.at[there], got.at[k], sems.at[2 * k - 1], sems.at[2 * k], peer_of(there)
                )
            )

    def start(self):
        self.own.start()
        for copy in self.copies:
            copy.start()

    def arrive(self):
        self.own.wait()
        for copy in self.copies:
            copy.wait_recv()

    def total(self, *index):
        summed = self.got[(0,) + index].astype(FULL)
        for k in range(1, self.length):
            summed += self.got[(k,) + index].astype(FULL)
        return summed

    def finish(self):
        for copy in self.copies:
            copy.wait_send()


def square_peer(n, k):
    x, y, kx, ky = lax.rem(n, 2), lax.div(n, 2), lax.rem(k, 2), lax.div(k, 2)
    return 2 * (y + ky - 2 * y * ky) + x + kx - 2 * x * kx


class SquareShare:
    def __init__(self, rows, got, send, recv, n, w):
        self.half = half = rows.shape[0] // 2
        low, high = pl.ds(0, half), pl.ds(half, half)
        beside, across = (square_peer(n, 1), w), (square_peer(n, 2), w)
        self.first = [
            remote(rows, got.at[1], send.at[1], recv.at[1], beside),
            remote(rows, got.at[2], send.at[2], recv.at[2], across),
        ]
        self.second = [
            remote(got.at[1, low], got.at[3, low], send.at[0], recv.at[0], across),
            remote(got.at[2, high], got.at[3, high], send.at[3], recv.at[3], beside),
        ]

    def start(self):
        for copy in self.first:
            copy.start()

    def relay(self, i):
        self.first[i].wait_recv()
        self.second[i].start()

    def arrive(self):
        for copy in self.second:
            copy.wait_recv()

    def finish(self):
        for copy in self.first + self.second:
            copy.wait_send()


def square_of(n, narrow):
    return n + 1 - 2 * lax.rem(n, 2), n + 2 - 4 * lax.div(n, 2), narrow - 1 - n


class SquareSum:
    def __init__(self, parts, own, held, got, sems, n, w, narrow):
        beside, across, corner = square_of(n, narrow)
        self.own, self.held, self.got = own, held, got
        self.half = half = parts.shape[1] // 2
        low, high = pl.ds(0, half), pl.ds(half, half)
        self.local = [
            pltpu.make_async_copy(parts.at[n], own, sems.at[0, 6]),
            pltpu.make_async_copy(parts.at[across, low], held.at[0], sems.at[0, 7]),
            pltpu.make_async_copy(parts.at[beside, high], held.at[1], sems.at[1, 6]),
        ]

        def send(i, src, peer):
            return remote(src, got.at[i], sems.at[0, i], sems.at[1, i], (peer, w))

        self.copies = [
            send(0, parts.at[corner, low], beside),
            send(1, parts.at[corner, high], across),
            send(2, parts.at[beside, low], beside),
            send(3, parts.at[across, high], across),
            send(4, held.at[1], beside),
            send(5, held.at[0], across),
        ]

    def start(self):
        for copy in self.local + self.copies[:4]:
            copy.start()

    def relay(self):
        for i in range(2):
            self.local[1 + i].wait()
            self.copies[i].wait_recv()
            for j in range(self.half):
                self.held[i, j] = (
                    self.held[i, j].astype(FULL) + self.got[i, j].astype(FULL)
                ).astype(LOW)
            self.copies[5 - i].start()

    def arrive(self):
        self.local[0].wait()
        for copy in self.copies[2:]:
            copy.wait_recv()

    def total(self, j):
        first, second = (2, 5) if j < self.half else (4, 3)
        summed = self.own[j].astype(FULL)
        for i in (first, second):
            summed += self.got[i, j % self.half].astype(FULL)
        return summed

    def finish(self):
        for copy in self.copies:
            copy.wait_send()


def end_kernel(
    narrow,
    depth,
    pack,
    sums,
    middle,
    up_sum,
    down_sum,
    pack_all,
    sums_all,
    middle_out,
    up_out,
    down_out,
    middle_got,
    up_got,
    down_got,
    pack_sems,
    sums_sems,
    middle_sems,
    back_send,
    back_recv,
    back_own,
):
    n, w = lax.axis_index(NARROW), lax.axis_index(WIDE)
    z, c = lax.div(w, 2), lax.rem(w, 2)
    greet_lines(narrow, depth)
    gathers = [
        StagedGather(pack, pack_all, pack_sems, narrow, depth),
        StagedGather(sums, sums_all, sums_sems, narrow, depth),
    ]
    line = LineSum(middle, middle_got, middle_sems, z, depth, lambda there: (n, there * 2 + c))
    backs = [
        Returned(
            values, landed, back_send.at[i], back_recv.at[i], back_own.at[i], n, w, narrow, i
        )
        for i, (values, landed) in enumerate(((up_sum, up_got), (down_sum, down_got)))
    ]
    for gather in gathers:
        gather.start()
    line.start()
    for back in backs:
        back.start()
    for gather in gathers:
        gather.spread()
    line.arrive()
    middle_out[...] = line.total()
    for gather in gathers:
        gather.cross()
    for back, landed, out in zip(backs, (up_got, down_got), (up_out, down_out)):
        back.arrive()
        out[...] = landed[...].astype(FULL)
    for gather in gathers:
        gather.finish()
    line.finish()
    for back in backs:
        back.finish()


class Returned:
    def __init__(self, values, got, send, recv, own, n, w, narrow, axis):
        span = values.shape[axis] // narrow
        other = values.shape[1 - axis]

        def block(m):
            mine = pl.ds(m * span, span)
            return values.at[mine, :] if axis == 0 else values.at[:, mine]

        there = pl.ds(n * other, other)
        landing = got.at[:, there] if axis == 0 else got.at[there, :]
        self.own = pltpu.make_async_copy(block(n), landing, own)
        self.copies = []
        for k in range(1, narrow):
            m = lax.rem(n + k, narrow)
            self.copies.append(
                remote(block(m), landing, send.at[k - 1], recv.at[k - 1], (m, w))
            )

    def start(self):
        self.own.start()
        for copy in self.copies:
            copy.start()

    def arrive(self):
        self.own.wait()
        for copy in self.copies:
            copy.wait_recv()

    def finish(self):
        for copy in self.copies:
            copy.wait_send()


def end_gather(pack, sums, middle, up_sum, down_sum, collective_id):
    narrow, wide = lax.axis_size(NARROW), lax.axis_size(WIDE)
    depth = wide // 2
    dma = pltpu.SemaphoreType.DMA
    anywhere = pl.BlockSpec(memory_space=pl.ANY)
    up_shape = (up_sum.shape[0] // narrow, up_sum.shape[1] * narrow)
    down_shape = (down_sum.shape[0] * narrow, down_sum.shape[1] // narrow)
    outs = pl.pallas_call(
        partial(end_kernel, narrow, depth),
        out_shape=[
            jax.ShapeDtypeStruct((narrow, depth, 2) + pack.shape, pack.dtype),
            jax.ShapeDtypeStruct((narrow, depth, 2) + sums.shape, sums.dtype),
            jax.ShapeDtypeStruct(middle.shape[1:], FULL),
            jax.ShapeDtypeStruct(up_shape, FULL),
            jax.ShapeDtypeStruct(down_shape, FULL),
        ],
        in_specs=[anywhere] * 5,
        out_specs=[anywhere] * 2 + [in_vmem()] * 3,
        scratch_shapes=[
            pltpu.VMEM(middle.shape, middle.dtype),
            pltpu.VMEM(up_shape, LOW),
            pltpu.VMEM(down_shape, LOW),
            dma((7,)),
            dma((7,)),
            dma((2 * depth,)),
            dma((2, narrow - 1)),
            dma((2, narrow - 1)),
            dma((2,)),
        ],
        compiler_params=pltpu.CompilerParams(
            collective_id=collective_id, has_side_effects=True, vmem_limit_bytes=10 << 20
        ),
        name="end_gather",
    )(pack, sums, middle, up_sum, down_sum)
    return [
        outs[0].reshape(-1, pack.shape[1]),
        outs[1].reshape((-1,) + sums.shape),
    ] + list(outs[2:])


def softplus(v):
    return jnp.maximum(v, 0.0) + jnp.log1p(jnp.exp(-jnp.abs(v)))


def convolved(window, marks, weight, bias):
    pre = bias + weight[CONV - 1 :] * window[8:]
    for lag in range(1, CONV):
        pre = pre + weight[CONV - 1 - lag : CONV - lag] * (
            window[8 - lag : 8 - lag + QUERY] * marks[:, lag : lag + 1]
        )
    return pre


def decays(marks, dt, step_bias, rate_scale):
    shape = (QUERY, QUERY)
    row = lax.broadcasted_iota(jnp.int32, shape, 0)
    column = lax.broadcasted_iota(jnp.int32, shape, 1)
    lower = (row >= column).astype(FULL)
    segment = jnp.broadcast_to(marks[:, :1], shape)
    visible = (segment == segment.T) & (row >= column)
    delta = jnp.broadcast_to(softplus(dt + step_bias), shape)
    total = nn(lower, -delta * rate_scale, highest)
    gap = jnp.where(visible, total - total.T, 0.0)
    decay = jnp.where(visible, jnp.exp(gap), 0.0)
    last = total[QUERY - 1 :, :]
    begun = jnp.exp(total) * marks[:, 4:5]
    tail = jnp.exp(last - total) * marks[:, 5:6]
    kept = jnp.exp(last) * marks[:1, 6:7]
    return lower, delta, decay, begun, tail, kept


def head_numbers(step_bias, log_rate, skip_gain, me):
    return step_bias[me], jnp.exp(jnp.full((1, QUERY), log_rate[me], FULL)), skip_gain[me]


def head_columns(values, me):
    start = pl.multiple_of(lax.div(me, 2) * 2 * HEAD_M, 2 * HEAD_M)
    pair = values[:, pl.ds(start, 2 * HEAD_M)]
    lane = lax.broadcasted_iota(jnp.int32, pair.shape, 1)
    moved = jnp.concatenate([pair[:, HEAD_M:], pair[:, :HEAD_M]], axis=1)
    odd = jnp.full(pair.shape, lax.rem(me, 2), jnp.int32) == 1
    return jnp.where(lane < HEAD_M, jnp.where(odd, moved, pair), 0.0)


def documents(doc_patches, pad_bytes):
    ends, end = [], 0
    for d in range(doc_patches.shape[0]):
        end = end + doc_patches[d]
        ends.append(end)

    def document(place):
        return sum((place >= end).astype(jnp.int32) for end in ends)

    def kept(place, offset):
        padded = [
            ((place == end - 1) & (offset >= PATCH - pad_bytes[d])).astype(FULL)
            for d, end in enumerate(ends)
        ]
        return 1.0 - sum(padded)

    return document, kept


def patch_marks(document, first, count):
    place = first + lax.broadcasted_iota(jnp.int32, (count, 8), 0)
    kind = lax.broadcasted_iota(jnp.int32, (count, 8), 1)
    opening = lax.div(place, QUERY) * QUERY
    block_mark = jnp.where(kind == CONV, opening - 1, opening + QUERY - 1)
    ahead = jnp.where(kind < CONV, place - kind, block_mark)
    facing = jnp.where(kind == CONV + 2, opening - 1, place)
    same = (document(ahead) == document(facing)) & (ahead >= 0) & (facing >= 0)
    return jnp.where(kind == 0, document(place).astype(FULL), same.astype(FULL))


def mixer_front_kernel(
    narrow,
    wide,
    doc_patches,
    pad_bytes,
    step_biases,
    log_rates,
    skip_gains,
    gain,
    conv_weight,
    conv_bias,
    pack,
    table,
    xz_blocks,
    gate,
    up,
    down,
    middle,
    cotangent,
    embedded,
    normed,
    xz,
    bc,
    dt,
    u_out,
    y_out,
    states,
    mixed_in,
    u_got,
    marks,
    keep_rows,
    keep_all,
    start,
    w_xz,
    gate_all,
    up_all,
    down_all,
    middle_all,
    others,
    table_all,
    gate_turned,
    up_turned,
    down_turned,
    mixed_all,
    xz_pad,
    bc_pad,
    state,
    u_blocks,
    u_send,
    u_recv,
    pack_sems,
    table_sems,
    xz_sems,
    turn_send,
    turn_recv,
    start_sems,
    depth_send,
    depth_recv,
    other_send,
    other_recv,
    own_sems,
    line_send,
    line_recv,
    cross_send,
    cross_recv,
    middle_sems,
):
    devices, depth = narrow * wide, wide // 2
    me, arrived = greet_all(devices, wide)
    n, w = lax.axis_index(NARROW), lax.axis_index(WIDE)
    z, c = lax.div(w, 2), lax.rem(w, 2)
    twin = (n, z * 2 + 1 - c)
    rows_in, units_in = gate.shape[0], gate.shape[1] // narrow
    columns_in = down.shape[1]
    gathers = [
        StagedGather(pack, start, pack_sems, narrow, depth),
        StagedGather(table, table_all, table_sems, narrow, depth),
    ]

    def pieces(m):
        mine = pl.ds(m * units_in, units_in)
        return (gate.at[:, mine], up.at[:, mine], down.at[mine, :])

    turned = (gate_turned, up_turned, down_turned)
    landing = (
        gate_turned.at[pl.ds(n * rows_in, rows_in), :],
        up_turned.at[pl.ds(n * rows_in, rows_in), :],
        down_turned.at[:, pl.ds(n * columns_in, columns_in)],
    )
    turns = []
    for k in range(1, narrow):
        m = lax.rem(n + k, narrow)
        for i, piece in enumerate(pieces(m)):
            turns.append(
                remote(piece, landing[i], turn_send.at[k - 1, i], turn_recv.at[k - 1, i], (m, w))
            )
    first_own = [
        pltpu.make_async_copy(piece, landing[i], start_sems.at[i])
        for i, piece in enumerate(pieces(n))
    ]
    own_xz = pltpu.make_async_copy(xz_blocks.at[me], w_xz.at[me], start_sems.at[3])
    own_middle = pltpu.make_async_copy(middle, middle_all.at[n, z, c], start_sems.at[4])

    def depth_copy(source, target):
        return remote(
            middle,
            middle_all.at[n, source, c],
            depth_send.at[target],
            depth_recv.at[source],
            (n, target * 2 + c),
        )

    share = SquareShare(cotangent, others, other_send, other_recv, n, w)
    results = (gate_all, up_all, down_all)
    own = [pltpu.make_async_copy(turned[i], results[i].at[z, c], own_sems.at[i]) for i in range(3)]
    beside, across, corner = square_of(n, narrow)

    def middle_copy(j, way, owner):
        there = middle_all.at[owner, j, c]
        peer = twin if way >= 4 else ((beside if way in (0, 3) else across), w)
        return remote(there, there, middle_sems.at[0, way, j], middle_sems.at[1, way, j], peer)

    def line_copy(i, source, step, src=None):
        there = results[i].at[source, c]
        return remote(
            there if src is None else src,
            there,
            line_send.at[i, source, max(step, 0)],
            line_recv.at[i, source],
            (n, (z + step) * 2 + c),
        )

    def along(i, source, step, src=None):
        @pl.when((z + step >= 0) & (z + step < depth))
        def _():
            line_copy(i, source, step, src).start()

    def middle_begin(j):
        @pl.when(z == j)
        def _():
            own_middle.wait()

        @pl.when(z != j)
        def _():
            depth_copy(j, z).wait_recv()

        for way in (0, 1, 7):
            middle_copy(j, way, n).start()

    def middle_on(j):
        middle_copy(j, 0, beside).wait_recv()
        if j % 2 == 0:
            middle_copy(j, 2, beside).start()
        middle_copy(j, 4, beside).start()
        middle_copy(j, 1, across).wait_recv()
        if j % 2 == 1:
            middle_copy(j, 3, across).start()
        middle_copy(j, 5, across).start()

    def line_side(distance, step):
        source = z - step * distance

        @pl.when((source >= 0) & (source < depth))
        def _():
            for i in range(3):
                line_copy(i, source, step).wait_recv()
                along(i, source, step)
                theirs = results[i].at[source, c]
                remote(theirs, theirs, cross_send.at[i], cross_recv.at[i], twin).start()

    def line_on(distance):
        @pl.when(2 * z < depth)
        def _():
            line_side(distance, 1)
            line_side(distance, -1)

        @pl.when(2 * z >= depth)
        def _():
            line_side(distance, -1)
            line_side(distance, 1)

    arrived()
    for gather in gathers:
        gather.start()
    for copy in turns + first_own + [own_xz, own_middle]:
        copy.start()
    send_blocks(me, devices, wide, xz_blocks, w_xz, xz_sems.at[0], xz_sems.at[1])
    for distance in range(1, depth):
        for target in (z + distance, z - distance):

            @pl.when((target >= 0) & (target < depth))
            def _():
                depth_copy(z, target).start()

    for gather in gathers:
        gather.spread()
    for copy in first_own[:3]:
        copy.wait()
    for copy in turns:
        copy.wait_recv()
    for i in range(3):
        along(i, z, 1, turned[i])
        along(i, z, -1, turned[i])
    for copy in own:
        copy.start()
    for gather in gathers:
        gather.cross()
    share.start()

    count = embedded.shape[0]
    patches = u_blocks.shape[1]
    block_rows = 2 * QUERY
    xz_pad[pl.ds(0, 8), :] = jnp.zeros((8, xz_pad.shape[1]), FULL)
    bc_pad[pl.ds(0, 8), :] = jnp.zeros((8, bc_pad.shape[1]), FULL)
    state[...] = jnp.zeros_like(state)
    step_bias, rate_scale, skip = head_numbers(step_biases, log_rates, skip_gains, me)
    document, kept_bytes = documents(doc_patches, pad_bytes)
    for first in range(0, count + 8, (count + 8) // 3):
        part = (count + 8) // 3
        marks[first : first + part, :] = patch_marks(document, first, part)
    byte = lax.broadcasted_iota(jnp.int32, keep_rows.shape[1:], 0)
    for k in range(narrow):
        there = (square_peer(n, k) * wide + w) * patches
        keep_rows[k] = kept_bytes(there + lax.div(byte, PATCH), lax.rem(byte, PATCH))
    wx, bx = head_columns(conv_weight, me), head_columns(conv_bias, me)
    wbc, bbc = conv_weight[:, DI:], conv_bias[:, DI:]
    for gather in gathers:
        gather.finish()
    own_xz.wait()
    wait_blocks(me, devices, wide, w_xz, xz_sems.at[0], xz_sems.at[1])
    words = lax.broadcasted_iota(jnp.int32, (block_rows, VOCAB), 1).astype(FULL)
    own_lane = lax.broadcasted_iota(jnp.int32, (block_rows, STATE), 1) == me

    word_rows = table_all[...].reshape(VOCAB, EMB).astype(LOW)

    def project(i, carry):
        rows = pl.ds(pl.multiple_of(i * block_rows, block_rows), block_rows)
        ids = start[i, :, :, :, 3 * STATE : 4 * STATE].reshape(block_rows, STATE).astype(FULL)
        place = i * block_rows + lax.broadcasted_iota(jnp.int32, (block_rows, PATCH), 0)
        kept = kept_bytes(place, lax.broadcasted_iota(jnp.int32, (block_rows, PATCH), 1))
        keep_all[rows, :] = kept
        for k in range(PATCH):
            chosen = jnp.where(ids[:, k : k + 1] == words, kept[:, k : k + 1], 0.0).astype(LOW)
            embedded[rows, k * EMB : (k + 1) * EMB] = nn(chosen, word_rows).astype(LOW)
        row_embedded = embedded[rows, :]
        for first in range(0, D, WEIGHT_STEP):
            columns = slice(first, first + WEIGHT_STEP)
            there = slice(4 * STATE + first, 4 * STATE + first + WEIGHT_STEP)
            weight = start[:, :, :, :, there].reshape(D, WEIGHT_STEP)
            mixed_all[rows, columns] = nn(row_embedded, weight)
        row_normed = (unit_rows(mixed_all[rows, :])[0] * gain[...]).astype(LOW)
        normed[rows, :] = row_normed
        row_xz = nn(row_normed, w_xz[...].reshape(D, 2 * HEAD_M)).astype(LOW)
        weight = start[:, :, :, :, : 3 * STATE].reshape(D, 3 * STATE)
        row_bcdt = nn(row_normed, weight).astype(LOW)
        xz[rows, :] = row_xz
        bc[rows, :] = row_bcdt[:, : 2 * STATE]
        own_dt = jnp.where(own_lane, row_bcdt[:, 2 * STATE :].astype(FULL), 0.0)
        dt[rows, :] = jnp.sum(own_dt, axis=1, keepdims=True)
        padded = pl.ds(pl.multiple_of(i * block_rows + 8, 8), block_rows)
        xz_pad[padded, :] = row_xz.astype(FULL)
        bc_pad[padded, :] = row_bcdt[:, : 2 * STATE].astype(FULL)
        return carry

    lax.fori_loop(0, count // block_rows, project, 0)
    for j in range(depth):
        middle_begin(j)
    for i in range(2):
        share.relay(i)
    mixed_in[...] = mixed_all[pl.ds(pl.multiple_of(me * patches, patches), patches), :]
    group = QUERY // patches

    def block(i, carry):
        first = pl.multiple_of(i * QUERY, QUERY)
        rows = pl.ds(first, QUERY)
        mark = marks[rows, :]
        act_x = jax.nn.silu(convolved(xz_pad[pl.ds(first, QUERY + 8), :], mark, wx, bx))
        act = jax.nn.silu(convolved(bc_pad[pl.ds(first, QUERY + 8), :], mark, wbc, bbc))
        x, b, c = act_x[:, :HEAD_M], act[:, :STATE], act[:, STATE:]
        lower, delta, decay, begun, tail, kept = decays(mark, dt[rows, :], step_bias, rate_scale)
        weight = nt(c, b, highest) * decay * delta.T
        held = state[...]
        states[i] = held
        y = (
            nn(weight, x, highest)
            + nt(c, held, highest) * begun[:, :HEAD_M]
            + skip * x
        )
        state[...] = held * kept + tn(x * (tail * delta)[:, :HEAD_M], b, highest)
        z = xz[rows, :].astype(FULL)[:, HEAD_M:]
        u = y * jax.nn.silu(z)
        y_out[rows, :] = y
        u_out[rows, :] = u
        u_blocks[pl.ds(i * group, group)] = u.astype(LOW).reshape(group, patches, HEAD_M)
        return carry

    lax.fori_loop(0, count // QUERY, block, 0)
    send_blocks(me, devices, wide, u_blocks, u_got, u_send, u_recv)
    u_got[me] = u_blocks[me]
    line_on(1)
    for copy in own:
        copy.wait()
    for i in range(3):
        mine = results[i].at[z, c]
        remote(mine, mine, cross_send.at[i], cross_recv.at[i], twin).start()
    middle_on(0)
    middle_on(1)
    line_on(2)
    middle_on(2)
    middle_on(3)
    for j in range(depth):
        middle_copy(j, 2 + j % 2, corner).wait_recv()
        middle_copy(j, 6, corner).start()
    line_on(3)
    wait_blocks(me, devices, wide, u_got, u_send, u_recv)
    share.arrive()
    share.finish()
    for copy in turns:
        copy.wait_send()
    for target in range(depth):

        @pl.when(target != z)
        def _():
            depth_copy(z, target).wait_send()

    for i in range(3):
        theirs = results[i].at[:, 1 - c]
        remote(theirs, theirs, cross_send.at[i], cross_recv.at[i], twin).wait()
    for j in range(depth):
        for way, owner in ((4, beside), (5, across), (6, corner), (7, n)):
            middle_copy(j, way, owner).wait()
        for way in (0, 1, 2 + j % 2):
            middle_copy(j, way, n).wait_send()
    for i in range(3):
        for source in range(depth):
            for step in (1, -1):

                @pl.when((step * (z - source) >= 0) & (z + step >= 0) & (z + step < depth))
                def _():
                    line_copy(i, source, step).wait_send()


def mixer_backward_kernel(
    narrow,
    wide,
    step_biases,
    log_rates,
    skip_gains,
    xz,
    bc,
    dt,
    marks,
    conv_weight,
    conv_bias,
    y_in,
    states,
    normed,
    w_xz,
    start,
    mixed_in,
    global_grad,
    gain,
    gated_scale,
    gain_grads,
    gated_gain_grads,
    du_blocks,
    up_parts,
    down_parts,
    middle_parts,
    gate_sum,
    mix_grad,
    end_pack,
    sums,
    bcdt_grads,
    xz_grads,
    up_sum,
    down_sum,
    middle_sums,
    gate_out,
    mix_all,
    w_bcdt,
    w_sem,
    dwx,
    dwbc,
    dnumbers,
    xz_pad,
    bc_pad,
    dx_pad,
    dbc_pad,
    dstate,
    du_got,
    dxz,
    dbcdt,
    partial_rows,
    core_got,
    narrow_got,
    z_rows,
    z_got,
    grads,
    grads_got,
    up_got,
    down_got,
    middle_own,
    middle_held,
    middle_got,
    gate_got,
    du_send,
    du_recv,
    core_send,
    core_recv,
    narrow_send,
    narrow_recv,
    z_send,
    z_recv,
    grads_send,
    grads_recv,
    up_sems,
    down_sems,
    middle_sems,
    back_send,
    back_recv,
    back_own,
    mix_sems,
):
    devices = narrow * wide
    depth = wide // 2
    me, arrived = greet_all(devices, wide)
    n, w = lax.axis_index(NARROW), lax.axis_index(WIDE)
    z_place, core = lax.div(w, 2), lax.rem(w, 2)
    twin = (n, z_place * 2 + 1 - core)
    count = xz.shape[0]
    blocks = count // QUERY
    xz_pad[pl.ds(0, 8), :] = jnp.zeros((8, xz_pad.shape[1]), FULL)
    bc_pad[pl.ds(0, 8), :] = jnp.zeros((8, bc_pad.shape[1]), FULL)
    dx_pad[pl.ds(count, 8), :] = jnp.zeros((8, dx_pad.shape[1]), FULL)
    dbc_pad[pl.ds(count, 8), :] = jnp.zeros((8, dbc_pad.shape[1]), FULL)
    dstate[...] = jnp.zeros_like(dstate)
    dwx[...] = jnp.zeros_like(dwx)
    dwbc[...] = jnp.zeros_like(dwbc)
    dnumbers[...] = jnp.zeros_like(dnumbers)
    step_bias, rate_scale, skip = head_numbers(step_biases, log_rates, skip_gains, me)
    wx, bx = head_columns(conv_weight, me), head_columns(conv_bias, me)
    wbc, bbc = conv_weight[:, DI:], conv_bias[:, DI:]
    weight_copy = pltpu.make_async_copy(start.at[:, pl.ds(0, 3 * STATE)], w_bcdt, w_sem)
    weight_copy.start()

    def fill(i, carry):
        first = pl.multiple_of(i * QUERY, QUERY)
        rows = pl.ds(first, QUERY)
        xz_pad[pl.ds(first + 8, QUERY), :] = xz[rows, :].astype(FULL)
        bc_pad[pl.ds(first + 8, QUERY), :] = bc[rows, :].astype(FULL)
        return carry

    arrived()
    send_blocks(me, devices, wide, du_blocks, du_got, du_send, du_recv)
    lines = [
        LineSum(parts, landed, line_sems, z_place, depth, lambda there: (n, there * 2 + core))
        for parts, landed, line_sems in (
            (down_parts, down_got, down_sems),
            (up_parts, up_got, up_sems),
        )
    ]
    middle_line = SquareSum(
        middle_parts, middle_own, middle_held, middle_got, middle_sems, n, w, narrow
    )
    back = Returned(gate_sum, gate_got, back_send, back_recv, back_own, n, w, narrow, 0)
    mix_gather = StagedGather(mix_grad, mix_all, mix_sems, narrow, depth)
    middle_line.start()
    mix_gather.start()
    for line in lines:
        line.start()
    back.start()
    du_got[me] = du_blocks[me]
    lax.fori_loop(0, blocks, fill, 0)
    wait_blocks(me, devices, wide, du_got, du_send, du_recv)
    patches = du_blocks.shape[1]
    group = QUERY // patches
    own_lane = lax.broadcasted_iota(jnp.int32, (QUERY, STATE), 1) == me

    def slope(pre):
        s = jax.nn.sigmoid(pre)
        return s * (1.0 + pre * (1.0 - s))

    def total(v):
        return jnp.sum(jnp.sum(v, axis=1, keepdims=True), axis=0, keepdims=True)

    def conv_back(pad, first, dpre_pad, dpre, weight, dw):
        mark = marks[pl.ds(first, QUERY), :]
        window = pad[pl.ds(first, QUERY + 8), :]
        later = dpre_pad[pl.ds(first, QUERY + 8), :]
        later_marks = marks[pl.ds(first, QUERY + 8), :]
        out = weight[CONV - 1 :] * dpre
        dw[CONV - 1 : CONV, :] += jnp.sum(dpre * window[8:], axis=0, keepdims=True)
        dw[CONV : CONV + 1, :] += jnp.sum(dpre, axis=0, keepdims=True)
        for lag in range(1, CONV):
            tap = CONV - 1 - lag
            out = out + weight[tap : tap + 1] * (
                (later * later_marks[:, lag : lag + 1])[lag : lag + QUERY]
            )
            dw[tap : tap + 1, :] += jnp.sum(
                dpre * (window[8 - lag : 8 - lag + QUERY] * mark[:, lag : lag + 1]),
                axis=0,
                keepdims=True,
            )
        return out

    def block(k, carry):
        i = blocks - 1 - k
        first = pl.multiple_of(i * QUERY, QUERY)
        rows = pl.ds(first, QUERY)
        mark = marks[rows, :]
        pre_x = convolved(xz_pad[pl.ds(first, QUERY + 8), :], mark, wx, bx)
        pre = convolved(bc_pad[pl.ds(first, QUERY + 8), :], mark, wbc, bbc)
        act = jax.nn.silu(pre)
        x, b, c = jax.nn.silu(pre_x)[:, :HEAD_M], act[:, :STATE], act[:, STATE:]
        step = dt[rows, :]
        lower, delta, decay, begun, tail, kept = decays(mark, step, step_bias, rate_scale)
        held, dheld = states[i], dstate[...]
        z = xz[rows, :].astype(FULL)[:, HEAD_M:]
        du = du_got[pl.ds(i * group, group)].astype(FULL).reshape(QUERY, HEAD_M)
        y = y_in[rows, :]
        dy = du * jax.nn.silu(z)
        dz = du * y * slope(z)
        scores = nt(c, b, highest)
        reach = decay * delta.T
        dweight = nt(dy, x, highest)
        dscores = dweight * reach
        fed = x * (tail * delta)[:, :HEAD_M]
        begun_dy = dy * begun[:, :HEAD_M]
        dc = nn(dscores, b, highest) + nn(begun_dy, held, highest)
        db = tn(dscores, c, highest) + nn(fed, dheld, highest)
        dfed = nt(b, dheld, highest)
        dx = skip * dy + tn(scores * reach, dy, highest) + (tail * delta)[:, :HEAD_M] * dfed
        moved = dweight * scores * decay
        turned = moved.T
        ddelta = jnp.sum(turned, axis=1, keepdims=True)
        dtotal = jnp.sum(moved * delta.T, axis=1, keepdims=True) - ddelta * delta[:, :1]
        dtotal += jnp.sum(begun_dy * nt(c, held, highest), axis=1, keepdims=True)
        dtail = jnp.sum(dfed * x, axis=1, keepdims=True)
        ddelta += dtail * tail[:, :1]
        dtail = dtail * (tail * delta)[:, :1]
        dtotal -= dtail
        dlast = jnp.sum(dtail, axis=0, keepdims=True) + total(dheld * held * kept)
        dlog = tn(lower, jnp.broadcast_to(dtotal, (QUERY, QUERY)), highest)[:, :1] + dlast
        ddelta -= dlog * rate_scale[:, :1]
        dstep = ddelta * jax.nn.sigmoid(step + step_bias)
        dbcdt[rows, 2 * STATE :] = jnp.where(own_lane, dstep, 0.0).astype(LOW)
        dnumbers[0:1, :] += jnp.broadcast_to(jnp.sum(dstep, axis=0, keepdims=True), (1, 128))
        dnumbers[1:2, :] -= jnp.broadcast_to(
            jnp.sum(dlog * delta[:, :1] * rate_scale[:, :1], axis=0, keepdims=True), (1, 128)
        )
        dnumbers[2:3, :] += jnp.broadcast_to(total(dy * x), (1, 128))
        dstate[...] = dheld * kept + tn(begun_dy, c, highest)
        dpre_x = jnp.concatenate([dx, jnp.zeros_like(dx)], axis=1) * slope(pre_x)
        dpre = jnp.concatenate([db, dc], axis=1) * slope(pre)
        dx_pad[rows, :] = dpre_x
        dbc_pad[rows, :] = dpre
        dxz[rows, :] = jnp.concatenate([dz, dz], axis=1).astype(LOW)
        return carry

    lax.fori_loop(0, blocks, block, 0)

    def unconvolve(i, carry):
        first = pl.multiple_of(i * QUERY, QUERY)
        rows = pl.ds(first, QUERY)
        dxr = conv_back(xz_pad, first, dx_pad, dx_pad[rows, :], wx, dwx)
        left = lax.broadcasted_iota(jnp.int32, dxr.shape, 1) < HEAD_M
        dxz[rows, :] = jnp.where(left, dxr, dxz[rows, :].astype(FULL)).astype(LOW)
        dbcdt[rows, : 2 * STATE] = conv_back(
            bc_pad, first, dbc_pad, dbc_pad[rows, :], wbc, dwbc
        ).astype(LOW)
        return carry

    middle_line.relay()
    mix_gather.spread()
    lax.fori_loop(0, blocks, unconvolve, 0)

    width = normed.shape[1]
    own_rows = xz_grads.shape[1]

    weight_copy.wait()

    def rows_of(m, carry):
        for z in range(depth):
            first = (m * depth + z) * 2 * patches
            rows = pl.ds(pl.multiple_of(first, 2 * patches), 2 * patches)
            values = nt(dxz[rows, :], w_xz[...]) + nt(dbcdt[rows, :], w_bcdt[...])
            partial_rows[m, z, :, :, :width] = values.astype(LOW).reshape(2, patches, width)
        return carry

    lax.fori_loop(0, narrow, rows_of, 0)

    def weight_grads(m, carry):
        span = width // narrow
        columns = pl.ds(pl.multiple_of(m * span, span), span)
        lhs = normed[:, columns]
        grads[pl.ds(m * 2 * depth, 2 * depth)] = (
            tn(lhs, dxz[...]).astype(LOW).reshape(2 * depth, own_rows, 2 * HEAD_M)
        )
        partial_rows[m, :, :, :, width:] = (
            tn(lhs, dbcdt[...]).astype(LOW).reshape(depth, 2, own_rows, 3 * STATE)
        )
        return carry

    lax.fori_loop(0, narrow, weight_grads, 0)
    to_twin = remote(partial_rows.at[:, :, 1 - core], core_got, core_send, core_recv, twin)
    to_twin.start()
    send_blocks(me, devices, wide, grads, grads_got, grads_send, grads_recv)
    grads_got[me] = grads[me]
    back.arrive()
    gate_out[...] = gate_got[...].astype(FULL)
    to_twin.wait_recv()

    def narrow_copy(k, m):
        return remote(
            core_got.at[m], narrow_got.at[k - 1], narrow_send.at[k - 1], narrow_recv.at[k - 1], (m, w)
        )

    for k in range(1, narrow):
        m = lax.rem(n + k, narrow)
        for z in range(depth):
            core_got[m, z] = (
                core_got[m, z].astype(FULL) + partial_rows[m, z, core].astype(FULL)
            ).astype(LOW)
        narrow_copy(k, m).start()
    mix_gather.cross()
    middle_line.arrive()
    for z in range(depth):
        middle_sums[z] = middle_line.total(z).astype(LOW)
    for k in range(1, narrow):
        narrow_copy(k, n).wait_recv()
    for z in range(depth):
        total_rows = core_got[n, z].astype(FULL) + partial_rows[n, z, core].astype(FULL)
        for k in range(1, narrow):
            total_rows += narrow_got[k - 1, z].astype(FULL)
        z_rows[z] = total_rows.astype(LOW)

    def z_copy(k, place):
        return remote(
            z_rows.at[place], z_got.at[k - 1], z_send.at[k - 1], z_recv.at[k - 1], (n, place * 2 + core)
        )

    for k in range(1, depth):
        z_copy(k, lax.rem(z_place + k, depth)).start()
    for line, out in zip(lines, (down_sum, up_sum)):
        line.arrive()
        out[...] = line.total().astype(LOW)
    wait_blocks(me, devices, wide, grads_got, grads_send, grads_recv)
    xz_grads[...] = grads_got[...]
    total_rows = z_rows[z_place].astype(FULL)
    for k in range(1, depth):
        z_copy(k, z_place).wait_recv()
        total_rows += z_got[k - 1].astype(FULL)
    bcdt_grads[...] = total_rows[:, width:]
    unit, scale = unit_rows(mixed_in[...])
    normed_grad = total_rows[:, :width]
    embed_grad = global_grad[...] + norm_back(normed_grad, gain[...], unit, scale)
    end_pack[:, :width] = embed_grad.astype(LOW)
    end_pack[:, width:] = gated_scale[...].astype(LOW)
    gain_mix_grad = jnp.sum(normed_grad * unit, axis=0, keepdims=True)
    wide_rows = [gain_mix_grad] + [gated_gain_grads[i : i + 1, :] for i in range(2)]
    wide_rows += [gain_grads[i : i + 1, :] for i in range(2)]
    wide_rows += [dwbc[i : i + 1, :] for i in range(CONV + 1)]
    wide_rows += [dwx[i : i + 1, :] for i in range(CONV + 1)]
    row = 0
    for values in wide_rows:
        for first in range(0, values.shape[1], 128):
            sums[row : row + 1, :] = values[:, first : first + 128]
            row += 1
    lane = lax.broadcasted_iota(jnp.int32, (1, 128), 1)
    sums[row : row + 1, :] = sum(
        jnp.where(lane == i, dnumbers[i : i + 1, :], 0.0) for i in range(3)
    )
    mix_gather.finish()
    for line in lines:
        line.finish()
    middle_line.finish()
    back.finish()
    to_twin.wait_send()
    for k in range(1, narrow):
        narrow_copy(k, n).wait_send()
    for k in range(1, depth):
        z_copy(k, z_place).wait_send()


def in_smem():
    return pl.BlockSpec(memory_space=pltpu.SMEM)


def in_vmem():
    return pl.BlockSpec(memory_space=pltpu.VMEM)


def mixer_front(scalars, gain, conv_weight, conv_bias, arrays, collective_id):
    narrow, wide = lax.axis_size(NARROW), lax.axis_size(WIDE)
    devices, depth = narrow * wide, wide // 2
    pack, table, xz_blocks, gate, up, down, middle, cotangent = arrays
    patches = cotangent.shape[0] // PATCH
    count = devices * patches
    units = gate.shape[1] // narrow
    dma = pltpu.SemaphoreType.DMA
    anywhere = pl.BlockSpec(memory_space=pl.ANY)

    def full(*shape):
        return jax.ShapeDtypeStruct(shape, FULL)

    def low(*shape):
        return jax.ShapeDtypeStruct(shape, LOW)

    outs = pl.pallas_call(
        partial(mixer_front_kernel, narrow, wide),
        out_shape=[
            low(count, D),
            low(count, D),
            low(count, 2 * HEAD_M),
            low(count, 2 * STATE),
            full(count, 1),
            full(count, HEAD_M),
            full(count, HEAD_M),
            full(count // QUERY, HEAD_M, STATE),
            full(patches, D),
            low(devices, patches, HEAD_M),
            full(count + 8, 8),
            full(narrow, patches * PATCH, 1),
            full(count, PATCH),
            low(narrow, depth, 2, *pack.shape),
            low(*xz_blocks.shape),
            low(depth, 2, D, units),
            low(depth, 2, D, units),
            low(depth, 2, units, D),
            low(narrow, depth, 2, *middle.shape),
            low(narrow, *cotangent.shape),
        ],
        in_specs=[in_smem()] * 5 + [in_vmem()] * 3 + [anywhere] * 8,
        out_specs=[in_vmem()] * 15 + [anywhere] * 5,
        scratch_shapes=[
            pltpu.VMEM((narrow, depth, 2) + table.shape, FULL),
            pltpu.VMEM((D, units), LOW),
            pltpu.VMEM((D, units), LOW),
            pltpu.VMEM((units, D), LOW),
            pltpu.VMEM((count, D), FULL),
            pltpu.VMEM((count + 8, 2 * HEAD_M), FULL),
            pltpu.VMEM((count + 8, 2 * STATE), FULL),
            pltpu.VMEM((HEAD_M, STATE), FULL),
            pltpu.VMEM((devices, patches, HEAD_M), LOW),
            dma,
            dma,
            dma((7,)),
            dma((7,)),
            dma((2,)),
            dma((narrow - 1, 3)),
            dma((narrow - 1, 3)),
            dma((5,)),
            dma((depth,)),
            dma((depth,)),
            dma((narrow,)),
            dma((narrow,)),
            dma((3,)),
            dma((3, depth, 2)),
            dma((3, depth)),
            dma((3,)),
            dma((3,)),
            dma((2, 8, depth)),
        ],
        compiler_params=pltpu.CompilerParams(
            collective_id=collective_id, has_side_effects=True, vmem_limit_bytes=52 << 20
        ),
        name="mixer_front",
    )(*scalars, gain, conv_weight, conv_bias, *arrays)
    start, w_xz, gate_all, up_all, down_all, middle_all, others = outs[13:]
    return (
        outs[:13],
        start.reshape(D, -1),
        w_xz.reshape(D, -1),
        gate_all.reshape(wide, D, -1),
        up_all.reshape(wide, D, -1),
        down_all.reshape(-1, D),
        middle_all.reshape(D, -1),
        others,
    )


def mixer_backward(
    scalars,
    xz,
    bc,
    dt,
    marks,
    conv_weight,
    conv_bias,
    y,
    states,
    normed,
    w_xz,
    start,
    mixed_in,
    global_grad,
    gain,
    gated_scale,
    gain_grads,
    gated_gain_grads,
    du_blocks,
    up_parts,
    down_parts,
    middle_parts,
    gate_sum,
    mix_grad,
    collective_id,
):
    narrow, wide = lax.axis_size(NARROW), lax.axis_size(WIDE)
    devices = narrow * wide
    count, width = normed.shape
    patches = count // devices
    own_rows = width // devices
    dma = pltpu.SemaphoreType.DMA
    low = partial(pltpu.VMEM, dtype=LOW)
    every = width + 3 * STATE
    back_shape = (gate_sum.shape[0] // narrow, gate_sum.shape[1] * narrow)
    anywhere = pl.BlockSpec(memory_space=pl.ANY)
    return pl.pallas_call(
        partial(mixer_backward_kernel, narrow, wide),
        out_shape=[
            jax.ShapeDtypeStruct((patches, width + 128), LOW),
            jax.ShapeDtypeStruct((SUM_ROWS + CONV + 2, 128), FULL),
            jax.ShapeDtypeStruct((own_rows, 3 * STATE), FULL),
            jax.ShapeDtypeStruct((devices, own_rows, 2 * HEAD_M), LOW),
            jax.ShapeDtypeStruct(up_parts.shape[1:], LOW),
            jax.ShapeDtypeStruct(down_parts.shape[1:], LOW),
            jax.ShapeDtypeStruct(middle_parts.shape[1:], LOW),
            jax.ShapeDtypeStruct(back_shape, FULL),
            jax.ShapeDtypeStruct((narrow, wide // 2, 2) + mix_grad.shape, LOW),
        ],
        in_specs=[in_smem()] * 3
        + [in_vmem()] * 10
        + [anywhere]
        + [in_vmem()] * 7
        + [anywhere] * 5,
        out_specs=[in_vmem()] * 8 + [anywhere],
        scratch_shapes=[
            low((width, 3 * STATE)),
            dma,
            pltpu.VMEM((8, 2 * HEAD_M), FULL),
            pltpu.VMEM((8, 2 * STATE), FULL),
            pltpu.VMEM((8, 128), FULL),
            pltpu.VMEM((count + 8, 2 * HEAD_M), FULL),
            pltpu.VMEM((count + 8, 2 * STATE), FULL),
            pltpu.VMEM((count + 8, 2 * HEAD_M), FULL),
            pltpu.VMEM((count + 8, 2 * STATE), FULL),
            pltpu.VMEM((HEAD_M, STATE), FULL),
            low((devices, patches, HEAD_M)),
            low((count, 2 * HEAD_M)),
            low((count, 3 * STATE)),
            low((narrow, wide // 2, 2, patches, every)),
            low((narrow, wide // 2, patches, every)),
            low((narrow - 1, wide // 2, patches, every)),
            low((wide // 2, patches, every)),
            low((wide // 2 - 1, patches, every)),
            low((devices, own_rows, 2 * HEAD_M)),
            low((devices, own_rows, 2 * HEAD_M)),
            low(up_parts.shape),
            low(down_parts.shape),
            low(middle_parts.shape[1:]),
            low((2, wide // 4) + middle_parts.shape[2:]),
            low((6, wide // 4) + middle_parts.shape[2:]),
            low(back_shape),
            dma,
            dma,
            dma,
            dma,
            dma((narrow - 1,)),
            dma((narrow - 1,)),
            dma((wide // 2 - 1,)),
            dma((wide // 2 - 1,)),
            dma,
            dma,
            dma((wide,)),
            dma((wide,)),
            dma((2, 8)),
            dma((narrow - 1,)),
            dma((narrow - 1,)),
            dma,
            dma((7,)),
        ],
        compiler_params=pltpu.CompilerParams(
            collective_id=collective_id, has_side_effects=True, vmem_limit_bytes=36 << 20
        ),
        name="mixer_backward",
    )(
        *scalars,
        xz,
        bc,
        dt,
        marks,
        conv_weight,
        conv_bias,
        y,
        states,
        normed,
        w_xz,
        start,
        mixed_in,
        global_grad,
        gain,
        gated_scale,
        gain_grads,
        gated_gain_grads,
        du_blocks,
        up_parts,
        down_parts,
        middle_parts,
        gate_sum,
        mix_grad,
    )


def finish_kernel(
    pack_all,
    mix_all,
    u,
    keep,
    middle,
    xz_grads,
    bcdt_grads,
    gated_gain,
    embedded,
    start,
    table_out,
    patch_out,
    in_out,
    out_out,
    local_out,
    query_out,
    key_out,
    value_out,
    attn_out,
    embedded_own,
    ids_all,
    patch_all,
    rows_of_four,
    sems,
):
    me = lax.axis_index(NARROW) * lax.axis_size(WIDE) + lax.axis_index(WIDE)
    own_rows = patch_out.shape[0]
    group = 128 // own_rows
    columns = pl.ds(pl.multiple_of(lax.div(me, group) * 128, 128), 128)
    copies = [
        pltpu.make_async_copy(embedded.at[:, columns], embedded_own, sems.at[0]),
        pltpu.make_async_copy(start.at[:, pl.ds(3 * STATE, 128)], ids_all, sems.at[1]),
        pltpu.make_async_copy(start.at[:, pl.ds(4 * STATE, D)], patch_all, sems.at[2]),
    ]
    for copy in copies:
        copy.start()
    for i, out in enumerate((query_out, key_out, value_out, attn_out)):
        out[...] = middle[:, i * D : (i + 1) * D]
    local_out[...] = middle[:, 4 * D :].T
    for pair in range(0, HEADS_M, 2):
        both = [xz_grads[pair + i].astype(FULL) for i in range(2)]
        first = pair * HEAD_M
        in_out[:, first : first + 128] = jnp.concatenate([v[:, HEAD_M:] for v in both], axis=1)
        in_out[:, DI + first : DI + first + 128] = jnp.concatenate(
            [v[:, :HEAD_M] for v in both], axis=1
        )
    in_out[:, 2 * DI : 2 * DI + 2 * STATE] = bcdt_grads[:, : 2 * STATE]
    in_out[:, 2 * DI + 2 * STATE :] = bcdt_grads[:, 2 * STATE : 2 * STATE + HEADS_M]
    scale = pack_all[:, D:].astype(FULL)[:, :HEAD_M]
    gain = head_columns(gated_gain, me)[:, :HEAD_M]
    gated = (u[...] * scale * gain).astype(LOW)
    out_out[...] = tn(gated, mix_all[...])
    copies[0].wait()
    copies[1].wait()
    grads = pack_all[:, :D]
    rows_of_four[...] = tn(embedded_own[...], grads)
    patch_out[...] = rows_of_four[pl.ds(pl.multiple_of(lax.rem(me, group) * own_rows, own_rows), own_rows), :]
    own_words = table_out.shape[0]
    count = pack_all.shape[0]
    lane = lax.broadcasted_iota(jnp.int32, (count, PATCH * own_words), 1)
    ids = jnp.zeros((count, PATCH * own_words), FULL)
    kept = jnp.zeros((count, PATCH * own_words), FULL)
    values = ids_all[...].astype(FULL)
    for k in range(PATCH):
        here = lax.div(lane, own_words) == k
        ids = jnp.where(here, values[:, k : k + 1], ids)
        kept = jnp.where(here, keep[:, k : k + 1], kept)
    words = (me * own_words + lax.rem(lane, own_words)).astype(FULL)
    sums = tn(jnp.where(ids == words, kept, 0.0).astype(LOW), grads)
    high = sums.astype(LOW)
    rest = (sums - high.astype(FULL)).astype(LOW)
    copies[2].wait()
    table = jnp.zeros(table_out.shape, FULL)
    for k in range(PATCH):
        rows = slice(k * own_words, (k + 1) * own_words)
        weight = patch_all[k * EMB : (k + 1) * EMB, :]
        table += nt(high[rows], weight) + nt(rest[rows], weight)
    table_out[...] = table


def finish(pack_all, mix_all, u, keep, middle, xz_grads, bcdt_grads, gated_gain, embedded, start):
    count = pack_all.shape[0]
    devices, own_rows = xz_grads.shape[:2]
    anywhere = pl.BlockSpec(memory_space=pl.ANY)

    def full(*shape):
        return jax.ShapeDtypeStruct(shape, FULL)

    return pl.pallas_call(
        finish_kernel,
        out_shape=[
            full(VOCAB // devices, EMB),
            full(own_rows, D),
            full(own_rows, 2 * DI + 2 * STATE + HEADS_M),
            full(DI // devices, D),
            full(EMB, own_rows),
        ]
        + [full(own_rows, D)] * 4,
        in_specs=[in_vmem()] * 8 + [anywhere] * 2,
        out_specs=[in_vmem()] * 9,
        scratch_shapes=[
            pltpu.VMEM((count, 128), LOW),
            pltpu.VMEM((count, 128), LOW),
            pltpu.VMEM((D, D), LOW),
            pltpu.VMEM((128, D), FULL),
            pltpu.SemaphoreType.DMA((3,)),
        ],
        compiler_params=pltpu.CompilerParams(vmem_limit_bytes=20 << 20),
        name="finish",
    )(pack_all, mix_all, u, keep, middle, xz_grads, bcdt_grads, gated_gain, embedded, start)


def patch_causal():
    row = lax.broadcasted_iota(jnp.int32, (BYTE_BLOCK, BYTE_BLOCK), 0)
    column = lax.broadcasted_iota(jnp.int32, (BYTE_BLOCK, BYTE_BLOCK), 1)
    return (lax.div(row, PATCH) == lax.div(column, PATCH)) & (row >= column)


def head_probs(q, k, causal):
    scores = jnp.where(causal, nt(q, k) * HEAD_A ** (-0.5), masked_score)
    grown = jnp.exp(scores - jnp.max(scores, axis=1, keepdims=True))
    return grown / jnp.sum(grown, axis=1, keepdims=True)


def of_head(block, half):
    lane = lax.broadcasted_iota(jnp.int32, block.shape, 1)
    return jnp.where(lax.div(lane, HEAD_A) == half, block, jnp.zeros_like(block))


def fetched(pack, places, blocks, sems):
    copies = []
    for i, place in enumerate(places):
        width = place.shape[1]
        start = blocks[i]
        copies.append(
            pltpu.make_async_copy(pack.at[:, pl.ds(start, width)], place, sems.at[i])
        )
        copies[-1].start()
    return [copy.wait for copy in copies]


def split_gain(gain):
    half = HEAD_M // 2
    rows = []
    for i in range(2):
        groups = []
        for first in range(0, HEADS_M, 4):
            starts = [(first + j) * HEAD_M + i * half for j in range(4)]
            groups.append(jnp.concatenate([gain[:, a : a + half] for a in starts], axis=1))
        rows.append(jnp.concatenate(groups, axis=1))
    return rows


def unit_rows(values):
    scale = lax.rsqrt(jnp.mean(values * values, axis=1, keepdims=True) + epsilon)
    return values * scale, scale


def norm_back(grad, gain, unit, scale):
    scaled = grad * gain
    return scale * (scaled - unit * jnp.mean(scaled * unit, axis=1, keepdims=True))


WEIGHT_STEP = 256


def attend_pairs(qkv, mixed):
    causal = patch_causal()
    blocks = qkv.shape[0] // BYTE_BLOCK

    def pair(i, carry):
        def lanes(part):
            start = part * D + i * (2 * HEAD_A)
            return pl.ds(pl.multiple_of(start, 2 * HEAD_A), 2 * HEAD_A)

        for block in range(blocks):
            rows = pl.ds(block * BYTE_BLOCK, BYTE_BLOCK)
            q, k, v = qkv[rows, lanes(0)], qkv[rows, lanes(1)], qkv[rows, lanes(2)]
            total = jnp.zeros(q.shape, FULL)
            for half in range(2):
                probs = head_probs(of_head(q, half), k, causal)
                total += nn(probs.astype(LOW), of_head(v, half))
            mixed[rows, lanes(0)] = total.astype(LOW)
        return carry

    lax.fori_loop(0, HEADS_A // 2, pair, 0)


def attend_pairs_back(qkv, heads_grad, qkv_grad):
    causal = patch_causal()
    blocks = qkv.shape[0] // BYTE_BLOCK
    scale = HEAD_A ** (-0.5)

    def pair(i, carry):
        def lanes(part):
            start = part * D + i * (2 * HEAD_A)
            return pl.ds(pl.multiple_of(start, 2 * HEAD_A), 2 * HEAD_A)

        for block in range(blocks):
            rows = pl.ds(block * BYTE_BLOCK, BYTE_BLOCK)
            q, k, v = qkv[rows, lanes(0)], qkv[rows, lanes(1)], qkv[rows, lanes(2)]
            g = heads_grad[rows, lanes(0)]
            dq = jnp.zeros(q.shape, FULL)
            dk = jnp.zeros(q.shape, FULL)
            dv = jnp.zeros(q.shape, FULL)
            for half in range(2):
                own_q, own_k, own_g = of_head(q, half), of_head(k, half), of_head(g, half)
                probs = head_probs(own_q, k, causal)
                dprobs = nt(own_g, v)
                dv += tn(probs.astype(LOW), own_g)
                dscores = probs * (dprobs - jnp.sum(probs * dprobs, axis=1, keepdims=True))
                dscores = dscores.astype(LOW)
                dq += nn(dscores, own_k)
                dk += tn(dscores, own_q)
            qkv_grad[rows, lanes(0)] = (dq * scale).astype(LOW)
            qkv_grad[rows, lanes(1)] = (dk * scale).astype(LOW)
            qkv_grad[rows, lanes(2)] = dv.astype(LOW)
        return carry

    lax.fori_loop(0, HEADS_A // 2, pair, 0)


def bytes_forward_kernel(
    u_blocks,
    mixed_in,
    attn_gain,
    feed_gain,
    gated_gain,
    pack,
    gated_out,
    local_out,
    stream_out,
    normed_out,
    qkv,
    mixed,
    after_out,
    feed_out,
    w_out0,
    w_out1,
    w_local,
    w_q,
    w_k,
    w_v,
    w_attn,
    pieces,
    sems,
):
    places = (w_out0, w_out1, w_local, w_q, w_k, w_v, w_attn)
    blocks = [4 * D, 5 * D, 6 * D, 0, D, 2 * D, 3 * D]
    waits = fetched(pack, places, blocks, sems)
    patches = mixed_in.shape[0]
    half = HEAD_M // 2
    for i in range(2):
        for first in range(0, HEADS_M, 4):
            gated_out[i, :, first * half : (first + 4) * half] = jnp.concatenate(
                [
                    u_blocks[first + j].astype(FULL)[:, i * half : (i + 1) * half]
                    for j in range(4)
                ],
                axis=1,
            )
    held = [gated_out[0], gated_out[1]]
    square = sum(jnp.sum(v * v, axis=1, keepdims=True) for v in held)
    scale = lax.rsqrt(square / (2 * D) + epsilon)
    split = split_gain(gated_gain)
    gated = [(held[i] * scale * split[i]).astype(LOW) for i in range(2)]
    waits[0]()
    waits[1]()
    joined = mixed_in[...] + nn(gated[0], w_out0[...]) + nn(gated[1], w_out1[...])
    for k in range(PATCH):
        pieces[pl.ds(k, patches, stride=PATCH), :] = joined[:, k * EMB : (k + 1) * EMB]
    local = pieces[...].astype(LOW)
    local_out[...] = local
    waits[2]()
    stream = nt(local, w_local[...])
    stream_out[...] = stream
    normed = (unit_rows(stream)[0] * attn_gain[...]).astype(LOW)
    normed_out[...] = normed
    for i, weight in enumerate((w_q, w_k, w_v)):
        waits[3 + i]()
        for first in range(0, D, WEIGHT_STEP):
            qkv[:, i * D + first : i * D + first + WEIGHT_STEP] = nn(
                normed, weight[:, first : first + WEIGHT_STEP]
            ).astype(LOW)
    attend_pairs(qkv, mixed)
    waits[6]()
    heads = mixed[...]
    for first in range(0, D, WEIGHT_STEP):
        columns = slice(first, first + WEIGHT_STEP)
        after_out[:, columns] = stream_out[:, columns] + nn(heads, w_attn[:, columns])
    feed_out[...] = (unit_rows(after_out[...])[0] * feed_gain[...]).astype(LOW)


def bytes_forward(u_blocks, mixed_in, attn_gain, feed_gain, gated_gain, pack):
    patches = mixed_in.shape[0]
    rows = patches * PATCH

    def full(shape, kind):
        return jax.ShapeDtypeStruct(shape, kind)

    return pl.pallas_call(
        bytes_forward_kernel,
        out_shape=[
            full((2, patches, D), FULL),
            full((rows, EMB), LOW),
            full((rows, D), FULL),
            full((rows, D), LOW),
            full((rows, 3 * D), LOW),
            full((rows, D), LOW),
            full((rows, D), FULL),
            full((rows, D), LOW),
        ],
        in_specs=[in_vmem()] * 5 + [pl.BlockSpec(memory_space=pl.ANY)],
        out_specs=[in_vmem()] * 8,
        scratch_shapes=[pltpu.VMEM((D, D), LOW)] * 2
        + [pltpu.VMEM((D, EMB), LOW)]
        + [pltpu.VMEM((D, D), LOW)] * 4
        + [pltpu.VMEM((rows, EMB), FULL), pltpu.SemaphoreType.DMA((7,))],
        compiler_params=pltpu.CompilerParams(vmem_limit_bytes=48 << 20),
        name="bytes_forward",
    )(u_blocks, mixed_in, attn_gain, feed_gain, gated_gain, pack)


def bytes_backward_kernel(
    narrow,
    feed_in_grad,
    cotangent,
    keep,
    after,
    stream_in,
    normed_in,
    qkv,
    mixed,
    local_in,
    gated_rows,
    attn_gain,
    feed_gain,
    gated_gain,
    pack,
    feed_parts,
    gate_parts,
    global_out,
    mix_out,
    scale_out,
    sums,
    gain_grads,
    gated_gain_grads,
    du_blocks,
    rows_out,
    gate_out,
    w_attn,
    w_q,
    w_k,
    w_v,
    w_local,
    w_out0,
    w_out1,
    after_grad,
    heads_grad,
    qkv_grad,
    pieces,
    parts_got,
    grads,
    grads_got,
    gate_got,
    sems,
    p_send,
    p_recv,
    t_send,
    t_recv,
    gate_sems,
):
    n, wide_place = lax.axis_index(NARROW), lax.axis_index(WIDE)
    core = lax.rem(wide_place, 2)
    twin = (n, wide_place + 1 - 2 * core)
    depth = gate_parts.shape[0]
    z_place = lax.div(wide_place, 2)
    line = LineSum(
        gate_parts, gate_got, gate_sems, z_place, depth, lambda there: (n, there * 2 + core)
    )

    def twin_copy(i, columns):
        return remote(
            grads.at[:, 1 - core, :, columns],
            grads_got.at[:, :, columns],
            t_send.at[i],
            t_recv.at[i],
            twin,
        )

    def give(i, columns, part):
        grads[:, :, :, columns] = part.astype(LOW).reshape(grads.shape[:3] + part.shape[1:])
        twin_copy(i, columns).start()

    def part_copy(k):
        peer = (square_peer(n, k), wide_place)
        return remote(feed_parts.at[k], parts_got.at[k], p_send.at[k - 1], p_recv.at[k - 1], peer)

    own_part = pltpu.make_async_copy(feed_parts.at[0], parts_got.at[0], sems.at[7])
    own_part.start()
    places = (w_attn, w_q, w_k, w_v, w_local, w_out0, w_out1)
    blocks = [3 * D, 0, D, 2 * D, 6 * D, 4 * D, 5 * D]
    waits = fetched(pack, places, blocks, sems)
    greet_lines(narrow, depth)
    line.start()
    for k in range(1, narrow):
        part_copy(k).start()
    patches = global_out.shape[0]
    unit, scale = unit_rows(after[...])
    grad = feed_in_grad[...].astype(LOW).astype(FULL)
    gain_grads[1:2, :] = jnp.sum(grad * unit, axis=0, keepdims=True)
    after_grad[...] = cotangent[...].astype(FULL) * keep[0] + norm_back(
        grad, feed_gain[...], unit, scale
    )
    attn_grad = after_grad[...].astype(LOW)
    waits[0]()
    for first in range(0, D, WEIGHT_STEP):
        columns = slice(first, first + WEIGHT_STEP)
        heads_grad[:, columns] = nt(attn_grad, w_attn[columns, :]).astype(LOW)
        give(
            (3 * D + first) // WEIGHT_STEP,
            pl.ds(3 * D + first, WEIGHT_STEP),
            tn(mixed[...], attn_grad[:, columns]),
        )
    attend_pairs_back(qkv, heads_grad, qkv_grad)
    normed_grad = jnp.zeros(after_grad.shape, FULL)
    for i, weight in enumerate((w_q, w_k, w_v)):
        waits[1 + i]()
        normed_grad += nt(qkv_grad[:, i * D : (i + 1) * D], weight[...])
    unit, scale = unit_rows(stream_in[...])
    gain_grads[0:1, :] = jnp.sum(normed_grad * unit, axis=0, keepdims=True)
    stream_grad = (after_grad[...] + norm_back(normed_grad, attn_gain[...], unit, scale)).astype(LOW)
    waits[4]()
    pieces[...] = nn(stream_grad, w_local[...])
    for k in range(PATCH):
        global_out[:, k * EMB : (k + 1) * EMB] = pieces[pl.ds(k, patches, stride=PATCH), :]
    mix_grad = global_out[...].astype(LOW)
    mix_out[...] = mix_grad
    waits[5]()
    waits[6]()
    inner = [nt(mix_grad, w_out0[...]), nt(mix_grad, w_out1[...])]
    held = [gated_rows[0], gated_rows[1]]
    square = sum(jnp.sum(v * v, axis=1, keepdims=True) for v in held)
    scale = lax.rsqrt(square / (2 * D) + epsilon)
    units = [v * scale for v in held]
    split = split_gain(gated_gain)
    scaled = [inner[i] * split[i] for i in range(2)]
    mean = sum(jnp.sum(scaled[i] * units[i], axis=1, keepdims=True) for i in range(2)) / (2 * D)
    for i in range(2):
        gated_gain_grads[i : i + 1, :] = jnp.sum(inner[i] * units[i], axis=0, keepdims=True)
    scale_out[...] = jnp.broadcast_to(scale, scale_out.shape)
    rows_grads = [scale * (scaled[i] - units[i] * mean) for i in range(2)]
    half = HEAD_M // 2
    for head in range(HEADS_M):
        lanes = slice(head * half, (head + 1) * half)
        du_blocks[head] = jnp.concatenate([part[:, lanes] for part in rows_grads], axis=1).astype(LOW)
    give(4 * D // WEIGHT_STEP, pl.ds(4 * D, EMB), tn(stream_grad, local_in[...]))

    def weight_grads(i, carry):
        columns = pl.ds(pl.multiple_of(i * WEIGHT_STEP, WEIGHT_STEP), WEIGHT_STEP)
        give(i, columns, tn(normed_in[...], qkv_grad[:, columns]))
        return carry

    lax.fori_loop(0, 3 * D // WEIGHT_STEP, weight_grads, 0)
    own_part.wait()
    for k in range(1, narrow):
        part_copy(k).wait_recv()
    for first in range(0, D, WEIGHT_STEP):
        columns = slice(first, first + WEIGHT_STEP)
        feed = parts_got[0, :, columns].astype(FULL)
        for k in range(1, narrow):
            feed += parts_got[k, :, columns].astype(FULL)
        feed = feed.astype(LOW).astype(FULL)
        rows_out[:, columns] = ((after[:, columns] + feed) * keep[0]).astype(LOW)

    def add_twin(i, columns):
        twin_copy(i, columns).wait_recv()
        sums[:, :, columns] = (
            grads[:, core, :, columns].astype(FULL) + grads_got[:, :, columns].astype(FULL)
        ).astype(LOW)

    def add_one(i, carry):
        add_twin(i, pl.ds(pl.multiple_of(i * WEIGHT_STEP, WEIGHT_STEP), WEIGHT_STEP))
        return carry

    def end_one(i, carry):
        twin_copy(i, pl.ds(pl.multiple_of(i * WEIGHT_STEP, WEIGHT_STEP), WEIGHT_STEP)).wait_send()
        return carry

    steps = 4 * D // WEIGHT_STEP
    add_twin(steps, pl.ds(4 * D, EMB))
    lax.fori_loop(0, steps, add_one, 0)
    line.arrive()
    gate_out[...] = line.total().astype(LOW)
    line.finish()
    twin_copy(steps, pl.ds(4 * D, EMB)).wait_send()
    lax.fori_loop(0, steps, end_one, 0)
    for k in range(1, narrow):
        part_copy(k).wait_send()


def bytes_backward(
    feed_in_grad,
    cotangent,
    keep,
    after,
    stream,
    normed,
    qkv,
    mixed,
    local,
    gated_rows,
    attn_gain,
    feed_gain,
    gated_gain,
    pack,
    feed_parts,
    gate_parts,
    collective_id,
):
    narrow = feed_parts.shape[0]
    every = 4 * D + EMB
    rows = after.shape[0]
    patches = rows // PATCH

    def full(shape, kind):
        return jax.ShapeDtypeStruct(shape, kind)

    return pl.pallas_call(
        partial(bytes_backward_kernel, narrow),
        out_shape=[
            full((patches, D), FULL),
            full((patches, D), LOW),
            full((patches, 128), FULL),
            full((HEADS_M // 2, D // HEADS_M, every), LOW),
            full((2, D), FULL),
            full((2, D), FULL),
            full((HEADS_M, patches, HEAD_M), LOW),
            full((rows, D), LOW),
            full(gate_parts.shape[1:], LOW),
        ],
        in_specs=[in_vmem()] * 13 + [pl.BlockSpec(memory_space=pl.ANY)] * 3,
        out_specs=[in_vmem()] * 9,
        scratch_shapes=[pltpu.VMEM((D, D), LOW)] * 4
        + [pltpu.VMEM((D, EMB), LOW)]
        + [pltpu.VMEM((D, D), LOW)] * 2
        + [
            pltpu.VMEM((rows, D), FULL),
            pltpu.VMEM((rows, D), LOW),
            pltpu.VMEM((rows, 3 * D), LOW),
            pltpu.VMEM((rows, EMB), FULL),
            pltpu.VMEM((narrow, rows, D), LOW),
            pltpu.VMEM((HEADS_M // 2, 2, D // HEADS_M, every), LOW),
            pltpu.VMEM((HEADS_M // 2, D // HEADS_M, every), LOW),
            pltpu.VMEM(gate_parts.shape, LOW),
            pltpu.SemaphoreType.DMA((8,)),
            pltpu.SemaphoreType.DMA((narrow - 1,)),
            pltpu.SemaphoreType.DMA((narrow - 1,)),
            pltpu.SemaphoreType.DMA((4 * D // WEIGHT_STEP + 1,)),
            pltpu.SemaphoreType.DMA((4 * D // WEIGHT_STEP + 1,)),
            pltpu.SemaphoreType.DMA((2 * gate_parts.shape[0],)),
        ],
        compiler_params=pltpu.CompilerParams(
            collective_id=collective_id, has_side_effects=True, vmem_limit_bytes=44 << 20
        ),
        name="bytes_backward",
    )(
        feed_in_grad,
        cotangent,
        keep,
        after,
        stream,
        normed,
        qkv,
        mixed,
        local,
        gated_rows,
        attn_gain,
        feed_gain,
        gated_gain,
        pack,
        feed_parts,
        gate_parts,
    )


def feed_kernel(narrow, x_in, g_own, g_others, keep, *refs):
    gate_in, up_in, down_in, f_out, gx_out, gate_sum, up_sum, down_sum = refs[:8]
    wg, wu, wd, x, xt, g, hid, gg, gu, sent, got = refs[8:19]
    gate_twin, up_twin, down_twin, gate_got, up_got, down_got = refs[19:25]
    w_sem, g_sem, x_sem, x_send, x_recv, r_send, r_recv, t_send, t_recv = refs[25:]
    n, wide_place = lax.axis_index(NARROW), lax.axis_index(WIDE)
    core = lax.rem(wide_place, 2)
    twin = (n, wide_place + 1 - 2 * core)
    barrier = pltpu.get_barrier_semaphore()
    pl.semaphore_signal(barrier, inc=1, device_id=twin, device_id_type=MESH)
    for k in range(1, narrow):
        peer = (lax.rem(n + k, narrow), wide_place)
        pl.semaphore_signal(barrier, inc=1, device_id=peer, device_id_type=MESH)
    places, width, share = gate_in.shape
    rows = x_in.shape[0]
    hidden = places * share
    depth = places // 2
    chunk = 2 * share
    own_x = pltpu.make_async_copy(x_in, x.at[0], x_sem)
    own_x.start()
    g_copies = [
        pltpu.make_async_copy(g_own, g.at[0], g_sem.at[0]),
        pltpu.make_async_copy(
            g_others.at[pl.ds(1, narrow - 1)], g.at[pl.ds(1, narrow - 1)], g_sem.at[1]
        ),
    ]
    w_copies = [pltpu.make_async_copy(down_in, wd, w_sem.at[2 * places])]
    for place in range(places):
        units = slice(place * share, (place + 1) * share)
        w_copies.append(pltpu.make_async_copy(gate_in.at[place], wg.at[:, units], w_sem.at[place]))
        w_copies.append(
            pltpu.make_async_copy(up_in.at[place], wu.at[:, units], w_sem.at[places + place])
        )
    g_copies[0].start()
    for copy in w_copies:
        copy.start()
    for copy in g_copies[1:]:
        copy.start()
    pl.semaphore_wait(barrier, narrow)

    share_x = SquareShare(x_in, x, x_send, x_recv, n, wide_place)

    def r_copy(k):
        peer = (square_peer(n, k), wide_place)
        return remote(sent.at[k - 1], got.at[k - 1], r_send.at[k - 1], r_recv.at[k - 1], peer)

    share_x.start()
    own_x.wait()
    for copy in w_copies:
        copy.wait()
    for copy in g_copies:
        copy.wait()

    def block(k, carry):
        @pl.when(k == 1)
        def _():
            share_x.relay(0)
            share_x.relay(1)

        @pl.when(k == narrow - 1)
        def _():
            share_x.arrive()

        xk = x[k]
        gk = (g[k].astype(FULL) * keep[k]).astype(LOW)
        g[k] = gk
        xt[:, pl.ds(pl.multiple_of(k * rows, rows), rows)] = xk.T
        for first in range(0, hidden, chunk):
            units = slice(first, first + chunk)
            gate = nn(xk, wg[:, units])
            up = nn(xk, wu[:, units])
            dhid = nt(gk, wd[units, :])
            s = jax.nn.sigmoid(gate)
            act = gate * s
            hid[k, :, units] = (act * up).astype(LOW)
            gg[k, :, units] = (dhid * up * s * (1.0 + gate * (1.0 - s))).astype(LOW)
            gu[k, :, units] = (dhid * act).astype(LOW)
        ggk, guk, hidk = gg[k], gu[k], hid[k]
        for first in range(0, width, chunk):
            columns = slice(first, first + chunk)
            gx = nt(ggk, wg[columns, :]) + nt(guk, wu[columns, :])

            @pl.when(k == 0)
            def _():
                gx_out[:, columns] = gx

            @pl.when(k > 0)
            def _():
                sent[k - 1, :, columns] = gx.astype(LOW)

        @pl.when(k > 0)
        def _():
            r_copy(k).start()

        for first in range(0, width, chunk):
            columns = slice(first, first + chunk)
            f_out[k, :, columns] = nn(hidk, wd[:, columns]).astype(LOW)
        return carry

    lax.fori_loop(0, narrow, block, 0)

    def units_of(j, of_core):
        start = (2 * j + of_core) * share
        return pl.ds(pl.multiple_of(start, share), share)

    def two_places(left, j, of_core):
        pair = [left[:, :, units_of(2 * j + i, of_core)] for i in range(2)]
        return jnp.concatenate(pair, axis=2).reshape(narrow * rows, chunk)

    def columns_grads(left, j, of_core):
        total = nn(xt[...], two_places(left, j, of_core))
        return total[:, :share], total[:, share:]

    def rows_grads(j, of_core):
        total = tn(two_places(hid, j, of_core), g[...].reshape(narrow * rows, width))
        return total[:share], total[share:]

    outs = (gate_twin, up_twin, down_twin)
    ins = (gate_got, up_got, down_got)

    def t_copy(i, j):
        return remote(outs[i].at[j], ins[i].at[j], t_send.at[i, j], t_recv.at[i, j], twin)

    def for_twin(j, carry):
        for i, left in enumerate((gg, gu)):
            for half, part in enumerate(columns_grads(left, j, 1 - core)):
                outs[i][2 * j + half] = part.astype(LOW)
                t_copy(i, 2 * j + half).start()
        for half, part in enumerate(rows_grads(j, 1 - core)):
            outs[2][2 * j + half] = part.astype(LOW)
            t_copy(2, 2 * j + half).start()
        return carry

    def for_own(j, carry):
        for i, (left, total) in enumerate(((gg, gate_sum), (gu, up_sum))):
            for half, part in enumerate(columns_grads(left, j, core)):
                t_copy(i, 2 * j + half).wait_recv()
                total[2 * j + half] = (part + ins[i][2 * j + half].astype(FULL)).astype(LOW)
        for half, part in enumerate(rows_grads(j, core)):
            t_copy(2, 2 * j + half).wait_recv()
            down_sum[2 * j + half] = (part + ins[2][2 * j + half].astype(FULL)).astype(LOW)
        return carry

    lax.fori_loop(0, depth // 2, for_twin, 0)
    lax.fori_loop(0, depth // 2, for_own, 0)
    for k in range(1, narrow):
        r_copy(k).wait_recv()
        gx_out[...] += got[k - 1].astype(FULL)
    share_x.finish()
    for k in range(1, narrow):
        r_copy(k).wait_send()
    for i in range(3):
        for j in range(depth):
            t_copy(i, j).wait_send()


def feed_forward_back(x_own, g_own, g_others, keep, gate_all, up_all, down_all, collective_id):
    narrow = keep.shape[0]
    rows, width = x_own.shape
    places, _, share = gate_all.shape
    hidden, depth = places * share, places // 2
    dma = pltpu.SemaphoreType.DMA
    anywhere = pl.BlockSpec(memory_space=pl.ANY)

    def low(*shape):
        return pltpu.VMEM(shape, LOW)

    sums = [(depth, width, share), (depth, width, share), (depth, share, width)]
    return pl.pallas_call(
        partial(feed_kernel, narrow),
        out_shape=[
            jax.ShapeDtypeStruct((narrow, rows, width), LOW),
            jax.ShapeDtypeStruct((rows, width), FULL),
        ]
        + [jax.ShapeDtypeStruct(shape, LOW) for shape in sums],
        in_specs=[anywhere] * 3 + [in_vmem()] + [anywhere] * 3,
        out_specs=[in_vmem()] * 5,
        scratch_shapes=[
            low(width, hidden),
            low(width, hidden),
            low(hidden, width),
            low(narrow, rows, width),
            low(width, narrow * rows),
            low(narrow, rows, width),
            low(narrow, rows, hidden),
            low(narrow, rows, hidden),
            low(narrow, rows, hidden),
            low(narrow - 1, rows, width),
            low(narrow - 1, rows, width),
        ]
        + [low(*shape) for shape in sums + sums]
        + [
            dma((2 * places + 1,)),
            dma((2,)),
            dma,
            dma((narrow,)),
            dma((narrow,)),
            dma((narrow - 1,)),
            dma((narrow - 1,)),
            dma((3, depth)),
            dma((3, depth)),
        ],
        compiler_params=pltpu.CompilerParams(
            collective_id=collective_id, has_side_effects=True, vmem_limit_bytes=36 << 20
        ),
        name="feed",
    )(x_own, g_own, g_others, keep, gate_all, up_all, down_all)


def per_device_heads(
    byte_ids,
    doc_patches,
    pad_bytes,
    byte_table,
    patch_weight,
    gain_mix,
    in_weight,
    conv_weight,
    conv_bias,
    step_bias,
    log_rate,
    skip_gain,
    gated_gain,
    out_weight,
    local_weight,
    gain_attn,
    query_weight,
    key_weight,
    value_weight,
    attn_weight,
    feed_gain,
    gate_weight,
    up_weight,
    down_weight,
    cotangent,
):
    narrow, wide = lax.axis_size(NARROW), lax.axis_size(WIDE)
    devices = narrow * wide
    device = lax.axis_index(BOTH)
    rows = byte_ids.shape[0]
    patches = rows // PATCH
    everything = devices * patches
    own_rows = patch_weight.shape[0]
    hidden_width = gate_weight.shape[1]
    share = hidden_width // narrow

    ids_low = byte_ids.astype(LOW).reshape(patches, PATCH)
    bcdt_width = 2 * STATE + HEADS_M
    start_pack = jnp.concatenate(
        [
            jnp.pad(in_weight[:, 2 * DI :], ((0, 0), (0, 96))),
            jnp.pad(ids_low, ((0, 0), (0, 120))),
            patch_weight,
        ],
        axis=1,
    )
    xz_blocks = jnp.concatenate(
        [
            in_weight[:, DI : 2 * DI].reshape(own_rows, HEADS_M, HEAD_M),
            in_weight[:, :DI].reshape(own_rows, HEADS_M, HEAD_M),
        ],
        axis=2,
    ).transpose(1, 0, 2)
    middle_pack = jnp.concatenate(
        [
            query_weight,
            key_weight,
            value_weight,
            attn_weight,
            out_weight[:own_rows],
            out_weight[own_rows:],
            local_weight.T,
        ],
        axis=1,
    )
    numbers = (step_bias, log_rate, skip_gain)
    conv = (conv_weight, conv_bias[None])
    front, start_all, xz_weight, gate_all, up_all, down_all, middle_all, others = mixer_front(
        (doc_patches, pad_bytes) + numbers,
        gain_mix[None],
        *conv,
        (
            start_pack,
            byte_table.astype(FULL),
            xz_blocks,
            gate_weight,
            up_weight,
            down_weight,
            middle_pack,
            cotangent,
        ),
        5,
    )
    embedded, normed_all, xz, bc, dt, u, y, states, mixed_in, u_blocks, marks, keep_rows, keep_all = front
    half = HEAD_M // 2

    byte_gains = (gain_attn[None], feed_gain[None], gated_gain[None])
    (
        gated_rows,
        local_rows,
        stream,
        normed_attn,
        qkv,
        mixed_heads,
        after_attn,
        normed_feed,
    ) = bytes_forward(u_blocks, mixed_in, *byte_gains, middle_all)
    feed_parts, feed_in_grad, gate_parts, up_parts, down_parts = feed_forward_back(
        normed_feed, cotangent, others, keep_rows, gate_all, up_all, down_all, 2
    )

    (
        global_grad,
        mix_grad,
        gated_scale,
        middle_parts,
        byte_gain_grads,
        gated_gain_grads,
        du_blocks,
        out_rows,
        gate_sum,
    ) = bytes_backward(
        feed_in_grad,
        cotangent,
        keep_rows,
        after_attn,
        stream,
        normed_attn,
        qkv,
        mixed_heads,
        local_rows,
        gated_rows,
        *byte_gains,
        middle_all,
        feed_parts,
        gate_parts,
        4,
    )
    middle_parts = middle_parts.reshape(narrow, wide // 2, own_rows, -1)

    (
        end_pack,
        sums_pack,
        bcdt_grads,
        xz_grads,
        up_sum,
        down_sum,
        middle_sums,
        grad_gate,
        mix_grad_all,
    ) = mixer_backward(
        numbers,
        xz,
        bc,
        dt,
        marks,
        *conv,
        y,
        states,
        normed_all,
        xz_weight,
        start_all,
        mixed_in,
        global_grad,
        gain_mix[None],
        gated_scale,
        byte_gain_grads,
        gated_gain_grads,
        du_blocks,
        up_parts,
        down_parts,
        middle_parts,
        gate_sum,
        mix_grad,
        3,
    )
    mix_grad_all = mix_grad_all.reshape(everything, D)

    end_all, sums_all, middle_sums, grad_up, grad_down = end_gather(
        end_pack, sums_pack, middle_sums, up_sum, down_sum, 1
    )
    (
        grad_table,
        grad_patch,
        grad_in,
        grad_out,
        grad_local,
        grad_query,
        grad_key,
        grad_value,
        grad_attn,
    ) = finish(
        end_all,
        mix_grad_all,
        u,
        keep_all,
        middle_sums,
        xz_grads,
        bcdt_grads,
        gated_gain[None],
        embedded,
        start_all,
    )
    small = jnp.sum(sums_all[:, :SUM_ROWS], axis=0).reshape(-1)
    gain_grads = jnp.split(small[: 3 * D + DI], [D, D + DI, 2 * D + DI])
    gain_grads[1] = gain_grads[1].reshape(2, devices, half).transpose(1, 0, 2).reshape(DI)
    conv_own = sums_all[:, SUM_ROWS : SUM_ROWS + CONV + 1, :HEAD_M].transpose(1, 0, 2)
    conv_grads = jnp.concatenate(
        [conv_own.reshape(CONV + 1, DI), small[3 * D + DI :].reshape(CONV + 1, 2 * STATE)], axis=1
    )
    number_grads = sums_all[:, SUM_ROWS + CONV + 1, :3].T
    return (
        out_rows,
        grad_table,
        grad_patch,
        gain_grads[0],
        grad_in,
        conv_grads[:CONV],
        conv_grads[CONV],
        number_grads[0],
        number_grads[1],
        number_grads[2],
        gain_grads[1],
        grad_out,
        grad_local,
        gain_grads[2],
        grad_query,
        grad_key,
        grad_value,
        grad_attn,
        gain_grads[3],
        grad_gate,
        grad_up,
        grad_down,
    )


def solution(mesh):
    placed = (
        P((NARROW, WIDE)),
        P(),
        P(),
        P((NARROW, WIDE), None),
        P((NARROW, WIDE), None),
        P(),
        P((NARROW, WIDE), None),
        P(),
        P(),
        P(),
        P(),
        P(),
        P(),
        P((NARROW, WIDE), None),
        P(None, (NARROW, WIDE)),
        P(),
        P((NARROW, WIDE), None),
        P((NARROW, WIDE), None),
        P((NARROW, WIDE), None),
        P((NARROW, WIDE), None),
        P(),
        P(NARROW, WIDE),
        P(NARROW, WIDE),
        P(WIDE, NARROW),
        P((NARROW, WIDE), None),
    )
    return jax.shard_map(
        per_device_heads if mesh.size == HEADS_M else per_device_rows,
        mesh=mesh,
        in_specs=placed,
        out_specs=(
            P((NARROW, WIDE), None),
            P((NARROW, WIDE), None),
            P((NARROW, WIDE), None),
            P(),
            P((NARROW, WIDE), None),
            P(),
            P(),
            P(),
            P(),
            P(),
            P(),
            P((NARROW, WIDE), None),
            P(None, (NARROW, WIDE)),
            P(),
            P((NARROW, WIDE), None),
            P((NARROW, WIDE), None),
            P((NARROW, WIDE), None),
            P((NARROW, WIDE), None),
            P(),
            P(NARROW, WIDE),
            P(NARROW, WIDE),
            P(WIDE, NARROW),
        ),
        check_vma=False,
    )
```

```python
from functools import partial

import jax
import jax.numpy as jnp
from jax import lax
from jax.experimental import pallas as pl
from jax.experimental.pallas import tpu as pltpu
from jax.sharding import PartitionSpec as P

NARROW = "narrow"
WIDE = "wide"
D = 1024
PATCH = 8
EMB = 128
VOCAB = 256
HEADS_M = 32
HEAD_M = 64
DI = 2048
STATE = 128
CONV = 4
HEADS_A = 16
HEAD_A = 64


epsilon = 1e-05
highest = lax.Precision.HIGHEST
masked_score = -1e30


def running_sum(x):
    place = jnp.arange(x.shape[0])
    seen = place[:, None] >= place[None, :]
    if x.ndim == 1:
        return jnp.sum(jnp.where(seen, x[None, :], 0), axis=1).astype(x.dtype)
    return jnp.dot(seen.astype(x.dtype), x, precision=highest)


def passed_along(x, axis, by):
    peers = lax.axis_size(axis)
    pairs = [(i, i + by) for i in range(peers) if 0 <= i + by < peers]
    return lax.ppermute(x, axis, pairs)


def prefix_2(x, axis, join, neutral):
    place = lax.axis_index(axis)
    gathered = jax.tree.map(
        lambda a, kind: lax.all_gather(a.astype(kind), axis), x, (jnp.bfloat16, jnp.bfloat16)
    )
    state = jax.tree.map(lambda a, e: jnp.zeros_like(a) + jnp.asarray(e, a.dtype), x, neutral)

    def prefix_one(hop, state):
        return join(
            state,
            jax.tree.map(
                lambda a, own: lax.dynamic_index_in_dim(a, hop, 0, False).astype(own.dtype),
                gathered,
                x,
            ),
        )

    return lax.fori_loop(0, place, prefix_one, state)


def carried_in_2(x, axis, join, neutral):
    count = lax.axis_size(axis)
    place = lax.axis_index(axis)
    ahead = count - 1 - place
    gathered = jax.tree.map(
        lambda a, kind: lax.all_gather(a.astype(kind), axis),
        x,
        jax.tree.map(lambda a: jnp.bfloat16 if a.dtype == jnp.float32 else a.dtype, x),
    )
    state = jax.tree.map(lambda a, e: jnp.zeros_like(a) + jnp.asarray(e, a.dtype), x, neutral)

    def carried_one(hop, state):
        source = count - 1 - hop
        return join(
            state,
            jax.tree.map(
                lambda a, own: lax.dynamic_index_in_dim(a, source, 0, False).astype(own.dtype),
                gathered,
                x,
            ),
        )

    return lax.fori_loop(0, ahead, carried_one, state)


def root_norm(values, gain):
    return values * lax.rsqrt(jnp.mean(values * values, axis=-1, keepdims=True) + epsilon) * gain


def patch_layout(doc_patches, pad_bytes, first_index, patch_count):
    patch_index = first_index + jnp.arange(patch_count, dtype=jnp.int32)
    doc_ends = running_sum(doc_patches)
    doc_index = jnp.arange(doc_patches.shape[0], dtype=jnp.int32)
    segment = jnp.sum((patch_index[:, None] >= doc_ends[None, :]).astype(jnp.int32), axis=1)
    owner_mask = segment[:, None] == doc_index[None, :]
    last_end = jnp.sum(jnp.where(owner_mask, doc_ends[None, :] - 1, 0), axis=1)
    doc_starts = jnp.sum(jnp.where(owner_mask, (doc_ends - doc_patches)[None, :], 0), axis=1)
    pad_count = jnp.sum(jnp.where(owner_mask, pad_bytes[None, :], 0), axis=1)
    offset = jnp.arange(PATCH, dtype=jnp.int32)
    padded = (patch_index == last_end)[:, None] & (offset[None, :] >= PATCH - pad_count[:, None])
    keep_mask = 1.0 - padded.astype(jnp.float32).reshape(-1)
    return (segment, (patch_index == doc_starts).astype(jnp.int32), keep_mask)


def ssd_terms(layout, projected, rim_rows, small_params):
    conv_weight, conv_bias, step_bias, log_rate, skip_gain = small_params
    segment, rim_segment, first_patch = layout
    conv_in = projected[:, DI : 2 * DI + 2 * STATE]
    patch_count = conv_in.shape[0]
    padded = jnp.concatenate([rim_rows, conv_in], 0)
    padded_seg = jnp.concatenate([rim_segment, segment], 0)
    conv_sum = conv_bias
    for conv_tap in range(CONV):
        same_doc = (padded_seg[conv_tap : conv_tap + patch_count] == segment).astype(jnp.float32)[
            :, None
        ]
        conv_sum = (
            conv_sum + conv_weight[conv_tap] * padded[conv_tap : conv_tap + patch_count] * same_doc
        )
    activated = jax.nn.silu(conv_sum)
    values = activated[:, :DI].reshape(patch_count, HEADS_M, HEAD_M)
    input_map = activated[:, DI : DI + STATE]
    output_map = activated[:, DI + STATE :]
    time_steps = jax.nn.softplus(projected[:, 2 * DI + 2 * STATE :] + step_bias)
    cumulative = running_sum(-time_steps * jnp.exp(log_rate))
    no_reset = (running_sum(first_patch) == 0).astype(jnp.float32)
    return (values, input_map, output_map, time_steps, cumulative, no_reset)


def local_state(layout, projected, rim_rows, small_params):
    values, input_map, output_map, time_steps, cumulative, no_reset = ssd_terms(
        layout, projected, rim_rows, small_params
    )
    segment = layout[0]
    decay_tail = (
        jnp.exp(cumulative[-1][None, :] - cumulative)
        * (segment == segment[-1]).astype(jnp.float32)[:, None]
        * time_steps
    )
    state_local = jnp.einsum("sh,shp,sn->hpn", decay_tail, values, input_map, precision=highest)
    decay_total = jnp.exp(cumulative[-1]) * no_reset[-1]
    return (decay_total, state_local)


def mixer_output(layout, projected, rim_rows, small_params, incoming, gated_gain):
    values, input_map, output_map, time_steps, cumulative, no_reset = ssd_terms(
        layout, projected, rim_rows, small_params
    )
    segment = layout[0]
    patch_count = values.shape[0]
    position = jnp.arange(patch_count)
    visible = (segment[:, None] == segment[None, :]) & (position[:, None] >= position[None, :])
    log_gap = jnp.where(visible[:, :, None], cumulative[:, None, :] - cumulative[None, :, :], 0.0)
    inner = jnp.dot(output_map, input_map.T, precision=highest)
    weight = (
        jnp.exp(log_gap)
        * visible[:, :, None].astype(jnp.float32)
        * time_steps[None, :, :]
        * inner[:, :, None]
    )
    within = jnp.einsum("tsh,shp->thp", weight, values, precision=highest)
    carried_in = (
        jnp.einsum("tn,hpn->thp", output_map, incoming, precision=highest)
        * (jnp.exp(cumulative) * no_reset[:, None])[:, :, None]
    )
    result = (within + carried_in + small_params[4][None, :, None] * values).reshape(
        patch_count, DI
    )
    gated_rows = result * jax.nn.silu(projected[:, :DI])
    return root_norm(gated_rows, gated_gain)


def combine_states(earlier, following):
    return (earlier[0] * following[0], following[0][:, None, None] * earlier[1] + following[1])


def attend(stream, gain_attn, query_all, key_all, value_all):
    head_shape = (-1, PATCH, HEADS_A, HEAD_A)
    normed_attn = root_norm(stream, gain_attn).astype(jnp.bfloat16)
    queries = jnp.dot(normed_attn, query_all, preferred_element_type=jnp.float32).astype(
        jnp.bfloat16
    )
    key_rows = jnp.dot(normed_attn, key_all, preferred_element_type=jnp.float32).astype(
        jnp.bfloat16
    )
    value_rows = jnp.dot(normed_attn, value_all, preferred_element_type=jnp.float32).astype(
        jnp.bfloat16
    )
    scores = jnp.einsum(
        "pqhe,pkhe->phqk",
        queries.reshape(head_shape),
        key_rows.reshape(head_shape),
        preferred_element_type=jnp.float32,
    ) * HEAD_A ** (-0.5)
    position = jnp.arange(PATCH)
    causal = position[:, None] >= position[None, :]
    attn_probs = jax.nn.softmax(jnp.where(causal, scores, masked_score), axis=-1)
    mixed_heads = jnp.einsum(
        "phqk,pkhe->pqhe",
        attn_probs.astype(jnp.bfloat16),
        value_rows.reshape(head_shape),
        preferred_element_type=jnp.float32,
    )
    mixed_heads = mixed_heads.reshape(stream.shape[0], -1).astype(jnp.bfloat16)
    return (normed_attn, queries, key_rows, value_rows, attn_probs, mixed_heads)


def spread(values):
    by_rows = lax.all_to_all(values, NARROW, split_axis=1, concat_axis=0, tiled=True)
    return lax.all_gather(by_rows, WIDE, axis=0, tiled=True)


def collect(term_fn, row_count):
    summed = lax.psum_scatter(
        term_fn(jnp.int32(0), row_count * lax.axis_size(WIDE)).astype(jnp.bfloat16),
        WIDE,
        scatter_dimension=0,
        tiled=True,
    )
    return lax.all_to_all(summed, NARROW, split_axis=0, concat_axis=1, tiled=True)


def narrow_total(partial_rows):
    return lax.psum(partial_rows, NARROW).astype(jnp.float32)


def silu_back(gate_up, hidden_grad, hidden_width):
    gate_rows = gate_up[:, :hidden_width]
    up_rows = gate_up[:, hidden_width:]
    sigmoid = jax.nn.sigmoid(gate_rows)
    gate_grad = hidden_grad * up_rows * sigmoid * (1.0 + gate_rows * (1.0 - sigmoid))
    up_grad = hidden_grad * gate_rows * sigmoid
    return jnp.concatenate([gate_grad, up_grad], axis=1)


def per_device_rows(
    byte_ids,
    doc_patches,
    pad_bytes,
    byte_table,
    patch_weight,
    gain_mix,
    in_weight,
    conv_weight,
    conv_bias,
    step_bias,
    log_rate,
    skip_gain,
    gated_gain,
    out_weight,
    local_weight,
    gain_attn,
    query_weight,
    key_weight,
    value_weight,
    attn_weight,
    feed_gain,
    gate_weight,
    up_weight,
    down_weight,
    cotangent,
):
    byte_rows = byte_ids.shape[0]
    patches = byte_rows // PATCH
    device = lax.axis_index((NARROW, WIDE))
    wide_count = lax.axis_size(WIDE)
    segment, first_patch, keep_mask = patch_layout(
        doc_patches, pad_bytes, device * patches, patches
    )
    rim_segment = patch_layout(doc_patches, pad_bytes, device * patches - (CONV - 1), CONV - 1)[0]
    layout = (segment, rim_segment, first_patch)
    gathered = (
        lax.all_gather(byte_table, (NARROW, WIDE), axis=0, tiled=True),
        lax.all_gather(patch_weight, (NARROW, WIDE), axis=0, tiled=True),
        lax.all_gather(in_weight, (NARROW, WIDE), axis=0, tiled=True),
        lax.all_gather(out_weight, (NARROW, WIDE), axis=0, tiled=True),
        lax.all_gather(local_weight, (NARROW, WIDE), axis=1, tiled=True),
        lax.all_gather(query_weight, (NARROW, WIDE), axis=0, tiled=True),
        lax.all_gather(key_weight, (NARROW, WIDE), axis=0, tiled=True),
        lax.all_gather(value_weight, (NARROW, WIDE), axis=0, tiled=True),
        lax.all_gather(attn_weight, (NARROW, WIDE), axis=0, tiled=True),
    )
    table_all, patch_all, in_all, out_all, local_all, query_all, key_all, value_all, attn_all = (
        gathered
    )
    onehot = (byte_ids[:, None] == jnp.arange(VOCAB, dtype=jnp.int32)[None, :]).astype(jnp.bfloat16)
    embedded = (
        (jnp.dot(onehot, table_all, preferred_element_type=jnp.float32) * keep_mask[:, None])
        .astype(jnp.bfloat16)
        .reshape(patches, D)
    )
    mixed_in = jnp.dot(embedded, patch_all, preferred_element_type=jnp.float32)
    normed_mix = root_norm(mixed_in, gain_mix).astype(jnp.bfloat16)
    projected = jnp.dot(normed_mix, in_all, preferred_element_type=jnp.float32).astype(jnp.bfloat16)
    rim_rows = passed_along(
        projected[patches - (CONV - 1) :, DI : 2 * DI + 2 * STATE], (NARROW, WIDE), 1
    ).astype(jnp.float32)
    projected_f = projected.astype(jnp.float32)
    small_params = (conv_weight, conv_bias, step_bias, log_rate, skip_gain)
    (decay_total, state_local), state_back = jax.vjp(
        partial(local_state, layout), projected_f, rim_rows, small_params
    )
    prefix = prefix_2(
        (decay_total, state_local),
        (NARROW, WIDE),
        combine_states,
        (jnp.ones_like(decay_total), jnp.zeros_like(state_local)),
    )
    incoming = prefix[1]
    gated_norm, mixer_back = jax.vjp(
        partial(mixer_output, layout), projected_f, rim_rows, small_params, incoming, gated_gain
    )
    gated_low = gated_norm.astype(jnp.bfloat16)
    global_out = mixed_in + jnp.dot(gated_low, out_all, preferred_element_type=jnp.float32)
    local_rows = global_out.astype(jnp.bfloat16).reshape(byte_rows, EMB)
    stream = jnp.dot(local_rows, local_all, preferred_element_type=jnp.float32)
    normed_attn, queries, key_rows, value_rows, attn_probs, mixed_heads = attend(
        stream, gain_attn, query_all, key_all, value_all
    )
    after_attn = stream + jnp.dot(mixed_heads, attn_all, preferred_element_type=jnp.float32)
    normed_feed = root_norm(after_attn, feed_gain).astype(jnp.bfloat16)
    out_grad = cotangent.astype(jnp.float32) * keep_mask[:, None]
    feed_grad = out_grad.astype(jnp.bfloat16)
    grid_in = spread(normed_feed)
    both_weights = jnp.concatenate([gate_weight, up_weight], axis=1)
    hidden_width = gate_weight.shape[1]
    grid_share = grid_in.shape[0] // wide_count
    gate_up_part = jnp.dot(grid_in, both_weights, preferred_element_type=jnp.float32).astype(
        jnp.bfloat16
    )
    gate_up = narrow_total(gate_up_part)
    hidden = (jax.nn.silu(gate_up[:, :hidden_width]) * gate_up[:, hidden_width:]).astype(
        jnp.bfloat16
    )

    def down_term(first_row, row_count):
        return jnp.dot(hidden, down_weight, preferred_element_type=jnp.float32)

    feed_out = collect(down_term, grid_share)
    grid_grad = spread(feed_grad)
    grad_down = jnp.einsum("gf,gd->fd", hidden, grid_grad, preferred_element_type=jnp.float32)
    hidden_part = jnp.einsum(
        "gd,fd->gf", grid_grad, down_weight, preferred_element_type=jnp.float32
    ).astype(jnp.bfloat16)
    hidden_grad = narrow_total(hidden_part)
    gate_up_grad = silu_back(gate_up, hidden_grad, hidden_width).astype(jnp.bfloat16)
    grad_both = jnp.einsum("gd,gf->df", grid_in, gate_up_grad, preferred_element_type=jnp.float32)

    def back_term(first_row, row_count):
        return jnp.einsum(
            "gf,df->gd", gate_up_grad, both_weights, preferred_element_type=jnp.float32
        )

    feed_in_grad = collect(back_term, grid_share)
    grad_gate = grad_both[:, :hidden_width]
    grad_up = grad_both[:, hidden_width:]
    after_feed = after_attn + feed_out.astype(jnp.float32)
    out_rows = (after_feed * keep_mask[:, None]).astype(jnp.bfloat16)
    feed_normed, feed_norm_back = jax.vjp(root_norm, after_attn, feed_gain)
    after_norm_grad, grad_feed_gain = feed_norm_back(feed_in_grad.astype(jnp.float32))
    after_grad = out_grad + after_norm_grad
    head_shape = (-1, PATCH, HEADS_A, HEAD_A)
    score_scale = HEAD_A ** (-0.5)
    attn_grad = after_grad.astype(jnp.bfloat16)
    grad_attn = jnp.einsum("rd,re->de", mixed_heads, attn_grad, preferred_element_type=jnp.float32)
    heads_grad = (
        jnp.einsum("re,de->rd", attn_grad, attn_all, preferred_element_type=jnp.float32)
        .astype(jnp.bfloat16)
        .reshape(head_shape)
    )
    probs_grad = jnp.einsum(
        "pqhe,pkhe->phqk",
        heads_grad,
        value_rows.reshape(head_shape),
        preferred_element_type=jnp.float32,
    )
    value_grad = (
        jnp.einsum(
            "phqk,pqhe->pkhe",
            attn_probs.astype(jnp.bfloat16),
            heads_grad,
            preferred_element_type=jnp.float32,
        )
        .reshape(byte_rows, D)
        .astype(jnp.bfloat16)
    )
    score_grad = (
        attn_probs * (probs_grad - jnp.sum(attn_probs * probs_grad, axis=-1, keepdims=True))
    ).astype(jnp.bfloat16)
    query_grad = (
        (
            jnp.einsum(
                "phqk,pkhe->pqhe",
                score_grad,
                key_rows.reshape(head_shape),
                preferred_element_type=jnp.float32,
            )
            * score_scale
        )
        .reshape(byte_rows, D)
        .astype(jnp.bfloat16)
    )
    key_grad = (
        (
            jnp.einsum(
                "phqk,pqhe->pkhe",
                score_grad,
                queries.reshape(head_shape),
                preferred_element_type=jnp.float32,
            )
            * score_scale
        )
        .reshape(byte_rows, D)
        .astype(jnp.bfloat16)
    )
    grad_query = jnp.einsum(
        "rd,re->de", normed_attn, query_grad, preferred_element_type=jnp.float32
    )
    grad_key = jnp.einsum("rd,re->de", normed_attn, key_grad, preferred_element_type=jnp.float32)
    grad_value = jnp.einsum(
        "rd,re->de", normed_attn, value_grad, preferred_element_type=jnp.float32
    )
    normed_grad = jnp.einsum("re,de->rd", query_grad, query_all, preferred_element_type=jnp.float32)
    normed_grad = normed_grad + jnp.einsum(
        "re,de->rd", key_grad, key_all, preferred_element_type=jnp.float32
    )
    normed_grad = normed_grad + jnp.einsum(
        "re,de->rd", value_grad, value_all, preferred_element_type=jnp.float32
    )
    attn_normed, attn_norm_back = jax.vjp(root_norm, stream, gain_attn)
    stream_norm_grad, grad_gain_attn = attn_norm_back(normed_grad)
    stream_grad = (after_grad + stream_norm_grad).astype(jnp.bfloat16)
    grad_local = jnp.einsum(
        "re,rd->ed", local_rows, stream_grad, preferred_element_type=jnp.float32
    )
    global_grad = jnp.einsum(
        "rd,ed->re", stream_grad, local_all, preferred_element_type=jnp.float32
    ).reshape(patches, D)
    mix_grad = global_grad.astype(jnp.bfloat16)
    grad_out = jnp.einsum("pi,pd->id", gated_low, mix_grad, preferred_element_type=jnp.float32)
    gated_grad = jnp.einsum("pd,id->pi", mix_grad, out_all, preferred_element_type=jnp.float32)
    proj_grad_mix, rim_grad_mix, small_grad_mix, incoming_grad, grad_gated_gain = mixer_back(
        gated_grad
    )
    suffix = carried_in_2(
        (decay_total, incoming_grad),
        (NARROW, WIDE),
        combine_states,
        (jnp.ones_like(decay_total), jnp.zeros_like(incoming_grad)),
    )
    later_grad = suffix[1]
    decay_grad = jnp.sum(later_grad * incoming, axis=(1, 2))
    proj_grad_state, rim_grad_state, small_grad_state = state_back((decay_grad, later_grad))
    rim_from_next = passed_along(rim_grad_mix + rim_grad_state, (NARROW, WIDE), -1)
    proj_grad = proj_grad_mix + proj_grad_state
    proj_grad = proj_grad.at[patches - (CONV - 1) :, DI : 2 * DI + 2 * STATE].add(rim_from_next)
    proj_low = proj_grad.astype(jnp.bfloat16)
    grad_in = jnp.einsum("pd,pk->dk", normed_mix, proj_low, preferred_element_type=jnp.float32)
    normed_mix_grad = jnp.einsum("pk,dk->pd", proj_low, in_all, preferred_element_type=jnp.float32)
    mix_normed, mix_norm_back = jax.vjp(root_norm, mixed_in, gain_mix)
    mixed_norm_grad, grad_gain_mix = mix_norm_back(normed_mix_grad)
    embed_grad = (global_grad + mixed_norm_grad).astype(jnp.bfloat16)
    grad_patch = jnp.einsum("pi,pd->id", embedded, embed_grad, preferred_element_type=jnp.float32)
    byte_grad = (
        jnp.einsum("pd,id->pi", embed_grad, patch_all, preferred_element_type=jnp.float32).reshape(
            byte_rows, EMB
        )
        * keep_mask[:, None]
    )
    grad_table = jnp.dot(onehot.astype(jnp.float32).T, byte_grad, precision=highest)
    shared = (
        lax.psum_scatter(grad_table, (NARROW, WIDE), scatter_dimension=0, tiled=True),
        lax.psum_scatter(grad_patch, (NARROW, WIDE), scatter_dimension=0, tiled=True),
        lax.psum_scatter(grad_in, (NARROW, WIDE), scatter_dimension=0, tiled=True),
        lax.psum_scatter(grad_out, (NARROW, WIDE), scatter_dimension=0, tiled=True),
        lax.psum_scatter(grad_local, (NARROW, WIDE), scatter_dimension=1, tiled=True),
        lax.psum_scatter(grad_query, (NARROW, WIDE), scatter_dimension=0, tiled=True),
        lax.psum_scatter(grad_key, (NARROW, WIDE), scatter_dimension=0, tiled=True),
        lax.psum_scatter(grad_value, (NARROW, WIDE), scatter_dimension=0, tiled=True),
        lax.psum_scatter(grad_attn, (NARROW, WIDE), scatter_dimension=0, tiled=True),
    )
    small_sum = lax.psum(
        (
            small_grad_mix[0] + small_grad_state[0],
            small_grad_mix[1] + small_grad_state[1],
            small_grad_mix[2] + small_grad_state[2],
            small_grad_mix[3] + small_grad_state[3],
            small_grad_mix[4] + small_grad_state[4],
            grad_gain_mix,
            grad_gated_gain,
            grad_gain_attn,
            grad_feed_gain,
        ),
        (NARROW, WIDE),
    )
    return (
        out_rows,
        shared[0],
        shared[1],
        small_sum[5],
        shared[2],
        small_sum[0],
        small_sum[1],
        small_sum[2],
        small_sum[3],
        small_sum[4],
        small_sum[6],
        shared[3],
        shared[4],
        small_sum[7],
        shared[5],
        shared[6],
        shared[7],
        shared[8],
        small_sum[8],
        grad_gate,
        grad_up,
        grad_down,
    )


QUERY = 128
BYTE_BLOCK = 128
MESH = pl.DeviceIdType.MESH
SUM_ROWS = (3 * D + DI + (CONV + 1) * 2 * STATE) // 128
LOW = jnp.bfloat16
FULL = jnp.float32
BOTH = (NARROW, WIDE)


def nn(a, b, precision=None):
    return lax.dot_general(
        a, b, (((1,), (0,)), ((), ())), precision=precision, preferred_element_type=FULL
    )


def nt(a, b, precision=None):
    return lax.dot_general(
        a, b, (((1,), (1,)), ((), ())), precision=precision, preferred_element_type=FULL
    )


def tn(a, b, precision=None):
    return lax.dot_general(
        a, b, (((0,), (0,)), ((), ())), precision=precision, preferred_element_type=FULL
    )


def device_at(place, wide):
    return (lax.div(place, wide), lax.rem(place, wide))


def remote(src, dst, send, recv, peer):
    return pltpu.make_async_remote_copy(
        src_ref=src, dst_ref=dst, send_sem=send, recv_sem=recv, device_id=peer, device_id_type=MESH
    )


def greet_all(devices, wide):
    me = lax.axis_index(NARROW) * wide + lax.axis_index(WIDE)
    barrier = pltpu.get_barrier_semaphore()

    def greet(k, carry):
        peer = device_at(lax.rem(me + k, devices), wide)
        pl.semaphore_signal(barrier, inc=1, device_id=peer, device_id_type=MESH)
        return carry

    lax.fori_loop(1, devices, greet, 0)
    return me, lambda: pl.semaphore_wait(barrier, devices - 1)


def send_blocks(me, devices, wide, src, dst, send, recv):
    def one(k, carry):
        place = lax.rem(me + k, devices)
        remote(src.at[place], dst.at[me], send, recv, device_at(place, wide)).start()
        return carry

    lax.fori_loop(1, devices, one, 0)


def wait_blocks(me, devices, wide, dst, send, recv):
    part = dst.at[pl.ds(0, devices - 1)]
    remote(part, part, send, recv, device_at(me, wide)).wait()


class StagedGather:
    def __init__(self, block, out, sems, narrow, depth):
        n, w = lax.axis_index(NARROW), lax.axis_index(WIDE)
        z, c = lax.div(w, 2), lax.rem(w, 2)
        self.out, self.narrow, self.depth = out, narrow, depth
        self.n, self.c = n, c
        self.sems = [sems.at[i] for i in range(7)]
        self.twin = (n, z * 2 + 1 - c)
        self.n_peers = [lax.rem(n + k, narrow) for k in range(1, narrow)]
        self.w = w
        self.own = pltpu.make_async_copy(block, out.at[n, z, c], self.sems[0])
        self.first = [
            remote(
                block,
                out.at[n, z, c],
                self.sems[1],
                self.sems[2],
                (n, lax.rem(z + k, depth) * 2 + c),
            )
            for k in range(1, depth)
        ]

    def wait_for(self, part, i):
        return remote(part, part, self.sems[i], self.sems[i + 1], self.twin)

    def z_part(self):
        return self.wait_for(self.out.at[self.n, pl.ds(0, self.depth - 1), self.c], 1)

    def n_part(self):
        return self.wait_for(self.out.at[pl.ds(0, self.narrow - 1), :, self.c], 3)

    def start(self):
        self.own.start()
        for copy in self.first:
            copy.start()

    def spread(self):
        self.own.wait()
        self.z_part().wait_recv()
        mine = self.out.at[self.n, :, self.c]
        for m in self.n_peers:
            remote(mine, mine, self.sems[3], self.sems[4], (m, self.w)).start()
        self.wait_for(mine, 5).start()

    def cross(self):
        self.n_part().wait_recv()
        for m in self.n_peers:
            self.wait_for(self.out.at[m, :, self.c], 5).start()

    def finish(self):
        self.wait_for(self.out.at[:, :, 1 - self.c], 5).wait()
        self.z_part().wait_send()
        self.n_part().wait_send()


def greet_lines(narrow, depth):
    n, w = lax.axis_index(NARROW), lax.axis_index(WIDE)
    z, c = lax.div(w, 2), lax.rem(w, 2)
    peers = [(n, lax.rem(z + k, depth) * 2 + c) for k in range(1, depth)]
    peers += [(lax.rem(n + k, narrow), w) for k in range(1, narrow)]
    peers += [(n, z * 2 + 1 - c)]
    barrier = pltpu.get_barrier_semaphore()
    for peer in peers:
        pl.semaphore_signal(barrier, inc=1, device_id=peer, device_id_type=MESH)
    pl.semaphore_wait(barrier, len(peers))


class LineSum:
    def __init__(self, parts, got, sems, place, length, peer_of):
        self.got, self.length = got, length
        self.own = pltpu.make_async_copy(parts.at[place], got.at[0], sems.at[0])
        self.copies = []
        for k in range(1, length):
            there = lax.rem(place + k, length)
            self.copies.append(
                remote(
                    parts.at[there], got.at[k], sems.at[2 * k - 1], sems.at[2 * k], peer_of(there)
                )
            )

    def start(self):
        self.own.start()
        for copy in self.copies:
            copy.start()

    def arrive(self):
        self.own.wait()
        for copy in self.copies:
            copy.wait_recv()

    def total(self, *index):
        summed = self.got[(0,) + index].astype(FULL)
        for k in range(1, self.length):
            summed += self.got[(k,) + index].astype(FULL)
        return summed

    def finish(self):
        for copy in self.copies:
            copy.wait_send()


def square_peer(n, k):
    x, y, kx, ky = lax.rem(n, 2), lax.div(n, 2), lax.rem(k, 2), lax.div(k, 2)
    return 2 * (y + ky - 2 * y * ky) + x + kx - 2 * x * kx


class SquareShare:
    def __init__(self, rows, got, send, recv, n, w):
        self.half = half = rows.shape[0] // 2
        low, high = pl.ds(0, half), pl.ds(half, half)
        beside, across = (square_peer(n, 1), w), (square_peer(n, 2), w)
        self.first = [
            remote(rows, got.at[1], send.at[1], recv.at[1], beside),
            remote(rows, got.at[2], send.at[2], recv.at[2], across),
        ]
        self.second = [
            remote(got.at[1, low], got.at[3, low], send.at[0], recv.at[0], across),
            remote(got.at[2, high], got.at[3, high], send.at[3], recv.at[3], beside),
        ]

    def start(self):
        for copy in self.first:
            copy.start()

    def relay(self, i):
        self.first[i].wait_recv()
        self.second[i].start()

    def arrive(self):
        for copy in self.second:
            copy.wait_recv()

    def finish(self):
        for copy in self.first + self.second:
            copy.wait_send()


def square_of(n, narrow):
    return n + 1 - 2 * lax.rem(n, 2), n + 2 - 4 * lax.div(n, 2), narrow - 1 - n


class SquareSum:
    def __init__(self, parts, own, held, got, sems, n, w, narrow):
        beside, across, corner = square_of(n, narrow)
        self.own, self.held, self.got = own, held, got
        self.half = half = parts.shape[1] // 2
        low, high = pl.ds(0, half), pl.ds(half, half)
        self.local = [
            pltpu.make_async_copy(parts.at[n], own, sems.at[0, 6]),
            pltpu.make_async_copy(parts.at[across, low], held.at[0], sems.at[0, 7]),
            pltpu.make_async_copy(parts.at[beside, high], held.at[1], sems.at[1, 6]),
        ]

        def send(i, src, peer):
            return remote(src, got.at[i], sems.at[0, i], sems.at[1, i], (peer, w))

        self.copies = [
            send(0, parts.at[corner, low], beside),
            send(1, parts.at[corner, high], across),
            send(2, parts.at[beside, low], beside),
            send(3, parts.at[across, high], across),
            send(4, held.at[1], beside),
            send(5, held.at[0], across),
        ]

    def start(self):
        for copy in self.local + self.copies[:4]:
            copy.start()

    def relay(self):
        for i in range(2):
            self.local[1 + i].wait()
            self.copies[i].wait_recv()
            for j in range(self.half):
                self.held[i, j] = (
                    self.held[i, j].astype(FULL) + self.got[i, j].astype(FULL)
                ).astype(LOW)
            self.copies[5 - i].start()

    def arrive(self):
        self.local[0].wait()
        for copy in self.copies[2:]:
            copy.wait_recv()

    def total(self, j):
        first, second = (2, 5) if j < self.half else (4, 3)
        summed = self.own[j].astype(FULL)
        for i in (first, second):
            summed += self.got[i, j % self.half].astype(FULL)
        return summed

    def finish(self):
        for copy in self.copies:
            copy.wait_send()


def end_kernel(
    narrow,
    depth,
    pack,
    sums,
    middle,
    up_sum,
    down_sum,
    pack_all,
    sums_all,
    middle_out,
    up_out,
    down_out,
    middle_got,
    up_got,
    down_got,
    pack_sems,
    sums_sems,
    middle_sems,
    back_send,
    back_recv,
    back_own,
):
    n, w = lax.axis_index(NARROW), lax.axis_index(WIDE)
    z, c = lax.div(w, 2), lax.rem(w, 2)
    greet_lines(narrow, depth)
    gathers = [
        StagedGather(pack, pack_all, pack_sems, narrow, depth),
        StagedGather(sums, sums_all, sums_sems, narrow, depth),
    ]
    line = LineSum(middle, middle_got, middle_sems, z, depth, lambda there: (n, there * 2 + c))
    backs = [
        Returned(
            values, landed, back_send.at[i], back_recv.at[i], back_own.at[i], n, w, narrow, i
        )
        for i, (values, landed) in enumerate(((up_sum, up_got), (down_sum, down_got)))
    ]
    for gather in gathers:
        gather.start()
    line.start()
    for back in backs:
        back.start()
    for gather in gathers:
        gather.spread()
    for gather in gathers:
        gather.cross()
    line.arrive()
    middle_out[...] = line.total()
    for back, landed, out in zip(backs, (up_got, down_got), (up_out, down_out)):
        back.arrive()
        out[...] = landed[...].astype(FULL)
    for gather in gathers:
        gather.finish()
    line.finish()
    for back in backs:
        back.finish()


class Returned:
    def __init__(self, values, got, send, recv, own, n, w, narrow, axis):
        span = values.shape[axis] // narrow
        other = values.shape[1 - axis]

        def block(m):
            mine = pl.ds(m * span, span)
            return values.at[mine, :] if axis == 0 else values.at[:, mine]

        there = pl.ds(n * other, other)
        landing = got.at[:, there] if axis == 0 else got.at[there, :]
        self.own = pltpu.make_async_copy(block(n), landing, own)
        self.copies = []
        for k in range(1, narrow):
            m = lax.rem(n + k, narrow)
            self.copies.append(
                remote(block(m), landing, send.at[k - 1], recv.at[k - 1], (m, w))
            )

    def start(self):
        self.own.start()
        for copy in self.copies:
            copy.start()

    def arrive(self):
        self.own.wait()
        for copy in self.copies:
            copy.wait_recv()

    def finish(self):
        for copy in self.copies:
            copy.wait_send()


def end_gather(pack, sums, middle, up_sum, down_sum, collective_id):
    narrow, wide = lax.axis_size(NARROW), lax.axis_size(WIDE)
    depth = wide // 2
    dma = pltpu.SemaphoreType.DMA
    anywhere = pl.BlockSpec(memory_space=pl.ANY)
    up_shape = (up_sum.shape[0] // narrow, up_sum.shape[1] * narrow)
    down_shape = (down_sum.shape[0] * narrow, down_sum.shape[1] // narrow)
    outs = pl.pallas_call(
        partial(end_kernel, narrow, depth),
        out_shape=[
            jax.ShapeDtypeStruct((narrow, depth, 2) + pack.shape, pack.dtype),
            jax.ShapeDtypeStruct((narrow, depth, 2) + sums.shape, sums.dtype),
            jax.ShapeDtypeStruct(middle.shape[1:], FULL),
            jax.ShapeDtypeStruct(up_shape, FULL),
            jax.ShapeDtypeStruct(down_shape, FULL),
        ],
        in_specs=[anywhere] * 5,
        out_specs=[anywhere] * 2 + [in_vmem()] * 3,
        scratch_shapes=[
            pltpu.VMEM(middle.shape, middle.dtype),
            pltpu.VMEM(up_shape, LOW),
            pltpu.VMEM(down_shape, LOW),
            dma((7,)),
            dma((7,)),
            dma((2 * depth,)),
            dma((2, narrow - 1)),
            dma((2, narrow - 1)),
            dma((2,)),
        ],
        compiler_params=pltpu.CompilerParams(
            collective_id=collective_id, has_side_effects=True, vmem_limit_bytes=10 << 20
        ),
        name="end_gather",
    )(pack, sums, middle, up_sum, down_sum)
    return [
        outs[0].reshape(-1, pack.shape[1]),
        outs[1].reshape((-1,) + sums.shape),
    ] + list(outs[2:])


def softplus(v):
    return jnp.maximum(v, 0.0) + jnp.log1p(jnp.exp(-jnp.abs(v)))


def convolved(window, marks, weight, bias):
    pre = bias + weight[CONV - 1 :] * window[8:]
    for lag in range(1, CONV):
        pre = pre + weight[CONV - 1 - lag : CONV - lag] * (
            window[8 - lag : 8 - lag + QUERY] * marks[:, lag : lag + 1]
        )
    return pre


def decays(marks, dt, step_bias, rate_scale):
    shape = (QUERY, QUERY)
    row = lax.broadcasted_iota(jnp.int32, shape, 0)
    column = lax.broadcasted_iota(jnp.int32, shape, 1)
    lower = (row >= column).astype(FULL)
    segment = jnp.broadcast_to(marks[:, :1], shape)
    visible = (segment == segment.T) & (row >= column)
    delta = jnp.broadcast_to(softplus(dt + step_bias), shape)
    total = nn(lower, -delta * rate_scale, highest)
    gap = jnp.where(visible, total - total.T, 0.0)
    decay = jnp.where(visible, jnp.exp(gap), 0.0)
    last = total[QUERY - 1 :, :]
    begun = jnp.exp(total) * marks[:, 4:5]
    tail = jnp.exp(last - total) * marks[:, 5:6]
    kept = jnp.exp(last) * marks[:1, 6:7]
    return lower, delta, decay, begun, tail, kept


def head_numbers(step_bias, log_rate, skip_gain, me):
    return step_bias[me], jnp.exp(jnp.full((1, QUERY), log_rate[me], FULL)), skip_gain[me]


def head_columns(values, me):
    start = pl.multiple_of(lax.div(me, 2) * 2 * HEAD_M, 2 * HEAD_M)
    pair = values[:, pl.ds(start, 2 * HEAD_M)]
    lane = lax.broadcasted_iota(jnp.int32, pair.shape, 1)
    moved = jnp.concatenate([pair[:, HEAD_M:], pair[:, :HEAD_M]], axis=1)
    odd = jnp.full(pair.shape, lax.rem(me, 2), jnp.int32) == 1
    return jnp.where(lane < HEAD_M, jnp.where(odd, moved, pair), 0.0)


def documents(doc_patches, pad_bytes):
    ends, end = [], 0
    for d in range(doc_patches.shape[0]):
        end = end + doc_patches[d]
        ends.append(end)

    def document(place):
        return sum((place >= end).astype(jnp.int32) for end in ends)

    def kept(place, offset):
        padded = [
            ((place == end - 1) & (offset >= PATCH - pad_bytes[d])).astype(FULL)
            for d, end in enumerate(ends)
        ]
        return 1.0 - sum(padded)

    return document, kept


def patch_marks(document, first, count):
    place = first + lax.broadcasted_iota(jnp.int32, (count, 8), 0)
    kind = lax.broadcasted_iota(jnp.int32, (count, 8), 1)
    opening = lax.div(place, QUERY) * QUERY
    block_mark = jnp.where(kind == CONV, opening - 1, opening + QUERY - 1)
    ahead = jnp.where(kind < CONV, place - kind, block_mark)
    facing = jnp.where(kind == CONV + 2, opening - 1, place)
    same = (document(ahead) == document(facing)) & (ahead >= 0) & (facing >= 0)
    return jnp.where(kind == 0, document(place).astype(FULL), same.astype(FULL))


def mixer_front_kernel(
    narrow,
    wide,
    doc_patches,
    pad_bytes,
    step_biases,
    log_rates,
    skip_gains,
    gain,
    conv_weight,
    conv_bias,
    pack,
    table,
    xz_blocks,
    gate,
    up,
    down,
    middle,
    cotangent,
    embedded,
    normed,
    xz,
    bc,
    dt,
    u_out,
    y_out,
    states,
    mixed_in,
    u_got,
    marks,
    keep_rows,
    keep_all,
    start,
    w_xz,
    gate_all,
    up_all,
    down_all,
    middle_all,
    others,
    table_all,
    gate_turned,
    up_turned,
    down_turned,
    mixed_all,
    xz_pad,
    bc_pad,
    state,
    u_blocks,
    u_send,
    u_recv,
    pack_sems,
    table_sems,
    xz_sems,
    turn_send,
    turn_recv,
    start_sems,
    depth_send,
    depth_recv,
    other_send,
    other_recv,
    own_sems,
    line_send,
    line_recv,
    cross_send,
    cross_recv,
    middle_sems,
):
    devices, depth = narrow * wide, wide // 2
    me, arrived = greet_all(devices, wide)
    n, w = lax.axis_index(NARROW), lax.axis_index(WIDE)
    z, c = lax.div(w, 2), lax.rem(w, 2)
    twin = (n, z * 2 + 1 - c)
    rows_in, units_in = gate.shape[0], gate.shape[1] // narrow
    columns_in = down.shape[1]
    gathers = [
        StagedGather(pack, start, pack_sems, narrow, depth),
        StagedGather(table, table_all, table_sems, narrow, depth),
    ]

    def pieces(m):
        mine = pl.ds(m * units_in, units_in)
        return (gate.at[:, mine], up.at[:, mine], down.at[mine, :])

    turned = (gate_turned, up_turned, down_turned)
    landing = (
        gate_turned.at[pl.ds(n * rows_in, rows_in), :],
        up_turned.at[pl.ds(n * rows_in, rows_in), :],
        down_turned.at[:, pl.ds(n * columns_in, columns_in)],
    )
    turns = []
    for k in range(1, narrow):
        m = lax.rem(n + k, narrow)
        for i, piece in enumerate(pieces(m)):
            turns.append(
                remote(piece, landing[i], turn_send.at[k - 1, i], turn_recv.at[k - 1, i], (m, w))
            )
    first_own = [
        pltpu.make_async_copy(piece, landing[i], start_sems.at[i])
        for i, piece in enumerate(pieces(n))
    ]
    own_xz = pltpu.make_async_copy(xz_blocks.at[me], w_xz.at[me], start_sems.at[3])
    own_middle = pltpu.make_async_copy(middle, middle_all.at[n, z, c], start_sems.at[4])

    def depth_copy(source, target):
        return remote(
            middle,
            middle_all.at[n, source, c],
            depth_send.at[target],
            depth_recv.at[source],
            (n, target * 2 + c),
        )

    share = SquareShare(cotangent, others, other_send, other_recv, n, w)
    results = (gate_all, up_all, down_all)
    own = [pltpu.make_async_copy(turned[i], results[i].at[z, c], own_sems.at[i]) for i in range(3)]
    beside, across, corner = square_of(n, narrow)

    def middle_copy(j, way, owner):
        there = middle_all.at[owner, j, c]
        peer = twin if way >= 4 else ((beside if way in (0, 3) else across), w)
        return remote(there, there, middle_sems.at[0, way, j], middle_sems.at[1, way, j], peer)

    def line_copy(i, source, step, src=None):
        there = results[i].at[source, c]
        return remote(
            there if src is None else src,
            there,
            line_send.at[i, source, max(step, 0)],
            line_recv.at[i, source],
            (n, (z + step) * 2 + c),
        )

    def along(i, source, step, src=None):
        @pl.when((z + step >= 0) & (z + step < depth))
        def _():
            line_copy(i, source, step, src).start()

    def middle_begin(j):
        @pl.when(z == j)
        def _():
            own_middle.wait()

        @pl.when(z != j)
        def _():
            depth_copy(j, z).wait_recv()

        for way in (0, 1, 7):
            middle_copy(j, way, n).start()

    def middle_on(j):
        middle_copy(j, 0, beside).wait_recv()
        if j % 2 == 0:
            middle_copy(j, 2, beside).start()
        middle_copy(j, 4, beside).start()
        middle_copy(j, 1, across).wait_recv()
        if j % 2 == 1:
            middle_copy(j, 3, across).start()
        middle_copy(j, 5, across).start()

    def line_side(distance, step):
        source = z - step * distance

        @pl.when((source >= 0) & (source < depth))
        def _():
            for i in range(3):
                line_copy(i, source, step).wait_recv()
                along(i, source, step)
                theirs = results[i].at[source, c]
                remote(theirs, theirs, cross_send.at[i], cross_recv.at[i], twin).start()

    def line_on(distance):
        @pl.when(2 * z < depth)
        def _():
            line_side(distance, 1)
            line_side(distance, -1)

        @pl.when(2 * z >= depth)
        def _():
            line_side(distance, -1)
            line_side(distance, 1)

    arrived()
    for gather in gathers:
        gather.start()
    for copy in turns + first_own + [own_xz, own_middle]:
        copy.start()
    send_blocks(me, devices, wide, xz_blocks, w_xz, xz_sems.at[0], xz_sems.at[1])
    for distance in range(1, depth):
        for target in (z + distance, z - distance):

            @pl.when((target >= 0) & (target < depth))
            def _():
                depth_copy(z, target).start()

    for gather in gathers:
        gather.spread()
    for copy in first_own[:3]:
        copy.wait()
    for copy in turns:
        copy.wait_recv()
    for i in range(3):
        along(i, z, 1, turned[i])
        along(i, z, -1, turned[i])
    for copy in own:
        copy.start()
    for gather in gathers:
        gather.cross()
    share.start()

    count = embedded.shape[0]
    patches = u_blocks.shape[1]
    block_rows = 2 * QUERY
    xz_pad[pl.ds(0, 8), :] = jnp.zeros((8, xz_pad.shape[1]), FULL)
    bc_pad[pl.ds(0, 8), :] = jnp.zeros((8, bc_pad.shape[1]), FULL)
    state[...] = jnp.zeros_like(state)
    step_bias, rate_scale, skip = head_numbers(step_biases, log_rates, skip_gains, me)
    document, kept_bytes = documents(doc_patches, pad_bytes)
    for first in range(0, count + 8, (count + 8) // 3):
        part = (count + 8) // 3
        marks[first : first + part, :] = patch_marks(document, first, part)
    byte = lax.broadcasted_iota(jnp.int32, keep_rows.shape[1:], 0)
    for k in range(narrow):
        there = (square_peer(n, k) * wide + w) * patches
        keep_rows[k] = kept_bytes(there + lax.div(byte, PATCH), lax.rem(byte, PATCH))
    wx, bx = head_columns(conv_weight, me), head_columns(conv_bias, me)
    wbc, bbc = conv_weight[:, DI:], conv_bias[:, DI:]
    for gather in gathers:
        gather.finish()
    own_xz.wait()
    wait_blocks(me, devices, wide, w_xz, xz_sems.at[0], xz_sems.at[1])
    words = lax.broadcasted_iota(jnp.int32, (block_rows, VOCAB), 1).astype(FULL)
    own_lane = lax.broadcasted_iota(jnp.int32, (block_rows, STATE), 1) == me

    word_rows = table_all[...].reshape(VOCAB, EMB).astype(LOW)

    def project(i, carry):
        rows = pl.ds(pl.multiple_of(i * block_rows, block_rows), block_rows)
        ids = start[i, :, :, :, 3 * STATE : 4 * STATE].reshape(block_rows, STATE).astype(FULL)
        place = i * block_rows + lax.broadcasted_iota(jnp.int32, (block_rows, PATCH), 0)
        kept = kept_bytes(place, lax.broadcasted_iota(jnp.int32, (block_rows, PATCH), 1))
        keep_all[rows, :] = kept
        for k in range(PATCH):
            chosen = jnp.where(ids[:, k : k + 1] == words, kept[:, k : k + 1], 0.0).astype(LOW)
            embedded[rows, k * EMB : (k + 1) * EMB] = nn(chosen, word_rows).astype(LOW)
        row_embedded = embedded[rows, :]
        for first in range(0, D, WEIGHT_STEP):
            columns = slice(first, first + WEIGHT_STEP)
            there = slice(4 * STATE + first, 4 * STATE + first + WEIGHT_STEP)
            weight = start[:, :, :, :, there].reshape(D, WEIGHT_STEP)
            mixed_all[rows, columns] = nn(row_embedded, weight)
        row_normed = (unit_rows(mixed_all[rows, :])[0] * gain[...]).astype(LOW)
        normed[rows, :] = row_normed
        row_xz = nn(row_normed, w_xz[...].reshape(D, 2 * HEAD_M)).astype(LOW)
        weight = start[:, :, :, :, : 3 * STATE].reshape(D, 3 * STATE)
        row_bcdt = nn(row_normed, weight).astype(LOW)
        xz[rows, :] = row_xz
        bc[rows, :] = row_bcdt[:, : 2 * STATE]
        own_dt = jnp.where(own_lane, row_bcdt[:, 2 * STATE :].astype(FULL), 0.0)
        dt[rows, :] = jnp.sum(own_dt, axis=1, keepdims=True)
        padded = pl.ds(pl.multiple_of(i * block_rows + 8, 8), block_rows)
        xz_pad[padded, :] = row_xz.astype(FULL)
        bc_pad[padded, :] = row_bcdt[:, : 2 * STATE].astype(FULL)
        return carry

    lax.fori_loop(0, count // block_rows, project, 0)
    for j in range(depth):
        middle_begin(j)
    for i in range(2):
        share.relay(i)
    mixed_in[...] = mixed_all[pl.ds(pl.multiple_of(me * patches, patches), patches), :]
    group = QUERY // patches

    def block(i, carry):
        first = pl.multiple_of(i * QUERY, QUERY)
        rows = pl.ds(first, QUERY)
        mark = marks[rows, :]
        act_x = jax.nn.silu(convolved(xz_pad[pl.ds(first, QUERY + 8), :], mark, wx, bx))
        act = jax.nn.silu(convolved(bc_pad[pl.ds(first, QUERY + 8), :], mark, wbc, bbc))
        x, b, c = act_x[:, :HEAD_M], act[:, :STATE], act[:, STATE:]
        lower, delta, decay, begun, tail, kept = decays(mark, dt[rows, :], step_bias, rate_scale)
        weight = nt(c, b, highest) * decay * delta.T
        held = state[...]
        states[i] = held
        y = (
            nn(weight, x, highest)
            + nt(c, held, highest) * begun[:, :HEAD_M]
            + skip * x
        )
        state[...] = held * kept + tn(x * (tail * delta)[:, :HEAD_M], b, highest)
        z = xz[rows, :].astype(FULL)[:, HEAD_M:]
        u = y * jax.nn.silu(z)
        y_out[rows, :] = y
        u_out[rows, :] = u
        u_blocks[pl.ds(i * group, group)] = u.astype(LOW).reshape(group, patches, HEAD_M)
        return carry

    lax.fori_loop(0, count // QUERY, block, 0)
    send_blocks(me, devices, wide, u_blocks, u_got, u_send, u_recv)
    u_got[me] = u_blocks[me]
    line_on(1)
    for copy in own:
        copy.wait()
    for i in range(3):
        mine = results[i].at[z, c]
        remote(mine, mine, cross_send.at[i], cross_recv.at[i], twin).start()
    middle_on(0)
    middle_on(1)
    line_on(2)
    middle_on(2)
    middle_on(3)
    for j in range(depth):
        middle_copy(j, 2 + j % 2, corner).wait_recv()
        middle_copy(j, 6, corner).start()
    line_on(3)
    wait_blocks(me, devices, wide, u_got, u_send, u_recv)
    share.arrive()
    share.finish()
    for copy in turns:
        copy.wait_send()
    for target in range(depth):

        @pl.when(target != z)
        def _():
            depth_copy(z, target).wait_send()

    for i in range(3):
        theirs = results[i].at[:, 1 - c]
        remote(theirs, theirs, cross_send.at[i], cross_recv.at[i], twin).wait()
    for j in range(depth):
        for way, owner in ((4, beside), (5, across), (6, corner), (7, n)):
            middle_copy(j, way, owner).wait()
        for way in (0, 1, 2 + j % 2):
            middle_copy(j, way, n).wait_send()
    for i in range(3):
        for source in range(depth):
            for step in (1, -1):

                @pl.when((step * (z - source) >= 0) & (z + step >= 0) & (z + step < depth))
                def _():
                    line_copy(i, source, step).wait_send()


def mixer_backward_kernel(
    narrow,
    wide,
    step_biases,
    log_rates,
    skip_gains,
    xz,
    bc,
    dt,
    marks,
    conv_weight,
    conv_bias,
    y_in,
    states,
    normed,
    w_xz,
    start,
    mixed_in,
    global_grad,
    gain,
    gated_scale,
    gain_grads,
    gated_gain_grads,
    du_blocks,
    up_parts,
    down_parts,
    middle_parts,
    gate_sum,
    mix_grad,
    end_pack,
    sums,
    bcdt_grads,
    xz_grads,
    up_sum,
    down_sum,
    middle_sums,
    gate_out,
    mix_all,
    w_bcdt,
    w_sem,
    dwx,
    dwbc,
    dnumbers,
    xz_pad,
    bc_pad,
    dx_pad,
    dbc_pad,
    dstate,
    du_got,
    dxz,
    dbcdt,
    partial_rows,
    core_got,
    narrow_got,
    z_rows,
    z_got,
    grads,
    grads_got,
    up_got,
    down_got,
    middle_own,
    middle_held,
    middle_got,
    gate_got,
    du_send,
    du_recv,
    core_send,
    core_recv,
    narrow_send,
    narrow_recv,
    z_send,
    z_recv,
    grads_send,
    grads_recv,
    up_sems,
    down_sems,
    middle_sems,
    back_send,
    back_recv,
    back_own,
    mix_sems,
):
    devices = narrow * wide
    depth = wide // 2
    me, arrived = greet_all(devices, wide)
    n, w = lax.axis_index(NARROW), lax.axis_index(WIDE)
    z_place, core = lax.div(w, 2), lax.rem(w, 2)
    twin = (n, z_place * 2 + 1 - core)
    count = xz.shape[0]
    blocks = count // QUERY
    xz_pad[pl.ds(0, 8), :] = jnp.zeros((8, xz_pad.shape[1]), FULL)
    bc_pad[pl.ds(0, 8), :] = jnp.zeros((8, bc_pad.shape[1]), FULL)
    dx_pad[pl.ds(count, 8), :] = jnp.zeros((8, dx_pad.shape[1]), FULL)
    dbc_pad[pl.ds(count, 8), :] = jnp.zeros((8, dbc_pad.shape[1]), FULL)
    dstate[...] = jnp.zeros_like(dstate)
    dwx[...] = jnp.zeros_like(dwx)
    dwbc[...] = jnp.zeros_like(dwbc)
    dnumbers[...] = jnp.zeros_like(dnumbers)
    step_bias, rate_scale, skip = head_numbers(step_biases, log_rates, skip_gains, me)
    wx, bx = head_columns(conv_weight, me), head_columns(conv_bias, me)
    wbc, bbc = conv_weight[:, DI:], conv_bias[:, DI:]
    weight_copy = pltpu.make_async_copy(start.at[:, pl.ds(0, 3 * STATE)], w_bcdt, w_sem)
    weight_copy.start()

    def fill(i, carry):
        first = pl.multiple_of(i * QUERY, QUERY)
        rows = pl.ds(first, QUERY)
        xz_pad[pl.ds(first + 8, QUERY), :] = xz[rows, :].astype(FULL)
        bc_pad[pl.ds(first + 8, QUERY), :] = bc[rows, :].astype(FULL)
        return carry

    arrived()
    send_blocks(me, devices, wide, du_blocks, du_got, du_send, du_recv)
    lines = [
        LineSum(parts, landed, line_sems, z_place, depth, lambda there: (n, there * 2 + core))
        for parts, landed, line_sems in (
            (down_parts, down_got, down_sems),
            (up_parts, up_got, up_sems),
        )
    ]
    middle_line = SquareSum(
        middle_parts, middle_own, middle_held, middle_got, middle_sems, n, w, narrow
    )
    back = Returned(gate_sum, gate_got, back_send, back_recv, back_own, n, w, narrow, 0)
    mix_gather = StagedGather(mix_grad, mix_all, mix_sems, narrow, depth)
    middle_line.start()
    mix_gather.start()
    for line in lines:
        line.start()
    back.start()
    du_got[me] = du_blocks[me]
    lax.fori_loop(0, blocks, fill, 0)
    wait_blocks(me, devices, wide, du_got, du_send, du_recv)
    patches = du_blocks.shape[1]
    group = QUERY // patches
    own_lane = lax.broadcasted_iota(jnp.int32, (QUERY, STATE), 1) == me

    def slope(pre):
        s = jax.nn.sigmoid(pre)
        return s * (1.0 + pre * (1.0 - s))

    def total(v):
        return jnp.sum(jnp.sum(v, axis=1, keepdims=True), axis=0, keepdims=True)

    def conv_back(pad, first, dpre_pad, dpre, weight, dw):
        mark = marks[pl.ds(first, QUERY), :]
        window = pad[pl.ds(first, QUERY + 8), :]
        later = dpre_pad[pl.ds(first, QUERY + 8), :]
        later_marks = marks[pl.ds(first, QUERY + 8), :]
        out = weight[CONV - 1 :] * dpre
        dw[CONV - 1 : CONV, :] += jnp.sum(dpre * window[8:], axis=0, keepdims=True)
        dw[CONV : CONV + 1, :] += jnp.sum(dpre, axis=0, keepdims=True)
        for lag in range(1, CONV):
            tap = CONV - 1 - lag
            out = out + weight[tap : tap + 1] * (
                (later * later_marks[:, lag : lag + 1])[lag : lag + QUERY]
            )
            dw[tap : tap + 1, :] += jnp.sum(
                dpre * (window[8 - lag : 8 - lag + QUERY] * mark[:, lag : lag + 1]),
                axis=0,
                keepdims=True,
            )
        return out

    def block(k, carry):
        i = blocks - 1 - k
        first = pl.multiple_of(i * QUERY, QUERY)
        rows = pl.ds(first, QUERY)
        mark = marks[rows, :]
        pre_x = convolved(xz_pad[pl.ds(first, QUERY + 8), :], mark, wx, bx)
        pre = convolved(bc_pad[pl.ds(first, QUERY + 8), :], mark, wbc, bbc)
        act = jax.nn.silu(pre)
        x, b, c = jax.nn.silu(pre_x)[:, :HEAD_M], act[:, :STATE], act[:, STATE:]
        step = dt[rows, :]
        lower, delta, decay, begun, tail, kept = decays(mark, step, step_bias, rate_scale)
        held, dheld = states[i], dstate[...]
        z = xz[rows, :].astype(FULL)[:, HEAD_M:]
        du = du_got[pl.ds(i * group, group)].astype(FULL).reshape(QUERY, HEAD_M)
        y = y_in[rows, :]
        dy = du * jax.nn.silu(z)
        dz = du * y * slope(z)
        scores = nt(c, b, highest)
        reach = decay * delta.T
        dweight = nt(dy, x, highest)
        dscores = dweight * reach
        fed = x * (tail * delta)[:, :HEAD_M]
        begun_dy = dy * begun[:, :HEAD_M]
        dc = nn(dscores, b, highest) + nn(begun_dy, held, highest)
        db = tn(dscores, c, highest) + nn(fed, dheld, highest)
        dfed = nt(b, dheld, highest)
        dx = skip * dy + tn(scores * reach, dy, highest) + (tail * delta)[:, :HEAD_M] * dfed
        moved = dweight * scores * decay
        turned = moved.T
        ddelta = jnp.sum(turned, axis=1, keepdims=True)
        dtotal = jnp.sum(moved * delta.T, axis=1, keepdims=True) - ddelta * delta[:, :1]
        dtotal += jnp.sum(begun_dy * nt(c, held, highest), axis=1, keepdims=True)
        dtail = jnp.sum(dfed * x, axis=1, keepdims=True)
        ddelta += dtail * tail[:, :1]
        dtail = dtail * (tail * delta)[:, :1]
        dtotal -= dtail
        dlast = jnp.sum(dtail, axis=0, keepdims=True) + total(dheld * held * kept)
        dlog = tn(lower, jnp.broadcast_to(dtotal, (QUERY, QUERY)), highest)[:, :1] + dlast
        ddelta -= dlog * rate_scale[:, :1]
        dstep = ddelta * jax.nn.sigmoid(step + step_bias)
        dbcdt[rows, 2 * STATE :] = jnp.where(own_lane, dstep, 0.0).astype(LOW)
        dnumbers[0:1, :] += jnp.broadcast_to(jnp.sum(dstep, axis=0, keepdims=True), (1, 128))
        dnumbers[1:2, :] -= jnp.broadcast_to(
            jnp.sum(dlog * delta[:, :1] * rate_scale[:, :1], axis=0, keepdims=True), (1, 128)
        )
        dnumbers[2:3, :] += jnp.broadcast_to(total(dy * x), (1, 128))
        dstate[...] = dheld * kept + tn(begun_dy, c, highest)
        dpre_x = jnp.concatenate([dx, jnp.zeros_like(dx)], axis=1) * slope(pre_x)
        dpre = jnp.concatenate([db, dc], axis=1) * slope(pre)
        dx_pad[rows, :] = dpre_x
        dbc_pad[rows, :] = dpre
        dxz[rows, :] = jnp.concatenate([dz, dz], axis=1).astype(LOW)
        return carry

    lax.fori_loop(0, blocks, block, 0)

    def unconvolve(i, carry):
        first = pl.multiple_of(i * QUERY, QUERY)
        rows = pl.ds(first, QUERY)
        dxr = conv_back(xz_pad, first, dx_pad, dx_pad[rows, :], wx, dwx)
        left = lax.broadcasted_iota(jnp.int32, dxr.shape, 1) < HEAD_M
        dxz[rows, :] = jnp.where(left, dxr, dxz[rows, :].astype(FULL)).astype(LOW)
        dbcdt[rows, : 2 * STATE] = conv_back(
            bc_pad, first, dbc_pad, dbc_pad[rows, :], wbc, dwbc
        ).astype(LOW)
        return carry

    middle_line.relay()
    mix_gather.spread()
    lax.fori_loop(0, blocks, unconvolve, 0)

    width = normed.shape[1]
    own_rows = xz_grads.shape[1]

    weight_copy.wait()

    def rows_of(m, carry):
        for z in range(depth):
            first = (m * depth + z) * 2 * patches
            rows = pl.ds(pl.multiple_of(first, 2 * patches), 2 * patches)
            values = nt(dxz[rows, :], w_xz[...]) + nt(dbcdt[rows, :], w_bcdt[...])
            partial_rows[m, z, :, :, :width] = values.astype(LOW).reshape(2, patches, width)
        return carry

    lax.fori_loop(0, narrow, rows_of, 0)

    def weight_grads(m, carry):
        span = width // narrow
        columns = pl.ds(pl.multiple_of(m * span, span), span)
        lhs = normed[:, columns]
        grads[pl.ds(m * 2 * depth, 2 * depth)] = (
            tn(lhs, dxz[...]).astype(LOW).reshape(2 * depth, own_rows, 2 * HEAD_M)
        )
        partial_rows[m, :, :, :, width:] = (
            tn(lhs, dbcdt[...]).astype(LOW).reshape(depth, 2, own_rows, 3 * STATE)
        )
        return carry

    lax.fori_loop(0, narrow, weight_grads, 0)
    to_twin = remote(partial_rows.at[:, :, 1 - core], core_got, core_send, core_recv, twin)
    to_twin.start()
    send_blocks(me, devices, wide, grads, grads_got, grads_send, grads_recv)
    grads_got[me] = grads[me]
    back.arrive()
    gate_out[...] = gate_got[...].astype(FULL)
    to_twin.wait_recv()

    def narrow_copy(k, m):
        return remote(
            core_got.at[m], narrow_got.at[k - 1], narrow_send.at[k - 1], narrow_recv.at[k - 1], (m, w)
        )

    for k in range(1, narrow):
        m = lax.rem(n + k, narrow)
        for z in range(depth):
            core_got[m, z] = (
                core_got[m, z].astype(FULL) + partial_rows[m, z, core].astype(FULL)
            ).astype(LOW)
        narrow_copy(k, m).start()
    mix_gather.cross()
    middle_line.arrive()
    for z in range(depth):
        middle_sums[z] = middle_line.total(z).astype(LOW)
    for k in range(1, narrow):
        narrow_copy(k, n).wait_recv()
    for z in range(depth):
        total_rows = core_got[n, z].astype(FULL) + partial_rows[n, z, core].astype(FULL)
        for k in range(1, narrow):
            total_rows += narrow_got[k - 1, z].astype(FULL)
        z_rows[z] = total_rows.astype(LOW)

    def z_copy(k, place):
        return remote(
            z_rows.at[place], z_got.at[k - 1], z_send.at[k - 1], z_recv.at[k - 1], (n, place * 2 + core)
        )

    for k in range(1, depth):
        z_copy(k, lax.rem(z_place + k, depth)).start()
    for line, out in zip(lines, (down_sum, up_sum)):
        line.arrive()
        out[...] = line.total().astype(LOW)
    wait_blocks(me, devices, wide, grads_got, grads_send, grads_recv)
    xz_grads[...] = grads_got[...]
    total_rows = z_rows[z_place].astype(FULL)
    for k in range(1, depth):
        z_copy(k, z_place).wait_recv()
        total_rows += z_got[k - 1].astype(FULL)
    bcdt_grads[...] = total_rows[:, width:]
    unit, scale = unit_rows(mixed_in[...])
    normed_grad = total_rows[:, :width]
    embed_grad = global_grad[...] + norm_back(normed_grad, gain[...], unit, scale)
    end_pack[:, :width] = embed_grad.astype(LOW)
    end_pack[:, width:] = gated_scale[...].astype(LOW)
    gain_mix_grad = jnp.sum(normed_grad * unit, axis=0, keepdims=True)
    wide_rows = [gain_mix_grad] + [gated_gain_grads[i : i + 1, :] for i in range(2)]
    wide_rows += [gain_grads[i : i + 1, :] for i in range(2)]
    wide_rows += [dwbc[i : i + 1, :] for i in range(CONV + 1)]
    wide_rows += [dwx[i : i + 1, :] for i in range(CONV + 1)]
    row = 0
    for values in wide_rows:
        for first in range(0, values.shape[1], 128):
            sums[row : row + 1, :] = values[:, first : first + 128]
            row += 1
    lane = lax.broadcasted_iota(jnp.int32, (1, 128), 1)
    sums[row : row + 1, :] = sum(
        jnp.where(lane == i, dnumbers[i : i + 1, :], 0.0) for i in range(3)
    )
    mix_gather.finish()
    for line in lines:
        line.finish()
    middle_line.finish()
    back.finish()
    to_twin.wait_send()
    for k in range(1, narrow):
        narrow_copy(k, n).wait_send()
    for k in range(1, depth):
        z_copy(k, z_place).wait_send()


def in_smem():
    return pl.BlockSpec(memory_space=pltpu.SMEM)


def in_vmem():
    return pl.BlockSpec(memory_space=pltpu.VMEM)


def mixer_front(scalars, gain, conv_weight, conv_bias, arrays, collective_id):
    narrow, wide = lax.axis_size(NARROW), lax.axis_size(WIDE)
    devices, depth = narrow * wide, wide // 2
    pack, table, xz_blocks, gate, up, down, middle, cotangent = arrays
    patches = cotangent.shape[0] // PATCH
    count = devices * patches
    units = gate.shape[1] // narrow
    dma = pltpu.SemaphoreType.DMA
    anywhere = pl.BlockSpec(memory_space=pl.ANY)

    def full(*shape):
        return jax.ShapeDtypeStruct(shape, FULL)

    def low(*shape):
        return jax.ShapeDtypeStruct(shape, LOW)

    outs = pl.pallas_call(
        partial(mixer_front_kernel, narrow, wide),
        out_shape=[
            low(count, D),
            low(count, D),
            low(count, 2 * HEAD_M),
            low(count, 2 * STATE),
            full(count, 1),
            full(count, HEAD_M),
            full(count, HEAD_M),
            full(count // QUERY, HEAD_M, STATE),
            full(patches, D),
            low(devices, patches, HEAD_M),
            full(count + 8, 8),
            full(narrow, patches * PATCH, 1),
            full(count, PATCH),
            low(narrow, depth, 2, *pack.shape),
            low(*xz_blocks.shape),
            low(depth, 2, D, units),
            low(depth, 2, D, units),
            low(depth, 2, units, D),
            low(narrow, depth, 2, *middle.shape),
            low(narrow, *cotangent.shape),
        ],
        in_specs=[in_smem()] * 5 + [in_vmem()] * 3 + [anywhere] * 8,
        out_specs=[in_vmem()] * 15 + [anywhere] * 5,
        scratch_shapes=[
            pltpu.VMEM((narrow, depth, 2) + table.shape, FULL),
            pltpu.VMEM((D, units), LOW),
            pltpu.VMEM((D, units), LOW),
            pltpu.VMEM((units, D), LOW),
            pltpu.VMEM((count, D), FULL),
            pltpu.VMEM((count + 8, 2 * HEAD_M), FULL),
            pltpu.VMEM((count + 8, 2 * STATE), FULL),
            pltpu.VMEM((HEAD_M, STATE), FULL),
            pltpu.VMEM((devices, patches, HEAD_M), LOW),
            dma,
            dma,
            dma((7,)),
            dma((7,)),
            dma((2,)),
            dma((narrow - 1, 3)),
            dma((narrow - 1, 3)),
            dma((5,)),
            dma((depth,)),
            dma((depth,)),
            dma((narrow,)),
            dma((narrow,)),
            dma((3,)),
            dma((3, depth, 2)),
            dma((3, depth)),
            dma((3,)),
            dma((3,)),
            dma((2, 8, depth)),
        ],
        compiler_params=pltpu.CompilerParams(
            collective_id=collective_id, has_side_effects=True, vmem_limit_bytes=52 << 20
        ),
        name="mixer_front",
    )(*scalars, gain, conv_weight, conv_bias, *arrays)
    start, w_xz, gate_all, up_all, down_all, middle_all, others = outs[13:]
    return (
        outs[:13],
        start.reshape(D, -1),
        w_xz.reshape(D, -1),
        gate_all.reshape(wide, D, -1),
        up_all.reshape(wide, D, -1),
        down_all.reshape(-1, D),
        middle_all.reshape(D, -1),
        others,
    )


def mixer_backward(
    scalars,
    xz,
    bc,
    dt,
    marks,
    conv_weight,
    conv_bias,
    y,
    states,
    normed,
    w_xz,
    start,
    mixed_in,
    global_grad,
    gain,
    gated_scale,
    gain_grads,
    gated_gain_grads,
    du_blocks,
    up_parts,
    down_parts,
    middle_parts,
    gate_sum,
    mix_grad,
    collective_id,
):
    narrow, wide = lax.axis_size(NARROW), lax.axis_size(WIDE)
    devices = narrow * wide
    count, width = normed.shape
    patches = count // devices
    own_rows = width // devices
    dma = pltpu.SemaphoreType.DMA
    low = partial(pltpu.VMEM, dtype=LOW)
    every = width + 3 * STATE
    back_shape = (gate_sum.shape[0] // narrow, gate_sum.shape[1] * narrow)
    anywhere = pl.BlockSpec(memory_space=pl.ANY)
    return pl.pallas_call(
        partial(mixer_backward_kernel, narrow, wide),
        out_shape=[
            jax.ShapeDtypeStruct((patches, width + 128), LOW),
            jax.ShapeDtypeStruct((SUM_ROWS + CONV + 2, 128), FULL),
            jax.ShapeDtypeStruct((own_rows, 3 * STATE), FULL),
            jax.ShapeDtypeStruct((devices, own_rows, 2 * HEAD_M), LOW),
            jax.ShapeDtypeStruct(up_parts.shape[1:], LOW),
            jax.ShapeDtypeStruct(down_parts.shape[1:], LOW),
            jax.ShapeDtypeStruct(middle_parts.shape[1:], LOW),
            jax.ShapeDtypeStruct(back_shape, FULL),
            jax.ShapeDtypeStruct((narrow, wide // 2, 2) + mix_grad.shape, LOW),
        ],
        in_specs=[in_smem()] * 3
        + [in_vmem()] * 10
        + [anywhere]
        + [in_vmem()] * 7
        + [anywhere] * 5,
        out_specs=[in_vmem()] * 8 + [anywhere],
        scratch_shapes=[
            low((width, 3 * STATE)),
            dma,
            pltpu.VMEM((8, 2 * HEAD_M), FULL),
            pltpu.VMEM((8, 2 * STATE), FULL),
            pltpu.VMEM((8, 128), FULL),
            pltpu.VMEM((count + 8, 2 * HEAD_M), FULL),
            pltpu.VMEM((count + 8, 2 * STATE), FULL),
            pltpu.VMEM((count + 8, 2 * HEAD_M), FULL),
            pltpu.VMEM((count + 8, 2 * STATE), FULL),
            pltpu.VMEM((HEAD_M, STATE), FULL),
            low((devices, patches, HEAD_M)),
            low((count, 2 * HEAD_M)),
            low((count, 3 * STATE)),
            low((narrow, wide // 2, 2, patches, every)),
            low((narrow, wide // 2, patches, every)),
            low((narrow - 1, wide // 2, patches, every)),
            low((wide // 2, patches, every)),
            low((wide // 2 - 1, patches, every)),
            low((devices, own_rows, 2 * HEAD_M)),
            low((devices, own_rows, 2 * HEAD_M)),
            low(up_parts.shape),
            low(down_parts.shape),
            low(middle_parts.shape[1:]),
            low((2, wide // 4) + middle_parts.shape[2:]),
            low((6, wide // 4) + middle_parts.shape[2:]),
            low(back_shape),
            dma,
            dma,
            dma,
            dma,
            dma((narrow - 1,)),
            dma((narrow - 1,)),
            dma((wide // 2 - 1,)),
            dma((wide // 2 - 1,)),
            dma,
            dma,
            dma((wide,)),
            dma((wide,)),
            dma((2, 8)),
            dma((narrow - 1,)),
            dma((narrow - 1,)),
            dma,
            dma((7,)),
        ],
        compiler_params=pltpu.CompilerParams(
            collective_id=collective_id, has_side_effects=True, vmem_limit_bytes=36 << 20
        ),
        name="mixer_backward",
    )(
        *scalars,
        xz,
        bc,
        dt,
        marks,
        conv_weight,
        conv_bias,
        y,
        states,
        normed,
        w_xz,
        start,
        mixed_in,
        global_grad,
        gain,
        gated_scale,
        gain_grads,
        gated_gain_grads,
        du_blocks,
        up_parts,
        down_parts,
        middle_parts,
        gate_sum,
        mix_grad,
    )


def finish_kernel(
    pack_all,
    mix_all,
    u,
    keep,
    middle,
    xz_grads,
    bcdt_grads,
    gated_gain,
    embedded,
    start,
    table_out,
    patch_out,
    in_out,
    out_out,
    local_out,
    query_out,
    key_out,
    value_out,
    attn_out,
    embedded_own,
    ids_all,
    patch_all,
    rows_of_four,
    sems,
):
    me = lax.axis_index(NARROW) * lax.axis_size(WIDE) + lax.axis_index(WIDE)
    own_rows = patch_out.shape[0]
    group = 128 // own_rows
    columns = pl.ds(pl.multiple_of(lax.div(me, group) * 128, 128), 128)
    copies = [
        pltpu.make_async_copy(embedded.at[:, columns], embedded_own, sems.at[0]),
        pltpu.make_async_copy(start.at[:, pl.ds(3 * STATE, 128)], ids_all, sems.at[1]),
        pltpu.make_async_copy(start.at[:, pl.ds(4 * STATE, D)], patch_all, sems.at[2]),
    ]
    for copy in copies:
        copy.start()
    for i, out in enumerate((query_out, key_out, value_out, attn_out)):
        out[...] = middle[:, i * D : (i + 1) * D]
    local_out[...] = middle[:, 4 * D :].T
    for pair in range(0, HEADS_M, 2):
        both = [xz_grads[pair + i].astype(FULL) for i in range(2)]
        first = pair * HEAD_M
        in_out[:, first : first + 128] = jnp.concatenate([v[:, HEAD_M:] for v in both], axis=1)
        in_out[:, DI + first : DI + first + 128] = jnp.concatenate(
            [v[:, :HEAD_M] for v in both], axis=1
        )
    in_out[:, 2 * DI : 2 * DI + 2 * STATE] = bcdt_grads[:, : 2 * STATE]
    in_out[:, 2 * DI + 2 * STATE :] = bcdt_grads[:, 2 * STATE : 2 * STATE + HEADS_M]
    scale = pack_all[:, D:].astype(FULL)[:, :HEAD_M]
    gain = head_columns(gated_gain, me)[:, :HEAD_M]
    gated = (u[...] * scale * gain).astype(LOW)
    out_out[...] = tn(gated, mix_all[...])
    copies[0].wait()
    copies[1].wait()
    grads = pack_all[:, :D]
    rows_of_four[...] = tn(embedded_own[...], grads)
    patch_out[...] = rows_of_four[pl.ds(pl.multiple_of(lax.rem(me, group) * own_rows, own_rows), own_rows), :]
    own_words = table_out.shape[0]
    count = pack_all.shape[0]
    lane = lax.broadcasted_iota(jnp.int32, (count, PATCH * own_words), 1)
    ids = jnp.zeros((count, PATCH * own_words), FULL)
    kept = jnp.zeros((count, PATCH * own_words), FULL)
    values = ids_all[...].astype(FULL)
    for k in range(PATCH):
        here = lax.div(lane, own_words) == k
        ids = jnp.where(here, values[:, k : k + 1], ids)
        kept = jnp.where(here, keep[:, k : k + 1], kept)
    words = (me * own_words + lax.rem(lane, own_words)).astype(FULL)
    sums = tn(jnp.where(ids == words, kept, 0.0).astype(LOW), grads)
    high = sums.astype(LOW)
    rest = (sums - high.astype(FULL)).astype(LOW)
    copies[2].wait()
    table = jnp.zeros(table_out.shape, FULL)
    for k in range(PATCH):
        rows = slice(k * own_words, (k + 1) * own_words)
        weight = patch_all[k * EMB : (k + 1) * EMB, :]
        table += nt(high[rows], weight) + nt(rest[rows], weight)
    table_out[...] = table


def finish(pack_all, mix_all, u, keep, middle, xz_grads, bcdt_grads, gated_gain, embedded, start):
    count = pack_all.shape[0]
    devices, own_rows = xz_grads.shape[:2]
    anywhere = pl.BlockSpec(memory_space=pl.ANY)

    def full(*shape):
        return jax.ShapeDtypeStruct(shape, FULL)

    return pl.pallas_call(
        finish_kernel,
        out_shape=[
            full(VOCAB // devices, EMB),
            full(own_rows, D),
            full(own_rows, 2 * DI + 2 * STATE + HEADS_M),
            full(DI // devices, D),
            full(EMB, own_rows),
        ]
        + [full(own_rows, D)] * 4,
        in_specs=[in_vmem()] * 8 + [anywhere] * 2,
        out_specs=[in_vmem()] * 9,
        scratch_shapes=[
            pltpu.VMEM((count, 128), LOW),
            pltpu.VMEM((count, 128), LOW),
            pltpu.VMEM((D, D), LOW),
            pltpu.VMEM((128, D), FULL),
            pltpu.SemaphoreType.DMA((3,)),
        ],
        compiler_params=pltpu.CompilerParams(vmem_limit_bytes=20 << 20),
        name="finish",
    )(pack_all, mix_all, u, keep, middle, xz_grads, bcdt_grads, gated_gain, embedded, start)


def patch_causal():
    row = lax.broadcasted_iota(jnp.int32, (BYTE_BLOCK, BYTE_BLOCK), 0)
    column = lax.broadcasted_iota(jnp.int32, (BYTE_BLOCK, BYTE_BLOCK), 1)
    return (lax.div(row, PATCH) == lax.div(column, PATCH)) & (row >= column)


def head_probs(q, k, causal):
    scores = jnp.where(causal, nt(q, k) * HEAD_A ** (-0.5), masked_score)
    grown = jnp.exp(scores - jnp.max(scores, axis=1, keepdims=True))
    return grown / jnp.sum(grown, axis=1, keepdims=True)


def of_head(block, half):
    lane = lax.broadcasted_iota(jnp.int32, block.shape, 1)
    return jnp.where(lax.div(lane, HEAD_A) == half, block, jnp.zeros_like(block))


def fetched(pack, places, blocks, sems):
    copies = []
    for i, place in enumerate(places):
        width = place.shape[1]
        start = blocks[i]
        copies.append(
            pltpu.make_async_copy(pack.at[:, pl.ds(start, width)], place, sems.at[i])
        )
        copies[-1].start()
    return [copy.wait for copy in copies]


def split_gain(gain):
    half = HEAD_M // 2
    rows = []
    for i in range(2):
        groups = []
        for first in range(0, HEADS_M, 4):
            starts = [(first + j) * HEAD_M + i * half for j in range(4)]
            groups.append(jnp.concatenate([gain[:, a : a + half] for a in starts], axis=1))
        rows.append(jnp.concatenate(groups, axis=1))
    return rows


def unit_rows(values):
    scale = lax.rsqrt(jnp.mean(values * values, axis=1, keepdims=True) + epsilon)
    return values * scale, scale


def norm_back(grad, gain, unit, scale):
    scaled = grad * gain
    return scale * (scaled - unit * jnp.mean(scaled * unit, axis=1, keepdims=True))


WEIGHT_STEP = 256


def attend_pairs(qkv, mixed):
    causal = patch_causal()
    blocks = qkv.shape[0] // BYTE_BLOCK

    def pair(i, carry):
        def lanes(part):
            start = part * D + i * (2 * HEAD_A)
            return pl.ds(pl.multiple_of(start, 2 * HEAD_A), 2 * HEAD_A)

        for block in range(blocks):
            rows = pl.ds(block * BYTE_BLOCK, BYTE_BLOCK)
            q, k, v = qkv[rows, lanes(0)], qkv[rows, lanes(1)], qkv[rows, lanes(2)]
            total = jnp.zeros(q.shape, FULL)
            for half in range(2):
                probs = head_probs(of_head(q, half), k, causal)
                total += nn(probs.astype(LOW), of_head(v, half))
            mixed[rows, lanes(0)] = total.astype(LOW)
        return carry

    lax.fori_loop(0, HEADS_A // 2, pair, 0)


def attend_pairs_back(qkv, heads_grad, qkv_grad):
    causal = patch_causal()
    blocks = qkv.shape[0] // BYTE_BLOCK
    scale = HEAD_A ** (-0.5)

    def pair(i, carry):
        def lanes(part):
            start = part * D + i * (2 * HEAD_A)
            return pl.ds(pl.multiple_of(start, 2 * HEAD_A), 2 * HEAD_A)

        for block in range(blocks):
            rows = pl.ds(block * BYTE_BLOCK, BYTE_BLOCK)
            q, k, v = qkv[rows, lanes(0)], qkv[rows, lanes(1)], qkv[rows, lanes(2)]
            g = heads_grad[rows, lanes(0)]
            dq = jnp.zeros(q.shape, FULL)
            dk = jnp.zeros(q.shape, FULL)
            dv = jnp.zeros(q.shape, FULL)
            for half in range(2):
                own_q, own_k, own_g = of_head(q, half), of_head(k, half), of_head(g, half)
                probs = head_probs(own_q, k, causal)
                dprobs = nt(own_g, v)
                dv += tn(probs.astype(LOW), own_g)
                dscores = probs * (dprobs - jnp.sum(probs * dprobs, axis=1, keepdims=True))
                dscores = dscores.astype(LOW)
                dq += nn(dscores, own_k)
                dk += tn(dscores, own_q)
            qkv_grad[rows, lanes(0)] = (dq * scale).astype(LOW)
            qkv_grad[rows, lanes(1)] = (dk * scale).astype(LOW)
            qkv_grad[rows, lanes(2)] = dv.astype(LOW)
        return carry

    lax.fori_loop(0, HEADS_A // 2, pair, 0)


def bytes_forward_kernel(
    u_blocks,
    mixed_in,
    attn_gain,
    feed_gain,
    gated_gain,
    pack,
    gated_out,
    local_out,
    stream_out,
    normed_out,
    qkv,
    mixed,
    after_out,
    feed_out,
    w_out0,
    w_out1,
    w_local,
    w_q,
    w_k,
    w_v,
    w_attn,
    pieces,
    sems,
):
    places = (w_out0, w_out1, w_local, w_q, w_k, w_v, w_attn)
    blocks = [4 * D, 5 * D, 6 * D, 0, D, 2 * D, 3 * D]
    waits = fetched(pack, places, blocks, sems)
    patches = mixed_in.shape[0]
    half = HEAD_M // 2
    for i in range(2):
        for first in range(0, HEADS_M, 4):
            gated_out[i, :, first * half : (first + 4) * half] = jnp.concatenate(
                [
                    u_blocks[first + j].astype(FULL)[:, i * half : (i + 1) * half]
                    for j in range(4)
                ],
                axis=1,
            )
    held = [gated_out[0], gated_out[1]]
    square = sum(jnp.sum(v * v, axis=1, keepdims=True) for v in held)
    scale = lax.rsqrt(square / (2 * D) + epsilon)
    split = split_gain(gated_gain)
    gated = [(held[i] * scale * split[i]).astype(LOW) for i in range(2)]
    waits[0]()
    waits[1]()
    joined = mixed_in[...] + nn(gated[0], w_out0[...]) + nn(gated[1], w_out1[...])
    for k in range(PATCH):
        pieces[pl.ds(k, patches, stride=PATCH), :] = joined[:, k * EMB : (k + 1) * EMB]
    local = pieces[...].astype(LOW)
    local_out[...] = local
    waits[2]()
    stream = nt(local, w_local[...])
    stream_out[...] = stream
    normed = (unit_rows(stream)[0] * attn_gain[...]).astype(LOW)
    normed_out[...] = normed
    for i, weight in enumerate((w_q, w_k, w_v)):
        waits[3 + i]()
        for first in range(0, D, WEIGHT_STEP):
            qkv[:, i * D + first : i * D + first + WEIGHT_STEP] = nn(
                normed, weight[:, first : first + WEIGHT_STEP]
            ).astype(LOW)
    attend_pairs(qkv, mixed)
    waits[6]()
    heads = mixed[...]
    for first in range(0, D, WEIGHT_STEP):
        columns = slice(first, first + WEIGHT_STEP)
        after_out[:, columns] = stream_out[:, columns] + nn(heads, w_attn[:, columns])
    feed_out[...] = (unit_rows(after_out[...])[0] * feed_gain[...]).astype(LOW)


def bytes_forward(u_blocks, mixed_in, attn_gain, feed_gain, gated_gain, pack):
    patches = mixed_in.shape[0]
    rows = patches * PATCH

    def full(shape, kind):
        return jax.ShapeDtypeStruct(shape, kind)

    return pl.pallas_call(
        bytes_forward_kernel,
        out_shape=[
            full((2, patches, D), FULL),
            full((rows, EMB), LOW),
            full((rows, D), FULL),
            full((rows, D), LOW),
            full((rows, 3 * D), LOW),
            full((rows, D), LOW),
            full((rows, D), FULL),
            full((rows, D), LOW),
        ],
        in_specs=[in_vmem()] * 5 + [pl.BlockSpec(memory_space=pl.ANY)],
        out_specs=[in_vmem()] * 8,
        scratch_shapes=[pltpu.VMEM((D, D), LOW)] * 2
        + [pltpu.VMEM((D, EMB), LOW)]
        + [pltpu.VMEM((D, D), LOW)] * 4
        + [pltpu.VMEM((rows, EMB), FULL), pltpu.SemaphoreType.DMA((7,))],
        compiler_params=pltpu.CompilerParams(vmem_limit_bytes=48 << 20),
        name="bytes_forward",
    )(u_blocks, mixed_in, attn_gain, feed_gain, gated_gain, pack)


def bytes_backward_kernel(
    narrow,
    feed_in_grad,
    cotangent,
    keep,
    after,
    stream_in,
    normed_in,
    qkv,
    mixed,
    local_in,
    gated_rows,
    attn_gain,
    feed_gain,
    gated_gain,
    pack,
    feed_parts,
    gate_parts,
    global_out,
    mix_out,
    scale_out,
    sums,
    gain_grads,
    gated_gain_grads,
    du_blocks,
    rows_out,
    gate_out,
    w_attn,
    w_q,
    w_k,
    w_v,
    w_local,
    w_out0,
    w_out1,
    after_grad,
    heads_grad,
    qkv_grad,
    pieces,
    parts_got,
    grads,
    grads_got,
    gate_got,
    sems,
    p_send,
    p_recv,
    t_send,
    t_recv,
    gate_sems,
):
    n, wide_place = lax.axis_index(NARROW), lax.axis_index(WIDE)
    core = lax.rem(wide_place, 2)
    twin = (n, wide_place + 1 - 2 * core)
    depth = gate_parts.shape[0]
    z_place = lax.div(wide_place, 2)
    line = LineSum(
        gate_parts, gate_got, gate_sems, z_place, depth, lambda there: (n, there * 2 + core)
    )

    def twin_copy(i, columns):
        return remote(
            grads.at[:, 1 - core, :, columns],
            grads_got.at[:, :, columns],
            t_send.at[i],
            t_recv.at[i],
            twin,
        )

    def give(i, columns, part):
        grads[:, :, :, columns] = part.astype(LOW).reshape(grads.shape[:3] + part.shape[1:])
        twin_copy(i, columns).start()

    def part_copy(k):
        peer = (square_peer(n, k), wide_place)
        return remote(feed_parts.at[k], parts_got.at[k], p_send.at[k - 1], p_recv.at[k - 1], peer)

    own_part = pltpu.make_async_copy(feed_parts.at[0], parts_got.at[0], sems.at[7])
    own_part.start()
    places = (w_attn, w_q, w_k, w_v, w_local, w_out0, w_out1)
    blocks = [3 * D, 0, D, 2 * D, 6 * D, 4 * D, 5 * D]
    waits = fetched(pack, places, blocks, sems)
    greet_lines(narrow, depth)
    line.start()
    for k in range(1, narrow):
        part_copy(k).start()
    patches = global_out.shape[0]
    unit, scale = unit_rows(after[...])
    grad = feed_in_grad[...].astype(LOW).astype(FULL)
    gain_grads[1:2, :] = jnp.sum(grad * unit, axis=0, keepdims=True)
    after_grad[...] = cotangent[...].astype(FULL) * keep[0] + norm_back(
        grad, feed_gain[...], unit, scale
    )
    attn_grad = after_grad[...].astype(LOW)
    waits[0]()
    for first in range(0, D, WEIGHT_STEP):
        columns = slice(first, first + WEIGHT_STEP)
        heads_grad[:, columns] = nt(attn_grad, w_attn[columns, :]).astype(LOW)
        give(
            (3 * D + first) // WEIGHT_STEP,
            pl.ds(3 * D + first, WEIGHT_STEP),
            tn(mixed[...], attn_grad[:, columns]),
        )
    attend_pairs_back(qkv, heads_grad, qkv_grad)
    normed_grad = jnp.zeros(after_grad.shape, FULL)
    for i, weight in enumerate((w_q, w_k, w_v)):
        waits[1 + i]()
        normed_grad += nt(qkv_grad[:, i * D : (i + 1) * D], weight[...])
    unit, scale = unit_rows(stream_in[...])
    gain_grads[0:1, :] = jnp.sum(normed_grad * unit, axis=0, keepdims=True)
    stream_grad = (after_grad[...] + norm_back(normed_grad, attn_gain[...], unit, scale)).astype(LOW)
    waits[4]()
    pieces[...] = nn(stream_grad, w_local[...])
    for k in range(PATCH):
        global_out[:, k * EMB : (k + 1) * EMB] = pieces[pl.ds(k, patches, stride=PATCH), :]
    mix_grad = global_out[...].astype(LOW)
    mix_out[...] = mix_grad
    waits[5]()
    waits[6]()
    inner = [nt(mix_grad, w_out0[...]), nt(mix_grad, w_out1[...])]
    held = [gated_rows[0], gated_rows[1]]
    square = sum(jnp.sum(v * v, axis=1, keepdims=True) for v in held)
    scale = lax.rsqrt(square / (2 * D) + epsilon)
    units = [v * scale for v in held]
    split = split_gain(gated_gain)
    scaled = [inner[i] * split[i] for i in range(2)]
    mean = sum(jnp.sum(scaled[i] * units[i], axis=1, keepdims=True) for i in range(2)) / (2 * D)
    for i in range(2):
        gated_gain_grads[i : i + 1, :] = jnp.sum(inner[i] * units[i], axis=0, keepdims=True)
    scale_out[...] = jnp.broadcast_to(scale, scale_out.shape)
    rows_grads = [scale * (scaled[i] - units[i] * mean) for i in range(2)]
    half = HEAD_M // 2
    for head in range(HEADS_M):
        lanes = slice(head * half, (head + 1) * half)
        du_blocks[head] = jnp.concatenate([part[:, lanes] for part in rows_grads], axis=1).astype(LOW)
    give(4 * D // WEIGHT_STEP, pl.ds(4 * D, EMB), tn(stream_grad, local_in[...]))

    def weight_grads(i, carry):
        columns = pl.ds(pl.multiple_of(i * WEIGHT_STEP, WEIGHT_STEP), WEIGHT_STEP)
        give(i, columns, tn(normed_in[...], qkv_grad[:, columns]))
        return carry

    lax.fori_loop(0, 3 * D // WEIGHT_STEP, weight_grads, 0)
    own_part.wait()
    for k in range(1, narrow):
        part_copy(k).wait_recv()
    for first in range(0, D, WEIGHT_STEP):
        columns = slice(first, first + WEIGHT_STEP)
        feed = parts_got[0, :, columns].astype(FULL)
        for k in range(1, narrow):
            feed += parts_got[k, :, columns].astype(FULL)
        feed = feed.astype(LOW).astype(FULL)
        rows_out[:, columns] = ((after[:, columns] + feed) * keep[0]).astype(LOW)

    def add_twin(i, columns):
        twin_copy(i, columns).wait_recv()
        sums[:, :, columns] = (
            grads[:, core, :, columns].astype(FULL) + grads_got[:, :, columns].astype(FULL)
        ).astype(LOW)

    def add_one(i, carry):
        add_twin(i, pl.ds(pl.multiple_of(i * WEIGHT_STEP, WEIGHT_STEP), WEIGHT_STEP))
        return carry

    def end_one(i, carry):
        twin_copy(i, pl.ds(pl.multiple_of(i * WEIGHT_STEP, WEIGHT_STEP), WEIGHT_STEP)).wait_send()
        return carry

    steps = 4 * D // WEIGHT_STEP
    add_twin(steps, pl.ds(4 * D, EMB))
    lax.fori_loop(0, steps, add_one, 0)
    line.arrive()
    gate_out[...] = line.total().astype(LOW)
    line.finish()
    twin_copy(steps, pl.ds(4 * D, EMB)).wait_send()
    lax.fori_loop(0, steps, end_one, 0)
    for k in range(1, narrow):
        part_copy(k).wait_send()


def bytes_backward(
    feed_in_grad,
    cotangent,
    keep,
    after,
    stream,
    normed,
    qkv,
    mixed,
    local,
    gated_rows,
    attn_gain,
    feed_gain,
    gated_gain,
    pack,
    feed_parts,
    gate_parts,
    collective_id,
):
    narrow = feed_parts.shape[0]
    every = 4 * D + EMB
    rows = after.shape[0]
    patches = rows // PATCH

    def full(shape, kind):
        return jax.ShapeDtypeStruct(shape, kind)

    return pl.pallas_call(
        partial(bytes_backward_kernel, narrow),
        out_shape=[
            full((patches, D), FULL),
            full((patches, D), LOW),
            full((patches, 128), FULL),
            full((HEADS_M // 2, D // HEADS_M, every), LOW),
            full((2, D), FULL),
            full((2, D), FULL),
            full((HEADS_M, patches, HEAD_M), LOW),
            full((rows, D), LOW),
            full(gate_parts.shape[1:], LOW),
        ],
        in_specs=[in_vmem()] * 13 + [pl.BlockSpec(memory_space=pl.ANY)] * 3,
        out_specs=[in_vmem()] * 9,
        scratch_shapes=[pltpu.VMEM((D, D), LOW)] * 4
        + [pltpu.VMEM((D, EMB), LOW)]
        + [pltpu.VMEM((D, D), LOW)] * 2
        + [
            pltpu.VMEM((rows, D), FULL),
            pltpu.VMEM((rows, D), LOW),
            pltpu.VMEM((rows, 3 * D), LOW),
            pltpu.VMEM((rows, EMB), FULL),
            pltpu.VMEM((narrow, rows, D), LOW),
            pltpu.VMEM((HEADS_M // 2, 2, D // HEADS_M, every), LOW),
            pltpu.VMEM((HEADS_M // 2, D // HEADS_M, every), LOW),
            pltpu.VMEM(gate_parts.shape, LOW),
            pltpu.SemaphoreType.DMA((8,)),
            pltpu.SemaphoreType.DMA((narrow - 1,)),
            pltpu.SemaphoreType.DMA((narrow - 1,)),
            pltpu.SemaphoreType.DMA((4 * D // WEIGHT_STEP + 1,)),
            pltpu.SemaphoreType.DMA((4 * D // WEIGHT_STEP + 1,)),
            pltpu.SemaphoreType.DMA((2 * gate_parts.shape[0],)),
        ],
        compiler_params=pltpu.CompilerParams(
            collective_id=collective_id, has_side_effects=True, vmem_limit_bytes=44 << 20
        ),
        name="bytes_backward",
    )(
        feed_in_grad,
        cotangent,
        keep,
        after,
        stream,
        normed,
        qkv,
        mixed,
        local,
        gated_rows,
        attn_gain,
        feed_gain,
        gated_gain,
        pack,
        feed_parts,
        gate_parts,
    )


def feed_kernel(narrow, x_in, g_own, g_others, keep, *refs):
    gate_in, up_in, down_in, f_out, gx_out, gate_sum, up_sum, down_sum = refs[:8]
    wg, wu, wd, x, xt, g, hid, gg, gu, sent, got = refs[8:19]
    gate_twin, up_twin, down_twin, gate_got, up_got, down_got = refs[19:25]
    w_sem, g_sem, x_sem, x_send, x_recv, r_send, r_recv, t_send, t_recv = refs[25:]
    n, wide_place = lax.axis_index(NARROW), lax.axis_index(WIDE)
    core = lax.rem(wide_place, 2)
    twin = (n, wide_place + 1 - 2 * core)
    barrier = pltpu.get_barrier_semaphore()
    pl.semaphore_signal(barrier, inc=1, device_id=twin, device_id_type=MESH)
    for k in range(1, narrow):
        peer = (lax.rem(n + k, narrow), wide_place)
        pl.semaphore_signal(barrier, inc=1, device_id=peer, device_id_type=MESH)
    places, width, share = gate_in.shape
    rows = x_in.shape[0]
    hidden = places * share
    depth = places // 2
    chunk = 2 * share
    own_x = pltpu.make_async_copy(x_in, x.at[0], x_sem)
    own_x.start()
    g_copies = [
        pltpu.make_async_copy(g_own, g.at[0], g_sem.at[0]),
        pltpu.make_async_copy(
            g_others.at[pl.ds(1, narrow - 1)], g.at[pl.ds(1, narrow - 1)], g_sem.at[1]
        ),
    ]
    w_copies = [pltpu.make_async_copy(down_in, wd, w_sem.at[2 * places])]
    for place in range(places):
        units = slice(place * share, (place + 1) * share)
        w_copies.append(pltpu.make_async_copy(gate_in.at[place], wg.at[:, units], w_sem.at[place]))
        w_copies.append(
            pltpu.make_async_copy(up_in.at[place], wu.at[:, units], w_sem.at[places + place])
        )
    g_copies[0].start()
    for copy in w_copies:
        copy.start()
    for copy in g_copies[1:]:
        copy.start()
    pl.semaphore_wait(barrier, narrow)

    share_x = SquareShare(x_in, x, x_send, x_recv, n, wide_place)

    def r_copy(k):
        peer = (square_peer(n, k), wide_place)
        return remote(sent.at[k - 1], got.at[k - 1], r_send.at[k - 1], r_recv.at[k - 1], peer)

    share_x.start()
    own_x.wait()
    for copy in w_copies:
        copy.wait()
    for copy in g_copies:
        copy.wait()

    def block(k, carry):
        @pl.when(k == 1)
        def _():
            share_x.relay(0)
            share_x.relay(1)

        @pl.when(k == narrow - 1)
        def _():
            share_x.arrive()

        xk = x[k]
        gk = (g[k].astype(FULL) * keep[k]).astype(LOW)
        g[k] = gk
        xt[:, pl.ds(pl.multiple_of(k * rows, rows), rows)] = xk.T
        for first in range(0, hidden, chunk):
            units = slice(first, first + chunk)
            gate = nn(xk, wg[:, units])
            up = nn(xk, wu[:, units])
            dhid = nt(gk, wd[units, :])
            s = jax.nn.sigmoid(gate)
            act = gate * s
            hid[k, :, units] = (act * up).astype(LOW)
            gg[k, :, units] = (dhid * up * s * (1.0 + gate * (1.0 - s))).astype(LOW)
            gu[k, :, units] = (dhid * act).astype(LOW)
        ggk, guk, hidk = gg[k], gu[k], hid[k]
        for first in range(0, width, chunk):
            columns = slice(first, first + chunk)
            gx = nt(ggk, wg[columns, :]) + nt(guk, wu[columns, :])

            @pl.when(k == 0)
            def _():
                gx_out[:, columns] = gx

            @pl.when(k > 0)
            def _():
                sent[k - 1, :, columns] = gx.astype(LOW)

        @pl.when(k > 0)
        def _():
            r_copy(k).start()

        for first in range(0, width, chunk):
            columns = slice(first, first + chunk)
            f_out[k, :, columns] = nn(hidk, wd[:, columns]).astype(LOW)
        return carry

    lax.fori_loop(0, narrow, block, 0)

    def units_of(j, of_core):
        start = (2 * j + of_core) * share
        return pl.ds(pl.multiple_of(start, share), share)

    def two_places(left, j, of_core):
        pair = [left[:, :, units_of(2 * j + i, of_core)] for i in range(2)]
        return jnp.concatenate(pair, axis=2).reshape(narrow * rows, chunk)

    def columns_grads(left, j, of_core):
        total = nn(xt[...], two_places(left, j, of_core))
        return total[:, :share], total[:, share:]

    def rows_grads(j, of_core):
        total = tn(two_places(hid, j, of_core), g[...].reshape(narrow * rows, width))
        return total[:share], total[share:]

    outs = (gate_twin, up_twin, down_twin)
    ins = (gate_got, up_got, down_got)

    def t_copy(i, j):
        return remote(outs[i].at[j], ins[i].at[j], t_send.at[i, j], t_recv.at[i, j], twin)

    def for_twin(j, carry):
        for i, left in enumerate((gg, gu)):
            for half, part in enumerate(columns_grads(left, j, 1 - core)):
                outs[i][2 * j + half] = part.astype(LOW)
                t_copy(i, 2 * j + half).start()
        for half, part in enumerate(rows_grads(j, 1 - core)):
            outs[2][2 * j + half] = part.astype(LOW)
            t_copy(2, 2 * j + half).start()
        return carry

    def for_own(j, carry):
        for i, (left, total) in enumerate(((gg, gate_sum), (gu, up_sum))):
            for half, part in enumerate(columns_grads(left, j, core)):
                t_copy(i, 2 * j + half).wait_recv()
                total[2 * j + half] = (part + ins[i][2 * j + half].astype(FULL)).astype(LOW)
        for half, part in enumerate(rows_grads(j, core)):
            t_copy(2, 2 * j + half).wait_recv()
            down_sum[2 * j + half] = (part + ins[2][2 * j + half].astype(FULL)).astype(LOW)
        return carry

    lax.fori_loop(0, depth // 2, for_twin, 0)
    lax.fori_loop(0, depth // 2, for_own, 0)
    for k in range(1, narrow):
        r_copy(k).wait_recv()
        gx_out[...] += got[k - 1].astype(FULL)
    share_x.finish()
    for k in range(1, narrow):
        r_copy(k).wait_send()
    for i in range(3):
        for j in range(depth):
            t_copy(i, j).wait_send()


def feed_forward_back(x_own, g_own, g_others, keep, gate_all, up_all, down_all, collective_id):
    narrow = keep.shape[0]
    rows, width = x_own.shape
    places, _, share = gate_all.shape
    hidden, depth = places * share, places // 2
    dma = pltpu.SemaphoreType.DMA
    anywhere = pl.BlockSpec(memory_space=pl.ANY)

    def low(*shape):
        return pltpu.VMEM(shape, LOW)

    sums = [(depth, width, share), (depth, width, share), (depth, share, width)]
    return pl.pallas_call(
        partial(feed_kernel, narrow),
        out_shape=[
            jax.ShapeDtypeStruct((narrow, rows, width), LOW),
            jax.ShapeDtypeStruct((rows, width), FULL),
        ]
        + [jax.ShapeDtypeStruct(shape, LOW) for shape in sums],
        in_specs=[anywhere] * 3 + [in_vmem()] + [anywhere] * 3,
        out_specs=[in_vmem()] * 5,
        scratch_shapes=[
            low(width, hidden),
            low(width, hidden),
            low(hidden, width),
            low(narrow, rows, width),
            low(width, narrow * rows),
            low(narrow, rows, width),
            low(narrow, rows, hidden),
            low(narrow, rows, hidden),
            low(narrow, rows, hidden),
            low(narrow - 1, rows, width),
            low(narrow - 1, rows, width),
        ]
        + [low(*shape) for shape in sums + sums]
        + [
            dma((2 * places + 1,)),
            dma((2,)),
            dma,
            dma((narrow,)),
            dma((narrow,)),
            dma((narrow - 1,)),
            dma((narrow - 1,)),
            dma((3, depth)),
            dma((3, depth)),
        ],
        compiler_params=pltpu.CompilerParams(
            collective_id=collective_id, has_side_effects=True, vmem_limit_bytes=36 << 20
        ),
        name="feed",
    )(x_own, g_own, g_others, keep, gate_all, up_all, down_all)


def per_device_heads(
    byte_ids,
    doc_patches,
    pad_bytes,
    byte_table,
    patch_weight,
    gain_mix,
    in_weight,
    conv_weight,
    conv_bias,
    step_bias,
    log_rate,
    skip_gain,
    gated_gain,
    out_weight,
    local_weight,
    gain_attn,
    query_weight,
    key_weight,
    value_weight,
    attn_weight,
    feed_gain,
    gate_weight,
    up_weight,
    down_weight,
    cotangent,
):
    narrow, wide = lax.axis_size(NARROW), lax.axis_size(WIDE)
    devices = narrow * wide
    device = lax.axis_index(BOTH)
    rows = byte_ids.shape[0]
    patches = rows // PATCH
    everything = devices * patches
    own_rows = patch_weight.shape[0]
    hidden_width = gate_weight.shape[1]
    share = hidden_width // narrow

    ids_low = byte_ids.astype(LOW).reshape(patches, PATCH)
    bcdt_width = 2 * STATE + HEADS_M
    start_pack = jnp.concatenate(
        [
            jnp.pad(in_weight[:, 2 * DI :], ((0, 0), (0, 96))),
            jnp.pad(ids_low, ((0, 0), (0, 120))),
            patch_weight,
        ],
        axis=1,
    )
    xz_blocks = jnp.concatenate(
        [
            in_weight[:, DI : 2 * DI].reshape(own_rows, HEADS_M, HEAD_M),
            in_weight[:, :DI].reshape(own_rows, HEADS_M, HEAD_M),
        ],
        axis=2,
    ).transpose(1, 0, 2)
    middle_pack = jnp.concatenate(
        [
            query_weight,
            key_weight,
            value_weight,
            attn_weight,
            out_weight[:own_rows],
            out_weight[own_rows:],
            local_weight.T,
        ],
        axis=1,
    )
    numbers = (step_bias, log_rate, skip_gain)
    conv = (conv_weight, conv_bias[None])
    front, start_all, xz_weight, gate_all, up_all, down_all, middle_all, others = mixer_front(
        (doc_patches, pad_bytes) + numbers,
        gain_mix[None],
        *conv,
        (
            start_pack,
            byte_table.astype(FULL),
            xz_blocks,
            gate_weight,
            up_weight,
            down_weight,
            middle_pack,
            cotangent,
        ),
        5,
    )
    embedded, normed_all, xz, bc, dt, u, y, states, mixed_in, u_blocks, marks, keep_rows, keep_all = front
    half = HEAD_M // 2

    byte_gains = (gain_attn[None], feed_gain[None], gated_gain[None])
    (
        gated_rows,
        local_rows,
        stream,
        normed_attn,
        qkv,
        mixed_heads,
        after_attn,
        normed_feed,
    ) = bytes_forward(u_blocks, mixed_in, *byte_gains, middle_all)
    feed_parts, feed_in_grad, gate_parts, up_parts, down_parts = feed_forward_back(
        normed_feed, cotangent, others, keep_rows, gate_all, up_all, down_all, 2
    )

    (
        global_grad,
        mix_grad,
        gated_scale,
        middle_parts,
        byte_gain_grads,
        gated_gain_grads,
        du_blocks,
        out_rows,
        gate_sum,
    ) = bytes_backward(
        feed_in_grad,
        cotangent,
        keep_rows,
        after_attn,
        stream,
        normed_attn,
        qkv,
        mixed_heads,
        local_rows,
        gated_rows,
        *byte_gains,
        middle_all,
        feed_parts,
        gate_parts,
        4,
    )
    middle_parts = middle_parts.reshape(narrow, wide // 2, own_rows, -1)

    (
        end_pack,
        sums_pack,
        bcdt_grads,
        xz_grads,
        up_sum,
        down_sum,
        middle_sums,
        grad_gate,
        mix_grad_all,
    ) = mixer_backward(
        numbers,
        xz,
        bc,
        dt,
        marks,
        *conv,
        y,
        states,
        normed_all,
        xz_weight,
        start_all,
        mixed_in,
        global_grad,
        gain_mix[None],
        gated_scale,
        byte_gain_grads,
        gated_gain_grads,
        du_blocks,
        up_parts,
        down_parts,
        middle_parts,
        gate_sum,
        mix_grad,
        3,
    )
    mix_grad_all = mix_grad_all.reshape(everything, D)

    end_all, sums_all, middle_sums, grad_up, grad_down = end_gather(
        end_pack, sums_pack, middle_sums, up_sum, down_sum, 1
    )
    (
        grad_table,
        grad_patch,
        grad_in,
        grad_out,
        grad_local,
        grad_query,
        grad_key,
        grad_value,
        grad_attn,
    ) = finish(
        end_all,
        mix_grad_all,
        u,
        keep_all,
        middle_sums,
        xz_grads,
        bcdt_grads,
        gated_gain[None],
        embedded,
        start_all,
    )
    small = jnp.sum(sums_all[:, :SUM_ROWS], axis=0).reshape(-1)
    gain_grads = jnp.split(small[: 3 * D + DI], [D, D + DI, 2 * D + DI])
    gain_grads[1] = gain_grads[1].reshape(2, devices, half).transpose(1, 0, 2).reshape(DI)
    conv_own = sums_all[:, SUM_ROWS : SUM_ROWS + CONV + 1, :HEAD_M].transpose(1, 0, 2)
    conv_grads = jnp.concatenate(
        [conv_own.reshape(CONV + 1, DI), small[3 * D + DI :].reshape(CONV + 1, 2 * STATE)], axis=1
    )
    number_grads = sums_all[:, SUM_ROWS + CONV + 1, :3].T
    return (
        out_rows,
        grad_table,
        grad_patch,
        gain_grads[0],
        grad_in,
        conv_grads[:CONV],
        conv_grads[CONV],
        number_grads[0],
        number_grads[1],
        number_grads[2],
        gain_grads[1],
        grad_out,
        grad_local,
        gain_grads[2],
        grad_query,
        grad_key,
        grad_value,
        grad_attn,
        gain_grads[3],
        grad_gate,
        grad_up,
        grad_down,
    )


def solution(mesh):
    placed = (
        P((NARROW, WIDE)),
        P(),
        P(),
        P((NARROW, WIDE), None),
        P((NARROW, WIDE), None),
        P(),
        P((NARROW, WIDE), None),
        P(),
        P(),
        P(),
        P(),
        P(),
        P(),
        P((NARROW, WIDE), None),
        P(None, (NARROW, WIDE)),
        P(),
        P((NARROW, WIDE), None),
        P((NARROW, WIDE), None),
        P((NARROW, WIDE), None),
        P((NARROW, WIDE), None),
        P(),
        P(NARROW, WIDE),
        P(NARROW, WIDE),
        P(WIDE, NARROW),
        P((NARROW, WIDE), None),
    )
    return jax.shard_map(
        per_device_heads if mesh.size == HEADS_M else per_device_rows,
        mesh=mesh,
        in_specs=placed,
        out_specs=(
            P((NARROW, WIDE), None),
            P((NARROW, WIDE), None),
            P((NARROW, WIDE), None),
            P(),
            P((NARROW, WIDE), None),
            P(),
            P(),
            P(),
            P(),
            P(),
            P(),
            P((NARROW, WIDE), None),
            P(None, (NARROW, WIDE)),
            P(),
            P((NARROW, WIDE), None),
            P((NARROW, WIDE), None),
            P((NARROW, WIDE), None),
            P((NARROW, WIDE), None),
            P(),
            P(NARROW, WIDE),
            P(NARROW, WIDE),
            P(WIDE, NARROW),
        ),
        check_vma=False,
    )
```
